32 devices in a mesh: fsdp: 4 (over z), ctx: 2 (over y), tp: 4 (over x, core).
Axes of the slice: x: 2, y: 2, z: 4, core: 2. Of those that a mesh axis runs over, the one named last changes fastest.
Arguments:
- hidden_in: bfloat16 [16, 1024, 1536], P('fsdp', 'ctx'), may hold values from -6 to 6
- cotangent: bfloat16 [16, 1024, 1536], P('fsdp', 'ctx'), may hold values from -6 to 6
- seq_lengths: int32 [16], replicated, may hold values from 128 to 1024, as said below
- positions: int32 [16, 1024], P(None, 'ctx'), may hold values from 0 to 1023, as said below
- permutation: int32 [16], replicated, may hold values from 0 to 15, as said below
- query_weight: bfloat16 [1536, 1536], P(('fsdp', 'ctx'), 'tp'), may hold values from -0.15625 to 0.15625
- keyval_weight: bfloat16 [1536, 512], P(('fsdp', 'ctx')), may hold values from -0.15625 to 0.15625
- output_weight: bfloat16 [1536, 1536], P('tp', ('fsdp', 'ctx')), may hold values from -2 to 2
- norm_gains: bfloat16 [2, 1536], P(None, ('fsdp', 'ctx')), may hold values from 0.25 to 1.75
- bias_query: bfloat16 [12, 128], P('tp'), may hold values from -3 to 3
- bias_keyval: bfloat16 [4, 128], replicated, may hold values from -3 to 3
- gate_weight: bfloat16 [1536, 8960], P(('fsdp', 'ctx'), 'tp'), may hold values from -0.15625 to 0.15625
- up_weight: bfloat16 [1536, 8960], P(('fsdp', 'ctx'), 'tp'), may hold values from -0.15625 to 0.15625
- down_weight: bfloat16 [8960, 1536], P('tp', ('fsdp', 'ctx')), may hold values from -0.09375 to 0.09375
Outputs:
- block_out: bfloat16 [16, 1024, 1536], P('fsdp', 'ctx')
- input_grad: bfloat16 [16, 1024, 1536], P('fsdp', 'ctx')
- query_weight_grad: float32 [1536, 1536], P(('fsdp', 'ctx'), 'tp')
- keyval_weight_grad: float32 [1536, 512], P(('fsdp', 'ctx'), 'tp')
- output_weight_grad: float32 [1536, 1536], P('tp', ('fsdp', 'ctx'))
- norm_gain_grad: float32 [2, 1536], P(None, ('fsdp', 'ctx'))
- query_bias_grad: float32 [12, 128], P('tp', ('fsdp', 'ctx'))
- keyval_bias_grad: float32 [4, 128], P('tp', ('fsdp', 'ctx'))
- gate_weight_grad: float32 [1536, 8960], P(('fsdp', 'ctx'), 'tp')
- up_weight_grad: float32 [1536, 8960], P(('fsdp', 'ctx'), 'tp')
- down_weight_grad: float32 [8960, 1536], P('tp', ('fsdp', 'ctx'))
The draws below stay inside these ranges and needn't reach their ends.
Inputs may be any that keep to these rules, and one draw needn't show every extreme that they name: `seq_lengths`: tokens at or after the length of a home sequence are padding, never visible as keys; one sequence has all 1024 tokens and one has 128. Along a home sequence the positions rise by one from token to token and fall back to 0 where a document starts; home sequence 0 is one document. A permutation of the 16 home sequences; group f of fsdp holds the working slots f * 4 to (f + 1) * 4 - 1 and receives exactly 1 sequence from the home range of each group.
All inputs are finite; a program needn't handle non-finite values.
Results may differ from the reference program's by a relative error of at most 0.015.
Values may be sent and summed in bfloat16 or wider, within the bound.
A program may use at most 256 MiB of HBM per device.

```python
import math
import jax
import jax.numpy as jnp
from jax import lax

D = 1536
HEADS = 12
KV_HEADS = 2
HEAD_DIM = 128
FF = 8960
PER_PEER = 1
LEN = 1024
SEQ_GRP = 4
SEQS = 16
N_FSDP = 4


def draw_seq_lengths(key, part):
    first_key, second_key = jax.random.split(key)
    drawn_lengths = jax.random.randint(first_key, (SEQS,), LEN // 8, LEN + 1)
    longest = jax.random.randint(second_key, (), 0, SEQS)
    slot_index = jnp.arange(SEQS)
    drawn_lengths = jnp.where(slot_index == longest, LEN, drawn_lengths)
    drawn_lengths = jnp.where(slot_index == (longest + 1) % SEQS, LEN // 8, drawn_lengths)
    return drawn_lengths.astype(jnp.int32)


def draw_positions(key, part):
    marks = jax.random.randint(key, (SEQS, LEN), 0, max(LEN // 4, 2))
    column = jnp.arange(LEN, dtype=jnp.int32)[None, :]
    starts = (marks == 0) & (column > 0) & (jnp.arange(SEQS)[:, None] > 0)
    begins = jnp.where(starts, column, 0).astype(jnp.int32)
    latest = lax.cummax(begins, axis=1)
    return (column - latest).astype(jnp.int32)


def draw_permutation(key, part):
    first_key, second_key = jax.random.split(key)
    shuffles = jax.vmap(lambda sub_key: jax.random.permutation(sub_key, SEQ_GRP))(jax.random.split(first_key, N_FSDP))
    sources = jnp.arange(N_FSDP)[:, None] * SEQ_GRP + shuffles
    arrivals = jnp.transpose(sources.reshape(N_FSDP, N_FSDP, PER_PEER), (1, 0, 2)).reshape(N_FSDP, SEQ_GRP)
    orders = jax.vmap(lambda sub_key: jax.random.permutation(sub_key, SEQ_GRP))(jax.random.split(second_key, N_FSDP))
    placed = jnp.take_along_axis(arrivals, orders, axis=1)
    return placed.reshape(SEQS).astype(jnp.int32)


def draw_bias_keyval(key, part):
    noise = jnp.clip(jax.random.normal(key, (2 * KV_HEADS, HEAD_DIM), dtype=jnp.float32), -3.0, 3.0)
    row_scale = jnp.where(jnp.arange(2 * KV_HEADS) % 2 == 0, 1.0, 0.05).astype(jnp.float32)
    return (noise * row_scale[:, None]).astype(jnp.bfloat16)


def shard_levels(key, shape, cuts, smallest, high):
    def one(axis_at, blocks):
        draws = jax.random.uniform(jax.random.fold_in(jax.random.fold_in(key, 6), axis_at), (blocks,), jnp.float32, smallest / len(cuts), high / len(cuts))
        return jnp.repeat(jnp.exp(draws), shape[axis_at] // blocks).reshape((-1,) + (1,) * (len(shape) - axis_at - 1))

    gain = one(*cuts[0])
    for cut in cuts[1:]:
        gain = gain * one(*cut)
    return gain


def gaussian(key, extent, deviation, reach, cuts=(), kind=jnp.bfloat16):
    values = deviation * jax.random.normal(key, extent, jnp.float32)
    if cuts:
        values = values * shard_levels(key, extent, cuts, -0.22, 0.18)
    return jnp.clip(values, -reach, reach).astype(kind)


def setup_inputs(seed: int = 0) -> dict:
    keys = jax.random.split(jax.random.key(seed), 15)
    hidden_in = gaussian(keys[0], (SEQS, LEN, D), 1.0, 6.0, ((0, 4), (1, 2)))
    cotangent = gaussian(keys[1], (SEQS, LEN, D), 1.0, 6.0, ((0, 4), (1, 2)))
    seq_lengths = draw_seq_lengths(jax.random.fold_in(keys[14], 71), 0)
    positions = draw_positions(jax.random.fold_in(keys[14], 71), 0)
    permutation = draw_permutation(jax.random.fold_in(keys[14], 71), 0)
    query_weight = gaussian(keys[5], (D, HEADS * HEAD_DIM), D ** -0.5, 0.15625, ((0, 8), (1, 4)))
    keyval_weight = gaussian(keys[6], (D, 2 * KV_HEADS * HEAD_DIM), D ** -0.5, 0.15625, ((0, 8),))
    output_weight = gaussian(keys[7], (HEADS * HEAD_DIM, D), (4 * HEADS * HEAD_DIM // LEN + 4) ** -0.5, 2.0, ((0, 4), (1, 8)))
    norm_gains = jnp.clip(1.0 + 0.15 * jax.random.normal(keys[8], (2, D), jnp.float32), 0.25, 1.75).astype(jnp.bfloat16)
    bias_query = gaussian(keys[9], (HEADS, HEAD_DIM), 0.5, 3.0, ((0, 4),))
    bias_keyval = draw_bias_keyval(jax.random.fold_in(keys[14], 71), 0)
    gate_weight = gaussian(keys[11], (D, FF), D ** -0.5, 0.15625, ((0, 8), (1, 4)))
    up_weight = gaussian(keys[12], (D, FF), D ** -0.5, 0.15625, ((0, 8), (1, 4)))
    down_weight = gaussian(keys[13], (FF, D), (FF // 2) ** -0.5, 0.09375, ((0, 4), (1, 8)))
    return {"hidden_in": hidden_in, "cotangent": cotangent, "seq_lengths": seq_lengths, "positions": positions, "permutation": permutation, "query_weight": query_weight, "keyval_weight": keyval_weight, "output_weight": output_weight, "norm_gains": norm_gains, "bias_query": bias_query, "bias_keyval": bias_keyval, "gate_weight": gate_weight, "up_weight": up_weight, "down_weight": down_weight}


EPS = 1e-06
ROPE_BASE = 10000.0
NEG_FILL = -1e+30
HIGHEST_PRECISION = lax.Precision.HIGHEST

@jax.custom_vjp
def low(v):
    return lax.optimization_barrier(v.astype(jnp.bfloat16)).astype(jnp.float32)

@jax.custom_vjp
def low_back(v):
    return v

def low_keep(v):
    return (low(v), None)

def low_pass(kept, grad):
    return (grad,)

def back_keep(v):
    return (v, None)

def back_low(kept, grad):
    return (low(grad),)
low.defvjp(low_keep, low_pass)
low_back.defvjp(back_keep, back_low)

def rope_tables(positions, head_dim):
    frequency = 1.0 / ROPE_BASE ** (jnp.arange(0, head_dim, 2, dtype=jnp.float32) / head_dim)
    angles = positions.astype(jnp.float32)[..., None] * frequency
    return (jnp.cos(angles), jnp.sin(angles))

def rotate(values, cosine, sine_part):
    half_width = values.shape[-1] // 2
    first_half = values[..., :half_width]
    second_half = values[..., half_width:]
    return jnp.concatenate([first_half * cosine - second_half * sine_part, second_half * cosine + first_half * sine_part], axis=-1)

def norm_apply(values, gain_row):
    scale_inv = lax.rsqrt(lax.optimization_barrier(jnp.mean(values * values, axis=-1, keepdims=True)) + EPS)
    return values * scale_inv * gain_row

def attend_one(seq_items):
    query_rot, key_rot, value_low, length = seq_items
    grouped = query_rot.reshape(LEN, KV_HEADS, HEADS // KV_HEADS, HEAD_DIM)
    scores = jnp.einsum('ikge,jke->kgij', grouped, key_rot, precision=HIGHEST_PRECISION) * (1.0 / math.sqrt(HEAD_DIM))
    scores = low_back(scores)
    query_pos = jnp.arange(LEN)[:, None]
    key_pos = jnp.arange(LEN)[None, :]
    visible = (key_pos <= query_pos) & (key_pos < length)
    masked = jnp.where(visible, scores, NEG_FILL)
    row_max = lax.optimization_barrier(jnp.max(masked, axis=-1, keepdims=True))
    exponent = jnp.exp(masked - row_max)
    probs = exponent / lax.optimization_barrier(jnp.sum(exponent, axis=-1, keepdims=True))
    mixed_rows = jnp.einsum('kgij,jke->ikge', low(probs), value_low, precision=HIGHEST_PRECISION)
    return mixed_rows.reshape(LEN, HEADS * HEAD_DIM)

def layer(params, hidden, positions_now, lengths_now):
    query_w, keyval_w, output_w, gains, bias_q, bias_kv, gate_w, up_w, down_w = params
    batch_count = hidden.shape[0]
    normed_one = low(norm_apply(hidden, gains[0]))
    query_lin = low_back(jnp.einsum('bld,de->ble', normed_one, query_w, precision=HIGHEST_PRECISION) + bias_q.reshape(-1))
    keyval_lin = low_back(jnp.einsum('bld,de->ble', normed_one, keyval_w, precision=HIGHEST_PRECISION) + bias_kv.reshape(-1))
    query_lin = query_lin.reshape(batch_count, LEN, HEADS, HEAD_DIM)
    keyval_lin = keyval_lin.reshape(batch_count, LEN, KV_HEADS, 2, HEAD_DIM)
    cosine, sine_part = rope_tables(positions_now, HEAD_DIM)
    cosine = cosine[:, :, None, :]
    sine_part = sine_part[:, :, None, :]
    query_rot = low(rotate(query_lin, cosine, sine_part))
    key_rot = low(rotate(keyval_lin[:, :, :, 0, :], cosine, sine_part))
    value_low = low(keyval_lin[:, :, :, 1, :])
    mixed = lax.map(jax.checkpoint(attend_one), (query_rot, key_rot, value_low, lengths_now))
    mixed = low(low_back(mixed))
    branch = low_back(jnp.einsum('ble,ed->bld', mixed, output_w, precision=HIGHEST_PRECISION))
    middle = hidden + branch
    normed_two = low(norm_apply(middle, gains[1]))
    gate_lin = low_back(jnp.einsum('bld,df->blf', normed_two, gate_w, precision=HIGHEST_PRECISION))
    up_lin = low_back(jnp.einsum('bld,df->blf', normed_two, up_w, precision=HIGHEST_PRECISION))
    hidden_act = low(jax.nn.silu(gate_lin) * up_lin)
    return middle + low_back(jnp.einsum('blf,fd->bld', hidden_act, down_w, precision=HIGHEST_PRECISION))

def reference(hidden_in, cotangent, seq_lengths, positions, permutation, query_weight, keyval_weight, output_weight, norm_gains, bias_query, bias_keyval, gate_weight, up_weight, down_weight):
    params = tuple((weight_now.astype(jnp.float32) for weight_now in (query_weight, keyval_weight, output_weight, norm_gains, bias_query, bias_keyval, gate_weight, up_weight, down_weight)))
    group_size = math.gcd(SEQS, max(1, 4096 // LEN))
    step_count = SEQS // group_size
    slot_order = permutation.reshape(step_count, group_size)
    targets = cotangent.reshape(step_count, group_size, LEN, D)
    zero_grads = tuple((jnp.zeros_like(weight_now) for weight_now in params))

    def advance(totals, step_items):
        slot_now, grad_out = step_items
        hidden = hidden_in[slot_now].astype(jnp.float32)
        positions_now = positions[slot_now]
        lengths_now = seq_lengths[slot_now]
        result, pullback = jax.vjp(lambda weights, inputs: layer(weights, inputs, positions_now, lengths_now), params, hidden)
        weight_grads, input_grads = pullback(grad_out.astype(jnp.float32))
        totals = tuple((total_now + grad_now for total_now, grad_now in zip(totals, weight_grads)))
        return (totals, (result.astype(jnp.bfloat16), input_grads.astype(jnp.bfloat16)))
    totals, (outs_work, grads_work) = lax.scan(advance, zero_grads, (slot_order, targets))
    block_out = jnp.zeros((SEQS, LEN, D), jnp.bfloat16).at[permutation].set(outs_work.reshape(SEQS, LEN, D))
    input_grad = jnp.zeros((SEQS, LEN, D), jnp.bfloat16).at[permutation].set(grads_work.reshape(SEQS, LEN, D))
    return (block_out, input_grad, totals[0], totals[1], totals[2], totals[3], totals[4], totals[5], totals[6], totals[7], totals[8])
```

```python
import functools
import math

import jax
import jax.numpy as jnp
from jax import lax
from jax.experimental import pallas as pl
from jax.experimental.pallas import tpu as pltpu
from jax.sharding import PartitionSpec as P

EPS = 1e-06
ROPE_BASE = 10000.0
NEG_FILL = -1e30
LOW = jnp.bfloat16
WIDE = jnp.float32
DEAL_SHIFT = (0, 2, 1, 3)


def from_partner(value, axis, apart):
    pairs = [(source, source ^ apart) for source in range(lax.axis_size(axis))]
    return lax.ppermute(value, axis, pairs)


def product(left_side, right_side, kind=WIDE):
    return jnp.dot(left_side, right_side, preferred_element_type=WIDE).astype(kind)


def contract_rows(left_side, right_side, kind=WIDE):
    return lax.dot_general(
        left_side, right_side, (((0,), (0,)), ((), ())), preferred_element_type=WIDE
    ).astype(kind)


def contract_cols(left_side, right_side, kind=WIDE):
    return lax.dot_general(
        left_side, right_side, (((1,), (1,)), ((), ())), preferred_element_type=WIDE
    ).astype(kind)


def norm_backward(values, scale_inv, gain_row, upstream):
    scaled = gain_row * upstream
    inner_mean = jnp.mean(values * scaled, axis=-1, keepdims=True)
    grad_in = scale_inv * scaled - values * (scale_inv * scale_inv * scale_inv) * inner_mean
    gain_grad = jnp.sum(upstream * values * scale_inv, axis=0)
    return (grad_in, gain_grad)


def spread_rows(own):
    far = from_partner(own, "tp", 2)
    near = from_partner(own, "tp", 1)
    cross = from_partner(far, "tp", 1)
    return (own, near, far, cross)


def collect_rows(parts):
    wide = parts[2].astype(WIDE) + from_partner(parts[3], "tp", 1).astype(WIDE)
    far = from_partner(wide.astype(LOW), "tp", 2)
    near = from_partner(parts[1], "tp", 1)
    return parts[0].astype(WIDE) + near.astype(WIDE) + far.astype(WIDE)


def interleave(own, other, ctx_rank):
    first = jnp.where(ctx_rank == 0, own, other)
    second = jnp.where(ctx_rank == 0, other, own)
    return (first, second)


def gather_small(shard, ctx_rank):
    if lax.axis_size("ctx") != 2:
        return lax.all_gather(shard, ("fsdp", "ctx"), axis=0, tiled=True)
    both = jnp.stack(interleave(shard, from_partner(shard, "ctx", 1), ctx_rank), axis=0)
    full = lax.all_gather(both, "fsdp", axis=0, tiled=False)
    return full.reshape(-1, shard.shape[1])


def gather_large(shard, ctx_rank):
    if lax.axis_size("ctx") != 2:
        return lax.all_gather(shard, ("fsdp", "ctx"), axis=0, tiled=True)
    held = lax.all_gather(shard, "fsdp", axis=0, tiled=False)
    other = from_partner(held, "ctx", 1)
    return jnp.stack(interleave(held, other, ctx_rank), axis=1).reshape(-1, shard.shape[1])


def scatter_sum(grad, ctx_rank, kind):
    fsdp_count, ctx_count = lax.axis_size("fsdp"), lax.axis_size("ctx")
    rows, cols = grad.shape
    blocks = grad.reshape(fsdp_count, ctx_count, rows // (fsdp_count * ctx_count), cols)
    if ctx_count == 2:
        kept = lax.dynamic_index_in_dim(blocks, ctx_rank, 1, keepdims=False)
        sent = lax.dynamic_index_in_dim(blocks, 1 - ctx_rank, 1, keepdims=False)
        got = from_partner(sent, "ctx", 1)
        held = (kept.astype(WIDE) + got.astype(WIDE)).astype(kind)
    else:
        swapped = jnp.swapaxes(blocks, 0, 1).reshape(rows, cols)
        held = lax.psum_scatter(swapped, "ctx", scatter_dimension=0, tiled=True)
    held = held.reshape(rows // ctx_count, cols)
    return lax.psum_scatter(held, "fsdp", scatter_dimension=0, tiled=True)


def turn(values, cosine, sine_signed):
    return values * cosine + pltpu.roll(values, values.shape[-1] // 2, 1) * sine_signed


def turn_back(values, cosine, sine_signed):
    return values * cosine - pltpu.roll(values, values.shape[-1] // 2, 1) * sine_signed


def project_kernel(
    heads, head_dim, x0, x1, x2, x3, gain, weight, bias, cosine, sine, h_out, q_out, k_out, v_out
):
    slot = pl.program_id(0)

    def run(x_ref):
        x = x_ref[...].astype(WIDE)
        scale_inv = lax.rsqrt(jnp.mean(x * x, axis=-1, keepdims=True) + EPS)
        normed = (x * scale_inv * gain[...]).astype(LOW)
        h_out[0] = normed
        lin = jnp.dot(normed, weight[...], preferred_element_type=WIDE) + bias[...]
        cos, sin = cosine[0], sine[0]
        for h in range(heads + 1):
            part = turn(lin[:, h * head_dim : (h + 1) * head_dim], cos, sin).astype(LOW)
            if h < heads:
                q_out[0, :, h * head_dim : (h + 1) * head_dim] = part
            else:
                k_out[0] = part
        v_out[0] = lin[:, (heads + 1) * head_dim :].astype(LOW)

    for r, x_ref in enumerate((x0, x1, x2, x3)):
        pl.when(slot == r)(functools.partial(run, x_ref))


def project(rows, gain, weight, bias, cosine, sine, heads, head_dim):
    length, width = rows[0].shape
    count = len(rows)
    cols = (heads + 2) * head_dim
    whole = lambda *shape: pl.BlockSpec(shape, lambda s: (0,) * len(shape))
    by_slot = lambda *shape: pl.BlockSpec((1, *shape), lambda s: (s,) + (0,) * len(shape))
    return pl.pallas_call(
        functools.partial(project_kernel, heads, head_dim),
        grid=(count,),
        in_specs=[whole(length, width)] * count
        + [whole(1, width), whole(width, cols), whole(1, cols)]
        + [by_slot(length, head_dim)] * 2,
        out_specs=[
            by_slot(length, width),
            by_slot(length, heads * head_dim),
            by_slot(length, head_dim),
            by_slot(length, head_dim),
        ],
        out_shape=[
            jax.ShapeDtypeStruct((count, length, width), LOW),
            jax.ShapeDtypeStruct((count, length, heads * head_dim), LOW),
            jax.ShapeDtypeStruct((count, length, head_dim), LOW),
            jax.ShapeDtypeStruct((count, length, head_dim), LOW),
        ],
        compiler_params=pltpu.CompilerParams(vmem_limit_bytes=56 << 20),
        cost_estimate=pl.CostEstimate(
            flops=2 * count * length * width * cols,
            bytes_accessed=count * length * (2 * width + cols) * 2 + width * cols * 2,
            transcendentals=0,
        ),
    )(*rows, gain, weight, bias, cosine, sine)


def row_blocks(length):
    return [(i, min(256, length)) for i in range(0, length, min(256, length))]


def key_biases(length, offset, start, rows, past, keys):
    past_pos = lax.broadcasted_iota(jnp.int32, (1, past), 1)
    past_bias = jnp.where((past_pos < offset) & (past_pos < length), 0.0, NEG_FILL)
    query_pos = offset + start + lax.broadcasted_iota(jnp.int32, (rows, keys), 0)
    own_pos = offset + lax.broadcasted_iota(jnp.int32, (rows, keys), 1)
    own_bias = jnp.where((own_pos <= query_pos) & (own_pos < length), 0.0, NEG_FILL)
    return past_bias, own_bias


def dot_cols(left, right):
    return lax.dot_general(left, right, (((1,), (1,)), ((), ())), preferred_element_type=WIDE)


def dot_rows(left, right):
    return lax.dot_general(left, right, (((0,), (0,)), ((), ())), preferred_element_type=WIDE)


def attend_kernel(heads, head_dim, scale, info, q, k_past, v_past, k_own, v_own, out, lse):
    slot = pl.program_id(0)
    length, offset = info[slot], info[pl.num_programs(0)]
    past = k_past.shape[1]
    for start, rows in row_blocks(q.shape[1]):
        keys = start + rows
        past_bias, own_bias = key_biases(length, offset, start, rows, past, keys)
        here = slice(start, start + rows)
        for h in range(heads):
            cols = slice(h * head_dim, (h + 1) * head_dim)
            query = q[0, here, cols]
            s_past = dot_cols(query, k_past[0]) * scale + past_bias
            s_own = dot_cols(query, k_own[0, :keys]) * scale + own_bias
            top = jnp.maximum(
                jnp.max(s_past, axis=1, keepdims=True), jnp.max(s_own, axis=1, keepdims=True)
            )
            e_past, e_own = jnp.exp(s_past - top), jnp.exp(s_own - top)
            total = jnp.sum(e_past, axis=1, keepdims=True) + jnp.sum(e_own, axis=1, keepdims=True)
            inverse = 1.0 / total
            mixed = jnp.dot(
                (e_past * inverse).astype(LOW), v_past[0], preferred_element_type=WIDE
            ) + jnp.dot((e_own * inverse).astype(LOW), v_own[0, :keys], preferred_element_type=WIDE)
            out[0, here, cols] = mixed.astype(LOW)
            lse[0, here, h : h + 1] = top + jnp.log(total)


def attend_forward(info, q, k_past, v_past, k_own, v_own, heads, head_dim, scale):
    count, length, width = q.shape
    past = k_past.shape[1]
    by_slot = lambda *shape: pl.BlockSpec((1, *shape), lambda s, info: (s,) + (0,) * len(shape))
    keys = count * length * (past + length) * heads
    return pl.pallas_call(
        functools.partial(attend_kernel, heads, head_dim, scale),
        grid_spec=pltpu.PrefetchScalarGridSpec(
            num_scalar_prefetch=1,
            grid=(count,),
            in_specs=[
                by_slot(length, width),
                by_slot(past, head_dim),
                by_slot(past, head_dim),
                by_slot(length, head_dim),
                by_slot(length, head_dim),
            ],
            out_specs=[by_slot(length, width), by_slot(length, 128)],
        ),
        out_shape=[
            jax.ShapeDtypeStruct((count, length, width), LOW),
            jax.ShapeDtypeStruct((count, length, 128), WIDE),
        ],
        compiler_params=pltpu.CompilerParams(vmem_limit_bytes=56 << 20),
        cost_estimate=pl.CostEstimate(
            flops=4 * keys * head_dim, bytes_accessed=4 * count * length * width, transcendentals=keys
        ),
    )(info, q, k_past, v_past, k_own, v_own)


def attend_back_kernel(
    heads,
    head_dim,
    scale,
    info,
    q,
    k_past,
    v_past,
    k_own,
    v_own,
    grad,
    lse,
    cosine,
    sine,
    dq_out,
    mine_past,
    mine_own,
    other_past,
    other_own,
    dk_past,
    dk_own,
    dv_past,
    dv_own,
):
    slot = pl.program_id(0)
    length, offset = info[slot], info[pl.num_programs(0)]
    parity = info[pl.num_programs(0) + 1]
    past = k_past.shape[1]
    for total in (dk_past, dk_own, dv_past, dv_own):
        total[...] = jnp.zeros_like(total)
    for start, rows in row_blocks(q.shape[1]):
        keys = start + rows
        past_bias, own_bias = key_biases(length, offset, start, rows, past, keys)
        here = slice(start, start + rows)
        cos, sin = cosine[0, here], sine[0, here]
        for h in range(heads):
            cols = slice(h * head_dim, (h + 1) * head_dim)
            query, upstream = q[0, here, cols], grad[0, here, cols]
            log_total = lse[0, here, h : h + 1]
            p_past = jnp.exp(dot_cols(query, k_past[0]) * scale + past_bias - log_total)
            p_own = jnp.exp(dot_cols(query, k_own[0, :keys]) * scale + own_bias - log_total)
            g_past = dot_cols(upstream, v_past[0])
            g_own = dot_cols(upstream, v_own[0, :keys])
            row_dot = jnp.sum(p_past * g_past, axis=1, keepdims=True) + jnp.sum(
                p_own * g_own, axis=1, keepdims=True
            )
            s_past = (p_past * (g_past - row_dot)).astype(LOW)
            s_own = (p_own * (g_own - row_dot)).astype(LOW)
            dq = (
                jnp.dot(s_past, k_past[0], preferred_element_type=WIDE)
                + jnp.dot(s_own, k_own[0, :keys], preferred_element_type=WIDE)
            ) * scale
            dq_out[0, here, cols] = turn_back(dq, cos, sin).astype(LOW)
            dk_past[...] += dot_rows(s_past, query)
            dk_own[:keys] += dot_rows(s_own, query)
            dv_past[...] += dot_rows(p_past.astype(LOW), upstream)
            dv_own[:keys] += dot_rows(p_own.astype(LOW), upstream)

    @pl.when(parity == 0)
    def _():
        mine_past[0] = dk_past[...] * scale
        mine_own[0] = dk_own[...] * scale
        other_past[0] = dv_past[...]
        other_own[0] = dv_own[...]

    @pl.when(parity != 0)
    def _():
        mine_past[0] = dv_past[...]
        mine_own[0] = dv_own[...]
        other_past[0] = dk_past[...] * scale
        other_own[0] = dk_own[...] * scale


def attend_backward(
    info, q, k_past, v_past, k_own, v_own, grad, lse, cosine, sine, heads, head_dim, scale
):
    count, length, width = q.shape
    past = k_past.shape[1]
    by_slot = lambda *shape: pl.BlockSpec((1, *shape), lambda s, info: (s,) + (0,) * len(shape))
    keys = count * length * (past + length) * heads
    return pl.pallas_call(
        functools.partial(attend_back_kernel, heads, head_dim, scale),
        grid_spec=pltpu.PrefetchScalarGridSpec(
            num_scalar_prefetch=1,
            grid=(count,),
            in_specs=[
                by_slot(length, width),
                by_slot(past, head_dim),
                by_slot(past, head_dim),
                by_slot(length, head_dim),
                by_slot(length, head_dim),
                by_slot(length, width),
                by_slot(length, 128),
                by_slot(length, head_dim),
                by_slot(length, head_dim),
            ],
            out_specs=[
                by_slot(length, width),
                by_slot(past, head_dim),
                by_slot(length, head_dim),
                by_slot(past, head_dim),
                by_slot(length, head_dim),
            ],
            scratch_shapes=[
                pltpu.VMEM((past, head_dim), WIDE),
                pltpu.VMEM((length, head_dim), WIDE),
                pltpu.VMEM((past, head_dim), WIDE),
                pltpu.VMEM((length, head_dim), WIDE),
            ],
        ),
        out_shape=[
            jax.ShapeDtypeStruct((count, length, width), LOW),
            jax.ShapeDtypeStruct((count, past, head_dim), WIDE),
            jax.ShapeDtypeStruct((count, length, head_dim), WIDE),
            jax.ShapeDtypeStruct((count, past, head_dim), WIDE),
            jax.ShapeDtypeStruct((count, length, head_dim), WIDE),
        ],
        compiler_params=pltpu.CompilerParams(vmem_limit_bytes=56 << 20),
        cost_estimate=pl.CostEstimate(
            flops=10 * keys * head_dim, bytes_accessed=8 * count * length * width, transcendentals=keys
        ),
    )(info, q, k_past, v_past, k_own, v_own, grad, lse, cosine, sine)


def local(
    hidden_in,
    cotangent,
    seq_lengths,
    positions,
    permutation,
    query_weight,
    keyval_weight,
    output_weight,
    norm_gains,
    bias_query,
    bias_keyval,
    gate_weight,
    up_weight,
    down_weight,
):
    group_rank = lax.axis_index("fsdp")
    ctx_rank = lax.axis_index("ctx")
    tensor_rank = lax.axis_index("tp")
    fsdp_count = lax.axis_size("fsdp")
    ctx_count = lax.axis_size("ctx")
    tensor_count = lax.axis_size("tp")
    seq_grp, local_len, model_width = hidden_in.shape
    heads, head_dim = bias_query.shape
    keyval_heads = bias_keyval.shape[0] // 2
    assert seq_grp == tensor_count == fsdp_count == len(DEAL_SHIFT)
    token_count = seq_grp * local_len
    scale = 1.0 / math.sqrt(head_dim)
    offset = ctx_rank * local_len
    head_pair = tensor_rank // (tensor_count // keyval_heads)
    parity = tensor_rank % 2
    shifts = jnp.array(DEAL_SHIFT, jnp.int32)

    table = permutation.reshape(fsdp_count, seq_grp)
    far_group = lax.rem(group_rank + shifts[tensor_rank], fsdp_count)
    far_row = lax.dynamic_index_in_dim(table, far_group, 0, keepdims=False)
    leaving = jnp.sum(jnp.where(far_row // seq_grp == group_rank, far_row - group_rank * seq_grp, 0))
    own_row = lax.dynamic_index_in_dim(table, group_rank, 0, keepdims=False)
    slot_now, seq_now, home_now = [], [], []
    for r in range(seq_grp):
        shift = shifts[tensor_rank ^ r]
        source = lax.rem(group_rank - shift + fsdp_count, fsdp_count)
        hit = own_row // seq_grp == source
        slot_now.append(jnp.sum(jnp.where(hit, jnp.arange(seq_grp), 0)))
        seq_now.append(jnp.sum(jnp.where(hit, own_row, 0)))
        target = lax.rem(group_rank + shift, fsdp_count)
        target_row = lax.dynamic_index_in_dim(table, target, 0, keepdims=False)
        home_now.append(
            jnp.sum(jnp.where(target_row // seq_grp == group_rank, target_row - group_rank * seq_grp, 0))
        )
    there = [
        (f * tensor_count + t, (f + DEAL_SHIFT[t]) % fsdp_count * tensor_count + t)
        for f in range(fsdp_count)
        for t in range(tensor_count)
    ]
    back = [(target, source) for source, target in there]

    outgoing = lax.dynamic_index_in_dim(hidden_in, leaving, 0, keepdims=False)
    own_in = lax.ppermute(outgoing, ("fsdp", "tp"), there)
    head_width = 2 * head_dim
    small = jnp.concatenate(
        [
            query_weight,
            lax.dynamic_slice_in_dim(keyval_weight, head_pair * head_width, head_width, axis=1),
            output_weight.T,
            jnp.pad(norm_gains.T, ((0, 0), (0, 128 - norm_gains.shape[0]))),
        ],
        axis=1,
    )
    small_full = gather_small(small, ctx_rank)
    down_full = gather_large(down_weight.T, ctx_rank)
    gate_full = gather_large(gate_weight, ctx_rank)
    up_full = gather_large(up_weight, ctx_rank)
    query_cols = heads * head_dim
    project_full = small_full[:, : query_cols + head_width]
    output_full = small_full[:, query_cols + head_width : 2 * query_cols + head_width]
    gains_now = small_full[:, 2 * query_cols + head_width :][:, :2].astype(WIDE).T
    own_weight = lax.dynamic_slice_in_dim(
        project_full, query_cols + parity * head_dim, head_dim, axis=1
    )
    back_full = jnp.concatenate([project_full[:, :query_cols], own_weight], axis=1)

    lengths_now = jnp.stack([seq_lengths[s] for s in seq_now])
    info = jnp.concatenate([lengths_now, jnp.stack([offset, parity])]).astype(jnp.int32)
    positions_now = jnp.stack(
        [lax.dynamic_index_in_dim(positions, s, 0, keepdims=False) for s in seq_now]
    )
    lane = jnp.arange(head_dim)
    frequency = 1.0 / ROPE_BASE ** (
        (lane % (head_dim // 2)).astype(WIDE) * 2.0 / head_dim
    )
    angles = positions_now.astype(WIDE)[..., None] * frequency
    cosine = jnp.cos(angles)
    sine = jnp.sin(angles) * jnp.where(lane < head_dim // 2, -1.0, 1.0)
    grad_rows = jnp.concatenate(
        [lax.dynamic_index_in_dim(cotangent, s, 0, keepdims=False) for s in slot_now], axis=0
    )

    bias_head = lax.dynamic_slice_in_dim(bias_keyval, head_pair * 2, 2, axis=0)
    bias_row = jnp.concatenate([bias_query.reshape(1, -1), bias_head.reshape(1, -1)], axis=1).astype(WIDE)
    rows_in = spread_rows(own_in)
    normed_one, query_rot, key_own, value_own = project(
        rows_in, gains_now[0:1], project_full, bias_row, cosine, sine, heads, head_dim
    )
    if ctx_count == 2:
        key_past, value_past = lax.ppermute((key_own, value_own), "ctx", [(0, 1)])
    else:
        key_past = lax.all_gather(key_own, "ctx", axis=1, tiled=True)
        value_past = lax.all_gather(value_own, "ctx", axis=1, tiled=True)
    mixed, lse = attend_forward(
        info, query_rot, key_past, value_past, key_own, value_own, heads, head_dim, scale
    )
    in_share = own_in.astype(WIDE)

    def row_parts(far_part, near_part):
        far_part = far_part.reshape(2, local_len, model_width)
        near_part = near_part.reshape(2, local_len, model_width)
        return (near_part[0], near_part[1], far_part[0], far_part[1])

    def halves(value):
        half = token_count // 2
        return value[half:], value[:half]

    mixed_flat = mixed.reshape(token_count, query_cols)
    attn_parts = row_parts(*[contract_cols(m, output_full, LOW) for m in halves(mixed_flat)])
    middle_share = in_share + collect_rows(attn_parts)
    inv_two = lax.rsqrt(jnp.mean(middle_share * middle_share, axis=-1, keepdims=True) + EPS)
    normed_share = (middle_share * inv_two * gains_now[1]).astype(LOW)
    normed_two = jnp.concatenate(spread_rows(normed_share), axis=0)

    grad_hidden = product(grad_rows, down_full)
    gate_lin = product(normed_two, gate_full)
    up_lin = product(normed_two, up_full)
    gate_sigmoid = jax.nn.sigmoid(gate_lin)
    silu_gate = gate_lin * gate_sigmoid
    hidden_act = (silu_gate * up_lin).astype(LOW)
    grad_gate = (
        grad_hidden * up_lin * gate_sigmoid * (1.0 + gate_lin * (1.0 - gate_sigmoid))
    ).astype(LOW)
    grad_up = (grad_hidden * silu_gate).astype(LOW)
    back_parts = row_parts(
        *[
            (contract_cols(g, gate_full) + contract_cols(u, up_full)).astype(LOW)
            for g, u in zip(halves(grad_gate), halves(grad_up))
        ]
    )
    grad_two_share = collect_rows(back_parts)
    down_grad = scatter_sum(contract_rows(grad_rows, hidden_act, LOW), ctx_rank, LOW)
    gate_grad = scatter_sum(contract_rows(normed_two, grad_gate, LOW), ctx_rank, LOW)
    up_grad = scatter_sum(contract_rows(normed_two, grad_up, LOW), ctx_rank, LOW)
    mlp_parts = row_parts(*[contract_cols(a, down_full, LOW) for a in halves(hidden_act)])
    block_share = (middle_share + collect_rows(mlp_parts)).astype(LOW)

    grad_norm_two, gain_two = norm_backward(middle_share, inv_two, gains_now[1], grad_two_share)
    grad_middle = grad_rows[:local_len].astype(WIDE) + grad_norm_two
    grad_branch = jnp.concatenate(spread_rows(grad_middle.astype(LOW)), axis=0)
    grad_mixed = product(grad_branch, output_full, LOW)
    output_grad = contract_rows(grad_branch, mixed_flat, LOW)

    grad_query, mine_past, mine_own, other_past, other_own = attend_backward(
        info,
        query_rot,
        key_past,
        value_past,
        key_own,
        value_own,
        grad_mixed.reshape(seq_grp, local_len, query_cols),
        lse,
        cosine,
        sine,
        heads,
        head_dim,
        scale,
    )
    swap = lambda value: jnp.stack([value[r ^ 1] for r in range(seq_grp)])
    got_past, got_own = from_partner((other_past, other_own), "tp", 1)
    past_sum = mine_past + swap(got_past)
    own_sum = mine_own + swap(got_own)
    if ctx_count == 2:
        own_sum = own_sum + lax.ppermute(past_sum.astype(LOW), "ctx", [(1, 0)]).astype(WIDE)
    else:
        own_sum = own_sum + lax.psum_scatter(past_sum, "ctx", scatter_dimension=1, tiled=True)
    half_lanes = head_dim // 2
    turned = own_sum * cosine - jnp.roll(own_sum, half_lanes, axis=-1) * sine
    own_grad = jnp.where(parity == 0, turned, own_sum).astype(LOW).reshape(token_count, head_dim)
    line_grad = jnp.concatenate([grad_query.reshape(token_count, query_cols), own_grad], axis=1)
    normed_flat = normed_one.reshape(token_count, model_width)
    line_weight_grad = contract_rows(normed_flat, line_grad, LOW)
    bias_grad = jnp.sum(line_grad.astype(WIDE), axis=0)
    line_parts = row_parts(*[contract_cols(g, back_full, LOW) for g in halves(line_grad)])
    grad_one_share = collect_rows(line_parts)
    inv_one = lax.rsqrt(jnp.mean(in_share * in_share, axis=-1, keepdims=True) + EPS)
    grad_norm_one, gain_one = norm_backward(in_share, inv_one, gains_now[0], grad_one_share)
    input_share = (grad_middle + grad_norm_one).astype(LOW)

    def go_home(share):
        rows = spread_rows(lax.ppermute(share, ("fsdp", "tp"), back))
        out = jnp.zeros((seq_grp, local_len, model_width), LOW)
        for home, row in zip(home_now, rows):
            out = lax.dynamic_update_index_in_dim(out, row, home, 0)
        return out

    block_out = go_home(block_share)
    input_grad = go_home(input_share)

    attn_grad = scatter_sum(jnp.concatenate([line_weight_grad, output_grad], axis=1), ctx_rank, LOW)
    gain_grad = jnp.stack([gain_one, gain_two], axis=1)
    gain_grad = gain_grad + from_partner(gain_grad, "tp", 1)
    gain_grad = gain_grad + from_partner(gain_grad, "tp", 2)
    shards = fsdp_count * ctx_count
    bias_cols = bias_grad.reshape(heads + 1, shards, head_dim // shards)
    bias_cols = jnp.transpose(bias_cols, (1, 2, 0))
    bias_cols = jnp.pad(bias_cols, ((0, 0), (0, (model_width - head_dim) // shards), (0, 0)))
    tiny = jnp.concatenate([gain_grad, bias_cols.reshape(model_width, heads + 1)], axis=1)
    tiny = jnp.pad(tiny, ((0, 0), (0, 8 - tiny.shape[1])))
    tiny_grad = scatter_sum(tiny, ctx_rank, WIDE)
    share = head_dim // shards
    return (
        block_out,
        input_grad,
        attn_grad[:, :query_cols].astype(WIDE),
        attn_grad[:, query_cols : query_cols + head_dim].astype(WIDE),
        attn_grad[:, query_cols + head_dim :].astype(WIDE).T,
        tiny_grad[:, :2].T,
        tiny_grad[:share, 2 : 2 + heads].T,
        tiny_grad[:share, 2 + heads : 3 + heads].T,
        gate_grad.astype(WIDE),
        up_grad.astype(WIDE),
        down_grad.astype(WIDE).T,
    )


def solution(mesh):
    placed = (
        P("fsdp", "ctx", None),
        P("fsdp", "ctx", None),
        P(),
        P(None, "ctx"),
        P(),
        P(("fsdp", "ctx"), "tp"),
        P(("fsdp", "ctx"), None),
        P("tp", ("fsdp", "ctx")),
        P(None, ("fsdp", "ctx")),
        P("tp", None),
        P(),
        P(("fsdp", "ctx"), "tp"),
        P(("fsdp", "ctx"), "tp"),
        P("tp", ("fsdp", "ctx")),
    )
    return jax.shard_map(
        local,
        mesh=mesh,
        in_specs=placed,
        out_specs=(
            P("fsdp", "ctx", None),
            P("fsdp", "ctx", None),
            P(("fsdp", "ctx"), "tp"),
            P(("fsdp", "ctx"), "tp"),
            P("tp", ("fsdp", "ctx")),
            P(None, ("fsdp", "ctx")),
            P("tp", ("fsdp", "ctx")),
            P("tp", ("fsdp", "ctx")),
            P(("fsdp", "ctx"), "tp"),
            P(("fsdp", "ctx"), "tp"),
            P("tp", ("fsdp", "ctx")),
        ),
        check_vma=False,
    )
```

```python
import functools
import math

import jax
import jax.numpy as jnp
from jax import lax
from jax.experimental import pallas as pl
from jax.experimental.pallas import tpu as pltpu
from jax.sharding import PartitionSpec as P

EPS = 1e-06
ROPE_BASE = 10000.0
NEG_FILL = -1e30
LOW = jnp.bfloat16
WIDE = jnp.float32
DEAL_SHIFT = (0, 2, 1, 3)


def from_partner(value, axis, apart):
    pairs = [(source, source ^ apart) for source in range(lax.axis_size(axis))]
    return lax.ppermute(value, axis, pairs)


def product(left_side, right_side, kind=WIDE):
    return jnp.dot(left_side, right_side, preferred_element_type=WIDE).astype(kind)


def contract_rows(left_side, right_side, kind=WIDE):
    return lax.dot_general(
        left_side, right_side, (((0,), (0,)), ((), ())), preferred_element_type=WIDE
    ).astype(kind)


def contract_cols(left_side, right_side, kind=WIDE):
    return lax.dot_general(
        left_side, right_side, (((1,), (1,)), ((), ())), preferred_element_type=WIDE
    ).astype(kind)


def norm_backward(values, scale_inv, gain_row, upstream):
    scaled = gain_row * upstream
    inner_mean = jnp.mean(values * scaled, axis=-1, keepdims=True)
    grad_in = scale_inv * scaled - values * (scale_inv * scale_inv * scale_inv) * inner_mean
    gain_grad = jnp.sum(upstream * values * scale_inv, axis=0)
    return (grad_in, gain_grad)


def after(value, *earlier):
    return lax.optimization_barrier((value, *earlier))[0]


def collect_far(far_part, cross_part):
    wide = far_part.astype(WIDE) + from_partner(cross_part, "tp", 1).astype(WIDE)
    return wide.astype(LOW)


def units_split():
    return lax.axis_size("ctx") == 2


def all_rows(shard):
    return lax.all_gather(shard, "fsdp", axis=0, tiled=True)


def scatter_ctx(blocks, ctx_rank):
    kept = lax.dynamic_index_in_dim(blocks, ctx_rank, 1, keepdims=False)
    sent = lax.dynamic_index_in_dim(blocks, 1 - ctx_rank, 1, keepdims=False)
    return kept, sent


def scatter_sum(grad, ctx_rank, kind, *earlier):
    fsdp_count, ctx_count = lax.axis_size("fsdp"), lax.axis_size("ctx")
    rows, cols = grad.shape
    blocks = grad.reshape(fsdp_count, ctx_count, rows // (fsdp_count * ctx_count), cols)
    if ctx_count == 2:
        kept, sent = scatter_ctx(blocks, ctx_rank)
        got = from_partner(sent, "ctx", 1)
        held = (after(kept, *earlier).astype(WIDE) + got.astype(WIDE)).astype(kind)
    else:
        swapped = jnp.swapaxes(blocks, 0, 1).reshape(rows, cols)
        held = lax.psum_scatter(swapped, "ctx", scatter_dimension=0, tiled=True)
    held = held.reshape(rows // ctx_count, cols)
    return lax.psum_scatter(held, "fsdp", scatter_dimension=0, tiled=True)


def whole_spec(*shape, once=False):
    mode = {"pipeline_mode": pl.Buffered(1)} if once else {}
    return pl.BlockSpec(shape, lambda *_: (0,) * len(shape), **mode)


def gate_kernel(count, *refs):
    slot = pl.program_id(0)
    weight, lin, stacked = refs[count:]

    def run(x):
        value = x[...]
        stacked[...] = value
        lin[...] = jnp.dot(value, weight[...], preferred_element_type=WIDE).astype(LOW)

    for r in range(count):
        pl.when(slot == r)(functools.partial(run, refs[r]))


def gate_rows(rows, weight):
    length, width = rows[0].shape
    count, cols = len(rows), weight.shape[1]
    return pl.pallas_call(
        functools.partial(gate_kernel, count),
        grid=(count,),
        in_specs=[whole_spec(length, width, once=True)] * count
        + [whole_spec(width, cols, once=True)],
        out_specs=[
            pl.BlockSpec((length, cols), lambda s: (s, 0)),
            pl.BlockSpec((length, width), lambda s: (s, 0)),
        ],
        out_shape=[
            jax.ShapeDtypeStruct((count * length, cols), LOW),
            jax.ShapeDtypeStruct((count * length, width), LOW),
        ],
        compiler_params=pltpu.CompilerParams(vmem_limit_bytes=60 << 20),
        cost_estimate=pl.CostEstimate(
            flops=2 * count * length * width * cols,
            bytes_accessed=2 * (count * length * (2 * width + cols) + width * cols),
            transcendentals=0,
        ),
    )(*rows, weight)


def units_kernel(h, up, gate, grad, hid, grad_gate, grad_up):
    up_lin = jnp.dot(h[...], up[...], preferred_element_type=WIDE)
    gate_lin = gate[...].astype(WIDE)
    grad_hidden = grad[...].astype(WIDE)
    sigmoid = 1.0 / (1.0 + jnp.exp(-gate_lin))
    silu = gate_lin * sigmoid
    hid[...] = (silu * up_lin).astype(LOW)
    grad_gate[...] = (grad_hidden * up_lin * sigmoid * (1.0 + gate_lin * (1.0 - sigmoid))).astype(LOW)
    grad_up[...] = (grad_hidden * silu).astype(LOW)


def hidden_units(h, up, gate_lin, grad_hidden):
    tokens, width = h.shape
    cols = up.shape[1]
    step = math.gcd(512, tokens)
    by_row = lambda n: pl.BlockSpec((step, n), lambda i: (i, 0))
    return pl.pallas_call(
        units_kernel,
        grid=(tokens // step,),
        in_specs=[by_row(width), whole_spec(width, cols, once=True), by_row(cols), by_row(cols)],
        out_specs=[by_row(cols)] * 3,
        out_shape=[jax.ShapeDtypeStruct((tokens, cols), LOW)] * 3,
        compiler_params=pltpu.CompilerParams(vmem_limit_bytes=60 << 20),
        cost_estimate=pl.CostEstimate(
            flops=2 * tokens * width * cols,
            bytes_accessed=2 * (tokens * width + width * cols + 5 * tokens * cols),
            transcendentals=tokens * cols,
        ),
    )(h, up, gate_lin, grad_hidden)


def back_kernel(terms, *refs):
    lefts, weights, out = refs[:terms], refs[terms:-1], refs[-1]
    total = None
    for left, weight in zip(lefts, weights):
        term = dot_cols(left[...], weight[...])
        total = term if total is None else total + term
    out[0] = total.astype(LOW)


def back_rows(lefts, weights, first_slot, slots, length):
    width = weights[0].shape[0]
    depth = sum(left.shape[1] for left in lefts)
    return pl.pallas_call(
        functools.partial(back_kernel, len(lefts)),
        grid=(slots,),
        in_specs=[
            pl.BlockSpec((length, left.shape[1]), lambda s: (first_slot + s, 0)) for left in lefts
        ]
        + [whole_spec(*w.shape, once=True) for w in weights],
        out_specs=pl.BlockSpec((1, length, width), lambda s: (s, 0, 0)),
        out_shape=jax.ShapeDtypeStruct((slots, length, width), LOW),
        compiler_params=pltpu.CompilerParams(vmem_limit_bytes=60 << 20),
        cost_estimate=pl.CostEstimate(
            flops=2 * slots * length * width * depth,
            bytes_accessed=2 * (slots * length * (width + depth) + width * depth),
            transcendentals=0,
        ),
    )(*lefts, *weights)


def turn(values, cosine, sine_signed):
    return values * cosine + pltpu.roll(values, values.shape[-1] // 2, 1) * sine_signed


def turn_back(values, cosine, sine_signed):
    return values * cosine - pltpu.roll(values, values.shape[-1] // 2, 1) * sine_signed


def project_kernel(
    heads, head_dim, x0, x1, x2, x3, gain, weight, bias, cosine, sine, h_out, q_out, k_out, v_out
):
    slot = pl.program_id(0)

    def run(x_ref):
        x = x_ref[...].astype(WIDE)
        scale_inv = lax.rsqrt(jnp.mean(x * x, axis=-1, keepdims=True) + EPS)
        normed = (x * scale_inv * gain[...]).astype(LOW)
        h_out[0] = normed
        lin = jnp.dot(normed, weight[...], preferred_element_type=WIDE) + bias[...]
        cos, sin = cosine[0], sine[0]
        for h in range(heads + 1):
            part = turn(lin[:, h * head_dim : (h + 1) * head_dim], cos, sin).astype(LOW)
            if h < heads:
                q_out[0, :, h * head_dim : (h + 1) * head_dim] = part
            else:
                k_out[0] = part
        v_out[0] = lin[:, (heads + 1) * head_dim :].astype(LOW)

    for r, x_ref in enumerate((x0, x1, x2, x3)):
        pl.when(slot == r)(functools.partial(run, x_ref))


def project(rows, gain, weight, bias, cosine, sine, heads, head_dim):
    length, width = rows[0].shape
    count = len(rows)
    cols = (heads + 2) * head_dim
    whole = whole_spec
    by_slot = lambda *shape: pl.BlockSpec((1, *shape), lambda s: (s,) + (0,) * len(shape))
    return pl.pallas_call(
        functools.partial(project_kernel, heads, head_dim),
        grid=(count,),
        in_specs=[whole(length, width)] * count
        + [whole(1, width), whole(width, cols), whole(1, cols)]
        + [by_slot(length, head_dim)] * 2,
        out_specs=[
            by_slot(length, width),
            by_slot(length, heads * head_dim),
            by_slot(length, head_dim),
            by_slot(length, head_dim),
        ],
        out_shape=[
            jax.ShapeDtypeStruct((count, length, width), LOW),
            jax.ShapeDtypeStruct((count, length, heads * head_dim), LOW),
            jax.ShapeDtypeStruct((count, length, head_dim), LOW),
            jax.ShapeDtypeStruct((count, length, head_dim), LOW),
        ],
        compiler_params=pltpu.CompilerParams(vmem_limit_bytes=56 << 20),
        cost_estimate=pl.CostEstimate(
            flops=2 * count * length * width * cols,
            bytes_accessed=count * length * (2 * width + cols) * 2 + width * cols * 2,
            transcendentals=0,
        ),
    )(*rows, gain, weight, bias, cosine, sine)


def row_blocks(length):
    return [(i, min(256, length)) for i in range(0, length, min(256, length))]


def key_biases(length, offset, start, rows, past, keys):
    past_pos = lax.broadcasted_iota(jnp.int32, (1, past), 1)
    past_bias = jnp.where((past_pos < offset) & (past_pos < length), 0.0, NEG_FILL)
    query_pos = offset + start + lax.broadcasted_iota(jnp.int32, (rows, keys), 0)
    own_pos = offset + lax.broadcasted_iota(jnp.int32, (rows, keys), 1)
    own_bias = jnp.where((own_pos <= query_pos) & (own_pos < length), 0.0, NEG_FILL)
    return past_bias, own_bias


def dot_cols(left, right):
    return lax.dot_general(left, right, (((1,), (1,)), ((), ())), preferred_element_type=WIDE)


def dot_rows(left, right):
    return lax.dot_general(left, right, (((0,), (0,)), ((), ())), preferred_element_type=WIDE)


def attend_kernel(heads, head_dim, scale, first, total_slots, info, q, k_past, v_past, k_own, v_own, out, lse):
    length, offset = info[first + pl.program_id(0)], info[total_slots]
    past = k_past.shape[1]
    for start, rows in row_blocks(q.shape[1]):
        keys = start + rows
        past_bias, own_bias = key_biases(length, offset, start, rows, past, keys)
        here = slice(start, start + rows)
        for h in range(heads):
            cols = slice(h * head_dim, (h + 1) * head_dim)
            query = q[0, here, cols]
            s_past = dot_cols(query, k_past[0]) * scale + past_bias
            s_own = dot_cols(query, k_own[0, :keys]) * scale + own_bias
            top = jnp.maximum(
                jnp.max(s_past, axis=1, keepdims=True), jnp.max(s_own, axis=1, keepdims=True)
            )
            e_past, e_own = jnp.exp(s_past - top), jnp.exp(s_own - top)
            total = jnp.sum(e_past, axis=1, keepdims=True) + jnp.sum(e_own, axis=1, keepdims=True)
            inverse = 1.0 / total
            mixed = jnp.dot(
                (e_past * inverse).astype(LOW), v_past[0], preferred_element_type=WIDE
            ) + jnp.dot((e_own * inverse).astype(LOW), v_own[0, :keys], preferred_element_type=WIDE)
            out[0, here, cols] = mixed.astype(LOW)
            lse[0, here, h : h + 1] = top + jnp.log(total)


def attend_forward(info, q, k_past, v_past, k_own, v_own, heads, head_dim, scale, first, count):
    _, length, width = q.shape
    past = k_past.shape[1]
    by_slot = lambda *shape: pl.BlockSpec((1, *shape), lambda s, info: (first + s,) + (0,) * len(shape))
    out_slot = lambda *shape: pl.BlockSpec((1, *shape), lambda s, info: (s,) + (0,) * len(shape))
    keys = count * length * (past + length) * heads
    return pl.pallas_call(
        functools.partial(attend_kernel, heads, head_dim, scale, first, q.shape[0]),
        grid_spec=pltpu.PrefetchScalarGridSpec(
            num_scalar_prefetch=1,
            grid=(count,),
            in_specs=[
                by_slot(length, width),
                by_slot(past, head_dim),
                by_slot(past, head_dim),
                by_slot(length, head_dim),
                by_slot(length, head_dim),
            ],
            out_specs=[out_slot(length, width), out_slot(length, 128)],
        ),
        out_shape=[
            jax.ShapeDtypeStruct((count, length, width), LOW),
            jax.ShapeDtypeStruct((count, length, 128), WIDE),
        ],
        compiler_params=pltpu.CompilerParams(vmem_limit_bytes=56 << 20),
        cost_estimate=pl.CostEstimate(
            flops=4 * keys * head_dim, bytes_accessed=4 * count * length * width, transcendentals=keys
        ),
    )(info, q, k_past, v_past, k_own, v_own)


def attend_back_kernel(
    heads,
    head_dim,
    scale,
    info,
    q,
    k_past,
    v_past,
    k_own,
    v_own,
    grad,
    lse,
    cosine,
    sine,
    dq_out,
    mine_past,
    mine_own,
    other_past,
    other_own,
    dk_past,
    dk_own,
    dv_past,
    dv_own,
):
    slot = pl.program_id(0)
    length, offset = info[slot], info[pl.num_programs(0)]
    parity = info[pl.num_programs(0) + 1]
    past = k_past.shape[1]
    for total in (dk_past, dk_own, dv_past, dv_own):
        total[...] = jnp.zeros_like(total)
    for start, rows in row_blocks(q.shape[1]):
        keys = start + rows
        past_bias, own_bias = key_biases(length, offset, start, rows, past, keys)
        here = slice(start, start + rows)
        cos, sin = cosine[0, here], sine[0, here]
        for h in range(heads):
            cols = slice(h * head_dim, (h + 1) * head_dim)
            query, upstream = q[0, here, cols], grad[0, here, cols]
            log_total = lse[0, here, h : h + 1]
            p_past = jnp.exp(dot_cols(query, k_past[0]) * scale + past_bias - log_total)
            p_own = jnp.exp(dot_cols(query, k_own[0, :keys]) * scale + own_bias - log_total)
            g_past = dot_cols(upstream, v_past[0])
            g_own = dot_cols(upstream, v_own[0, :keys])
            row_dot = jnp.sum(p_past * g_past, axis=1, keepdims=True) + jnp.sum(
                p_own * g_own, axis=1, keepdims=True
            )
            s_past = (p_past * (g_past - row_dot)).astype(LOW)
            s_own = (p_own * (g_own - row_dot)).astype(LOW)
            dq = (
                jnp.dot(s_past, k_past[0], preferred_element_type=WIDE)
                + jnp.dot(s_own, k_own[0, :keys], preferred_element_type=WIDE)
            ) * scale
            dq_out[0, here, cols] = turn_back(dq, cos, sin).astype(LOW)
            dk_past[...] += dot_rows(s_past, query)
            dk_own[:keys] += dot_rows(s_own, query)
            dv_past[...] += dot_rows(p_past.astype(LOW), upstream)
            dv_own[:keys] += dot_rows(p_own.astype(LOW), upstream)

    @pl.when(parity == 0)
    def _():
        mine_past[0] = dk_past[...] * scale
        mine_own[0] = dk_own[...] * scale
        other_past[0] = dv_past[...]
        other_own[0] = dv_own[...]

    @pl.when(parity != 0)
    def _():
        mine_past[0] = dv_past[...]
        mine_own[0] = dv_own[...]
        other_past[0] = dk_past[...] * scale
        other_own[0] = dk_own[...] * scale


def attend_backward(
    info, q, k_past, v_past, k_own, v_own, grad, lse, cosine, sine, heads, head_dim, scale
):
    count, length, width = q.shape
    past = k_past.shape[1]
    by_slot = lambda *shape: pl.BlockSpec((1, *shape), lambda s, info: (s,) + (0,) * len(shape))
    keys = count * length * (past + length) * heads
    return pl.pallas_call(
        functools.partial(attend_back_kernel, heads, head_dim, scale),
        grid_spec=pltpu.PrefetchScalarGridSpec(
            num_scalar_prefetch=1,
            grid=(count,),
            in_specs=[
                by_slot(length, width),
                by_slot(past, head_dim),
                by_slot(past, head_dim),
                by_slot(length, head_dim),
                by_slot(length, head_dim),
                by_slot(length, width),
                by_slot(length, 128),
                by_slot(length, head_dim),
                by_slot(length, head_dim),
            ],
            out_specs=[
                by_slot(length, width),
                by_slot(past, head_dim),
                by_slot(length, head_dim),
                by_slot(past, head_dim),
                by_slot(length, head_dim),
            ],
            scratch_shapes=[
                pltpu.VMEM((past, head_dim), WIDE),
                pltpu.VMEM((length, head_dim), WIDE),
                pltpu.VMEM((past, head_dim), WIDE),
                pltpu.VMEM((length, head_dim), WIDE),
            ],
        ),
        out_shape=[
            jax.ShapeDtypeStruct((count, length, width), LOW),
            jax.ShapeDtypeStruct((count, past, head_dim), WIDE),
            jax.ShapeDtypeStruct((count, length, head_dim), WIDE),
            jax.ShapeDtypeStruct((count, past, head_dim), WIDE),
            jax.ShapeDtypeStruct((count, length, head_dim), WIDE),
        ],
        compiler_params=pltpu.CompilerParams(vmem_limit_bytes=56 << 20),
        cost_estimate=pl.CostEstimate(
            flops=10 * keys * head_dim, bytes_accessed=8 * count * length * width, transcendentals=keys
        ),
    )(info, q, k_past, v_past, k_own, v_own, grad, lse, cosine, sine)


def local(
    hidden_in,
    cotangent,
    seq_lengths,
    positions,
    permutation,
    query_weight,
    keyval_weight,
    output_weight,
    norm_gains,
    bias_query,
    bias_keyval,
    gate_weight,
    up_weight,
    down_weight,
):
    group_rank = lax.axis_index("fsdp")
    ctx_rank = lax.axis_index("ctx")
    tensor_rank = lax.axis_index("tp")
    fsdp_count = lax.axis_size("fsdp")
    ctx_count = lax.axis_size("ctx")
    tensor_count = lax.axis_size("tp")
    seq_grp, local_len, model_width = hidden_in.shape
    heads, head_dim = bias_query.shape
    keyval_heads = bias_keyval.shape[0] // 2
    assert seq_grp == tensor_count == fsdp_count == len(DEAL_SHIFT)
    token_count = seq_grp * local_len
    scale = 1.0 / math.sqrt(head_dim)
    offset = ctx_rank * local_len
    head_pair = tensor_rank // (tensor_count // keyval_heads)
    parity = tensor_rank % 2
    shifts = jnp.array(DEAL_SHIFT, jnp.int32)

    table = permutation.reshape(fsdp_count, seq_grp)
    far_group = lax.rem(group_rank + shifts[tensor_rank], fsdp_count)
    far_row = lax.dynamic_index_in_dim(table, far_group, 0, keepdims=False)
    leaving = jnp.sum(jnp.where(far_row // seq_grp == group_rank, far_row - group_rank * seq_grp, 0))
    own_row = lax.dynamic_index_in_dim(table, group_rank, 0, keepdims=False)
    slot_now, seq_now, home_now = [], [], []
    for r in range(seq_grp):
        shift = shifts[tensor_rank ^ r]
        source = lax.rem(group_rank - shift + fsdp_count, fsdp_count)
        hit = own_row // seq_grp == source
        slot_now.append(jnp.sum(jnp.where(hit, jnp.arange(seq_grp), 0)))
        seq_now.append(jnp.sum(jnp.where(hit, own_row, 0)))
        target = lax.rem(group_rank + shift, fsdp_count)
        target_row = lax.dynamic_index_in_dim(table, target, 0, keepdims=False)
        home_now.append(
            jnp.sum(jnp.where(target_row // seq_grp == group_rank, target_row - group_rank * seq_grp, 0))
        )
    there = [
        (f * tensor_count + t, (f + DEAL_SHIFT[t]) % fsdp_count * tensor_count + t)
        for f in range(fsdp_count)
        for t in range(tensor_count)
    ]
    back = [(target, source) for source, target in there]

    split = units_split()
    head_width = 2 * head_dim
    query_cols = heads * head_dim
    near_cols = query_cols + head_width + 128

    outgoing = lax.dynamic_index_in_dim(hidden_in, leaving, 0, keepdims=False)
    own_in = lax.ppermute(outgoing, ("fsdp", "tp"), there)
    small = jnp.concatenate(
        [
            query_weight,
            lax.dynamic_slice_in_dim(keyval_weight, head_pair * head_width, head_width, axis=1),
            jnp.pad(norm_gains.T, ((0, 0), (0, 128 - norm_gains.shape[0]))),
            output_weight.T,
        ],
        axis=1,
    )
    units = gate_weight.shape[1]
    units_pad = -(-units // 256) * 256
    widen = lambda w: jnp.pad(w, ((0, 0), (0, units_pad - units)))
    shards = [widen(w) for w in (down_weight.T, gate_weight, up_weight)]
    if split:
        half_units = units_pad // 2
        cut = lambda w, c: lax.dynamic_slice_in_dim(w, c * half_units, half_units, axis=1)

        def in_order(own, other):
            return jnp.stack(
                [jnp.where(ctx_rank == 0, own, other), jnp.where(ctx_rank == 0, other, own)]
            )

        def all_rows(both, *earlier):
            full = lax.all_gather(after(both, *earlier), "fsdp", axis=0, tiled=False)
            return full.reshape(-1, both.shape[-1])

        small_both = in_order(small, from_partner(after(small, outgoing), "ctx", 1))
        leaving_units = jnp.concatenate([cut(w, 1 - ctx_rank) for w in shards], axis=1)
        arriving_units = from_partner(after(leaving_units, small), "ctx", 1)
        unit_both = [
            in_order(cut(w, ctx_rank), arriving_units[:, i * half_units : (i + 1) * half_units])
            for i, w in enumerate(shards)
        ]
    else:
        all_rows = lambda shard, *earlier: lax.all_gather(
            shard, ("fsdp", "ctx"), axis=0, tiled=True
        )
        small_both, unit_both = small, shards
    far_in = from_partner(own_in, "tp", 2)
    near_in = from_partner(own_in, "tp", 1)
    cross_in = from_partner(far_in, "tp", 1)

    lengths_now = jnp.stack([seq_lengths[s] for s in seq_now])
    info = jnp.concatenate([lengths_now, jnp.stack([offset, parity])]).astype(jnp.int32)
    positions_now = jnp.stack(
        [lax.dynamic_index_in_dim(positions, s, 0, keepdims=False) for s in seq_now]
    )
    lane = jnp.arange(head_dim)
    frequency = 1.0 / ROPE_BASE ** ((lane % (head_dim // 2)).astype(WIDE) * 2.0 / head_dim)
    angles = positions_now.astype(WIDE)[..., None] * frequency
    cosine = jnp.cos(angles)
    sine = jnp.sin(angles) * jnp.where(lane < head_dim // 2, -1.0, 1.0)
    grad_slots = [lax.dynamic_index_in_dim(cotangent, s, 0, keepdims=False) for s in slot_now]

    near_full = all_rows(small_both[..., :near_cols], own_in)
    output_full = all_rows(small_both[..., near_cols:], far_in)
    down_full = all_rows(unit_both[0], cross_in)
    project_full = near_full[:, : query_cols + head_width]
    gains_now = near_full[:, query_cols + head_width :][:, :2].astype(WIDE).T
    bias_head = lax.dynamic_slice_in_dim(bias_keyval, head_pair * 2, 2, axis=0)
    bias_row = jnp.concatenate([bias_query.reshape(1, -1), bias_head.reshape(1, -1)], axis=1).astype(WIDE)
    normed_one, query_rot, key_own, value_own = project(
        (own_in, near_in, far_in, cross_in),
        gains_now[0:1],
        project_full,
        bias_row,
        cosine,
        sine,
        heads,
        head_dim,
    )
    gate_full = all_rows(unit_both[1], query_rot)
    if split:
        key_past, value_past = lax.ppermute((key_own, value_own), "ctx", [(0, 1)])
        grad_pair = after(jnp.stack([grad_slots[0], grad_slots[2]]), value_past)
        other_pair = from_partner(grad_pair, "ctx", 1)
        cross_pair = from_partner(other_pair, "tp", 1)
        others = [other_pair[0], cross_pair[0], other_pair[1], cross_pair[1]]
    else:
        key_past = lax.all_gather(key_own, "ctx", axis=1, tiled=True)
        value_past = lax.all_gather(value_own, "ctx", axis=1, tiled=True)
        others = []
    attend = lambda first, *held: attend_forward(
        info, query_rot, *held, key_own, value_own, heads, head_dim, scale, first, 2
    )
    in_share = own_in.astype(WIDE)

    mixed_far, lse_far = attend(2, key_past, value_past)
    attn_far = contract_cols(mixed_far.reshape(-1, query_cols), output_full, LOW)
    attn_far = attn_far.reshape(2, local_len, model_width)
    attn_wide = collect_far(attn_far[0], attn_far[1])
    attn_got = from_partner(attn_wide, "tp", 2)
    mixed_near, lse_near = attend(0, after(key_past, attn_wide), value_past)
    attn_near = contract_cols(mixed_near.reshape(-1, query_cols), output_full, LOW)
    attn_near = attn_near.reshape(2, local_len, model_width)
    attn_core = from_partner(attn_near[1], "tp", 1)
    up_full = all_rows(unit_both[2], attn_near)
    middle_share = (
        in_share
        + attn_near[0].astype(WIDE)
        + attn_core.astype(WIDE)
        + attn_got.astype(WIDE)
    )
    inv_two = lax.rsqrt(jnp.mean(middle_share * middle_share, axis=-1, keepdims=True) + EPS)
    normed_share = (middle_share * inv_two * gains_now[1]).astype(LOW)
    half_len = local_len // 2

    def spread_all(own, then):
        far = from_partner(own, "tp", 2)
        near = from_partner(own, "tp", 1)
        if not split:
            return (own, near, far, from_partner(far, "tp", 1)), then()
        side = from_partner(own, "ctx", 1)
        between = then()
        diagonal = (
            from_partner(far[:half_len], "ctx", 1),
            from_partner(side[half_len:], "tp", 2),
        )
        diagonal = jnp.concatenate(diagonal, axis=0)
        cores = [from_partner(v, "tp", 1) for v in (far, side, diagonal)]
        return (own, near, far, cores[0], side, cores[1], diagonal, cores[2]), between

    grad_rows = jnp.concatenate(grad_slots + others, axis=0)
    normed_rows, grad_hidden = spread_all(
        normed_share, lambda: product(after(grad_rows, normed_share), down_full, LOW)
    )
    gate_lin, normed_two = gate_rows(normed_rows, gate_full)
    hidden_act, grad_gate, grad_up = hidden_units(normed_two, up_full, gate_lin, grad_hidden)

    def collect_all(lefts, weights, *earlier):
        lefts = list(lefts)
        lefts[0] = after(lefts[0], *earlier)
        if split:
            last = back_rows(lefts, weights, 6, 2, local_len)
            diagonal = collect_far(last[0], last[1])
            to_far = from_partner(diagonal[:half_len], "tp", 2)
            to_side = from_partner(diagonal[half_len:], "ctx", 1)
            lefts[0] = after(lefts[0], diagonal)
            middle = back_rows(lefts, weights, 2, 4, local_len)
            core_far, core_side = (from_partner(middle[i], "tp", 1) for i in (1, 3))
            far = middle[0].astype(WIDE) + core_far.astype(WIDE)
            side = middle[2].astype(WIDE) + core_side.astype(WIDE)
            side = jnp.concatenate(
                [side[:half_len] + to_far.astype(WIDE), side[half_len:]], axis=0
            ).astype(LOW)
            far = jnp.concatenate(
                [far[:half_len], far[half_len:] + to_side.astype(WIDE)], axis=0
            ).astype(LOW)
            got = [from_partner(far, "tp", 2), from_partner(side, "ctx", 1)]
            lefts[0] = after(lefts[0], far, side)
        else:
            last = back_rows(lefts, weights, 2, 2, local_len)
            got = [from_partner(collect_far(last[0], last[1]), "tp", 2)]
        first = back_rows(lefts, weights, 0, 2, local_len)
        got.append(from_partner(first[1], "tp", 1))

        def finish():
            return sum((v.astype(WIDE) for v in got), first[0].astype(WIDE))

        return first, finish

    first_back, finish_back = collect_all((grad_gate, grad_up), (gate_full, up_full))
    down_grad = contract_rows(after(grad_rows, first_back), hidden_act, LOW)
    gate_grad = contract_rows(normed_two, after(grad_gate, down_grad), LOW)
    grad_two_share = finish_back()
    grad_norm_two, gain_two = norm_backward(middle_share, inv_two, gains_now[1], grad_two_share)
    grad_middle = grad_slots[0].astype(WIDE) + grad_norm_two
    branch_own = grad_middle.astype(LOW)
    branch_far = from_partner(branch_own, "tp", 2)
    branch_near = from_partner(branch_own, "tp", 1)
    branch_cross = from_partner(branch_far, "tp", 1)
    grad_branch = jnp.concatenate([branch_own, branch_near, branch_far, branch_cross], axis=0)
    up_grad = contract_rows(normed_two, after(grad_up, branch_own), LOW)

    def scatter_units(grad):
        if not split:
            return scatter_sum(grad, ctx_rank, LOW)
        return lax.psum_scatter(grad, "fsdp", scatter_dimension=0, tiled=True)

    unit_sums = [scatter_units(g) for g in (down_grad, gate_grad, up_grad)]

    grad_mixed = product(grad_branch, output_full, LOW)
    mixed_flat = jnp.concatenate([mixed_near, mixed_far], axis=0).reshape(token_count, query_cols)
    lse = jnp.concatenate([lse_near, lse_far], axis=0)
    grad_query, mine_past, mine_own, other_past, other_own = attend_backward(
        info,
        query_rot,
        key_past,
        value_past,
        key_own,
        value_own,
        grad_mixed.reshape(seq_grp, local_len, query_cols),
        lse,
        cosine,
        sine,
        heads,
        head_dim,
        scale,
    )
    swap = lambda value: jnp.stack([value[r ^ 1] for r in range(seq_grp)])
    got_past, got_own = from_partner((other_past, other_own), "tp", 1)
    past_sum = mine_past + swap(got_past)
    own_sum = mine_own + swap(got_own)
    if split:
        own_sum = own_sum + lax.ppermute(past_sum.astype(LOW), "ctx", [(1, 0)]).astype(WIDE)
    else:
        own_sum = own_sum + lax.psum_scatter(past_sum, "ctx", scatter_dimension=1, tiled=True)
    half_lanes = head_dim // 2
    turned = own_sum * cosine - jnp.roll(own_sum, half_lanes, axis=-1) * sine
    own_grad = jnp.where(parity == 0, turned, own_sum).astype(LOW).reshape(token_count, head_dim)
    line_grad = jnp.concatenate([grad_query.reshape(token_count, query_cols), own_grad], axis=1)
    own_weight = lax.dynamic_slice_in_dim(
        project_full, query_cols + parity * head_dim, head_dim, axis=1
    )
    back_full = jnp.concatenate([project_full[:, :query_cols], own_weight], axis=1)
    half = token_count // 2
    line_far = contract_cols(line_grad[half:], back_full, LOW).reshape(2, local_len, model_width)
    line_near = contract_cols(line_grad[:half], back_full, LOW).reshape(2, local_len, model_width)
    line_wide = collect_far(line_far[0], line_far[1])
    line_got = from_partner(line_wide, "tp", 2)
    line_core = from_partner(line_near[1], "tp", 1)

    first_mlp, finish_mlp = collect_all((hidden_act,), (down_full,), up_grad, branch_far)
    block_share = (middle_share + finish_mlp()).astype(LOW)

    grad_one_share = line_near[0].astype(WIDE) + line_core.astype(WIDE) + line_got.astype(WIDE)
    inv_one = lax.rsqrt(jnp.mean(in_share * in_share, axis=-1, keepdims=True) + EPS)
    grad_norm_one, gain_one = norm_backward(in_share, inv_one, gains_now[0], grad_one_share)
    input_share = (grad_middle + grad_norm_one).astype(LOW)

    normed_flat = normed_one.reshape(token_count, model_width)
    late = after(line_grad, line_wide, line_near)
    attn_grad = jnp.concatenate(
        [contract_rows(normed_flat, late, LOW), contract_rows(grad_branch, mixed_flat, LOW)], axis=1
    )
    bias_grad = jnp.sum(late.astype(WIDE), axis=0)
    attn_end = scatter_sum(attn_grad, ctx_rank, LOW, input_share)

    def leave(share):
        return lax.ppermute(share, ("fsdp", "tp"), back)

    def arrive(own, *earlier):
        far = from_partner(after(own, *earlier), "tp", 2)
        near = from_partner(own, "tp", 1)
        cross = from_partner(far, "tp", 1)
        out = jnp.zeros((seq_grp, local_len, model_width), LOW)
        for home, row in zip(home_now, (own, near, far, cross)):
            out = lax.dynamic_update_index_in_dim(out, row, home, 0)
        return out

    block_home = leave(block_share)
    input_home = leave(input_share)
    block_out = arrive(block_home, input_share)
    input_grad = arrive(input_home)

    gain_grad = jnp.stack([gain_one, gain_two], axis=1)
    gain_grad = gain_grad + from_partner(gain_grad, "tp", 1)
    gain_grad = gain_grad + from_partner(gain_grad, "tp", 2)
    shard_count = fsdp_count * ctx_count
    share = head_dim // shard_count
    bias_cols = jnp.transpose(bias_grad.reshape(heads + 1, shard_count, share), (1, 2, 0))
    bias_cols = jnp.pad(bias_cols, ((0, 0), (0, (model_width - head_dim) // shard_count), (0, 0)))
    tiny = jnp.concatenate([gain_grad, bias_cols.reshape(model_width, heads + 1)], axis=1)
    tiny_grad = scatter_sum(jnp.pad(tiny, ((0, 0), (0, 8 - tiny.shape[1]))), ctx_rank, WIDE)

    def unit_end(total):
        if split:
            blocks = total.reshape(1, ctx_count, -1, half_units)
            kept, sent = scatter_ctx(blocks, ctx_rank)
            kept, got = kept[0], from_partner(sent[0], "ctx", 1)
            first = jnp.where(ctx_rank == 0, kept, got)
            second = jnp.where(ctx_rank == 0, got, kept)
            total = jnp.concatenate([first, second], axis=1)
        return total[:, :units].astype(WIDE)

    down_end, gate_end, up_end = (unit_end(after(t, input_share)) for t in unit_sums)
    return (
        block_out,
        input_grad,
        attn_end[:, :query_cols].astype(WIDE),
        attn_end[:, query_cols : query_cols + head_dim].astype(WIDE),
        attn_end[:, query_cols + head_dim :].astype(WIDE).T,
        tiny_grad[:, :2].T,
        tiny_grad[:share, 2 : 2 + heads].T,
        tiny_grad[:share, 2 + heads : 3 + heads].T,
        gate_end,
        up_end,
        down_end.T,
    )


def solution(mesh):
    placed = (
        P("fsdp", "ctx", None),
        P("fsdp", "ctx", None),
        P(),
        P(None, "ctx"),
        P(),
        P(("fsdp", "ctx"), "tp"),
        P(("fsdp", "ctx"), None),
        P("tp", ("fsdp", "ctx")),
        P(None, ("fsdp", "ctx")),
        P("tp", None),
        P(),
        P(("fsdp", "ctx"), "tp"),
        P(("fsdp", "ctx"), "tp"),
        P("tp", ("fsdp", "ctx")),
    )
    return jax.shard_map(
        local,
        mesh=mesh,
        in_specs=placed,
        out_specs=(
            P("fsdp", "ctx", None),
            P("fsdp", "ctx", None),
            P(("fsdp", "ctx"), "tp"),
            P(("fsdp", "ctx"), "tp"),
            P("tp", ("fsdp", "ctx")),
            P(None, ("fsdp", "ctx")),
            P("tp", ("fsdp", "ctx")),
            P("tp", ("fsdp", "ctx")),
            P(("fsdp", "ctx"), "tp"),
            P(("fsdp", "ctx"), "tp"),
            P("tp", ("fsdp", "ctx")),
        ),
        check_vma=False,
    )
```

```python
import functools
import math

import jax
import jax.numpy as jnp
from jax import lax
from jax.experimental import pallas as pl
from jax.experimental.pallas import tpu as pltpu
from jax.sharding import PartitionSpec as P

EPS = 1e-06
ROPE_BASE = 10000.0
NEG_FILL = -1e30
LOW = jnp.bfloat16
WIDE = jnp.float32
DEAL_SHIFT = (0, 2, 1, 3)


def from_partner(value, axis, apart):
    pairs = [(source, source ^ apart) for source in range(lax.axis_size(axis))]
    return lax.ppermute(value, axis, pairs)


def product(left_side, right_side, kind=WIDE):
    return jnp.dot(left_side, right_side, preferred_element_type=WIDE).astype(kind)


def contract_rows(left_side, right_side, kind=WIDE):
    return lax.dot_general(
        left_side, right_side, (((0,), (0,)), ((), ())), preferred_element_type=WIDE
    ).astype(kind)


def contract_cols(left_side, right_side, kind=WIDE):
    return lax.dot_general(
        left_side, right_side, (((1,), (1,)), ((), ())), preferred_element_type=WIDE
    ).astype(kind)


def norm_backward(values, scale_inv, gain_row, upstream):
    scaled = gain_row * upstream
    inner_mean = jnp.mean(values * scaled, axis=-1, keepdims=True)
    grad_in = scale_inv * scaled - values * (scale_inv * scale_inv * scale_inv) * inner_mean
    gain_grad = jnp.sum(upstream * values * scale_inv, axis=0, keepdims=True)
    return (grad_in, gain_grad)


def after(value, *earlier):
    return lax.optimization_barrier((value, *earlier))[0]


def collect_far(far_part, cross_part):
    wide = far_part.astype(WIDE) + from_partner(cross_part, "tp", 1).astype(WIDE)
    return wide.astype(LOW)


def units_split():
    return lax.axis_size("ctx") == 2


def all_rows(shard):
    return lax.all_gather(shard, "fsdp", axis=0, tiled=True)


def scatter_ctx(blocks, ctx_rank):
    kept = lax.dynamic_index_in_dim(blocks, ctx_rank, 1, keepdims=False)
    sent = lax.dynamic_index_in_dim(blocks, 1 - ctx_rank, 1, keepdims=False)
    return kept, sent


def scatter_sum(grad, ctx_rank, kind, *earlier):
    fsdp_count, ctx_count = lax.axis_size("fsdp"), lax.axis_size("ctx")
    rows, cols = grad.shape
    blocks = grad.reshape(fsdp_count, ctx_count, rows // (fsdp_count * ctx_count), cols)
    if ctx_count == 2:
        kept, sent = scatter_ctx(blocks, ctx_rank)
        got = from_partner(sent, "ctx", 1)
        held = (after(kept, *earlier).astype(WIDE) + got.astype(WIDE)).astype(kind)
    else:
        swapped = jnp.swapaxes(blocks, 0, 1).reshape(rows, cols)
        held = lax.psum_scatter(swapped, "ctx", scatter_dimension=0, tiled=True)
    held = held.reshape(rows // ctx_count, cols)
    return lax.psum_scatter(held, "fsdp", scatter_dimension=0, tiled=True)


def estimate(flops, moved, transcendentals=0):
    return pl.CostEstimate(flops=flops, bytes_accessed=moved, transcendentals=transcendentals)


def part_spec(rows, cols, part):
    return pl.BlockSpec((rows, cols), lambda *_: (0, part), pipeline_mode=pl.Buffered(1))


def whole_spec(*shape, once=False):
    mode = {"pipeline_mode": pl.Buffered(1)} if once else {}
    return pl.BlockSpec(shape, lambda *_: (0,) * len(shape), **mode)


def rows_kernel(groups, *refs):
    slot = pl.program_id(0)
    weight, lin, stacked = refs[-3:]

    def run(pieces):
        start = 0
        for piece in pieces:
            stacked[start : start + piece.shape[0]] = piece[...]
            start += piece.shape[0]
        lin[...] = jnp.dot(stacked[...], weight[...], preferred_element_type=WIDE).astype(LOW)

    first = 0
    for r, pieces in enumerate(groups):
        pl.when(slot == r)(functools.partial(run, refs[first : first + pieces]))
        first += pieces


def stack_rows(slots, weight, part, parts):
    groups = [len(s) for s in slots]
    rows = [piece for s in slots for piece in s]
    width, length = rows[0].shape[1], sum(piece.shape[0] for piece in slots[0])
    count, cols = len(slots), weight.shape[1] // parts
    return pl.pallas_call(
        functools.partial(rows_kernel, groups),
        grid=(count,),
        in_specs=[whole_spec(*piece.shape, once=True) for piece in rows]
        + [part_spec(width, cols, part)],
        out_specs=[
            pl.BlockSpec((length, cols), lambda s: (s, 0)),
            pl.BlockSpec((length, width), lambda s: (s, 0)),
        ],
        out_shape=[
            jax.ShapeDtypeStruct((count * length, cols), LOW),
            jax.ShapeDtypeStruct((count * length, width), LOW),
        ],
        compiler_params=pltpu.CompilerParams(vmem_limit_bytes=60 << 20),
        cost_estimate=estimate(
            2 * count * length * width * cols, 2 * (count * length * (2 * width + cols) + width * cols)
        ),
    )(*rows, weight)


def units_kernel(h, up, gate, grad, hid, grad_gate, grad_up):
    up_lin = jnp.dot(h[...], up[...], preferred_element_type=WIDE)
    gate_lin = gate[...].astype(WIDE)
    grad_hidden = grad[...].astype(WIDE)
    sigmoid = 1.0 / (1.0 + jnp.exp(-gate_lin))
    silu = gate_lin * sigmoid
    hid[...] = (silu * up_lin).astype(LOW)
    grad_gate[...] = (grad_hidden * up_lin * sigmoid * (1.0 + gate_lin * (1.0 - sigmoid))).astype(LOW)
    grad_up[...] = (grad_hidden * silu).astype(LOW)


def hidden_units(h, up, part, parts, gate_lin, grad_hidden):
    tokens, width = h.shape
    cols = up.shape[1] // parts
    step = math.gcd(512, tokens)
    by_row = lambda n: pl.BlockSpec((step, n), lambda i: (i, 0))
    return pl.pallas_call(
        units_kernel,
        grid=(tokens // step,),
        in_specs=[by_row(width), part_spec(width, cols, part), by_row(cols), by_row(cols)],
        out_specs=[by_row(cols)] * 3,
        out_shape=[jax.ShapeDtypeStruct((tokens, cols), LOW)] * 3,
        compiler_params=pltpu.CompilerParams(vmem_limit_bytes=60 << 20),
        cost_estimate=estimate(
            2 * tokens * width * cols, 2 * (tokens * width + width * cols + 5 * tokens * cols)
        ),
    )(h, up, gate_lin, grad_hidden)


def back_kernel(terms, *refs):
    lefts, weights, outs = refs[:terms], refs[terms : 2 * terms], refs[2 * terms :]
    total = None
    for left, weight in zip(lefts, weights):
        term = dot_cols(left[...], weight[...])
        total = term if total is None else total + term
    for i, out in enumerate(outs):

        @pl.when(pl.program_id(0) == i)
        def _():
            out[...] = total.astype(LOW)


def back_rows(lefts, weights, first_slot, slots, length):
    width = weights[0][0].shape[0]
    depth = sum(left.shape[1] for left in lefts)
    return pl.pallas_call(
        functools.partial(back_kernel, len(lefts)),
        grid=(slots,),
        in_specs=[
            pl.BlockSpec((length, left.shape[1]), lambda s: (first_slot + s, 0)) for left in lefts
        ]
        + [part_spec(width, w.shape[1] // parts, part) for w, part, parts in weights],
        out_specs=[whole_spec(length, width)] * slots,
        out_shape=[jax.ShapeDtypeStruct((length, width), LOW)] * slots,
        compiler_params=pltpu.CompilerParams(vmem_limit_bytes=60 << 20),
        cost_estimate=estimate(
            2 * slots * length * width * depth,
            2 * (slots * length * (width + depth) + width * depth),
        ),
    )(*lefts, *[w for w, _, _ in weights])


MESH_ID = pl.DeviceIdType.MESH


def meet(partners):
    barrier = pltpu.get_barrier_semaphore()
    for partner in partners:
        pl.semaphore_signal(barrier, inc=1, device_id=partner, device_id_type=MESH_ID)
    pl.semaphore_wait(barrier, len(partners))


def partners_of():
    tensor_rank, ctx_rank = lax.axis_index("tp"), lax.axis_index("ctx")
    return {"tp": tensor_rank ^ 1}, {"tp": tensor_rank ^ 2}, {"ctx": ctx_rank ^ 1}


def collect_kernel(
    slots, gate, up, weight_gate, weight_up, left, right, total, grad, parts, core_in, across_in,
    last_in, held, send, recv, load
):
    step = pl.program_id(0)
    steps = pl.num_programs(0)
    core, far, side = partners_of()
    half = total.shape[0] // 2

    def remote(source, target, index, partner):
        return pltpu.make_async_remote_copy(
            source, target, send.at[index], recv.at[index], device_id=partner, device_id_type=MESH_ID
        )

    cores = [remote(parts.at[7 - 2 * k], core_in.at[k], k, core) for k in range(4)]
    across = [
        remote(parts.at[6, pl.ds(0, half)], across_in.at[0], 4, far),
        remote(parts.at[6, pl.ds(half, half)], across_in.at[1], 5, side),
    ]
    lasts = [
        remote(parts.at[2], last_in.at[0], 6, far),
        remote(parts.at[4, pl.ds(half, half)], last_in.at[1, pl.ds(half, half)], 7, side),
        remote(parts.at[4, pl.ds(0, half)], last_in.at[1, pl.ds(0, half)], 8, side),
    ]
    loading = pltpu.make_async_copy(right, held, load)

    @pl.when(step == 0)
    def _():
        loading.start()
        meet((core, far, side))

    @pl.when(step < slots)
    def _():
        part = dot_cols(gate[...], weight_gate[...]) + dot_cols(up[...], weight_up[...])
        parts[slots - 1 - step] = part.astype(LOW)

        @pl.when(step == slots - 1)
        def _():
            total[...] = part

    for k in range(4):
        pl.when(step == 2 * k)(cores[k].start)

    def add(slot, rows, value):
        parts[slot, rows] = (parts[slot, rows].astype(WIDE) + value.astype(WIDE)).astype(LOW)

    whole, low, high = slice(None), pl.ds(0, half), pl.ds(half, half)

    @pl.when(step == 1)
    def _():
        cores[0].wait_recv()
        add(6, whole, core_in[0])
        for copy in across:
            copy.start()

    @pl.when(step == 3)
    def _():
        cores[1].wait_recv()
        add(4, whole, core_in[1])
        lasts[1].start()

    @pl.when(step == 5)
    def _():
        cores[2].wait_recv()
        add(2, whole, core_in[2])
        across[1].wait_recv()
        add(2, high, across_in[1])
        lasts[0].start()
        across[0].wait_recv()
        add(4, low, across_in[0])
        lasts[2].start()

    @pl.when(step >= slots)
    def _():
        pl.when(step == slots)(loading.wait)
        grad[...] = dot_rows(left[...], held[...]).astype(LOW)

    @pl.when(step == steps - 1)
    def _():
        cores[3].wait_recv()
        for copy in lasts:
            copy.wait_recv()
        total[...] += (
            core_in[3].astype(WIDE) + last_in[0].astype(WIDE) + last_in[1].astype(WIDE)
        )
        for copy in (*cores, *across, *lasts):
            copy.wait_send()


def collect_back(grad_gate, grad_up, weight, left, right, length):
    tokens, cols = grad_gate.shape
    width = weight.shape[0]
    slots, tile = tokens // length, 256
    tiles = width // tile
    row = pl.BlockSpec((length, cols), lambda i: (jnp.maximum(slots - 1 - i, 0), 0))
    column = lambda i: jnp.clip(i - slots, 0, tiles - 1)
    return pl.pallas_call(
        functools.partial(collect_kernel, slots),
        grid=(slots + tiles,),
        in_specs=[
            row,
            row,
            part_spec(width, cols, 0),
            part_spec(width, cols, 1),
            pl.BlockSpec((tokens, tile), lambda i: (0, column(i))),
            pl.BlockSpec(memory_space=pl.ANY),
        ],
        out_specs=[
            pl.BlockSpec((length, width), lambda i: (0, 0)),
            pl.BlockSpec((tile, cols), lambda i: (column(i), 0)),
        ],
        out_shape=[
            jax.ShapeDtypeStruct((length, width), WIDE),
            jax.ShapeDtypeStruct((width, cols), LOW),
        ],
        scratch_shapes=[
            pltpu.VMEM((slots, length, width), LOW),
            pltpu.VMEM((4, length, width), LOW),
            pltpu.VMEM((2, length // 2, width), LOW),
            pltpu.VMEM((2, length, width), LOW),
            pltpu.VMEM((tokens, cols), LOW),
            pltpu.SemaphoreType.DMA((9,)),
            pltpu.SemaphoreType.DMA((9,)),
            pltpu.SemaphoreType.DMA,
        ],
        compiler_params=pltpu.CompilerParams(
            vmem_limit_bytes=63 << 20, collective_id=1, has_side_effects=True
        ),
        cost_estimate=estimate(6 * tokens * width * cols, 10 * tokens * cols),
    )(grad_gate, grad_up, weight, weight, left, right)


def remote_copy(send, recv):
    def make(source, target, index, partner):
        return pltpu.make_async_remote_copy(
            source, target, send.at[index], recv.at[index], device_id=partner, device_id_type=MESH_ID
        )

    return make


def branch_kernel(
    slots, tiles, total, middle, own_grad, gain, hid, weight, turned, gate, grad_middle, gain_grad,
    gate_out, branch, mlp_own, mlp_far, mlp_side, mlp_first, mlp_second, own, parts, core_in, held,
    send, recv, load
):
    step = pl.program_id(0)
    core, far, _ = partners_of()
    half = own.shape[0] // 2
    remote = remote_copy(send, recv)
    to_far = remote(own, branch.at[2], 0, far)
    to_near = remote(own, branch.at[1], 1, core)
    to_cross = remote(branch.at[2], branch.at[3], 2, core)
    keep = pltpu.make_async_copy(own, branch.at[0], load.at[0])
    loading = pltpu.make_async_copy(gate, held, load.at[1])
    cores = [remote(parts.at[7 - 2 * k], core_in.at[k], 3 + k, core) for k in range(4)]
    store = lambda source, target, i: pltpu.make_async_copy(source, target, load.at[i])
    stores = [
        [
            store(parts.at[6, pl.ds(0, half)], mlp_first, 2),
            store(parts.at[6, pl.ds(half, half)], mlp_second, 3),
        ],
        [store(parts.at[4], mlp_side, 4)],
        [store(parts.at[2], mlp_far, 5)],
        [store(parts.at[0], mlp_own, 6)],
    ]

    @pl.when(step == 0)
    def _():
        loading.start()
        meet((core, far))
        values, upstream = middle[...], total[...]
        inverse = lax.rsqrt(jnp.mean(values * values, axis=-1, keepdims=True) + EPS)
        grad_in, gain_grad[...] = norm_backward(values, inverse, gain[...], upstream)
        grad_in = own_grad[...].astype(WIDE) + grad_in
        grad_middle[...] = grad_in
        own[...] = grad_in.astype(LOW)
        for copy in (to_far, to_near, keep):
            copy.start()

    @pl.when(step < slots)
    def _():
        parts[slots - 1 - step] = dot_cols(hid[...], weight[...]).astype(LOW)

    for k in range(4):
        pl.when(step == 2 * k)(cores[k].start)

        def finish(k=k):
            slot = 6 - 2 * k
            cores[k].wait_recv()
            parts[slot] = (parts[slot].astype(WIDE) + core_in[k].astype(WIDE)).astype(LOW)
            for copy in stores[k]:
                copy.start()

        pl.when(step == 2 * k + 1)(finish)

    @pl.when(step >= slots)
    def _():
        pl.when(step == slots)(loading.wait)
        gate_out[...] = dot_rows(turned[...], held[...]).astype(LOW)

    @pl.when(step == slots + tiles - 2)
    def _():
        to_far.wait_recv()
        to_cross.start()

    @pl.when(step == slots + tiles - 1)
    def _():
        to_near.wait_recv()
        to_cross.wait_recv()
        keep.wait()
        for group in stores:
            for copy in group:
                copy.wait()
        for copy in (to_far, to_near, to_cross, *cores):
            copy.wait_send()


ANYWHERE = pl.BlockSpec(memory_space=pl.ANY)


def spread_branch(total, middle, own_grad, gain, hid, weight, rows, grad_gate):
    length, width = total.shape
    tokens, cols = grad_gate.shape
    slots, tile = tokens // length, 256
    tiles = width // tile
    once = whole_spec(length, width, once=True)
    column = lambda i: jnp.clip(i - slots, 0, tiles - 1)
    part = jax.ShapeDtypeStruct((length, width), LOW)
    piece = jax.ShapeDtypeStruct((length // 2, width), LOW)
    return pl.pallas_call(
        functools.partial(branch_kernel, slots, tiles),
        grid=(slots + tiles,),
        in_specs=[
            once,
            once,
            once,
            whole_spec(1, width),
            pl.BlockSpec((length, cols), lambda i: (jnp.maximum(slots - 1 - i, 0), 0)),
            part_spec(width, cols, 0),
            pl.BlockSpec((tokens, tile), lambda i: (0, column(i))),
            ANYWHERE,
        ],
        out_specs=[
            whole_spec(length, width, once=True),
            whole_spec(1, width),
            pl.BlockSpec((tile, cols), lambda i: (column(i), 0)),
        ]
        + [ANYWHERE] * 6,
        out_shape=[
            jax.ShapeDtypeStruct((length, width), WIDE),
            jax.ShapeDtypeStruct((1, width), WIDE),
            jax.ShapeDtypeStruct((width, cols), LOW),
            jax.ShapeDtypeStruct((4, length, width), LOW),
            part,
            part,
            part,
            piece,
            piece,
        ],
        scratch_shapes=[
            pltpu.VMEM((length, width), LOW),
            pltpu.VMEM((slots, length, width), LOW),
            pltpu.VMEM((4, length, width), LOW),
            pltpu.VMEM((tokens, cols), LOW),
            pltpu.SemaphoreType.DMA((7,)),
            pltpu.SemaphoreType.DMA((7,)),
            pltpu.SemaphoreType.DMA((7,)),
        ],
        compiler_params=pltpu.CompilerParams(
            vmem_limit_bytes=63 << 20, collective_id=2, has_side_effects=True
        ),
        cost_estimate=estimate(4 * tokens * width * cols, 10 * tokens * cols),
    )(total, middle, own_grad, gain, hid, weight, rows, grad_gate)


def line_kernel(
    slots, tiles, line, weight, own_in, grad_middle, gain, turned, up, rows_one, branch, line_all,
    mixed, share, gain_grad, up_out, attn_out, bias_out, parts, core_in, far_in, total, held, send,
    recv, load
):
    step = pl.program_id(0)
    core, far, _ = partners_of()
    remote = remote_copy(send, recv)
    cores = [remote(parts.at[3 - 2 * k], core_in.at[k], k, core) for k in range(2)]
    to_far = remote(parts.at[2], far_in, 2, far)
    loading = pltpu.make_async_copy(up, held, load)

    @pl.when(step == 0)
    def _():
        loading.start()
        meet((core, far))

    @pl.when(step < slots)
    def _():
        part = dot_cols(line[...], weight[...])
        parts[slots - 1 - step] = part.astype(LOW)

        @pl.when(step == slots - 1)
        def _():
            total[...] = part

    for k in range(2):
        pl.when(step == 2 * k)(cores[k].start)

    @pl.when(step == 1)
    def _():
        cores[0].wait_recv()
        parts[2] = (parts[2].astype(WIDE) + core_in[0].astype(WIDE)).astype(LOW)
        to_far.start()

    @pl.when(step == slots - 1)
    def _():
        bias_out[...] = jnp.sum(line_all[...].astype(WIDE), axis=0, keepdims=True)

    @pl.when(step >= slots)
    def _():
        pl.when(step == slots)(loading.wait)
        up_out[...] = dot_rows(turned[...], held[...]).astype(LOW)
        cols = line_all.shape[1]
        attn_out[:, :cols] = dot_rows(rows_one[...], line_all[...]).astype(LOW)
        attn_out[:, cols:] = dot_rows(branch[...], mixed[...]).astype(LOW)

    @pl.when(step == slots + tiles - 1)
    def _():
        cores[1].wait_recv()
        to_far.wait_recv()
        upstream = total[...] + core_in[1].astype(WIDE) + far_in[...].astype(WIDE)
        values = own_in[...].astype(WIDE)
        inverse = lax.rsqrt(jnp.mean(values * values, axis=-1, keepdims=True) + EPS)
        grad_in, gain_grad[...] = norm_backward(values, inverse, gain[...], upstream)
        share[...] = (grad_middle[...] + grad_in).astype(LOW)
        for copy in (*cores, to_far):
            copy.wait_send()


def finish_rows(line, weight, own_in, grad_middle, gain, rows_two, grad_up, rows_one, branch, mixed):
    length, width = own_in.shape
    tokens, cols = grad_up.shape
    near_tokens, line_cols = line.shape
    slots, tile = near_tokens // length, 256
    tiles = width // tile
    once = whole_spec(length, width, once=True)
    column = lambda i: jnp.clip(i - slots, 0, tiles - 1)
    by_column = lambda n: pl.BlockSpec((n, tile), lambda i: (0, column(i)))
    attn_cols = line_cols + mixed.shape[1]
    return pl.pallas_call(
        functools.partial(line_kernel, slots, tiles),
        grid=(slots + tiles,),
        in_specs=[
            pl.BlockSpec((length, line_cols), lambda i: (jnp.maximum(slots - 1 - i, 0), 0)),
            whole_spec(width, line_cols, once=True),
            once,
            once,
            whole_spec(1, width),
            by_column(tokens),
            ANYWHERE,
            by_column(near_tokens),
            by_column(near_tokens),
            whole_spec(near_tokens, line_cols, once=True),
            whole_spec(*mixed.shape, once=True),
        ],
        out_specs=[
            whole_spec(length, width),
            whole_spec(1, width),
            pl.BlockSpec((tile, cols), lambda i: (column(i), 0)),
            pl.BlockSpec((tile, attn_cols), lambda i: (column(i), 0)),
            whole_spec(1, line_cols),
        ],
        out_shape=[
            jax.ShapeDtypeStruct((length, width), LOW),
            jax.ShapeDtypeStruct((1, width), WIDE),
            jax.ShapeDtypeStruct((width, cols), LOW),
            jax.ShapeDtypeStruct((width, attn_cols), LOW),
            jax.ShapeDtypeStruct((1, line_cols), WIDE),
        ],
        scratch_shapes=[
            pltpu.VMEM((slots, length, width), LOW),
            pltpu.VMEM((2, length, width), LOW),
            pltpu.VMEM((length, width), LOW),
            pltpu.VMEM((length, width), WIDE),
            pltpu.VMEM((tokens, cols), LOW),
            pltpu.SemaphoreType.DMA((3,)),
            pltpu.SemaphoreType.DMA((3,)),
            pltpu.SemaphoreType.DMA,
        ],
        compiler_params=pltpu.CompilerParams(
            vmem_limit_bytes=63 << 20, collective_id=3, has_side_effects=True
        ),
        cost_estimate=estimate(2 * tokens * width * cols, 10 * tokens * cols),
    )(line, weight, own_in, grad_middle, gain, rows_two, grad_up, rows_one, branch, line, mixed)


def turn(values, cosine, sine_signed):
    return values * cosine + pltpu.roll(values, values.shape[-1] // 2, 1) * sine_signed


def turn_back(values, cosine, sine_signed):
    return values * cosine - pltpu.roll(values, values.shape[-1] // 2, 1) * sine_signed


def project_kernel(
    heads, head_dim, x0, x1, x2, x3, gains, weight, bias, cosine, sine, h_out, q_out, k_out, v_out, gain
):
    slot = pl.program_id(0)

    @pl.when(slot == 0)
    def _():
        gain[...] = gains[...].astype(WIDE).T[:8]


    def run(x_ref):
        x = x_ref[...].astype(WIDE)
        scale_inv = lax.rsqrt(jnp.mean(x * x, axis=-1, keepdims=True) + EPS)
        normed = (x * scale_inv * gain[0:1]).astype(LOW)
        h_out[0] = normed
        lin = jnp.dot(normed, weight[...], preferred_element_type=WIDE) + bias[...]
        cos, sin = cosine[0], sine[0]
        for h in range(heads + 1):
            part = turn(lin[:, h * head_dim : (h + 1) * head_dim], cos, sin).astype(LOW)
            if h < heads:
                q_out[0, :, h * head_dim : (h + 1) * head_dim] = part
            else:
                k_out[0] = part
        v_out[0] = lin[:, (heads + 1) * head_dim :].astype(LOW)

    for r, x_ref in enumerate((x0, x1, x2, x3)):
        pl.when(slot == r)(functools.partial(run, x_ref))


def project(rows, held, bias, cosine, sine, heads, head_dim):
    length, width = rows[0].shape
    count = len(rows)
    cols = (heads + 2) * head_dim
    whole = whole_spec
    by_slot = lambda *shape: pl.BlockSpec((1, *shape), lambda s: (s,) + (0,) * len(shape))
    return pl.pallas_call(
        functools.partial(project_kernel, heads, head_dim),
        grid=(count,),
        in_specs=[whole(length, width)] * count
        + [part_spec(width, 128, cols // 128), part_spec(width, cols, 0), whole(1, cols)]
        + [by_slot(length, head_dim)] * 2,
        out_specs=[
            by_slot(length, width),
            by_slot(length, heads * head_dim),
            by_slot(length, head_dim),
            by_slot(length, head_dim),
        ],
        out_shape=[
            jax.ShapeDtypeStruct((count, length, width), LOW),
            jax.ShapeDtypeStruct((count, length, heads * head_dim), LOW),
            jax.ShapeDtypeStruct((count, length, head_dim), LOW),
            jax.ShapeDtypeStruct((count, length, head_dim), LOW),
        ],
        scratch_shapes=[pltpu.VMEM((8, width), WIDE)],
        compiler_params=pltpu.CompilerParams(vmem_limit_bytes=56 << 20),
        cost_estimate=pl.CostEstimate(
            flops=2 * count * length * width * cols,
            bytes_accessed=count * length * (2 * width + cols) * 2 + width * cols * 2,
            transcendentals=0,
        ),
    )(*rows, held, held, bias, cosine, sine)


def row_blocks(length):
    return [(i, min(256, length)) for i in range(0, length, min(256, length))]


def key_biases(length, offset, start, rows, past, keys):
    past_pos = lax.broadcasted_iota(jnp.int32, (1, past), 1)
    past_bias = jnp.where((past_pos < offset) & (past_pos < length), 0.0, NEG_FILL)
    query_pos = offset + start + lax.broadcasted_iota(jnp.int32, (rows, keys), 0)
    own_pos = offset + lax.broadcasted_iota(jnp.int32, (rows, keys), 1)
    own_bias = jnp.where((own_pos <= query_pos) & (own_pos < length), 0.0, NEG_FILL)
    return past_bias, own_bias


def dot_cols(left, right):
    return lax.dot_general(left, right, (((1,), (1,)), ((), ())), preferred_element_type=WIDE)


def dot_rows(left, right):
    return lax.dot_general(left, right, (((0,), (0,)), ((), ())), preferred_element_type=WIDE)


def attend_kernel(
    heads, head_dim, scale, first, total_slots, info, q, k_past, v_past, k_own, v_own, weight, out, lse, *parts
):
    length, offset = info[first + pl.program_id(0)], info[total_slots]
    past = k_past.shape[1]
    for start, rows in row_blocks(q.shape[1]):
        keys = start + rows
        past_bias, own_bias = key_biases(length, offset, start, rows, past, keys)
        here = slice(start, start + rows)
        for h in range(heads):
            cols = slice(h * head_dim, (h + 1) * head_dim)
            query = q[0, here, cols]
            s_past = dot_cols(query, k_past[0]) * scale + past_bias
            s_own = dot_cols(query, k_own[0, :keys]) * scale + own_bias
            top = jnp.maximum(
                jnp.max(s_past, axis=1, keepdims=True), jnp.max(s_own, axis=1, keepdims=True)
            )
            e_past, e_own = jnp.exp(s_past - top), jnp.exp(s_own - top)
            total = jnp.sum(e_past, axis=1, keepdims=True) + jnp.sum(e_own, axis=1, keepdims=True)
            inverse = 1.0 / total
            mixed = jnp.dot(
                (e_past * inverse).astype(LOW), v_past[0], preferred_element_type=WIDE
            ) + jnp.dot((e_own * inverse).astype(LOW), v_own[0, :keys], preferred_element_type=WIDE)
            out[0, here, cols] = mixed.astype(LOW)
            lse[0, here, h : h + 1] = top + jnp.log(total)
        rows_out = dot_cols(out[0, here], weight[...]).astype(LOW)
        for i, part in enumerate(parts):

            @pl.when(pl.program_id(0) == i)
            def _():
                part[here] = rows_out


def attend_forward(info, q, k_past, v_past, k_own, v_own, weight, heads, head_dim, scale, first, count):
    _, length, width = q.shape
    past = k_past.shape[1]
    by_slot = lambda *shape: pl.BlockSpec((1, *shape), lambda s, info: (first + s,) + (0,) * len(shape))
    out_slot = lambda *shape: pl.BlockSpec((1, *shape), lambda s, info: (s,) + (0,) * len(shape))
    keys = count * length * (past + length) * heads
    return pl.pallas_call(
        functools.partial(attend_kernel, heads, head_dim, scale, first, q.shape[0]),
        grid_spec=pltpu.PrefetchScalarGridSpec(
            num_scalar_prefetch=1,
            grid=(count,),
            in_specs=[
                by_slot(length, width),
                by_slot(past, head_dim),
                by_slot(past, head_dim),
                by_slot(length, head_dim),
                by_slot(length, head_dim),
                whole_spec(*weight.shape, once=True),
            ],
            out_specs=[out_slot(length, width), out_slot(length, 128)]
            + [whole_spec(length, weight.shape[0])] * count,
        ),
        out_shape=[
            jax.ShapeDtypeStruct((count, length, width), LOW),
            jax.ShapeDtypeStruct((count, length, 128), WIDE),
        ]
        + [jax.ShapeDtypeStruct((length, weight.shape[0]), LOW)] * count,
        compiler_params=pltpu.CompilerParams(vmem_limit_bytes=56 << 20),
        cost_estimate=estimate(4 * keys * head_dim, 4 * count * length * width, keys),
    )(info, q, k_past, v_past, k_own, v_own, weight)


def attend_back_kernel(
    heads,
    head_dim,
    scale,
    info,
    q,
    k_past,
    v_past,
    k_own,
    v_own,
    grad,
    lse,
    cosine,
    sine,
    dq_out,
    mine_past,
    mine_own,
    other_past,
    other_own,
    dk_past,
    dk_own,
    dv_past,
    dv_own,
):
    slot = pl.program_id(0)
    length, offset = info[slot], info[pl.num_programs(0)]
    parity = info[pl.num_programs(0) + 1]
    past = k_past.shape[1]
    for total in (dk_past, dk_own, dv_past, dv_own):
        total[...] = jnp.zeros_like(total)
    for start, rows in row_blocks(q.shape[1]):
        keys = start + rows
        past_bias, own_bias = key_biases(length, offset, start, rows, past, keys)
        here = slice(start, start + rows)
        cos, sin = cosine[0, here], sine[0, here]
        for h in range(heads):
            cols = slice(h * head_dim, (h + 1) * head_dim)
            query, upstream = q[0, here, cols], grad[0, here, cols]
            log_total = lse[0, here, h : h + 1]
            p_past = jnp.exp(dot_cols(query, k_past[0]) * scale + past_bias - log_total)
            p_own = jnp.exp(dot_cols(query, k_own[0, :keys]) * scale + own_bias - log_total)
            g_past = dot_cols(upstream, v_past[0])
            g_own = dot_cols(upstream, v_own[0, :keys])
            row_dot = jnp.sum(p_past * g_past, axis=1, keepdims=True) + jnp.sum(
                p_own * g_own, axis=1, keepdims=True
            )
            s_past = (p_past * (g_past - row_dot)).astype(LOW)
            s_own = (p_own * (g_own - row_dot)).astype(LOW)
            dq = (
                jnp.dot(s_past, k_past[0], preferred_element_type=WIDE)
                + jnp.dot(s_own, k_own[0, :keys], preferred_element_type=WIDE)
            ) * scale
            dq_out[0, here, cols] = turn_back(dq, cos, sin).astype(LOW)
            dk_past[...] += dot_rows(s_past, query)
            dk_own[:keys] += dot_rows(s_own, query)
            dv_past[...] += dot_rows(p_past.astype(LOW), upstream)
            dv_own[:keys] += dot_rows(p_own.astype(LOW), upstream)

    @pl.when(parity == 0)
    def _():
        mine_past[0] = dk_past[...] * scale
        mine_own[0] = dk_own[...] * scale
        other_past[0] = dv_past[...]
        other_own[0] = dv_own[...]

    @pl.when(parity != 0)
    def _():
        mine_past[0] = dv_past[...]
        mine_own[0] = dv_own[...]
        other_past[0] = dk_past[...] * scale
        other_own[0] = dk_own[...] * scale


def attend_backward(
    info, q, k_past, v_past, k_own, v_own, grad, lse, cosine, sine, heads, head_dim, scale
):
    count, length, width = q.shape
    past = k_past.shape[1]
    by_slot = lambda *shape: pl.BlockSpec((1, *shape), lambda s, info: (s,) + (0,) * len(shape))
    keys = count * length * (past + length) * heads
    return pl.pallas_call(
        functools.partial(attend_back_kernel, heads, head_dim, scale),
        grid_spec=pltpu.PrefetchScalarGridSpec(
            num_scalar_prefetch=1,
            grid=(count,),
            in_specs=[
                by_slot(length, width),
                by_slot(past, head_dim),
                by_slot(past, head_dim),
                by_slot(length, head_dim),
                by_slot(length, head_dim),
                by_slot(length, width),
                by_slot(length, 128),
                by_slot(length, head_dim),
                by_slot(length, head_dim),
            ],
            out_specs=[
                by_slot(length, width),
                by_slot(past, head_dim),
                by_slot(length, head_dim),
                by_slot(past, head_dim),
                by_slot(length, head_dim),
            ],
            scratch_shapes=[
                pltpu.VMEM((past, head_dim), WIDE),
                pltpu.VMEM((length, head_dim), WIDE),
                pltpu.VMEM((past, head_dim), WIDE),
                pltpu.VMEM((length, head_dim), WIDE),
            ],
        ),
        out_shape=[
            jax.ShapeDtypeStruct((count, length, width), LOW),
            jax.ShapeDtypeStruct((count, past, head_dim), WIDE),
            jax.ShapeDtypeStruct((count, length, head_dim), WIDE),
            jax.ShapeDtypeStruct((count, past, head_dim), WIDE),
            jax.ShapeDtypeStruct((count, length, head_dim), WIDE),
        ],
        compiler_params=pltpu.CompilerParams(vmem_limit_bytes=56 << 20),
        cost_estimate=estimate(10 * keys * head_dim, 8 * count * length * width, keys),
    )(info, q, k_past, v_past, k_own, v_own, grad, lse, cosine, sine)


def local(
    hidden_in,
    cotangent,
    seq_lengths,
    positions,
    permutation,
    query_weight,
    keyval_weight,
    output_weight,
    norm_gains,
    bias_query,
    bias_keyval,
    gate_weight,
    up_weight,
    down_weight,
):
    group_rank = lax.axis_index("fsdp")
    ctx_rank = lax.axis_index("ctx")
    tensor_rank = lax.axis_index("tp")
    fsdp_count = lax.axis_size("fsdp")
    ctx_count = lax.axis_size("ctx")
    tensor_count = lax.axis_size("tp")
    seq_grp, local_len, model_width = hidden_in.shape
    heads, head_dim = bias_query.shape
    keyval_heads = bias_keyval.shape[0] // 2
    assert seq_grp == tensor_count == fsdp_count == len(DEAL_SHIFT)
    token_count = seq_grp * local_len
    scale = 1.0 / math.sqrt(head_dim)
    offset = ctx_rank * local_len
    head_pair = tensor_rank // (tensor_count // keyval_heads)
    parity = tensor_rank % 2
    shifts = jnp.array(DEAL_SHIFT, jnp.int32)

    table = permutation.reshape(fsdp_count, seq_grp)
    far_group = lax.rem(group_rank + shifts[tensor_rank], fsdp_count)
    far_row = lax.dynamic_index_in_dim(table, far_group, 0, keepdims=False)
    leaving = jnp.sum(jnp.where(far_row // seq_grp == group_rank, far_row - group_rank * seq_grp, 0))
    own_row = lax.dynamic_index_in_dim(table, group_rank, 0, keepdims=False)
    slot_now, seq_now, home_now = [], [], []
    for r in range(seq_grp):
        shift = shifts[tensor_rank ^ r]
        source = lax.rem(group_rank - shift + fsdp_count, fsdp_count)
        hit = own_row // seq_grp == source
        slot_now.append(jnp.sum(jnp.where(hit, jnp.arange(seq_grp), 0)))
        seq_now.append(jnp.sum(jnp.where(hit, own_row, 0)))
        target = lax.rem(group_rank + shift, fsdp_count)
        target_row = lax.dynamic_index_in_dim(table, target, 0, keepdims=False)
        home_now.append(
            jnp.sum(jnp.where(target_row // seq_grp == group_rank, target_row - group_rank * seq_grp, 0))
        )
    there = [
        (f * tensor_count + t, (f + DEAL_SHIFT[t]) % fsdp_count * tensor_count + t)
        for f in range(fsdp_count)
        for t in range(tensor_count)
    ]
    back = [(target, source) for source, target in there]

    split = units_split()
    head_width = 2 * head_dim
    query_cols = heads * head_dim
    near_cols = query_cols + head_width + 128

    outgoing = lax.dynamic_index_in_dim(hidden_in, leaving, 0, keepdims=False)
    own_in = lax.ppermute(outgoing, ("fsdp", "tp"), there)
    small = jnp.concatenate(
        [
            query_weight,
            lax.dynamic_slice_in_dim(keyval_weight, head_pair * head_width, head_width, axis=1),
            jnp.pad(norm_gains.T, ((0, 0), (0, 128 - norm_gains.shape[0]))),
            output_weight.T,
        ],
        axis=1,
    )
    units = gate_weight.shape[1]
    units_pad = -(-units // 256) * 256
    widen = lambda w: jnp.pad(w, ((0, 0), (0, units_pad - units)))
    shards = [widen(w) for w in (down_weight.T, gate_weight, up_weight)]
    if split:
        half_units = units_pad // 2
        cut = lambda w, c: lax.dynamic_slice_in_dim(w, c * half_units, half_units, axis=1)

        def in_order(own, other):
            return jnp.stack(
                [jnp.where(ctx_rank == 0, own, other), jnp.where(ctx_rank == 0, other, own)]
            )

        def all_rows(both, *earlier):
            full = lax.all_gather(after(both, *earlier), "fsdp", axis=0, tiled=False)
            return full.reshape(-1, both.shape[-1])

        small_both = in_order(small, from_partner(after(small, outgoing), "ctx", 1))
        leaving_units = jnp.concatenate([cut(w, 1 - ctx_rank) for w in shards], axis=1)
        arriving_units = from_partner(after(leaving_units, small), "ctx", 1)
        own_units = jnp.concatenate([cut(w, ctx_rank) for w in shards], axis=1)
        unit_both = in_order(own_units, arriving_units)
    else:
        all_rows = lambda shard, *earlier: lax.all_gather(
            shard, ("fsdp", "ctx"), axis=0, tiled=True
        )
        small_both, unit_both, half_units = small, jnp.concatenate(shards, axis=1), units_pad
    far_in = from_partner(own_in, "tp", 2)
    near_in = from_partner(own_in, "tp", 1)
    cross_in = from_partner(far_in, "tp", 1)

    lengths_now = jnp.stack([seq_lengths[s] for s in seq_now])
    info = jnp.concatenate([lengths_now, jnp.stack([offset, parity])]).astype(jnp.int32)
    positions_now = jnp.stack(
        [lax.dynamic_index_in_dim(positions, s, 0, keepdims=False) for s in seq_now]
    )
    lane = jnp.arange(head_dim)
    frequency = 1.0 / ROPE_BASE ** ((lane % (head_dim // 2)).astype(WIDE) * 2.0 / head_dim)
    angles = positions_now.astype(WIDE)[..., None] * frequency
    cosine = jnp.cos(angles)
    sine = jnp.sin(angles) * jnp.where(lane < head_dim // 2, -1.0, 1.0)
    grad_slots = [lax.dynamic_index_in_dim(cotangent, s, 0, keepdims=False) for s in slot_now]

    near_full = all_rows(small_both, own_in)
    down_full = all_rows(unit_both[..., :half_units], cross_in)
    gate_up_full = all_rows(unit_both[..., half_units:], cross_in)
    project_full = near_full[:, : query_cols + head_width]
    output_full = near_full[:, near_cols:]
    bias_head = lax.dynamic_slice_in_dim(bias_keyval, head_pair * 2, 2, axis=0)
    bias_row = jnp.concatenate([bias_query.reshape(1, -1), bias_head.reshape(1, -1)], axis=1).astype(WIDE)
    normed_one, query_rot, key_own, value_own = project(
        (own_in, near_in, far_in, cross_in),
        near_full,
        bias_row,
        cosine,
        sine,
        heads,
        head_dim,
    )
    gains_now = near_full[:, query_cols + head_width : near_cols][:, :2].astype(WIDE).T
    if split:
        key_past, value_past = lax.ppermute((key_own, value_own), "ctx", [(0, 1)])
        grad_pair = after(jnp.stack([grad_slots[0], grad_slots[2]]), value_past)
        other_pair = from_partner(grad_pair, "ctx", 1)
        cross_pair = functools.partial(from_partner, axis="tp", apart=1)
    else:
        key_past = lax.all_gather(key_own, "ctx", axis=1, tiled=True)
        value_past = lax.all_gather(value_own, "ctx", axis=1, tiled=True)
    attend = lambda first, *held: attend_forward(
        info, query_rot, *held, key_own, value_own, output_full, heads, head_dim, scale, first, 2
    )
    in_share = own_in.astype(WIDE)

    mixed_far, lse_far, *attn_far = attend(2, key_past, value_past)
    attn_wide = collect_far(attn_far[0], attn_far[1])
    attn_got = from_partner(attn_wide, "tp", 2)
    mixed_near, lse_near, *attn_near = attend(0, after(key_past, attn_wide), value_past)
    attn_core = from_partner(attn_near[1], "tp", 1)
    middle_share = (
        in_share
        + attn_near[0].astype(WIDE)
        + attn_core.astype(WIDE)
        + attn_got.astype(WIDE)
    )
    inv_two = lax.rsqrt(jnp.mean(middle_share * middle_share, axis=-1, keepdims=True) + EPS)
    normed_share = (middle_share * inv_two * gains_now[1]).astype(LOW)
    half_len = local_len // 2

    others = []
    if split:
        cross_pair = cross_pair(after(other_pair, normed_share))
        others = [other_pair[0], cross_pair[0], other_pair[1], cross_pair[1]]

    grad_hidden, grad_rows = stack_rows(
        [(after(grad_slots[0], normed_share),)] + [(g,) for g in grad_slots[1:] + others], down_full, 0, 1
    )

    def spread_all(own):
        far = from_partner(own, "tp", 2)
        near = from_partner(own, "tp", 1)
        if not split:
            return (own, near, far, from_partner(far, "tp", 1))
        side = from_partner(own, "ctx", 1)
        held = after(far, grad_hidden), after(side, grad_hidden)
        across = from_partner(held[0][:half_len], "ctx", 1), from_partner(held[1][half_len:], "tp", 2)
        cores = [from_partner(v, "tp", 1) for v in (*held, *across)]
        return (own, near, far, cores[0], side, cores[1], *across, *cores[2:])

    def in_slots(rows):
        if not split:
            return [(row,) for row in rows]
        return [(row,) for row in rows[:6]] + [rows[6:8], rows[8:]]

    gate_lin, normed_two = stack_rows(in_slots(spread_all(normed_share)), gate_up_full, 0, 2)
    hidden_act, grad_gate, grad_up = hidden_units(
        normed_two, gate_up_full, 1, 2, gate_lin, grad_hidden
    )

    def collect_all(lefts, weights, *earlier):
        lefts = list(lefts)
        lefts[0] = after(lefts[0], *earlier)
        last = back_rows(lefts, weights, 2, 2, local_len)
        got = [from_partner(collect_far(last[0], last[1]), "tp", 2)]
        first = back_rows(lefts, weights, 0, 2, local_len)
        got.append(from_partner(first[1], "tp", 1))

        def finish():
            return sum((v.astype(WIDE) for v in got), first[0].astype(WIDE))

        return first[0], finish

    if split:
        grad_two_share, down_grad = collect_back(
            grad_gate, grad_up, gate_up_full, grad_rows, hidden_act, local_len
        )
        grad_middle, gain_two, gate_grad, grad_branch, *mlp = spread_branch(
            grad_two_share,
            middle_share,
            grad_slots[0],
            gains_now[1:2],
            hidden_act,
            down_full,
            normed_two,
            grad_gate,
        )
        grad_branch = grad_branch.reshape(token_count, model_width)
    else:
        first_back, finish_back = collect_all(
            (grad_gate, grad_up), ((gate_up_full, 0, 2), (gate_up_full, 1, 2))
        )
        down_grad = contract_rows(after(grad_rows, first_back), hidden_act, LOW)
        gate_grad = contract_rows(normed_two, after(grad_gate, down_grad), LOW)
        grad_two_share = finish_back()
        grad_norm_two, gain_two = norm_backward(
            middle_share, inv_two, gains_now[1], grad_two_share
        )
        grad_middle = grad_slots[0].astype(WIDE) + grad_norm_two
        branch_own = grad_middle.astype(LOW)
        branch_far = from_partner(branch_own, "tp", 2)
        branch_near = from_partner(branch_own, "tp", 1)
        branch_cross = from_partner(branch_far, "tp", 1)
        grad_branch = jnp.concatenate([branch_own, branch_near, branch_far, branch_cross], axis=0)
        up_grad = contract_rows(normed_two, after(grad_up, branch_own), LOW)

    grad_mixed = product(grad_branch, output_full, LOW)
    mixed_flat = jnp.concatenate([mixed_near, mixed_far], axis=0).reshape(token_count, query_cols)
    lse = jnp.concatenate([lse_near, lse_far], axis=0)
    grad_query, mine_past, mine_own, other_past, other_own = attend_backward(
        info,
        query_rot,
        key_past,
        value_past,
        key_own,
        value_own,
        grad_mixed.reshape(seq_grp, local_len, query_cols),
        lse,
        cosine,
        sine,
        heads,
        head_dim,
        scale,
    )
    swap = lambda value: jnp.stack([value[r ^ 1] for r in range(seq_grp)])
    got_past, got_own = from_partner((other_past, other_own), "tp", 1)
    past_sum = mine_past + swap(got_past)
    own_sum = mine_own + swap(got_own)
    if split:
        own_sum = own_sum + lax.ppermute(past_sum.astype(LOW), "ctx", [(1, 0)]).astype(WIDE)
    else:
        own_sum = own_sum + lax.psum_scatter(past_sum, "ctx", scatter_dimension=1, tiled=True)
    half_lanes = head_dim // 2
    turned = own_sum * cosine - jnp.roll(own_sum, half_lanes, axis=-1) * sine
    own_grad = jnp.where(parity == 0, turned, own_sum).astype(LOW).reshape(token_count, head_dim)
    line_grad = jnp.concatenate([grad_query.reshape(token_count, query_cols), own_grad], axis=1)
    own_weight = lax.dynamic_slice_in_dim(
        project_full, query_cols + parity * head_dim, head_dim, axis=1
    )
    back_full = jnp.concatenate([project_full[:, :query_cols], own_weight], axis=1)
    normed_flat = normed_one.reshape(token_count, model_width)
    if split:
        mlp_own, mlp_far, mlp_side, mlp_first, mlp_second = mlp
        got_first = from_partner(mlp_first, "tp", 2).astype(WIDE)
        got_second = from_partner(mlp_second, "ctx", 1).astype(WIDE)
        add_half = lambda rows, low, high: jnp.concatenate(
            [
                rows[:half_len] if low is None else (rows[:half_len].astype(WIDE) + low).astype(LOW),
                rows[half_len:] if high is None else (rows[half_len:].astype(WIDE) + high).astype(LOW),
            ],
            axis=0,
        )
        mlp_sum = (
            mlp_own.astype(WIDE)
            + from_partner(add_half(mlp_far, None, got_second), "tp", 2).astype(WIDE)
            + from_partner(add_half(mlp_side, got_first, None), "ctx", 1).astype(WIDE)
        )
        block_share = (middle_share + mlp_sum).astype(LOW)
        input_share, gain_one, up_grad, attn_grad, bias_grad = finish_rows(
            line_grad,
            back_full,
            own_in,
            grad_middle,
            gains_now[0:1],
            normed_two,
            grad_up,
            normed_flat,
            grad_branch,
            mixed_flat,
        )
    else:
        half = token_count // 2
        line_far = contract_cols(line_grad[half:], back_full, LOW).reshape(2, local_len, model_width)
        line_near = contract_cols(line_grad[:half], back_full, LOW).reshape(2, local_len, model_width)
        line_wide = collect_far(line_far[0], line_far[1])
        line_got = from_partner(line_wide, "tp", 2)
        line_core = from_partner(line_near[1], "tp", 1)
        first_mlp, finish_mlp = collect_all((hidden_act,), ((down_full, 0, 1),), up_grad, branch_far)
        block_share = (middle_share + finish_mlp()).astype(LOW)
        grad_one_share = line_near[0].astype(WIDE) + line_core.astype(WIDE) + line_got.astype(WIDE)
        inv_one = lax.rsqrt(jnp.mean(in_share * in_share, axis=-1, keepdims=True) + EPS)
        grad_norm_one, gain_one = norm_backward(in_share, inv_one, gains_now[0], grad_one_share)
        input_share = (grad_middle + grad_norm_one).astype(LOW)
        attn_grad = jnp.concatenate(
            [contract_rows(normed_flat, line_grad, LOW), contract_rows(grad_branch, mixed_flat, LOW)],
            axis=1,
        )
        bias_grad = jnp.sum(line_grad.astype(WIDE), axis=0)

    def scatter_units(grad):
        if not split:
            return scatter_sum(grad, ctx_rank, LOW)
        return lax.psum_scatter(grad, "fsdp", scatter_dimension=0, tiled=True)

    unit_sums = [scatter_units(g) for g in (down_grad, gate_grad, up_grad)]

    attn_end = scatter_sum(attn_grad, ctx_rank, LOW, *unit_sums)

    def leave(share):
        return lax.ppermute(share, ("fsdp", "tp"), back)

    def arrive(own, *earlier):
        far = from_partner(after(own, *earlier), "tp", 2)
        near = from_partner(own, "tp", 1)
        cross = from_partner(far, "tp", 1)
        out = jnp.zeros((seq_grp, local_len, model_width), LOW)
        for home, row in zip(home_now, (own, near, far, cross)):
            out = lax.dynamic_update_index_in_dim(out, row, home, 0)
        return out

    block_home = leave(block_share)
    input_home = leave(input_share)
    block_out = arrive(block_home, input_share)
    input_grad = arrive(input_home)

    gain_grad = jnp.concatenate([gain_one, gain_two], axis=0).T
    gain_grad = gain_grad + from_partner(gain_grad, "tp", 1)
    gain_grad = gain_grad + from_partner(gain_grad, "tp", 2)
    shard_count = fsdp_count * ctx_count
    share = head_dim // shard_count
    bias_cols = jnp.transpose(bias_grad.reshape(heads + 1, shard_count, share), (1, 2, 0))
    bias_cols = jnp.pad(bias_cols, ((0, 0), (0, (model_width - head_dim) // shard_count), (0, 0)))
    tiny = jnp.concatenate([gain_grad, bias_cols.reshape(model_width, heads + 1)], axis=1)
    tiny = jnp.pad(tiny, ((0, 0), (0, 8 - tiny.shape[1])))
    tiny = tiny.reshape(fsdp_count, ctx_count, model_width // shard_count, 8)
    if split:
        kept, sent = scatter_ctx(tiny, ctx_rank)
        tiny = kept + from_partner(sent, "ctx", 1)
    else:
        tiny = lax.psum_scatter(tiny, "ctx", scatter_dimension=1, tiled=True)
    tiny = tiny.reshape(fsdp_count, -1, 8)
    pick = lambda shift: lax.dynamic_index_in_dim(
        tiny, lax.rem(group_rank + shift, fsdp_count), 0, keepdims=False
    )
    tiny_grad = pick(0)
    for shift in range(1, fsdp_count):
        pairs = [(f, (f + shift) % fsdp_count) for f in range(fsdp_count)]
        tiny_grad = tiny_grad + lax.ppermute(pick(shift), "fsdp", pairs)

    def unit_end(total):
        if split:
            blocks = total.reshape(1, ctx_count, -1, half_units)
            kept, sent = scatter_ctx(blocks, ctx_rank)
            kept, got = kept[0], from_partner(sent[0], "ctx", 1)
            first = jnp.where(ctx_rank == 0, kept, got)
            second = jnp.where(ctx_rank == 0, got, kept)
            total = jnp.concatenate([first, second], axis=1)
        return total[:, :units].astype(WIDE)

    down_end, gate_end, up_end = (unit_end(after(t, input_share)) for t in unit_sums)
    return (
        block_out,
        input_grad,
        attn_end[:, :query_cols].astype(WIDE),
        attn_end[:, query_cols : query_cols + head_dim].astype(WIDE),
        attn_end[:, query_cols + head_dim :].astype(WIDE).T,
        tiny_grad[:, :2].T,
        tiny_grad[:share, 2 : 2 + heads].T,
        tiny_grad[:share, 2 + heads : 3 + heads].T,
        gate_end,
        up_end,
        down_end.T,
    )


def solution(mesh):
    placed = (
        P("fsdp", "ctx", None),
        P("fsdp", "ctx", None),
        P(),
        P(None, "ctx"),
        P(),
        P(("fsdp", "ctx"), "tp"),
        P(("fsdp", "ctx"), None),
        P("tp", ("fsdp", "ctx")),
        P(None, ("fsdp", "ctx")),
        P("tp", None),
        P(),
        P(("fsdp", "ctx"), "tp"),
        P(("fsdp", "ctx"), "tp"),
        P("tp", ("fsdp", "ctx")),
    )
    return jax.shard_map(
        local,
        mesh=mesh,
        in_specs=placed,
        out_specs=(
            P("fsdp", "ctx", None),
            P("fsdp", "ctx", None),
            P(("fsdp", "ctx"), "tp"),
            P(("fsdp", "ctx"), "tp"),
            P("tp", ("fsdp", "ctx")),
            P(None, ("fsdp", "ctx")),
            P("tp", ("fsdp", "ctx")),
            P("tp", ("fsdp", "ctx")),
            P(("fsdp", "ctx"), "tp"),
            P(("fsdp", "ctx"), "tp"),
            P("tp", ("fsdp", "ctx")),
        ),
        check_vma=False,
    )
```

```python
import functools
import math

import jax
import jax.numpy as jnp
from jax import lax
from jax.experimental import pallas as pl
from jax.experimental.pallas import tpu as pltpu
from jax.sharding import PartitionSpec as P

EPS = 1e-06
ROPE_BASE = 10000.0
NEG_FILL = -1e30
LOW = jnp.bfloat16
WIDE = jnp.float32
DEAL_SHIFT = (0, 2, 1, 3)


def from_partner(value, axis, apart):
    pairs = [(source, source ^ apart) for source in range(lax.axis_size(axis))]
    return lax.ppermute(value, axis, pairs)


def product(left_side, right_side, kind=WIDE):
    return jnp.dot(left_side, right_side, preferred_element_type=WIDE).astype(kind)


def contract_rows(left_side, right_side, kind=WIDE):
    return lax.dot_general(
        left_side, right_side, (((0,), (0,)), ((), ())), preferred_element_type=WIDE
    ).astype(kind)


def contract_cols(left_side, right_side, kind=WIDE):
    return lax.dot_general(
        left_side, right_side, (((1,), (1,)), ((), ())), preferred_element_type=WIDE
    ).astype(kind)


def norm_backward(values, scale_inv, gain_row, upstream):
    scaled = gain_row * upstream
    inner_mean = jnp.mean(values * scaled, axis=-1, keepdims=True)
    grad_in = scale_inv * scaled - values * (scale_inv * scale_inv * scale_inv) * inner_mean
    gain_grad = jnp.sum(upstream * values * scale_inv, axis=0, keepdims=True)
    return (grad_in, gain_grad)


def after(value, *earlier):
    return lax.optimization_barrier((value, *earlier))[0]


def collect_far(far_part, cross_part):
    wide = far_part.astype(WIDE) + from_partner(cross_part, "tp", 1).astype(WIDE)
    return wide.astype(LOW)


def units_split():
    return lax.axis_size("ctx") == 2


def all_rows(shard):
    return lax.all_gather(shard, "fsdp", axis=0, tiled=True)


def scatter_ctx(blocks, ctx_rank):
    kept = lax.dynamic_index_in_dim(blocks, ctx_rank, 1, keepdims=False)
    sent = lax.dynamic_index_in_dim(blocks, 1 - ctx_rank, 1, keepdims=False)
    return kept, sent


def scatter_sum(grad, ctx_rank, kind, *earlier):
    fsdp_count, ctx_count = lax.axis_size("fsdp"), lax.axis_size("ctx")
    rows, cols = grad.shape
    blocks = grad.reshape(fsdp_count, ctx_count, rows // (fsdp_count * ctx_count), cols)
    if ctx_count == 2:
        kept, sent = scatter_ctx(blocks, ctx_rank)
        got = from_partner(sent, "ctx", 1)
        held = (after(kept, *earlier).astype(WIDE) + got.astype(WIDE)).astype(kind)
    else:
        swapped = jnp.swapaxes(blocks, 0, 1).reshape(rows, cols)
        held = lax.psum_scatter(swapped, "ctx", scatter_dimension=0, tiled=True)
    held = held.reshape(rows // ctx_count, cols)
    return lax.psum_scatter(held, "fsdp", scatter_dimension=0, tiled=True)


def estimate(flops, moved, transcendentals=0):
    return pl.CostEstimate(flops=flops, bytes_accessed=moved, transcendentals=transcendentals)


def part_spec(rows, cols, part):
    return pl.BlockSpec((rows, cols), lambda *_: (0, part), pipeline_mode=pl.Buffered(1))


def whole_spec(*shape, once=False):
    mode = {"pipeline_mode": pl.Buffered(1)} if once else {}
    return pl.BlockSpec(shape, lambda *_: (0,) * len(shape), **mode)


def rows_kernel(groups, *refs):
    slot = pl.program_id(0)
    weight, lin, stacked = refs[-3:]

    def run(pieces):
        start = 0
        for piece in pieces:
            stacked[start : start + piece.shape[0]] = piece[...]
            start += piece.shape[0]
        lin[...] = jnp.dot(stacked[...], weight[...], preferred_element_type=WIDE).astype(LOW)

    first = 0
    for r, pieces in enumerate(groups):
        pl.when(slot == r)(functools.partial(run, refs[first : first + pieces]))
        first += pieces


def stack_rows(slots, weight, part, parts):
    groups = [len(s) for s in slots]
    rows = [piece for s in slots for piece in s]
    width, length = rows[0].shape[1], sum(piece.shape[0] for piece in slots[0])
    count, cols = len(slots), weight.shape[1] // parts
    return pl.pallas_call(
        functools.partial(rows_kernel, groups),
        grid=(count,),
        in_specs=[whole_spec(*piece.shape, once=True) for piece in rows]
        + [part_spec(width, cols, part)],
        out_specs=[
            pl.BlockSpec((length, cols), lambda s: (s, 0)),
            pl.BlockSpec((length, width), lambda s: (s, 0)),
        ],
        out_shape=[
            jax.ShapeDtypeStruct((count * length, cols), LOW),
            jax.ShapeDtypeStruct((count * length, width), LOW),
        ],
        compiler_params=pltpu.CompilerParams(vmem_limit_bytes=60 << 20),
        cost_estimate=estimate(
            2 * count * length * width * cols, 2 * (count * length * (2 * width + cols) + width * cols)
        ),
    )(*rows, weight)


def units_kernel(h, up, gate, grad, hid, grad_gate, grad_up):
    up_lin = jnp.dot(h[...], up[...], preferred_element_type=WIDE)
    gate_lin = gate[...].astype(WIDE)
    grad_hidden = grad[...].astype(WIDE)
    sigmoid = 1.0 / (1.0 + jnp.exp(-gate_lin))
    silu = gate_lin * sigmoid
    hid[...] = (silu * up_lin).astype(LOW)
    grad_gate[...] = (grad_hidden * up_lin * sigmoid * (1.0 + gate_lin * (1.0 - sigmoid))).astype(LOW)
    grad_up[...] = (grad_hidden * silu).astype(LOW)


def hidden_units(h, up, part, parts, gate_lin, grad_hidden):
    tokens, width = h.shape
    cols = up.shape[1] // parts
    step = math.gcd(512, tokens)
    by_row = lambda n: pl.BlockSpec((step, n), lambda i: (i, 0))
    return pl.pallas_call(
        units_kernel,
        grid=(tokens // step,),
        in_specs=[by_row(width), part_spec(width, cols, part), by_row(cols), by_row(cols)],
        out_specs=[by_row(cols)] * 3,
        out_shape=[jax.ShapeDtypeStruct((tokens, cols), LOW)] * 3,
        compiler_params=pltpu.CompilerParams(vmem_limit_bytes=60 << 20),
        cost_estimate=estimate(
            2 * tokens * width * cols, 2 * (tokens * width + width * cols + 5 * tokens * cols)
        ),
    )(h, up, gate_lin, grad_hidden)


def back_kernel(terms, *refs):
    lefts, weights, outs = refs[:terms], refs[terms : 2 * terms], refs[2 * terms :]
    total = None
    for left, weight in zip(lefts, weights):
        term = dot_cols(left[...], weight[...])
        total = term if total is None else total + term
    for i, out in enumerate(outs):

        @pl.when(pl.program_id(0) == i)
        def _():
            out[...] = total.astype(LOW)


def back_rows(lefts, weights, first_slot, slots, length):
    width = weights[0][0].shape[0]
    depth = sum(left.shape[1] for left in lefts)
    return pl.pallas_call(
        functools.partial(back_kernel, len(lefts)),
        grid=(slots,),
        in_specs=[
            pl.BlockSpec((length, left.shape[1]), lambda s: (first_slot + s, 0)) for left in lefts
        ]
        + [part_spec(width, w.shape[1] // parts, part) for w, part, parts in weights],
        out_specs=[whole_spec(length, width)] * slots,
        out_shape=[jax.ShapeDtypeStruct((length, width), LOW)] * slots,
        compiler_params=pltpu.CompilerParams(vmem_limit_bytes=60 << 20),
        cost_estimate=estimate(
            2 * slots * length * width * depth,
            2 * (slots * length * (width + depth) + width * depth),
        ),
    )(*lefts, *[w for w, _, _ in weights])


MESH_ID = pl.DeviceIdType.MESH


def meet(partners):
    barrier = pltpu.get_barrier_semaphore()
    for partner in partners:
        pl.semaphore_signal(barrier, inc=1, device_id=partner, device_id_type=MESH_ID)
    pl.semaphore_wait(barrier, len(partners))


def partners_of():
    tensor_rank, ctx_rank = lax.axis_index("tp"), lax.axis_index("ctx")
    return {"tp": tensor_rank ^ 1}, {"tp": tensor_rank ^ 2}, {"ctx": ctx_rank ^ 1}


def collect_kernel(
    slots, gate, up, weight_gate, weight_up, left, right, total, grad, parts, core_in, across_in,
    last_in, held, send, recv, load
):
    step = pl.program_id(0)
    steps = pl.num_programs(0)
    core, far, side = partners_of()
    half = total.shape[0] // 2

    def remote(source, target, index, partner):
        return pltpu.make_async_remote_copy(
            source, target, send.at[index], recv.at[index], device_id=partner, device_id_type=MESH_ID
        )

    cores = [remote(parts.at[7 - 2 * k], core_in.at[k], k, core) for k in range(4)]
    across = [
        remote(parts.at[6, pl.ds(0, half)], across_in.at[0], 4, far),
        remote(parts.at[6, pl.ds(half, half)], across_in.at[1], 5, side),
    ]
    lasts = [
        remote(parts.at[2], last_in.at[0], 6, far),
        remote(parts.at[4, pl.ds(half, half)], last_in.at[1, pl.ds(half, half)], 7, side),
        remote(parts.at[4, pl.ds(0, half)], last_in.at[1, pl.ds(0, half)], 8, side),
    ]
    loading = pltpu.make_async_copy(right, held, load)

    @pl.when(step == 0)
    def _():
        loading.start()
        meet((core, far, side))

    @pl.when(step < slots)
    def _():
        part = dot_cols(gate[...], weight_gate[...]) + dot_cols(up[...], weight_up[...])
        parts[slots - 1 - step] = part.astype(LOW)

        @pl.when(step == slots - 1)
        def _():
            total[...] = part

    for k in range(4):
        pl.when(step == 2 * k)(cores[k].start)

    def add(slot, rows, value):
        parts[slot, rows] = (parts[slot, rows].astype(WIDE) + value.astype(WIDE)).astype(LOW)

    whole, low, high = slice(None), pl.ds(0, half), pl.ds(half, half)

    @pl.when(step == 1)
    def _():
        cores[0].wait_recv()
        add(6, whole, core_in[0])
        for copy in across:
            copy.start()

    @pl.when(step == 3)
    def _():
        cores[1].wait_recv()
        add(4, whole, core_in[1])
        lasts[1].start()

    @pl.when(step == 5)
    def _():
        cores[2].wait_recv()
        add(2, whole, core_in[2])
        across[1].wait_recv()
        add(2, high, across_in[1])
        lasts[0].start()
        across[0].wait_recv()
        add(4, low, across_in[0])
        lasts[2].start()

    @pl.when(step >= slots)
    def _():
        pl.when(step == slots)(loading.wait)
        grad[...] = dot_rows(left[...], held[...]).astype(LOW)

    @pl.when(step == steps - 1)
    def _():
        cores[3].wait_recv()
        for copy in lasts:
            copy.wait_recv()
        total[...] += (
            core_in[3].astype(WIDE) + last_in[0].astype(WIDE) + last_in[1].astype(WIDE)
        )
        for copy in (*cores, *across, *lasts):
            copy.wait_send()


def collect_back(grad_gate, grad_up, weight, left, right, length):
    tokens, cols = grad_gate.shape
    width = weight.shape[0]
    slots, tile = tokens // length, 256
    tiles = width // tile
    row = pl.BlockSpec((length, cols), lambda i: (jnp.maximum(slots - 1 - i, 0), 0))
    column = lambda i: jnp.clip(i - slots, 0, tiles - 1)
    return pl.pallas_call(
        functools.partial(collect_kernel, slots),
        grid=(slots + tiles,),
        in_specs=[
            row,
            row,
            part_spec(width, cols, 0),
            part_spec(width, cols, 1),
            pl.BlockSpec((tokens, tile), lambda i: (0, column(i))),
            pl.BlockSpec(memory_space=pl.ANY),
        ],
        out_specs=[
            pl.BlockSpec((length, width), lambda i: (0, 0)),
            pl.BlockSpec((tile, cols), lambda i: (column(i), 0)),
        ],
        out_shape=[
            jax.ShapeDtypeStruct((length, width), WIDE),
            jax.ShapeDtypeStruct((width, cols), LOW),
        ],
        scratch_shapes=[
            pltpu.VMEM((slots, length, width), LOW),
            pltpu.VMEM((4, length, width), LOW),
            pltpu.VMEM((2, length // 2, width), LOW),
            pltpu.VMEM((2, length, width), LOW),
            pltpu.VMEM((tokens, cols), LOW),
            pltpu.SemaphoreType.DMA((9,)),
            pltpu.SemaphoreType.DMA((9,)),
            pltpu.SemaphoreType.DMA,
        ],
        compiler_params=pltpu.CompilerParams(
            vmem_limit_bytes=63 << 20, collective_id=1, has_side_effects=True
        ),
        cost_estimate=estimate(6 * tokens * width * cols, 10 * tokens * cols),
    )(grad_gate, grad_up, weight, weight, left, right)


def remote_copy(send, recv):
    def make(source, target, index, partner):
        return pltpu.make_async_remote_copy(
            source, target, send.at[index], recv.at[index], device_id=partner, device_id_type=MESH_ID
        )

    return make


def branch_kernel(
    slots, tiles, total, middle, own_grad, gain, hid, weight, turned, gate, grad_middle, gain_grad,
    gate_out, branch, mlp_own, mlp_far, mlp_side, mlp_first, mlp_second, own, parts, core_in, held,
    send, recv, load
):
    step = pl.program_id(0)
    core, far, _ = partners_of()
    half = own.shape[0] // 2
    remote = remote_copy(send, recv)
    to_far = remote(own, branch.at[2], 0, far)
    to_near = remote(own, branch.at[1], 1, core)
    to_cross = remote(branch.at[2], branch.at[3], 2, core)
    keep = pltpu.make_async_copy(own, branch.at[0], load.at[0])
    loading = pltpu.make_async_copy(gate, held, load.at[1])
    cores = [remote(parts.at[7 - 2 * k], core_in.at[k], 3 + k, core) for k in range(4)]
    store = lambda source, target, i: pltpu.make_async_copy(source, target, load.at[i])
    stores = [
        [
            store(parts.at[6, pl.ds(0, half)], mlp_first, 2),
            store(parts.at[6, pl.ds(half, half)], mlp_second, 3),
        ],
        [store(parts.at[4], mlp_side, 4)],
        [store(parts.at[2], mlp_far, 5)],
        [store(parts.at[0], mlp_own, 6)],
    ]

    @pl.when(step == 0)
    def _():
        loading.start()
        meet((core, far))
        values, upstream = middle[...], total[...]
        inverse = lax.rsqrt(jnp.mean(values * values, axis=-1, keepdims=True) + EPS)
        grad_in, gain_grad[...] = norm_backward(values, inverse, gain[...], upstream)
        grad_in = own_grad[...].astype(WIDE) + grad_in
        grad_middle[...] = grad_in
        own[...] = grad_in.astype(LOW)
        for copy in (to_far, to_near, keep):
            copy.start()

    @pl.when(step < slots)
    def _():
        parts[slots - 1 - step] = dot_cols(hid[...], weight[...]).astype(LOW)

    for k in range(4):
        pl.when(step == 2 * k)(cores[k].start)

        def finish(k=k):
            slot = 6 - 2 * k
            cores[k].wait_recv()
            parts[slot] = (parts[slot].astype(WIDE) + core_in[k].astype(WIDE)).astype(LOW)
            for copy in stores[k]:
                copy.start()

        pl.when(step == 2 * k + 1)(finish)

    @pl.when(step >= slots)
    def _():
        pl.when(step == slots)(loading.wait)
        gate_out[...] = dot_rows(turned[...], held[...]).astype(LOW)

    @pl.when(step == slots + tiles - 2)
    def _():
        to_far.wait_recv()
        to_cross.start()

    @pl.when(step == slots + tiles - 1)
    def _():
        to_near.wait_recv()
        to_cross.wait_recv()
        keep.wait()
        for group in stores:
            for copy in group:
                copy.wait()
        for copy in (to_far, to_near, to_cross, *cores):
            copy.wait_send()


ANYWHERE = pl.BlockSpec(memory_space=pl.ANY)


def spread_branch(total, middle, own_grad, gain, hid, weight, rows, grad_gate):
    length, width = total.shape
    tokens, cols = grad_gate.shape
    slots, tile = tokens // length, 256
    tiles = width // tile
    once = whole_spec(length, width, once=True)
    column = lambda i: jnp.clip(i - slots, 0, tiles - 1)
    part = jax.ShapeDtypeStruct((length, width), LOW)
    piece = jax.ShapeDtypeStruct((length // 2, width), LOW)
    return pl.pallas_call(
        functools.partial(branch_kernel, slots, tiles),
        grid=(slots + tiles,),
        in_specs=[
            once,
            once,
            once,
            whole_spec(1, width),
            pl.BlockSpec((length, cols), lambda i: (jnp.maximum(slots - 1 - i, 0), 0)),
            part_spec(width, cols, 0),
            pl.BlockSpec((tokens, tile), lambda i: (0, column(i))),
            ANYWHERE,
        ],
        out_specs=[
            whole_spec(length, width, once=True),
            whole_spec(1, width),
            pl.BlockSpec((tile, cols), lambda i: (column(i), 0)),
        ]
        + [ANYWHERE] * 6,
        out_shape=[
            jax.ShapeDtypeStruct((length, width), WIDE),
            jax.ShapeDtypeStruct((1, width), WIDE),
            jax.ShapeDtypeStruct((width, cols), LOW),
            jax.ShapeDtypeStruct((4, length, width), LOW),
            part,
            part,
            part,
            piece,
            piece,
        ],
        scratch_shapes=[
            pltpu.VMEM((length, width), LOW),
            pltpu.VMEM((slots, length, width), LOW),
            pltpu.VMEM((4, length, width), LOW),
            pltpu.VMEM((tokens, cols), LOW),
            pltpu.SemaphoreType.DMA((7,)),
            pltpu.SemaphoreType.DMA((7,)),
            pltpu.SemaphoreType.DMA((7,)),
        ],
        compiler_params=pltpu.CompilerParams(
            vmem_limit_bytes=63 << 20, collective_id=2, has_side_effects=True
        ),
        cost_estimate=estimate(4 * tokens * width * cols, 10 * tokens * cols),
    )(total, middle, own_grad, gain, hid, weight, rows, grad_gate)


def line_kernel(
    slots, tiles, line, weight, own_in, grad_middle, gain, rows_one, branch, line_all, mixed, block, share,
    gain_grad, attn_out, bias_out, home, parts, core_in, far_in, total, send, recv, load
):
    step = pl.program_id(0)
    core, far, _ = partners_of()
    tensor_rank, group = lax.axis_index("tp"), lax.axis_index("fsdp")
    shift = (tensor_rank % 2) * 2 + tensor_rank // 2
    target = {"fsdp": (group + slots - shift) % slots}
    source = {"fsdp": (group + shift) % slots}
    stays = shift == 0
    remote = remote_copy(send, recv)
    cores = [remote(parts.at[3 - 2 * k], core_in.at[k], k, core) for k in range(2)]
    to_far = remote(parts.at[2], far_in, 2, far)
    leave = remote(block, home, 3, target)
    keep = pltpu.make_async_copy(block, home, load)

    @pl.when(step == 0)
    def _():
        barrier = pltpu.get_barrier_semaphore()
        for partner in (core, far):
            pl.semaphore_signal(barrier, inc=1, device_id=partner, device_id_type=MESH_ID)

        @pl.when(stays)
        def _():
            pl.semaphore_wait(barrier, 2)
            keep.start()

        @pl.when(jnp.logical_not(stays))
        def _():
            for partner in (target, source):
                pl.semaphore_signal(barrier, inc=1, device_id=partner, device_id_type=MESH_ID)
            pl.semaphore_wait(barrier, 4)
            leave.start()

    @pl.when(step < slots)
    def _():
        part = dot_cols(line[...], weight[...])
        parts[slots - 1 - step] = part.astype(LOW)

        @pl.when(step == slots - 1)
        def _():
            total[...] = part

    for k in range(2):
        pl.when(step == 2 * k)(cores[k].start)

    @pl.when(step == 1)
    def _():
        cores[0].wait_recv()
        parts[2] = (parts[2].astype(WIDE) + core_in[0].astype(WIDE)).astype(LOW)
        to_far.start()

    @pl.when(step == slots - 1)
    def _():
        bias_out[...] = jnp.sum(line_all[...].astype(WIDE), axis=0, keepdims=True)

    @pl.when(step >= slots)
    def _():
        cols = line_all.shape[1]
        attn_out[:, :cols] = dot_rows(rows_one[...], line_all[...]).astype(LOW)
        attn_out[:, cols:] = dot_rows(branch[...], mixed[...]).astype(LOW)

    @pl.when(step == slots + tiles - 1)
    def _():
        cores[1].wait_recv()
        to_far.wait_recv()
        upstream = total[...] + core_in[1].astype(WIDE) + far_in[...].astype(WIDE)
        values = own_in[...].astype(WIDE)
        inverse = lax.rsqrt(jnp.mean(values * values, axis=-1, keepdims=True) + EPS)
        grad_in, gain_grad[...] = norm_backward(values, inverse, gain[...], upstream)
        share[...] = (grad_middle[...] + grad_in).astype(LOW)
        for copy in (*cores, to_far):
            copy.wait_send()
        pl.when(stays)(keep.wait)

        @pl.when(jnp.logical_not(stays))
        def _():
            leave.wait_recv()
            leave.wait_send()


def finish_rows(line, weight, own_in, grad_middle, gain, rows_one, branch, mixed, block):
    length, width = own_in.shape
    near_tokens, line_cols = line.shape
    slots, tile = near_tokens // length, 256
    tiles = width // tile
    once = whole_spec(length, width, once=True)
    column = lambda i: jnp.clip(i - slots, 0, tiles - 1)
    by_column = lambda n: pl.BlockSpec((n, tile), lambda i: (0, column(i)))
    attn_cols = line_cols + mixed.shape[1]
    return pl.pallas_call(
        functools.partial(line_kernel, slots, tiles),
        grid=(slots + tiles,),
        in_specs=[
            pl.BlockSpec((length, line_cols), lambda i: (jnp.maximum(slots - 1 - i, 0), 0)),
            whole_spec(width, line_cols, once=True),
            once,
            once,
            whole_spec(1, width),
            by_column(near_tokens),
            by_column(near_tokens),
            whole_spec(near_tokens, line_cols, once=True),
            whole_spec(*mixed.shape, once=True),
            ANYWHERE,
        ],
        out_specs=[
            whole_spec(length, width),
            whole_spec(1, width),
            pl.BlockSpec((tile, attn_cols), lambda i: (column(i), 0)),
            whole_spec(1, line_cols),
            ANYWHERE,
        ],
        out_shape=[
            jax.ShapeDtypeStruct((length, width), LOW),
            jax.ShapeDtypeStruct((1, width), WIDE),
            jax.ShapeDtypeStruct((width, attn_cols), LOW),
            jax.ShapeDtypeStruct((1, line_cols), WIDE),
            jax.ShapeDtypeStruct((length, width), LOW),
        ],
        scratch_shapes=[
            pltpu.VMEM((slots, length, width), LOW),
            pltpu.VMEM((2, length, width), LOW),
            pltpu.VMEM((length, width), LOW),
            pltpu.VMEM((length, width), WIDE),
            pltpu.SemaphoreType.DMA((4,)),
            pltpu.SemaphoreType.DMA((4,)),
            pltpu.SemaphoreType.DMA,
        ],
        compiler_params=pltpu.CompilerParams(
            vmem_limit_bytes=63 << 20, collective_id=3, has_side_effects=True
        ),
        cost_estimate=estimate(2 * near_tokens * width * attn_cols, 10 * near_tokens * width),
    )(line, weight, own_in, grad_middle, gain, rows_one, branch, line, mixed, block)


def place_kernel(count, info, *refs):
    out = refs[count]
    for r in range(count):

        @pl.when(pl.program_id(0) == r)
        def _():
            out[0] = refs[r][...]


def place_rows(rows, order):
    length, width = rows[0].shape
    count = len(rows)
    held = pl.BlockSpec((length, width), lambda s, info: (0, 0), pipeline_mode=pl.Buffered(1))
    return pl.pallas_call(
        functools.partial(place_kernel, count),
        grid_spec=pltpu.PrefetchScalarGridSpec(
            num_scalar_prefetch=1,
            grid=(count,),
            in_specs=[held] * count,
            out_specs=pl.BlockSpec((1, length, width), lambda s, info: (info[s], 0, 0)),
        ),
        out_shape=jax.ShapeDtypeStruct((count, length, width), LOW),
        compiler_params=pltpu.CompilerParams(vmem_limit_bytes=32 << 20),
        cost_estimate=estimate(0, 4 * count * length * width),
    )(order, *rows)


def turn(values, cosine, sine_signed):
    return values * cosine + pltpu.roll(values, values.shape[-1] // 2, 1) * sine_signed


def turn_back(values, cosine, sine_signed):
    return values * cosine - pltpu.roll(values, values.shape[-1] // 2, 1) * sine_signed


def project_kernel(
    heads, head_dim, x0, x1, x2, x3, gains, weight, bias, cosine, sine, h_out, q_out, k_out, v_out, gain
):
    slot = pl.program_id(0)

    @pl.when(slot == 0)
    def _():
        gain[...] = gains[...].astype(WIDE).T[:8]


    def run(x_ref):
        x = x_ref[...].astype(WIDE)
        scale_inv = lax.rsqrt(jnp.mean(x * x, axis=-1, keepdims=True) + EPS)
        normed = (x * scale_inv * gain[0:1]).astype(LOW)
        h_out[0] = normed
        lin = jnp.dot(normed, weight[...], preferred_element_type=WIDE) + bias[...]
        cos, sin = cosine[0], sine[0]
        for h in range(heads + 1):
            part = turn(lin[:, h * head_dim : (h + 1) * head_dim], cos, sin).astype(LOW)
            if h < heads:
                q_out[0, :, h * head_dim : (h + 1) * head_dim] = part
            else:
                k_out[0] = part
        v_out[0] = lin[:, (heads + 1) * head_dim :].astype(LOW)

    for r, x_ref in enumerate((x0, x1, x2, x3)):
        pl.when(slot == r)(functools.partial(run, x_ref))


def project(rows, held, bias, cosine, sine, heads, head_dim):
    length, width = rows[0].shape
    count = len(rows)
    cols = (heads + 2) * head_dim
    whole = whole_spec
    by_slot = lambda *shape: pl.BlockSpec((1, *shape), lambda s: (s,) + (0,) * len(shape))
    return pl.pallas_call(
        functools.partial(project_kernel, heads, head_dim),
        grid=(count,),
        in_specs=[whole(length, width)] * count
        + [part_spec(width, 128, cols // 128), part_spec(width, cols, 0), whole(1, cols)]
        + [by_slot(length, head_dim)] * 2,
        out_specs=[
            by_slot(length, width),
            by_slot(length, heads * head_dim),
            by_slot(length, head_dim),
            by_slot(length, head_dim),
        ],
        out_shape=[
            jax.ShapeDtypeStruct((count, length, width), LOW),
            jax.ShapeDtypeStruct((count, length, heads * head_dim), LOW),
            jax.ShapeDtypeStruct((count, length, head_dim), LOW),
            jax.ShapeDtypeStruct((count, length, head_dim), LOW),
        ],
        scratch_shapes=[pltpu.VMEM((8, width), WIDE)],
        compiler_params=pltpu.CompilerParams(vmem_limit_bytes=56 << 20),
        cost_estimate=pl.CostEstimate(
            flops=2 * count * length * width * cols,
            bytes_accessed=count * length * (2 * width + cols) * 2 + width * cols * 2,
            transcendentals=0,
        ),
    )(*rows, held, held, bias, cosine, sine)


def row_blocks(length):
    return [(i, min(256, length)) for i in range(0, length, min(256, length))]


def key_biases(length, offset, start, rows, past, keys):
    past_pos = lax.broadcasted_iota(jnp.int32, (1, past), 1)
    past_bias = jnp.where((past_pos < offset) & (past_pos < length), 0.0, NEG_FILL)
    query_pos = offset + start + lax.broadcasted_iota(jnp.int32, (rows, keys), 0)
    own_pos = offset + lax.broadcasted_iota(jnp.int32, (rows, keys), 1)
    own_bias = jnp.where((own_pos <= query_pos) & (own_pos < length), 0.0, NEG_FILL)
    return past_bias, own_bias


def dot_cols(left, right):
    return lax.dot_general(left, right, (((1,), (1,)), ((), ())), preferred_element_type=WIDE)


def dot_rows(left, right):
    return lax.dot_general(left, right, (((0,), (0,)), ((), ())), preferred_element_type=WIDE)


def attend_kernel(
    heads, head_dim, scale, first, total_slots, info, q, k_past, v_past, k_own, v_own, weight, out, lse, *parts
):
    length, offset = info[first + pl.program_id(0)], info[total_slots]
    past = k_past.shape[1]
    for start, rows in row_blocks(q.shape[1]):
        keys = start + rows
        past_bias, own_bias = key_biases(length, offset, start, rows, past, keys)
        here = slice(start, start + rows)
        for h in range(heads):
            cols = slice(h * head_dim, (h + 1) * head_dim)
            query = q[0, here, cols]
            s_past = dot_cols(query, k_past[0]) * scale + past_bias
            s_own = dot_cols(query, k_own[0, :keys]) * scale + own_bias
            top = jnp.maximum(
                jnp.max(s_past, axis=1, keepdims=True), jnp.max(s_own, axis=1, keepdims=True)
            )
            e_past, e_own = jnp.exp(s_past - top), jnp.exp(s_own - top)
            total = jnp.sum(e_past, axis=1, keepdims=True) + jnp.sum(e_own, axis=1, keepdims=True)
            inverse = 1.0 / total
            mixed = jnp.dot(
                (e_past * inverse).astype(LOW), v_past[0], preferred_element_type=WIDE
            ) + jnp.dot((e_own * inverse).astype(LOW), v_own[0, :keys], preferred_element_type=WIDE)
            out[0, here, cols] = mixed.astype(LOW)
            lse[0, here, h : h + 1] = top + jnp.log(total)
        rows_out = dot_cols(out[0, here], weight[...]).astype(LOW)
        for i, part in enumerate(parts):

            @pl.when(pl.program_id(0) == i)
            def _():
                part[here] = rows_out


def attend_forward(info, q, k_past, v_past, k_own, v_own, weight, heads, head_dim, scale, first, count):
    _, length, width = q.shape
    past = k_past.shape[1]
    by_slot = lambda *shape: pl.BlockSpec((1, *shape), lambda s, info: (first + s,) + (0,) * len(shape))
    out_slot = lambda *shape: pl.BlockSpec((1, *shape), lambda s, info: (s,) + (0,) * len(shape))
    keys = count * length * (past + length) * heads
    return pl.pallas_call(
        functools.partial(attend_kernel, heads, head_dim, scale, first, q.shape[0]),
        grid_spec=pltpu.PrefetchScalarGridSpec(
            num_scalar_prefetch=1,
            grid=(count,),
            in_specs=[
                by_slot(length, width),
                by_slot(past, head_dim),
                by_slot(past, head_dim),
                by_slot(length, head_dim),
                by_slot(length, head_dim),
                whole_spec(*weight.shape, once=True),
            ],
            out_specs=[out_slot(length, width), out_slot(length, 128)]
            + [whole_spec(length, weight.shape[0])] * count,
        ),
        out_shape=[
            jax.ShapeDtypeStruct((count, length, width), LOW),
            jax.ShapeDtypeStruct((count, length, 128), WIDE),
        ]
        + [jax.ShapeDtypeStruct((length, weight.shape[0]), LOW)] * count,
        compiler_params=pltpu.CompilerParams(vmem_limit_bytes=56 << 20),
        cost_estimate=estimate(4 * keys * head_dim, 4 * count * length * width, keys),
    )(info, q, k_past, v_past, k_own, v_own, weight)


def attend_back_rows(
    heads, head_dim, scale, length, offset, q, k_past, v_past, k_own, v_own, grad, lse, cosine, sine, put,
    dk_past, dk_own, dv_past, dv_own
):
    past = k_past.shape[1]
    for start, rows in row_blocks(q.shape[1]):
        keys = start + rows
        past_bias, own_bias = key_biases(length, offset, start, rows, past, keys)
        here = slice(start, start + rows)
        cos, sin = cosine[0, here], sine[0, here]
        for h in range(heads):
            cols = slice(h * head_dim, (h + 1) * head_dim)
            query, upstream = q[0, here, cols], grad[0, here, cols]
            log_total = lse[0, here, h : h + 1]
            p_past = jnp.exp(dot_cols(query, k_past[0]) * scale + past_bias - log_total)
            p_own = jnp.exp(dot_cols(query, k_own[0, :keys]) * scale + own_bias - log_total)
            g_past = dot_cols(upstream, v_past[0])
            g_own = dot_cols(upstream, v_own[0, :keys])
            row_dot = jnp.sum(p_past * g_past, axis=1, keepdims=True) + jnp.sum(
                p_own * g_own, axis=1, keepdims=True
            )
            s_past = (p_past * (g_past - row_dot)).astype(LOW)
            s_own = (p_own * (g_own - row_dot)).astype(LOW)
            dq = (
                jnp.dot(s_past, k_past[0], preferred_element_type=WIDE)
                + jnp.dot(s_own, k_own[0, :keys], preferred_element_type=WIDE)
            ) * scale
            put(here, cols, turn_back(dq, cos, sin).astype(LOW))
            dk_past[...] += dot_rows(s_past, query)
            dk_own[:keys] += dot_rows(s_own, query)
            dv_past[...] += dot_rows(p_past.astype(LOW), upstream)
            dv_own[:keys] += dot_rows(p_own.astype(LOW), upstream)


def attend_back_kernel(
    heads,
    head_dim,
    scale,
    info,
    q,
    k_past,
    v_past,
    k_own,
    v_own,
    grad,
    lse,
    cosine,
    sine,
    dq_out,
    mine_past,
    mine_own,
    other_past,
    other_own,
    dk_past,
    dk_own,
    dv_past,
    dv_own,
):
    slot = pl.program_id(0)
    length, offset = info[slot], info[pl.num_programs(0)]
    parity = info[pl.num_programs(0) + 1]
    for total in (dk_past, dk_own, dv_past, dv_own):
        total[...] = jnp.zeros_like(total)
    attend_back_rows(
        heads, head_dim, scale, length, offset, q, k_past, v_past, k_own, v_own, grad, lse, cosine, sine,
        lambda here, cols, value: dq_out.__setitem__((0, here, cols), value),
        dk_past, dk_own, dv_past, dv_own,
    )

    @pl.when(parity == 0)
    def _():
        mine_past[0] = dk_past[...] * scale
        mine_own[0] = dk_own[...] * scale
        other_past[0] = dv_past[...]
        other_own[0] = dv_own[...]

    @pl.when(parity != 0)
    def _():
        mine_past[0] = dv_past[...]
        mine_own[0] = dv_own[...]
        other_past[0] = dk_past[...] * scale
        other_own[0] = dk_own[...] * scale


def attend_backward(
    info, q, k_past, v_past, k_own, v_own, grad, lse, cosine, sine, heads, head_dim, scale
):
    count, length, width = q.shape
    past = k_past.shape[1]
    by_slot = lambda *shape: pl.BlockSpec((1, *shape), lambda s, info: (s,) + (0,) * len(shape))
    keys = count * length * (past + length) * heads
    return pl.pallas_call(
        functools.partial(attend_back_kernel, heads, head_dim, scale),
        grid_spec=pltpu.PrefetchScalarGridSpec(
            num_scalar_prefetch=1,
            grid=(count,),
            in_specs=[
                by_slot(length, width),
                by_slot(past, head_dim),
                by_slot(past, head_dim),
                by_slot(length, head_dim),
                by_slot(length, head_dim),
                by_slot(length, width),
                by_slot(length, 128),
                by_slot(length, head_dim),
                by_slot(length, head_dim),
            ],
            out_specs=[
                by_slot(length, width),
                by_slot(past, head_dim),
                by_slot(length, head_dim),
                by_slot(past, head_dim),
                by_slot(length, head_dim),
            ],
            scratch_shapes=[
                pltpu.VMEM((past, head_dim), WIDE),
                pltpu.VMEM((length, head_dim), WIDE),
                pltpu.VMEM((past, head_dim), WIDE),
                pltpu.VMEM((length, head_dim), WIDE),
            ],
        ),
        out_shape=[
            jax.ShapeDtypeStruct((count, length, width), LOW),
            jax.ShapeDtypeStruct((count, past, head_dim), WIDE),
            jax.ShapeDtypeStruct((count, length, head_dim), WIDE),
            jax.ShapeDtypeStruct((count, past, head_dim), WIDE),
            jax.ShapeDtypeStruct((count, length, head_dim), WIDE),
        ],
        compiler_params=pltpu.CompilerParams(vmem_limit_bytes=56 << 20),
        cost_estimate=estimate(10 * keys * head_dim, 8 * count * length * width, keys),
    )(info, q, k_past, v_past, k_own, v_own, grad, lse, cosine, sine)


def exchange_kernel(
    heads, head_dim, scale, slots, tiles, info, q, k_past, v_past, k_own, v_own, grad, lse, cosine, sine,
    cosine_all, sine_all, turned, up, line, up_out, mine_past, mine_own, other_past, other_own, got_past,
    got_own, side_out, side_in, dk_past, dk_own, dv_past, dv_own, held, send, recv, load
):
    step = pl.program_id(0)
    tensor_rank = lax.axis_index("tp")
    core, _, side = partners_of()
    parity = lax.rem(tensor_rank, 2)
    offset = lax.axis_index("ctx") * q.shape[1]
    remote = remote_copy(send, recv)
    pasts = [remote(other_past.at[r], got_past.at[r ^ 1], r, core) for r in range(slots)]
    owns = [remote(other_own.at[r], got_own.at[r ^ 1], slots + r, core) for r in range(slots)]
    sides = [remote(side_out.at[r], side_in.at[r], 2 * slots + r, side) for r in range(slots)]
    loading = pltpu.make_async_copy(up, held, load)

    @pl.when(step == 0)
    def _():
        loading.start()
        meet((core, side))

    @pl.when(step < slots)
    def _():
        length = info[jnp.minimum(step, slots - 1)]
        for total in (dk_past, dk_own, dv_past, dv_own):
            total[...] = jnp.zeros_like(total)
        attend_back_rows(
            heads, head_dim, scale, length, offset, q, k_past, v_past, k_own, v_own, grad, lse, cosine,
            sine, lambda here, cols, value: line.__setitem__((step, here, cols), value),
            dk_past, dk_own, dv_past, dv_own,
        )

        @pl.when(parity == 0)
        def _():
            mine_past[step] = dk_past[...] * scale
            mine_own[step] = dk_own[...] * scale
            other_past[step] = dv_past[...]
            other_own[step] = dv_own[...]

        @pl.when(parity != 0)
        def _():
            mine_past[step] = dv_past[...]
            mine_own[step] = dv_own[...]
            other_past[step] = dk_past[...] * scale
            other_own[step] = dk_own[...] * scale

    for r in range(slots):

        def start(r=r):
            pasts[r].start()
            owns[r].start()

        pl.when(step == r)(start)

    for pair in range(0, slots, 2):

        def merge(pair=pair):
            for r in (pair, pair + 1):
                pasts[r ^ 1].wait_recv()
                side_out[r] = (mine_past[r] + got_past[r]).astype(LOW)
                sides[r].start()

        pl.when(step == pair + 1)(merge)

    @pl.when(step >= slots)
    def _():
        pl.when(step == slots)(loading.wait)
        up_out[...] = dot_rows(turned[...], held[...]).astype(LOW)

    @pl.when(step == slots + tiles - 1)
    def _():
        for r in range(slots):
            owns[r ^ 1].wait_recv()
            sides[r].wait_recv()
            total = mine_own[r] + got_own[r] + side_in[r].astype(WIDE)
            back = turn_back(total, cosine_all[r], sine_all[r])
            line[r, :, heads * head_dim :] = jnp.where(parity == 0, back, total).astype(LOW)
        for copy in (*pasts, *owns, *sides):
            copy.wait_send()


def attend_exchange(
    info, q, k_past, v_past, k_own, v_own, grad, lse, cosine, sine, heads, head_dim, scale, rows, grad_up
):
    count, length, width = q.shape
    past = k_past.shape[1]
    tokens, cols = grad_up.shape
    model_width = rows.shape[1]
    tile = 256
    tiles = model_width // tile
    slot = lambda i: jnp.minimum(i, count - 1)
    by_slot = lambda *shape: pl.BlockSpec((1, *shape), lambda i, info: (slot(i),) + (0,) * len(shape))
    column = lambda i: jnp.clip(i - count, 0, tiles - 1)
    held = lambda *shape: pl.BlockSpec(
        shape, lambda i, info: (0,) * len(shape), pipeline_mode=pl.Buffered(1)
    )
    line_cols = width + head_dim
    return pl.pallas_call(
        functools.partial(exchange_kernel, heads, head_dim, scale, count, tiles),
        grid_spec=pltpu.PrefetchScalarGridSpec(
            num_scalar_prefetch=1,
            grid=(count + tiles,),
            in_specs=[
                by_slot(length, width),
                by_slot(past, head_dim),
                by_slot(past, head_dim),
                by_slot(length, head_dim),
                by_slot(length, head_dim),
                by_slot(length, width),
                by_slot(length, 128),
                by_slot(length, head_dim),
                by_slot(length, head_dim),
                held(count, length, head_dim),
                held(count, length, head_dim),
                pl.BlockSpec((tokens, tile), lambda i, info: (0, column(i))),
                ANYWHERE,
            ],
            out_specs=[
                pl.BlockSpec((count, length, line_cols), lambda i, info: (0, 0, 0)),
                pl.BlockSpec((tile, cols), lambda i, info: (column(i), 0)),
            ],
            scratch_shapes=[pltpu.VMEM((count, length, head_dim), WIDE)] * 6
            + [pltpu.VMEM((count, length, head_dim), LOW)] * 2
            + [pltpu.VMEM((length, head_dim), WIDE)] * 4
            + [
                pltpu.VMEM((tokens, cols), LOW),
                pltpu.SemaphoreType.DMA((3 * count,)),
                pltpu.SemaphoreType.DMA((3 * count,)),
                pltpu.SemaphoreType.DMA,
            ],
        ),
        out_shape=[
            jax.ShapeDtypeStruct((count, length, line_cols), LOW),
            jax.ShapeDtypeStruct((model_width, cols), LOW),
        ],
        compiler_params=pltpu.CompilerParams(
            vmem_limit_bytes=63 << 20, collective_id=4, has_side_effects=True
        ),
        cost_estimate=estimate(2 * tokens * model_width * cols, 10 * tokens * cols),
    )(info, q, k_past, v_past, k_own, v_own, grad, lse, cosine, sine, cosine, sine, rows, grad_up)


def local(
    hidden_in,
    cotangent,
    seq_lengths,
    positions,
    permutation,
    query_weight,
    keyval_weight,
    output_weight,
    norm_gains,
    bias_query,
    bias_keyval,
    gate_weight,
    up_weight,
    down_weight,
):
    group_rank = lax.axis_index("fsdp")
    ctx_rank = lax.axis_index("ctx")
    tensor_rank = lax.axis_index("tp")
    fsdp_count = lax.axis_size("fsdp")
    ctx_count = lax.axis_size("ctx")
    tensor_count = lax.axis_size("tp")
    seq_grp, local_len, model_width = hidden_in.shape
    heads, head_dim = bias_query.shape
    keyval_heads = bias_keyval.shape[0] // 2
    assert seq_grp == tensor_count == fsdp_count == len(DEAL_SHIFT)
    token_count = seq_grp * local_len
    scale = 1.0 / math.sqrt(head_dim)
    offset = ctx_rank * local_len
    head_pair = tensor_rank // (tensor_count // keyval_heads)
    parity = tensor_rank % 2
    shifts = jnp.array(DEAL_SHIFT, jnp.int32)

    table = permutation.reshape(fsdp_count, seq_grp)
    far_group = lax.rem(group_rank + shifts[tensor_rank], fsdp_count)
    far_row = lax.dynamic_index_in_dim(table, far_group, 0, keepdims=False)
    leaving = jnp.sum(jnp.where(far_row // seq_grp == group_rank, far_row - group_rank * seq_grp, 0))
    own_row = lax.dynamic_index_in_dim(table, group_rank, 0, keepdims=False)
    slot_now, seq_now, home_now = [], [], []
    for r in range(seq_grp):
        shift = shifts[tensor_rank ^ r]
        source = lax.rem(group_rank - shift + fsdp_count, fsdp_count)
        hit = own_row // seq_grp == source
        slot_now.append(jnp.sum(jnp.where(hit, jnp.arange(seq_grp), 0)))
        seq_now.append(jnp.sum(jnp.where(hit, own_row, 0)))
        target = lax.rem(group_rank + shift, fsdp_count)
        target_row = lax.dynamic_index_in_dim(table, target, 0, keepdims=False)
        home_now.append(
            jnp.sum(jnp.where(target_row // seq_grp == group_rank, target_row - group_rank * seq_grp, 0))
        )
    there = [
        (f * tensor_count + t, (f + DEAL_SHIFT[t]) % fsdp_count * tensor_count + t)
        for f in range(fsdp_count)
        for t in range(tensor_count)
    ]
    back = [(target, source) for source, target in there]

    split = units_split()
    head_width = 2 * head_dim
    query_cols = heads * head_dim
    near_cols = query_cols + head_width + 128

    outgoing = lax.dynamic_index_in_dim(hidden_in, leaving, 0, keepdims=False)
    own_in = lax.ppermute(outgoing, ("fsdp", "tp"), there)
    small = jnp.concatenate(
        [
            query_weight,
            lax.dynamic_slice_in_dim(keyval_weight, head_pair * head_width, head_width, axis=1),
            jnp.pad(norm_gains.T, ((0, 0), (0, 128 - norm_gains.shape[0]))),
            output_weight.T,
        ],
        axis=1,
    )
    units = gate_weight.shape[1]
    units_pad = -(-units // 256) * 256
    widen = lambda w: jnp.pad(w, ((0, 0), (0, units_pad - units)))
    shards = [widen(w) for w in (down_weight.T, gate_weight, up_weight)]
    if split:
        half_units = units_pad // 2
        cut = lambda w, c: lax.dynamic_slice_in_dim(w, c * half_units, half_units, axis=1)

        def in_order(own, other):
            return jnp.stack(
                [jnp.where(ctx_rank == 0, own, other), jnp.where(ctx_rank == 0, other, own)]
            )

        def all_rows(both, *earlier):
            full = lax.all_gather(after(both, *earlier), "fsdp", axis=0, tiled=False)
            return full.reshape(-1, both.shape[-1])

        small_both = in_order(small, from_partner(after(small, outgoing), "ctx", 1))
        leaving_units = jnp.concatenate([cut(w, 1 - ctx_rank) for w in shards], axis=1)
        arriving_units = from_partner(after(leaving_units, small), "ctx", 1)
        own_units = jnp.concatenate([cut(w, ctx_rank) for w in shards], axis=1)
        unit_both = in_order(own_units, arriving_units)
    else:
        all_rows = lambda shard, *earlier: lax.all_gather(
            shard, ("fsdp", "ctx"), axis=0, tiled=True
        )
        small_both, unit_both, half_units = small, jnp.concatenate(shards, axis=1), units_pad
    far_in = from_partner(own_in, "tp", 2)
    near_in = from_partner(own_in, "tp", 1)
    cross_in = from_partner(far_in, "tp", 1)

    lengths_now = jnp.stack([seq_lengths[s] for s in seq_now])
    info = jnp.concatenate([lengths_now, jnp.stack([offset, parity])]).astype(jnp.int32)
    positions_now = jnp.stack(
        [lax.dynamic_index_in_dim(positions, s, 0, keepdims=False) for s in seq_now]
    )
    lane = jnp.arange(head_dim)
    frequency = 1.0 / ROPE_BASE ** ((lane % (head_dim // 2)).astype(WIDE) * 2.0 / head_dim)
    angles = positions_now.astype(WIDE)[..., None] * frequency
    cosine = jnp.cos(angles)
    sine = jnp.sin(angles) * jnp.where(lane < head_dim // 2, -1.0, 1.0)
    grad_slots = [lax.dynamic_index_in_dim(cotangent, s, 0, keepdims=False) for s in slot_now]

    near_full = all_rows(small_both, own_in)
    down_full = all_rows(unit_both[..., :half_units], cross_in)
    gate_up_full = all_rows(unit_both[..., half_units:], cross_in)
    project_full = near_full[:, : query_cols + head_width]
    output_full = near_full[:, near_cols:]
    bias_head = lax.dynamic_slice_in_dim(bias_keyval, head_pair * 2, 2, axis=0)
    bias_row = jnp.concatenate([bias_query.reshape(1, -1), bias_head.reshape(1, -1)], axis=1).astype(WIDE)
    normed_one, query_rot, key_own, value_own = project(
        (own_in, near_in, far_in, cross_in),
        near_full,
        bias_row,
        cosine,
        sine,
        heads,
        head_dim,
    )
    gains_now = near_full[:, query_cols + head_width : near_cols][:, :2].astype(WIDE).T
    if split:
        key_past, value_past = lax.ppermute((key_own, value_own), "ctx", [(0, 1)])
        other_pair = [from_partner(after(grad_slots[r], value_past), "ctx", 1) for r in (0, 2)]
        cross_pair = functools.partial(from_partner, axis="tp", apart=1)
    else:
        key_past = lax.all_gather(key_own, "ctx", axis=1, tiled=True)
        value_past = lax.all_gather(value_own, "ctx", axis=1, tiled=True)
    attend = lambda first, *held: attend_forward(
        info, query_rot, *held, key_own, value_own, output_full, heads, head_dim, scale, first, 2
    )
    in_share = own_in.astype(WIDE)

    mixed_far, lse_far, *attn_far = attend(2, key_past, value_past)
    attn_wide = collect_far(attn_far[0], attn_far[1])
    attn_got = from_partner(attn_wide, "tp", 2)
    mixed_near, lse_near, *attn_near = attend(0, after(key_past, attn_wide), value_past)
    attn_core = from_partner(attn_near[1], "tp", 1)
    middle_share = (
        in_share
        + attn_near[0].astype(WIDE)
        + attn_core.astype(WIDE)
        + attn_got.astype(WIDE)
    )
    inv_two = lax.rsqrt(jnp.mean(middle_share * middle_share, axis=-1, keepdims=True) + EPS)
    normed_share = (middle_share * inv_two * gains_now[1]).astype(LOW)
    half_len = local_len // 2

    others = []
    if split:
        cross_pair = [cross_pair(after(v, normed_share)) for v in other_pair]
        others = [other_pair[0], cross_pair[0], other_pair[1], cross_pair[1]]

    grad_hidden, grad_rows = stack_rows(
        [(after(grad_slots[0], normed_share),)] + [(g,) for g in grad_slots[1:] + others], down_full, 0, 1
    )

    def spread_all(own):
        far = from_partner(own, "tp", 2)
        near = from_partner(own, "tp", 1)
        if not split:
            return (own, near, far, from_partner(far, "tp", 1))
        side = from_partner(own, "ctx", 1)
        held = after(far, grad_hidden), after(side, grad_hidden)
        across = from_partner(held[0][:half_len], "ctx", 1), from_partner(held[1][half_len:], "tp", 2)
        cores = [from_partner(v, "tp", 1) for v in (*held, *across)]
        return (own, near, far, cores[0], side, cores[1], *across, *cores[2:])

    def in_slots(rows):
        if not split:
            return [(row,) for row in rows]
        return [(row,) for row in rows[:6]] + [rows[6:8], rows[8:]]

    gate_lin, normed_two = stack_rows(in_slots(spread_all(normed_share)), gate_up_full, 0, 2)
    hidden_act, grad_gate, grad_up = hidden_units(
        normed_two, gate_up_full, 1, 2, gate_lin, grad_hidden
    )

    def collect_all(lefts, weights, *earlier):
        lefts = list(lefts)
        lefts[0] = after(lefts[0], *earlier)
        last = back_rows(lefts, weights, 2, 2, local_len)
        got = [from_partner(collect_far(last[0], last[1]), "tp", 2)]
        first = back_rows(lefts, weights, 0, 2, local_len)
        got.append(from_partner(first[1], "tp", 1))

        def finish():
            return sum((v.astype(WIDE) for v in got), first[0].astype(WIDE))

        return first[0], finish

    if split:
        grad_two_share, down_grad = collect_back(
            grad_gate, grad_up, gate_up_full, grad_rows, hidden_act, local_len
        )
        grad_middle, gain_two, gate_grad, grad_branch, *mlp = spread_branch(
            grad_two_share,
            middle_share,
            grad_slots[0],
            gains_now[1:2],
            hidden_act,
            down_full,
            normed_two,
            grad_gate,
        )
        grad_branch = grad_branch.reshape(token_count, model_width)
    else:
        first_back, finish_back = collect_all(
            (grad_gate, grad_up), ((gate_up_full, 0, 2), (gate_up_full, 1, 2))
        )
        down_grad = contract_rows(after(grad_rows, first_back), hidden_act, LOW)
        gate_grad = contract_rows(normed_two, after(grad_gate, down_grad), LOW)
        grad_two_share = finish_back()
        grad_norm_two, gain_two = norm_backward(
            middle_share, inv_two, gains_now[1], grad_two_share
        )
        grad_middle = grad_slots[0].astype(WIDE) + grad_norm_two
        branch_own = grad_middle.astype(LOW)
        branch_far = from_partner(branch_own, "tp", 2)
        branch_near = from_partner(branch_own, "tp", 1)
        branch_cross = from_partner(branch_far, "tp", 1)
        grad_branch = jnp.concatenate([branch_own, branch_near, branch_far, branch_cross], axis=0)
        up_grad = contract_rows(normed_two, after(grad_up, branch_own), LOW)

    grad_mixed = product(grad_branch, output_full, LOW)
    mixed_flat = jnp.concatenate([mixed_near, mixed_far], axis=0).reshape(token_count, query_cols)
    lse = jnp.concatenate([lse_near, lse_far], axis=0)
    attend_args = (
        info,
        query_rot,
        key_past,
        value_past,
        key_own,
        value_own,
        grad_mixed.reshape(seq_grp, local_len, query_cols),
        lse,
        cosine,
        sine,
        heads,
        head_dim,
        scale,
    )
    if split:
        line_grad, up_grad = attend_exchange(*attend_args, normed_two, grad_up)
        line_grad = line_grad.reshape(token_count, -1)
    else:
        grad_query, mine_past, mine_own, other_past, other_own = attend_backward(*attend_args)
        swap = lambda value: jnp.stack([value[r ^ 1] for r in range(seq_grp)])
        got_past, got_own = from_partner((other_past, other_own), "tp", 1)
        past_sum = mine_past + swap(got_past)
        own_sum = mine_own + swap(got_own)
        own_sum = own_sum + lax.psum_scatter(past_sum, "ctx", scatter_dimension=1, tiled=True)
        half_lanes = head_dim // 2
        turned = own_sum * cosine - jnp.roll(own_sum, half_lanes, axis=-1) * sine
        own_grad = jnp.where(parity == 0, turned, own_sum).astype(LOW).reshape(token_count, head_dim)
        line_grad = jnp.concatenate([grad_query.reshape(token_count, query_cols), own_grad], axis=1)
    own_weight = lax.dynamic_slice_in_dim(
        project_full, query_cols + parity * head_dim, head_dim, axis=1
    )
    back_full = jnp.concatenate([project_full[:, :query_cols], own_weight], axis=1)
    normed_flat = normed_one.reshape(token_count, model_width)
    if split:
        mlp_own, mlp_far, mlp_side, mlp_first, mlp_second = mlp
        got_first = from_partner(mlp_first, "tp", 2).astype(WIDE)
        got_second = from_partner(mlp_second, "ctx", 1).astype(WIDE)
        add_half = lambda rows, low, high: jnp.concatenate(
            [
                rows[:half_len] if low is None else (rows[:half_len].astype(WIDE) + low).astype(LOW),
                rows[half_len:] if high is None else (rows[half_len:].astype(WIDE) + high).astype(LOW),
            ],
            axis=0,
        )
        mlp_sum = (
            mlp_own.astype(WIDE)
            + from_partner(add_half(mlp_far, None, got_second), "tp", 2).astype(WIDE)
            + from_partner(add_half(mlp_side, got_first, None), "ctx", 1).astype(WIDE)
        )
        block_share = (middle_share + mlp_sum).astype(LOW)
        input_share, gain_one, attn_grad, bias_grad, block_home = finish_rows(
            line_grad,
            back_full,
            own_in,
            grad_middle,
            gains_now[0:1],
            normed_flat,
            grad_branch,
            mixed_flat,
            block_share,
        )
    else:
        half = token_count // 2
        line_far = contract_cols(line_grad[half:], back_full, LOW).reshape(2, local_len, model_width)
        line_near = contract_cols(line_grad[:half], back_full, LOW).reshape(2, local_len, model_width)
        line_wide = collect_far(line_far[0], line_far[1])
        line_got = from_partner(line_wide, "tp", 2)
        line_core = from_partner(line_near[1], "tp", 1)
        first_mlp, finish_mlp = collect_all((hidden_act,), ((down_full, 0, 1),), up_grad, branch_far)
        block_share = (middle_share + finish_mlp()).astype(LOW)
        grad_one_share = line_near[0].astype(WIDE) + line_core.astype(WIDE) + line_got.astype(WIDE)
        inv_one = lax.rsqrt(jnp.mean(in_share * in_share, axis=-1, keepdims=True) + EPS)
        grad_norm_one, gain_one = norm_backward(in_share, inv_one, gains_now[0], grad_one_share)
        input_share = (grad_middle + grad_norm_one).astype(LOW)
        attn_grad = jnp.concatenate(
            [contract_rows(normed_flat, line_grad, LOW), contract_rows(grad_branch, mixed_flat, LOW)],
            axis=1,
        )
        bias_grad = jnp.sum(line_grad.astype(WIDE), axis=0)

    def scatter_units(grad):
        if not split:
            return scatter_sum(grad, ctx_rank, LOW)
        return lax.psum_scatter(grad, "fsdp", scatter_dimension=0, tiled=True)

    unit_sums = [scatter_units(g) for g in (down_grad, gate_grad, up_grad)]

    attn_end = scatter_sum(attn_grad, ctx_rank, LOW, *unit_sums)

    home_order = jnp.stack(home_now).astype(jnp.int32)

    def leave(share):
        return lax.ppermute(share, ("fsdp", "tp"), back)

    def arrive(own):
        far = from_partner(own, "tp", 2)
        near = from_partner(own, "tp", 1)
        return place_rows((own, near, far, from_partner(far, "tp", 1)), home_order)

    input_home = leave(input_share)
    if not split:
        block_home = leave(block_share)
    block_out = arrive(block_home)
    input_grad = arrive(input_home)

    gain_grad = jnp.concatenate([gain_one, gain_two], axis=0).T
    gain_grad = gain_grad + from_partner(gain_grad, "tp", 1)
    gain_grad = gain_grad + from_partner(gain_grad, "tp", 2)
    shard_count = fsdp_count * ctx_count
    share = head_dim // shard_count
    bias_cols = jnp.transpose(bias_grad.reshape(heads + 1, shard_count, share), (1, 2, 0))
    bias_cols = jnp.pad(bias_cols, ((0, 0), (0, (model_width - head_dim) // shard_count), (0, 0)))
    tiny = jnp.concatenate([gain_grad, bias_cols.reshape(model_width, heads + 1)], axis=1)
    tiny = jnp.pad(tiny, ((0, 0), (0, 8 - tiny.shape[1])))
    tiny = tiny.reshape(fsdp_count, ctx_count, model_width // shard_count, 8)
    if split:
        kept, sent = scatter_ctx(tiny, ctx_rank)
        tiny = kept + from_partner(sent, "ctx", 1)
    else:
        tiny = lax.psum_scatter(tiny, "ctx", scatter_dimension=1, tiled=True)
    tiny = tiny.reshape(fsdp_count, -1, 8)
    pick = lambda shift: lax.dynamic_index_in_dim(
        tiny, lax.rem(group_rank + shift, fsdp_count), 0, keepdims=False
    )
    tiny_grad = pick(0)
    for shift in range(1, fsdp_count):
        pairs = [(f, (f + shift) % fsdp_count) for f in range(fsdp_count)]
        tiny_grad = tiny_grad + lax.ppermute(pick(shift), "fsdp", pairs)

    def unit_end(total):
        if split:
            blocks = total.reshape(1, ctx_count, -1, half_units)
            kept, sent = scatter_ctx(blocks, ctx_rank)
            kept, got = kept[0], from_partner(sent[0], "ctx", 1)
            first = jnp.where(ctx_rank == 0, kept, got)
            second = jnp.where(ctx_rank == 0, got, kept)
            total = jnp.concatenate([first, second], axis=1)
        return total[:, :units].astype(WIDE)

    down_end, gate_end, up_end = (unit_end(after(t, input_share)) for t in unit_sums)
    return (
        block_out,
        input_grad,
        attn_end[:, :query_cols].astype(WIDE),
        attn_end[:, query_cols : query_cols + head_dim].astype(WIDE),
        attn_end[:, query_cols + head_dim :].astype(WIDE).T,
        tiny_grad[:, :2].T,
        tiny_grad[:share, 2 : 2 + heads].T,
        tiny_grad[:share, 2 + heads : 3 + heads].T,
        gate_end,
        up_end,
        down_end.T,
    )


def solution(mesh):
    placed = (
        P("fsdp", "ctx", None),
        P("fsdp", "ctx", None),
        P(),
        P(None, "ctx"),
        P(),
        P(("fsdp", "ctx"), "tp"),
        P(("fsdp", "ctx"), None),
        P("tp", ("fsdp", "ctx")),
        P(None, ("fsdp", "ctx")),
        P("tp", None),
        P(),
        P(("fsdp", "ctx"), "tp"),
        P(("fsdp", "ctx"), "tp"),
        P("tp", ("fsdp", "ctx")),
    )
    return jax.shard_map(
        local,
        mesh=mesh,
        in_specs=placed,
        out_specs=(
            P("fsdp", "ctx", None),
            P("fsdp", "ctx", None),
            P(("fsdp", "ctx"), "tp"),
            P(("fsdp", "ctx"), "tp"),
            P("tp", ("fsdp", "ctx")),
            P(None, ("fsdp", "ctx")),
            P("tp", ("fsdp", "ctx")),
            P("tp", ("fsdp", "ctx")),
            P(("fsdp", "ctx"), "tp"),
            P(("fsdp", "ctx"), "tp"),
            P("tp", ("fsdp", "ctx")),
        ),
        check_vma=False,
    )
```

```python
import functools
import math

import jax
import jax.numpy as jnp
from jax import lax
from jax.experimental import pallas as pl
from jax.experimental.pallas import tpu as pltpu
from jax.sharding import PartitionSpec as P

EPS = 1e-06
ROPE_BASE = 10000.0
NEG_FILL = -1e30
LOW = jnp.bfloat16
WIDE = jnp.float32
DEAL_SHIFT = (0, 2, 1, 3)


def from_partner(value, axis, apart):
    pairs = [(source, source ^ apart) for source in range(lax.axis_size(axis))]
    return lax.ppermute(value, axis, pairs)


def product(left_side, right_side, kind=WIDE):
    return jnp.dot(left_side, right_side, preferred_element_type=WIDE).astype(kind)


def contract_rows(left_side, right_side, kind=WIDE):
    return lax.dot_general(
        left_side, right_side, (((0,), (0,)), ((), ())), preferred_element_type=WIDE
    ).astype(kind)


def contract_cols(left_side, right_side, kind=WIDE):
    return lax.dot_general(
        left_side, right_side, (((1,), (1,)), ((), ())), preferred_element_type=WIDE
    ).astype(kind)


def norm_backward(values, scale_inv, gain_row, upstream):
    scaled = gain_row * upstream
    inner_mean = jnp.mean(values * scaled, axis=-1, keepdims=True)
    grad_in = scale_inv * scaled - values * (scale_inv * scale_inv * scale_inv) * inner_mean
    gain_grad = jnp.sum(upstream * values * scale_inv, axis=0, keepdims=True)
    return (grad_in, gain_grad)


def after(value, *earlier):
    return lax.optimization_barrier((value, *earlier))[0]


def collect_far(far_part, cross_part):
    wide = far_part.astype(WIDE) + from_partner(cross_part, "tp", 1).astype(WIDE)
    return wide.astype(LOW)


def units_split():
    return lax.axis_size("ctx") == 2


def all_rows(shard):
    return lax.all_gather(shard, "fsdp", axis=0, tiled=True)


def scatter_ctx(blocks, ctx_rank):
    kept = lax.dynamic_index_in_dim(blocks, ctx_rank, 1, keepdims=False)
    sent = lax.dynamic_index_in_dim(blocks, 1 - ctx_rank, 1, keepdims=False)
    return kept, sent


def scatter_sum(grad, ctx_rank, kind, *earlier):
    fsdp_count, ctx_count = lax.axis_size("fsdp"), lax.axis_size("ctx")
    rows, cols = grad.shape
    blocks = grad.reshape(fsdp_count, ctx_count, rows // (fsdp_count * ctx_count), cols)
    if ctx_count == 2:
        kept, sent = scatter_ctx(blocks, ctx_rank)
        got = from_partner(sent, "ctx", 1)
        held = (after(kept, *earlier).astype(WIDE) + got.astype(WIDE)).astype(kind)
    else:
        swapped = jnp.swapaxes(blocks, 0, 1).reshape(rows, cols)
        held = lax.psum_scatter(swapped, "ctx", scatter_dimension=0, tiled=True)
    held = held.reshape(rows // ctx_count, cols)
    return lax.psum_scatter(held, "fsdp", scatter_dimension=0, tiled=True)


def estimate(flops, moved, transcendentals=0):
    return pl.CostEstimate(flops=flops, bytes_accessed=moved, transcendentals=transcendentals)


def part_spec(rows, cols, part):
    return pl.BlockSpec((rows, cols), lambda *_: (0, part), pipeline_mode=pl.Buffered(1))


def whole_spec(*shape, once=False):
    mode = {"pipeline_mode": pl.Buffered(1)} if once else {}
    return pl.BlockSpec(shape, lambda *_: (0,) * len(shape), **mode)


def rows_kernel(groups, *refs):
    slot = pl.program_id(0)
    weight, lin, stacked = refs[-3:]

    def run(pieces):
        start = 0
        for piece in pieces:
            stacked[start : start + piece.shape[0]] = piece[...]
            start += piece.shape[0]
        lin[...] = jnp.dot(stacked[...], weight[...], preferred_element_type=WIDE).astype(LOW)

    first = 0
    for r, pieces in enumerate(groups):
        pl.when(slot == r)(functools.partial(run, refs[first : first + pieces]))
        first += pieces


def stack_rows(slots, weight, part, parts):
    groups = [len(s) for s in slots]
    rows = [piece for s in slots for piece in s]
    width, length = rows[0].shape[1], sum(piece.shape[0] for piece in slots[0])
    count, cols = len(slots), weight.shape[1] // parts
    return pl.pallas_call(
        functools.partial(rows_kernel, groups),
        grid=(count,),
        in_specs=[whole_spec(*piece.shape, once=True) for piece in rows]
        + [part_spec(width, cols, part)],
        out_specs=[
            pl.BlockSpec((length, cols), lambda s: (s, 0)),
            pl.BlockSpec((length, width), lambda s: (s, 0)),
        ],
        out_shape=[
            jax.ShapeDtypeStruct((count * length, cols), LOW),
            jax.ShapeDtypeStruct((count * length, width), LOW),
        ],
        compiler_params=pltpu.CompilerParams(vmem_limit_bytes=60 << 20),
        cost_estimate=estimate(
            2 * count * length * width * cols, 2 * (count * length * (2 * width + cols) + width * cols)
        ),
    )(*rows, weight)


def units_kernel(h, up, gate, grad, hid, grad_gate, grad_up):
    up_lin = jnp.dot(h[...], up[...], preferred_element_type=WIDE)
    gate_lin = gate[...].astype(WIDE)
    grad_hidden = grad[...].astype(WIDE)
    sigmoid = 1.0 / (1.0 + jnp.exp(-gate_lin))
    silu = gate_lin * sigmoid
    hid[...] = (silu * up_lin).astype(LOW)
    grad_gate[...] = (grad_hidden * up_lin * sigmoid * (1.0 + gate_lin * (1.0 - sigmoid))).astype(LOW)
    grad_up[...] = (grad_hidden * silu).astype(LOW)


def hidden_units(h, up, part, parts, gate_lin, grad_hidden):
    tokens, width = h.shape
    cols = up.shape[1] // parts
    step = math.gcd(512, tokens)
    by_row = lambda n: pl.BlockSpec((step, n), lambda i: (i, 0))
    return pl.pallas_call(
        units_kernel,
        grid=(tokens // step,),
        in_specs=[by_row(width), part_spec(width, cols, part), by_row(cols), by_row(cols)],
        out_specs=[by_row(cols)] * 3,
        out_shape=[jax.ShapeDtypeStruct((tokens, cols), LOW)] * 3,
        compiler_params=pltpu.CompilerParams(vmem_limit_bytes=60 << 20),
        cost_estimate=estimate(
            2 * tokens * width * cols, 2 * (tokens * width + width * cols + 5 * tokens * cols)
        ),
    )(h, up, gate_lin, grad_hidden)


def back_kernel(terms, *refs):
    lefts, weights, outs = refs[:terms], refs[terms : 2 * terms], refs[2 * terms :]
    total = None
    for left, weight in zip(lefts, weights):
        term = dot_cols(left[...], weight[...])
        total = term if total is None else total + term
    for i, out in enumerate(outs):

        @pl.when(pl.program_id(0) == i)
        def _():
            out[...] = total.astype(LOW)


def back_rows(lefts, weights, first_slot, slots, length):
    width = weights[0][0].shape[0]
    depth = sum(left.shape[1] for left in lefts)
    return pl.pallas_call(
        functools.partial(back_kernel, len(lefts)),
        grid=(slots,),
        in_specs=[
            pl.BlockSpec((length, left.shape[1]), lambda s: (first_slot + s, 0)) for left in lefts
        ]
        + [part_spec(width, w.shape[1] // parts, part) for w, part, parts in weights],
        out_specs=[whole_spec(length, width)] * slots,
        out_shape=[jax.ShapeDtypeStruct((length, width), LOW)] * slots,
        compiler_params=pltpu.CompilerParams(vmem_limit_bytes=60 << 20),
        cost_estimate=estimate(
            2 * slots * length * width * depth,
            2 * (slots * length * (width + depth) + width * depth),
        ),
    )(*lefts, *[w for w, _, _ in weights])


def chosen_kernel(near, count, info, cotangent, *refs):
    slot = pl.program_id(0)
    others, (weight, lin, stacked) = refs[:count], refs[count:]

    @pl.when(slot < near)
    def _():
        stacked[...] = cotangent[0]

    for k, other in enumerate(others):

        @pl.when((slot >= near) & (info[slot] == k))
        def _():
            stacked[...] = other[...]

    lin[...] = jnp.dot(stacked[...], weight[...], preferred_element_type=WIDE).astype(LOW)


def chosen_rows(info, cotangent, others, weight, part, parts):
    near, length, width = cotangent.shape
    slots, cols = near + len(others), weight.shape[1] // parts
    held = lambda rows, n, at: pl.BlockSpec(
        (rows, n), lambda s, info: (0, at), pipeline_mode=pl.Buffered(1)
    )
    return pl.pallas_call(
        functools.partial(chosen_kernel, near, len(others)),
        grid_spec=pltpu.PrefetchScalarGridSpec(
            num_scalar_prefetch=1,
            grid=(slots,),
            in_specs=[
                pl.BlockSpec((1, length, width), lambda s, info: (info[jnp.minimum(s, near - 1)], 0, 0))
            ]
            + [held(length, width, 0)] * len(others)
            + [held(width, cols, part)],
            out_specs=[
                pl.BlockSpec((length, cols), lambda s, info: (s, 0)),
                pl.BlockSpec((length, width), lambda s, info: (s, 0)),
            ],
        ),
        out_shape=[
            jax.ShapeDtypeStruct((slots * length, cols), LOW),
            jax.ShapeDtypeStruct((slots * length, width), LOW),
        ],
        compiler_params=pltpu.CompilerParams(vmem_limit_bytes=60 << 20),
        cost_estimate=estimate(
            2 * slots * length * width * cols, 2 * (slots * length * (2 * width + cols) + width * cols)
        ),
    )(info, cotangent, *others, weight)


def full_units_kernel(h, g, down, gate, up, hid, grad_gate, grad_up):
    gate_lin = jnp.dot(h[...], gate[...], preferred_element_type=WIDE)
    up_lin = jnp.dot(h[...], up[...], preferred_element_type=WIDE)
    grad_hidden = jnp.dot(g[...], down[...], preferred_element_type=WIDE)
    sigmoid = 1.0 / (1.0 + jnp.exp(-gate_lin))
    silu = gate_lin * sigmoid
    hid[...] = (silu * up_lin).astype(LOW)
    grad_gate[...] = (grad_hidden * up_lin * sigmoid * (1.0 + gate_lin * (1.0 - sigmoid))).astype(LOW)
    grad_up[...] = (grad_hidden * silu).astype(LOW)


def full_units(h, g, weight):
    tokens, width = h.shape
    cols = weight.shape[1] // 3
    step = math.gcd(512, tokens)
    by_row = lambda n: pl.BlockSpec((step, n), lambda i: (i, 0))
    return pl.pallas_call(
        full_units_kernel,
        grid=(tokens // step,),
        in_specs=[by_row(width)] * 2 + [part_spec(width, cols, i) for i in range(3)],
        out_specs=[by_row(cols)] * 3,
        out_shape=[jax.ShapeDtypeStruct((tokens, cols), LOW)] * 3,
        compiler_params=pltpu.CompilerParams(vmem_limit_bytes=60 << 20),
        cost_estimate=estimate(
            6 * tokens * width * cols, 2 * (2 * tokens * width + 3 * width * cols + 3 * tokens * cols)
        ),
    )(h, g, weight, weight, weight)


def first_grads_kernel(g, h, hid, gate, up, out):
    part = pl.program_id(0)
    for i, (left, right) in enumerate(((g, hid), (h, gate), (h, up))):

        @pl.when(part == i)
        def _():
            out[...] = dot_rows(left[...], right[...]).astype(LOW)


def first_grads(grad_rows, rows, hid, grad_gate, grad_up):
    tokens, width = rows.shape
    cols, tile = hid.shape[1], 256
    tiles = width // tile
    return pl.pallas_call(
        first_grads_kernel,
        grid=(3, tiles),
        in_specs=[
            pl.BlockSpec((tokens, tile), lambda p, i: (0, jnp.where(p == 0, i, tiles - 1))),
            pl.BlockSpec((tokens, tile), lambda p, i: (0, jnp.where(p == 0, 0, i))),
        ]
        + [whole_spec(tokens, cols, once=True)] * 3,
        out_specs=pl.BlockSpec((tile, cols), lambda p, i: (i, p)),
        out_shape=jax.ShapeDtypeStruct((width, 3 * cols), LOW),
        compiler_params=pltpu.CompilerParams(vmem_limit_bytes=60 << 20),
        cost_estimate=estimate(6 * tokens * width * cols, 6 * tokens * cols + 6 * width * cols),
    )(grad_rows, rows, hid, grad_gate, grad_up)


MESH_ID = pl.DeviceIdType.MESH


def meet(partners):
    barrier = pltpu.get_barrier_semaphore()
    for partner in partners:
        pl.semaphore_signal(barrier, inc=1, device_id=partner, device_id_type=MESH_ID)
    pl.semaphore_wait(barrier, len(partners))


def partners_of():
    tensor_rank, ctx_rank = lax.axis_index("tp"), lax.axis_index("ctx")
    return {"tp": tensor_rank ^ 1}, {"tp": tensor_rank ^ 2}, {"ctx": ctx_rank ^ 1}


def collect_kernel(
    slots, tiles, gate_a, up_a, gate_b, up_b, w_gate_a, w_up_a, w_gate_b, w_up_b, left, right, hid, up, total,
    down_out, up_out, parts, sent, core_in, across_in, last_in, held, send, recv, load
):
    step = pl.program_id(0)
    steps = pl.num_programs(0)
    core, far, side = partners_of()
    half = total.shape[0] // 2
    remote = remote_copy(send, recv)
    cores = [remote(sent.at[k % 2], core_in.at[k], k, core) for k in range(4)]
    across = [
        remote(parts.at[3, pl.ds(0, half)], across_in.at[0], 4, far),
        remote(parts.at[3, pl.ds(half, half)], across_in.at[1], 5, side),
    ]
    lasts = [
        remote(parts.at[1], last_in.at[0], 6, far),
        remote(parts.at[2, pl.ds(half, half)], last_in.at[1, pl.ds(half, half)], 7, side),
        remote(parts.at[2, pl.ds(0, half)], last_in.at[1, pl.ds(0, half)], 8, side),
    ]
    loading = [
        pltpu.make_async_copy(source, held.at[i], load.at[i]) for i, source in enumerate((hid, up))
    ]

    @pl.when(step == 0)
    def _():
        for copy in loading:
            copy.start()
        meet((core, far, side))

    for k in (2, 3):
        pl.when(step == 2 * k)(cores[k - 2].wait_send)

    @pl.when(step < slots)
    def _():
        part = (
            dot_cols(gate_a[...], w_gate_a[...])
            + dot_cols(up_a[...], w_up_a[...])
            + dot_cols(gate_b[...], w_gate_b[...])
            + dot_cols(up_b[...], w_up_b[...])
        )

        @pl.when(step == slots - 1)
        def _():
            total[...] = part

        for k in range(4):

            @pl.when(step == 2 * k)
            def _():
                sent[k % 2] = part.astype(LOW)
                cores[k].start()

            if k < 3:

                @pl.when(step == 2 * k + 1)
                def _():
                    cores[k].wait_recv()
                    parts[3 - k] = (part + core_in[k].astype(WIDE)).astype(LOW)

    def add(slot, rows, value):
        parts[slot, rows] = (parts[slot, rows].astype(WIDE) + value.astype(WIDE)).astype(LOW)

    low, high = pl.ds(0, half), pl.ds(half, half)

    @pl.when(step == 1)
    def _():
        for copy in across:
            copy.start()

    pl.when(step == 3)(lasts[1].start)

    @pl.when(step == 5)
    def _():
        across[1].wait_recv()
        add(1, high, across_in[1])
        lasts[0].start()
        across[0].wait_recv()
        add(2, low, across_in[0])
        lasts[2].start()

    @pl.when((step >= slots) & (step < slots + tiles))
    def _():
        pl.when(step == slots)(loading[0].wait)
        down_out[...] = dot_rows(left[...], held[0]).astype(LOW)

    @pl.when(step >= slots + tiles)
    def _():
        pl.when(step == slots + tiles)(loading[1].wait)
        up_out[...] = dot_rows(right[...], held[1]).astype(LOW)

    @pl.when(step == steps - 1)
    def _():
        cores[3].wait_recv()
        for copy in lasts:
            copy.wait_recv()
        total[...] += (
            core_in[3].astype(WIDE) + last_in[0].astype(WIDE) + last_in[1].astype(WIDE)
        )
        for copy in (*cores[2:], *across, *lasts):
            copy.wait_send()


def collect_back(first, second, weight_a, weight_b, grad_rows, rows, hid, length):
    tokens, cols_a = first[0].shape
    cols = second[0].shape[1]
    width = weight_a.shape[0]
    slots, tile = tokens // length, 256
    tiles = width // tile
    row = lambda n: pl.BlockSpec((length, n), lambda i: (jnp.maximum(slots - 1 - i, 0), 0))
    column = lambda i, start: jnp.clip(i - start, 0, tiles - 1)
    down_at, up_at = (lambda i: column(i, slots)), (lambda i: column(i, slots + tiles))
    return pl.pallas_call(
        functools.partial(collect_kernel, slots, tiles),
        grid=(slots + 2 * tiles,),
        in_specs=[row(cols_a), row(cols_a), row(cols), row(cols)]
        + [part_spec(width, cols_a, 1), part_spec(width, cols_a, 2)]
        + [part_spec(width, cols, 1), part_spec(width, cols, 2)]
        + [
            pl.BlockSpec((tokens, tile), lambda i: (0, down_at(i))),
            pl.BlockSpec((tokens, tile), lambda i: (0, up_at(i))),
            ANYWHERE,
            ANYWHERE,
        ],
        out_specs=[
            whole_spec(length, width, once=True),
            pl.BlockSpec((tile, cols), lambda i: (down_at(i), 0)),
            pl.BlockSpec((tile, cols), lambda i: (up_at(i), 0)),
        ],
        out_shape=[
            jax.ShapeDtypeStruct((length, width), WIDE),
            jax.ShapeDtypeStruct((width, cols), LOW),
            jax.ShapeDtypeStruct((width, cols), LOW),
        ],
        scratch_shapes=[
            pltpu.VMEM((4, length, width), LOW),
            pltpu.VMEM((2, length, width), LOW),
            pltpu.VMEM((4, length, width), LOW),
            pltpu.VMEM((2, length // 2, width), LOW),
            pltpu.VMEM((2, length, width), LOW),
            pltpu.VMEM((2, tokens, cols), LOW),
            pltpu.SemaphoreType.DMA((9,)),
            pltpu.SemaphoreType.DMA((9,)),
            pltpu.SemaphoreType.DMA((2,)),
        ],
        compiler_params=pltpu.CompilerParams(
            vmem_limit_bytes=63 << 20, collective_id=1, has_side_effects=True
        ),
        cost_estimate=estimate(6 * tokens * width * cols, 10 * tokens * cols),
    )(*first, *second, weight_a, weight_a, weight_b, weight_b, grad_rows, rows, hid, second[1])


def remote_copy(send, recv):
    def make(source, target, index, partner):
        return pltpu.make_async_remote_copy(
            source, target, send.at[index], recv.at[index], device_id=partner, device_id_type=MESH_ID
        )

    return make


def branch_kernel(
    slots, tiles, total, middle, own_grad, gain, hid_a, hid_b, w_a, w_b, turned, gate, grad_middle, gain_grad,
    gate_out, branch, mlp_own, mlp_far, mlp_side, mlp_first, mlp_second, own, parts, core_in, held,
    send, recv, load
):
    step = pl.program_id(0)
    core, far, _ = partners_of()
    half = own.shape[0] // 2
    remote = remote_copy(send, recv)
    to_far = remote(own, branch.at[2], 0, far)
    to_near = remote(own, branch.at[1], 1, core)
    to_cross = remote(branch.at[2], branch.at[3], 2, core)
    keep = pltpu.make_async_copy(own, branch.at[0], load.at[0])
    loading = pltpu.make_async_copy(gate, held, load.at[1])
    cores = [remote(parts.at[7 - 2 * k], core_in.at[k], 3 + k, core) for k in range(4)]
    store = lambda source, target, i: pltpu.make_async_copy(source, target, load.at[i])
    stores = [
        [
            store(parts.at[6, pl.ds(0, half)], mlp_first, 2),
            store(parts.at[6, pl.ds(half, half)], mlp_second, 3),
        ],
        [store(parts.at[4], mlp_side, 4)],
        [store(parts.at[2], mlp_far, 5)],
        [store(parts.at[0], mlp_own, 6)],
    ]

    @pl.when(step == 0)
    def _():
        loading.start()
        meet((core, far))
        values, upstream = middle[...], total[...]
        inverse = lax.rsqrt(jnp.mean(values * values, axis=-1, keepdims=True) + EPS)
        grad_in, gain_grad[...] = norm_backward(values, inverse, gain[...], upstream)
        grad_in = own_grad[...].astype(WIDE) + grad_in
        grad_middle[...] = grad_in
        own[...] = grad_in.astype(LOW)
        for copy in (to_far, to_near, keep):
            copy.start()

    @pl.when(step < slots)
    def _():
        part = dot_cols(hid_a[...], w_a[...]) + dot_cols(hid_b[...], w_b[...])
        parts[slots - 1 - step] = part.astype(LOW)

    for k in range(4):
        pl.when(step == 2 * k)(cores[k].start)

        def finish(k=k):
            slot = 6 - 2 * k
            cores[k].wait_recv()
            parts[slot] = (parts[slot].astype(WIDE) + core_in[k].astype(WIDE)).astype(LOW)
            for copy in stores[k]:
                copy.start()

        pl.when(step == 2 * k + 1)(finish)

    @pl.when(step >= slots)
    def _():
        pl.when(step == slots)(loading.wait)
        gate_out[...] = dot_rows(turned[...], held[...]).astype(LOW)

    @pl.when(step == slots + tiles - 2)
    def _():
        to_far.wait_recv()
        to_cross.start()

    @pl.when(step == slots + tiles - 1)
    def _():
        to_near.wait_recv()
        to_cross.wait_recv()
        keep.wait()
        for group in stores:
            for copy in group:
                copy.wait()
        for copy in (to_far, to_near, to_cross, *cores):
            copy.wait_send()


ANYWHERE = pl.BlockSpec(memory_space=pl.ANY)


def spread_branch(total, middle, own_grad, gain, hid_a, hid_b, weight_a, weight_b, rows, grad_gate):
    length, width = total.shape
    tokens, cols = grad_gate.shape
    slots, tile = tokens // length, 256
    tiles = width // tile
    once = whole_spec(length, width, once=True)
    column = lambda i: jnp.clip(i - slots, 0, tiles - 1)
    part = jax.ShapeDtypeStruct((length, width), LOW)
    piece = jax.ShapeDtypeStruct((length // 2, width), LOW)
    return pl.pallas_call(
        functools.partial(branch_kernel, slots, tiles),
        grid=(slots + tiles,),
        in_specs=[
            once,
            once,
            once,
            whole_spec(1, width),
            pl.BlockSpec((length, hid_a.shape[1]), lambda i: (jnp.maximum(slots - 1 - i, 0), 0)),
            pl.BlockSpec((length, cols), lambda i: (jnp.maximum(slots - 1 - i, 0), 0)),
            part_spec(width, hid_a.shape[1], 0),
            part_spec(width, cols, 0),
            pl.BlockSpec((tokens, tile), lambda i: (0, column(i))),
            ANYWHERE,
        ],
        out_specs=[
            whole_spec(length, width, once=True),
            whole_spec(1, width),
            pl.BlockSpec((tile, cols), lambda i: (column(i), 0)),
        ]
        + [ANYWHERE] * 6,
        out_shape=[
            jax.ShapeDtypeStruct((length, width), WIDE),
            jax.ShapeDtypeStruct((1, width), WIDE),
            jax.ShapeDtypeStruct((width, cols), LOW),
            jax.ShapeDtypeStruct((4, length, width), LOW),
            part,
            part,
            part,
            piece,
            piece,
        ],
        scratch_shapes=[
            pltpu.VMEM((length, width), LOW),
            pltpu.VMEM((slots, length, width), LOW),
            pltpu.VMEM((4, length, width), LOW),
            pltpu.VMEM((tokens, cols), LOW),
            pltpu.SemaphoreType.DMA((7,)),
            pltpu.SemaphoreType.DMA((7,)),
            pltpu.SemaphoreType.DMA((7,)),
        ],
        compiler_params=pltpu.CompilerParams(
            vmem_limit_bytes=63 << 20, collective_id=2, has_side_effects=True
        ),
        cost_estimate=estimate(4 * tokens * width * cols, 10 * tokens * cols),
    )(total, middle, own_grad, gain, hid_a, hid_b, weight_a, weight_b, rows, grad_gate)


def line_kernel(
    slots, tiles, line, weight, own_in, grad_middle, gain, rows_one, line_all, block, share,
    gain_grad, attn_out, bias_out, home, parts, core_in, far_in, total, send, recv, load
):
    step = pl.program_id(0)
    core, far, _ = partners_of()
    tensor_rank, group = lax.axis_index("tp"), lax.axis_index("fsdp")
    shift = (tensor_rank % 2) * 2 + tensor_rank // 2
    target = {"fsdp": (group + slots - shift) % slots}
    source = {"fsdp": (group + shift) % slots}
    stays = shift == 0
    remote = remote_copy(send, recv)
    cores = [remote(parts.at[3 - 2 * k], core_in.at[k], k, core) for k in range(2)]
    to_far = remote(parts.at[2], far_in, 2, far)
    leave = remote(block, home, 3, target)
    keep = pltpu.make_async_copy(block, home, load)

    @pl.when(step == 0)
    def _():
        barrier = pltpu.get_barrier_semaphore()
        for partner in (core, far):
            pl.semaphore_signal(barrier, inc=1, device_id=partner, device_id_type=MESH_ID)

        @pl.when(stays)
        def _():
            pl.semaphore_wait(barrier, 2)
            keep.start()

        @pl.when(jnp.logical_not(stays))
        def _():
            for partner in (target, source):
                pl.semaphore_signal(barrier, inc=1, device_id=partner, device_id_type=MESH_ID)
            pl.semaphore_wait(barrier, 4)
            leave.start()

    @pl.when(step < slots)
    def _():
        part = dot_cols(line[...], weight[...])
        parts[slots - 1 - step] = part.astype(LOW)

        @pl.when(step == slots - 1)
        def _():
            total[...] = part

    for k in range(2):
        pl.when(step == 2 * k)(cores[k].start)

    @pl.when(step == 1)
    def _():
        cores[0].wait_recv()
        parts[2] = (parts[2].astype(WIDE) + core_in[0].astype(WIDE)).astype(LOW)
        to_far.start()

    @pl.when(step == slots - 1)
    def _():
        bias_out[...] = jnp.sum(line_all[...].astype(WIDE), axis=0, keepdims=True)

    @pl.when(step >= slots)
    def _():
        attn_out[...] = dot_rows(rows_one[...], line_all[...]).astype(LOW)

    @pl.when(step == slots + tiles - 1)
    def _():
        cores[1].wait_recv()
        to_far.wait_recv()
        upstream = total[...] + core_in[1].astype(WIDE) + far_in[...].astype(WIDE)
        values = own_in[...].astype(WIDE)
        inverse = lax.rsqrt(jnp.mean(values * values, axis=-1, keepdims=True) + EPS)
        grad_in, gain_grad[...] = norm_backward(values, inverse, gain[...], upstream)
        share[...] = (grad_middle[...] + grad_in).astype(LOW)
        for copy in (*cores, to_far):
            copy.wait_send()
        pl.when(stays)(keep.wait)

        @pl.when(jnp.logical_not(stays))
        def _():
            leave.wait_recv()
            leave.wait_send()


def finish_rows(line, weight, own_in, grad_middle, gain, rows_one, block):
    length, width = own_in.shape
    near_tokens, line_cols = line.shape
    slots, tile = near_tokens // length, 256
    tiles = width // tile
    once = whole_spec(length, width, once=True)
    column = lambda i: jnp.clip(i - slots, 0, tiles - 1)
    by_column = lambda n: pl.BlockSpec((n, tile), lambda i: (0, column(i)))
    attn_cols = line_cols
    return pl.pallas_call(
        functools.partial(line_kernel, slots, tiles),
        grid=(slots + tiles,),
        in_specs=[
            pl.BlockSpec((length, line_cols), lambda i: (jnp.maximum(slots - 1 - i, 0), 0)),
            whole_spec(width, line_cols, once=True),
            once,
            once,
            whole_spec(1, width),
            by_column(near_tokens),
            whole_spec(near_tokens, line_cols, once=True),
            ANYWHERE,
        ],
        out_specs=[
            whole_spec(length, width),
            whole_spec(1, width),
            pl.BlockSpec((tile, attn_cols), lambda i: (column(i), 0)),
            whole_spec(1, line_cols),
            ANYWHERE,
        ],
        out_shape=[
            jax.ShapeDtypeStruct((length, width), LOW),
            jax.ShapeDtypeStruct((1, width), WIDE),
            jax.ShapeDtypeStruct((width, attn_cols), LOW),
            jax.ShapeDtypeStruct((1, line_cols), WIDE),
            jax.ShapeDtypeStruct((length, width), LOW),
        ],
        scratch_shapes=[
            pltpu.VMEM((slots, length, width), LOW),
            pltpu.VMEM((2, length, width), LOW),
            pltpu.VMEM((length, width), LOW),
            pltpu.VMEM((length, width), WIDE),
            pltpu.SemaphoreType.DMA((4,)),
            pltpu.SemaphoreType.DMA((4,)),
            pltpu.SemaphoreType.DMA,
        ],
        compiler_params=pltpu.CompilerParams(
            vmem_limit_bytes=63 << 20, collective_id=3, has_side_effects=True
        ),
        cost_estimate=estimate(2 * near_tokens * width * attn_cols, 10 * near_tokens * width),
    )(line, weight, own_in, grad_middle, gain, rows_one, line, block)


def place_kernel(count, info, *refs):
    out = refs[count]
    for r in range(count):

        @pl.when(pl.program_id(0) == r)
        def _():
            out[0] = refs[r][...]


def place_rows(rows, order):
    length, width = rows[0].shape
    count = len(rows)
    held = pl.BlockSpec((length, width), lambda s, info: (0, 0), pipeline_mode=pl.Buffered(1))
    return pl.pallas_call(
        functools.partial(place_kernel, count),
        grid_spec=pltpu.PrefetchScalarGridSpec(
            num_scalar_prefetch=1,
            grid=(count,),
            in_specs=[held] * count,
            out_specs=pl.BlockSpec((1, length, width), lambda s, info: (info[s], 0, 0)),
        ),
        out_shape=jax.ShapeDtypeStruct((count, length, width), LOW),
        compiler_params=pltpu.CompilerParams(vmem_limit_bytes=32 << 20),
        cost_estimate=estimate(0, 4 * count * length * width),
    )(order, *rows)


def turn(values, cosine, sine_signed):
    return values * cosine + pltpu.roll(values, values.shape[-1] // 2, 1) * sine_signed


def turn_back(values, cosine, sine_signed):
    return values * cosine - pltpu.roll(values, values.shape[-1] // 2, 1) * sine_signed


def project_kernel(
    heads, head_dim, x0, x1, x2, x3, gains, weight, bias, cosine, sine, h_out, q_out, k_out, v_out, gain
):
    slot = pl.program_id(0)

    @pl.when(slot == 0)
    def _():
        gain[...] = gains[...].astype(WIDE).T[:8]


    def run(x_ref):
        x = x_ref[...].astype(WIDE)
        scale_inv = lax.rsqrt(jnp.mean(x * x, axis=-1, keepdims=True) + EPS)
        normed = (x * scale_inv * gain[0:1]).astype(LOW)
        h_out[0] = normed
        lin = jnp.dot(normed, weight[...], preferred_element_type=WIDE) + bias[...]
        cos, sin = cosine[0], sine[0]
        for h in range(heads + 1):
            part = turn(lin[:, h * head_dim : (h + 1) * head_dim], cos, sin).astype(LOW)
            if h < heads:
                q_out[0, :, h * head_dim : (h + 1) * head_dim] = part
            else:
                k_out[0] = part
        v_out[0] = lin[:, (heads + 1) * head_dim :].astype(LOW)

    for r, x_ref in enumerate((x0, x1, x2, x3)):
        pl.when(slot == r)(functools.partial(run, x_ref))


def project(rows, held, bias, cosine, sine, heads, head_dim):
    length, width = rows[0].shape
    count = len(rows)
    cols = (heads + 2) * head_dim
    whole = whole_spec
    by_slot = lambda *shape: pl.BlockSpec((1, *shape), lambda s: (s,) + (0,) * len(shape))
    return pl.pallas_call(
        functools.partial(project_kernel, heads, head_dim),
        grid=(count,),
        in_specs=[whole(length, width)] * count
        + [part_spec(width, 128, cols // 128), part_spec(width, cols, 0), whole(1, cols)]
        + [by_slot(length, head_dim)] * 2,
        out_specs=[
            by_slot(length, width),
            by_slot(length, heads * head_dim),
            by_slot(length, head_dim),
            by_slot(length, head_dim),
        ],
        out_shape=[
            jax.ShapeDtypeStruct((count, length, width), LOW),
            jax.ShapeDtypeStruct((count, length, heads * head_dim), LOW),
            jax.ShapeDtypeStruct((count, length, head_dim), LOW),
            jax.ShapeDtypeStruct((count, length, head_dim), LOW),
        ],
        scratch_shapes=[pltpu.VMEM((8, width), WIDE)],
        compiler_params=pltpu.CompilerParams(vmem_limit_bytes=56 << 20),
        cost_estimate=pl.CostEstimate(
            flops=2 * count * length * width * cols,
            bytes_accessed=count * length * (2 * width + cols) * 2 + width * cols * 2,
            transcendentals=0,
        ),
    )(*rows, held, held, bias, cosine, sine)


def row_blocks(length):
    return [(i, min(256, length)) for i in range(0, length, min(256, length))]


def key_biases(length, offset, start, rows, past, keys):
    past_pos = lax.broadcasted_iota(jnp.int32, (1, past), 1)
    past_bias = jnp.where((past_pos < offset) & (past_pos < length), 0.0, NEG_FILL)
    query_pos = offset + start + lax.broadcasted_iota(jnp.int32, (rows, keys), 0)
    own_pos = offset + lax.broadcasted_iota(jnp.int32, (rows, keys), 1)
    own_bias = jnp.where((own_pos <= query_pos) & (own_pos < length), 0.0, NEG_FILL)
    return past_bias, own_bias


def dot_cols(left, right):
    return lax.dot_general(left, right, (((1,), (1,)), ((), ())), preferred_element_type=WIDE)


def dot_rows(left, right):
    return lax.dot_general(left, right, (((0,), (0,)), ((), ())), preferred_element_type=WIDE)


def attend_kernel(
    heads, head_dim, scale, first, total_slots, info, q, k_past, v_past, k_own, v_own, weight, out, lse, *parts
):
    length, offset = info[first + pl.program_id(0)], info[total_slots]
    past = k_past.shape[1]
    for start, rows in row_blocks(q.shape[1]):
        keys = start + rows
        past_bias, own_bias = key_biases(length, offset, start, rows, past, keys)
        here = slice(start, start + rows)
        for h in range(heads):
            cols = slice(h * head_dim, (h + 1) * head_dim)
            query = q[0, here, cols]
            s_past = dot_cols(query, k_past[0]) * scale + past_bias
            s_own = dot_cols(query, k_own[0, :keys]) * scale + own_bias
            top = jnp.maximum(
                jnp.max(s_past, axis=1, keepdims=True), jnp.max(s_own, axis=1, keepdims=True)
            )
            e_past, e_own = jnp.exp(s_past - top), jnp.exp(s_own - top)
            total = jnp.sum(e_past, axis=1, keepdims=True) + jnp.sum(e_own, axis=1, keepdims=True)
            inverse = 1.0 / total
            mixed = jnp.dot(
                (e_past * inverse).astype(LOW), v_past[0], preferred_element_type=WIDE
            ) + jnp.dot((e_own * inverse).astype(LOW), v_own[0, :keys], preferred_element_type=WIDE)
            out[0, here, cols] = mixed.astype(LOW)
            lse[0, here, h : h + 1] = top + jnp.log(total)
        rows_out = dot_cols(out[0, here], weight[...]).astype(LOW)
        for i, part in enumerate(parts):

            @pl.when(pl.program_id(0) == i)
            def _():
                part[here] = rows_out


def attend_forward(info, q, k_past, v_past, k_own, v_own, weight, heads, head_dim, scale, first, count):
    _, length, width = q.shape
    past = k_past.shape[1]
    by_slot = lambda *shape: pl.BlockSpec((1, *shape), lambda s, info: (first + s,) + (0,) * len(shape))
    out_slot = lambda *shape: pl.BlockSpec((1, *shape), lambda s, info: (s,) + (0,) * len(shape))
    keys = count * length * (past + length) * heads
    return pl.pallas_call(
        functools.partial(attend_kernel, heads, head_dim, scale, first, q.shape[0]),
        grid_spec=pltpu.PrefetchScalarGridSpec(
            num_scalar_prefetch=1,
            grid=(count,),
            in_specs=[
                by_slot(length, width),
                by_slot(past, head_dim),
                by_slot(past, head_dim),
                by_slot(length, head_dim),
                by_slot(length, head_dim),
                whole_spec(*weight.shape, once=True),
            ],
            out_specs=[out_slot(length, width), out_slot(length, 128)]
            + [whole_spec(length, weight.shape[0])] * count,
        ),
        out_shape=[
            jax.ShapeDtypeStruct((count, length, width), LOW),
            jax.ShapeDtypeStruct((count, length, 128), WIDE),
        ]
        + [jax.ShapeDtypeStruct((length, weight.shape[0]), LOW)] * count,
        compiler_params=pltpu.CompilerParams(vmem_limit_bytes=56 << 20),
        cost_estimate=estimate(4 * keys * head_dim, 4 * count * length * width, keys),
    )(info, q, k_past, v_past, k_own, v_own, weight)


def attend_back_rows(
    heads, head_dim, scale, length, offset, q, k_past, v_past, k_own, v_own, grad, lse, cosine, sine, put,
    dk_past, dk_own, dv_past, dv_own
):
    past = k_past.shape[1]
    for start, rows in row_blocks(q.shape[1]):
        keys = start + rows
        past_bias, own_bias = key_biases(length, offset, start, rows, past, keys)
        here = slice(start, start + rows)
        cos, sin = cosine[0, here], sine[0, here]
        for h in range(heads):
            cols = slice(h * head_dim, (h + 1) * head_dim)
            query, upstream = q[0, here, cols], grad[0, here, cols]
            log_total = lse[0, here, h : h + 1]
            p_past = jnp.exp(dot_cols(query, k_past[0]) * scale + past_bias - log_total)
            p_own = jnp.exp(dot_cols(query, k_own[0, :keys]) * scale + own_bias - log_total)
            g_past = dot_cols(upstream, v_past[0])
            g_own = dot_cols(upstream, v_own[0, :keys])
            row_dot = jnp.sum(p_past * g_past, axis=1, keepdims=True) + jnp.sum(
                p_own * g_own, axis=1, keepdims=True
            )
            s_past = (p_past * (g_past - row_dot)).astype(LOW)
            s_own = (p_own * (g_own - row_dot)).astype(LOW)
            dq = (
                jnp.dot(s_past, k_past[0], preferred_element_type=WIDE)
                + jnp.dot(s_own, k_own[0, :keys], preferred_element_type=WIDE)
            ) * scale
            put(here, cols, turn_back(dq, cos, sin).astype(LOW))
            dk_past[...] += dot_rows(s_past, query)
            dk_own[:keys] += dot_rows(s_own, query)
            dv_past[...] += dot_rows(p_past.astype(LOW), upstream)
            dv_own[:keys] += dot_rows(p_own.astype(LOW), upstream)


def attend_back_kernel(
    heads,
    head_dim,
    scale,
    info,
    q,
    k_past,
    v_past,
    k_own,
    v_own,
    grad,
    lse,
    cosine,
    sine,
    dq_out,
    mine_past,
    mine_own,
    other_past,
    other_own,
    dk_past,
    dk_own,
    dv_past,
    dv_own,
):
    slot = pl.program_id(0)
    length, offset = info[slot], info[pl.num_programs(0)]
    parity = info[pl.num_programs(0) + 1]
    for total in (dk_past, dk_own, dv_past, dv_own):
        total[...] = jnp.zeros_like(total)
    attend_back_rows(
        heads, head_dim, scale, length, offset, q, k_past, v_past, k_own, v_own, grad, lse, cosine, sine,
        lambda here, cols, value: dq_out.__setitem__((0, here, cols), value),
        dk_past, dk_own, dv_past, dv_own,
    )

    @pl.when(parity == 0)
    def _():
        mine_past[0] = dk_past[...] * scale
        mine_own[0] = dk_own[...] * scale
        other_past[0] = dv_past[...]
        other_own[0] = dv_own[...]

    @pl.when(parity != 0)
    def _():
        mine_past[0] = dv_past[...]
        mine_own[0] = dv_own[...]
        other_past[0] = dk_past[...] * scale
        other_own[0] = dk_own[...] * scale


def attend_backward(
    info, q, k_past, v_past, k_own, v_own, grad, lse, cosine, sine, heads, head_dim, scale
):
    count, length, width = q.shape
    past = k_past.shape[1]
    by_slot = lambda *shape: pl.BlockSpec((1, *shape), lambda s, info: (s,) + (0,) * len(shape))
    keys = count * length * (past + length) * heads
    return pl.pallas_call(
        functools.partial(attend_back_kernel, heads, head_dim, scale),
        grid_spec=pltpu.PrefetchScalarGridSpec(
            num_scalar_prefetch=1,
            grid=(count,),
            in_specs=[
                by_slot(length, width),
                by_slot(past, head_dim),
                by_slot(past, head_dim),
                by_slot(length, head_dim),
                by_slot(length, head_dim),
                by_slot(length, width),
                by_slot(length, 128),
                by_slot(length, head_dim),
                by_slot(length, head_dim),
            ],
            out_specs=[
                by_slot(length, width),
                by_slot(past, head_dim),
                by_slot(length, head_dim),
                by_slot(past, head_dim),
                by_slot(length, head_dim),
            ],
            scratch_shapes=[
                pltpu.VMEM((past, head_dim), WIDE),
                pltpu.VMEM((length, head_dim), WIDE),
                pltpu.VMEM((past, head_dim), WIDE),
                pltpu.VMEM((length, head_dim), WIDE),
            ],
        ),
        out_shape=[
            jax.ShapeDtypeStruct((count, length, width), LOW),
            jax.ShapeDtypeStruct((count, past, head_dim), WIDE),
            jax.ShapeDtypeStruct((count, length, head_dim), WIDE),
            jax.ShapeDtypeStruct((count, past, head_dim), WIDE),
            jax.ShapeDtypeStruct((count, length, head_dim), WIDE),
        ],
        compiler_params=pltpu.CompilerParams(vmem_limit_bytes=56 << 20),
        cost_estimate=estimate(10 * keys * head_dim, 8 * count * length * width, keys),
    )(info, q, k_past, v_past, k_own, v_own, grad, lse, cosine, sine)


def exchange_kernel(
    heads, head_dim, scale, slots, tiles, info, q, k_past, v_past, k_own, v_own, grad, lse, cosine, sine,
    cosine_all, sine_all, branch, mixed, first, second, mlp_far, mlp_side, mlp_own, middle, line, out_grad,
    block, mine_past, mine_own, other_past, other_own, got_past, got_own, side_out, side_in, dk_past, dk_own,
    dv_past, dv_own, across_in, rows, last_in, send, recv, load
):
    step = pl.program_id(0)
    tensor_rank = lax.axis_index("tp")
    core, far, side = partners_of()
    parity = lax.rem(tensor_rank, 2)
    offset = lax.axis_index("ctx") * q.shape[1]
    remote = remote_copy(send, recv)
    pasts = [remote(other_past.at[r], got_past.at[r ^ 1], r, core) for r in range(slots)]
    owns = [remote(other_own.at[r], got_own.at[r ^ 1], slots + r, core) for r in range(slots)]
    sides = [remote(side_out.at[r], side_in.at[r], 2 * slots + r, side) for r in range(slots)]
    across = [
        remote(first, across_in.at[0], 3 * slots, far),
        remote(second, across_in.at[1], 3 * slots + 1, side),
    ]
    lasts = [
        remote(rows.at[0], last_in.at[0], 3 * slots + 2, far),
        remote(rows.at[1], last_in.at[1], 3 * slots + 3, side),
    ]
    loading = [
        pltpu.make_async_copy(source, rows.at[i], load.at[i])
        for i, source in enumerate((mlp_far, mlp_side, mlp_own))
    ]
    half = across_in.shape[1]

    @pl.when(step == 0)
    def _():
        for copy in loading:
            copy.start()
        meet((core, far, side))
        for copy in across:
            copy.start()

    @pl.when(step < slots)
    def _():
        length = info[jnp.minimum(step, slots - 1)]
        for total in (dk_past, dk_own, dv_past, dv_own):
            total[...] = jnp.zeros_like(total)
        attend_back_rows(
            heads, head_dim, scale, length, offset, q, k_past, v_past, k_own, v_own, grad, lse, cosine,
            sine, lambda here, cols, value: line.__setitem__((step, here, cols), value),
            dk_past, dk_own, dv_past, dv_own,
        )

        @pl.when(parity == 0)
        def _():
            mine_past[step] = dk_past[...] * scale
            mine_own[step] = dk_own[...] * scale
            other_past[step] = dv_past[...]
            other_own[step] = dv_own[...]

        @pl.when(parity != 0)
        def _():
            mine_past[step] = dv_past[...]
            mine_own[step] = dv_own[...]
            other_past[step] = dk_past[...] * scale
            other_own[step] = dk_own[...] * scale

    for r in range(slots):

        def start(r=r):
            pasts[r].start()
            owns[r].start()

        pl.when(step == r)(start)

    for pair in range(0, slots, 2):

        def merge(pair=pair):
            for r in (pair, pair + 1):
                pasts[r ^ 1].wait_recv()
                side_out[r] = (mine_past[r] + got_past[r]).astype(LOW)
                sides[r].start()

        pl.when(step == pair + 1)(merge)

    @pl.when(step == slots - 1)
    def _():
        for copy in loading:
            copy.wait()
        for copy in across:
            copy.wait_recv()
        for i, here in ((0, pl.ds(half, half)), (1, pl.ds(0, half))):
            rows[i, here] = (rows[i, here].astype(WIDE) + across_in[1 - i].astype(WIDE)).astype(LOW)
            lasts[i].start()

    @pl.when(step >= slots)
    def _():
        out_grad[...] = dot_rows(branch[...], mixed[...]).astype(LOW)

    @pl.when(step == slots + tiles - 1)
    def _():
        for r in range(slots):
            owns[r ^ 1].wait_recv()
            sides[r].wait_recv()
            total = mine_own[r] + got_own[r] + side_in[r].astype(WIDE)
            back = turn_back(total, cosine_all[r], sine_all[r])
            line[r, :, heads * head_dim :] = jnp.where(parity == 0, back, total).astype(LOW)
        for copy in lasts:
            copy.wait_recv()
        block[...] = (
            middle[...] + rows[2].astype(WIDE) + last_in[0].astype(WIDE) + last_in[1].astype(WIDE)
        ).astype(LOW)
        for copy in (*pasts, *owns, *sides, *across, *lasts):
            copy.wait_send()


def attend_exchange(
    info, q, k_past, v_past, k_own, v_own, grad, lse, cosine, sine, heads, head_dim, scale, branch, mixed, mlp, middle
):
    count, length, width = q.shape
    past = k_past.shape[1]
    tokens, model_width = branch.shape
    tile = 256
    tiles = model_width // tile
    slot = lambda i: jnp.minimum(i, count - 1)
    by_slot = lambda *shape: pl.BlockSpec((1, *shape), lambda i, info: (slot(i),) + (0,) * len(shape))
    column = lambda i: jnp.clip(i - count, 0, tiles - 1)
    held = lambda *shape: pl.BlockSpec(
        shape, lambda i, info: (0,) * len(shape), pipeline_mode=pl.Buffered(1)
    )
    line_cols = width + head_dim
    return pl.pallas_call(
        functools.partial(exchange_kernel, heads, head_dim, scale, count, tiles),
        grid_spec=pltpu.PrefetchScalarGridSpec(
            num_scalar_prefetch=1,
            grid=(count + tiles,),
            in_specs=[
                by_slot(length, width),
                by_slot(past, head_dim),
                by_slot(past, head_dim),
                by_slot(length, head_dim),
                by_slot(length, head_dim),
                by_slot(length, width),
                by_slot(length, 128),
                by_slot(length, head_dim),
                by_slot(length, head_dim),
                held(count, length, head_dim),
                held(count, length, head_dim),
                pl.BlockSpec((tokens, tile), lambda i, info: (0, column(i))),
                held(*mixed.shape),
            ]
            + [ANYWHERE] * 5
            + [held(length, model_width)],
            out_specs=[
                held(count, length, line_cols),
                pl.BlockSpec((tile, width), lambda i, info: (column(i), 0)),
                held(length, model_width),
            ],
            scratch_shapes=[pltpu.VMEM((count, length, head_dim), WIDE)] * 6
            + [pltpu.VMEM((count, length, head_dim), LOW)] * 2
            + [pltpu.VMEM((length, head_dim), WIDE)] * 4
            + [
                pltpu.VMEM((2, length // 2, model_width), LOW),
                pltpu.VMEM((3, length, model_width), LOW),
                pltpu.VMEM((2, length, model_width), LOW),
                pltpu.SemaphoreType.DMA((3 * count + 4,)),
                pltpu.SemaphoreType.DMA((3 * count + 4,)),
                pltpu.SemaphoreType.DMA((3,)),
            ],
        ),
        out_shape=[
            jax.ShapeDtypeStruct((count, length, line_cols), LOW),
            jax.ShapeDtypeStruct((model_width, width), LOW),
            jax.ShapeDtypeStruct((length, model_width), LOW),
        ],
        compiler_params=pltpu.CompilerParams(
            vmem_limit_bytes=63 << 20, collective_id=4, has_side_effects=True
        ),
        cost_estimate=estimate(2 * tokens * model_width * width, 10 * tokens * width),
    )(info, q, k_past, v_past, k_own, v_own, grad, lse, cosine, sine, cosine, sine, branch, mixed, *mlp, middle)


def local(
    hidden_in,
    cotangent,
    seq_lengths,
    positions,
    permutation,
    query_weight,
    keyval_weight,
    output_weight,
    norm_gains,
    bias_query,
    bias_keyval,
    gate_weight,
    up_weight,
    down_weight,
):
    group_rank = lax.axis_index("fsdp")
    ctx_rank = lax.axis_index("ctx")
    tensor_rank = lax.axis_index("tp")
    fsdp_count = lax.axis_size("fsdp")
    ctx_count = lax.axis_size("ctx")
    tensor_count = lax.axis_size("tp")
    seq_grp, local_len, model_width = hidden_in.shape
    heads, head_dim = bias_query.shape
    keyval_heads = bias_keyval.shape[0] // 2
    assert seq_grp == tensor_count == fsdp_count == len(DEAL_SHIFT)
    token_count = seq_grp * local_len
    scale = 1.0 / math.sqrt(head_dim)
    offset = ctx_rank * local_len
    head_pair = tensor_rank // (tensor_count // keyval_heads)
    parity = tensor_rank % 2
    shifts = jnp.array(DEAL_SHIFT, jnp.int32)

    table = permutation.reshape(fsdp_count, seq_grp)
    far_group = lax.rem(group_rank + shifts[tensor_rank], fsdp_count)
    far_row = lax.dynamic_index_in_dim(table, far_group, 0, keepdims=False)
    leaving = jnp.sum(jnp.where(far_row // seq_grp == group_rank, far_row - group_rank * seq_grp, 0))
    own_row = lax.dynamic_index_in_dim(table, group_rank, 0, keepdims=False)
    slot_now, seq_now, home_now = [], [], []
    for r in range(seq_grp):
        shift = shifts[tensor_rank ^ r]
        source = lax.rem(group_rank - shift + fsdp_count, fsdp_count)
        hit = own_row // seq_grp == source
        slot_now.append(jnp.sum(jnp.where(hit, jnp.arange(seq_grp), 0)))
        seq_now.append(jnp.sum(jnp.where(hit, own_row, 0)))
        target = lax.rem(group_rank + shift, fsdp_count)
        target_row = lax.dynamic_index_in_dim(table, target, 0, keepdims=False)
        home_now.append(
            jnp.sum(jnp.where(target_row // seq_grp == group_rank, target_row - group_rank * seq_grp, 0))
        )
    there = [
        (f * tensor_count + t, (f + DEAL_SHIFT[t]) % fsdp_count * tensor_count + t)
        for f in range(fsdp_count)
        for t in range(tensor_count)
    ]
    back = [(target, source) for source, target in there]

    split = units_split()
    head_width = 2 * head_dim
    query_cols = heads * head_dim
    near_cols = query_cols + head_width + 128

    outgoing = lax.dynamic_index_in_dim(hidden_in, leaving, 0, keepdims=False)
    own_in = lax.ppermute(outgoing, ("fsdp", "tp"), there)
    small = jnp.concatenate(
        [
            query_weight,
            lax.dynamic_slice_in_dim(keyval_weight, head_pair * head_width, head_width, axis=1),
            jnp.pad(norm_gains.T, ((0, 0), (0, 128 - norm_gains.shape[0]))),
            output_weight.T,
        ],
        axis=1,
    )
    units = gate_weight.shape[1]
    units_pad = -(-units // 256) * 256
    widen = lambda w: jnp.pad(w, ((0, 0), (0, units_pad - units)))
    shards = [widen(w) for w in (down_weight.T, gate_weight, up_weight)]
    if split:
        half_units = units_pad // 2
        cut = lambda w, c: lax.dynamic_slice_in_dim(w, c * half_units, half_units, axis=1)

        def in_order(own, other):
            return jnp.stack(
                [jnp.where(ctx_rank == 0, own, other), jnp.where(ctx_rank == 0, other, own)]
            )

        def all_rows(both, *earlier):
            full = lax.all_gather(after(both, *earlier), "fsdp", axis=0, tiled=False)
            return full.reshape(-1, both.shape[-1])

        small_both = in_order(small, from_partner(after(small, outgoing), "ctx", 1))
        first_units = half_units // 2 // 256 * 256
        first_cols = 3 * first_units

        def in_parts(c):
            halves = [cut(w, c) for w in shards]
            return jnp.concatenate(
                [w[:, :first_units] for w in halves] + [w[:, first_units:] for w in halves], axis=1
            )

        arriving_units = from_partner(after(in_parts(1 - ctx_rank), small), "ctx", 1)
        unit_both = in_order(in_parts(ctx_rank), arriving_units)
        slot_pick = lax.dynamic_index_in_dim(cotangent, tensor_rank, 0, keepdims=False)
        other_own = from_partner(after(slot_pick, arriving_units), "ctx", 1)
        other_far = from_partner(other_own, "tp", 2)
        other_near = from_partner(other_own, "tp", 1)
    else:
        all_rows = lambda shard, *earlier: lax.all_gather(
            shard, ("fsdp", "ctx"), axis=0, tiled=True
        )
        small_both, unit_both, half_units = small, jnp.concatenate(shards, axis=1), units_pad
    far_in = from_partner(own_in, "tp", 2)
    near_in = from_partner(own_in, "tp", 1)
    cross_in = from_partner(far_in, "tp", 1)

    lengths_now = jnp.stack([seq_lengths[s] for s in seq_now])
    info = jnp.concatenate([lengths_now, jnp.stack([offset, parity])]).astype(jnp.int32)
    positions_now = jnp.stack(
        [lax.dynamic_index_in_dim(positions, s, 0, keepdims=False) for s in seq_now]
    )
    lane = jnp.arange(head_dim)
    frequency = 1.0 / ROPE_BASE ** ((lane % (head_dim // 2)).astype(WIDE) * 2.0 / head_dim)
    angles = positions_now.astype(WIDE)[..., None] * frequency
    cosine = jnp.cos(angles)
    sine = jnp.sin(angles) * jnp.where(lane < head_dim // 2, -1.0, 1.0)
    grad_slots = [lax.dynamic_index_in_dim(cotangent, s, 0, keepdims=False) for s in slot_now]

    near_full = all_rows(small_both, own_in)
    if split:
        units_a = all_rows(unit_both[..., :first_cols], cross_in)
        units_b = all_rows(unit_both[..., first_cols:], cross_in)
    else:
        down_full = all_rows(unit_both[..., :half_units], cross_in)
        gate_up_full = all_rows(unit_both[..., half_units:], cross_in)
    project_full = near_full[:, : query_cols + head_width]
    output_full = near_full[:, near_cols:]
    bias_head = lax.dynamic_slice_in_dim(bias_keyval, head_pair * 2, 2, axis=0)
    bias_row = jnp.concatenate([bias_query.reshape(1, -1), bias_head.reshape(1, -1)], axis=1).astype(WIDE)
    normed_one, query_rot, key_own, value_own = project(
        (own_in, near_in, far_in, cross_in),
        near_full,
        bias_row,
        after(cosine, other_own, unit_both) if split else cosine,
        sine,
        heads,
        head_dim,
    )
    gains_now = near_full[:, query_cols + head_width : near_cols][:, :2].astype(WIDE).T
    if split:
        key_past, value_past = lax.ppermute((key_own, value_own), "ctx", [(0, 1)])
        other_cross = from_partner(after(other_far, query_rot), "tp", 1)
        other_rows = (other_own, other_near, other_far, other_cross)
        key_past = after(key_past, *other_rows)
    else:
        key_past = lax.all_gather(key_own, "ctx", axis=1, tiled=True)
        value_past = lax.all_gather(value_own, "ctx", axis=1, tiled=True)
    attend = lambda first, *held: attend_forward(
        info, query_rot, *held, key_own, value_own, output_full, heads, head_dim, scale, first, 2
    )
    in_share = own_in.astype(WIDE)

    mixed_far, lse_far, *attn_far = attend(2, key_past, value_past)
    attn_wide = collect_far(attn_far[0], attn_far[1])
    attn_got = from_partner(attn_wide, "tp", 2)
    mixed_near, lse_near, *attn_near = attend(0, after(key_past, attn_wide), value_past)
    attn_core = from_partner(attn_near[1], "tp", 1)
    middle_share = (
        in_share
        + attn_near[0].astype(WIDE)
        + attn_core.astype(WIDE)
        + attn_got.astype(WIDE)
    )
    inv_two = lax.rsqrt(jnp.mean(middle_share * middle_share, axis=-1, keepdims=True) + EPS)
    normed_share = (middle_share * inv_two * gains_now[1]).astype(LOW)
    half_len = local_len // 2

    if split:
        picks = [s ^ tensor_rank for s in slot_now]
        grad_hidden, grad_rows = chosen_rows(
            jnp.stack(slot_now + picks).astype(jnp.int32),
            after(cotangent, normed_share),
            other_rows,
            units_a,
            0,
            3,
        )
    else:
        grad_hidden, grad_rows = stack_rows([(g,) for g in grad_slots], down_full, 0, 1)

    def spread_all(own):
        far = from_partner(own, "tp", 2)
        near = from_partner(own, "tp", 1)
        if not split:
            return (own, near, far, from_partner(far, "tp", 1))
        side = from_partner(own, "ctx", 1)
        held = after(far, grad_hidden), after(side, grad_hidden)
        across = from_partner(held[0][:half_len], "ctx", 1), from_partner(held[1][half_len:], "tp", 2)
        cores = [from_partner(v, "tp", 1) for v in (*held, *across)]
        return (own, near, far, cores[0], side, cores[1], *across, *cores[2:])

    def in_slots(rows):
        if not split:
            return [(row,) for row in rows]
        return [(row,) for row in rows[:6]] + [rows[6:8], rows[8:]]

    normed_slots = in_slots(spread_all(normed_share))
    if split:
        gate_lin, normed_two = stack_rows(normed_slots, units_a, 1, 3)
        hidden_a, gate_a, up_a = hidden_units(normed_two, units_a, 2, 3, gate_lin, grad_hidden)
        grad_a = first_grads(grad_rows, normed_two, hidden_a, gate_a, up_a)
        hidden_b, gate_b, up_b = full_units(after(normed_two, grad_a), grad_rows, units_b)
    else:
        gate_lin, normed_two = stack_rows(normed_slots, gate_up_full, 0, 2)
        hidden_act, grad_gate, grad_up = hidden_units(
            normed_two, gate_up_full, 1, 2, gate_lin, grad_hidden
        )

    def collect_all(lefts, weights, *earlier):
        lefts = list(lefts)
        lefts[0] = after(lefts[0], *earlier)
        last = back_rows(lefts, weights, 2, 2, local_len)
        got = [from_partner(collect_far(last[0], last[1]), "tp", 2)]
        first = back_rows(lefts, weights, 0, 2, local_len)
        got.append(from_partner(first[1], "tp", 1))

        def finish():
            return sum((v.astype(WIDE) for v in got), first[0].astype(WIDE))

        return first[0], finish

    if split:
        grad_two_share, down_b, up_grad_b = collect_back(
            (gate_a, up_a),
            (gate_b, up_b),
            units_a,
            units_b,
            grad_rows,
            normed_two,
            hidden_b,
            local_len,
        )
        grad_middle, gain_two, gate_grad_b, grad_branch, *mlp = spread_branch(
            grad_two_share,
            middle_share,
            grad_slots[0],
            gains_now[1:2],
            hidden_a,
            hidden_b,
            units_a,
            units_b,
            normed_two,
            gate_b,
        )
        mlp_own, mlp_far, mlp_side, mlp_first, mlp_second = mlp
        grad_branch = grad_branch.reshape(token_count, model_width)
    else:
        first_back, finish_back = collect_all(
            (grad_gate, grad_up), ((gate_up_full, 0, 2), (gate_up_full, 1, 2))
        )
        down_grad = contract_rows(after(grad_rows, first_back), hidden_act, LOW)
        gate_grad = contract_rows(normed_two, after(grad_gate, down_grad), LOW)
        grad_two_share = finish_back()
        grad_norm_two, gain_two = norm_backward(
            middle_share, inv_two, gains_now[1], grad_two_share
        )
        grad_middle = grad_slots[0].astype(WIDE) + grad_norm_two
        branch_own = grad_middle.astype(LOW)
        branch_far = from_partner(branch_own, "tp", 2)
        branch_near = from_partner(branch_own, "tp", 1)
        branch_cross = from_partner(branch_far, "tp", 1)
        grad_branch = jnp.concatenate([branch_own, branch_near, branch_far, branch_cross], axis=0)
        up_grad = contract_rows(normed_two, after(grad_up, branch_own), LOW)

    grad_mixed = product(grad_branch, output_full, LOW)
    mixed_flat = jnp.concatenate([mixed_near, mixed_far], axis=0).reshape(token_count, query_cols)
    lse = jnp.concatenate([lse_near, lse_far], axis=0)
    attend_args = (
        info,
        query_rot,
        key_past,
        value_past,
        key_own,
        value_own,
        grad_mixed.reshape(seq_grp, local_len, query_cols),
        lse,
        cosine,
        sine,
        heads,
        head_dim,
        scale,
    )
    if split:
        line_grad, output_grad, block_share = attend_exchange(
            *attend_args,
            grad_branch,
            mixed_flat,
            (mlp_first, mlp_second, mlp_far, mlp_side, mlp_own),
            middle_share,
        )
        line_grad = line_grad.reshape(token_count, -1)
    else:
        grad_query, mine_past, mine_own, other_past, other_own = attend_backward(*attend_args)
        swap = lambda value: jnp.stack([value[r ^ 1] for r in range(seq_grp)])
        got_past, got_own = from_partner((other_past, other_own), "tp", 1)
        past_sum = mine_past + swap(got_past)
        own_sum = mine_own + swap(got_own)
        own_sum = own_sum + lax.psum_scatter(past_sum, "ctx", scatter_dimension=1, tiled=True)
        half_lanes = head_dim // 2
        turned = own_sum * cosine - jnp.roll(own_sum, half_lanes, axis=-1) * sine
        own_grad = jnp.where(parity == 0, turned, own_sum).astype(LOW).reshape(token_count, head_dim)
        line_grad = jnp.concatenate([grad_query.reshape(token_count, query_cols), own_grad], axis=1)
    own_weight = lax.dynamic_slice_in_dim(
        project_full, query_cols + parity * head_dim, head_dim, axis=1
    )
    back_full = jnp.concatenate([project_full[:, :query_cols], own_weight], axis=1)
    normed_flat = normed_one.reshape(token_count, model_width)
    if split:
        input_share, gain_one, attn_grad, bias_grad, block_home = finish_rows(
            line_grad,
            back_full,
            own_in,
            grad_middle,
            gains_now[0:1],
            normed_flat,
            block_share,
        )
        attn_grad = jnp.concatenate([attn_grad, output_grad], axis=1)
    else:
        half = token_count // 2
        line_far = contract_cols(line_grad[half:], back_full, LOW).reshape(2, local_len, model_width)
        line_near = contract_cols(line_grad[:half], back_full, LOW).reshape(2, local_len, model_width)
        line_wide = collect_far(line_far[0], line_far[1])
        line_got = from_partner(line_wide, "tp", 2)
        line_core = from_partner(line_near[1], "tp", 1)
        first_mlp, finish_mlp = collect_all((hidden_act,), ((down_full, 0, 1),), up_grad, branch_far)
        block_share = (middle_share + finish_mlp()).astype(LOW)
        grad_one_share = line_near[0].astype(WIDE) + line_core.astype(WIDE) + line_got.astype(WIDE)
        inv_one = lax.rsqrt(jnp.mean(in_share * in_share, axis=-1, keepdims=True) + EPS)
        grad_norm_one, gain_one = norm_backward(in_share, inv_one, gains_now[0], grad_one_share)
        input_share = (grad_middle + grad_norm_one).astype(LOW)
        attn_grad = jnp.concatenate(
            [contract_rows(normed_flat, line_grad, LOW), contract_rows(grad_branch, mixed_flat, LOW)],
            axis=1,
        )
        bias_grad = jnp.sum(line_grad.astype(WIDE), axis=0)

    def scatter_units(grad):
        if not split:
            return scatter_sum(grad, ctx_rank, LOW)
        return lax.psum_scatter(grad, "fsdp", scatter_dimension=0, tiled=True)

    unit_grads = (grad_a, down_b, up_grad_b, gate_grad_b) if split else (down_grad, gate_grad, up_grad)
    unit_sums = [scatter_units(g) for g in unit_grads]

    attn_end = scatter_sum(attn_grad, ctx_rank, LOW, *unit_sums)

    home_order = jnp.stack(home_now).astype(jnp.int32)

    def leave(share):
        return lax.ppermute(share, ("fsdp", "tp"), back)

    def arrive(own):
        far = from_partner(own, "tp", 2)
        near = from_partner(own, "tp", 1)
        return place_rows((own, near, far, from_partner(far, "tp", 1)), home_order)

    input_home = leave(input_share)
    if not split:
        block_home = leave(block_share)
    block_out = arrive(block_home)
    input_grad = arrive(input_home)

    gain_grad = jnp.concatenate([gain_one, gain_two], axis=0).T
    gain_grad = gain_grad + from_partner(gain_grad, "tp", 1)
    gain_grad = gain_grad + from_partner(gain_grad, "tp", 2)
    shard_count = fsdp_count * ctx_count
    share = head_dim // shard_count
    bias_cols = jnp.transpose(bias_grad.reshape(heads + 1, shard_count, share), (1, 2, 0))
    bias_cols = jnp.pad(bias_cols, ((0, 0), (0, (model_width - head_dim) // shard_count), (0, 0)))
    tiny = jnp.concatenate([gain_grad, bias_cols.reshape(model_width, heads + 1)], axis=1)
    tiny = jnp.pad(tiny, ((0, 0), (0, 8 - tiny.shape[1])))
    tiny = tiny.reshape(fsdp_count, ctx_count, model_width // shard_count, 8)
    if split:
        kept, sent = scatter_ctx(tiny, ctx_rank)
        tiny = kept + from_partner(sent, "ctx", 1)
    else:
        tiny = lax.psum_scatter(tiny, "ctx", scatter_dimension=1, tiled=True)
    tiny = tiny.reshape(fsdp_count, -1, 8)
    pick = lambda shift: lax.dynamic_index_in_dim(
        tiny, lax.rem(group_rank + shift, fsdp_count), 0, keepdims=False
    )
    tiny_grad = pick(0)
    for shift in range(1, fsdp_count):
        pairs = [(f, (f + shift) % fsdp_count) for f in range(fsdp_count)]
        tiny_grad = tiny_grad + lax.ppermute(pick(shift), "fsdp", pairs)

    if split:

        def unit_end(total, *earlier):
            kept, sent = scatter_ctx(total.reshape(1, ctx_count, -1, total.shape[1]), ctx_rank)
            return kept[0], from_partner(after(sent[0], *earlier), "ctx", 1)

        own_a, got_a = unit_end(unit_sums[0], line_grad)
        ends = [unit_end(t, line_grad) for t in unit_sums[1:]]

        def joined(part, end):
            cols = slice(part * first_units, (part + 1) * first_units)
            own = jnp.concatenate([own_a[:, cols], end[0]], axis=1)
            got = jnp.concatenate([got_a[:, cols], end[1]], axis=1)
            first, second = jnp.where(ctx_rank == 0, own, got), jnp.where(ctx_rank == 0, got, own)
            return jnp.concatenate([first, second], axis=1)[:, :units].astype(WIDE)

        down_end, gate_end, up_end = joined(0, ends[0]), joined(1, ends[2]), joined(2, ends[1])
    else:
        down_end, gate_end, up_end = (t[:, :units].astype(WIDE) for t in unit_sums)
    return (
        block_out,
        input_grad,
        attn_end[:, :query_cols].astype(WIDE),
        attn_end[:, query_cols : query_cols + head_dim].astype(WIDE),
        attn_end[:, query_cols + head_dim :].astype(WIDE).T,
        tiny_grad[:, :2].T,
        tiny_grad[:share, 2 : 2 + heads].T,
        tiny_grad[:share, 2 + heads : 3 + heads].T,
        gate_end,
        up_end,
        down_end.T,
    )


def solution(mesh):
    placed = (
        P("fsdp", "ctx", None),
        P("fsdp", "ctx", None),
        P(),
        P(None, "ctx"),
        P(),
        P(("fsdp", "ctx"), "tp"),
        P(("fsdp", "ctx"), None),
        P("tp", ("fsdp", "ctx")),
        P(None, ("fsdp", "ctx")),
        P("tp", None),
        P(),
        P(("fsdp", "ctx"), "tp"),
        P(("fsdp", "ctx"), "tp"),
        P("tp", ("fsdp", "ctx")),
    )
    return jax.shard_map(
        local,
        mesh=mesh,
        in_specs=placed,
        out_specs=(
            P("fsdp", "ctx", None),
            P("fsdp", "ctx", None),
            P(("fsdp", "ctx"), "tp"),
            P(("fsdp", "ctx"), "tp"),
            P("tp", ("fsdp", "ctx")),
            P(None, ("fsdp", "ctx")),
            P("tp", ("fsdp", "ctx")),
            P("tp", ("fsdp", "ctx")),
            P(("fsdp", "ctx"), "tp"),
            P(("fsdp", "ctx"), "tp"),
            P("tp", ("fsdp", "ctx")),
        ),
        check_vma=False,
    )
```

```python
import functools
import math

import jax
import jax.numpy as jnp
from jax import lax
from jax.experimental import pallas as pl
from jax.experimental.pallas import tpu as pltpu
from jax.sharding import PartitionSpec as P

EPS = 1e-06
ROPE_BASE = 10000.0
NEG_FILL = -1e30
LOW = jnp.bfloat16
WIDE = jnp.float32
DEAL_SHIFT = (0, 2, 1, 3)


def from_partner(value, axis, apart):
    pairs = [(source, source ^ apart) for source in range(lax.axis_size(axis))]
    return lax.ppermute(value, axis, pairs)


def product(left_side, right_side, kind=WIDE):
    return jnp.dot(left_side, right_side, preferred_element_type=WIDE).astype(kind)


def contract_rows(left_side, right_side, kind=WIDE):
    return lax.dot_general(
        left_side, right_side, (((0,), (0,)), ((), ())), preferred_element_type=WIDE
    ).astype(kind)


def contract_cols(left_side, right_side, kind=WIDE):
    return lax.dot_general(
        left_side, right_side, (((1,), (1,)), ((), ())), preferred_element_type=WIDE
    ).astype(kind)


def norm_backward(values, scale_inv, gain_row, upstream):
    scaled = gain_row * upstream
    inner_mean = jnp.mean(values * scaled, axis=-1, keepdims=True)
    grad_in = scale_inv * scaled - values * (scale_inv * scale_inv * scale_inv) * inner_mean
    gain_grad = jnp.sum(upstream * values * scale_inv, axis=0, keepdims=True)
    return (grad_in, gain_grad)


def after(value, *earlier):
    return lax.optimization_barrier((value, *earlier))[0]


def collect_far(far_part, cross_part):
    wide = far_part.astype(WIDE) + from_partner(cross_part, "tp", 1).astype(WIDE)
    return wide.astype(LOW)


def units_split():
    return lax.axis_size("ctx") == 2


def all_rows(shard):
    return lax.all_gather(shard, "fsdp", axis=0, tiled=True)


def scatter_ctx(blocks, ctx_rank):
    kept = lax.dynamic_index_in_dim(blocks, ctx_rank, 1, keepdims=False)
    sent = lax.dynamic_index_in_dim(blocks, 1 - ctx_rank, 1, keepdims=False)
    return kept, sent


def scatter_sum(grad, ctx_rank, kind, *earlier):
    fsdp_count, ctx_count = lax.axis_size("fsdp"), lax.axis_size("ctx")
    rows, cols = grad.shape
    blocks = grad.reshape(fsdp_count, ctx_count, rows // (fsdp_count * ctx_count), cols)
    if ctx_count == 2:
        kept, sent = scatter_ctx(blocks, ctx_rank)
        got = from_partner(sent, "ctx", 1)
        held = (after(kept, *earlier).astype(WIDE) + got.astype(WIDE)).astype(kind)
    else:
        swapped = jnp.swapaxes(blocks, 0, 1).reshape(rows, cols)
        held = lax.psum_scatter(swapped, "ctx", scatter_dimension=0, tiled=True)
    held = held.reshape(rows // ctx_count, cols)
    return lax.psum_scatter(held, "fsdp", scatter_dimension=0, tiled=True)


def estimate(flops, moved, transcendentals=0):
    return pl.CostEstimate(flops=flops, bytes_accessed=moved, transcendentals=transcendentals)


def part_spec(rows, cols, part):
    return pl.BlockSpec((rows, cols), lambda *_: (0, part), pipeline_mode=pl.Buffered(1))


def whole_spec(*shape, once=False):
    mode = {"pipeline_mode": pl.Buffered(1)} if once else {}
    return pl.BlockSpec(shape, lambda *_: (0,) * len(shape), **mode)


def rows_kernel(groups, *refs):
    slot = pl.program_id(0)
    weight, lin, stacked = refs[-3:]

    def run(pieces):
        start = 0
        for piece in pieces:
            stacked[start : start + piece.shape[0]] = piece[...]
            start += piece.shape[0]
        lin[...] = jnp.dot(stacked[...], weight[...], preferred_element_type=WIDE).astype(LOW)

    first = 0
    for r, pieces in enumerate(groups):
        pl.when(slot == r)(functools.partial(run, refs[first : first + pieces]))
        first += pieces


def stack_rows(slots, weight, part, parts):
    groups = [len(s) for s in slots]
    rows = [piece for s in slots for piece in s]
    width, length = rows[0].shape[1], sum(piece.shape[0] for piece in slots[0])
    count, cols = len(slots), weight.shape[1] // parts
    return pl.pallas_call(
        functools.partial(rows_kernel, groups),
        grid=(count,),
        in_specs=[whole_spec(*piece.shape, once=True) for piece in rows]
        + [part_spec(width, cols, part)],
        out_specs=[
            pl.BlockSpec((length, cols), lambda s: (s, 0)),
            pl.BlockSpec((length, width), lambda s: (s, 0)),
        ],
        out_shape=[
            jax.ShapeDtypeStruct((count * length, cols), LOW),
            jax.ShapeDtypeStruct((count * length, width), LOW),
        ],
        compiler_params=pltpu.CompilerParams(vmem_limit_bytes=60 << 20),
        cost_estimate=estimate(
            2 * count * length * width * cols, 2 * (count * length * (2 * width + cols) + width * cols)
        ),
    )(*rows, weight)


def units_kernel(h, up, gate, grad, hid, grad_gate, grad_up):
    up_lin = jnp.dot(h[...], up[...], preferred_element_type=WIDE)
    gate_lin = gate[...].astype(WIDE)
    grad_hidden = grad[...].astype(WIDE)
    sigmoid = 1.0 / (1.0 + jnp.exp(-gate_lin))
    silu = gate_lin * sigmoid
    hid[...] = (silu * up_lin).astype(LOW)
    grad_gate[...] = (grad_hidden * up_lin * sigmoid * (1.0 + gate_lin * (1.0 - sigmoid))).astype(LOW)
    grad_up[...] = (grad_hidden * silu).astype(LOW)


def hidden_units(h, up, part, parts, gate_lin, grad_hidden):
    tokens, width = h.shape
    cols = up.shape[1] // parts
    step = math.gcd(512, tokens)
    by_row = lambda n: pl.BlockSpec((step, n), lambda i: (i, 0))
    return pl.pallas_call(
        units_kernel,
        grid=(tokens // step,),
        in_specs=[by_row(width), part_spec(width, cols, part), by_row(cols), by_row(cols)],
        out_specs=[by_row(cols)] * 3,
        out_shape=[jax.ShapeDtypeStruct((tokens, cols), LOW)] * 3,
        compiler_params=pltpu.CompilerParams(vmem_limit_bytes=60 << 20),
        cost_estimate=estimate(
            2 * tokens * width * cols, 2 * (tokens * width + width * cols + 5 * tokens * cols)
        ),
    )(h, up, gate_lin, grad_hidden)


def back_kernel(terms, *refs):
    lefts, weights, outs = refs[:terms], refs[terms : 2 * terms], refs[2 * terms :]
    total = None
    for left, weight in zip(lefts, weights):
        term = dot_cols(left[...], weight[...])
        total = term if total is None else total + term
    for i, out in enumerate(outs):

        @pl.when(pl.program_id(0) == i)
        def _():
            out[...] = total.astype(LOW)


def back_rows(lefts, weights, first_slot, slots, length):
    width = weights[0][0].shape[0]
    depth = sum(left.shape[1] for left in lefts)
    return pl.pallas_call(
        functools.partial(back_kernel, len(lefts)),
        grid=(slots,),
        in_specs=[
            pl.BlockSpec((length, left.shape[1]), lambda s: (first_slot + s, 0)) for left in lefts
        ]
        + [part_spec(width, w.shape[1] // parts, part) for w, part, parts in weights],
        out_specs=[whole_spec(length, width)] * slots,
        out_shape=[jax.ShapeDtypeStruct((length, width), LOW)] * slots,
        compiler_params=pltpu.CompilerParams(vmem_limit_bytes=60 << 20),
        cost_estimate=estimate(
            2 * slots * length * width * depth,
            2 * (slots * length * (width + depth) + width * depth),
        ),
    )(*lefts, *[w for w, _, _ in weights])


def chosen_kernel(near, count, info, cotangent, *refs):
    slot = pl.program_id(0)
    others, (weight, lin, stacked) = refs[:count], refs[count:]

    @pl.when(slot < near)
    def _():
        stacked[...] = cotangent[0]

    for k, other in enumerate(others):

        @pl.when((slot >= near) & (info[slot] == k))
        def _():
            stacked[...] = other[...]

    lin[...] = jnp.dot(stacked[...], weight[...], preferred_element_type=WIDE).astype(LOW)


def chosen_rows(info, cotangent, others, weight, part, parts):
    near, length, width = cotangent.shape
    slots, cols = near + len(others), weight.shape[1] // parts
    held = lambda rows, n, at: pl.BlockSpec(
        (rows, n), lambda s, info: (0, at), pipeline_mode=pl.Buffered(1)
    )
    return pl.pallas_call(
        functools.partial(chosen_kernel, near, len(others)),
        grid_spec=pltpu.PrefetchScalarGridSpec(
            num_scalar_prefetch=1,
            grid=(slots,),
            in_specs=[
                pl.BlockSpec((1, length, width), lambda s, info: (info[jnp.minimum(s, near - 1)], 0, 0))
            ]
            + [held(length, width, 0)] * len(others)
            + [held(width, cols, part)],
            out_specs=[
                pl.BlockSpec((length, cols), lambda s, info: (s, 0)),
                pl.BlockSpec((length, width), lambda s, info: (s, 0)),
            ],
        ),
        out_shape=[
            jax.ShapeDtypeStruct((slots * length, cols), LOW),
            jax.ShapeDtypeStruct((slots * length, width), LOW),
        ],
        compiler_params=pltpu.CompilerParams(vmem_limit_bytes=60 << 20),
        cost_estimate=estimate(
            2 * slots * length * width * cols, 2 * (slots * length * (2 * width + cols) + width * cols)
        ),
    )(info, cotangent, *others, weight)


def full_units_kernel(h, g, down, gate, up, hid, grad_gate, grad_up):
    gate_lin = jnp.dot(h[...], gate[...], preferred_element_type=WIDE)
    up_lin = jnp.dot(h[...], up[...], preferred_element_type=WIDE)
    grad_hidden = jnp.dot(g[...], down[...], preferred_element_type=WIDE)
    sigmoid = 1.0 / (1.0 + jnp.exp(-gate_lin))
    silu = gate_lin * sigmoid
    hid[...] = (silu * up_lin).astype(LOW)
    grad_gate[...] = (grad_hidden * up_lin * sigmoid * (1.0 + gate_lin * (1.0 - sigmoid))).astype(LOW)
    grad_up[...] = (grad_hidden * silu).astype(LOW)


def full_units(h, g, weight):
    tokens, width = h.shape
    cols = weight.shape[1] // 3
    step = math.gcd(512, tokens)
    by_row = lambda n: pl.BlockSpec((step, n), lambda i: (i, 0))
    return pl.pallas_call(
        full_units_kernel,
        grid=(tokens // step,),
        in_specs=[by_row(width)] * 2 + [part_spec(width, cols, i) for i in range(3)],
        out_specs=[by_row(cols)] * 3,
        out_shape=[jax.ShapeDtypeStruct((tokens, cols), LOW)] * 3,
        compiler_params=pltpu.CompilerParams(vmem_limit_bytes=60 << 20),
        cost_estimate=estimate(
            6 * tokens * width * cols, 2 * (2 * tokens * width + 3 * width * cols + 3 * tokens * cols)
        ),
    )(h, g, weight, weight, weight)


def first_grads_kernel(g, h, hid, gate, up, out):
    part = pl.program_id(0)
    for i, (left, right) in enumerate(((g, hid), (h, gate), (h, up))):

        @pl.when(part == i)
        def _():
            out[...] = dot_rows(left[...], right[...]).astype(LOW)


def first_grads(grad_rows, rows, hid, grad_gate, grad_up):
    tokens, width = rows.shape
    cols, tile = hid.shape[1], 256
    tiles = width // tile
    return pl.pallas_call(
        first_grads_kernel,
        grid=(3, tiles),
        in_specs=[
            pl.BlockSpec((tokens, tile), lambda p, i: (0, jnp.where(p == 0, i, tiles - 1))),
            pl.BlockSpec((tokens, tile), lambda p, i: (0, jnp.where(p == 0, 0, i))),
        ]
        + [whole_spec(tokens, cols, once=True)] * 3,
        out_specs=pl.BlockSpec((tile, cols), lambda p, i: (i, p)),
        out_shape=jax.ShapeDtypeStruct((width, 3 * cols), LOW),
        compiler_params=pltpu.CompilerParams(vmem_limit_bytes=60 << 20),
        cost_estimate=estimate(6 * tokens * width * cols, 6 * tokens * cols + 6 * width * cols),
    )(grad_rows, rows, hid, grad_gate, grad_up)


MESH_ID = pl.DeviceIdType.MESH


def meet(partners):
    barrier = pltpu.get_barrier_semaphore()
    for partner in partners:
        pl.semaphore_signal(barrier, inc=1, device_id=partner, device_id_type=MESH_ID)
    pl.semaphore_wait(barrier, len(partners))


def partners_of():
    tensor_rank, ctx_rank = lax.axis_index("tp"), lax.axis_index("ctx")
    return {"tp": tensor_rank ^ 1}, {"tp": tensor_rank ^ 2}, {"ctx": ctx_rank ^ 1}


def collect_kernel(
    slots, tiles, gate_a, up_a, gate_b, up_b, w_gate_a, w_up_a, w_gate_b, w_up_b, left, right, hid, up, total,
    down_out, up_out, parts, sent, core_in, across_in, last_in, held, send, recv, load
):
    step = pl.program_id(0)
    steps = pl.num_programs(0)
    core, far, side = partners_of()
    half = total.shape[0] // 2
    remote = remote_copy(send, recv)
    cores = [remote(sent.at[k % 2], core_in.at[k], k, core) for k in range(4)]
    across = [
        remote(parts.at[3, pl.ds(0, half)], across_in.at[0], 4, far),
        remote(parts.at[3, pl.ds(half, half)], across_in.at[1], 5, side),
    ]
    lasts = [
        remote(parts.at[1], last_in.at[0], 6, far),
        remote(parts.at[2, pl.ds(half, half)], last_in.at[1, pl.ds(half, half)], 7, side),
        remote(parts.at[2, pl.ds(0, half)], last_in.at[1, pl.ds(0, half)], 8, side),
    ]
    loading = [
        pltpu.make_async_copy(source, held.at[i], load.at[i]) for i, source in enumerate((hid, up))
    ]

    @pl.when(step == 0)
    def _():
        for copy in loading:
            copy.start()
        meet((core, far, side))

    for k in (2, 3):
        pl.when(step == 2 * k)(cores[k - 2].wait_send)

    @pl.when(step < slots)
    def _():
        part = (
            dot_cols(gate_a[...], w_gate_a[...])
            + dot_cols(up_a[...], w_up_a[...])
            + dot_cols(gate_b[...], w_gate_b[...])
            + dot_cols(up_b[...], w_up_b[...])
        )

        @pl.when(step == slots - 1)
        def _():
            total[...] = part

        for k in range(4):

            @pl.when(step == 2 * k)
            def _():
                sent[k % 2] = part.astype(LOW)
                cores[k].start()

            if k < 3:

                @pl.when(step == 2 * k + 1)
                def _():
                    cores[k].wait_recv()
                    parts[3 - k] = (part + core_in[k].astype(WIDE)).astype(LOW)

    def add(slot, rows, value):
        parts[slot, rows] = (parts[slot, rows].astype(WIDE) + value.astype(WIDE)).astype(LOW)

    low, high = pl.ds(0, half), pl.ds(half, half)

    @pl.when(step == 1)
    def _():
        for copy in across:
            copy.start()

    pl.when(step == 3)(lasts[1].start)

    @pl.when(step == 5)
    def _():
        across[1].wait_recv()
        add(1, high, across_in[1])
        lasts[0].start()
        across[0].wait_recv()
        add(2, low, across_in[0])
        lasts[2].start()

    @pl.when((step >= slots) & (step < slots + tiles))
    def _():
        pl.when(step == slots)(loading[0].wait)
        down_out[...] = dot_rows(left[...], held[0]).astype(LOW)

    @pl.when(step >= slots + tiles)
    def _():
        pl.when(step == slots + tiles)(loading[1].wait)
        up_out[...] = dot_rows(right[...], held[1]).astype(LOW)

    @pl.when(step == steps - 1)
    def _():
        cores[3].wait_recv()
        for copy in lasts:
            copy.wait_recv()
        total[...] += (
            core_in[3].astype(WIDE) + last_in[0].astype(WIDE) + last_in[1].astype(WIDE)
        )
        for copy in (*cores[2:], *across, *lasts):
            copy.wait_send()


def collect_back(first, second, weight_a, weight_b, grad_rows, rows, hid, length):
    tokens, cols_a = first[0].shape
    cols = second[0].shape[1]
    width = weight_a.shape[0]
    slots, tile = tokens // length, 256
    tiles = width // tile
    row = lambda n: pl.BlockSpec((length, n), lambda i: (jnp.maximum(slots - 1 - i, 0), 0))
    column = lambda i, start: jnp.clip(i - start, 0, tiles - 1)
    down_at, up_at = (lambda i: column(i, slots)), (lambda i: column(i, slots + tiles))
    return pl.pallas_call(
        functools.partial(collect_kernel, slots, tiles),
        grid=(slots + 2 * tiles,),
        in_specs=[row(cols_a), row(cols_a), row(cols), row(cols)]
        + [part_spec(width, cols_a, 1), part_spec(width, cols_a, 2)]
        + [part_spec(width, cols, 1), part_spec(width, cols, 2)]
        + [
            pl.BlockSpec((tokens, tile), lambda i: (0, down_at(i))),
            pl.BlockSpec((tokens, tile), lambda i: (0, up_at(i))),
            ANYWHERE,
            ANYWHERE,
        ],
        out_specs=[
            whole_spec(length, width, once=True),
            pl.BlockSpec((tile, cols), lambda i: (down_at(i), 0)),
            pl.BlockSpec((tile, cols), lambda i: (up_at(i), 0)),
        ],
        out_shape=[
            jax.ShapeDtypeStruct((length, width), WIDE),
            jax.ShapeDtypeStruct((width, cols), LOW),
            jax.ShapeDtypeStruct((width, cols), LOW),
        ],
        scratch_shapes=[
            pltpu.VMEM((4, length, width), LOW),
            pltpu.VMEM((2, length, width), LOW),
            pltpu.VMEM((4, length, width), LOW),
            pltpu.VMEM((2, length // 2, width), LOW),
            pltpu.VMEM((2, length, width), LOW),
            pltpu.VMEM((2, tokens, cols), LOW),
            pltpu.SemaphoreType.DMA((9,)),
            pltpu.SemaphoreType.DMA((9,)),
            pltpu.SemaphoreType.DMA((2,)),
        ],
        compiler_params=pltpu.CompilerParams(
            vmem_limit_bytes=63 << 20, collective_id=1, has_side_effects=True
        ),
        cost_estimate=estimate(6 * tokens * width * cols, 10 * tokens * cols),
    )(*first, *second, weight_a, weight_a, weight_b, weight_b, grad_rows, rows, hid, second[1])


def remote_copy(send, recv):
    def make(source, target, index, partner):
        return pltpu.make_async_remote_copy(
            source, target, send.at[index], recv.at[index], device_id=partner, device_id_type=MESH_ID
        )

    return make


def branch_kernel(
    slots, tiles, total, middle, own_grad, gain, hid_a, hid_b, w_a, w_b, turned, gate, grad_middle, gain_grad,
    gate_out, branch, mlp_own, mlp_far, mlp_side, own, parts, core_in, across_in, held, send, recv, load
):
    step = pl.program_id(0)
    core, far, side = partners_of()
    half = own.shape[0] // 2
    low, high = pl.ds(0, half), pl.ds(half, half)
    remote = remote_copy(send, recv)
    to_far = remote(own, branch.at[2], 0, far)
    to_near = remote(own, branch.at[1], 1, core)
    to_cross = remote(branch.at[2], branch.at[3], 2, core)
    keep = pltpu.make_async_copy(own, branch.at[0], load.at[0])
    loading = pltpu.make_async_copy(gate, held, load.at[1])
    cores = [remote(parts.at[7 - 2 * k], core_in.at[k], 3 + k, core) for k in range(4)]
    across = [
        remote(parts.at[6, low], across_in.at[0], 7, far),
        remote(parts.at[6, high], across_in.at[1], 8, side),
    ]
    stores = [
        pltpu.make_async_copy(parts.at[4], mlp_side, load.at[2]),
        pltpu.make_async_copy(parts.at[2], mlp_far, load.at[3]),
        pltpu.make_async_copy(parts.at[0], mlp_own, load.at[4]),
    ]

    @pl.when(step == 0)
    def _():
        loading.start()
        meet((core, far, side))
        values, upstream = middle[...], total[...]
        inverse = lax.rsqrt(jnp.mean(values * values, axis=-1, keepdims=True) + EPS)
        grad_in, gain_grad[...] = norm_backward(values, inverse, gain[...], upstream)
        grad_in = own_grad[...].astype(WIDE) + grad_in
        grad_middle[...] = grad_in
        own[...] = grad_in.astype(LOW)
        for copy in (to_far, to_near, keep):
            copy.start()

    @pl.when(step < slots)
    def _():
        part = dot_cols(hid_a[...], w_a[...]) + dot_cols(hid_b[...], w_b[...])
        parts[slots - 1 - step] = part.astype(LOW)

    for k in range(4):
        pl.when(step == 2 * k)(cores[k].start)

        def finish(k=k):
            slot = 6 - 2 * k
            cores[k].wait_recv()
            parts[slot] = (parts[slot].astype(WIDE) + core_in[k].astype(WIDE)).astype(LOW)
            if k == 0:
                for copy in across:
                    copy.start()
            if k == 3:
                stores[2].start()

        pl.when(step == 2 * k + 1)(finish)

    @pl.when(step >= slots)
    def _():
        pl.when(step == slots)(loading.wait)
        gate_out[...] = dot_rows(turned[...], held[...]).astype(LOW)

    @pl.when(step == slots + tiles - 2)
    def _():
        to_far.wait_recv()
        to_cross.start()

    @pl.when(step == slots + tiles - 1)
    def _():
        to_near.wait_recv()
        to_cross.wait_recv()
        for i, (slot, here) in enumerate(((4, low), (2, high))):
            across[i].wait_recv()
            parts[slot, here] = (
                parts[slot, here].astype(WIDE) + across_in[i].astype(WIDE)
            ).astype(LOW)
            stores[i].start()
        keep.wait()
        for copy in stores:
            copy.wait()
        for copy in (to_far, to_near, to_cross, *cores, *across):
            copy.wait_send()


ANYWHERE = pl.BlockSpec(memory_space=pl.ANY)


def spread_branch(total, middle, own_grad, gain, hid_a, hid_b, weight_a, weight_b, rows, grad_gate):
    length, width = total.shape
    tokens, cols = grad_gate.shape
    slots, tile = tokens // length, 256
    tiles = width // tile
    once = whole_spec(length, width, once=True)
    column = lambda i: jnp.clip(i - slots, 0, tiles - 1)
    part = jax.ShapeDtypeStruct((length, width), LOW)
    return pl.pallas_call(
        functools.partial(branch_kernel, slots, tiles),
        grid=(slots + tiles,),
        in_specs=[
            once,
            once,
            once,
            whole_spec(1, width),
            pl.BlockSpec((length, hid_a.shape[1]), lambda i: (jnp.maximum(slots - 1 - i, 0), 0)),
            pl.BlockSpec((length, cols), lambda i: (jnp.maximum(slots - 1 - i, 0), 0)),
            part_spec(width, hid_a.shape[1], 0),
            part_spec(width, cols, 0),
            pl.BlockSpec((tokens, tile), lambda i: (0, column(i))),
            ANYWHERE,
        ],
        out_specs=[
            whole_spec(length, width, once=True),
            whole_spec(1, width),
            pl.BlockSpec((tile, cols), lambda i: (column(i), 0)),
        ]
        + [ANYWHERE] * 4,
        out_shape=[
            jax.ShapeDtypeStruct((length, width), WIDE),
            jax.ShapeDtypeStruct((1, width), WIDE),
            jax.ShapeDtypeStruct((width, cols), LOW),
            jax.ShapeDtypeStruct((4, length, width), LOW),
            part,
            part,
            part,
        ],
        scratch_shapes=[
            pltpu.VMEM((length, width), LOW),
            pltpu.VMEM((slots, length, width), LOW),
            pltpu.VMEM((4, length, width), LOW),
            pltpu.VMEM((2, length // 2, width), LOW),
            pltpu.VMEM((tokens, cols), LOW),
            pltpu.SemaphoreType.DMA((9,)),
            pltpu.SemaphoreType.DMA((9,)),
            pltpu.SemaphoreType.DMA((5,)),
        ],
        compiler_params=pltpu.CompilerParams(
            vmem_limit_bytes=63 << 20, collective_id=2, has_side_effects=True
        ),
        cost_estimate=estimate(4 * tokens * width * cols, 10 * tokens * cols),
    )(total, middle, own_grad, gain, hid_a, hid_b, weight_a, weight_b, rows, grad_gate)


def line_kernel(
    slots, tiles, line, weight, own_in, grad_middle, gain, rows_one, line_all, block, share,
    gain_grad, attn_out, bias_out, home, parts, core_in, far_in, total, send, recv, load
):
    step = pl.program_id(0)
    core, far, _ = partners_of()
    tensor_rank, group = lax.axis_index("tp"), lax.axis_index("fsdp")
    shift = (tensor_rank % 2) * 2 + tensor_rank // 2
    target = {"fsdp": (group + slots - shift) % slots}
    source = {"fsdp": (group + shift) % slots}
    stays = shift == 0
    remote = remote_copy(send, recv)
    cores = [remote(parts.at[3 - 2 * k], core_in.at[k], k, core) for k in range(2)]
    to_far = remote(parts.at[2], far_in, 2, far)
    leave = remote(block, home, 3, target)
    keep = pltpu.make_async_copy(block, home, load)

    @pl.when(step == 0)
    def _():
        barrier = pltpu.get_barrier_semaphore()
        for partner in (core, far):
            pl.semaphore_signal(barrier, inc=1, device_id=partner, device_id_type=MESH_ID)

        @pl.when(stays)
        def _():
            pl.semaphore_wait(barrier, 2)
            keep.start()

        @pl.when(jnp.logical_not(stays))
        def _():
            for partner in (target, source):
                pl.semaphore_signal(barrier, inc=1, device_id=partner, device_id_type=MESH_ID)
            pl.semaphore_wait(barrier, 4)
            leave.start()

    @pl.when(step < slots)
    def _():
        part = dot_cols(line[...], weight[...])
        parts[slots - 1 - step] = part.astype(LOW)

        @pl.when(step == slots - 1)
        def _():
            total[...] = part

    for k in range(2):
        pl.when(step == 2 * k)(cores[k].start)

    @pl.when(step == 1)
    def _():
        cores[0].wait_recv()
        parts[2] = (parts[2].astype(WIDE) + core_in[0].astype(WIDE)).astype(LOW)
        to_far.start()

    @pl.when(step == slots - 1)
    def _():
        bias_out[...] = jnp.sum(line_all[...].astype(WIDE), axis=0, keepdims=True)

    @pl.when(step >= slots)
    def _():
        attn_out[...] = dot_rows(rows_one[...], line_all[...]).astype(LOW)

    @pl.when(step == slots + tiles - 1)
    def _():
        cores[1].wait_recv()
        to_far.wait_recv()
        upstream = total[...] + core_in[1].astype(WIDE) + far_in[...].astype(WIDE)
        values = own_in[...].astype(WIDE)
        inverse = lax.rsqrt(jnp.mean(values * values, axis=-1, keepdims=True) + EPS)
        grad_in, gain_grad[...] = norm_backward(values, inverse, gain[...], upstream)
        share[...] = (grad_middle[...] + grad_in).astype(LOW)
        for copy in (*cores, to_far):
            copy.wait_send()
        pl.when(stays)(keep.wait)

        @pl.when(jnp.logical_not(stays))
        def _():
            leave.wait_recv()
            leave.wait_send()


def finish_rows(line, weight, own_in, grad_middle, gain, rows_one, block):
    length, width = own_in.shape
    near_tokens, line_cols = line.shape
    slots, tile = near_tokens // length, 256
    tiles = width // tile
    once = whole_spec(length, width, once=True)
    column = lambda i: jnp.clip(i - slots, 0, tiles - 1)
    by_column = lambda n: pl.BlockSpec((n, tile), lambda i: (0, column(i)))
    attn_cols = line_cols
    return pl.pallas_call(
        functools.partial(line_kernel, slots, tiles),
        grid=(slots + tiles,),
        in_specs=[
            pl.BlockSpec((length, line_cols), lambda i: (jnp.maximum(slots - 1 - i, 0), 0)),
            whole_spec(width, line_cols, once=True),
            once,
            once,
            whole_spec(1, width),
            by_column(near_tokens),
            whole_spec(near_tokens, line_cols, once=True),
            ANYWHERE,
        ],
        out_specs=[
            whole_spec(length, width),
            whole_spec(1, width),
            pl.BlockSpec((tile, attn_cols), lambda i: (column(i), 0)),
            whole_spec(1, line_cols),
            ANYWHERE,
        ],
        out_shape=[
            jax.ShapeDtypeStruct((length, width), LOW),
            jax.ShapeDtypeStruct((1, width), WIDE),
            jax.ShapeDtypeStruct((width, attn_cols), LOW),
            jax.ShapeDtypeStruct((1, line_cols), WIDE),
            jax.ShapeDtypeStruct((length, width), LOW),
        ],
        scratch_shapes=[
            pltpu.VMEM((slots, length, width), LOW),
            pltpu.VMEM((2, length, width), LOW),
            pltpu.VMEM((length, width), LOW),
            pltpu.VMEM((length, width), WIDE),
            pltpu.SemaphoreType.DMA((4,)),
            pltpu.SemaphoreType.DMA((4,)),
            pltpu.SemaphoreType.DMA,
        ],
        compiler_params=pltpu.CompilerParams(
            vmem_limit_bytes=63 << 20, collective_id=3, has_side_effects=True
        ),
        cost_estimate=estimate(2 * near_tokens * width * attn_cols, 10 * near_tokens * width),
    )(line, weight, own_in, grad_middle, gain, rows_one, line, block)


def place_kernel(count, info, *refs):
    out = refs[count]
    for r in range(count):

        @pl.when(pl.program_id(0) == r)
        def _():
            out[0] = refs[r][...]


def place_rows(rows, order):
    length, width = rows[0].shape
    count = len(rows)
    held = pl.BlockSpec((length, width), lambda s, info: (0, 0), pipeline_mode=pl.Buffered(1))
    return pl.pallas_call(
        functools.partial(place_kernel, count),
        grid_spec=pltpu.PrefetchScalarGridSpec(
            num_scalar_prefetch=1,
            grid=(count,),
            in_specs=[held] * count,
            out_specs=pl.BlockSpec((1, length, width), lambda s, info: (info[s], 0, 0)),
        ),
        out_shape=jax.ShapeDtypeStruct((count, length, width), LOW),
        compiler_params=pltpu.CompilerParams(vmem_limit_bytes=32 << 20),
        cost_estimate=estimate(0, 4 * count * length * width),
    )(order, *rows)


def turn(values, cosine, sine_signed):
    return values * cosine + pltpu.roll(values, values.shape[-1] // 2, 1) * sine_signed


def turn_back(values, cosine, sine_signed):
    return values * cosine - pltpu.roll(values, values.shape[-1] // 2, 1) * sine_signed


def project_kernel(
    heads, head_dim, x0, x1, x2, x3, gains, weight, bias, cosine, sine, h_out, q_out, k_out, v_out, gain
):
    slot = pl.program_id(0)

    @pl.when(slot == 0)
    def _():
        gain[...] = gains[...].astype(WIDE).T[:8]


    def run(x_ref):
        x = x_ref[...].astype(WIDE)
        scale_inv = lax.rsqrt(jnp.mean(x * x, axis=-1, keepdims=True) + EPS)
        normed = (x * scale_inv * gain[0:1]).astype(LOW)
        h_out[0] = normed
        lin = jnp.dot(normed, weight[...], preferred_element_type=WIDE) + bias[...]
        cos, sin = cosine[0], sine[0]
        for h in range(heads + 1):
            part = turn(lin[:, h * head_dim : (h + 1) * head_dim], cos, sin).astype(LOW)
            if h < heads:
                q_out[0, :, h * head_dim : (h + 1) * head_dim] = part
            else:
                k_out[0] = part
        v_out[0] = lin[:, (heads + 1) * head_dim :].astype(LOW)

    for r, x_ref in enumerate((x0, x1, x2, x3)):
        pl.when(slot == r)(functools.partial(run, x_ref))


def project(rows, held, bias, cosine, sine, heads, head_dim):
    length, width = rows[0].shape
    count = len(rows)
    cols = (heads + 2) * head_dim
    whole = whole_spec
    by_slot = lambda *shape: pl.BlockSpec((1, *shape), lambda s: (s,) + (0,) * len(shape))
    return pl.pallas_call(
        functools.partial(project_kernel, heads, head_dim),
        grid=(count,),
        in_specs=[whole(length, width)] * count
        + [part_spec(width, 128, cols // 128), part_spec(width, cols, 0), whole(1, cols)]
        + [by_slot(length, head_dim)] * 2,
        out_specs=[
            by_slot(length, width),
            by_slot(length, heads * head_dim),
            by_slot(length, head_dim),
            by_slot(length, head_dim),
        ],
        out_shape=[
            jax.ShapeDtypeStruct((count, length, width), LOW),
            jax.ShapeDtypeStruct((count, length, heads * head_dim), LOW),
            jax.ShapeDtypeStruct((count, length, head_dim), LOW),
            jax.ShapeDtypeStruct((count, length, head_dim), LOW),
        ],
        scratch_shapes=[pltpu.VMEM((8, width), WIDE)],
        compiler_params=pltpu.CompilerParams(vmem_limit_bytes=56 << 20),
        cost_estimate=pl.CostEstimate(
            flops=2 * count * length * width * cols,
            bytes_accessed=count * length * (2 * width + cols) * 2 + width * cols * 2,
            transcendentals=0,
        ),
    )(*rows, held, held, bias, cosine, sine)


def row_blocks(length):
    return [(i, min(256, length)) for i in range(0, length, min(256, length))]


def key_biases(length, offset, start, rows, past, keys):
    past_pos = lax.broadcasted_iota(jnp.int32, (1, past), 1)
    past_bias = jnp.where((past_pos < offset) & (past_pos < length), 0.0, NEG_FILL)
    query_pos = offset + start + lax.broadcasted_iota(jnp.int32, (rows, keys), 0)
    own_pos = offset + lax.broadcasted_iota(jnp.int32, (rows, keys), 1)
    own_bias = jnp.where((own_pos <= query_pos) & (own_pos < length), 0.0, NEG_FILL)
    return past_bias, own_bias


def dot_cols(left, right):
    return lax.dot_general(left, right, (((1,), (1,)), ((), ())), preferred_element_type=WIDE)


def dot_rows(left, right):
    return lax.dot_general(left, right, (((0,), (0,)), ((), ())), preferred_element_type=WIDE)


def attend_kernel(
    heads, head_dim, scale, first, total_slots, info, q, k_past, v_past, k_own, v_own, weight, out, lse, *parts
):
    length, offset = info[first + pl.program_id(0)], info[total_slots]
    past = k_past.shape[1]
    for start, rows in row_blocks(q.shape[1]):
        keys = start + rows
        past_bias, own_bias = key_biases(length, offset, start, rows, past, keys)
        here = slice(start, start + rows)
        for h in range(heads):
            cols = slice(h * head_dim, (h + 1) * head_dim)
            query = q[0, here, cols]
            s_past = dot_cols(query, k_past[0]) * scale + past_bias
            s_own = dot_cols(query, k_own[0, :keys]) * scale + own_bias
            top = jnp.maximum(
                jnp.max(s_past, axis=1, keepdims=True), jnp.max(s_own, axis=1, keepdims=True)
            )
            e_past, e_own = jnp.exp(s_past - top), jnp.exp(s_own - top)
            total = jnp.sum(e_past, axis=1, keepdims=True) + jnp.sum(e_own, axis=1, keepdims=True)
            inverse = 1.0 / total
            mixed = jnp.dot(
                (e_past * inverse).astype(LOW), v_past[0], preferred_element_type=WIDE
            ) + jnp.dot((e_own * inverse).astype(LOW), v_own[0, :keys], preferred_element_type=WIDE)
            out[0, here, cols] = mixed.astype(LOW)
            lse[0, here, h : h + 1] = top + jnp.log(total)
        rows_out = dot_cols(out[0, here], weight[...]).astype(LOW)
        for i, part in enumerate(parts):

            @pl.when(pl.program_id(0) == i)
            def _():
                part[here] = rows_out


def attend_forward(info, q, k_past, v_past, k_own, v_own, weight, heads, head_dim, scale, first, count):
    _, length, width = q.shape
    past = k_past.shape[1]
    by_slot = lambda *shape: pl.BlockSpec((1, *shape), lambda s, info: (first + s,) + (0,) * len(shape))
    out_slot = lambda *shape: pl.BlockSpec((1, *shape), lambda s, info: (s,) + (0,) * len(shape))
    keys = count * length * (past + length) * heads
    return pl.pallas_call(
        functools.partial(attend_kernel, heads, head_dim, scale, first, q.shape[0]),
        grid_spec=pltpu.PrefetchScalarGridSpec(
            num_scalar_prefetch=1,
            grid=(count,),
            in_specs=[
                by_slot(length, width),
                by_slot(past, head_dim),
                by_slot(past, head_dim),
                by_slot(length, head_dim),
                by_slot(length, head_dim),
                whole_spec(*weight.shape, once=True),
            ],
            out_specs=[out_slot(length, width), out_slot(length, 128)]
            + [whole_spec(length, weight.shape[0])] * count,
        ),
        out_shape=[
            jax.ShapeDtypeStruct((count, length, width), LOW),
            jax.ShapeDtypeStruct((count, length, 128), WIDE),
        ]
        + [jax.ShapeDtypeStruct((length, weight.shape[0]), LOW)] * count,
        compiler_params=pltpu.CompilerParams(vmem_limit_bytes=56 << 20),
        cost_estimate=estimate(4 * keys * head_dim, 4 * count * length * width, keys),
    )(info, q, k_past, v_past, k_own, v_own, weight)


def attend_back_rows(
    heads, head_dim, scale, length, offset, q, k_past, v_past, k_own, v_own, grad, lse, cosine, sine, put,
    dk_past, dk_own, dv_past, dv_own
):
    past = k_past.shape[1]
    for start, rows in row_blocks(q.shape[1]):
        keys = start + rows
        past_bias, own_bias = key_biases(length, offset, start, rows, past, keys)
        here = slice(start, start + rows)
        cos, sin = cosine[0, here], sine[0, here]
        for h in range(heads):
            cols = slice(h * head_dim, (h + 1) * head_dim)
            query, upstream = q[0, here, cols], grad[0, here, cols]
            log_total = lse[0, here, h : h + 1]
            p_past = jnp.exp(dot_cols(query, k_past[0]) * scale + past_bias - log_total)
            p_own = jnp.exp(dot_cols(query, k_own[0, :keys]) * scale + own_bias - log_total)
            g_past = dot_cols(upstream, v_past[0])
            g_own = dot_cols(upstream, v_own[0, :keys])
            row_dot = jnp.sum(p_past * g_past, axis=1, keepdims=True) + jnp.sum(
                p_own * g_own, axis=1, keepdims=True
            )
            s_past = (p_past * (g_past - row_dot)).astype(LOW)
            s_own = (p_own * (g_own - row_dot)).astype(LOW)
            dq = (
                jnp.dot(s_past, k_past[0], preferred_element_type=WIDE)
                + jnp.dot(s_own, k_own[0, :keys], preferred_element_type=WIDE)
            ) * scale
            put(here, cols, turn_back(dq, cos, sin).astype(LOW))
            dk_past[...] += dot_rows(s_past, query)
            dk_own[:keys] += dot_rows(s_own, query)
            dv_past[...] += dot_rows(p_past.astype(LOW), upstream)
            dv_own[:keys] += dot_rows(p_own.astype(LOW), upstream)


def attend_back_kernel(
    heads,
    head_dim,
    scale,
    info,
    q,
    k_past,
    v_past,
    k_own,
    v_own,
    grad,
    lse,
    cosine,
    sine,
    dq_out,
    mine_past,
    mine_own,
    other_past,
    other_own,
    dk_past,
    dk_own,
    dv_past,
    dv_own,
):
    slot = pl.program_id(0)
    length, offset = info[slot], info[pl.num_programs(0)]
    parity = info[pl.num_programs(0) + 1]
    for total in (dk_past, dk_own, dv_past, dv_own):
        total[...] = jnp.zeros_like(total)
    attend_back_rows(
        heads, head_dim, scale, length, offset, q, k_past, v_past, k_own, v_own, grad, lse, cosine, sine,
        lambda here, cols, value: dq_out.__setitem__((0, here, cols), value),
        dk_past, dk_own, dv_past, dv_own,
    )

    @pl.when(parity == 0)
    def _():
        mine_past[0] = dk_past[...] * scale
        mine_own[0] = dk_own[...] * scale
        other_past[0] = dv_past[...]
        other_own[0] = dv_own[...]

    @pl.when(parity != 0)
    def _():
        mine_past[0] = dv_past[...]
        mine_own[0] = dv_own[...]
        other_past[0] = dk_past[...] * scale
        other_own[0] = dk_own[...] * scale


def attend_backward(
    info, q, k_past, v_past, k_own, v_own, grad, lse, cosine, sine, heads, head_dim, scale
):
    count, length, width = q.shape
    past = k_past.shape[1]
    by_slot = lambda *shape: pl.BlockSpec((1, *shape), lambda s, info: (s,) + (0,) * len(shape))
    keys = count * length * (past + length) * heads
    return pl.pallas_call(
        functools.partial(attend_back_kernel, heads, head_dim, scale),
        grid_spec=pltpu.PrefetchScalarGridSpec(
            num_scalar_prefetch=1,
            grid=(count,),
            in_specs=[
                by_slot(length, width),
                by_slot(past, head_dim),
                by_slot(past, head_dim),
                by_slot(length, head_dim),
                by_slot(length, head_dim),
                by_slot(length, width),
                by_slot(length, 128),
                by_slot(length, head_dim),
                by_slot(length, head_dim),
            ],
            out_specs=[
                by_slot(length, width),
                by_slot(past, head_dim),
                by_slot(length, head_dim),
                by_slot(past, head_dim),
                by_slot(length, head_dim),
            ],
            scratch_shapes=[
                pltpu.VMEM((past, head_dim), WIDE),
                pltpu.VMEM((length, head_dim), WIDE),
                pltpu.VMEM((past, head_dim), WIDE),
                pltpu.VMEM((length, head_dim), WIDE),
            ],
        ),
        out_shape=[
            jax.ShapeDtypeStruct((count, length, width), LOW),
            jax.ShapeDtypeStruct((count, past, head_dim), WIDE),
            jax.ShapeDtypeStruct((count, length, head_dim), WIDE),
            jax.ShapeDtypeStruct((count, past, head_dim), WIDE),
            jax.ShapeDtypeStruct((count, length, head_dim), WIDE),
        ],
        compiler_params=pltpu.CompilerParams(vmem_limit_bytes=56 << 20),
        cost_estimate=estimate(10 * keys * head_dim, 8 * count * length * width, keys),
    )(info, q, k_past, v_past, k_own, v_own, grad, lse, cosine, sine)


def exchange_kernel(
    heads, head_dim, scale, slots, tiles, info, q, k_past, v_past, k_own, v_own, grad, lse, cosine, sine,
    cosine_all, sine_all, branch, mixed, mlp_far, mlp_side, mlp_own, middle, line, out_grad, block, mine_past,
    mine_own, other_past, other_own, got_past, got_own, side_out, side_in, dk_past, dk_own, dv_past, dv_own,
    own_rows, last_in, send, recv, load
):
    step = pl.program_id(0)
    tensor_rank = lax.axis_index("tp")
    core, far, side = partners_of()
    parity = lax.rem(tensor_rank, 2)
    offset = lax.axis_index("ctx") * q.shape[1]
    remote = remote_copy(send, recv)
    pasts = [remote(other_past.at[r], got_past.at[r ^ 1], r, core) for r in range(slots)]
    owns = [remote(other_own.at[r], got_own.at[r ^ 1], slots + r, core) for r in range(slots)]
    sides = [remote(side_out.at[r], side_in.at[r], 2 * slots + r, side) for r in range(slots)]
    lasts = [
        remote(mlp_far, last_in.at[0], 3 * slots, far),
        remote(mlp_side, last_in.at[1], 3 * slots + 1, side),
    ]
    loading = pltpu.make_async_copy(mlp_own, own_rows, load)

    @pl.when(step == 0)
    def _():
        loading.start()
        meet((core, far, side))
        for copy in lasts:
            copy.start()

    @pl.when(step < slots)
    def _():
        length = info[jnp.minimum(step, slots - 1)]
        for total in (dk_past, dk_own, dv_past, dv_own):
            total[...] = jnp.zeros_like(total)
        attend_back_rows(
            heads, head_dim, scale, length, offset, q, k_past, v_past, k_own, v_own, grad, lse, cosine,
            sine, lambda here, cols, value: line.__setitem__((step, here, cols), value),
            dk_past, dk_own, dv_past, dv_own,
        )

        @pl.when(parity == 0)
        def _():
            mine_past[step] = dk_past[...] * scale
            mine_own[step] = dk_own[...] * scale
            other_past[step] = dv_past[...]
            other_own[step] = dv_own[...]

        @pl.when(parity != 0)
        def _():
            mine_past[step] = dv_past[...]
            mine_own[step] = dv_own[...]
            other_past[step] = dk_past[...] * scale
            other_own[step] = dk_own[...] * scale

    for r in range(slots):

        def start(r=r):
            pasts[r].start()
            owns[r].start()

        pl.when(step == r)(start)

    for pair in range(0, slots, 2):

        def merge(pair=pair):
            for r in (pair, pair + 1):
                pasts[r ^ 1].wait_recv()
                side_out[r] = (mine_past[r] + got_past[r]).astype(LOW)
                sides[r].start()

        pl.when(step == pair + 1)(merge)

    @pl.when(step >= slots)
    def _():
        out_grad[...] = dot_rows(branch[...], mixed[...]).astype(LOW)

    @pl.when(step == slots + tiles - 1)
    def _():
        for r in range(slots):
            owns[r ^ 1].wait_recv()
            sides[r].wait_recv()
            total = mine_own[r] + got_own[r] + side_in[r].astype(WIDE)
            back = turn_back(total, cosine_all[r], sine_all[r])
            line[r, :, heads * head_dim :] = jnp.where(parity == 0, back, total).astype(LOW)
        loading.wait()
        for copy in lasts:
            copy.wait_recv()
        block[...] = (
            middle[...] + own_rows[...].astype(WIDE) + last_in[0].astype(WIDE) + last_in[1].astype(WIDE)
        ).astype(LOW)
        for copy in (*pasts, *owns, *sides, *lasts):
            copy.wait_send()


def attend_exchange(
    info, q, k_past, v_past, k_own, v_own, grad, lse, cosine, sine, heads, head_dim, scale, branch, mixed, mlp, middle
):
    count, length, width = q.shape
    past = k_past.shape[1]
    tokens, model_width = branch.shape
    tile = 256
    tiles = model_width // tile
    slot = lambda i: jnp.minimum(i, count - 1)
    by_slot = lambda *shape: pl.BlockSpec((1, *shape), lambda i, info: (slot(i),) + (0,) * len(shape))
    column = lambda i: jnp.clip(i - count, 0, tiles - 1)
    held = lambda *shape: pl.BlockSpec(
        shape, lambda i, info: (0,) * len(shape), pipeline_mode=pl.Buffered(1)
    )
    line_cols = width + head_dim
    return pl.pallas_call(
        functools.partial(exchange_kernel, heads, head_dim, scale, count, tiles),
        grid_spec=pltpu.PrefetchScalarGridSpec(
            num_scalar_prefetch=1,
            grid=(count + tiles,),
            in_specs=[
                by_slot(length, width),
                by_slot(past, head_dim),
                by_slot(past, head_dim),
                by_slot(length, head_dim),
                by_slot(length, head_dim),
                by_slot(length, width),
                by_slot(length, 128),
                by_slot(length, head_dim),
                by_slot(length, head_dim),
                held(count, length, head_dim),
                held(count, length, head_dim),
                pl.BlockSpec((tokens, tile), lambda i, info: (0, column(i))),
                held(*mixed.shape),
            ]
            + [ANYWHERE] * 3
            + [held(length, model_width)],
            out_specs=[
                held(count, length, line_cols),
                pl.BlockSpec((tile, width), lambda i, info: (column(i), 0)),
                held(length, model_width),
            ],
            scratch_shapes=[pltpu.VMEM((count, length, head_dim), WIDE)] * 6
            + [pltpu.VMEM((count, length, head_dim), LOW)] * 2
            + [pltpu.VMEM((length, head_dim), WIDE)] * 4
            + [
                pltpu.VMEM((length, model_width), LOW),
                pltpu.VMEM((2, length, model_width), LOW),
                pltpu.SemaphoreType.DMA((3 * count + 2,)),
                pltpu.SemaphoreType.DMA((3 * count + 2,)),
                pltpu.SemaphoreType.DMA,
            ],
        ),
        out_shape=[
            jax.ShapeDtypeStruct((count, length, line_cols), LOW),
            jax.ShapeDtypeStruct((model_width, width), LOW),
            jax.ShapeDtypeStruct((length, model_width), LOW),
        ],
        compiler_params=pltpu.CompilerParams(
            vmem_limit_bytes=63 << 20, collective_id=4, has_side_effects=True
        ),
        cost_estimate=estimate(2 * tokens * model_width * width, 10 * tokens * width),
    )(info, q, k_past, v_past, k_own, v_own, grad, lse, cosine, sine, cosine, sine, branch, mixed, *mlp, middle)


def local(
    hidden_in,
    cotangent,
    seq_lengths,
    positions,
    permutation,
    query_weight,
    keyval_weight,
    output_weight,
    norm_gains,
    bias_query,
    bias_keyval,
    gate_weight,
    up_weight,
    down_weight,
):
    group_rank = lax.axis_index("fsdp")
    ctx_rank = lax.axis_index("ctx")
    tensor_rank = lax.axis_index("tp")
    fsdp_count = lax.axis_size("fsdp")
    ctx_count = lax.axis_size("ctx")
    tensor_count = lax.axis_size("tp")
    seq_grp, local_len, model_width = hidden_in.shape
    heads, head_dim = bias_query.shape
    keyval_heads = bias_keyval.shape[0] // 2
    assert seq_grp == tensor_count == fsdp_count == len(DEAL_SHIFT)
    token_count = seq_grp * local_len
    scale = 1.0 / math.sqrt(head_dim)
    offset = ctx_rank * local_len
    head_pair = tensor_rank // (tensor_count // keyval_heads)
    parity = tensor_rank % 2
    shifts = jnp.array(DEAL_SHIFT, jnp.int32)

    table = permutation.reshape(fsdp_count, seq_grp)
    far_group = lax.rem(group_rank + shifts[tensor_rank], fsdp_count)
    far_row = lax.dynamic_index_in_dim(table, far_group, 0, keepdims=False)
    leaving = jnp.sum(jnp.where(far_row // seq_grp == group_rank, far_row - group_rank * seq_grp, 0))
    own_row = lax.dynamic_index_in_dim(table, group_rank, 0, keepdims=False)
    slot_now, seq_now, home_now = [], [], []
    for r in range(seq_grp):
        shift = shifts[tensor_rank ^ r]
        source = lax.rem(group_rank - shift + fsdp_count, fsdp_count)
        hit = own_row // seq_grp == source
        slot_now.append(jnp.sum(jnp.where(hit, jnp.arange(seq_grp), 0)))
        seq_now.append(jnp.sum(jnp.where(hit, own_row, 0)))
        target = lax.rem(group_rank + shift, fsdp_count)
        target_row = lax.dynamic_index_in_dim(table, target, 0, keepdims=False)
        home_now.append(
            jnp.sum(jnp.where(target_row // seq_grp == group_rank, target_row - group_rank * seq_grp, 0))
        )
    there = [
        (f * tensor_count + t, (f + DEAL_SHIFT[t]) % fsdp_count * tensor_count + t)
        for f in range(fsdp_count)
        for t in range(tensor_count)
    ]
    back = [(target, source) for source, target in there]

    split = units_split()
    head_width = 2 * head_dim
    query_cols = heads * head_dim
    near_cols = query_cols + head_width + 128

    outgoing = lax.dynamic_index_in_dim(hidden_in, leaving, 0, keepdims=False)
    own_in = lax.ppermute(outgoing, ("fsdp", "tp"), there)
    small = jnp.concatenate(
        [
            query_weight,
            lax.dynamic_slice_in_dim(keyval_weight, head_pair * head_width, head_width, axis=1),
            jnp.pad(norm_gains.T, ((0, 0), (0, 128 - norm_gains.shape[0]))),
            output_weight.T,
        ],
        axis=1,
    )
    lengths_now = jnp.stack([seq_lengths[s] for s in seq_now])
    info = jnp.concatenate([lengths_now, jnp.stack([offset, parity])]).astype(jnp.int32)
    positions_now = jnp.stack(
        [lax.dynamic_index_in_dim(positions, s, 0, keepdims=False) for s in seq_now]
    )
    lane = jnp.arange(head_dim)
    frequency = 1.0 / ROPE_BASE ** ((lane % (head_dim // 2)).astype(WIDE) * 2.0 / head_dim)
    angles = positions_now.astype(WIDE)[..., None] * frequency
    cosine = jnp.cos(angles)
    sine = jnp.sin(angles) * jnp.where(lane < head_dim // 2, -1.0, 1.0)
    pick_info = jnp.stack(slot_now + [s ^ tensor_rank for s in slot_now]).astype(jnp.int32)
    units = gate_weight.shape[1]
    units_pad = -(-units // 256) * 256
    widen = lambda w: jnp.pad(w, ((0, 0), (0, units_pad - units)))
    shards = [widen(w) for w in (down_weight.T, gate_weight, up_weight)]
    if split:
        half_units = units_pad // 2
        cut = lambda w, c: lax.dynamic_slice_in_dim(w, c * half_units, half_units, axis=1)

        def in_order(own, other):
            return jnp.stack(
                [jnp.where(ctx_rank == 0, own, other), jnp.where(ctx_rank == 0, other, own)]
            )

        def all_rows(both, *earlier):
            full = lax.all_gather(after(both, *earlier), "fsdp", axis=0, tiled=False)
            return full.reshape(-1, both.shape[-1])

        first_units = half_units // 2 // 256 * 256
        first_cols = 3 * first_units

        def in_parts(c):
            halves = [cut(w, c) for w in shards]
            return jnp.concatenate(
                [w[:, :first_units] for w in halves] + [w[:, first_units:] for w in halves], axis=1
            )

        leaving_units, own_units = in_parts(1 - ctx_rank), in_parts(ctx_rank)
        slot_pick = lax.dynamic_index_in_dim(cotangent, tensor_rank, 0, keepdims=False)
        small = after(small, outgoing, cosine, sine, info, pick_info, leaving_units, own_units, slot_pick)
        small_both = in_order(small, from_partner(small, "ctx", 1))
        arriving_units = from_partner(after(leaving_units, small_both), "ctx", 1)
        other_own = from_partner(after(slot_pick, arriving_units), "ctx", 1)
        both_a = in_order(own_units[:, :first_cols], arriving_units[:, :first_cols])
        both_b = in_order(own_units[:, first_cols:], arriving_units[:, first_cols:])
    else:
        all_rows = lambda shard, *earlier: lax.all_gather(
            shard, ("fsdp", "ctx"), axis=0, tiled=True
        )
        small_both, unit_both, half_units = small, jnp.concatenate(shards, axis=1), units_pad
    far_in = from_partner(own_in, "tp", 2)
    near_in = from_partner(own_in, "tp", 1)
    cross_in = from_partner(far_in, "tp", 1)
    grad_slots = [lax.dynamic_index_in_dim(cotangent, s, 0, keepdims=False) for s in slot_now]

    near_full = all_rows(small_both, own_in)
    if split:
        units_a = all_rows(both_a, cross_in)
        units_b = all_rows(both_b, cross_in)
    else:
        down_full = all_rows(unit_both[..., :half_units], cross_in)
        gate_up_full = all_rows(unit_both[..., half_units:], cross_in)
    project_full = near_full[:, : query_cols + head_width]
    output_full = near_full[:, near_cols:]
    bias_head = lax.dynamic_slice_in_dim(bias_keyval, head_pair * 2, 2, axis=0)
    bias_row = jnp.concatenate([bias_query.reshape(1, -1), bias_head.reshape(1, -1)], axis=1).astype(WIDE)
    normed_one, query_rot, key_own, value_own = project(
        (own_in, near_in, far_in, cross_in),
        near_full,
        bias_row,
        after(cosine, other_own, both_a, both_b, info, pick_info) if split else cosine,
        sine,
        heads,
        head_dim,
    )
    gains_now = near_full[:, query_cols + head_width : near_cols][:, :2].astype(WIDE).T
    if split:
        key_past, value_past = lax.ppermute((key_own, value_own), "ctx", [(0, 1)])
        other_far = from_partner(other_own, "tp", 2)
        other_near = from_partner(after(other_own, key_past), "tp", 1)
        other_cross = from_partner(after(other_far, key_past), "tp", 1)
        other_rows = (other_own, other_near, other_far, other_cross)
        key_past = after(key_past, other_far)
    else:
        key_past = lax.all_gather(key_own, "ctx", axis=1, tiled=True)
        value_past = lax.all_gather(value_own, "ctx", axis=1, tiled=True)
    attend = lambda first, *held: attend_forward(
        info, query_rot, *held, key_own, value_own, output_full, heads, head_dim, scale, first, 2
    )
    in_share = own_in.astype(WIDE)

    mixed_far, lse_far, *attn_far = attend(2, key_past, value_past)
    attn_wide = collect_far(attn_far[0], attn_far[1])
    attn_got = from_partner(attn_wide, "tp", 2)
    mixed_near, lse_near, *attn_near = attend(0, after(key_past, attn_wide), value_past)
    attn_core = from_partner(attn_near[1], "tp", 1)
    middle_share = (
        in_share
        + attn_near[0].astype(WIDE)
        + attn_core.astype(WIDE)
        + attn_got.astype(WIDE)
    )
    inv_two = lax.rsqrt(jnp.mean(middle_share * middle_share, axis=-1, keepdims=True) + EPS)
    normed_share = (middle_share * inv_two * gains_now[1]).astype(LOW)
    half_len = local_len // 2

    if split:
        grad_hidden, grad_rows = chosen_rows(
            pick_info,
            after(cotangent, normed_share),
            other_rows,
            units_a,
            0,
            3,
        )
    else:
        grad_hidden, grad_rows = stack_rows([(g,) for g in grad_slots], down_full, 0, 1)

    def spread_all(own):
        far = from_partner(own, "tp", 2)
        near = from_partner(own, "tp", 1)
        if not split:
            return (own, near, far, from_partner(far, "tp", 1))
        side = from_partner(own, "ctx", 1)
        held = after(far, grad_hidden), after(side, grad_hidden)
        across = from_partner(held[0][:half_len], "ctx", 1), from_partner(held[1][half_len:], "tp", 2)
        cores = [from_partner(v, "tp", 1) for v in (*held, *across)]
        return (own, near, far, cores[0], side, cores[1], *across, *cores[2:])

    def in_slots(rows):
        if not split:
            return [(row,) for row in rows]
        return [(row,) for row in rows[:6]] + [rows[6:8], rows[8:]]

    normed_slots = in_slots(spread_all(normed_share))
    if split:
        gate_lin, normed_two = stack_rows(normed_slots, units_a, 1, 3)
        hidden_a, gate_a, up_a = hidden_units(normed_two, units_a, 2, 3, gate_lin, grad_hidden)
        grad_a = first_grads(grad_rows, normed_two, hidden_a, gate_a, up_a)
        hidden_b, gate_b, up_b = full_units(after(normed_two, grad_a), grad_rows, units_b)
    else:
        gate_lin, normed_two = stack_rows(normed_slots, gate_up_full, 0, 2)
        hidden_act, grad_gate, grad_up = hidden_units(
            normed_two, gate_up_full, 1, 2, gate_lin, grad_hidden
        )

    def collect_all(lefts, weights, *earlier):
        lefts = list(lefts)
        lefts[0] = after(lefts[0], *earlier)
        last = back_rows(lefts, weights, 2, 2, local_len)
        got = [from_partner(collect_far(last[0], last[1]), "tp", 2)]
        first = back_rows(lefts, weights, 0, 2, local_len)
        got.append(from_partner(first[1], "tp", 1))

        def finish():
            return sum((v.astype(WIDE) for v in got), first[0].astype(WIDE))

        return first[0], finish

    if split:
        grad_two_share, down_b, up_grad_b = collect_back(
            (gate_a, up_a),
            (gate_b, up_b),
            units_a,
            units_b,
            grad_rows,
            normed_two,
            hidden_b,
            local_len,
        )
        grad_middle, gain_two, gate_grad_b, grad_branch, *mlp = spread_branch(
            grad_two_share,
            middle_share,
            grad_slots[0],
            gains_now[1:2],
            hidden_a,
            hidden_b,
            units_a,
            units_b,
            normed_two,
            gate_b,
        )
        mlp_own, mlp_far, mlp_side = mlp
        grad_branch = grad_branch.reshape(token_count, model_width)
    else:
        first_back, finish_back = collect_all(
            (grad_gate, grad_up), ((gate_up_full, 0, 2), (gate_up_full, 1, 2))
        )
        down_grad = contract_rows(after(grad_rows, first_back), hidden_act, LOW)
        gate_grad = contract_rows(normed_two, after(grad_gate, down_grad), LOW)
        grad_two_share = finish_back()
        grad_norm_two, gain_two = norm_backward(
            middle_share, inv_two, gains_now[1], grad_two_share
        )
        grad_middle = grad_slots[0].astype(WIDE) + grad_norm_two
        branch_own = grad_middle.astype(LOW)
        branch_far = from_partner(branch_own, "tp", 2)
        branch_near = from_partner(branch_own, "tp", 1)
        branch_cross = from_partner(branch_far, "tp", 1)
        grad_branch = jnp.concatenate([branch_own, branch_near, branch_far, branch_cross], axis=0)
        up_grad = contract_rows(normed_two, after(grad_up, branch_own), LOW)

    grad_mixed = product(grad_branch, output_full, LOW)
    mixed_flat = jnp.concatenate([mixed_near, mixed_far], axis=0).reshape(token_count, query_cols)
    lse = jnp.concatenate([lse_near, lse_far], axis=0)
    attend_args = (
        info,
        query_rot,
        key_past,
        value_past,
        key_own,
        value_own,
        grad_mixed.reshape(seq_grp, local_len, query_cols),
        lse,
        cosine,
        sine,
        heads,
        head_dim,
        scale,
    )
    if split:
        line_grad, output_grad, block_share = attend_exchange(
            *attend_args,
            grad_branch,
            mixed_flat,
            (mlp_far, mlp_side, mlp_own),
            middle_share,
        )
        line_grad = line_grad.reshape(token_count, -1)
    else:
        grad_query, mine_past, mine_own, other_past, other_own = attend_backward(*attend_args)
        swap = lambda value: jnp.stack([value[r ^ 1] for r in range(seq_grp)])
        got_past, got_own = from_partner((other_past, other_own), "tp", 1)
        past_sum = mine_past + swap(got_past)
        own_sum = mine_own + swap(got_own)
        own_sum = own_sum + lax.psum_scatter(past_sum, "ctx", scatter_dimension=1, tiled=True)
        half_lanes = head_dim // 2
        turned = own_sum * cosine - jnp.roll(own_sum, half_lanes, axis=-1) * sine
        own_grad = jnp.where(parity == 0, turned, own_sum).astype(LOW).reshape(token_count, head_dim)
        line_grad = jnp.concatenate([grad_query.reshape(token_count, query_cols), own_grad], axis=1)
    own_weight = lax.dynamic_slice_in_dim(
        project_full, query_cols + parity * head_dim, head_dim, axis=1
    )
    back_full = jnp.concatenate([project_full[:, :query_cols], own_weight], axis=1)
    normed_flat = normed_one.reshape(token_count, model_width)
    if split:
        input_share, gain_one, attn_grad, bias_grad, block_home = finish_rows(
            line_grad,
            back_full,
            own_in,
            grad_middle,
            gains_now[0:1],
            normed_flat,
            block_share,
        )
        attn_grad = jnp.concatenate([attn_grad, output_grad], axis=1)
    else:
        half = token_count // 2
        line_far = contract_cols(line_grad[half:], back_full, LOW).reshape(2, local_len, model_width)
        line_near = contract_cols(line_grad[:half], back_full, LOW).reshape(2, local_len, model_width)
        line_wide = collect_far(line_far[0], line_far[1])
        line_got = from_partner(line_wide, "tp", 2)
        line_core = from_partner(line_near[1], "tp", 1)
        first_mlp, finish_mlp = collect_all((hidden_act,), ((down_full, 0, 1),), up_grad, branch_far)
        block_share = (middle_share + finish_mlp()).astype(LOW)
        grad_one_share = line_near[0].astype(WIDE) + line_core.astype(WIDE) + line_got.astype(WIDE)
        inv_one = lax.rsqrt(jnp.mean(in_share * in_share, axis=-1, keepdims=True) + EPS)
        grad_norm_one, gain_one = norm_backward(in_share, inv_one, gains_now[0], grad_one_share)
        input_share = (grad_middle + grad_norm_one).astype(LOW)
        attn_grad = jnp.concatenate(
            [contract_rows(normed_flat, line_grad, LOW), contract_rows(grad_branch, mixed_flat, LOW)],
            axis=1,
        )
        bias_grad = jnp.sum(line_grad.astype(WIDE), axis=0)

    def scatter_units(grad):
        if not split:
            return scatter_sum(grad, ctx_rank, LOW)
        return lax.psum_scatter(grad, "fsdp", scatter_dimension=0, tiled=True)

    unit_grads = (grad_a, down_b, up_grad_b, gate_grad_b) if split else (down_grad, gate_grad, up_grad)
    unit_sums = [scatter_units(unit_grads[0])]
    if split:
        unit_sums += [scatter_units(after(g, unit_sums[0])) for g in unit_grads[1:3]]
        unit_sums += [scatter_units(after(unit_grads[3], *unit_sums))]
    else:
        unit_sums += [scatter_units(g) for g in unit_grads[1:]]

    attn_end = scatter_sum(attn_grad, ctx_rank, LOW, *unit_sums)

    home_order = jnp.stack(home_now).astype(jnp.int32)

    def leave(share):
        return lax.ppermute(share, ("fsdp", "tp"), back)

    def arrive(own):
        far = from_partner(own, "tp", 2)
        near = from_partner(own, "tp", 1)
        return place_rows((own, near, far, from_partner(far, "tp", 1)), home_order)

    input_home = leave(input_share)
    if not split:
        block_home = leave(block_share)
    block_out = arrive(block_home)
    input_grad = arrive(input_home)

    gain_grad = jnp.concatenate([gain_one, gain_two], axis=0).T
    gain_grad = gain_grad + from_partner(gain_grad, "tp", 1)
    gain_grad = gain_grad + from_partner(gain_grad, "tp", 2)
    shard_count = fsdp_count * ctx_count
    share = head_dim // shard_count
    bias_cols = jnp.transpose(bias_grad.reshape(heads + 1, shard_count, share), (1, 2, 0))
    bias_cols = jnp.pad(bias_cols, ((0, 0), (0, (model_width - head_dim) // shard_count), (0, 0)))
    tiny = jnp.concatenate([gain_grad, bias_cols.reshape(model_width, heads + 1)], axis=1)
    tiny = jnp.pad(tiny, ((0, 0), (0, 8 - tiny.shape[1])))
    tiny = tiny.reshape(fsdp_count, ctx_count, model_width // shard_count, 8)
    if split:
        kept, sent = scatter_ctx(tiny, ctx_rank)
        tiny = kept + from_partner(sent, "ctx", 1)
    else:
        tiny = lax.psum_scatter(tiny, "ctx", scatter_dimension=1, tiled=True)
    tiny = tiny.reshape(fsdp_count, -1, 8)
    pick = lambda shift: lax.dynamic_index_in_dim(
        tiny, lax.rem(group_rank + shift, fsdp_count), 0, keepdims=False
    )
    tiny_grad = pick(0)
    for shift in range(1, fsdp_count):
        pairs = [(f, (f + shift) % fsdp_count) for f in range(fsdp_count)]
        tiny_grad = tiny_grad + lax.ppermute(pick(shift), "fsdp", pairs)

    if split:

        def unit_end(total, *earlier):
            kept, sent = scatter_ctx(total.reshape(1, ctx_count, -1, total.shape[1]), ctx_rank)
            return kept[0], from_partner(after(sent[0], *earlier), "ctx", 1)

        own_a, got_a = unit_end(unit_sums[0], line_grad)
        ends = [unit_end(t, line_grad) for t in unit_sums[1:]]

        def joined(part, end):
            cols = slice(part * first_units, (part + 1) * first_units)
            own = jnp.concatenate([own_a[:, cols], end[0]], axis=1)
            got = jnp.concatenate([got_a[:, cols], end[1]], axis=1)
            first, second = jnp.where(ctx_rank == 0, own, got), jnp.where(ctx_rank == 0, got, own)
            return jnp.concatenate([first, second], axis=1)[:, :units].astype(WIDE)

        down_end, gate_end, up_end = joined(0, ends[0]), joined(1, ends[2]), joined(2, ends[1])
    else:
        down_end, gate_end, up_end = (t[:, :units].astype(WIDE) for t in unit_sums)
    return (
        block_out,
        input_grad,
        attn_end[:, :query_cols].astype(WIDE),
        attn_end[:, query_cols : query_cols + head_dim].astype(WIDE),
        attn_end[:, query_cols + head_dim :].astype(WIDE).T,
        tiny_grad[:, :2].T,
        tiny_grad[:share, 2 : 2 + heads].T,
        tiny_grad[:share, 2 + heads : 3 + heads].T,
        gate_end,
        up_end,
        down_end.T,
    )


def solution(mesh):
    placed = (
        P("fsdp", "ctx", None),
        P("fsdp", "ctx", None),
        P(),
        P(None, "ctx"),
        P(),
        P(("fsdp", "ctx"), "tp"),
        P(("fsdp", "ctx"), None),
        P("tp", ("fsdp", "ctx")),
        P(None, ("fsdp", "ctx")),
        P("tp", None),
        P(),
        P(("fsdp", "ctx"), "tp"),
        P(("fsdp", "ctx"), "tp"),
        P("tp", ("fsdp", "ctx")),
    )
    return jax.shard_map(
        local,
        mesh=mesh,
        in_specs=placed,
        out_specs=(
            P("fsdp", "ctx", None),
            P("fsdp", "ctx", None),
            P(("fsdp", "ctx"), "tp"),
            P(("fsdp", "ctx"), "tp"),
            P("tp", ("fsdp", "ctx")),
            P(None, ("fsdp", "ctx")),
            P("tp", ("fsdp", "ctx")),
            P("tp", ("fsdp", "ctx")),
            P(("fsdp", "ctx"), "tp"),
            P(("fsdp", "ctx"), "tp"),
            P("tp", ("fsdp", "ctx")),
        ),
        check_vma=False,
    )
```

```python
import functools
import math

import jax
import jax.numpy as jnp
from jax import lax
from jax.experimental import pallas as pl
from jax.experimental.pallas import tpu as pltpu
from jax.sharding import PartitionSpec as P

EPS = 1e-06
ROPE_BASE = 10000.0
NEG_FILL = -1e30
LOW = jnp.bfloat16
WIDE = jnp.float32
DEAL_SHIFT = (0, 2, 1, 3)


def from_partner(value, axis, apart):
    pairs = [(source, source ^ apart) for source in range(lax.axis_size(axis))]
    return lax.ppermute(value, axis, pairs)


def product(left_side, right_side, kind=WIDE):
    return jnp.dot(left_side, right_side, preferred_element_type=WIDE).astype(kind)


def contract_rows(left_side, right_side, kind=WIDE):
    return lax.dot_general(
        left_side, right_side, (((0,), (0,)), ((), ())), preferred_element_type=WIDE
    ).astype(kind)


def contract_cols(left_side, right_side, kind=WIDE):
    return lax.dot_general(
        left_side, right_side, (((1,), (1,)), ((), ())), preferred_element_type=WIDE
    ).astype(kind)


def norm_backward(values, scale_inv, gain_row, upstream):
    scaled = gain_row * upstream
    inner_mean = jnp.mean(values * scaled, axis=-1, keepdims=True)
    grad_in = scale_inv * scaled - values * (scale_inv * scale_inv * scale_inv) * inner_mean
    gain_grad = jnp.sum(upstream * values * scale_inv, axis=0, keepdims=True)
    return (grad_in, gain_grad)


def after(value, *earlier):
    return lax.optimization_barrier((value, *earlier))[0]


def collect_far(far_part, cross_part):
    wide = far_part.astype(WIDE) + from_partner(cross_part, "tp", 1).astype(WIDE)
    return wide.astype(LOW)


def units_split():
    return lax.axis_size("ctx") == 2


def all_rows(shard):
    return lax.all_gather(shard, "fsdp", axis=0, tiled=True)


def scatter_ctx(blocks, ctx_rank):
    kept = lax.dynamic_index_in_dim(blocks, ctx_rank, 1, keepdims=False)
    sent = lax.dynamic_index_in_dim(blocks, 1 - ctx_rank, 1, keepdims=False)
    return kept, sent


def scatter_sum(grad, ctx_rank, kind, *earlier):
    fsdp_count, ctx_count = lax.axis_size("fsdp"), lax.axis_size("ctx")
    rows, cols = grad.shape
    blocks = grad.reshape(fsdp_count, ctx_count, rows // (fsdp_count * ctx_count), cols)
    if ctx_count == 2:
        kept, sent = scatter_ctx(blocks, ctx_rank)
        got = from_partner(sent, "ctx", 1)
        held = (after(kept, *earlier).astype(WIDE) + got.astype(WIDE)).astype(kind)
    else:
        swapped = jnp.swapaxes(blocks, 0, 1).reshape(rows, cols)
        held = lax.psum_scatter(swapped, "ctx", scatter_dimension=0, tiled=True)
    held = held.reshape(rows // ctx_count, cols)
    return lax.psum_scatter(held, "fsdp", scatter_dimension=0, tiled=True)


def estimate(flops, moved, transcendentals=0):
    return pl.CostEstimate(flops=flops, bytes_accessed=moved, transcendentals=transcendentals)


def part_spec(rows, cols, part):
    return pl.BlockSpec((rows, cols), lambda *_: (0, part), pipeline_mode=pl.Buffered(1))


def whole_spec(*shape, once=False):
    mode = {"pipeline_mode": pl.Buffered(1)} if once else {}
    return pl.BlockSpec(shape, lambda *_: (0,) * len(shape), **mode)


def rows_kernel(groups, *refs):
    slot = pl.program_id(0)
    weight, lin, stacked = refs[-3:]

    def run(pieces):
        start = 0
        for piece in pieces:
            stacked[start : start + piece.shape[0]] = piece[...]
            start += piece.shape[0]
        lin[...] = jnp.dot(stacked[...], weight[...], preferred_element_type=WIDE).astype(LOW)

    first = 0
    for r, pieces in enumerate(groups):
        pl.when(slot == r)(functools.partial(run, refs[first : first + pieces]))
        first += pieces


def stack_rows(slots, weight, part, parts):
    groups = [len(s) for s in slots]
    rows = [piece for s in slots for piece in s]
    width, length = rows[0].shape[1], sum(piece.shape[0] for piece in slots[0])
    count, cols = len(slots), weight.shape[1] // parts
    return pl.pallas_call(
        functools.partial(rows_kernel, groups),
        grid=(count,),
        in_specs=[whole_spec(*piece.shape, once=True) for piece in rows]
        + [part_spec(width, cols, part)],
        out_specs=[
            pl.BlockSpec((length, cols), lambda s: (s, 0)),
            pl.BlockSpec((length, width), lambda s: (s, 0)),
        ],
        out_shape=[
            jax.ShapeDtypeStruct((count * length, cols), LOW),
            jax.ShapeDtypeStruct((count * length, width), LOW),
        ],
        compiler_params=pltpu.CompilerParams(vmem_limit_bytes=60 << 20),
        cost_estimate=estimate(
            2 * count * length * width * cols, 2 * (count * length * (2 * width + cols) + width * cols)
        ),
    )(*rows, weight)


def units_kernel(h, up, gate, grad, hid, grad_gate, grad_up):
    up_lin = jnp.dot(h[...], up[...], preferred_element_type=WIDE)
    gate_lin = gate[...].astype(WIDE)
    grad_hidden = grad[...].astype(WIDE)
    sigmoid = 1.0 / (1.0 + jnp.exp(-gate_lin))
    silu = gate_lin * sigmoid
    hid[...] = (silu * up_lin).astype(LOW)
    grad_gate[...] = (grad_hidden * up_lin * sigmoid * (1.0 + gate_lin * (1.0 - sigmoid))).astype(LOW)
    grad_up[...] = (grad_hidden * silu).astype(LOW)


def hidden_units(h, up, part, parts, gate_lin, grad_hidden):
    tokens, width = h.shape
    cols = up.shape[1] // parts
    step = math.gcd(512, tokens)
    by_row = lambda n: pl.BlockSpec((step, n), lambda i: (i, 0))
    return pl.pallas_call(
        units_kernel,
        grid=(tokens // step,),
        in_specs=[by_row(width), part_spec(width, cols, part), by_row(cols), by_row(cols)],
        out_specs=[by_row(cols)] * 3,
        out_shape=[jax.ShapeDtypeStruct((tokens, cols), LOW)] * 3,
        compiler_params=pltpu.CompilerParams(vmem_limit_bytes=60 << 20),
        cost_estimate=estimate(
            2 * tokens * width * cols, 2 * (tokens * width + width * cols + 5 * tokens * cols)
        ),
    )(h, up, gate_lin, grad_hidden)


def back_kernel(terms, *refs):
    lefts, weights, outs = refs[:terms], refs[terms : 2 * terms], refs[2 * terms :]
    total = None
    for left, weight in zip(lefts, weights):
        term = dot_cols(left[...], weight[...])
        total = term if total is None else total + term
    for i, out in enumerate(outs):

        @pl.when(pl.program_id(0) == i)
        def _():
            out[...] = total.astype(LOW)


def back_rows(lefts, weights, first_slot, slots, length):
    width = weights[0][0].shape[0]
    depth = sum(left.shape[1] for left in lefts)
    return pl.pallas_call(
        functools.partial(back_kernel, len(lefts)),
        grid=(slots,),
        in_specs=[
            pl.BlockSpec((length, left.shape[1]), lambda s: (first_slot + s, 0)) for left in lefts
        ]
        + [part_spec(width, w.shape[1] // parts, part) for w, part, parts in weights],
        out_specs=[whole_spec(length, width)] * slots,
        out_shape=[jax.ShapeDtypeStruct((length, width), LOW)] * slots,
        compiler_params=pltpu.CompilerParams(vmem_limit_bytes=60 << 20),
        cost_estimate=estimate(
            2 * slots * length * width * depth,
            2 * (slots * length * (width + depth) + width * depth),
        ),
    )(*lefts, *[w for w, _, _ in weights])


def chosen_kernel(near, count, info, cotangent, *refs):
    slot = pl.program_id(0)
    others, (weight, lin, stacked) = refs[:count], refs[count:]

    @pl.when(slot < near)
    def _():
        stacked[...] = cotangent[0]

    for k, other in enumerate(others):

        @pl.when((slot >= near) & (info[slot] == k))
        def _():
            stacked[...] = other[...]

    lin[...] = jnp.dot(stacked[...], weight[...], preferred_element_type=WIDE).astype(LOW)


def chosen_rows(info, cotangent, others, weight, part, parts):
    near, length, width = cotangent.shape
    slots, cols = near + len(others), weight.shape[1] // parts
    held = lambda rows, n, at: pl.BlockSpec(
        (rows, n), lambda s, info: (0, at), pipeline_mode=pl.Buffered(1)
    )
    return pl.pallas_call(
        functools.partial(chosen_kernel, near, len(others)),
        grid_spec=pltpu.PrefetchScalarGridSpec(
            num_scalar_prefetch=1,
            grid=(slots,),
            in_specs=[
                pl.BlockSpec((1, length, width), lambda s, info: (info[jnp.minimum(s, near - 1)], 0, 0))
            ]
            + [held(length, width, 0)] * len(others)
            + [held(width, cols, part)],
            out_specs=[
                pl.BlockSpec((length, cols), lambda s, info: (s, 0)),
                pl.BlockSpec((length, width), lambda s, info: (s, 0)),
            ],
        ),
        out_shape=[
            jax.ShapeDtypeStruct((slots * length, cols), LOW),
            jax.ShapeDtypeStruct((slots * length, width), LOW),
        ],
        compiler_params=pltpu.CompilerParams(vmem_limit_bytes=60 << 20),
        cost_estimate=estimate(
            2 * slots * length * width * cols, 2 * (slots * length * (2 * width + cols) + width * cols)
        ),
    )(info, cotangent, *others, weight)


def full_units_kernel(h, g, down, gate, up, hid, grad_gate, grad_up):
    gate_lin = jnp.dot(h[...], gate[...], preferred_element_type=WIDE)
    up_lin = jnp.dot(h[...], up[...], preferred_element_type=WIDE)
    grad_hidden = jnp.dot(g[...], down[...], preferred_element_type=WIDE)
    sigmoid = 1.0 / (1.0 + jnp.exp(-gate_lin))
    silu = gate_lin * sigmoid
    hid[...] = (silu * up_lin).astype(LOW)
    grad_gate[...] = (grad_hidden * up_lin * sigmoid * (1.0 + gate_lin * (1.0 - sigmoid))).astype(LOW)
    grad_up[...] = (grad_hidden * silu).astype(LOW)


def full_units(h, g, weight):
    tokens, width = h.shape
    cols = weight.shape[1] // 3
    step = math.gcd(512, tokens)
    by_row = lambda n: pl.BlockSpec((step, n), lambda i: (i, 0))
    return pl.pallas_call(
        full_units_kernel,
        grid=(tokens // step,),
        in_specs=[by_row(width)] * 2 + [part_spec(width, cols, i) for i in range(3)],
        out_specs=[by_row(cols)] * 3,
        out_shape=[jax.ShapeDtypeStruct((tokens, cols), LOW)] * 3,
        compiler_params=pltpu.CompilerParams(vmem_limit_bytes=60 << 20),
        cost_estimate=estimate(
            6 * tokens * width * cols, 2 * (2 * tokens * width + 3 * width * cols + 3 * tokens * cols)
        ),
    )(h, g, weight, weight, weight)


def first_grads_kernel(g, h, hid, gate, up, out):
    part = pl.program_id(0)
    for i, (left, right) in enumerate(((g, hid), (h, gate), (h, up))):

        @pl.when(part == i)
        def _():
            out[...] = dot_rows(left[...], right[...]).astype(LOW)


def first_grads(grad_rows, rows, hid, grad_gate, grad_up):
    tokens, width = rows.shape
    cols, tile = hid.shape[1], 256
    tiles = width // tile
    return pl.pallas_call(
        first_grads_kernel,
        grid=(3, tiles),
        in_specs=[
            pl.BlockSpec((tokens, tile), lambda p, i: (0, jnp.where(p == 0, i, tiles - 1))),
            pl.BlockSpec((tokens, tile), lambda p, i: (0, jnp.where(p == 0, 0, i))),
        ]
        + [whole_spec(tokens, cols, once=True)] * 3,
        out_specs=pl.BlockSpec((tile, cols), lambda p, i: (i, p)),
        out_shape=jax.ShapeDtypeStruct((width, 3 * cols), LOW),
        compiler_params=pltpu.CompilerParams(vmem_limit_bytes=60 << 20),
        cost_estimate=estimate(6 * tokens * width * cols, 6 * tokens * cols + 6 * width * cols),
    )(grad_rows, rows, hid, grad_gate, grad_up)


MESH_ID = pl.DeviceIdType.MESH


def meet(partners):
    barrier = pltpu.get_barrier_semaphore()
    for partner in partners:
        pl.semaphore_signal(barrier, inc=1, device_id=partner, device_id_type=MESH_ID)
    pl.semaphore_wait(barrier, len(partners))


def partners_of():
    tensor_rank, ctx_rank = lax.axis_index("tp"), lax.axis_index("ctx")
    return {"tp": tensor_rank ^ 1}, {"tp": tensor_rank ^ 2}, {"ctx": ctx_rank ^ 1}


def collect_kernel(
    slots, tiles, gate_a, up_a, gate_b, up_b, w_gate_a, w_up_a, w_gate_b, w_up_b, left, right, hid, up, total,
    down_out, up_out, parts, sent, core_in, across_in, last_in, held, send, recv, load
):
    step = pl.program_id(0)
    steps = pl.num_programs(0)
    core, far, side = partners_of()
    half = total.shape[0] // 2
    remote = remote_copy(send, recv)
    cores = [remote(sent.at[k % 2], core_in.at[k], k, core) for k in range(4)]
    across = [
        remote(parts.at[3, pl.ds(0, half)], across_in.at[0], 4, far),
        remote(parts.at[3, pl.ds(half, half)], across_in.at[1], 5, side),
    ]
    lasts = [
        remote(parts.at[1], last_in.at[0], 6, far),
        remote(parts.at[2, pl.ds(half, half)], last_in.at[1, pl.ds(half, half)], 7, side),
        remote(parts.at[2, pl.ds(0, half)], last_in.at[1, pl.ds(0, half)], 8, side),
    ]
    loading = [
        pltpu.make_async_copy(source, held.at[i], load.at[i]) for i, source in enumerate((hid, up))
    ]

    @pl.when(step == 0)
    def _():
        for copy in loading:
            copy.start()
        meet((core, far, side))

    for k in (2, 3):
        pl.when(step == 2 * k)(cores[k - 2].wait_send)

    @pl.when(step < slots)
    def _():
        part = (
            dot_cols(gate_a[...], w_gate_a[...])
            + dot_cols(up_a[...], w_up_a[...])
            + dot_cols(gate_b[...], w_gate_b[...])
            + dot_cols(up_b[...], w_up_b[...])
        )

        @pl.when(step == slots - 1)
        def _():
            total[...] = part

        for k in range(4):

            @pl.when(step == 2 * k)
            def _():
                sent[k % 2] = part.astype(LOW)
                cores[k].start()

            if k < 3:

                @pl.when(step == 2 * k + 1)
                def _():
                    cores[k].wait_recv()
                    parts[3 - k] = (part + core_in[k].astype(WIDE)).astype(LOW)

    def add(slot, rows, value):
        parts[slot, rows] = (parts[slot, rows].astype(WIDE) + value.astype(WIDE)).astype(LOW)

    low, high = pl.ds(0, half), pl.ds(half, half)

    @pl.when(step == 1)
    def _():
        for copy in across:
            copy.start()

    pl.when(step == 3)(lasts[1].start)

    @pl.when(step == 5)
    def _():
        across[1].wait_recv()
        add(1, high, across_in[1])
        lasts[0].start()
        across[0].wait_recv()
        add(2, low, across_in[0])
        lasts[2].start()

    @pl.when((step >= slots) & (step < slots + tiles))
    def _():
        pl.when(step == slots)(loading[0].wait)
        down_out[...] = dot_rows(left[...], held[0]).astype(LOW)

    @pl.when(step >= slots + tiles)
    def _():
        pl.when(step == slots + tiles)(loading[1].wait)
        up_out[...] = dot_rows(right[...], held[1]).astype(LOW)

    @pl.when(step == steps - 1)
    def _():
        cores[3].wait_recv()
        for copy in lasts:
            copy.wait_recv()
        total[...] += (
            core_in[3].astype(WIDE) + last_in[0].astype(WIDE) + last_in[1].astype(WIDE)
        )
        for copy in (*cores[2:], *across, *lasts):
            copy.wait_send()


def collect_back(first, second, weight_a, weight_b, grad_rows, rows, hid, length):
    tokens, cols_a = first[0].shape
    cols = second[0].shape[1]
    width = weight_a.shape[0]
    slots, tile = tokens // length, 256
    tiles = width // tile
    row = lambda n: pl.BlockSpec((length, n), lambda i: (jnp.maximum(slots - 1 - i, 0), 0))
    column = lambda i, start: jnp.clip(i - start, 0, tiles - 1)
    down_at, up_at = (lambda i: column(i, slots)), (lambda i: column(i, slots + tiles))
    return pl.pallas_call(
        functools.partial(collect_kernel, slots, tiles),
        grid=(slots + 2 * tiles,),
        in_specs=[row(cols_a), row(cols_a), row(cols), row(cols)]
        + [part_spec(width, cols_a, 1), part_spec(width, cols_a, 2)]
        + [part_spec(width, cols, 1), part_spec(width, cols, 2)]
        + [
            pl.BlockSpec((tokens, tile), lambda i: (0, down_at(i))),
            pl.BlockSpec((tokens, tile), lambda i: (0, up_at(i))),
            ANYWHERE,
            ANYWHERE,
        ],
        out_specs=[
            whole_spec(length, width, once=True),
            pl.BlockSpec((tile, cols), lambda i: (down_at(i), 0)),
            pl.BlockSpec((tile, cols), lambda i: (up_at(i), 0)),
        ],
        out_shape=[
            jax.ShapeDtypeStruct((length, width), WIDE),
            jax.ShapeDtypeStruct((width, cols), LOW),
            jax.ShapeDtypeStruct((width, cols), LOW),
        ],
        scratch_shapes=[
            pltpu.VMEM((4, length, width), LOW),
            pltpu.VMEM((2, length, width), LOW),
            pltpu.VMEM((4, length, width), LOW),
            pltpu.VMEM((2, length // 2, width), LOW),
            pltpu.VMEM((2, length, width), LOW),
            pltpu.VMEM((2, tokens, cols), LOW),
            pltpu.SemaphoreType.DMA((9,)),
            pltpu.SemaphoreType.DMA((9,)),
            pltpu.SemaphoreType.DMA((2,)),
        ],
        compiler_params=pltpu.CompilerParams(
            vmem_limit_bytes=63 << 20, collective_id=1, has_side_effects=True
        ),
        cost_estimate=estimate(6 * tokens * width * cols, 10 * tokens * cols),
    )(*first, *second, weight_a, weight_a, weight_b, weight_b, grad_rows, rows, hid, second[1])


def remote_copy(send, recv):
    def make(source, target, index, partner):
        return pltpu.make_async_remote_copy(
            source, target, send.at[index], recv.at[index], device_id=partner, device_id_type=MESH_ID
        )

    return make


def branch_kernel(
    slots, tiles, total, middle, own_grad, gain, hid_a, hid_b, w_a, w_b, turned, gate, grad_middle, gain_grad,
    gate_out, branch, mlp_own, mlp_far, mlp_side, own, parts, core_in, across_in, held, send, recv, load
):
    step = pl.program_id(0)
    core, far, side = partners_of()
    remote = remote_copy(send, recv)
    to_far = remote(own, branch.at[2], 0, far)
    to_near = remote(own, branch.at[1], 1, core)
    to_cross = remote(branch.at[2], branch.at[3], 2, core)
    keep = pltpu.make_async_copy(own, branch.at[0], load.at[0])
    loading = pltpu.make_async_copy(gate, held, load.at[1])
    cores = [remote(parts.at[7 - 2 * k], core_in.at[k], 3 + k, core) for k in range(4)]
    across = remote(parts.at[6], across_in, 7, side)
    stores = [
        pltpu.make_async_copy(parts.at[4], mlp_side, load.at[2]),
        pltpu.make_async_copy(parts.at[2], mlp_far, load.at[3]),
        pltpu.make_async_copy(parts.at[0], mlp_own, load.at[4]),
    ]

    @pl.when(step == 0)
    def _():
        loading.start()
        meet((core, far, side))
        values, upstream = middle[...], total[...]
        inverse = lax.rsqrt(jnp.mean(values * values, axis=-1, keepdims=True) + EPS)
        grad_in, gain_grad[...] = norm_backward(values, inverse, gain[...], upstream)
        grad_in = own_grad[...].astype(WIDE) + grad_in
        grad_middle[...] = grad_in
        own[...] = grad_in.astype(LOW)
        for copy in (to_far, to_near, keep):
            copy.start()

    @pl.when(step < slots)
    def _():
        part = dot_cols(hid_a[...], w_a[...]) + dot_cols(hid_b[...], w_b[...])
        parts[slots - 1 - step] = part.astype(LOW)

    for k in range(4):
        pl.when(step == 2 * k)(cores[k].start)

        def finish(k=k):
            slot = 6 - 2 * k
            cores[k].wait_recv()
            parts[slot] = (parts[slot].astype(WIDE) + core_in[k].astype(WIDE)).astype(LOW)
            if k == 0:
                across.start()
            if k == 1:
                stores[0].start()
            if k == 3:
                stores[2].start()

        pl.when(step == 2 * k + 1)(finish)

    @pl.when(step >= slots)
    def _():
        pl.when(step == slots)(loading.wait)
        gate_out[...] = dot_rows(turned[...], held[...]).astype(LOW)

    @pl.when(step == slots + tiles - 2)
    def _():
        to_far.wait_recv()
        to_cross.start()

    @pl.when(step == slots + tiles - 1)
    def _():
        to_near.wait_recv()
        to_cross.wait_recv()
        across.wait_recv()
        parts[2] = (parts[2].astype(WIDE) + across_in[...].astype(WIDE)).astype(LOW)
        stores[1].start()
        keep.wait()
        for copy in stores:
            copy.wait()
        for copy in (to_far, to_near, to_cross, *cores, across):
            copy.wait_send()


ANYWHERE = pl.BlockSpec(memory_space=pl.ANY)


def spread_branch(total, middle, own_grad, gain, hid_a, hid_b, weight_a, weight_b, rows, grad_gate):
    length, width = total.shape
    tokens, cols = grad_gate.shape
    slots, tile = tokens // length, 256
    tiles = width // tile
    once = whole_spec(length, width, once=True)
    column = lambda i: jnp.clip(i - slots, 0, tiles - 1)
    part = jax.ShapeDtypeStruct((length, width), LOW)
    return pl.pallas_call(
        functools.partial(branch_kernel, slots, tiles),
        grid=(slots + tiles,),
        in_specs=[
            once,
            once,
            once,
            whole_spec(1, width),
            pl.BlockSpec((length, hid_a.shape[1]), lambda i: (jnp.maximum(slots - 1 - i, 0), 0)),
            pl.BlockSpec((length, cols), lambda i: (jnp.maximum(slots - 1 - i, 0), 0)),
            part_spec(width, hid_a.shape[1], 0),
            part_spec(width, cols, 0),
            pl.BlockSpec((tokens, tile), lambda i: (0, column(i))),
            ANYWHERE,
        ],
        out_specs=[
            whole_spec(length, width, once=True),
            whole_spec(1, width),
            pl.BlockSpec((tile, cols), lambda i: (column(i), 0)),
        ]
        + [ANYWHERE] * 4,
        out_shape=[
            jax.ShapeDtypeStruct((length, width), WIDE),
            jax.ShapeDtypeStruct((1, width), WIDE),
            jax.ShapeDtypeStruct((width, cols), LOW),
            jax.ShapeDtypeStruct((4, length, width), LOW),
            part,
            part,
            part,
        ],
        scratch_shapes=[
            pltpu.VMEM((length, width), LOW),
            pltpu.VMEM((slots, length, width), LOW),
            pltpu.VMEM((4, length, width), LOW),
            pltpu.VMEM((length, width), LOW),
            pltpu.VMEM((tokens, cols), LOW),
            pltpu.SemaphoreType.DMA((8,)),
            pltpu.SemaphoreType.DMA((8,)),
            pltpu.SemaphoreType.DMA((5,)),
        ],
        compiler_params=pltpu.CompilerParams(
            vmem_limit_bytes=63 << 20, collective_id=2, has_side_effects=True
        ),
        cost_estimate=estimate(4 * tokens * width * cols, 10 * tokens * cols),
    )(total, middle, own_grad, gain, hid_a, hid_b, weight_a, weight_b, rows, grad_gate)


def line_kernel(
    slots, tiles, line, weight, own_in, grad_middle, gain, gain_two, rows_one, line_all, block, share,
    gain_grad, attn_out, bias_out, home, parts, core_in, far_in, total, gains, gains_in, send, recv, load
):
    step = pl.program_id(0)
    core, far, _ = partners_of()
    tensor_rank, group = lax.axis_index("tp"), lax.axis_index("fsdp")
    shift = (tensor_rank % 2) * 2 + tensor_rank // 2
    target = {"fsdp": (group + slots - shift) % slots}
    source = {"fsdp": (group + shift) % slots}
    stays = shift == 0
    remote = remote_copy(send, recv)
    cores = [remote(parts.at[3 - 2 * k], core_in.at[k], k, core) for k in range(2)]
    to_far = remote(parts.at[2], far_in, 2, far)
    leave = remote(block, home, 3, target)
    keep = pltpu.make_async_copy(block, home, load)
    cross = {"tp": tensor_rank ^ 3}
    gain_copies = [
        remote(gains, gains_in.at[i], 4 + i, partner) for i, partner in enumerate((core, far, cross))
    ]

    @pl.when(step == 0)
    def _():
        barrier = pltpu.get_barrier_semaphore()
        for partner in (core, far, cross):
            pl.semaphore_signal(barrier, inc=1, device_id=partner, device_id_type=MESH_ID)

        @pl.when(stays)
        def _():
            pl.semaphore_wait(barrier, 3)
            keep.start()

        @pl.when(jnp.logical_not(stays))
        def _():
            for partner in (target, source):
                pl.semaphore_signal(barrier, inc=1, device_id=partner, device_id_type=MESH_ID)
            pl.semaphore_wait(barrier, 5)
            leave.start()

    @pl.when(step < slots)
    def _():
        part = dot_cols(line[...], weight[...])
        parts[slots - 1 - step] = part.astype(LOW)

        @pl.when(step == slots - 1)
        def _():
            total[...] = part

    for k in range(2):
        pl.when(step == 2 * k)(cores[k].start)

    @pl.when(step == 1)
    def _():
        cores[0].wait_recv()
        parts[2] = (parts[2].astype(WIDE) + core_in[0].astype(WIDE)).astype(LOW)
        to_far.start()

    @pl.when(step == slots - 1)
    def _():
        bias_out[...] = jnp.sum(line_all[...].astype(WIDE), axis=0, keepdims=True)

    @pl.when(step >= slots)
    def _():
        attn_out[...] = dot_rows(rows_one[...], line_all[...]).astype(LOW)

    @pl.when(step == slots + tiles - 1)
    def _():
        cores[1].wait_recv()
        to_far.wait_recv()
        upstream = total[...] + core_in[1].astype(WIDE) + far_in[...].astype(WIDE)
        values = own_in[...].astype(WIDE)
        inverse = lax.rsqrt(jnp.mean(values * values, axis=-1, keepdims=True) + EPS)
        grad_in, gain_one = norm_backward(values, inverse, gain[...], upstream)
        gains[0:1] = gain_one
        gains[1:2] = gain_two[...]
        for copy in gain_copies:
            copy.start()
        share[...] = (grad_middle[...] + grad_in).astype(LOW)
        for copy in gain_copies:
            copy.wait_recv()
        gain_grad[...] = (gains[...] + gains_in[0]) + (gains_in[1] + gains_in[2])
        for copy in (*cores, to_far, *gain_copies):
            copy.wait_send()
        pl.when(stays)(keep.wait)

        @pl.when(jnp.logical_not(stays))
        def _():
            leave.wait_recv()
            leave.wait_send()


def finish_rows(line, weight, own_in, grad_middle, gain, gain_two, rows_one, block):
    length, width = own_in.shape
    near_tokens, line_cols = line.shape
    slots, tile = near_tokens // length, 256
    tiles = width // tile
    once = whole_spec(length, width, once=True)
    column = lambda i: jnp.clip(i - slots, 0, tiles - 1)
    by_column = lambda n: pl.BlockSpec((n, tile), lambda i: (0, column(i)))
    attn_cols = line_cols
    return pl.pallas_call(
        functools.partial(line_kernel, slots, tiles),
        grid=(slots + tiles,),
        in_specs=[
            pl.BlockSpec((length, line_cols), lambda i: (jnp.maximum(slots - 1 - i, 0), 0)),
            whole_spec(width, line_cols, once=True),
            once,
            once,
            whole_spec(1, width),
            whole_spec(1, width),
            by_column(near_tokens),
            whole_spec(near_tokens, line_cols, once=True),
            ANYWHERE,
        ],
        out_specs=[
            whole_spec(length, width),
            whole_spec(2, width),
            pl.BlockSpec((tile, attn_cols), lambda i: (column(i), 0)),
            whole_spec(1, line_cols),
            ANYWHERE,
        ],
        out_shape=[
            jax.ShapeDtypeStruct((length, width), LOW),
            jax.ShapeDtypeStruct((2, width), WIDE),
            jax.ShapeDtypeStruct((width, attn_cols), LOW),
            jax.ShapeDtypeStruct((1, line_cols), WIDE),
            jax.ShapeDtypeStruct((length, width), LOW),
        ],
        scratch_shapes=[
            pltpu.VMEM((slots, length, width), LOW),
            pltpu.VMEM((2, length, width), LOW),
            pltpu.VMEM((length, width), LOW),
            pltpu.VMEM((length, width), WIDE),
            pltpu.VMEM((2, width), WIDE),
            pltpu.VMEM((3, 2, width), WIDE),
            pltpu.SemaphoreType.DMA((7,)),
            pltpu.SemaphoreType.DMA((7,)),
            pltpu.SemaphoreType.DMA,
        ],
        compiler_params=pltpu.CompilerParams(
            vmem_limit_bytes=63 << 20, collective_id=3, has_side_effects=True
        ),
        cost_estimate=estimate(2 * near_tokens * width * attn_cols, 10 * near_tokens * width),
    )(line, weight, own_in, grad_middle, gain, gain_two, rows_one, line, block)


def place_kernel(count, info, *refs):
    out = refs[count]
    for r in range(count):

        @pl.when(pl.program_id(0) == r)
        def _():
            out[0] = refs[r][...]


def place_rows(rows, order):
    length, width = rows[0].shape
    count = len(rows)
    held = pl.BlockSpec((length, width), lambda s, info: (0, 0), pipeline_mode=pl.Buffered(1))
    return pl.pallas_call(
        functools.partial(place_kernel, count),
        grid_spec=pltpu.PrefetchScalarGridSpec(
            num_scalar_prefetch=1,
            grid=(count,),
            in_specs=[held] * count,
            out_specs=pl.BlockSpec((1, length, width), lambda s, info: (info[s], 0, 0)),
        ),
        out_shape=jax.ShapeDtypeStruct((count, length, width), LOW),
        compiler_params=pltpu.CompilerParams(vmem_limit_bytes=32 << 20),
        cost_estimate=estimate(0, 4 * count * length * width),
    )(order, *rows)


def turn(values, cosine, sine_signed):
    return values * cosine + pltpu.roll(values, values.shape[-1] // 2, 1) * sine_signed


def turn_back(values, cosine, sine_signed):
    return values * cosine - pltpu.roll(values, values.shape[-1] // 2, 1) * sine_signed


def project_kernel(
    heads, head_dim, x0, x1, x2, x3, gains, weight, bias, cosine, sine, h_out, q_out, k_out, v_out, gain
):
    slot = pl.program_id(0)

    @pl.when(slot == 0)
    def _():
        gain[...] = gains[...].astype(WIDE).T[:8]


    def run(x_ref):
        x = x_ref[...].astype(WIDE)
        scale_inv = lax.rsqrt(jnp.mean(x * x, axis=-1, keepdims=True) + EPS)
        normed = (x * scale_inv * gain[0:1]).astype(LOW)
        h_out[0] = normed
        lin = jnp.dot(normed, weight[...], preferred_element_type=WIDE) + bias[...]
        cos, sin = cosine[0], sine[0]
        for h in range(heads + 1):
            part = turn(lin[:, h * head_dim : (h + 1) * head_dim], cos, sin).astype(LOW)
            if h < heads:
                q_out[0, :, h * head_dim : (h + 1) * head_dim] = part
            else:
                k_out[0] = part
        v_out[0] = lin[:, (heads + 1) * head_dim :].astype(LOW)

    for r, x_ref in enumerate((x0, x1, x2, x3)):
        pl.when(slot == r)(functools.partial(run, x_ref))


def project(rows, held, bias, cosine, sine, heads, head_dim):
    length, width = rows[0].shape
    count = len(rows)
    cols = (heads + 2) * head_dim
    whole = whole_spec
    by_slot = lambda *shape: pl.BlockSpec((1, *shape), lambda s: (s,) + (0,) * len(shape))
    return pl.pallas_call(
        functools.partial(project_kernel, heads, head_dim),
        grid=(count,),
        in_specs=[whole(length, width)] * count
        + [part_spec(width, 128, cols // 128), part_spec(width, cols, 0), whole(1, cols)]
        + [by_slot(length, head_dim)] * 2,
        out_specs=[
            by_slot(length, width),
            by_slot(length, heads * head_dim),
            by_slot(length, head_dim),
            by_slot(length, head_dim),
        ],
        out_shape=[
            jax.ShapeDtypeStruct((count, length, width), LOW),
            jax.ShapeDtypeStruct((count, length, heads * head_dim), LOW),
            jax.ShapeDtypeStruct((count, length, head_dim), LOW),
            jax.ShapeDtypeStruct((count, length, head_dim), LOW),
        ],
        scratch_shapes=[pltpu.VMEM((8, width), WIDE)],
        compiler_params=pltpu.CompilerParams(vmem_limit_bytes=56 << 20),
        cost_estimate=pl.CostEstimate(
            flops=2 * count * length * width * cols,
            bytes_accessed=count * length * (2 * width + cols) * 2 + width * cols * 2,
            transcendentals=0,
        ),
    )(*rows, held, held, bias, cosine, sine)


def row_blocks(length):
    return [(i, min(256, length)) for i in range(0, length, min(256, length))]


def key_biases(length, offset, start, rows, past, keys):
    past_pos = lax.broadcasted_iota(jnp.int32, (1, past), 1)
    past_bias = jnp.where((past_pos < offset) & (past_pos < length), 0.0, NEG_FILL)
    query_pos = offset + start + lax.broadcasted_iota(jnp.int32, (rows, keys), 0)
    own_pos = offset + lax.broadcasted_iota(jnp.int32, (rows, keys), 1)
    own_bias = jnp.where((own_pos <= query_pos) & (own_pos < length), 0.0, NEG_FILL)
    return past_bias, own_bias


def dot_cols(left, right):
    return lax.dot_general(left, right, (((1,), (1,)), ((), ())), preferred_element_type=WIDE)


def dot_rows(left, right):
    return lax.dot_general(left, right, (((0,), (0,)), ((), ())), preferred_element_type=WIDE)


def attend_kernel(
    heads, head_dim, scale, first, total_slots, info, q, k_past, v_past, k_own, v_own, weight, out, lse, *parts
):
    length, offset = info[first + pl.program_id(0)], info[total_slots]
    past = k_past.shape[1]
    for start, rows in row_blocks(q.shape[1]):
        keys = start + rows
        past_bias, own_bias = key_biases(length, offset, start, rows, past, keys)
        here = slice(start, start + rows)
        for h in range(heads):
            cols = slice(h * head_dim, (h + 1) * head_dim)
            query = q[0, here, cols]
            s_past = dot_cols(query, k_past[0]) * scale + past_bias
            s_own = dot_cols(query, k_own[0, :keys]) * scale + own_bias
            top = jnp.maximum(
                jnp.max(s_past, axis=1, keepdims=True), jnp.max(s_own, axis=1, keepdims=True)
            )
            e_past, e_own = jnp.exp(s_past - top), jnp.exp(s_own - top)
            total = jnp.sum(e_past, axis=1, keepdims=True) + jnp.sum(e_own, axis=1, keepdims=True)
            inverse = 1.0 / total
            mixed = jnp.dot(
                (e_past * inverse).astype(LOW), v_past[0], preferred_element_type=WIDE
            ) + jnp.dot((e_own * inverse).astype(LOW), v_own[0, :keys], preferred_element_type=WIDE)
            out[0, here, cols] = mixed.astype(LOW)
            lse[0, here, h : h + 1] = top + jnp.log(total)
        rows_out = dot_cols(out[0, here], weight[...]).astype(LOW)
        for i, part in enumerate(parts):

            @pl.when(pl.program_id(0) == i)
            def _():
                part[here] = rows_out


def attend_forward(info, q, k_past, v_past, k_own, v_own, weight, heads, head_dim, scale, first, count):
    _, length, width = q.shape
    past = k_past.shape[1]
    by_slot = lambda *shape: pl.BlockSpec((1, *shape), lambda s, info: (first + s,) + (0,) * len(shape))
    out_slot = lambda *shape: pl.BlockSpec((1, *shape), lambda s, info: (s,) + (0,) * len(shape))
    keys = count * length * (past + length) * heads
    return pl.pallas_call(
        functools.partial(attend_kernel, heads, head_dim, scale, first, q.shape[0]),
        grid_spec=pltpu.PrefetchScalarGridSpec(
            num_scalar_prefetch=1,
            grid=(count,),
            in_specs=[
                by_slot(length, width),
                by_slot(past, head_dim),
                by_slot(past, head_dim),
                by_slot(length, head_dim),
                by_slot(length, head_dim),
                whole_spec(*weight.shape, once=True),
            ],
            out_specs=[out_slot(length, width), out_slot(length, 128)]
            + [whole_spec(length, weight.shape[0])] * count,
        ),
        out_shape=[
            jax.ShapeDtypeStruct((count, length, width), LOW),
            jax.ShapeDtypeStruct((count, length, 128), WIDE),
        ]
        + [jax.ShapeDtypeStruct((length, weight.shape[0]), LOW)] * count,
        compiler_params=pltpu.CompilerParams(vmem_limit_bytes=56 << 20),
        cost_estimate=estimate(4 * keys * head_dim, 4 * count * length * width, keys),
    )(info, q, k_past, v_past, k_own, v_own, weight)


def attend_back_rows(
    heads, head_dim, scale, length, offset, q, k_past, v_past, k_own, v_own, grad, lse, cosine, sine, put,
    dk_past, dk_own, dv_past, dv_own
):
    past = k_past.shape[1]
    for start, rows in row_blocks(q.shape[1]):
        keys = start + rows
        past_bias, own_bias = key_biases(length, offset, start, rows, past, keys)
        here = slice(start, start + rows)
        cos, sin = cosine[0, here], sine[0, here]
        for h in range(heads):
            cols = slice(h * head_dim, (h + 1) * head_dim)
            query, upstream = q[0, here, cols], grad[0, here, cols]
            log_total = lse[0, here, h : h + 1]
            p_past = jnp.exp(dot_cols(query, k_past[0]) * scale + past_bias - log_total)
            p_own = jnp.exp(dot_cols(query, k_own[0, :keys]) * scale + own_bias - log_total)
            g_past = dot_cols(upstream, v_past[0])
            g_own = dot_cols(upstream, v_own[0, :keys])
            row_dot = jnp.sum(p_past * g_past, axis=1, keepdims=True) + jnp.sum(
                p_own * g_own, axis=1, keepdims=True
            )
            s_past = (p_past * (g_past - row_dot)).astype(LOW)
            s_own = (p_own * (g_own - row_dot)).astype(LOW)
            dq = (
                jnp.dot(s_past, k_past[0], preferred_element_type=WIDE)
                + jnp.dot(s_own, k_own[0, :keys], preferred_element_type=WIDE)
            ) * scale
            put(here, cols, turn_back(dq, cos, sin).astype(LOW))
            dk_past[...] += dot_rows(s_past, query)
            dk_own[:keys] += dot_rows(s_own, query)
            dv_past[...] += dot_rows(p_past.astype(LOW), upstream)
            dv_own[:keys] += dot_rows(p_own.astype(LOW), upstream)


def attend_back_kernel(
    heads,
    head_dim,
    scale,
    info,
    q,
    k_past,
    v_past,
    k_own,
    v_own,
    grad,
    lse,
    cosine,
    sine,
    dq_out,
    mine_past,
    mine_own,
    other_past,
    other_own,
    dk_past,
    dk_own,
    dv_past,
    dv_own,
):
    slot = pl.program_id(0)
    length, offset = info[slot], info[pl.num_programs(0)]
    parity = info[pl.num_programs(0) + 1]
    for total in (dk_past, dk_own, dv_past, dv_own):
        total[...] = jnp.zeros_like(total)
    attend_back_rows(
        heads, head_dim, scale, length, offset, q, k_past, v_past, k_own, v_own, grad, lse, cosine, sine,
        lambda here, cols, value: dq_out.__setitem__((0, here, cols), value),
        dk_past, dk_own, dv_past, dv_own,
    )

    @pl.when(parity == 0)
    def _():
        mine_past[0] = dk_past[...] * scale
        mine_own[0] = dk_own[...] * scale
        other_past[0] = dv_past[...]
        other_own[0] = dv_own[...]

    @pl.when(parity != 0)
    def _():
        mine_past[0] = dv_past[...]
        mine_own[0] = dv_own[...]
        other_past[0] = dk_past[...] * scale
        other_own[0] = dk_own[...] * scale


def attend_backward(
    info, q, k_past, v_past, k_own, v_own, grad, lse, cosine, sine, heads, head_dim, scale
):
    count, length, width = q.shape
    past = k_past.shape[1]
    by_slot = lambda *shape: pl.BlockSpec((1, *shape), lambda s, info: (s,) + (0,) * len(shape))
    keys = count * length * (past + length) * heads
    return pl.pallas_call(
        functools.partial(attend_back_kernel, heads, head_dim, scale),
        grid_spec=pltpu.PrefetchScalarGridSpec(
            num_scalar_prefetch=1,
            grid=(count,),
            in_specs=[
                by_slot(length, width),
                by_slot(past, head_dim),
                by_slot(past, head_dim),
                by_slot(length, head_dim),
                by_slot(length, head_dim),
                by_slot(length, width),
                by_slot(length, 128),
                by_slot(length, head_dim),
                by_slot(length, head_dim),
            ],
            out_specs=[
                by_slot(length, width),
                by_slot(past, head_dim),
                by_slot(length, head_dim),
                by_slot(past, head_dim),
                by_slot(length, head_dim),
            ],
            scratch_shapes=[
                pltpu.VMEM((past, head_dim), WIDE),
                pltpu.VMEM((length, head_dim), WIDE),
                pltpu.VMEM((past, head_dim), WIDE),
                pltpu.VMEM((length, head_dim), WIDE),
            ],
        ),
        out_shape=[
            jax.ShapeDtypeStruct((count, length, width), LOW),
            jax.ShapeDtypeStruct((count, past, head_dim), WIDE),
            jax.ShapeDtypeStruct((count, length, head_dim), WIDE),
            jax.ShapeDtypeStruct((count, past, head_dim), WIDE),
            jax.ShapeDtypeStruct((count, length, head_dim), WIDE),
        ],
        compiler_params=pltpu.CompilerParams(vmem_limit_bytes=56 << 20),
        cost_estimate=estimate(10 * keys * head_dim, 8 * count * length * width, keys),
    )(info, q, k_past, v_past, k_own, v_own, grad, lse, cosine, sine)


def exchange_kernel(
    heads, head_dim, scale, slots, tiles, info, q, k_past, v_past, k_own, v_own, grad, lse, cosine, sine,
    cosine_all, sine_all, branch, mixed, mlp_far, mlp_side, mlp_own, middle, line, out_grad, block, mine_past,
    mine_own, other_past, other_own, got_past, got_own, side_out, side_in, dk_past, dk_own, dv_past, dv_own,
    own_rows, last_in, send, recv, load
):
    step = pl.program_id(0)
    tensor_rank = lax.axis_index("tp")
    core, far, side = partners_of()
    parity = lax.rem(tensor_rank, 2)
    offset = lax.axis_index("ctx") * q.shape[1]
    remote = remote_copy(send, recv)
    pasts = [remote(other_past.at[r], got_past.at[r ^ 1], r, core) for r in range(slots)]
    owns = [remote(other_own.at[r], got_own.at[r ^ 1], slots + r, core) for r in range(slots)]
    sides = [remote(side_out.at[r], side_in.at[r], 2 * slots + r, side) for r in range(slots)]
    lasts = [
        remote(mlp_far, last_in.at[0], 3 * slots, far),
        remote(mlp_side, last_in.at[1], 3 * slots + 1, side),
    ]
    loading = pltpu.make_async_copy(mlp_own, own_rows, load)

    @pl.when(step == 0)
    def _():
        loading.start()
        meet((core, far, side))
        for copy in lasts:
            copy.start()

    @pl.when(step < slots)
    def _():
        length = info[jnp.minimum(step, slots - 1)]
        for total in (dk_past, dk_own, dv_past, dv_own):
            total[...] = jnp.zeros_like(total)
        attend_back_rows(
            heads, head_dim, scale, length, offset, q, k_past, v_past, k_own, v_own, grad, lse, cosine,
            sine, lambda here, cols, value: line.__setitem__((step, here, cols), value),
            dk_past, dk_own, dv_past, dv_own,
        )

        @pl.when(parity == 0)
        def _():
            mine_past[step] = dk_past[...] * scale
            mine_own[step] = dk_own[...] * scale
            other_past[step] = dv_past[...]
            other_own[step] = dv_own[...]

        @pl.when(parity != 0)
        def _():
            mine_past[step] = dv_past[...]
            mine_own[step] = dv_own[...]
            other_past[step] = dk_past[...] * scale
            other_own[step] = dk_own[...] * scale

    for r in range(slots):

        def start(r=r):
            pasts[r].start()
            owns[r].start()

        pl.when(step == r)(start)

    for pair in range(0, slots, 2):

        def merge(pair=pair):
            for r in (pair, pair + 1):
                pasts[r ^ 1].wait_recv()
                side_out[r] = (mine_past[r] + got_past[r]).astype(LOW)
                sides[r].start()

        pl.when(step == pair + 1)(merge)

    @pl.when(step >= slots)
    def _():
        out_grad[...] = dot_rows(branch[...], mixed[...]).astype(LOW)

    @pl.when(step == slots + tiles - 1)
    def _():
        for r in range(slots):
            owns[r ^ 1].wait_recv()
            sides[r].wait_recv()
            total = mine_own[r] + got_own[r] + side_in[r].astype(WIDE)
            back = turn_back(total, cosine_all[r], sine_all[r])
            line[r, :, heads * head_dim :] = jnp.where(parity == 0, back, total).astype(LOW)
        loading.wait()
        for copy in lasts:
            copy.wait_recv()
        block[...] = (
            middle[...] + own_rows[...].astype(WIDE) + last_in[0].astype(WIDE) + last_in[1].astype(WIDE)
        ).astype(LOW)
        for copy in (*pasts, *owns, *sides, *lasts):
            copy.wait_send()


def attend_exchange(
    info, q, k_past, v_past, k_own, v_own, grad, lse, cosine, sine, heads, head_dim, scale, branch, mixed, mlp, middle
):
    count, length, width = q.shape
    past = k_past.shape[1]
    tokens, model_width = branch.shape
    tile = 256
    tiles = model_width // tile
    slot = lambda i: jnp.minimum(i, count - 1)
    by_slot = lambda *shape: pl.BlockSpec((1, *shape), lambda i, info: (slot(i),) + (0,) * len(shape))
    column = lambda i: jnp.clip(i - count, 0, tiles - 1)
    held = lambda *shape: pl.BlockSpec(
        shape, lambda i, info: (0,) * len(shape), pipeline_mode=pl.Buffered(1)
    )
    line_cols = width + head_dim
    return pl.pallas_call(
        functools.partial(exchange_kernel, heads, head_dim, scale, count, tiles),
        grid_spec=pltpu.PrefetchScalarGridSpec(
            num_scalar_prefetch=1,
            grid=(count + tiles,),
            in_specs=[
                by_slot(length, width),
                by_slot(past, head_dim),
                by_slot(past, head_dim),
                by_slot(length, head_dim),
                by_slot(length, head_dim),
                by_slot(length, width),
                by_slot(length, 128),
                by_slot(length, head_dim),
                by_slot(length, head_dim),
                held(count, length, head_dim),
                held(count, length, head_dim),
                pl.BlockSpec((tokens, tile), lambda i, info: (0, column(i))),
                held(*mixed.shape),
            ]
            + [ANYWHERE] * 3
            + [held(length, model_width)],
            out_specs=[
                held(count, length, line_cols),
                pl.BlockSpec((tile, width), lambda i, info: (column(i), 0)),
                held(length, model_width),
            ],
            scratch_shapes=[pltpu.VMEM((count, length, head_dim), WIDE)] * 6
            + [pltpu.VMEM((count, length, head_dim), LOW)] * 2
            + [pltpu.VMEM((length, head_dim), WIDE)] * 4
            + [
                pltpu.VMEM((length, model_width), LOW),
                pltpu.VMEM((2, length, model_width), LOW),
                pltpu.SemaphoreType.DMA((3 * count + 2,)),
                pltpu.SemaphoreType.DMA((3 * count + 2,)),
                pltpu.SemaphoreType.DMA,
            ],
        ),
        out_shape=[
            jax.ShapeDtypeStruct((count, length, line_cols), LOW),
            jax.ShapeDtypeStruct((model_width, width), LOW),
            jax.ShapeDtypeStruct((length, model_width), LOW),
        ],
        compiler_params=pltpu.CompilerParams(
            vmem_limit_bytes=63 << 20, collective_id=4, has_side_effects=True
        ),
        cost_estimate=estimate(2 * tokens * model_width * width, 10 * tokens * width),
    )(info, q, k_past, v_past, k_own, v_own, grad, lse, cosine, sine, cosine, sine, branch, mixed, *mlp, middle)


def local(
    hidden_in,
    cotangent,
    seq_lengths,
    positions,
    permutation,
    query_weight,
    keyval_weight,
    output_weight,
    norm_gains,
    bias_query,
    bias_keyval,
    gate_weight,
    up_weight,
    down_weight,
):
    group_rank = lax.axis_index("fsdp")
    ctx_rank = lax.axis_index("ctx")
    tensor_rank = lax.axis_index("tp")
    fsdp_count = lax.axis_size("fsdp")
    ctx_count = lax.axis_size("ctx")
    tensor_count = lax.axis_size("tp")
    seq_grp, local_len, model_width = hidden_in.shape
    heads, head_dim = bias_query.shape
    keyval_heads = bias_keyval.shape[0] // 2
    assert seq_grp == tensor_count == fsdp_count == len(DEAL_SHIFT)
    token_count = seq_grp * local_len
    scale = 1.0 / math.sqrt(head_dim)
    offset = ctx_rank * local_len
    head_pair = tensor_rank // (tensor_count // keyval_heads)
    parity = tensor_rank % 2
    shifts = jnp.array(DEAL_SHIFT, jnp.int32)

    table = permutation.reshape(fsdp_count, seq_grp)
    far_group = lax.rem(group_rank + shifts[tensor_rank], fsdp_count)
    far_row = lax.dynamic_index_in_dim(table, far_group, 0, keepdims=False)
    leaving = jnp.sum(jnp.where(far_row // seq_grp == group_rank, far_row - group_rank * seq_grp, 0))
    own_row = lax.dynamic_index_in_dim(table, group_rank, 0, keepdims=False)
    slot_now, seq_now, home_now = [], [], []
    for r in range(seq_grp):
        shift = shifts[tensor_rank ^ r]
        source = lax.rem(group_rank - shift + fsdp_count, fsdp_count)
        hit = own_row // seq_grp == source
        slot_now.append(jnp.sum(jnp.where(hit, jnp.arange(seq_grp), 0)))
        seq_now.append(jnp.sum(jnp.where(hit, own_row, 0)))
        target = lax.rem(group_rank + shift, fsdp_count)
        target_row = lax.dynamic_index_in_dim(table, target, 0, keepdims=False)
        home_now.append(
            jnp.sum(jnp.where(target_row // seq_grp == group_rank, target_row - group_rank * seq_grp, 0))
        )
    there = [
        (f * tensor_count + t, (f + DEAL_SHIFT[t]) % fsdp_count * tensor_count + t)
        for f in range(fsdp_count)
        for t in range(tensor_count)
    ]
    back = [(target, source) for source, target in there]

    split = units_split()
    head_width = 2 * head_dim
    query_cols = heads * head_dim
    near_cols = query_cols + head_width + 128

    outgoing = lax.dynamic_index_in_dim(hidden_in, leaving, 0, keepdims=False)
    own_in = lax.ppermute(outgoing, ("fsdp", "tp"), there)
    small = jnp.concatenate(
        [
            query_weight,
            lax.dynamic_slice_in_dim(keyval_weight, head_pair * head_width, head_width, axis=1),
            jnp.pad(norm_gains.T, ((0, 0), (0, 128 - norm_gains.shape[0]))),
            output_weight.T,
        ],
        axis=1,
    )
    lengths_now = jnp.stack([seq_lengths[s] for s in seq_now])
    info = jnp.concatenate([lengths_now, jnp.stack([offset, parity])]).astype(jnp.int32)
    positions_now = jnp.stack(
        [lax.dynamic_index_in_dim(positions, s, 0, keepdims=False) for s in seq_now]
    )
    lane = jnp.arange(head_dim)
    frequency = 1.0 / ROPE_BASE ** ((lane % (head_dim // 2)).astype(WIDE) * 2.0 / head_dim)
    angles = positions_now.astype(WIDE)[..., None] * frequency
    cosine = jnp.cos(angles)
    sine = jnp.sin(angles) * jnp.where(lane < head_dim // 2, -1.0, 1.0)
    pick_info = jnp.stack(slot_now + [s ^ tensor_rank for s in slot_now]).astype(jnp.int32)
    units = gate_weight.shape[1]
    units_pad = -(-units // 256) * 256
    widen = lambda w: jnp.pad(w, ((0, 0), (0, units_pad - units)))
    shards = [widen(w) for w in (down_weight.T, gate_weight, up_weight)]
    if split:
        half_units = units_pad // 2
        cut = lambda w, c: lax.dynamic_slice_in_dim(w, c * half_units, half_units, axis=1)

        def in_order(own, other):
            return jnp.stack(
                [jnp.where(ctx_rank == 0, own, other), jnp.where(ctx_rank == 0, other, own)]
            )

        def all_rows(both, *earlier):
            full = lax.all_gather(after(both, *earlier), "fsdp", axis=0, tiled=False)
            return full.reshape(-1, both.shape[-1])

        first_units = half_units // 2 // 256 * 256
        first_cols = 3 * first_units

        def in_parts(c):
            halves = [cut(w, c) for w in shards]
            return jnp.concatenate(
                [w[:, :first_units] for w in halves] + [w[:, first_units:] for w in halves], axis=1
            )

        leaving_units, own_units = in_parts(1 - ctx_rank), in_parts(ctx_rank)
        slot_pick = lax.dynamic_index_in_dim(cotangent, tensor_rank, 0, keepdims=False)
        small = after(small, outgoing, leaving_units)
        small_both = in_order(small, from_partner(small, "ctx", 1))
        arriving_units = from_partner(after(leaving_units, small_both), "ctx", 1)
        other_own = from_partner(after(slot_pick, arriving_units), "ctx", 1)
        both_a = in_order(own_units[:, :first_cols], arriving_units[:, :first_cols])
        both_b = in_order(own_units[:, first_cols:], arriving_units[:, first_cols:])
    else:
        all_rows = lambda shard, *earlier: lax.all_gather(
            shard, ("fsdp", "ctx"), axis=0, tiled=True
        )
        small_both, unit_both, half_units = small, jnp.concatenate(shards, axis=1), units_pad
    far_in = from_partner(own_in, "tp", 2)
    near_in = from_partner(own_in, "tp", 1)
    ready = (cosine, sine, info, pick_info, own_units, slot_pick) if split else (cosine, sine, info)
    cross_in = from_partner(after(far_in, *ready), "tp", 1)
    grad_slots = [lax.dynamic_index_in_dim(cotangent, s, 0, keepdims=False) for s in slot_now]

    near_full = all_rows(small_both, own_in)
    if split:
        units_a = all_rows(both_a, cross_in)
        units_b = all_rows(both_b, cross_in)
    else:
        down_full = all_rows(unit_both[..., :half_units], cross_in)
        gate_up_full = all_rows(unit_both[..., half_units:], cross_in)
    project_full = near_full[:, : query_cols + head_width]
    output_full = near_full[:, near_cols:]
    bias_head = lax.dynamic_slice_in_dim(bias_keyval, head_pair * 2, 2, axis=0)
    bias_row = jnp.concatenate([bias_query.reshape(1, -1), bias_head.reshape(1, -1)], axis=1).astype(WIDE)
    normed_one, query_rot, key_own, value_own = project(
        (own_in, near_in, far_in, cross_in),
        near_full,
        bias_row,
        after(cosine, other_own, both_a, both_b, info, pick_info) if split else cosine,
        sine,
        heads,
        head_dim,
    )
    gains_now = near_full[:, query_cols + head_width : near_cols][:, :2].astype(WIDE).T
    if split:
        key_past, value_past = lax.ppermute((key_own, value_own), "ctx", [(0, 1)])
        other_far = from_partner(other_own, "tp", 2)
        other_near = from_partner(after(other_own, key_past), "tp", 1)
        other_cross = from_partner(after(other_far, key_past), "tp", 1)
        other_rows = (other_own, other_near, other_far, other_cross)
        key_past = after(key_past, other_far)
    else:
        key_past = lax.all_gather(key_own, "ctx", axis=1, tiled=True)
        value_past = lax.all_gather(value_own, "ctx", axis=1, tiled=True)
    attend = lambda first, *held: attend_forward(
        info, query_rot, *held, key_own, value_own, output_full, heads, head_dim, scale, first, 2
    )
    in_share = own_in.astype(WIDE)

    mixed_far, lse_far, *attn_far = attend(2, key_past, value_past)
    attn_wide = collect_far(attn_far[0], attn_far[1])
    attn_got = from_partner(attn_wide, "tp", 2)
    mixed_near, lse_near, *attn_near = attend(0, after(key_past, attn_wide), value_past)
    attn_core = from_partner(attn_near[1], "tp", 1)
    middle_share = (
        in_share
        + attn_near[0].astype(WIDE)
        + attn_core.astype(WIDE)
        + attn_got.astype(WIDE)
    )
    inv_two = lax.rsqrt(jnp.mean(middle_share * middle_share, axis=-1, keepdims=True) + EPS)
    normed_share = (middle_share * inv_two * gains_now[1]).astype(LOW)
    half_len = local_len // 2

    if split:
        grad_hidden, grad_rows = chosen_rows(
            pick_info,
            after(cotangent, normed_share),
            other_rows,
            units_a,
            0,
            3,
        )
    else:
        grad_hidden, grad_rows = stack_rows([(g,) for g in grad_slots], down_full, 0, 1)

    def spread_all(own):
        far = from_partner(own, "tp", 2)
        near = from_partner(own, "tp", 1)
        if not split:
            return (own, near, far, from_partner(far, "tp", 1))
        side = from_partner(own, "ctx", 1)
        held = after(far, grad_hidden), after(side, grad_hidden)
        across = from_partner(held[0][:half_len], "ctx", 1), from_partner(held[1][half_len:], "tp", 2)
        cores = [from_partner(v, "tp", 1) for v in (*held, *across)]
        return (own, near, far, cores[0], side, cores[1], *across, *cores[2:])

    def in_slots(rows):
        if not split:
            return [(row,) for row in rows]
        return [(row,) for row in rows[:6]] + [rows[6:8], rows[8:]]

    normed_slots = in_slots(spread_all(normed_share))
    if split:
        gate_lin, normed_two = stack_rows(normed_slots, units_a, 1, 3)
        hidden_a, gate_a, up_a = hidden_units(normed_two, units_a, 2, 3, gate_lin, grad_hidden)
        grad_a = first_grads(grad_rows, normed_two, hidden_a, gate_a, up_a)
        hidden_b, gate_b, up_b = full_units(after(normed_two, grad_a), grad_rows, units_b)
    else:
        gate_lin, normed_two = stack_rows(normed_slots, gate_up_full, 0, 2)
        hidden_act, grad_gate, grad_up = hidden_units(
            normed_two, gate_up_full, 1, 2, gate_lin, grad_hidden
        )

    def collect_all(lefts, weights, *earlier):
        lefts = list(lefts)
        lefts[0] = after(lefts[0], *earlier)
        last = back_rows(lefts, weights, 2, 2, local_len)
        got = [from_partner(collect_far(last[0], last[1]), "tp", 2)]
        first = back_rows(lefts, weights, 0, 2, local_len)
        got.append(from_partner(first[1], "tp", 1))

        def finish():
            return sum((v.astype(WIDE) for v in got), first[0].astype(WIDE))

        return first[0], finish

    if split:
        grad_two_share, down_b, up_grad_b = collect_back(
            (gate_a, up_a),
            (gate_b, up_b),
            units_a,
            units_b,
            grad_rows,
            normed_two,
            hidden_b,
            local_len,
        )
        grad_middle, gain_two, gate_grad_b, grad_branch, *mlp = spread_branch(
            grad_two_share,
            middle_share,
            grad_slots[0],
            gains_now[1:2],
            hidden_a,
            hidden_b,
            units_a,
            units_b,
            normed_two,
            gate_b,
        )
        mlp_own, mlp_far, mlp_side = mlp
        grad_branch = grad_branch.reshape(token_count, model_width)
    else:
        first_back, finish_back = collect_all(
            (grad_gate, grad_up), ((gate_up_full, 0, 2), (gate_up_full, 1, 2))
        )
        down_grad = contract_rows(after(grad_rows, first_back), hidden_act, LOW)
        gate_grad = contract_rows(normed_two, after(grad_gate, down_grad), LOW)
        grad_two_share = finish_back()
        grad_norm_two, gain_two = norm_backward(
            middle_share, inv_two, gains_now[1], grad_two_share
        )
        grad_middle = grad_slots[0].astype(WIDE) + grad_norm_two
        branch_own = grad_middle.astype(LOW)
        branch_far = from_partner(branch_own, "tp", 2)
        branch_near = from_partner(branch_own, "tp", 1)
        branch_cross = from_partner(branch_far, "tp", 1)
        grad_branch = jnp.concatenate([branch_own, branch_near, branch_far, branch_cross], axis=0)
        up_grad = contract_rows(normed_two, after(grad_up, branch_own), LOW)

    grad_mixed = product(grad_branch, output_full, LOW)
    mixed_flat = jnp.concatenate([mixed_near, mixed_far], axis=0).reshape(token_count, query_cols)
    lse = jnp.concatenate([lse_near, lse_far], axis=0)
    attend_args = (
        info,
        query_rot,
        key_past,
        value_past,
        key_own,
        value_own,
        grad_mixed.reshape(seq_grp, local_len, query_cols),
        lse,
        cosine,
        sine,
        heads,
        head_dim,
        scale,
    )
    if split:
        line_grad, output_grad, block_share = attend_exchange(
            *attend_args,
            grad_branch,
            mixed_flat,
            (mlp_far, mlp_side, mlp_own),
            middle_share,
        )
        line_grad = line_grad.reshape(token_count, -1)
    else:
        grad_query, mine_past, mine_own, other_past, other_own = attend_backward(*attend_args)
        swap = lambda value: jnp.stack([value[r ^ 1] for r in range(seq_grp)])
        got_past, got_own = from_partner((other_past, other_own), "tp", 1)
        past_sum = mine_past + swap(got_past)
        own_sum = mine_own + swap(got_own)
        own_sum = own_sum + lax.psum_scatter(past_sum, "ctx", scatter_dimension=1, tiled=True)
        half_lanes = head_dim // 2
        turned = own_sum * cosine - jnp.roll(own_sum, half_lanes, axis=-1) * sine
        own_grad = jnp.where(parity == 0, turned, own_sum).astype(LOW).reshape(token_count, head_dim)
        line_grad = jnp.concatenate([grad_query.reshape(token_count, query_cols), own_grad], axis=1)
    own_weight = lax.dynamic_slice_in_dim(
        project_full, query_cols + parity * head_dim, head_dim, axis=1
    )
    back_full = jnp.concatenate([project_full[:, :query_cols], own_weight], axis=1)
    def scatter_units(grad):
        if not split:
            return scatter_sum(grad, ctx_rank, LOW)
        return lax.psum_scatter(grad, "fsdp", scatter_dimension=0, tiled=True)

    unit_grads = (grad_a, down_b, up_grad_b, gate_grad_b) if split else (down_grad, gate_grad, up_grad)
    unit_sums = [scatter_units(unit_grads[0])]
    if split:
        unit_sums += [scatter_units(after(g, unit_sums[0])) for g in unit_grads[1:3]]
        unit_sums += [scatter_units(after(unit_grads[3], unit_sums[0]))]
    else:
        unit_sums += [scatter_units(g) for g in unit_grads[1:]]

    normed_flat = normed_one.reshape(token_count, model_width)
    if split:
        input_share, gain_grad, attn_grad, bias_grad, block_home = finish_rows(
            line_grad,
            after(back_full, *unit_sums),
            own_in,
            grad_middle,
            gains_now[0:1],
            gain_two,
            normed_flat,
            block_share,
        )
        attn_grad = jnp.concatenate([attn_grad, output_grad], axis=1)
    else:
        half = token_count // 2
        line_far = contract_cols(line_grad[half:], back_full, LOW).reshape(2, local_len, model_width)
        line_near = contract_cols(line_grad[:half], back_full, LOW).reshape(2, local_len, model_width)
        line_wide = collect_far(line_far[0], line_far[1])
        line_got = from_partner(line_wide, "tp", 2)
        line_core = from_partner(line_near[1], "tp", 1)
        first_mlp, finish_mlp = collect_all((hidden_act,), ((down_full, 0, 1),), up_grad, branch_far)
        block_share = (middle_share + finish_mlp()).astype(LOW)
        grad_one_share = line_near[0].astype(WIDE) + line_core.astype(WIDE) + line_got.astype(WIDE)
        inv_one = lax.rsqrt(jnp.mean(in_share * in_share, axis=-1, keepdims=True) + EPS)
        grad_norm_one, gain_one = norm_backward(in_share, inv_one, gains_now[0], grad_one_share)
        input_share = (grad_middle + grad_norm_one).astype(LOW)
        attn_grad = jnp.concatenate(
            [contract_rows(normed_flat, line_grad, LOW), contract_rows(grad_branch, mixed_flat, LOW)],
            axis=1,
        )
        bias_grad = jnp.sum(line_grad.astype(WIDE), axis=0)

    shard_count = fsdp_count * ctx_count
    share = head_dim // shard_count
    if not split:
        gain_grad = jnp.concatenate([gain_one, gain_two], axis=0)
        gain_grad = gain_grad + from_partner(gain_grad, "tp", 1)
        gain_grad = gain_grad + from_partner(gain_grad, "tp", 2)
    bias_cols = jnp.transpose(bias_grad.reshape(heads + 1, shard_count, share), (1, 2, 0))
    bias_cols = jnp.pad(bias_cols, ((0, 0), (0, (model_width - head_dim) // shard_count), (0, 0)))
    tiny = jnp.concatenate([gain_grad.T, bias_cols.reshape(model_width, heads + 1)], axis=1)
    tiny = jnp.pad(tiny, ((0, 0), (0, 128 - tiny.shape[1]))).astype(LOW)
    attn_grad = jnp.concatenate([attn_grad, tiny], axis=1)
    if split:
        attn_blocks = attn_grad.reshape(fsdp_count, ctx_count, -1, attn_grad.shape[1])
        kept, sent = scatter_ctx(attn_blocks, ctx_rank)
        attn_held = (kept.astype(WIDE) + from_partner(sent, "ctx", 1).astype(WIDE)).astype(LOW)
        attn_held = attn_held.reshape(-1, attn_grad.shape[1])
        attn_end = lax.psum_scatter(after(attn_held, *unit_sums), "fsdp", scatter_dimension=0, tiled=True)
    else:
        attn_end = scatter_sum(attn_grad, ctx_rank, LOW, *unit_sums)

    home_order = jnp.stack(home_now).astype(jnp.int32)

    def leave(share):
        return lax.ppermute(share, ("fsdp", "tp"), back)

    def arrive(own, order):
        far = from_partner(own, "tp", 2)
        near = from_partner(own, "tp", 1)
        return place_rows((own, near, far, from_partner(far, "tp", 1)), order)

    input_home = leave(input_share)
    if not split:
        block_home = leave(block_share)
    block_out = arrive(block_home, home_order)
    if split:

        def unit_end(total, *earlier):
            kept, sent = scatter_ctx(total.reshape(1, ctx_count, -1, total.shape[1]), ctx_rank)
            return kept[0], from_partner(after(sent[0], *earlier), "ctx", 1)

        own_a, got_a = unit_end(unit_sums[0], grad_branch)
        ends = [unit_end(t, line_grad) for t in unit_sums[1:]]
        input_home = after(input_home, attn_held)
        home_order = after(home_order, got_a, *[end[1] for end in ends])
    input_grad = arrive(input_home, home_order)

    small_at = query_cols + head_dim + query_cols
    tiny_grad = attn_end[:, small_at:].astype(WIDE)

    if split:

        def joined(part, end):
            cols = slice(part * first_units, (part + 1) * first_units)
            own = jnp.concatenate([own_a[:, cols], end[0]], axis=1)
            got = jnp.concatenate([got_a[:, cols], end[1]], axis=1)
            first, second = jnp.where(ctx_rank == 0, own, got), jnp.where(ctx_rank == 0, got, own)
            return jnp.concatenate([first, second], axis=1)[:, :units].astype(WIDE)

        down_end, gate_end, up_end = joined(0, ends[0]), joined(1, ends[2]), joined(2, ends[1])
    else:
        down_end, gate_end, up_end = (t[:, :units].astype(WIDE) for t in unit_sums)
    return (
        block_out,
        input_grad,
        attn_end[:, :query_cols].astype(WIDE),
        attn_end[:, query_cols : query_cols + head_dim].astype(WIDE),
        attn_end[:, query_cols + head_dim : small_at].astype(WIDE).T,
        tiny_grad[:, :2].T,
        tiny_grad[:share, 2 : 2 + heads].T,
        tiny_grad[:share, 2 + heads : 3 + heads].T,
        gate_end,
        up_end,
        down_end.T,
    )


def solution(mesh):
    placed = (
        P("fsdp", "ctx", None),
        P("fsdp", "ctx", None),
        P(),
        P(None, "ctx"),
        P(),
        P(("fsdp", "ctx"), "tp"),
        P(("fsdp", "ctx"), None),
        P("tp", ("fsdp", "ctx")),
        P(None, ("fsdp", "ctx")),
        P("tp", None),
        P(),
        P(("fsdp", "ctx"), "tp"),
        P(("fsdp", "ctx"), "tp"),
        P("tp", ("fsdp", "ctx")),
    )
    return jax.shard_map(
        local,
        mesh=mesh,
        in_specs=placed,
        out_specs=(
            P("fsdp", "ctx", None),
            P("fsdp", "ctx", None),
            P(("fsdp", "ctx"), "tp"),
            P(("fsdp", "ctx"), "tp"),
            P("tp", ("fsdp", "ctx")),
            P(None, ("fsdp", "ctx")),
            P("tp", ("fsdp", "ctx")),
            P("tp", ("fsdp", "ctx")),
            P(("fsdp", "ctx"), "tp"),
            P(("fsdp", "ctx"), "tp"),
            P("tp", ("fsdp", "ctx")),
        ),
        check_vma=False,
    )
```

```python
import functools
import math

import jax
import jax.numpy as jnp
from jax import lax
from jax.experimental import pallas as pl
from jax.experimental.pallas import tpu as pltpu
from jax.sharding import PartitionSpec as P

EPS = 1e-06
ROPE_BASE = 10000.0
NEG_FILL = -1e30
LOW = jnp.bfloat16
WIDE = jnp.float32
DEAL_SHIFT = (0, 2, 1, 3)


def from_partner(value, axis, apart):
    pairs = [(source, source ^ apart) for source in range(lax.axis_size(axis))]
    return lax.ppermute(value, axis, pairs)


def product(left_side, right_side, kind=WIDE):
    return jnp.dot(left_side, right_side, preferred_element_type=WIDE).astype(kind)


def contract_rows(left_side, right_side, kind=WIDE):
    return lax.dot_general(
        left_side, right_side, (((0,), (0,)), ((), ())), preferred_element_type=WIDE
    ).astype(kind)


def contract_cols(left_side, right_side, kind=WIDE):
    return lax.dot_general(
        left_side, right_side, (((1,), (1,)), ((), ())), preferred_element_type=WIDE
    ).astype(kind)


def norm_backward(values, scale_inv, gain_row, upstream):
    scaled = gain_row * upstream
    inner_mean = jnp.mean(values * scaled, axis=-1, keepdims=True)
    grad_in = scale_inv * scaled - values * (scale_inv * scale_inv * scale_inv) * inner_mean
    gain_grad = jnp.sum(upstream * values * scale_inv, axis=0, keepdims=True)
    return (grad_in, gain_grad)


def after(value, *earlier):
    return lax.optimization_barrier((value, *earlier))[0]


def collect_far(far_part, cross_part):
    wide = far_part.astype(WIDE) + from_partner(cross_part, "tp", 1).astype(WIDE)
    return wide.astype(LOW)


def units_split():
    return lax.axis_size("ctx") == 2


def all_rows(shard):
    return lax.all_gather(shard, "fsdp", axis=0, tiled=True)


def scatter_ctx(blocks, ctx_rank):
    kept = lax.dynamic_index_in_dim(blocks, ctx_rank, 1, keepdims=False)
    sent = lax.dynamic_index_in_dim(blocks, 1 - ctx_rank, 1, keepdims=False)
    return kept, sent


def scatter_sum(grad, ctx_rank, kind, *earlier):
    fsdp_count, ctx_count = lax.axis_size("fsdp"), lax.axis_size("ctx")
    rows, cols = grad.shape
    blocks = grad.reshape(fsdp_count, ctx_count, rows // (fsdp_count * ctx_count), cols)
    if ctx_count == 2:
        kept, sent = scatter_ctx(blocks, ctx_rank)
        got = from_partner(sent, "ctx", 1)
        held = (after(kept, *earlier).astype(WIDE) + got.astype(WIDE)).astype(kind)
    else:
        swapped = jnp.swapaxes(blocks, 0, 1).reshape(rows, cols)
        held = lax.psum_scatter(swapped, "ctx", scatter_dimension=0, tiled=True)
    held = held.reshape(rows // ctx_count, cols)
    return lax.psum_scatter(held, "fsdp", scatter_dimension=0, tiled=True)


def estimate(flops, moved, transcendentals=0):
    return pl.CostEstimate(flops=flops, bytes_accessed=moved, transcendentals=transcendentals)


def part_spec(rows, cols, part):
    return pl.BlockSpec((rows, cols), lambda *_: (0, part), pipeline_mode=pl.Buffered(1))


def whole_spec(*shape, once=False):
    mode = {"pipeline_mode": pl.Buffered(1)} if once else {}
    return pl.BlockSpec(shape, lambda *_: (0,) * len(shape), **mode)


def rows_kernel(groups, *refs):
    slot = pl.program_id(0)
    weight, lin, stacked = refs[-3:]

    def run(pieces):
        start = 0
        for piece in pieces:
            stacked[start : start + piece.shape[0]] = piece[...]
            start += piece.shape[0]
        lin[...] = jnp.dot(stacked[...], weight[...], preferred_element_type=WIDE).astype(LOW)

    first = 0
    for r, pieces in enumerate(groups):
        pl.when(slot == r)(functools.partial(run, refs[first : first + pieces]))
        first += pieces


def stack_rows(slots, weight, part, parts):
    groups = [len(s) for s in slots]
    rows = [piece for s in slots for piece in s]
    width, length = rows[0].shape[1], sum(piece.shape[0] for piece in slots[0])
    count, cols = len(slots), weight.shape[1] // parts
    return pl.pallas_call(
        functools.partial(rows_kernel, groups),
        grid=(count,),
        in_specs=[whole_spec(*piece.shape, once=True) for piece in rows]
        + [part_spec(width, cols, part)],
        out_specs=[
            pl.BlockSpec((length, cols), lambda s: (s, 0)),
            pl.BlockSpec((length, width), lambda s: (s, 0)),
        ],
        out_shape=[
            jax.ShapeDtypeStruct((count * length, cols), LOW),
            jax.ShapeDtypeStruct((count * length, width), LOW),
        ],
        compiler_params=pltpu.CompilerParams(vmem_limit_bytes=60 << 20),
        cost_estimate=estimate(
            2 * count * length * width * cols, 2 * (count * length * (2 * width + cols) + width * cols)
        ),
    )(*rows, weight)


def units_kernel(h, up, gate, grad, hid, grad_gate, grad_up):
    up_lin = jnp.dot(h[...], up[...], preferred_element_type=WIDE)
    gate_lin = gate[...].astype(WIDE)
    grad_hidden = grad[...].astype(WIDE)
    sigmoid = 1.0 / (1.0 + jnp.exp(-gate_lin))
    silu = gate_lin * sigmoid
    hid[...] = (silu * up_lin).astype(LOW)
    grad_gate[...] = (grad_hidden * up_lin * sigmoid * (1.0 + gate_lin * (1.0 - sigmoid))).astype(LOW)
    grad_up[...] = (grad_hidden * silu).astype(LOW)


def hidden_units(h, up, part, parts, gate_lin, grad_hidden):
    tokens, width = h.shape
    cols = up.shape[1] // parts
    step = math.gcd(512, tokens)
    by_row = lambda n: pl.BlockSpec((step, n), lambda i: (i, 0))
    return pl.pallas_call(
        units_kernel,
        grid=(tokens // step,),
        in_specs=[by_row(width), part_spec(width, cols, part), by_row(cols), by_row(cols)],
        out_specs=[by_row(cols)] * 3,
        out_shape=[jax.ShapeDtypeStruct((tokens, cols), LOW)] * 3,
        compiler_params=pltpu.CompilerParams(vmem_limit_bytes=60 << 20),
        cost_estimate=estimate(
            2 * tokens * width * cols, 2 * (tokens * width + width * cols + 5 * tokens * cols)
        ),
    )(h, up, gate_lin, grad_hidden)


def back_kernel(terms, *refs):
    lefts, weights, outs = refs[:terms], refs[terms : 2 * terms], refs[2 * terms :]
    total = None
    for left, weight in zip(lefts, weights):
        term = dot_cols(left[...], weight[...])
        total = term if total is None else total + term
    for i, out in enumerate(outs):

        @pl.when(pl.program_id(0) == i)
        def _():
            out[...] = total.astype(LOW)


def back_rows(lefts, weights, first_slot, slots, length):
    width = weights[0][0].shape[0]
    depth = sum(left.shape[1] for left in lefts)
    return pl.pallas_call(
        functools.partial(back_kernel, len(lefts)),
        grid=(slots,),
        in_specs=[
            pl.BlockSpec((length, left.shape[1]), lambda s: (first_slot + s, 0)) for left in lefts
        ]
        + [part_spec(width, w.shape[1] // parts, part) for w, part, parts in weights],
        out_specs=[whole_spec(length, width)] * slots,
        out_shape=[jax.ShapeDtypeStruct((length, width), LOW)] * slots,
        compiler_params=pltpu.CompilerParams(vmem_limit_bytes=60 << 20),
        cost_estimate=estimate(
            2 * slots * length * width * depth,
            2 * (slots * length * (width + depth) + width * depth),
        ),
    )(*lefts, *[w for w, _, _ in weights])


def chosen_kernel(near, count, info, cotangent, *refs):
    slot = pl.program_id(0)
    others, (weight, lin, stacked) = refs[:count], refs[count:]

    @pl.when(slot < near)
    def _():
        stacked[...] = cotangent[0]

    for k, other in enumerate(others):

        @pl.when((slot >= near) & (info[slot] == k))
        def _():
            stacked[...] = other[...]

    lin[...] = jnp.dot(stacked[...], weight[...], preferred_element_type=WIDE).astype(LOW)


def chosen_rows(info, cotangent, others, weight, part, parts):
    near, length, width = cotangent.shape
    slots, cols = near + len(others), weight.shape[1] // parts
    held = lambda rows, n, at: pl.BlockSpec(
        (rows, n), lambda s, info: (0, at), pipeline_mode=pl.Buffered(1)
    )
    return pl.pallas_call(
        functools.partial(chosen_kernel, near, len(others)),
        grid_spec=pltpu.PrefetchScalarGridSpec(
            num_scalar_prefetch=1,
            grid=(slots,),
            in_specs=[
                pl.BlockSpec((1, length, width), lambda s, info: (info[jnp.minimum(s, near - 1)], 0, 0))
            ]
            + [held(length, width, 0)] * len(others)
            + [held(width, cols, part)],
            out_specs=[
                pl.BlockSpec((length, cols), lambda s, info: (s, 0)),
                pl.BlockSpec((length, width), lambda s, info: (s, 0)),
            ],
        ),
        out_shape=[
            jax.ShapeDtypeStruct((slots * length, cols), LOW),
            jax.ShapeDtypeStruct((slots * length, width), LOW),
        ],
        compiler_params=pltpu.CompilerParams(vmem_limit_bytes=60 << 20),
        cost_estimate=estimate(
            2 * slots * length * width * cols, 2 * (slots * length * (2 * width + cols) + width * cols)
        ),
    )(info, cotangent, *others, weight)


def full_units_kernel(h, g, down, gate, up, hid, grad_gate, grad_up):
    gate_lin = jnp.dot(h[...], gate[...], preferred_element_type=WIDE)
    up_lin = jnp.dot(h[...], up[...], preferred_element_type=WIDE)
    grad_hidden = jnp.dot(g[...], down[...], preferred_element_type=WIDE)
    sigmoid = 1.0 / (1.0 + jnp.exp(-gate_lin))
    silu = gate_lin * sigmoid
    hid[...] = (silu * up_lin).astype(LOW)
    grad_gate[...] = (grad_hidden * up_lin * sigmoid * (1.0 + gate_lin * (1.0 - sigmoid))).astype(LOW)
    grad_up[...] = (grad_hidden * silu).astype(LOW)


def full_units(h, g, weight):
    tokens, width = h.shape
    cols = weight.shape[1] // 3
    step = math.gcd(512, tokens)
    by_row = lambda n: pl.BlockSpec((step, n), lambda i: (i, 0))
    return pl.pallas_call(
        full_units_kernel,
        grid=(tokens // step,),
        in_specs=[by_row(width)] * 2 + [part_spec(width, cols, i) for i in range(3)],
        out_specs=[by_row(cols)] * 3,
        out_shape=[jax.ShapeDtypeStruct((tokens, cols), LOW)] * 3,
        compiler_params=pltpu.CompilerParams(vmem_limit_bytes=60 << 20),
        cost_estimate=estimate(
            6 * tokens * width * cols, 2 * (2 * tokens * width + 3 * width * cols + 3 * tokens * cols)
        ),
    )(h, g, weight, weight, weight)


def first_grads_kernel(g, h, hid, gate, up, out):
    part = pl.program_id(0)
    for i, (left, right) in enumerate(((g, hid), (h, gate), (h, up))):

        @pl.when(part == i)
        def _():
            out[...] = dot_rows(left[...], right[...]).astype(LOW)


def first_grads(grad_rows, rows, hid, grad_gate, grad_up):
    tokens, width = rows.shape
    cols, tile = hid.shape[1], 256
    tiles = width // tile
    return pl.pallas_call(
        first_grads_kernel,
        grid=(3, tiles),
        in_specs=[
            pl.BlockSpec((tokens, tile), lambda p, i: (0, jnp.where(p == 0, i, tiles - 1))),
            pl.BlockSpec((tokens, tile), lambda p, i: (0, jnp.where(p == 0, 0, i))),
        ]
        + [whole_spec(tokens, cols, once=True)] * 3,
        out_specs=pl.BlockSpec((tile, cols), lambda p, i: (i, p)),
        out_shape=jax.ShapeDtypeStruct((width, 3 * cols), LOW),
        compiler_params=pltpu.CompilerParams(vmem_limit_bytes=60 << 20),
        cost_estimate=estimate(6 * tokens * width * cols, 6 * tokens * cols + 6 * width * cols),
    )(grad_rows, rows, hid, grad_gate, grad_up)


MESH_ID = pl.DeviceIdType.MESH


def meet(partners):
    barrier = pltpu.get_barrier_semaphore()
    for partner in partners:
        pl.semaphore_signal(barrier, inc=1, device_id=partner, device_id_type=MESH_ID)
    pl.semaphore_wait(barrier, len(partners))


def partners_of():
    tensor_rank, ctx_rank = lax.axis_index("tp"), lax.axis_index("ctx")
    return {"tp": tensor_rank ^ 1}, {"tp": tensor_rank ^ 2}, {"ctx": ctx_rank ^ 1}


def collect_kernel(
    slots, tiles, gate_a, up_a, gate_b, up_b, w_gate_a, w_up_a, w_gate_b, w_up_b, left, right, hid, up, total,
    down_out, up_out, parts, sent, core_in, across_in, last_in, held, send, recv, load
):
    step = pl.program_id(0)
    steps = pl.num_programs(0)
    core, far, side = partners_of()
    half = total.shape[0] // 2
    remote = remote_copy(send, recv)
    cores = [remote(sent.at[k % 2], core_in.at[k], k, core) for k in range(4)]
    across = [
        remote(parts.at[3, pl.ds(0, half)], across_in.at[0], 4, far),
        remote(parts.at[3, pl.ds(half, half)], across_in.at[1], 5, side),
    ]
    lasts = [
        remote(parts.at[1], last_in.at[0], 6, far),
        remote(parts.at[2, pl.ds(half, half)], last_in.at[1, pl.ds(half, half)], 7, side),
        remote(parts.at[2, pl.ds(0, half)], last_in.at[1, pl.ds(0, half)], 8, side),
    ]
    loading = [
        pltpu.make_async_copy(source, held.at[i], load.at[i]) for i, source in enumerate((hid, up))
    ]

    @pl.when(step == 0)
    def _():
        for copy in loading:
            copy.start()
        meet((core, far, side))

    for k in (2, 3):
        pl.when(step == 2 * k)(cores[k - 2].wait_send)

    @pl.when(step < slots)
    def _():
        part = (
            dot_cols(gate_a[...], w_gate_a[...])
            + dot_cols(up_a[...], w_up_a[...])
            + dot_cols(gate_b[...], w_gate_b[...])
            + dot_cols(up_b[...], w_up_b[...])
        )

        @pl.when(step == slots - 1)
        def _():
            total[...] = part

        for k in range(4):

            @pl.when(step == 2 * k)
            def _():
                sent[k % 2] = part.astype(LOW)
                cores[k].start()

            if k < 3:

                @pl.when(step == 2 * k + 1)
                def _():
                    cores[k].wait_recv()
                    parts[3 - k] = (part + core_in[k].astype(WIDE)).astype(LOW)

    def add(slot, rows, value):
        parts[slot, rows] = (parts[slot, rows].astype(WIDE) + value.astype(WIDE)).astype(LOW)

    low, high = pl.ds(0, half), pl.ds(half, half)

    @pl.when(step == 1)
    def _():
        for copy in across:
            copy.start()

    pl.when(step == 3)(lasts[1].start)

    @pl.when(step == 5)
    def _():
        across[1].wait_recv()
        add(1, high, across_in[1])
        lasts[0].start()
        across[0].wait_recv()
        add(2, low, across_in[0])
        lasts[2].start()

    @pl.when((step >= slots) & (step < slots + tiles))
    def _():
        pl.when(step == slots)(loading[0].wait)
        down_out[...] = dot_rows(left[...], held[0]).astype(LOW)

    @pl.when(step >= slots + tiles)
    def _():
        pl.when(step == slots + tiles)(loading[1].wait)
        up_out[...] = dot_rows(right[...], held[1]).astype(LOW)

    @pl.when(step == steps - 1)
    def _():
        cores[3].wait_recv()
        for copy in lasts:
            copy.wait_recv()
        total[...] += (
            core_in[3].astype(WIDE) + last_in[0].astype(WIDE) + last_in[1].astype(WIDE)
        )
        for copy in (*cores[2:], *across, *lasts):
            copy.wait_send()


def collect_back(first, second, weight_a, weight_b, grad_rows, rows, hid, length):
    tokens, cols_a = first[0].shape
    cols = second[0].shape[1]
    width = weight_a.shape[0]
    slots, tile = tokens // length, 256
    tiles = width // tile
    row = lambda n: pl.BlockSpec((length, n), lambda i: (jnp.maximum(slots - 1 - i, 0), 0))
    column = lambda i, start: jnp.clip(i - start, 0, tiles - 1)
    down_at, up_at = (lambda i: column(i, slots)), (lambda i: column(i, slots + tiles))
    return pl.pallas_call(
        functools.partial(collect_kernel, slots, tiles),
        grid=(slots + 2 * tiles,),
        in_specs=[row(cols_a), row(cols_a), row(cols), row(cols)]
        + [part_spec(width, cols_a, 1), part_spec(width, cols_a, 2)]
        + [part_spec(width, cols, 1), part_spec(width, cols, 2)]
        + [
            pl.BlockSpec((tokens, tile), lambda i: (0, down_at(i))),
            pl.BlockSpec((tokens, tile), lambda i: (0, up_at(i))),
            ANYWHERE,
            ANYWHERE,
        ],
        out_specs=[
            whole_spec(length, width, once=True),
            pl.BlockSpec((tile, cols), lambda i: (down_at(i), 0)),
            pl.BlockSpec((tile, cols), lambda i: (up_at(i), 0)),
        ],
        out_shape=[
            jax.ShapeDtypeStruct((length, width), WIDE),
            jax.ShapeDtypeStruct((width, cols), LOW),
            jax.ShapeDtypeStruct((width, cols), LOW),
        ],
        scratch_shapes=[
            pltpu.VMEM((4, length, width), LOW),
            pltpu.VMEM((2, length, width), LOW),
            pltpu.VMEM((4, length, width), LOW),
            pltpu.VMEM((2, length // 2, width), LOW),
            pltpu.VMEM((2, length, width), LOW),
            pltpu.VMEM((2, tokens, cols), LOW),
            pltpu.SemaphoreType.DMA((9,)),
            pltpu.SemaphoreType.DMA((9,)),
            pltpu.SemaphoreType.DMA((2,)),
        ],
        compiler_params=pltpu.CompilerParams(
            vmem_limit_bytes=63 << 20, collective_id=1, has_side_effects=True
        ),
        cost_estimate=estimate(6 * tokens * width * cols, 10 * tokens * cols),
    )(*first, *second, weight_a, weight_a, weight_b, weight_b, grad_rows, rows, hid, second[1])


def remote_copy(send, recv):
    def make(source, target, index, partner):
        return pltpu.make_async_remote_copy(
            source, target, send.at[index], recv.at[index], device_id=partner, device_id_type=MESH_ID
        )

    return make


def branch_kernel(
    slots, tiles, total, middle, own_grad, gain, hid_a, hid_b, w_a, w_b, turned, gate, grad_middle, gain_grad,
    gate_out, branch, mlp_own, mlp_far, mlp_side, own, parts, core_in, across_in, held, send, recv, load
):
    step = pl.program_id(0)
    core, far, side = partners_of()
    remote = remote_copy(send, recv)
    to_far = remote(own, branch.at[2], 0, far)
    to_near = remote(own, branch.at[1], 1, core)
    to_cross = remote(branch.at[2], branch.at[3], 2, core)
    keep = pltpu.make_async_copy(own, branch.at[0], load.at[0])
    loading = pltpu.make_async_copy(gate, held, load.at[1])
    cores = [remote(parts.at[7 - 2 * k], core_in.at[k], 3 + k, core) for k in range(4)]
    across = remote(parts.at[6], across_in, 7, side)
    stores = [
        pltpu.make_async_copy(parts.at[4], mlp_side, load.at[2]),
        pltpu.make_async_copy(parts.at[2], mlp_far, load.at[3]),
        pltpu.make_async_copy(parts.at[0], mlp_own, load.at[4]),
    ]

    @pl.when(step == 0)
    def _():
        loading.start()
        meet((core, far, side))
        values, upstream = middle[...], total[...]
        inverse = lax.rsqrt(jnp.mean(values * values, axis=-1, keepdims=True) + EPS)
        grad_in, gain_grad[...] = norm_backward(values, inverse, gain[...], upstream)
        grad_in = own_grad[...].astype(WIDE) + grad_in
        grad_middle[...] = grad_in
        own[...] = grad_in.astype(LOW)
        for copy in (to_far, to_near, keep):
            copy.start()

    @pl.when(step < slots)
    def _():
        part = dot_cols(hid_a[...], w_a[...]) + dot_cols(hid_b[...], w_b[...])
        parts[slots - 1 - step] = part.astype(LOW)

    for k in range(4):
        pl.when(step == 2 * k)(cores[k].start)

        def finish(k=k):
            slot = 6 - 2 * k
            cores[k].wait_recv()
            parts[slot] = (parts[slot].astype(WIDE) + core_in[k].astype(WIDE)).astype(LOW)
            if k == 0:
                across.start()
            if k == 1:
                stores[0].start()
            if k == 3:
                stores[2].start()

        pl.when(step == 2 * k + 1)(finish)

    @pl.when(step >= slots)
    def _():
        pl.when(step == slots)(loading.wait)
        gate_out[...] = dot_rows(turned[...], held[...]).astype(LOW)

    @pl.when(step == slots + tiles - 2)
    def _():
        to_far.wait_recv()
        to_cross.start()

    @pl.when(step == slots + tiles - 1)
    def _():
        to_near.wait_recv()
        to_cross.wait_recv()
        across.wait_recv()
        parts[2] = (parts[2].astype(WIDE) + across_in[...].astype(WIDE)).astype(LOW)
        stores[1].start()
        keep.wait()
        for copy in stores:
            copy.wait()
        for copy in (to_far, to_near, to_cross, *cores, across):
            copy.wait_send()


ANYWHERE = pl.BlockSpec(memory_space=pl.ANY)


def spread_branch(total, middle, own_grad, gain, hid_a, hid_b, weight_a, weight_b, rows, grad_gate):
    length, width = total.shape
    tokens, cols = grad_gate.shape
    slots, tile = tokens // length, 256
    tiles = width // tile
    once = whole_spec(length, width, once=True)
    column = lambda i: jnp.clip(i - slots, 0, tiles - 1)
    part = jax.ShapeDtypeStruct((length, width), LOW)
    return pl.pallas_call(
        functools.partial(branch_kernel, slots, tiles),
        grid=(slots + tiles,),
        in_specs=[
            once,
            once,
            once,
            whole_spec(1, width),
            pl.BlockSpec((length, hid_a.shape[1]), lambda i: (jnp.maximum(slots - 1 - i, 0), 0)),
            pl.BlockSpec((length, cols), lambda i: (jnp.maximum(slots - 1 - i, 0), 0)),
            part_spec(width, hid_a.shape[1], 0),
            part_spec(width, cols, 0),
            pl.BlockSpec((tokens, tile), lambda i: (0, column(i))),
            ANYWHERE,
        ],
        out_specs=[
            whole_spec(length, width, once=True),
            whole_spec(1, width),
            pl.BlockSpec((tile, cols), lambda i: (column(i), 0)),
        ]
        + [ANYWHERE] * 4,
        out_shape=[
            jax.ShapeDtypeStruct((length, width), WIDE),
            jax.ShapeDtypeStruct((1, width), WIDE),
            jax.ShapeDtypeStruct((width, cols), LOW),
            jax.ShapeDtypeStruct((4, length, width), LOW),
            part,
            part,
            part,
        ],
        scratch_shapes=[
            pltpu.VMEM((length, width), LOW),
            pltpu.VMEM((slots, length, width), LOW),
            pltpu.VMEM((4, length, width), LOW),
            pltpu.VMEM((length, width), LOW),
            pltpu.VMEM((tokens, cols), LOW),
            pltpu.SemaphoreType.DMA((8,)),
            pltpu.SemaphoreType.DMA((8,)),
            pltpu.SemaphoreType.DMA((5,)),
        ],
        compiler_params=pltpu.CompilerParams(
            vmem_limit_bytes=63 << 20, collective_id=2, has_side_effects=True
        ),
        cost_estimate=estimate(4 * tokens * width * cols, 10 * tokens * cols),
    )(total, middle, own_grad, gain, hid_a, hid_b, weight_a, weight_b, rows, grad_gate)


def line_kernel(
    slots, tiles, line, weight, own_in, grad_middle, gain, gain_two, rows_one, line_all, block, share,
    gain_grad, attn_out, bias_out, home, parts, core_in, far_in, total, gains, gains_in, send, recv, load
):
    step = pl.program_id(0)
    core, far, _ = partners_of()
    tensor_rank, group = lax.axis_index("tp"), lax.axis_index("fsdp")
    shift = (tensor_rank % 2) * 2 + tensor_rank // 2
    target = {"fsdp": (group + slots - shift) % slots}
    source = {"fsdp": (group + shift) % slots}
    stays = shift == 0
    remote = remote_copy(send, recv)
    cores = [remote(parts.at[3 - 2 * k], core_in.at[k], k, core) for k in range(2)]
    to_far = remote(parts.at[2], far_in, 2, far)
    leave = remote(block, home, 3, target)
    keep = pltpu.make_async_copy(block, home, load)
    cross = {"tp": tensor_rank ^ 3}
    gain_copies = [
        remote(gains, gains_in.at[i], 4 + i, partner) for i, partner in enumerate((core, far, cross))
    ]

    @pl.when(step == 0)
    def _():
        barrier = pltpu.get_barrier_semaphore()
        for partner in (core, far, cross):
            pl.semaphore_signal(barrier, inc=1, device_id=partner, device_id_type=MESH_ID)

        @pl.when(stays)
        def _():
            pl.semaphore_wait(barrier, 3)
            keep.start()

        @pl.when(jnp.logical_not(stays))
        def _():
            for partner in (target, source):
                pl.semaphore_signal(barrier, inc=1, device_id=partner, device_id_type=MESH_ID)
            pl.semaphore_wait(barrier, 5)
            leave.start()

    @pl.when(step < slots)
    def _():
        part = dot_cols(line[...], weight[...])
        parts[slots - 1 - step] = part.astype(LOW)

        @pl.when(step == slots - 1)
        def _():
            total[...] = part

    for k in range(2):
        pl.when(step == 2 * k)(cores[k].start)

    @pl.when(step == 1)
    def _():
        cores[0].wait_recv()
        parts[2] = (parts[2].astype(WIDE) + core_in[0].astype(WIDE)).astype(LOW)
        to_far.start()

    @pl.when(step == slots - 1)
    def _():
        bias_out[...] = jnp.sum(line_all[...].astype(WIDE), axis=0, keepdims=True)

    @pl.when(step >= slots)
    def _():
        attn_out[...] = dot_rows(rows_one[...], line_all[...]).astype(LOW)

    @pl.when(step == slots + tiles - 1)
    def _():
        cores[1].wait_recv()
        to_far.wait_recv()
        upstream = total[...] + core_in[1].astype(WIDE) + far_in[...].astype(WIDE)
        values = own_in[...].astype(WIDE)
        inverse = lax.rsqrt(jnp.mean(values * values, axis=-1, keepdims=True) + EPS)
        grad_in, gain_one = norm_backward(values, inverse, gain[...], upstream)
        gains[0:1] = gain_one
        gains[1:2] = gain_two[...]
        for copy in gain_copies:
            copy.start()
        share[...] = (grad_middle[...] + grad_in).astype(LOW)
        for copy in gain_copies:
            copy.wait_recv()
        gain_grad[...] = (gains[...] + gains_in[0]) + (gains_in[1] + gains_in[2])
        for copy in (*cores, to_far, *gain_copies):
            copy.wait_send()
        pl.when(stays)(keep.wait)

        @pl.when(jnp.logical_not(stays))
        def _():
            leave.wait_recv()
            leave.wait_send()


def finish_rows(line, weight, own_in, grad_middle, gain, gain_two, rows_one, block):
    length, width = own_in.shape
    near_tokens, line_cols = line.shape
    slots, tile = near_tokens // length, 256
    tiles = width // tile
    once = whole_spec(length, width, once=True)
    column = lambda i: jnp.clip(i - slots, 0, tiles - 1)
    by_column = lambda n: pl.BlockSpec((n, tile), lambda i: (0, column(i)))
    attn_cols = line_cols
    return pl.pallas_call(
        functools.partial(line_kernel, slots, tiles),
        grid=(slots + tiles,),
        in_specs=[
            pl.BlockSpec((length, line_cols), lambda i: (jnp.maximum(slots - 1 - i, 0), 0)),
            whole_spec(width, line_cols, once=True),
            once,
            once,
            whole_spec(1, width),
            whole_spec(1, width),
            by_column(near_tokens),
            whole_spec(near_tokens, line_cols, once=True),
            ANYWHERE,
        ],
        out_specs=[
            whole_spec(length, width),
            whole_spec(2, width),
            pl.BlockSpec((tile, attn_cols), lambda i: (column(i), 0)),
            whole_spec(1, line_cols),
            ANYWHERE,
        ],
        out_shape=[
            jax.ShapeDtypeStruct((length, width), LOW),
            jax.ShapeDtypeStruct((2, width), WIDE),
            jax.ShapeDtypeStruct((width, attn_cols), LOW),
            jax.ShapeDtypeStruct((1, line_cols), WIDE),
            jax.ShapeDtypeStruct((length, width), LOW),
        ],
        scratch_shapes=[
            pltpu.VMEM((slots, length, width), LOW),
            pltpu.VMEM((2, length, width), LOW),
            pltpu.VMEM((length, width), LOW),
            pltpu.VMEM((length, width), WIDE),
            pltpu.VMEM((2, width), WIDE),
            pltpu.VMEM((3, 2, width), WIDE),
            pltpu.SemaphoreType.DMA((7,)),
            pltpu.SemaphoreType.DMA((7,)),
            pltpu.SemaphoreType.DMA,
        ],
        compiler_params=pltpu.CompilerParams(
            vmem_limit_bytes=63 << 20, collective_id=3, has_side_effects=True
        ),
        cost_estimate=estimate(2 * near_tokens * width * attn_cols, 10 * near_tokens * width),
    )(line, weight, own_in, grad_middle, gain, gain_two, rows_one, line, block)


def place_kernel(count, info, *refs):
    out = refs[count]
    for r in range(count):

        @pl.when(pl.program_id(0) == r)
        def _():
            out[0] = refs[r][...]


def place_rows(rows, order):
    length, width = rows[0].shape
    count = len(rows)
    held = pl.BlockSpec((length, width), lambda s, info: (0, 0), pipeline_mode=pl.Buffered(1))
    return pl.pallas_call(
        functools.partial(place_kernel, count),
        grid_spec=pltpu.PrefetchScalarGridSpec(
            num_scalar_prefetch=1,
            grid=(count,),
            in_specs=[held] * count,
            out_specs=pl.BlockSpec((1, length, width), lambda s, info: (info[s], 0, 0)),
        ),
        out_shape=jax.ShapeDtypeStruct((count, length, width), LOW),
        compiler_params=pltpu.CompilerParams(vmem_limit_bytes=32 << 20),
        cost_estimate=estimate(0, 4 * count * length * width),
    )(order, *rows)


def turn(values, cosine, sine_signed):
    return values * cosine + pltpu.roll(values, values.shape[-1] // 2, 1) * sine_signed


def turn_back(values, cosine, sine_signed):
    return values * cosine - pltpu.roll(values, values.shape[-1] // 2, 1) * sine_signed


def project_kernel(
    heads, head_dim, x0, x1, x2, x3, gains, weight, bias, cosine, sine, h_out, q_out, k_out, v_out, gain
):
    slot = pl.program_id(0)

    @pl.when(slot == 0)
    def _():
        gain[...] = gains[...].astype(WIDE).T[:8]


    def run(x_ref):
        x = x_ref[...].astype(WIDE)
        scale_inv = lax.rsqrt(jnp.mean(x * x, axis=-1, keepdims=True) + EPS)
        normed = (x * scale_inv * gain[0:1]).astype(LOW)
        h_out[0] = normed
        lin = jnp.dot(normed, weight[...], preferred_element_type=WIDE) + bias[...]
        cos, sin = cosine[0], sine[0]
        for h in range(heads + 1):
            part = turn(lin[:, h * head_dim : (h + 1) * head_dim], cos, sin).astype(LOW)
            if h < heads:
                q_out[0, :, h * head_dim : (h + 1) * head_dim] = part
            else:
                k_out[0] = part
        v_out[0] = lin[:, (heads + 1) * head_dim :].astype(LOW)

    for r, x_ref in enumerate((x0, x1, x2, x3)):
        pl.when(slot == r)(functools.partial(run, x_ref))


def project(rows, held, bias, cosine, sine, heads, head_dim):
    length, width = rows[0].shape
    count = len(rows)
    cols = (heads + 2) * head_dim
    whole = whole_spec
    by_slot = lambda *shape: pl.BlockSpec((1, *shape), lambda s: (s,) + (0,) * len(shape))
    return pl.pallas_call(
        functools.partial(project_kernel, heads, head_dim),
        grid=(count,),
        in_specs=[whole(length, width)] * count
        + [part_spec(width, 128, cols // 128), part_spec(width, cols, 0), whole(1, cols)]
        + [by_slot(length, head_dim)] * 2,
        out_specs=[
            by_slot(length, width),
            by_slot(length, heads * head_dim),
            by_slot(length, head_dim),
            by_slot(length, head_dim),
        ],
        out_shape=[
            jax.ShapeDtypeStruct((count, length, width), LOW),
            jax.ShapeDtypeStruct((count, length, heads * head_dim), LOW),
            jax.ShapeDtypeStruct((count, length, head_dim), LOW),
            jax.ShapeDtypeStruct((count, length, head_dim), LOW),
        ],
        scratch_shapes=[pltpu.VMEM((8, width), WIDE)],
        compiler_params=pltpu.CompilerParams(vmem_limit_bytes=56 << 20),
        cost_estimate=pl.CostEstimate(
            flops=2 * count * length * width * cols,
            bytes_accessed=count * length * (2 * width + cols) * 2 + width * cols * 2,
            transcendentals=0,
        ),
    )(*rows, held, held, bias, cosine, sine)


def row_blocks(length):
    return [(i, min(256, length)) for i in range(0, length, min(256, length))]


def key_biases(length, offset, start, rows, past, keys):
    past_pos = lax.broadcasted_iota(jnp.int32, (1, past), 1)
    past_bias = jnp.where((past_pos < offset) & (past_pos < length), 0.0, NEG_FILL)
    query_pos = offset + start + lax.broadcasted_iota(jnp.int32, (rows, keys), 0)
    own_pos = offset + lax.broadcasted_iota(jnp.int32, (rows, keys), 1)
    own_bias = jnp.where((own_pos <= query_pos) & (own_pos < length), 0.0, NEG_FILL)
    return past_bias, own_bias


def dot_cols(left, right):
    return lax.dot_general(left, right, (((1,), (1,)), ((), ())), preferred_element_type=WIDE)


def dot_rows(left, right):
    return lax.dot_general(left, right, (((0,), (0,)), ((), ())), preferred_element_type=WIDE)


def attend_rows(
    heads, head_dim, scale, length, offset, q, k_past, v_past, k_own, v_own, weight, out, lse, put
):
    past = k_past.shape[1]
    for start, rows in row_blocks(q.shape[1]):
        keys = start + rows
        past_bias, own_bias = key_biases(length, offset, start, rows, past, keys)
        here = slice(start, start + rows)
        for h in range(heads):
            cols = slice(h * head_dim, (h + 1) * head_dim)
            query = q[0, here, cols]
            s_past = dot_cols(query, k_past[0]) * scale + past_bias
            s_own = dot_cols(query, k_own[0, :keys]) * scale + own_bias
            top = jnp.maximum(
                jnp.max(s_past, axis=1, keepdims=True), jnp.max(s_own, axis=1, keepdims=True)
            )
            e_past, e_own = jnp.exp(s_past - top), jnp.exp(s_own - top)
            total = jnp.sum(e_past, axis=1, keepdims=True) + jnp.sum(e_own, axis=1, keepdims=True)
            inverse = 1.0 / total
            mixed = jnp.dot(
                (e_past * inverse).astype(LOW), v_past[0], preferred_element_type=WIDE
            ) + jnp.dot((e_own * inverse).astype(LOW), v_own[0, :keys], preferred_element_type=WIDE)
            out[0, here, cols] = mixed.astype(LOW)
            lse[0, here, h : h + 1] = top + jnp.log(total)
        rows_out = dot_cols(out[0, here], weight[...]).astype(LOW)
        put(here, rows_out)


def attend_kernel(
    heads, head_dim, scale, first, total_slots, info, q, k_past, v_past, k_own, v_own, weight, out, lse, *parts
):
    length, offset = info[first + pl.program_id(0)], info[total_slots]

    def put(here, value):
        for i, part in enumerate(parts):

            @pl.when(pl.program_id(0) == i)
            def _():
                part[here] = value

    attend_rows(heads, head_dim, scale, length, offset, q, k_past, v_past, k_own, v_own, weight, out, lse, put)


def attend_forward(info, q, k_past, v_past, k_own, v_own, weight, heads, head_dim, scale, first, count):
    _, length, width = q.shape
    past = k_past.shape[1]
    by_slot = lambda *shape: pl.BlockSpec((1, *shape), lambda s, info: (first + s,) + (0,) * len(shape))
    out_slot = lambda *shape: pl.BlockSpec((1, *shape), lambda s, info: (s,) + (0,) * len(shape))
    keys = count * length * (past + length) * heads
    return pl.pallas_call(
        functools.partial(attend_kernel, heads, head_dim, scale, first, q.shape[0]),
        grid_spec=pltpu.PrefetchScalarGridSpec(
            num_scalar_prefetch=1,
            grid=(count,),
            in_specs=[
                by_slot(length, width),
                by_slot(past, head_dim),
                by_slot(past, head_dim),
                by_slot(length, head_dim),
                by_slot(length, head_dim),
                whole_spec(*weight.shape, once=True),
            ],
            out_specs=[out_slot(length, width), out_slot(length, 128)]
            + [whole_spec(length, weight.shape[0])] * count,
        ),
        out_shape=[
            jax.ShapeDtypeStruct((count, length, width), LOW),
            jax.ShapeDtypeStruct((count, length, 128), WIDE),
        ]
        + [jax.ShapeDtypeStruct((length, weight.shape[0]), LOW)] * count,
        compiler_params=pltpu.CompilerParams(vmem_limit_bytes=56 << 20),
        cost_estimate=estimate(4 * keys * head_dim, 4 * count * length * width, keys),
    )(info, q, k_past, v_past, k_own, v_own, weight)


def attend_back_rows(
    heads, head_dim, scale, length, offset, q, k_past, v_past, k_own, v_own, grad, lse, cosine, sine, put,
    dk_past, dk_own, dv_past, dv_own
):
    past = k_past.shape[1]
    for start, rows in row_blocks(q.shape[1]):
        keys = start + rows
        past_bias, own_bias = key_biases(length, offset, start, rows, past, keys)
        here = slice(start, start + rows)
        cos, sin = cosine[0, here], sine[0, here]
        for h in range(heads):
            cols = slice(h * head_dim, (h + 1) * head_dim)
            query, upstream = q[0, here, cols], grad[0, here, cols]
            log_total = lse[0, here, h : h + 1]
            p_past = jnp.exp(dot_cols(query, k_past[0]) * scale + past_bias - log_total)
            p_own = jnp.exp(dot_cols(query, k_own[0, :keys]) * scale + own_bias - log_total)
            g_past = dot_cols(upstream, v_past[0])
            g_own = dot_cols(upstream, v_own[0, :keys])
            row_dot = jnp.sum(p_past * g_past, axis=1, keepdims=True) + jnp.sum(
                p_own * g_own, axis=1, keepdims=True
            )
            s_past = (p_past * (g_past - row_dot)).astype(LOW)
            s_own = (p_own * (g_own - row_dot)).astype(LOW)
            dq = (
                jnp.dot(s_past, k_past[0], preferred_element_type=WIDE)
                + jnp.dot(s_own, k_own[0, :keys], preferred_element_type=WIDE)
            ) * scale
            put(here, cols, turn_back(dq, cos, sin).astype(LOW))
            dk_past[...] += dot_rows(s_past, query)
            dk_own[:keys] += dot_rows(s_own, query)
            dv_past[...] += dot_rows(p_past.astype(LOW), upstream)
            dv_own[:keys] += dot_rows(p_own.astype(LOW), upstream)


def attend_back_kernel(
    heads,
    head_dim,
    scale,
    info,
    q,
    k_past,
    v_past,
    k_own,
    v_own,
    grad,
    lse,
    cosine,
    sine,
    dq_out,
    mine_past,
    mine_own,
    other_past,
    other_own,
    dk_past,
    dk_own,
    dv_past,
    dv_own,
):
    slot = pl.program_id(0)
    length, offset = info[slot], info[pl.num_programs(0)]
    parity = info[pl.num_programs(0) + 1]
    for total in (dk_past, dk_own, dv_past, dv_own):
        total[...] = jnp.zeros_like(total)
    attend_back_rows(
        heads, head_dim, scale, length, offset, q, k_past, v_past, k_own, v_own, grad, lse, cosine, sine,
        lambda here, cols, value: dq_out.__setitem__((0, here, cols), value),
        dk_past, dk_own, dv_past, dv_own,
    )

    @pl.when(parity == 0)
    def _():
        mine_past[0] = dk_past[...] * scale
        mine_own[0] = dk_own[...] * scale
        other_past[0] = dv_past[...]
        other_own[0] = dv_own[...]

    @pl.when(parity != 0)
    def _():
        mine_past[0] = dv_past[...]
        mine_own[0] = dv_own[...]
        other_past[0] = dk_past[...] * scale
        other_own[0] = dk_own[...] * scale


def attend_backward(
    info, q, k_past, v_past, k_own, v_own, grad, lse, cosine, sine, heads, head_dim, scale
):
    count, length, width = q.shape
    past = k_past.shape[1]
    by_slot = lambda *shape: pl.BlockSpec((1, *shape), lambda s, info: (s,) + (0,) * len(shape))
    keys = count * length * (past + length) * heads
    return pl.pallas_call(
        functools.partial(attend_back_kernel, heads, head_dim, scale),
        grid_spec=pltpu.PrefetchScalarGridSpec(
            num_scalar_prefetch=1,
            grid=(count,),
            in_specs=[
                by_slot(length, width),
                by_slot(past, head_dim),
                by_slot(past, head_dim),
                by_slot(length, head_dim),
                by_slot(length, head_dim),
                by_slot(length, width),
                by_slot(length, 128),
                by_slot(length, head_dim),
                by_slot(length, head_dim),
            ],
            out_specs=[
                by_slot(length, width),
                by_slot(past, head_dim),
                by_slot(length, head_dim),
                by_slot(past, head_dim),
                by_slot(length, head_dim),
            ],
            scratch_shapes=[
                pltpu.VMEM((past, head_dim), WIDE),
                pltpu.VMEM((length, head_dim), WIDE),
                pltpu.VMEM((past, head_dim), WIDE),
                pltpu.VMEM((length, head_dim), WIDE),
            ],
        ),
        out_shape=[
            jax.ShapeDtypeStruct((count, length, width), LOW),
            jax.ShapeDtypeStruct((count, past, head_dim), WIDE),
            jax.ShapeDtypeStruct((count, length, head_dim), WIDE),
            jax.ShapeDtypeStruct((count, past, head_dim), WIDE),
            jax.ShapeDtypeStruct((count, length, head_dim), WIDE),
        ],
        compiler_params=pltpu.CompilerParams(vmem_limit_bytes=56 << 20),
        cost_estimate=estimate(10 * keys * head_dim, 8 * count * length * width, keys),
    )(info, q, k_past, v_past, k_own, v_own, grad, lse, cosine, sine)


def attend_sum_kernel(
    heads, head_dim, scale, slots, info, q, k_past, v_past, k_own, v_own, weight, own_in, gain, out, lse, middle,
    normed, parts, core_in, far_in, send, recv
):
    step = pl.program_id(0)
    slot = slots - 1 - step
    core, far, _ = partners_of()
    remote = remote_copy(send, recv)
    cores = [remote(parts.at[3 - 2 * k], core_in.at[k], k, core) for k in range(2)]
    to_far = remote(parts.at[2], far_in, 2, far)

    @pl.when(step == 0)
    def _():
        meet((core, far))

    def put(here, value):
        parts[slot, here] = value

    offset = lax.axis_index("ctx") * q.shape[1]
    attend_rows(
        heads, head_dim, scale, info[slot], offset, q, k_past, v_past, k_own, v_own, weight, out, lse, put
    )
    for k in range(2):
        pl.when(step == 2 * k)(cores[k].start)

    @pl.when(step == 1)
    def _():
        cores[0].wait_recv()
        parts[2] = (parts[2].astype(WIDE) + core_in[0].astype(WIDE)).astype(LOW)
        to_far.start()

    @pl.when(step == slots - 1)
    def _():
        cores[1].wait_recv()
        to_far.wait_recv()
        rows = own_in[...].astype(WIDE) + parts[0].astype(WIDE)
        rows = rows + core_in[1].astype(WIDE) + far_in[...].astype(WIDE)
        middle[...] = rows
        inverse = lax.rsqrt(jnp.mean(rows * rows, axis=-1, keepdims=True) + EPS)
        normed[...] = (rows * inverse * gain[...]).astype(LOW)
        for copy in (*cores, to_far):
            copy.wait_send()


def attend_sum(info, q, k_past, v_past, k_own, v_own, weight, own_in, gain, heads, head_dim, scale):
    count, length, width = q.shape
    past, model_width = k_past.shape[1], own_in.shape[1]
    by_slot = lambda *shape: pl.BlockSpec(
        (1, *shape), lambda i, info: (count - 1 - i,) + (0,) * len(shape)
    )
    keys = count * length * (past + length) * heads
    return pl.pallas_call(
        functools.partial(attend_sum_kernel, heads, head_dim, scale, count),
        grid_spec=pltpu.PrefetchScalarGridSpec(
            num_scalar_prefetch=1,
            grid=(count,),
            in_specs=[
                by_slot(length, width),
                by_slot(past, head_dim),
                by_slot(past, head_dim),
                by_slot(length, head_dim),
                by_slot(length, head_dim),
                whole_spec(*weight.shape, once=True),
                whole_spec(length, model_width, once=True),
                whole_spec(1, model_width),
            ],
            out_specs=[
                by_slot(length, width),
                by_slot(length, 128),
                whole_spec(length, model_width, once=True),
                whole_spec(length, model_width, once=True),
            ],
            scratch_shapes=[
                pltpu.VMEM((count, length, model_width), LOW),
                pltpu.VMEM((2, length, model_width), LOW),
                pltpu.VMEM((length, model_width), LOW),
                pltpu.SemaphoreType.DMA((3,)),
                pltpu.SemaphoreType.DMA((3,)),
            ],
        ),
        out_shape=[
            jax.ShapeDtypeStruct((count, length, width), LOW),
            jax.ShapeDtypeStruct((count, length, 128), WIDE),
            jax.ShapeDtypeStruct((length, model_width), WIDE),
            jax.ShapeDtypeStruct((length, model_width), LOW),
        ],
        compiler_params=pltpu.CompilerParams(
            vmem_limit_bytes=56 << 20, collective_id=5, has_side_effects=True
        ),
        cost_estimate=estimate(4 * keys * head_dim, 4 * count * length * width, keys),
    )(info, q, k_past, v_past, k_own, v_own, weight, own_in, gain)


def exchange_kernel(
    heads, head_dim, scale, slots, tiles, info, q, k_past, v_past, k_own, v_own, grad, lse, cosine, sine,
    cosine_all, sine_all, branch, mixed, mlp_far, mlp_side, mlp_own, middle, line, out_grad, block, mine_past,
    mine_own, other_past, other_own, got_past, got_own, side_out, side_in, dk_past, dk_own, dv_past, dv_own,
    own_rows, last_in, send, recv, load
):
    step = pl.program_id(0)
    tensor_rank = lax.axis_index("tp")
    core, far, side = partners_of()
    parity = lax.rem(tensor_rank, 2)
    offset = lax.axis_index("ctx") * q.shape[1]
    remote = remote_copy(send, recv)
    pasts = [remote(other_past.at[r], got_past.at[r ^ 1], r, core) for r in range(slots)]
    owns = [remote(other_own.at[r], got_own.at[r ^ 1], slots + r, core) for r in range(slots)]
    sides = [remote(side_out.at[r], side_in.at[r], 2 * slots + r, side) for r in range(slots)]
    lasts = [
        remote(mlp_far, last_in.at[0], 3 * slots, far),
        remote(mlp_side, last_in.at[1], 3 * slots + 1, side),
    ]
    loading = pltpu.make_async_copy(mlp_own, own_rows, load)

    @pl.when(step == 0)
    def _():
        loading.start()
        meet((core, far, side))
        for copy in lasts:
            copy.start()

    @pl.when(step < slots)
    def _():
        length = info[jnp.minimum(step, slots - 1)]
        for total in (dk_past, dk_own, dv_past, dv_own):
            total[...] = jnp.zeros_like(total)
        attend_back_rows(
            heads, head_dim, scale, length, offset, q, k_past, v_past, k_own, v_own, grad, lse, cosine,
            sine, lambda here, cols, value: line.__setitem__((step, here, cols), value),
            dk_past, dk_own, dv_past, dv_own,
        )

        @pl.when(parity == 0)
        def _():
            mine_past[step] = dk_past[...] * scale
            mine_own[step] = dk_own[...] * scale
            other_past[step] = dv_past[...]
            other_own[step] = dv_own[...]

        @pl.when(parity != 0)
        def _():
            mine_past[step] = dv_past[...]
            mine_own[step] = dv_own[...]
            other_past[step] = dk_past[...] * scale
            other_own[step] = dk_own[...] * scale

    for r in range(slots):

        def start(r=r):
            pasts[r].start()
            owns[r].start()

        pl.when(step == r)(start)

    for pair in range(0, slots, 2):

        def merge(pair=pair):
            for r in (pair, pair + 1):
                pasts[r ^ 1].wait_recv()
                side_out[r] = (mine_past[r] + got_past[r]).astype(LOW)
                sides[r].start()

        pl.when(step == pair + 1)(merge)

    @pl.when(step >= slots)
    def _():
        out_grad[...] = dot_rows(branch[...], mixed[...]).astype(LOW)

    @pl.when(step == slots + tiles - 1)
    def _():
        for r in range(slots):
            owns[r ^ 1].wait_recv()
            sides[r].wait_recv()
            total = mine_own[r] + got_own[r] + side_in[r].astype(WIDE)
            back = turn_back(total, cosine_all[r], sine_all[r])
            line[r, :, heads * head_dim :] = jnp.where(parity == 0, back, total).astype(LOW)
        loading.wait()
        for copy in lasts:
            copy.wait_recv()
        block[...] = (
            middle[...] + own_rows[...].astype(WIDE) + last_in[0].astype(WIDE) + last_in[1].astype(WIDE)
        ).astype(LOW)
        for copy in (*pasts, *owns, *sides, *lasts):
            copy.wait_send()


def attend_exchange(
    info, q, k_past, v_past, k_own, v_own, grad, lse, cosine, sine, heads, head_dim, scale, branch, mixed, mlp, middle
):
    count, length, width = q.shape
    past = k_past.shape[1]
    tokens, model_width = branch.shape
    tile = 256
    tiles = model_width // tile
    slot = lambda i: jnp.minimum(i, count - 1)
    by_slot = lambda *shape: pl.BlockSpec((1, *shape), lambda i, info: (slot(i),) + (0,) * len(shape))
    column = lambda i: jnp.clip(i - count, 0, tiles - 1)
    held = lambda *shape: pl.BlockSpec(
        shape, lambda i, info: (0,) * len(shape), pipeline_mode=pl.Buffered(1)
    )
    line_cols = width + head_dim
    return pl.pallas_call(
        functools.partial(exchange_kernel, heads, head_dim, scale, count, tiles),
        grid_spec=pltpu.PrefetchScalarGridSpec(
            num_scalar_prefetch=1,
            grid=(count + tiles,),
            in_specs=[
                by_slot(length, width),
                by_slot(past, head_dim),
                by_slot(past, head_dim),
                by_slot(length, head_dim),
                by_slot(length, head_dim),
                by_slot(length, width),
                by_slot(length, 128),
                by_slot(length, head_dim),
                by_slot(length, head_dim),
                held(count, length, head_dim),
                held(count, length, head_dim),
                pl.BlockSpec((tokens, tile), lambda i, info: (0, column(i))),
                held(*mixed.shape),
            ]
            + [ANYWHERE] * 3
            + [held(length, model_width)],
            out_specs=[
                held(count, length, line_cols),
                pl.BlockSpec((tile, width), lambda i, info: (column(i), 0)),
                held(length, model_width),
            ],
            scratch_shapes=[pltpu.VMEM((count, length, head_dim), WIDE)] * 6
            + [pltpu.VMEM((count, length, head_dim), LOW)] * 2
            + [pltpu.VMEM((length, head_dim), WIDE)] * 4
            + [
                pltpu.VMEM((length, model_width), LOW),
                pltpu.VMEM((2, length, model_width), LOW),
                pltpu.SemaphoreType.DMA((3 * count + 2,)),
                pltpu.SemaphoreType.DMA((3 * count + 2,)),
                pltpu.SemaphoreType.DMA,
            ],
        ),
        out_shape=[
            jax.ShapeDtypeStruct((count, length, line_cols), LOW),
            jax.ShapeDtypeStruct((model_width, width), LOW),
            jax.ShapeDtypeStruct((length, model_width), LOW),
        ],
        compiler_params=pltpu.CompilerParams(
            vmem_limit_bytes=63 << 20, collective_id=4, has_side_effects=True
        ),
        cost_estimate=estimate(2 * tokens * model_width * width, 10 * tokens * width),
    )(info, q, k_past, v_past, k_own, v_own, grad, lse, cosine, sine, cosine, sine, branch, mixed, *mlp, middle)


def local(
    hidden_in,
    cotangent,
    seq_lengths,
    positions,
    permutation,
    query_weight,
    keyval_weight,
    output_weight,
    norm_gains,
    bias_query,
    bias_keyval,
    gate_weight,
    up_weight,
    down_weight,
):
    group_rank = lax.axis_index("fsdp")
    ctx_rank = lax.axis_index("ctx")
    tensor_rank = lax.axis_index("tp")
    fsdp_count = lax.axis_size("fsdp")
    ctx_count = lax.axis_size("ctx")
    tensor_count = lax.axis_size("tp")
    seq_grp, local_len, model_width = hidden_in.shape
    heads, head_dim = bias_query.shape
    keyval_heads = bias_keyval.shape[0] // 2
    assert seq_grp == tensor_count == fsdp_count == len(DEAL_SHIFT)
    token_count = seq_grp * local_len
    scale = 1.0 / math.sqrt(head_dim)
    offset = ctx_rank * local_len
    head_pair = tensor_rank // (tensor_count // keyval_heads)
    parity = tensor_rank % 2
    assert DEAL_SHIFT == tuple((t % 2) * 2 + t // 2 for t in range(tensor_count))

    entry = jnp.arange(permutation.shape[0])
    entry_group, entry_slot = entry // seq_grp, entry % seq_grp
    home_group, home_slot = lax.div(permutation, seq_grp), lax.rem(permutation, seq_grp)
    places = jnp.arange(2 * seq_grp)
    near_places = places < seq_grp
    slot_rank = tensor_rank ^ (places % seq_grp)
    shift_of = lambda rank: lax.rem(rank, 2) * 2 + lax.div(rank, 2)
    target = lax.rem(group_rank + shift_of(tensor_rank), fsdp_count)
    leaving = jnp.sum(jnp.where((entry_group == target) & (home_group == group_rank), home_slot, 0))
    source = lax.rem(group_rank + fsdp_count - shift_of(slot_rank), fsdp_count)
    hit = (entry_group == group_rank)[None] & (home_group[None] == source[:, None])
    slot_now = jnp.sum(jnp.where(hit, entry_slot[None], 0), axis=1)
    seq_now = jnp.sum(jnp.where(hit, permutation[None], 0), axis=1)
    targets = lax.rem(group_rank + shift_of(slot_rank), fsdp_count)
    back_hit = (entry_group[None] == targets[:, None]) & (home_group == group_rank)[None]
    home_order = jnp.sum(jnp.where(back_hit, home_slot[None], 0), axis=1)[:seq_grp]
    there = [
        (f * tensor_count + t, (f + DEAL_SHIFT[t]) % fsdp_count * tensor_count + t)
        for f in range(fsdp_count)
        for t in range(tensor_count)
    ]
    back = [(target, source) for source, target in there]

    split = units_split()
    head_width = 2 * head_dim
    query_cols = heads * head_dim
    near_cols = query_cols + head_width + 128

    outgoing = lax.dynamic_index_in_dim(hidden_in, leaving, 0, keepdims=False)
    own_in = lax.ppermute(outgoing, ("fsdp", "tp"), there)
    small = jnp.concatenate(
        [
            query_weight,
            lax.dynamic_slice_in_dim(keyval_weight, head_pair * head_width, head_width, axis=1),
            jnp.pad(norm_gains.T, ((0, 0), (0, 128 - norm_gains.shape[0]))),
            output_weight.T,
        ],
        axis=1,
    )
    seq_hit = seq_now[:, None] == entry[None]
    lengths_now = jnp.sum(jnp.where(seq_hit, seq_lengths[None], 0), axis=1)
    more = jnp.where(places == seq_grp, offset, jnp.where(places == seq_grp + 1, parity, 0))
    info = jnp.where(near_places, lengths_now, more).astype(jnp.int32)
    positions_now = jnp.sum(
        jnp.where(seq_hit[:seq_grp, :, None], positions[None], 0), axis=1
    )
    lane = jnp.arange(head_dim)
    frequency = 1.0 / ROPE_BASE ** ((lane % (head_dim // 2)).astype(WIDE) * 2.0 / head_dim)
    angles = positions_now.astype(WIDE)[..., None] * frequency
    cosine = jnp.cos(angles)
    sine = jnp.sin(angles) * jnp.where(lane < head_dim // 2, -1.0, 1.0)
    pick_info = jnp.where(near_places, slot_now, slot_now ^ tensor_rank).astype(jnp.int32)
    units = gate_weight.shape[1]
    units_pad = -(-units // 256) * 256
    widen = lambda w: jnp.pad(w, ((0, 0), (0, units_pad - units)))
    shards = [widen(w) for w in (down_weight.T, gate_weight, up_weight)]
    if split:
        half_units = units_pad // 2
        cut = lambda w, c: lax.dynamic_slice_in_dim(w, c * half_units, half_units, axis=1)

        def in_order(own, other):
            return jnp.stack(
                [jnp.where(ctx_rank == 0, own, other), jnp.where(ctx_rank == 0, other, own)]
            )

        def all_rows(both, *earlier):
            full = lax.all_gather(after(both, *earlier), "fsdp", axis=0, tiled=False)
            return full.reshape(-1, both.shape[-1])

        first_units = half_units // 2 // 256 * 256
        first_cols = 3 * first_units

        def in_parts(c):
            halves = [cut(w, c) for w in shards]
            return jnp.concatenate(
                [w[:, :first_units] for w in halves] + [w[:, first_units:] for w in halves], axis=1
            )

        leaving_units, own_units = in_parts(1 - ctx_rank), in_parts(ctx_rank)
        slot_pick = lax.dynamic_index_in_dim(cotangent, tensor_rank, 0, keepdims=False)
        small = after(small, outgoing, leaving_units, cosine, sine, slot_pick)
        small_both = in_order(small, from_partner(small, "ctx", 1))
        arriving_units = from_partner(after(leaving_units, small_both), "ctx", 1)
        other_own = from_partner(after(slot_pick, arriving_units), "ctx", 1)
        both_a = in_order(own_units[:, :first_cols], arriving_units[:, :first_cols])
        both_b = in_order(own_units[:, first_cols:], arriving_units[:, first_cols:])
    else:
        all_rows = lambda shard, *earlier: lax.all_gather(
            shard, ("fsdp", "ctx"), axis=0, tiled=True
        )
        small_both, unit_both, half_units = small, jnp.concatenate(shards, axis=1), units_pad
    far_in = from_partner(own_in, "tp", 2)
    near_in = from_partner(own_in, "tp", 1)
    ready = (info, pick_info, own_units, home_order) if split else (cosine, sine, info)
    cross_in = from_partner(after(far_in, *ready), "tp", 1)

    near_full = all_rows(small_both, own_in)
    if split:
        units_a = all_rows(both_a, cross_in)
        units_b = all_rows(both_b, cross_in)
    else:
        down_full = all_rows(unit_both[..., :half_units], cross_in)
        gate_up_full = all_rows(unit_both[..., half_units:], cross_in)
    project_full = near_full[:, : query_cols + head_width]
    output_full = near_full[:, near_cols:]
    bias_head = lax.dynamic_slice_in_dim(bias_keyval, head_pair * 2, 2, axis=0)
    bias_row = jnp.concatenate([bias_query.reshape(1, -1), bias_head.reshape(1, -1)], axis=1).astype(WIDE)
    normed_one, query_rot, key_own, value_own = project(
        (own_in, near_in, far_in, cross_in),
        near_full,
        bias_row,
        after(cosine, other_own, both_a, both_b, info, pick_info) if split else cosine,
        sine,
        heads,
        head_dim,
    )
    gains_now = near_full[:, query_cols + head_width : near_cols][:, :2].astype(WIDE).T
    if split:
        key_past, value_past = lax.ppermute((key_own, value_own), "ctx", [(0, 1)])
        other_far = from_partner(other_own, "tp", 2)
        other_near = from_partner(after(other_own, key_past), "tp", 1)
        other_cross = from_partner(after(other_far, key_past), "tp", 1)
        other_rows = (other_own, other_near, other_far, other_cross)
        key_past = after(key_past, other_far)
    else:
        key_past = lax.all_gather(key_own, "ctx", axis=1, tiled=True)
        value_past = lax.all_gather(value_own, "ctx", axis=1, tiled=True)
    in_share = own_in.astype(WIDE)
    if split:
        mixed, lse, middle_share, normed_share = attend_sum(
            info,
            query_rot,
            key_past,
            value_past,
            key_own,
            value_own,
            output_full,
            own_in,
            gains_now[1:2],
            heads,
            head_dim,
            scale,
        )
    else:
        attend = lambda first, *held: attend_forward(
            info, query_rot, *held, key_own, value_own, output_full, heads, head_dim, scale, first, 2
        )

        mixed_far, lse_far, *attn_far = attend(2, key_past, value_past)
        attn_wide = collect_far(attn_far[0], attn_far[1])
        attn_got = from_partner(attn_wide, "tp", 2)
        mixed_near, lse_near, *attn_near = attend(0, after(key_past, attn_wide), value_past)
        attn_core = from_partner(attn_near[1], "tp", 1)
        middle_share = (
            in_share
            + attn_near[0].astype(WIDE)
            + attn_core.astype(WIDE)
            + attn_got.astype(WIDE)
        )
        inv_two = lax.rsqrt(jnp.mean(middle_share * middle_share, axis=-1, keepdims=True) + EPS)
        normed_share = (middle_share * inv_two * gains_now[1]).astype(LOW)
        mixed = jnp.concatenate([mixed_near, mixed_far], axis=0)
        lse = jnp.concatenate([lse_near, lse_far], axis=0)
    half_len = local_len // 2

    if split:
        grad_hidden, grad_rows = chosen_rows(
            pick_info,
            after(cotangent, normed_share),
            other_rows,
            units_a,
            0,
            3,
        )
    else:
        grad_slots = [
            lax.dynamic_index_in_dim(cotangent, slot_now[r], 0, keepdims=False) for r in range(seq_grp)
        ]
        grad_hidden, grad_rows = stack_rows([(g,) for g in grad_slots], down_full, 0, 1)

    def spread_all(own):
        far = from_partner(own, "tp", 2)
        near = from_partner(own, "tp", 1)
        if not split:
            return (own, near, far, from_partner(far, "tp", 1))
        side = from_partner(own, "ctx", 1)
        held = after(far, grad_hidden), after(side, grad_hidden)
        across = from_partner(held[0][:half_len], "ctx", 1), from_partner(held[1][half_len:], "tp", 2)
        cores = [from_partner(v, "tp", 1) for v in (*held, *across)]
        return (own, near, far, cores[0], side, cores[1], *across, *cores[2:])

    def in_slots(rows):
        if not split:
            return [(row,) for row in rows]
        return [(row,) for row in rows[:6]] + [rows[6:8], rows[8:]]

    mixed_flat = mixed.reshape(token_count, query_cols)
    own_weight = lax.dynamic_slice_in_dim(
        project_full, query_cols + parity * head_dim, head_dim, axis=1
    )
    back_full = jnp.concatenate([project_full[:, :query_cols], own_weight], axis=1)
    normed_slots = in_slots(spread_all(normed_share))
    if split:
        early = after(units_a, back_full)
        gate_lin, normed_two = stack_rows(normed_slots, early, 1, 3)
        hidden_a, gate_a, up_a = hidden_units(normed_two, units_a, 2, 3, gate_lin, grad_hidden)
        grad_a = first_grads(grad_rows, normed_two, hidden_a, gate_a, up_a)
        hidden_b, gate_b, up_b = full_units(after(normed_two, grad_a), grad_rows, units_b)
    else:
        gate_lin, normed_two = stack_rows(normed_slots, gate_up_full, 0, 2)
        hidden_act, grad_gate, grad_up = hidden_units(
            normed_two, gate_up_full, 1, 2, gate_lin, grad_hidden
        )

    def collect_all(lefts, weights, *earlier):
        lefts = list(lefts)
        lefts[0] = after(lefts[0], *earlier)
        last = back_rows(lefts, weights, 2, 2, local_len)
        got = [from_partner(collect_far(last[0], last[1]), "tp", 2)]
        first = back_rows(lefts, weights, 0, 2, local_len)
        got.append(from_partner(first[1], "tp", 1))

        def finish():
            return sum((v.astype(WIDE) for v in got), first[0].astype(WIDE))

        return first[0], finish

    if split:
        grad_two_share, down_b, up_grad_b = collect_back(
            (gate_a, up_a),
            (gate_b, up_b),
            units_a,
            units_b,
            grad_rows,
            normed_two,
            hidden_b,
            local_len,
        )
        grad_middle, gain_two, gate_grad_b, grad_branch, *mlp = spread_branch(
            grad_two_share,
            middle_share,
            grad_rows,
            gains_now[1:2],
            hidden_a,
            hidden_b,
            units_a,
            units_b,
            normed_two,
            gate_b,
        )
        mlp_own, mlp_far, mlp_side = mlp
        grad_branch = grad_branch.reshape(token_count, model_width)
    else:
        first_back, finish_back = collect_all(
            (grad_gate, grad_up), ((gate_up_full, 0, 2), (gate_up_full, 1, 2))
        )
        down_grad = contract_rows(after(grad_rows, first_back), hidden_act, LOW)
        gate_grad = contract_rows(normed_two, after(grad_gate, down_grad), LOW)
        grad_two_share = finish_back()
        grad_norm_two, gain_two = norm_backward(
            middle_share, inv_two, gains_now[1], grad_two_share
        )
        grad_middle = grad_slots[0].astype(WIDE) + grad_norm_two
        branch_own = grad_middle.astype(LOW)
        branch_far = from_partner(branch_own, "tp", 2)
        branch_near = from_partner(branch_own, "tp", 1)
        branch_cross = from_partner(branch_far, "tp", 1)
        grad_branch = jnp.concatenate([branch_own, branch_near, branch_far, branch_cross], axis=0)
        up_grad = contract_rows(normed_two, after(grad_up, branch_own), LOW)

    grad_mixed = product(grad_branch, output_full, LOW)
    attend_args = (
        info,
        query_rot,
        key_past,
        value_past,
        key_own,
        value_own,
        grad_mixed.reshape(seq_grp, local_len, query_cols),
        lse,
        cosine,
        sine,
        heads,
        head_dim,
        scale,
    )
    if split:
        line_grad, output_grad, block_share = attend_exchange(
            *attend_args,
            grad_branch,
            mixed_flat,
            (mlp_far, mlp_side, mlp_own),
            middle_share,
        )
        line_grad = line_grad.reshape(token_count, -1)
    else:
        grad_query, mine_past, mine_own, other_past, other_own = attend_backward(*attend_args)
        swap = lambda value: jnp.stack([value[r ^ 1] for r in range(seq_grp)])
        got_past, got_own = from_partner((other_past, other_own), "tp", 1)
        past_sum = mine_past + swap(got_past)
        own_sum = mine_own + swap(got_own)
        own_sum = own_sum + lax.psum_scatter(past_sum, "ctx", scatter_dimension=1, tiled=True)
        half_lanes = head_dim // 2
        turned = own_sum * cosine - jnp.roll(own_sum, half_lanes, axis=-1) * sine
        own_grad = jnp.where(parity == 0, turned, own_sum).astype(LOW).reshape(token_count, head_dim)
        line_grad = jnp.concatenate([grad_query.reshape(token_count, query_cols), own_grad], axis=1)
    def scatter_units(grad):
        if not split:
            return scatter_sum(grad, ctx_rank, LOW)
        return lax.psum_scatter(grad, "fsdp", scatter_dimension=0, tiled=True)

    unit_grads = (grad_a, down_b, up_grad_b, gate_grad_b) if split else (down_grad, gate_grad, up_grad)
    unit_sums = [scatter_units(unit_grads[0])]
    if split:
        unit_sums += [scatter_units(after(g, unit_sums[0])) for g in unit_grads[1:3]]
        unit_sums += [scatter_units(after(unit_grads[3], unit_sums[0]))]
    else:
        unit_sums += [scatter_units(g) for g in unit_grads[1:]]

    normed_flat = normed_one.reshape(token_count, model_width)
    if split:
        input_share, gain_grad, attn_grad, bias_grad, block_home = finish_rows(
            line_grad,
            after(back_full, *unit_sums),
            own_in,
            grad_middle,
            gains_now[0:1],
            gain_two,
            normed_flat,
            block_share,
        )
        attn_grad = jnp.concatenate([attn_grad, output_grad], axis=1)
    else:
        half = token_count // 2
        line_far = contract_cols(line_grad[half:], back_full, LOW).reshape(2, local_len, model_width)
        line_near = contract_cols(line_grad[:half], back_full, LOW).reshape(2, local_len, model_width)
        line_wide = collect_far(line_far[0], line_far[1])
        line_got = from_partner(line_wide, "tp", 2)
        line_core = from_partner(line_near[1], "tp", 1)
        first_mlp, finish_mlp = collect_all((hidden_act,), ((down_full, 0, 1),), up_grad, branch_far)
        block_share = (middle_share + finish_mlp()).astype(LOW)
        grad_one_share = line_near[0].astype(WIDE) + line_core.astype(WIDE) + line_got.astype(WIDE)
        inv_one = lax.rsqrt(jnp.mean(in_share * in_share, axis=-1, keepdims=True) + EPS)
        grad_norm_one, gain_one = norm_backward(in_share, inv_one, gains_now[0], grad_one_share)
        input_share = (grad_middle + grad_norm_one).astype(LOW)
        attn_grad = jnp.concatenate(
            [contract_rows(normed_flat, line_grad, LOW), contract_rows(grad_branch, mixed_flat, LOW)],
            axis=1,
        )
        bias_grad = jnp.sum(line_grad.astype(WIDE), axis=0)

    shard_count = fsdp_count * ctx_count
    share = head_dim // shard_count
    if not split:
        gain_grad = jnp.concatenate([gain_one, gain_two], axis=0)
        gain_grad = gain_grad + from_partner(gain_grad, "tp", 1)
        gain_grad = gain_grad + from_partner(gain_grad, "tp", 2)
    bias_cols = jnp.transpose(bias_grad.reshape(heads + 1, shard_count, share), (1, 2, 0))
    bias_cols = jnp.pad(bias_cols, ((0, 0), (0, (model_width - head_dim) // shard_count), (0, 0)))
    tiny = jnp.concatenate([gain_grad.T, bias_cols.reshape(model_width, heads + 1)], axis=1)
    tiny = jnp.pad(tiny, ((0, 0), (0, 128 - tiny.shape[1]))).astype(LOW)
    attn_grad = jnp.concatenate([attn_grad, tiny], axis=1)
    if split:
        attn_blocks = attn_grad.reshape(fsdp_count, ctx_count, -1, attn_grad.shape[1])
        kept, sent = scatter_ctx(attn_blocks, ctx_rank)
        attn_held = (kept.astype(WIDE) + from_partner(sent, "ctx", 1).astype(WIDE)).astype(LOW)
        attn_held = attn_held.reshape(-1, attn_grad.shape[1])
        attn_end = lax.psum_scatter(after(attn_held, *unit_sums), "fsdp", scatter_dimension=0, tiled=True)
    else:
        attn_end = scatter_sum(attn_grad, ctx_rank, LOW, *unit_sums)


    def leave(share):
        return lax.ppermute(share, ("fsdp", "tp"), back)

    def arrive(own, order):
        far = from_partner(own, "tp", 2)
        near = from_partner(own, "tp", 1)
        return place_rows((own, near, far, from_partner(far, "tp", 1)), order)

    input_home = leave(input_share)
    if not split:
        block_home = leave(block_share)
    block_out = arrive(block_home, home_order)
    if split:

        def unit_end(total, *earlier):
            kept, sent = scatter_ctx(total.reshape(1, ctx_count, -1, total.shape[1]), ctx_rank)
            return kept[0], from_partner(after(sent[0], *earlier), "ctx", 1)

        own_a, got_a = unit_end(unit_sums[0], grad_branch)
        ends = [unit_end(t, line_grad) for t in unit_sums[1:]]
        input_home = after(input_home, attn_held)
        home_order = after(home_order, got_a, *[end[1] for end in ends])
    input_grad = arrive(input_home, home_order)

    small_at = query_cols + head_dim + query_cols
    tiny_grad = attn_end[:, small_at:].astype(WIDE)

    if split:

        def joined(part, end):
            cols = slice(part * first_units, (part + 1) * first_units)
            own = jnp.concatenate([own_a[:, cols], end[0]], axis=1)
            got = jnp.concatenate([got_a[:, cols], end[1]], axis=1)
            first, second = jnp.where(ctx_rank == 0, own, got), jnp.where(ctx_rank == 0, got, own)
            return jnp.concatenate([first, second], axis=1)[:, :units].astype(WIDE)

        down_end, gate_end, up_end = joined(0, ends[0]), joined(1, ends[2]), joined(2, ends[1])
    else:
        down_end, gate_end, up_end = (t[:, :units].astype(WIDE) for t in unit_sums)
    return (
        block_out,
        input_grad,
        attn_end[:, :query_cols].astype(WIDE),
        attn_end[:, query_cols : query_cols + head_dim].astype(WIDE),
        attn_end[:, query_cols + head_dim : small_at].astype(WIDE).T,
        tiny_grad[:, :2].T,
        tiny_grad[:share, 2 : 2 + heads].T,
        tiny_grad[:share, 2 + heads : 3 + heads].T,
        gate_end,
        up_end,
        down_end.T,
    )


def solution(mesh):
    placed = (
        P("fsdp", "ctx", None),
        P("fsdp", "ctx", None),
        P(),
        P(None, "ctx"),
        P(),
        P(("fsdp", "ctx"), "tp"),
        P(("fsdp", "ctx"), None),
        P("tp", ("fsdp", "ctx")),
        P(None, ("fsdp", "ctx")),
        P("tp", None),
        P(),
        P(("fsdp", "ctx"), "tp"),
        P(("fsdp", "ctx"), "tp"),
        P("tp", ("fsdp", "ctx")),
    )
    return jax.shard_map(
        local,
        mesh=mesh,
        in_specs=placed,
        out_specs=(
            P("fsdp", "ctx", None),
            P("fsdp", "ctx", None),
            P(("fsdp", "ctx"), "tp"),
            P(("fsdp", "ctx"), "tp"),
            P("tp", ("fsdp", "ctx")),
            P(None, ("fsdp", "ctx")),
            P("tp", ("fsdp", "ctx")),
            P("tp", ("fsdp", "ctx")),
            P(("fsdp", "ctx"), "tp"),
            P(("fsdp", "ctx"), "tp"),
            P("tp", ("fsdp", "ctx")),
        ),
        check_vma=False,
    )
```

```python
import functools
import math

import jax
import jax.numpy as jnp
from jax import lax
from jax.experimental import pallas as pl
from jax.experimental.pallas import tpu as pltpu
from jax.sharding import PartitionSpec as P

EPS = 1e-06
ROPE_BASE = 10000.0
NEG_FILL = -1e30
LOW = jnp.bfloat16
WIDE = jnp.float32
DEAL_SHIFT = (0, 2, 1, 3)


def from_partner(value, axis, apart):
    pairs = [(source, source ^ apart) for source in range(lax.axis_size(axis))]
    return lax.ppermute(value, axis, pairs)


def product(left_side, right_side, kind=WIDE):
    return jnp.dot(left_side, right_side, preferred_element_type=WIDE).astype(kind)


def contract_rows(left_side, right_side, kind=WIDE):
    return lax.dot_general(
        left_side, right_side, (((0,), (0,)), ((), ())), preferred_element_type=WIDE
    ).astype(kind)


def contract_cols(left_side, right_side, kind=WIDE):
    return lax.dot_general(
        left_side, right_side, (((1,), (1,)), ((), ())), preferred_element_type=WIDE
    ).astype(kind)


def norm_backward(values, scale_inv, gain_row, upstream):
    scaled = gain_row * upstream
    inner_mean = jnp.mean(values * scaled, axis=-1, keepdims=True)
    grad_in = scale_inv * scaled - values * (scale_inv * scale_inv * scale_inv) * inner_mean
    gain_grad = jnp.sum(upstream * values * scale_inv, axis=0, keepdims=True)
    return (grad_in, gain_grad)


def after(value, *earlier):
    return lax.optimization_barrier((value, *earlier))[0]


def collect_far(far_part, cross_part):
    wide = far_part.astype(WIDE) + from_partner(cross_part, "tp", 1).astype(WIDE)
    return wide.astype(LOW)


def units_split():
    return lax.axis_size("ctx") == 2


def all_rows(shard):
    return lax.all_gather(shard, "fsdp", axis=0, tiled=True)


def scatter_ctx(blocks, ctx_rank):
    kept = lax.dynamic_index_in_dim(blocks, ctx_rank, 1, keepdims=False)
    sent = lax.dynamic_index_in_dim(blocks, 1 - ctx_rank, 1, keepdims=False)
    return kept, sent


def scatter_sum(grad, ctx_rank, kind, *earlier):
    fsdp_count, ctx_count = lax.axis_size("fsdp"), lax.axis_size("ctx")
    rows, cols = grad.shape
    blocks = grad.reshape(fsdp_count, ctx_count, rows // (fsdp_count * ctx_count), cols)
    if ctx_count == 2:
        kept, sent = scatter_ctx(blocks, ctx_rank)
        got = from_partner(sent, "ctx", 1)
        held = (after(kept, *earlier).astype(WIDE) + got.astype(WIDE)).astype(kind)
    else:
        swapped = jnp.swapaxes(blocks, 0, 1).reshape(rows, cols)
        held = lax.psum_scatter(swapped, "ctx", scatter_dimension=0, tiled=True)
    held = held.reshape(rows // ctx_count, cols)
    return lax.psum_scatter(held, "fsdp", scatter_dimension=0, tiled=True)


def estimate(flops, moved, transcendentals=0):
    return pl.CostEstimate(flops=flops, bytes_accessed=moved, transcendentals=transcendentals)


def part_spec(rows, cols, part):
    return pl.BlockSpec((rows, cols), lambda *_: (0, part), pipeline_mode=pl.Buffered(1))


def whole_spec(*shape, once=False):
    mode = {"pipeline_mode": pl.Buffered(1)} if once else {}
    return pl.BlockSpec(shape, lambda *_: (0,) * len(shape), **mode)


def rows_kernel(groups, *refs):
    slot = pl.program_id(0)
    weight, (lin, stacked) = refs[sum(groups)], refs[-2:]

    def run(pieces):
        start = 0
        for piece in pieces:
            stacked[start : start + piece.shape[0]] = piece[...]
            start += piece.shape[0]
        lin[...] = jnp.dot(stacked[...], weight[...], preferred_element_type=WIDE).astype(LOW)

    first = 0
    for r, pieces in enumerate(groups):
        pl.when(slot == r)(functools.partial(run, refs[first : first + pieces]))
        first += pieces


def stack_rows(slots, weight, part, parts, into=None, first=0, total=None):
    groups = [len(s) for s in slots]
    rows = [piece for s in slots for piece in s]
    width, length = rows[0].shape[1], sum(piece.shape[0] for piece in slots[0])
    count, cols = len(slots), weight.shape[1] // parts
    total = total or count
    into = into or ()
    return pl.pallas_call(
        functools.partial(rows_kernel, groups),
        grid=(count,),
        in_specs=[whole_spec(*piece.shape, once=True) for piece in rows]
        + [part_spec(width, cols, part)]
        + [pl.BlockSpec(memory_space=pl.ANY)] * len(into),
        out_specs=[
            pl.BlockSpec((length, cols), lambda s: (first + s, 0)),
            pl.BlockSpec((length, width), lambda s: (first + s, 0)),
        ],
        out_shape=[
            jax.ShapeDtypeStruct((total * length, cols), LOW),
            jax.ShapeDtypeStruct((total * length, width), LOW),
        ],
        input_output_aliases={len(rows) + 1 + i: i for i in range(len(into))},
        compiler_params=pltpu.CompilerParams(vmem_limit_bytes=60 << 20),
        cost_estimate=estimate(
            2 * count * length * width * cols, 2 * (count * length * (2 * width + cols) + width * cols)
        ),
    )(*rows, weight, *into)


def units_kernel(h, up, gate, grad, hid, grad_gate, grad_up):
    up_lin = jnp.dot(h[...], up[...], preferred_element_type=WIDE)
    gate_lin = gate[...].astype(WIDE)
    grad_hidden = grad[...].astype(WIDE)
    sigmoid = 1.0 / (1.0 + jnp.exp(-gate_lin))
    silu = gate_lin * sigmoid
    hid[...] = (silu * up_lin).astype(LOW)
    grad_gate[...] = (grad_hidden * up_lin * sigmoid * (1.0 + gate_lin * (1.0 - sigmoid))).astype(LOW)
    grad_up[...] = (grad_hidden * silu).astype(LOW)


def hidden_units(h, up, part, parts, gate_lin, grad_hidden):
    tokens, width = h.shape
    cols = up.shape[1] // parts
    step = math.gcd(512, tokens)
    by_row = lambda n: pl.BlockSpec((step, n), lambda i: (i, 0))
    return pl.pallas_call(
        units_kernel,
        grid=(tokens // step,),
        in_specs=[by_row(width), part_spec(width, cols, part), by_row(cols), by_row(cols)],
        out_specs=[by_row(cols)] * 3,
        out_shape=[jax.ShapeDtypeStruct((tokens, cols), LOW)] * 3,
        compiler_params=pltpu.CompilerParams(vmem_limit_bytes=60 << 20),
        cost_estimate=estimate(
            2 * tokens * width * cols, 2 * (tokens * width + width * cols + 5 * tokens * cols)
        ),
    )(h, up, gate_lin, grad_hidden)


def back_kernel(terms, *refs):
    lefts, weights, outs = refs[:terms], refs[terms : 2 * terms], refs[2 * terms :]
    total = None
    for left, weight in zip(lefts, weights):
        term = dot_cols(left[...], weight[...])
        total = term if total is None else total + term
    for i, out in enumerate(outs):

        @pl.when(pl.program_id(0) == i)
        def _():
            out[...] = total.astype(LOW)


def back_rows(lefts, weights, first_slot, slots, length):
    width = weights[0][0].shape[0]
    depth = sum(left.shape[1] for left in lefts)
    return pl.pallas_call(
        functools.partial(back_kernel, len(lefts)),
        grid=(slots,),
        in_specs=[
            pl.BlockSpec((length, left.shape[1]), lambda s: (first_slot + s, 0)) for left in lefts
        ]
        + [part_spec(width, w.shape[1] // parts, part) for w, part, parts in weights],
        out_specs=[whole_spec(length, width)] * slots,
        out_shape=[jax.ShapeDtypeStruct((length, width), LOW)] * slots,
        compiler_params=pltpu.CompilerParams(vmem_limit_bytes=60 << 20),
        cost_estimate=estimate(
            2 * slots * length * width * depth,
            2 * (slots * length * (width + depth) + width * depth),
        ),
    )(*lefts, *[w for w, _, _ in weights])


def chosen_kernel(near, count, info, cotangent, *refs):
    slot = pl.program_id(0)
    others, (weight, lin, stacked) = refs[:count], refs[count:]

    @pl.when(slot < near)
    def _():
        stacked[...] = cotangent[0]

    for k, other in enumerate(others):

        @pl.when((slot >= near) & (info[slot] == k))
        def _():
            stacked[...] = other[...]

    lin[...] = jnp.dot(stacked[...], weight[...], preferred_element_type=WIDE).astype(LOW)


def chosen_rows(info, cotangent, others, weight, part, parts):
    near, length, width = cotangent.shape
    slots, cols = near + len(others), weight.shape[1] // parts
    held = lambda rows, n, at: pl.BlockSpec(
        (rows, n), lambda s, info: (0, at), pipeline_mode=pl.Buffered(1)
    )
    return pl.pallas_call(
        functools.partial(chosen_kernel, near, len(others)),
        grid_spec=pltpu.PrefetchScalarGridSpec(
            num_scalar_prefetch=1,
            grid=(slots,),
            in_specs=[
                pl.BlockSpec((1, length, width), lambda s, info: (info[jnp.minimum(s, near - 1)], 0, 0))
            ]
            + [held(length, width, 0)] * len(others)
            + [held(width, cols, part)],
            out_specs=[
                pl.BlockSpec((length, cols), lambda s, info: (s, 0)),
                pl.BlockSpec((length, width), lambda s, info: (s, 0)),
            ],
        ),
        out_shape=[
            jax.ShapeDtypeStruct((slots * length, cols), LOW),
            jax.ShapeDtypeStruct((slots * length, width), LOW),
        ],
        compiler_params=pltpu.CompilerParams(vmem_limit_bytes=60 << 20),
        cost_estimate=estimate(
            2 * slots * length * width * cols, 2 * (slots * length * (2 * width + cols) + width * cols)
        ),
    )(info, cotangent, *others, weight)


def full_units_kernel(h, g, down, gate, up, hid, grad_gate, grad_up):
    gate_lin = jnp.dot(h[...], gate[...], preferred_element_type=WIDE)
    up_lin = jnp.dot(h[...], up[...], preferred_element_type=WIDE)
    grad_hidden = jnp.dot(g[...], down[...], preferred_element_type=WIDE)
    sigmoid = 1.0 / (1.0 + jnp.exp(-gate_lin))
    silu = gate_lin * sigmoid
    hid[...] = (silu * up_lin).astype(LOW)
    grad_gate[...] = (grad_hidden * up_lin * sigmoid * (1.0 + gate_lin * (1.0 - sigmoid))).astype(LOW)
    grad_up[...] = (grad_hidden * silu).astype(LOW)


def full_units(h, g, weight):
    tokens, width = h.shape
    cols = weight.shape[1] // 3
    step = math.gcd(512, tokens)
    by_row = lambda n: pl.BlockSpec((step, n), lambda i: (i, 0))
    return pl.pallas_call(
        full_units_kernel,
        grid=(tokens // step,),
        in_specs=[by_row(width)] * 2 + [part_spec(width, cols, i) for i in range(3)],
        out_specs=[by_row(cols)] * 3,
        out_shape=[jax.ShapeDtypeStruct((tokens, cols), LOW)] * 3,
        compiler_params=pltpu.CompilerParams(vmem_limit_bytes=60 << 20),
        cost_estimate=estimate(
            6 * tokens * width * cols, 2 * (2 * tokens * width + 3 * width * cols + 3 * tokens * cols)
        ),
    )(h, g, weight, weight, weight)


def first_grads_kernel(g, h, hid, gate, up, out):
    part = pl.program_id(0)
    for i, (left, right) in enumerate(((g, hid), (h, gate), (h, up))):

        @pl.when(part == i)
        def _():
            out[...] = dot_rows(left[...], right[...]).astype(LOW)


def first_grads(grad_rows, rows, hid, grad_gate, grad_up):
    tokens, width = rows.shape
    cols, tile = hid.shape[1], 256
    tiles = width // tile
    return pl.pallas_call(
        first_grads_kernel,
        grid=(3, tiles),
        in_specs=[
            pl.BlockSpec((tokens, tile), lambda p, i: (0, jnp.where(p == 0, i, tiles - 1))),
            pl.BlockSpec((tokens, tile), lambda p, i: (0, jnp.where(p == 0, 0, i))),
        ]
        + [whole_spec(tokens, cols, once=True)] * 3,
        out_specs=pl.BlockSpec((tile, cols), lambda p, i: (i, p)),
        out_shape=jax.ShapeDtypeStruct((width, 3 * cols), LOW),
        compiler_params=pltpu.CompilerParams(vmem_limit_bytes=60 << 20),
        cost_estimate=estimate(6 * tokens * width * cols, 6 * tokens * cols + 6 * width * cols),
    )(grad_rows, rows, hid, grad_gate, grad_up)


MESH_ID = pl.DeviceIdType.MESH


def meet(partners):
    barrier = pltpu.get_barrier_semaphore()
    for partner in partners:
        pl.semaphore_signal(barrier, inc=1, device_id=partner, device_id_type=MESH_ID)
    pl.semaphore_wait(barrier, len(partners))


def partners_of():
    tensor_rank, ctx_rank = lax.axis_index("tp"), lax.axis_index("ctx")
    return {"tp": tensor_rank ^ 1}, {"tp": tensor_rank ^ 2}, {"ctx": ctx_rank ^ 1}


def collect_kernel(
    slots, tiles, gate_a, up_a, gate_b, up_b, w_gate_a, w_up_a, w_gate_b, w_up_b, left, right, hid, up, total,
    down_out, up_out, parts, sent, core_in, across_in, last_in, held, send, recv, load
):
    step = pl.program_id(0)
    steps = pl.num_programs(0)
    core, far, side = partners_of()
    half = total.shape[0] // 2
    remote = remote_copy(send, recv)
    cores = [remote(sent.at[k % 2], core_in.at[k], k, core) for k in range(4)]
    across = [
        remote(parts.at[3, pl.ds(0, half)], across_in.at[0], 4, far),
        remote(parts.at[3, pl.ds(half, half)], across_in.at[1], 5, side),
    ]
    lasts = [
        remote(parts.at[1], last_in.at[0], 6, far),
        remote(parts.at[2, pl.ds(half, half)], last_in.at[1, pl.ds(half, half)], 7, side),
        remote(parts.at[2, pl.ds(0, half)], last_in.at[1, pl.ds(0, half)], 8, side),
    ]
    loading = [
        pltpu.make_async_copy(source, held.at[i], load.at[i]) for i, source in enumerate((hid, up))
    ]

    @pl.when(step == 0)
    def _():
        for copy in loading:
            copy.start()
        meet((core, far, side))

    for k in (2, 3):
        pl.when(step == 2 * k)(cores[k - 2].wait_send)

    @pl.when(step < slots)
    def _():
        part = (
            dot_cols(gate_a[...], w_gate_a[...])
            + dot_cols(up_a[...], w_up_a[...])
            + dot_cols(gate_b[...], w_gate_b[...])
            + dot_cols(up_b[...], w_up_b[...])
        )

        @pl.when(step == slots - 1)
        def _():
            total[...] = part

        for k in range(4):

            @pl.when(step == 2 * k)
            def _():
                sent[k % 2] = part.astype(LOW)
                cores[k].start()

            if k < 3:

                @pl.when(step == 2 * k + 1)
                def _():
                    cores[k].wait_recv()
                    parts[3 - k] = (part + core_in[k].astype(WIDE)).astype(LOW)

    def add(slot, rows, value):
        parts[slot, rows] = (parts[slot, rows].astype(WIDE) + value.astype(WIDE)).astype(LOW)

    low, high = pl.ds(0, half), pl.ds(half, half)

    @pl.when(step == 1)
    def _():
        for copy in across:
            copy.start()

    pl.when(step == 3)(lasts[1].start)

    @pl.when(step == 5)
    def _():
        across[1].wait_recv()
        add(1, high, across_in[1])
        lasts[0].start()
        across[0].wait_recv()
        add(2, low, across_in[0])
        lasts[2].start()

    @pl.when((step >= slots) & (step < slots + tiles))
    def _():
        pl.when(step == slots)(loading[0].wait)
        down_out[...] = dot_rows(left[...], held[0]).astype(LOW)

    @pl.when(step >= slots + tiles)
    def _():
        pl.when(step == slots + tiles)(loading[1].wait)
        up_out[...] = dot_rows(right[...], held[1]).astype(LOW)

    @pl.when(step == steps - 1)
    def _():
        cores[3].wait_recv()
        for copy in lasts:
            copy.wait_recv()
        total[...] += (
            core_in[3].astype(WIDE) + last_in[0].astype(WIDE) + last_in[1].astype(WIDE)
        )
        for copy in (*cores[2:], *across, *lasts):
            copy.wait_send()


def collect_back(first, second, weight_a, weight_b, grad_rows, rows, hid, length):
    tokens, cols_a = first[0].shape
    cols = second[0].shape[1]
    width = weight_a.shape[0]
    slots, tile = tokens // length, 256
    tiles = width // tile
    row = lambda n: pl.BlockSpec((length, n), lambda i: (jnp.maximum(slots - 1 - i, 0), 0))
    column = lambda i, start: jnp.clip(i - start, 0, tiles - 1)
    down_at, up_at = (lambda i: column(i, slots)), (lambda i: column(i, slots + tiles))
    return pl.pallas_call(
        functools.partial(collect_kernel, slots, tiles),
        grid=(slots + 2 * tiles,),
        in_specs=[row(cols_a), row(cols_a), row(cols), row(cols)]
        + [part_spec(width, cols_a, 1), part_spec(width, cols_a, 2)]
        + [part_spec(width, cols, 1), part_spec(width, cols, 2)]
        + [
            pl.BlockSpec((tokens, tile), lambda i: (0, down_at(i))),
            pl.BlockSpec((tokens, tile), lambda i: (0, up_at(i))),
            ANYWHERE,
            ANYWHERE,
        ],
        out_specs=[
            whole_spec(length, width, once=True),
            pl.BlockSpec((tile, cols), lambda i: (down_at(i), 0)),
            pl.BlockSpec((tile, cols), lambda i: (up_at(i), 0)),
        ],
        out_shape=[
            jax.ShapeDtypeStruct((length, width), WIDE),
            jax.ShapeDtypeStruct((width, cols), LOW),
            jax.ShapeDtypeStruct((width, cols), LOW),
        ],
        scratch_shapes=[
            pltpu.VMEM((4, length, width), LOW),
            pltpu.VMEM((2, length, width), LOW),
            pltpu.VMEM((4, length, width), LOW),
            pltpu.VMEM((2, length // 2, width), LOW),
            pltpu.VMEM((2, length, width), LOW),
            pltpu.VMEM((2, tokens, cols), LOW),
            pltpu.SemaphoreType.DMA((9,)),
            pltpu.SemaphoreType.DMA((9,)),
            pltpu.SemaphoreType.DMA((2,)),
        ],
        compiler_params=pltpu.CompilerParams(
            vmem_limit_bytes=63 << 20, collective_id=1, has_side_effects=True
        ),
        cost_estimate=estimate(6 * tokens * width * cols, 10 * tokens * cols),
    )(*first, *second, weight_a, weight_a, weight_b, weight_b, grad_rows, rows, hid, second[1])


def remote_copy(send, recv):
    def make(source, target, index, partner):
        return pltpu.make_async_remote_copy(
            source, target, send.at[index], recv.at[index], device_id=partner, device_id_type=MESH_ID
        )

    return make


def branch_kernel(
    slots, tiles, total, middle, own_grad, gain, hid_a, hid_b, w_a, w_b, turned, gate, grad_middle, gain_grad,
    gate_out, branch, mlp_own, mlp_far, mlp_side, own, parts, core_in, across_in, held, send, recv, load
):
    step = pl.program_id(0)
    core, far, side = partners_of()
    remote = remote_copy(send, recv)
    to_far = remote(own, branch.at[2], 0, far)
    to_near = remote(own, branch.at[1], 1, core)
    to_cross = remote(branch.at[2], branch.at[3], 2, core)
    keep = pltpu.make_async_copy(own, branch.at[0], load.at[0])
    loading = pltpu.make_async_copy(gate, held, load.at[1])
    cores = [remote(parts.at[7 - 2 * k], core_in.at[k], 3 + k, core) for k in range(4)]
    across = remote(parts.at[6], across_in, 7, side)
    stores = [
        pltpu.make_async_copy(parts.at[4], mlp_side, load.at[2]),
        pltpu.make_async_copy(parts.at[2], mlp_far, load.at[3]),
        pltpu.make_async_copy(parts.at[0], mlp_own, load.at[4]),
    ]

    @pl.when(step == 0)
    def _():
        loading.start()
        meet((core, far, side))
        values, upstream = middle[...], total[...]
        inverse = lax.rsqrt(jnp.mean(values * values, axis=-1, keepdims=True) + EPS)
        grad_in, gain_grad[...] = norm_backward(values, inverse, gain[...], upstream)
        grad_in = own_grad[...].astype(WIDE) + grad_in
        grad_middle[...] = grad_in
        own[...] = grad_in.astype(LOW)
        for copy in (to_far, to_near, keep):
            copy.start()

    @pl.when(step < slots)
    def _():
        part = dot_cols(hid_a[...], w_a[...]) + dot_cols(hid_b[...], w_b[...])
        parts[slots - 1 - step] = part.astype(LOW)

    for k in range(4):
        pl.when(step == 2 * k)(cores[k].start)

        def finish(k=k):
            slot = 6 - 2 * k
            cores[k].wait_recv()
            parts[slot] = (parts[slot].astype(WIDE) + core_in[k].astype(WIDE)).astype(LOW)
            if k == 0:
                across.start()
            if k == 1:
                stores[0].start()
            if k == 3:
                stores[2].start()

        pl.when(step == 2 * k + 1)(finish)

    @pl.when(step >= slots)
    def _():
        pl.when(step == slots)(loading.wait)
        gate_out[...] = dot_rows(turned[...], held[...]).astype(LOW)

    @pl.when(step == slots + tiles - 2)
    def _():
        to_far.wait_recv()
        to_cross.start()

    @pl.when(step == slots + tiles - 1)
    def _():
        to_near.wait_recv()
        to_cross.wait_recv()
        across.wait_recv()
        parts[2] = (parts[2].astype(WIDE) + across_in[...].astype(WIDE)).astype(LOW)
        stores[1].start()
        keep.wait()
        for copy in stores:
            copy.wait()
        for copy in (to_far, to_near, to_cross, *cores, across):
            copy.wait_send()


ANYWHERE = pl.BlockSpec(memory_space=pl.ANY)


def spread_branch(total, middle, own_grad, gain, hid_a, hid_b, weight_a, weight_b, rows, grad_gate):
    length, width = total.shape
    tokens, cols = grad_gate.shape
    slots, tile = tokens // length, 256
    tiles = width // tile
    once = whole_spec(length, width, once=True)
    column = lambda i: jnp.clip(i - slots, 0, tiles - 1)
    part = jax.ShapeDtypeStruct((length, width), LOW)
    return pl.pallas_call(
        functools.partial(branch_kernel, slots, tiles),
        grid=(slots + tiles,),
        in_specs=[
            once,
            once,
            once,
            whole_spec(1, width),
            pl.BlockSpec((length, hid_a.shape[1]), lambda i: (jnp.maximum(slots - 1 - i, 0), 0)),
            pl.BlockSpec((length, cols), lambda i: (jnp.maximum(slots - 1 - i, 0), 0)),
            part_spec(width, hid_a.shape[1], 0),
            part_spec(width, cols, 0),
            pl.BlockSpec((tokens, tile), lambda i: (0, column(i))),
            ANYWHERE,
        ],
        out_specs=[
            whole_spec(length, width, once=True),
            whole_spec(1, width),
            pl.BlockSpec((tile, cols), lambda i: (column(i), 0)),
        ]
        + [ANYWHERE] * 4,
        out_shape=[
            jax.ShapeDtypeStruct((length, width), WIDE),
            jax.ShapeDtypeStruct((1, width), WIDE),
            jax.ShapeDtypeStruct((width, cols), LOW),
            jax.ShapeDtypeStruct((4, length, width), LOW),
            part,
            part,
            part,
        ],
        scratch_shapes=[
            pltpu.VMEM((length, width), LOW),
            pltpu.VMEM((slots, length, width), LOW),
            pltpu.VMEM((4, length, width), LOW),
            pltpu.VMEM((length, width), LOW),
            pltpu.VMEM((tokens, cols), LOW),
            pltpu.SemaphoreType.DMA((8,)),
            pltpu.SemaphoreType.DMA((8,)),
            pltpu.SemaphoreType.DMA((5,)),
        ],
        compiler_params=pltpu.CompilerParams(
            vmem_limit_bytes=63 << 20, collective_id=2, has_side_effects=True
        ),
        cost_estimate=estimate(4 * tokens * width * cols, 10 * tokens * cols),
    )(total, middle, own_grad, gain, hid_a, hid_b, weight_a, weight_b, rows, grad_gate)


def line_kernel(
    slots, tiles, line, weight, own_in, grad_middle, gain, gain_two, rows_one, line_all, block, share,
    gain_grad, attn_out, bias_out, home, parts, core_in, far_in, total, gains, gains_in, send, recv, load
):
    step = pl.program_id(0)
    core, far, _ = partners_of()
    tensor_rank, group = lax.axis_index("tp"), lax.axis_index("fsdp")
    shift = (tensor_rank % 2) * 2 + tensor_rank // 2
    target = {"fsdp": (group + slots - shift) % slots}
    source = {"fsdp": (group + shift) % slots}
    stays = shift == 0
    remote = remote_copy(send, recv)
    cores = [remote(parts.at[3 - 2 * k], core_in.at[k], k, core) for k in range(2)]
    to_far = remote(parts.at[2], far_in, 2, far)
    leave = remote(block, home, 3, target)
    keep = pltpu.make_async_copy(block, home, load)
    cross = {"tp": tensor_rank ^ 3}
    gain_copies = [
        remote(gains, gains_in.at[i], 4 + i, partner) for i, partner in enumerate((core, far, cross))
    ]

    @pl.when(step == 0)
    def _():
        barrier = pltpu.get_barrier_semaphore()
        for partner in (core, far, cross):
            pl.semaphore_signal(barrier, inc=1, device_id=partner, device_id_type=MESH_ID)

        @pl.when(stays)
        def _():
            pl.semaphore_wait(barrier, 3)
            keep.start()

        @pl.when(jnp.logical_not(stays))
        def _():
            for partner in (target, source):
                pl.semaphore_signal(barrier, inc=1, device_id=partner, device_id_type=MESH_ID)
            pl.semaphore_wait(barrier, 5)
            leave.start()

    @pl.when(step < slots)
    def _():
        part = dot_cols(line[...], weight[...])
        parts[slots - 1 - step] = part.astype(LOW)

        @pl.when(step == slots - 1)
        def _():
            total[...] = part

    for k in range(2):
        pl.when(step == 2 * k)(cores[k].start)

    @pl.when(step == 1)
    def _():
        cores[0].wait_recv()
        parts[2] = (parts[2].astype(WIDE) + core_in[0].astype(WIDE)).astype(LOW)
        to_far.start()

    @pl.when(step == slots - 1)
    def _():
        bias_out[...] = jnp.sum(line_all[...].astype(WIDE), axis=0, keepdims=True)

    @pl.when(step >= slots)
    def _():
        attn_out[...] = dot_rows(rows_one[...], line_all[...]).astype(LOW)

    @pl.when(step == slots + tiles - 1)
    def _():
        cores[1].wait_recv()
        to_far.wait_recv()
        upstream = total[...] + core_in[1].astype(WIDE) + far_in[...].astype(WIDE)
        values = own_in[...].astype(WIDE)
        inverse = lax.rsqrt(jnp.mean(values * values, axis=-1, keepdims=True) + EPS)
        grad_in, gain_one = norm_backward(values, inverse, gain[...], upstream)
        gains[0:1] = gain_one
        gains[1:2] = gain_two[...]
        for copy in gain_copies:
            copy.start()
        share[...] = (grad_middle[...] + grad_in).astype(LOW)
        for copy in gain_copies:
            copy.wait_recv()
        gain_grad[...] = (gains[...] + gains_in[0]) + (gains_in[1] + gains_in[2])
        for copy in (*cores, to_far, *gain_copies):
            copy.wait_send()
        pl.when(stays)(keep.wait)

        @pl.when(jnp.logical_not(stays))
        def _():
            leave.wait_recv()
            leave.wait_send()


def finish_rows(line, weight, own_in, grad_middle, gain, gain_two, rows_one, block):
    length, width = own_in.shape
    near_tokens, line_cols = line.shape
    slots, tile = near_tokens // length, 256
    tiles = width // tile
    once = whole_spec(length, width, once=True)
    column = lambda i: jnp.clip(i - slots, 0, tiles - 1)
    by_column = lambda n: pl.BlockSpec((n, tile), lambda i: (0, column(i)))
    attn_cols = line_cols
    return pl.pallas_call(
        functools.partial(line_kernel, slots, tiles),
        grid=(slots + tiles,),
        in_specs=[
            pl.BlockSpec((length, line_cols), lambda i: (jnp.maximum(slots - 1 - i, 0), 0)),
            whole_spec(width, line_cols, once=True),
            once,
            once,
            whole_spec(1, width),
            whole_spec(1, width),
            by_column(near_tokens),
            whole_spec(near_tokens, line_cols, once=True),
            ANYWHERE,
        ],
        out_specs=[
            whole_spec(length, width),
            whole_spec(2, width),
            pl.BlockSpec((tile, attn_cols), lambda i: (column(i), 0)),
            whole_spec(1, line_cols),
            ANYWHERE,
        ],
        out_shape=[
            jax.ShapeDtypeStruct((length, width), LOW),
            jax.ShapeDtypeStruct((2, width), WIDE),
            jax.ShapeDtypeStruct((width, attn_cols), LOW),
            jax.ShapeDtypeStruct((1, line_cols), WIDE),
            jax.ShapeDtypeStruct((length, width), LOW),
        ],
        scratch_shapes=[
            pltpu.VMEM((slots, length, width), LOW),
            pltpu.VMEM((2, length, width), LOW),
            pltpu.VMEM((length, width), LOW),
            pltpu.VMEM((length, width), WIDE),
            pltpu.VMEM((2, width), WIDE),
            pltpu.VMEM((3, 2, width), WIDE),
            pltpu.SemaphoreType.DMA((7,)),
            pltpu.SemaphoreType.DMA((7,)),
            pltpu.SemaphoreType.DMA,
        ],
        compiler_params=pltpu.CompilerParams(
            vmem_limit_bytes=63 << 20, collective_id=3, has_side_effects=True
        ),
        cost_estimate=estimate(2 * near_tokens * width * attn_cols, 10 * near_tokens * width),
    )(line, weight, own_in, grad_middle, gain, gain_two, rows_one, line, block)


def place_kernel(count, info, *refs):
    out = refs[count]
    for r in range(count):

        @pl.when(pl.program_id(0) == r)
        def _():
            out[0] = refs[r][...]


def place_rows(rows, order):
    length, width = rows[0].shape
    count = len(rows)
    held = pl.BlockSpec((length, width), lambda s, info: (0, 0), pipeline_mode=pl.Buffered(1))
    return pl.pallas_call(
        functools.partial(place_kernel, count),
        grid_spec=pltpu.PrefetchScalarGridSpec(
            num_scalar_prefetch=1,
            grid=(count,),
            in_specs=[held] * count,
            out_specs=pl.BlockSpec((1, length, width), lambda s, info: (info[s], 0, 0)),
        ),
        out_shape=jax.ShapeDtypeStruct((count, length, width), LOW),
        compiler_params=pltpu.CompilerParams(vmem_limit_bytes=32 << 20),
        cost_estimate=estimate(0, 4 * count * length * width),
    )(order, *rows)


def turn(values, cosine, sine_signed):
    return values * cosine + pltpu.roll(values, values.shape[-1] // 2, 1) * sine_signed


def turn_back(values, cosine, sine_signed):
    return values * cosine - pltpu.roll(values, values.shape[-1] // 2, 1) * sine_signed


def project_kernel(
    heads, head_dim, x0, x1, x2, x3, gains, weight, bias, cosine, sine, h_out, q_out, k_out, v_out, gain
):
    slot = pl.program_id(0)

    @pl.when(slot == 0)
    def _():
        gain[...] = gains[...].astype(WIDE).T[:8]


    def run(x_ref):
        x = x_ref[...].astype(WIDE)
        scale_inv = lax.rsqrt(jnp.mean(x * x, axis=-1, keepdims=True) + EPS)
        normed = (x * scale_inv * gain[0:1]).astype(LOW)
        h_out[0] = normed
        lin = jnp.dot(normed, weight[...], preferred_element_type=WIDE) + bias[...]
        cos, sin = cosine[0], sine[0]
        for h in range(heads + 1):
            part = turn(lin[:, h * head_dim : (h + 1) * head_dim], cos, sin).astype(LOW)
            if h < heads:
                q_out[0, :, h * head_dim : (h + 1) * head_dim] = part
            else:
                k_out[0] = part
        v_out[0] = lin[:, (heads + 1) * head_dim :].astype(LOW)

    for r, x_ref in enumerate((x0, x1, x2, x3)):
        pl.when(slot == r)(functools.partial(run, x_ref))


def project(rows, held, bias, cosine, sine, heads, head_dim):
    length, width = rows[0].shape
    count = len(rows)
    cols = (heads + 2) * head_dim
    whole = whole_spec
    by_slot = lambda *shape: pl.BlockSpec((1, *shape), lambda s: (s,) + (0,) * len(shape))
    return pl.pallas_call(
        functools.partial(project_kernel, heads, head_dim),
        grid=(count,),
        in_specs=[whole(length, width)] * count
        + [part_spec(width, 128, cols // 128), part_spec(width, cols, 0), whole(1, cols)]
        + [by_slot(length, head_dim)] * 2,
        out_specs=[
            by_slot(length, width),
            by_slot(length, heads * head_dim),
            by_slot(length, head_dim),
            by_slot(length, head_dim),
        ],
        out_shape=[
            jax.ShapeDtypeStruct((count, length, width), LOW),
            jax.ShapeDtypeStruct((count, length, heads * head_dim), LOW),
            jax.ShapeDtypeStruct((count, length, head_dim), LOW),
            jax.ShapeDtypeStruct((count, length, head_dim), LOW),
        ],
        scratch_shapes=[pltpu.VMEM((8, width), WIDE)],
        compiler_params=pltpu.CompilerParams(vmem_limit_bytes=56 << 20),
        cost_estimate=pl.CostEstimate(
            flops=2 * count * length * width * cols,
            bytes_accessed=count * length * (2 * width + cols) * 2 + width * cols * 2,
            transcendentals=0,
        ),
    )(*rows, held, held, bias, cosine, sine)


def row_blocks(length):
    return [(i, min(256, length)) for i in range(0, length, min(256, length))]


def key_biases(length, offset, start, rows, past, keys):
    past_pos = lax.broadcasted_iota(jnp.int32, (1, past), 1)
    past_bias = jnp.where((past_pos < offset) & (past_pos < length), 0.0, NEG_FILL)
    query_pos = offset + start + lax.broadcasted_iota(jnp.int32, (rows, keys), 0)
    own_pos = offset + lax.broadcasted_iota(jnp.int32, (rows, keys), 1)
    own_bias = jnp.where((own_pos <= query_pos) & (own_pos < length), 0.0, NEG_FILL)
    return past_bias, own_bias


def dot_cols(left, right):
    return lax.dot_general(left, right, (((1,), (1,)), ((), ())), preferred_element_type=WIDE)


def dot_rows(left, right):
    return lax.dot_general(left, right, (((0,), (0,)), ((), ())), preferred_element_type=WIDE)


def attend_rows(
    heads, head_dim, scale, length, offset, q, k_past, v_past, k_own, v_own, weight, out, lse, put
):
    past = k_past.shape[1]
    for start, rows in row_blocks(q.shape[1]):
        keys = start + rows
        past_bias, own_bias = key_biases(length, offset, start, rows, past, keys)
        here = slice(start, start + rows)
        for h in range(heads):
            cols = slice(h * head_dim, (h + 1) * head_dim)
            query = q[0, here, cols]
            s_past = dot_cols(query, k_past[0]) * scale + past_bias
            s_own = dot_cols(query, k_own[0, :keys]) * scale + own_bias
            top = jnp.maximum(
                jnp.max(s_past, axis=1, keepdims=True), jnp.max(s_own, axis=1, keepdims=True)
            )
            e_past, e_own = jnp.exp(s_past - top), jnp.exp(s_own - top)
            total = jnp.sum(e_past, axis=1, keepdims=True) + jnp.sum(e_own, axis=1, keepdims=True)
            inverse = 1.0 / total
            mixed = jnp.dot(
                (e_past * inverse).astype(LOW), v_past[0], preferred_element_type=WIDE
            ) + jnp.dot((e_own * inverse).astype(LOW), v_own[0, :keys], preferred_element_type=WIDE)
            out[0, here, cols] = mixed.astype(LOW)
            lse[0, here, h : h + 1] = top + jnp.log(total)
        rows_out = dot_cols(out[0, here], weight[...]).astype(LOW)
        put(here, rows_out)


def attend_kernel(
    heads, head_dim, scale, first, total_slots, info, q, k_past, v_past, k_own, v_own, weight, out, lse, *parts
):
    length, offset = info[first + pl.program_id(0)], info[total_slots]

    def put(here, value):
        for i, part in enumerate(parts):

            @pl.when(pl.program_id(0) == i)
            def _():
                part[here] = value

    attend_rows(heads, head_dim, scale, length, offset, q, k_past, v_past, k_own, v_own, weight, out, lse, put)


def attend_forward(info, q, k_past, v_past, k_own, v_own, weight, heads, head_dim, scale, first, count):
    _, length, width = q.shape
    past = k_past.shape[1]
    by_slot = lambda *shape: pl.BlockSpec((1, *shape), lambda s, info: (first + s,) + (0,) * len(shape))
    out_slot = lambda *shape: pl.BlockSpec((1, *shape), lambda s, info: (s,) + (0,) * len(shape))
    keys = count * length * (past + length) * heads
    return pl.pallas_call(
        functools.partial(attend_kernel, heads, head_dim, scale, first, q.shape[0]),
        grid_spec=pltpu.PrefetchScalarGridSpec(
            num_scalar_prefetch=1,
            grid=(count,),
            in_specs=[
                by_slot(length, width),
                by_slot(past, head_dim),
                by_slot(past, head_dim),
                by_slot(length, head_dim),
                by_slot(length, head_dim),
                whole_spec(*weight.shape, once=True),
            ],
            out_specs=[out_slot(length, width), out_slot(length, 128)]
            + [whole_spec(length, weight.shape[0])] * count,
        ),
        out_shape=[
            jax.ShapeDtypeStruct((count, length, width), LOW),
            jax.ShapeDtypeStruct((count, length, 128), WIDE),
        ]
        + [jax.ShapeDtypeStruct((length, weight.shape[0]), LOW)] * count,
        compiler_params=pltpu.CompilerParams(vmem_limit_bytes=56 << 20),
        cost_estimate=estimate(4 * keys * head_dim, 4 * count * length * width, keys),
    )(info, q, k_past, v_past, k_own, v_own, weight)


def attend_back_rows(
    heads, head_dim, scale, length, offset, q, k_past, v_past, k_own, v_own, grad, lse, cosine, sine, put,
    dk_past, dk_own, dv_past, dv_own
):
    past = k_past.shape[1]
    for start, rows in row_blocks(q.shape[1]):
        keys = start + rows
        past_bias, own_bias = key_biases(length, offset, start, rows, past, keys)
        here = slice(start, start + rows)
        cos, sin = cosine[0, here], sine[0, here]
        for h in range(heads):
            cols = slice(h * head_dim, (h + 1) * head_dim)
            query, upstream = q[0, here, cols], grad[0, here, cols]
            log_total = lse[0, here, h : h + 1]
            p_past = jnp.exp(dot_cols(query, k_past[0]) * scale + past_bias - log_total)
            p_own = jnp.exp(dot_cols(query, k_own[0, :keys]) * scale + own_bias - log_total)
            g_past = dot_cols(upstream, v_past[0])
            g_own = dot_cols(upstream, v_own[0, :keys])
            row_dot = jnp.sum(p_past * g_past, axis=1, keepdims=True) + jnp.sum(
                p_own * g_own, axis=1, keepdims=True
            )
            s_past = (p_past * (g_past - row_dot)).astype(LOW)
            s_own = (p_own * (g_own - row_dot)).astype(LOW)
            dq = (
                jnp.dot(s_past, k_past[0], preferred_element_type=WIDE)
                + jnp.dot(s_own, k_own[0, :keys], preferred_element_type=WIDE)
            ) * scale
            put(here, cols, turn_back(dq, cos, sin).astype(LOW))
            dk_past[...] += dot_rows(s_past, query)
            dk_own[:keys] += dot_rows(s_own, query)
            dv_past[...] += dot_rows(p_past.astype(LOW), upstream)
            dv_own[:keys] += dot_rows(p_own.astype(LOW), upstream)


def attend_back_kernel(
    heads,
    head_dim,
    scale,
    info,
    q,
    k_past,
    v_past,
    k_own,
    v_own,
    grad,
    lse,
    cosine,
    sine,
    dq_out,
    mine_past,
    mine_own,
    other_past,
    other_own,
    dk_past,
    dk_own,
    dv_past,
    dv_own,
):
    slot = pl.program_id(0)
    length, offset = info[slot], info[pl.num_programs(0)]
    parity = info[pl.num_programs(0) + 1]
    for total in (dk_past, dk_own, dv_past, dv_own):
        total[...] = jnp.zeros_like(total)
    attend_back_rows(
        heads, head_dim, scale, length, offset, q, k_past, v_past, k_own, v_own, grad, lse, cosine, sine,
        lambda here, cols, value: dq_out.__setitem__((0, here, cols), value),
        dk_past, dk_own, dv_past, dv_own,
    )

    @pl.when(parity == 0)
    def _():
        mine_past[0] = dk_past[...] * scale
        mine_own[0] = dk_own[...] * scale
        other_past[0] = dv_past[...]
        other_own[0] = dv_own[...]

    @pl.when(parity != 0)
    def _():
        mine_past[0] = dv_past[...]
        mine_own[0] = dv_own[...]
        other_past[0] = dk_past[...] * scale
        other_own[0] = dk_own[...] * scale


def attend_backward(
    info, q, k_past, v_past, k_own, v_own, grad, lse, cosine, sine, heads, head_dim, scale
):
    count, length, width = q.shape
    past = k_past.shape[1]
    by_slot = lambda *shape: pl.BlockSpec((1, *shape), lambda s, info: (s,) + (0,) * len(shape))
    keys = count * length * (past + length) * heads
    return pl.pallas_call(
        functools.partial(attend_back_kernel, heads, head_dim, scale),
        grid_spec=pltpu.PrefetchScalarGridSpec(
            num_scalar_prefetch=1,
            grid=(count,),
            in_specs=[
                by_slot(length, width),
                by_slot(past, head_dim),
                by_slot(past, head_dim),
                by_slot(length, head_dim),
                by_slot(length, head_dim),
                by_slot(length, width),
                by_slot(length, 128),
                by_slot(length, head_dim),
                by_slot(length, head_dim),
            ],
            out_specs=[
                by_slot(length, width),
                by_slot(past, head_dim),
                by_slot(length, head_dim),
                by_slot(past, head_dim),
                by_slot(length, head_dim),
            ],
            scratch_shapes=[
                pltpu.VMEM((past, head_dim), WIDE),
                pltpu.VMEM((length, head_dim), WIDE),
                pltpu.VMEM((past, head_dim), WIDE),
                pltpu.VMEM((length, head_dim), WIDE),
            ],
        ),
        out_shape=[
            jax.ShapeDtypeStruct((count, length, width), LOW),
            jax.ShapeDtypeStruct((count, past, head_dim), WIDE),
            jax.ShapeDtypeStruct((count, length, head_dim), WIDE),
            jax.ShapeDtypeStruct((count, past, head_dim), WIDE),
            jax.ShapeDtypeStruct((count, length, head_dim), WIDE),
        ],
        compiler_params=pltpu.CompilerParams(vmem_limit_bytes=56 << 20),
        cost_estimate=estimate(10 * keys * head_dim, 8 * count * length * width, keys),
    )(info, q, k_past, v_past, k_own, v_own, grad, lse, cosine, sine)


def attend_sum_kernel(
    heads, head_dim, scale, slots, info, q, k_past, v_past, k_own, v_own, weight, own_in, gain, out, lse, middle,
    normed, parts, core_in, far_in, send, recv
):
    step = pl.program_id(0)
    slot = slots - 1 - step
    core, far, _ = partners_of()
    remote = remote_copy(send, recv)
    cores = [remote(parts.at[3 - 2 * k], core_in.at[k], k, core) for k in range(2)]
    to_far = remote(parts.at[2], far_in, 2, far)

    @pl.when(step == 0)
    def _():
        meet((core, far))

    def put(here, value):
        parts[slot, here] = value

    offset = lax.axis_index("ctx") * q.shape[1]
    attend_rows(
        heads, head_dim, scale, info[slot], offset, q, k_past, v_past, k_own, v_own, weight, out, lse, put
    )
    for k in range(2):
        pl.when(step == 2 * k)(cores[k].start)

    @pl.when(step == 1)
    def _():
        cores[0].wait_recv()
        parts[2] = (parts[2].astype(WIDE) + core_in[0].astype(WIDE)).astype(LOW)
        to_far.start()

    @pl.when(step == slots - 1)
    def _():
        cores[1].wait_recv()
        to_far.wait_recv()
        rows = own_in[...].astype(WIDE) + parts[0].astype(WIDE)
        rows = rows + core_in[1].astype(WIDE) + far_in[...].astype(WIDE)
        middle[...] = rows
        inverse = lax.rsqrt(jnp.mean(rows * rows, axis=-1, keepdims=True) + EPS)
        normed[...] = (rows * inverse * gain[...]).astype(LOW)
        for copy in (*cores, to_far):
            copy.wait_send()


def attend_sum(info, q, k_past, v_past, k_own, v_own, weight, own_in, gain, heads, head_dim, scale):
    count, length, width = q.shape
    past, model_width = k_past.shape[1], own_in.shape[1]
    by_slot = lambda *shape: pl.BlockSpec(
        (1, *shape), lambda i, info: (count - 1 - i,) + (0,) * len(shape)
    )
    keys = count * length * (past + length) * heads
    return pl.pallas_call(
        functools.partial(attend_sum_kernel, heads, head_dim, scale, count),
        grid_spec=pltpu.PrefetchScalarGridSpec(
            num_scalar_prefetch=1,
            grid=(count,),
            in_specs=[
                by_slot(length, width),
                by_slot(past, head_dim),
                by_slot(past, head_dim),
                by_slot(length, head_dim),
                by_slot(length, head_dim),
                whole_spec(*weight.shape, once=True),
                whole_spec(length, model_width, once=True),
                whole_spec(1, model_width),
            ],
            out_specs=[
                by_slot(length, width),
                by_slot(length, 128),
                whole_spec(length, model_width, once=True),
                whole_spec(length, model_width, once=True),
            ],
            scratch_shapes=[
                pltpu.VMEM((count, length, model_width), LOW),
                pltpu.VMEM((2, length, model_width), LOW),
                pltpu.VMEM((length, model_width), LOW),
                pltpu.SemaphoreType.DMA((3,)),
                pltpu.SemaphoreType.DMA((3,)),
            ],
        ),
        out_shape=[
            jax.ShapeDtypeStruct((count, length, width), LOW),
            jax.ShapeDtypeStruct((count, length, 128), WIDE),
            jax.ShapeDtypeStruct((length, model_width), WIDE),
            jax.ShapeDtypeStruct((length, model_width), LOW),
        ],
        compiler_params=pltpu.CompilerParams(
            vmem_limit_bytes=56 << 20, collective_id=5, has_side_effects=True
        ),
        cost_estimate=estimate(4 * keys * head_dim, 4 * count * length * width, keys),
    )(info, q, k_past, v_past, k_own, v_own, weight, own_in, gain)


def exchange_kernel(
    heads, head_dim, scale, slots, tiles, info, q, k_past, v_past, k_own, v_own, rows, weight, lse, cosine, sine,
    cosine_all, sine_all, branch, mixed, mlp_far, mlp_side, mlp_own, middle, line, out_grad, block, mine_past,
    mine_own, other_past, other_own, got_past, got_own, side_out, side_in, dk_past, dk_own, dv_past, dv_own,
    own_rows, last_in, grad, send, recv, load
):
    step = pl.program_id(0)
    tensor_rank = lax.axis_index("tp")
    core, far, side = partners_of()
    parity = lax.rem(tensor_rank, 2)
    offset = lax.axis_index("ctx") * q.shape[1]
    remote = remote_copy(send, recv)
    pasts = [remote(other_past.at[r], got_past.at[r ^ 1], r, core) for r in range(slots)]
    owns = [remote(other_own.at[r], got_own.at[r ^ 1], slots + r, core) for r in range(slots)]
    sides = [remote(side_out.at[r], side_in.at[r], 2 * slots + r, side) for r in range(slots)]
    lasts = [
        remote(mlp_far, last_in.at[0], 3 * slots, far),
        remote(mlp_side, last_in.at[1], 3 * slots + 1, side),
    ]
    loading = pltpu.make_async_copy(mlp_own, own_rows, load)

    @pl.when(step == 0)
    def _():
        loading.start()
        meet((core, far, side))
        for copy in lasts:
            copy.start()

    @pl.when(step < slots)
    def _():
        length = info[jnp.minimum(step, slots - 1)]
        for total in (dk_past, dk_own, dv_past, dv_own):
            total[...] = jnp.zeros_like(total)
        grad[0] = jnp.dot(rows[...], weight[...], preferred_element_type=WIDE).astype(LOW)
        attend_back_rows(
            heads, head_dim, scale, length, offset, q, k_past, v_past, k_own, v_own, grad, lse, cosine,
            sine, lambda here, cols, value: line.__setitem__((step, here, cols), value),
            dk_past, dk_own, dv_past, dv_own,
        )

        @pl.when(parity == 0)
        def _():
            mine_past[step] = dk_past[...] * scale
            mine_own[step] = dk_own[...] * scale
            other_past[step] = dv_past[...]
            other_own[step] = dv_own[...]

        @pl.when(parity != 0)
        def _():
            mine_past[step] = dv_past[...]
            mine_own[step] = dv_own[...]
            other_past[step] = dk_past[...] * scale
            other_own[step] = dk_own[...] * scale

    for r in range(slots):

        def start(r=r):
            pasts[r].start()
            owns[r].start()

        pl.when(step == r)(start)

    for pair in range(0, slots, 2):

        def merge(pair=pair):
            for r in (pair, pair + 1):
                pasts[r ^ 1].wait_recv()
                side_out[r] = (mine_past[r] + got_past[r]).astype(LOW)
                sides[r].start()

        pl.when(step == pair + 1)(merge)

    @pl.when(step >= slots)
    def _():
        out_grad[...] = dot_rows(branch[...], mixed[...]).astype(LOW)

    @pl.when(step == slots + tiles - 1)
    def _():
        for r in range(slots):
            owns[r ^ 1].wait_recv()
            sides[r].wait_recv()
            total = mine_own[r] + got_own[r] + side_in[r].astype(WIDE)
            back = turn_back(total, cosine_all[r], sine_all[r])
            line[r, :, heads * head_dim :] = jnp.where(parity == 0, back, total).astype(LOW)
        loading.wait()
        for copy in lasts:
            copy.wait_recv()
        block[...] = (
            middle[...] + own_rows[...].astype(WIDE) + last_in[0].astype(WIDE) + last_in[1].astype(WIDE)
        ).astype(LOW)
        for copy in (*pasts, *owns, *sides, *lasts):
            copy.wait_send()


def attend_exchange(
    info, q, k_past, v_past, k_own, v_own, weight, lse, cosine, sine, heads, head_dim, scale, branch, mixed, mlp,
    middle
):
    count, length, width = q.shape
    past = k_past.shape[1]
    tokens, model_width = branch.shape
    tile = 256
    tiles = model_width // tile
    slot = lambda i: jnp.minimum(i, count - 1)
    by_slot = lambda *shape: pl.BlockSpec((1, *shape), lambda i, info: (slot(i),) + (0,) * len(shape))
    column = lambda i: jnp.clip(i - count, 0, tiles - 1)
    held = lambda *shape: pl.BlockSpec(
        shape, lambda i, info: (0,) * len(shape), pipeline_mode=pl.Buffered(1)
    )
    line_cols = width + head_dim
    return pl.pallas_call(
        functools.partial(exchange_kernel, heads, head_dim, scale, count, tiles),
        grid_spec=pltpu.PrefetchScalarGridSpec(
            num_scalar_prefetch=1,
            grid=(count + tiles,),
            in_specs=[
                by_slot(length, width),
                by_slot(past, head_dim),
                by_slot(past, head_dim),
                by_slot(length, head_dim),
                by_slot(length, head_dim),
                pl.BlockSpec((length, model_width), lambda i, info: (slot(i), 0)),
                held(*weight.shape),
                by_slot(length, 128),
                by_slot(length, head_dim),
                by_slot(length, head_dim),
                held(count, length, head_dim),
                held(count, length, head_dim),
                pl.BlockSpec((tokens, tile), lambda i, info: (0, column(i))),
                held(*mixed.shape),
            ]
            + [ANYWHERE] * 3
            + [held(length, model_width)],
            out_specs=[
                held(count, length, line_cols),
                pl.BlockSpec((tile, width), lambda i, info: (column(i), 0)),
                held(length, model_width),
            ],
            scratch_shapes=[pltpu.VMEM((count, length, head_dim), WIDE)] * 6
            + [pltpu.VMEM((count, length, head_dim), LOW)] * 2
            + [pltpu.VMEM((length, head_dim), WIDE)] * 4
            + [
                pltpu.VMEM((length, model_width), LOW),
                pltpu.VMEM((2, length, model_width), LOW),
                pltpu.VMEM((1, length, width), LOW),
                pltpu.SemaphoreType.DMA((3 * count + 2,)),
                pltpu.SemaphoreType.DMA((3 * count + 2,)),
                pltpu.SemaphoreType.DMA,
            ],
        ),
        out_shape=[
            jax.ShapeDtypeStruct((count, length, line_cols), LOW),
            jax.ShapeDtypeStruct((model_width, width), LOW),
            jax.ShapeDtypeStruct((length, model_width), LOW),
        ],
        compiler_params=pltpu.CompilerParams(
            vmem_limit_bytes=63 << 20, collective_id=4, has_side_effects=True
        ),
        cost_estimate=estimate(2 * tokens * model_width * width, 10 * tokens * width),
    )(info, q, k_past, v_past, k_own, v_own, branch, weight, lse, cosine, sine, cosine, sine, branch, mixed, *mlp, middle)


def local(
    hidden_in,
    cotangent,
    seq_lengths,
    positions,
    permutation,
    query_weight,
    keyval_weight,
    output_weight,
    norm_gains,
    bias_query,
    bias_keyval,
    gate_weight,
    up_weight,
    down_weight,
):
    group_rank = lax.axis_index("fsdp")
    ctx_rank = lax.axis_index("ctx")
    tensor_rank = lax.axis_index("tp")
    fsdp_count = lax.axis_size("fsdp")
    ctx_count = lax.axis_size("ctx")
    tensor_count = lax.axis_size("tp")
    seq_grp, local_len, model_width = hidden_in.shape
    heads, head_dim = bias_query.shape
    keyval_heads = bias_keyval.shape[0] // 2
    assert seq_grp == tensor_count == fsdp_count == len(DEAL_SHIFT)
    token_count = seq_grp * local_len
    scale = 1.0 / math.sqrt(head_dim)
    offset = ctx_rank * local_len
    head_pair = tensor_rank // (tensor_count // keyval_heads)
    parity = tensor_rank % 2
    assert DEAL_SHIFT == tuple((t % 2) * 2 + t // 2 for t in range(tensor_count))

    entry = jnp.arange(permutation.shape[0])
    entry_group, entry_slot = entry // seq_grp, entry % seq_grp
    home_group, home_slot = lax.div(permutation, seq_grp), lax.rem(permutation, seq_grp)
    places = jnp.arange(2 * seq_grp)
    near_places = places < seq_grp
    slot_rank = tensor_rank ^ (places % seq_grp)
    shift_of = lambda rank: lax.rem(rank, 2) * 2 + lax.div(rank, 2)
    target = lax.rem(group_rank + shift_of(tensor_rank), fsdp_count)
    leaving = jnp.sum(jnp.where((entry_group == target) & (home_group == group_rank), home_slot, 0))
    source = lax.rem(group_rank + fsdp_count - shift_of(slot_rank), fsdp_count)
    hit = (entry_group == group_rank)[None] & (home_group[None] == source[:, None])
    slot_now = jnp.sum(jnp.where(hit, entry_slot[None], 0), axis=1)
    seq_now = jnp.sum(jnp.where(hit, permutation[None], 0), axis=1)
    targets = lax.rem(group_rank + shift_of(slot_rank), fsdp_count)
    back_hit = (entry_group[None] == targets[:, None]) & (home_group == group_rank)[None]
    home_order = jnp.sum(jnp.where(back_hit, home_slot[None], 0), axis=1)[:seq_grp]
    there = [
        (f * tensor_count + t, (f + DEAL_SHIFT[t]) % fsdp_count * tensor_count + t)
        for f in range(fsdp_count)
        for t in range(tensor_count)
    ]
    back = [(target, source) for source, target in there]

    split = units_split()
    head_width = 2 * head_dim
    query_cols = heads * head_dim
    near_cols = query_cols + head_width + 128

    outgoing = lax.dynamic_index_in_dim(hidden_in, leaving, 0, keepdims=False)
    own_in = lax.ppermute(outgoing, ("fsdp", "tp"), there)
    small = jnp.concatenate(
        [
            query_weight,
            lax.dynamic_slice_in_dim(keyval_weight, head_pair * head_width, head_width, axis=1),
            jnp.pad(norm_gains.T, ((0, 0), (0, 128 - norm_gains.shape[0]))),
            output_weight.T,
        ],
        axis=1,
    )
    seq_hit = seq_now[:, None] == entry[None]
    lengths_now = jnp.sum(jnp.where(seq_hit, seq_lengths[None], 0), axis=1)
    more = jnp.where(places == seq_grp, offset, jnp.where(places == seq_grp + 1, parity, 0))
    info = jnp.where(near_places, lengths_now, more).astype(jnp.int32)
    positions_now = jnp.sum(
        jnp.where(seq_hit[:seq_grp, :, None], positions[None], 0), axis=1
    )
    lane = jnp.arange(head_dim)
    frequency = 1.0 / ROPE_BASE ** ((lane % (head_dim // 2)).astype(WIDE) * 2.0 / head_dim)
    angles = positions_now.astype(WIDE)[..., None] * frequency
    cosine = jnp.cos(angles)
    sine = jnp.sin(angles) * jnp.where(lane < head_dim // 2, -1.0, 1.0)
    pick_info = jnp.where(near_places, slot_now, slot_now ^ tensor_rank).astype(jnp.int32)
    units = gate_weight.shape[1]
    units_pad = -(-units // 256) * 256
    widen = lambda w: jnp.pad(w, ((0, 0), (0, units_pad - units)))
    shards = [widen(w) for w in (down_weight.T, gate_weight, up_weight)]
    if split:
        half_units = units_pad // 2
        cut = lambda w, c: lax.dynamic_slice_in_dim(w, c * half_units, half_units, axis=1)

        def in_order(own, other):
            return jnp.stack(
                [jnp.where(ctx_rank == 0, own, other), jnp.where(ctx_rank == 0, other, own)]
            )

        def all_rows(both, *earlier):
            full = lax.all_gather(after(both, *earlier), "fsdp", axis=0, tiled=False)
            return full.reshape(-1, both.shape[-1])

        first_units = half_units // 2 // 256 * 256
        first_cols = 3 * first_units

        def in_parts(c):
            halves = [cut(w, c) for w in shards]
            return jnp.concatenate(
                [w[:, :first_units] for w in halves] + [w[:, first_units:] for w in halves], axis=1
            )

        leaving_units, own_units = in_parts(1 - ctx_rank), in_parts(ctx_rank)
        slot_pick = lax.dynamic_index_in_dim(cotangent, tensor_rank, 0, keepdims=False)
        small = after(small, outgoing, leaving_units, cosine, sine, slot_pick)
        small_both = in_order(small, from_partner(small, "ctx", 1))
        arriving_units = from_partner(after(leaving_units, small_both), "ctx", 1)
        other_own = from_partner(after(slot_pick, arriving_units), "ctx", 1)
        both_a = in_order(own_units[:, :first_cols], arriving_units[:, :first_cols])
        both_b = in_order(own_units[:, first_cols:], arriving_units[:, first_cols:])
    else:
        all_rows = lambda shard, *earlier: lax.all_gather(
            shard, ("fsdp", "ctx"), axis=0, tiled=True
        )
        small_both, unit_both, half_units = small, jnp.concatenate(shards, axis=1), units_pad
    far_in = from_partner(own_in, "tp", 2)
    near_in = from_partner(own_in, "tp", 1)
    ready = (info, pick_info, own_units, home_order) if split else (cosine, sine, info)
    cross_in = from_partner(after(far_in, *ready), "tp", 1)

    near_full = all_rows(small_both, own_in)
    if split:
        units_a = all_rows(both_a, cross_in)
        units_b = all_rows(both_b, cross_in)
    else:
        down_full = all_rows(unit_both[..., :half_units], cross_in)
        gate_up_full = all_rows(unit_both[..., half_units:], cross_in)
    project_full = near_full[:, : query_cols + head_width]
    output_full = near_full[:, near_cols:]
    bias_head = lax.dynamic_slice_in_dim(bias_keyval, head_pair * 2, 2, axis=0)
    bias_row = jnp.concatenate([bias_query.reshape(1, -1), bias_head.reshape(1, -1)], axis=1).astype(WIDE)
    normed_one, query_rot, key_own, value_own = project(
        (own_in, near_in, far_in, cross_in),
        near_full,
        bias_row,
        after(cosine, other_own, both_a, both_b, info, pick_info) if split else cosine,
        sine,
        heads,
        head_dim,
    )
    gains_now = near_full[:, query_cols + head_width : near_cols][:, :2].astype(WIDE).T
    if split:
        key_past, value_past = lax.ppermute((key_own, value_own), "ctx", [(0, 1)])
        other_far = from_partner(other_own, "tp", 2)
        other_near = from_partner(after(other_own, key_past), "tp", 1)
        other_cross = from_partner(after(other_far, key_past), "tp", 1)
        other_rows = (other_own, other_near, other_far, other_cross)
        key_past = after(key_past, other_far)
    else:
        key_past = lax.all_gather(key_own, "ctx", axis=1, tiled=True)
        value_past = lax.all_gather(value_own, "ctx", axis=1, tiled=True)
    in_share = own_in.astype(WIDE)
    if split:
        mixed, lse, middle_share, normed_share = attend_sum(
            info,
            query_rot,
            key_past,
            value_past,
            key_own,
            value_own,
            output_full,
            own_in,
            gains_now[1:2],
            heads,
            head_dim,
            scale,
        )
    else:
        attend = lambda first, *held: attend_forward(
            info, query_rot, *held, key_own, value_own, output_full, heads, head_dim, scale, first, 2
        )

        mixed_far, lse_far, *attn_far = attend(2, key_past, value_past)
        attn_wide = collect_far(attn_far[0], attn_far[1])
        attn_got = from_partner(attn_wide, "tp", 2)
        mixed_near, lse_near, *attn_near = attend(0, after(key_past, attn_wide), value_past)
        attn_core = from_partner(attn_near[1], "tp", 1)
        middle_share = (
            in_share
            + attn_near[0].astype(WIDE)
            + attn_core.astype(WIDE)
            + attn_got.astype(WIDE)
        )
        inv_two = lax.rsqrt(jnp.mean(middle_share * middle_share, axis=-1, keepdims=True) + EPS)
        normed_share = (middle_share * inv_two * gains_now[1]).astype(LOW)
        mixed = jnp.concatenate([mixed_near, mixed_far], axis=0)
        lse = jnp.concatenate([lse_near, lse_far], axis=0)
    half_len = local_len // 2

    if split:
        grad_hidden, grad_rows = chosen_rows(
            pick_info,
            after(cotangent, normed_share),
            other_rows,
            units_a,
            0,
            3,
        )
    else:
        grad_slots = [
            lax.dynamic_index_in_dim(cotangent, slot_now[r], 0, keepdims=False) for r in range(seq_grp)
        ]
        grad_hidden, grad_rows = stack_rows([(g,) for g in grad_slots], down_full, 0, 1)

    def spread_all(own):
        far = from_partner(own, "tp", 2)
        near = from_partner(own, "tp", 1)
        if not split:
            return (own, near, far, from_partner(far, "tp", 1))
        side = from_partner(own, "ctx", 1)
        held = after(far, grad_hidden), after(side, grad_hidden)
        across = from_partner(held[0][:half_len], "ctx", 1), from_partner(held[1][half_len:], "tp", 2)
        cores = [from_partner(v, "tp", 1) for v in held]
        return (own, near, far, cores[0], side, cores[1], *across)

    def in_slots(rows):
        if not split:
            return [(row,) for row in rows]
        return [(row,) for row in rows[:6]] + [rows[6:]]

    mixed_flat = mixed.reshape(token_count, query_cols)
    own_weight = lax.dynamic_slice_in_dim(
        project_full, query_cols + parity * head_dim, head_dim, axis=1
    )
    back_full = jnp.concatenate([project_full[:, :query_cols], own_weight], axis=1)
    normed_slots = in_slots(spread_all(normed_share))
    if split:
        early = after(units_a, back_full)
        ahead = stack_rows(normed_slots[:6], early, 1, 3, total=8)
        last = [normed_slots[6], tuple(from_partner(after(v, ahead[0]), "tp", 1) for v in normed_slots[6])]
        gate_lin, normed_two = stack_rows(last, units_a, 1, 3, into=ahead, first=6, total=8)
        hidden_a, gate_a, up_a = hidden_units(normed_two, units_a, 2, 3, gate_lin, grad_hidden)
        grad_a = first_grads(grad_rows, normed_two, hidden_a, gate_a, up_a)
        hidden_b, gate_b, up_b = full_units(after(normed_two, grad_a), grad_rows, units_b)
    else:
        gate_lin, normed_two = stack_rows(normed_slots, gate_up_full, 0, 2)
        hidden_act, grad_gate, grad_up = hidden_units(
            normed_two, gate_up_full, 1, 2, gate_lin, grad_hidden
        )

    def collect_all(lefts, weights, *earlier):
        lefts = list(lefts)
        lefts[0] = after(lefts[0], *earlier)
        last = back_rows(lefts, weights, 2, 2, local_len)
        got = [from_partner(collect_far(last[0], last[1]), "tp", 2)]
        first = back_rows(lefts, weights, 0, 2, local_len)
        got.append(from_partner(first[1], "tp", 1))

        def finish():
            return sum((v.astype(WIDE) for v in got), first[0].astype(WIDE))

        return first[0], finish

    if split:
        grad_two_share, down_b, up_grad_b = collect_back(
            (gate_a, up_a),
            (gate_b, up_b),
            units_a,
            units_b,
            grad_rows,
            normed_two,
            hidden_b,
            local_len,
        )
        grad_middle, gain_two, gate_grad_b, grad_branch, *mlp = spread_branch(
            grad_two_share,
            middle_share,
            grad_rows,
            gains_now[1:2],
            hidden_a,
            hidden_b,
            units_a,
            units_b,
            normed_two,
            gate_b,
        )
        mlp_own, mlp_far, mlp_side = mlp
        grad_branch = grad_branch.reshape(token_count, model_width)
    else:
        first_back, finish_back = collect_all(
            (grad_gate, grad_up), ((gate_up_full, 0, 2), (gate_up_full, 1, 2))
        )
        down_grad = contract_rows(after(grad_rows, first_back), hidden_act, LOW)
        gate_grad = contract_rows(normed_two, after(grad_gate, down_grad), LOW)
        grad_two_share = finish_back()
        grad_norm_two, gain_two = norm_backward(
            middle_share, inv_two, gains_now[1], grad_two_share
        )
        grad_middle = grad_slots[0].astype(WIDE) + grad_norm_two
        branch_own = grad_middle.astype(LOW)
        branch_far = from_partner(branch_own, "tp", 2)
        branch_near = from_partner(branch_own, "tp", 1)
        branch_cross = from_partner(branch_far, "tp", 1)
        grad_branch = jnp.concatenate([branch_own, branch_near, branch_far, branch_cross], axis=0)
        up_grad = contract_rows(normed_two, after(grad_up, branch_own), LOW)

    grad_mixed = None if split else product(grad_branch, output_full, LOW)
    attend_args = (
        info,
        query_rot,
        key_past,
        value_past,
        key_own,
        value_own,
        output_full if split else grad_mixed.reshape(seq_grp, local_len, query_cols),
        lse,
        cosine,
        sine,
        heads,
        head_dim,
        scale,
    )
    if split:
        line_grad, output_grad, block_share = attend_exchange(
            *attend_args,
            grad_branch,
            mixed_flat,
            (mlp_far, mlp_side, mlp_own),
            middle_share,
        )
        line_grad = line_grad.reshape(token_count, -1)
    else:
        grad_query, mine_past, mine_own, other_past, other_own = attend_backward(*attend_args)
        swap = lambda value: jnp.stack([value[r ^ 1] for r in range(seq_grp)])
        got_past, got_own = from_partner((other_past, other_own), "tp", 1)
        past_sum = mine_past + swap(got_past)
        own_sum = mine_own + swap(got_own)
        own_sum = own_sum + lax.psum_scatter(past_sum, "ctx", scatter_dimension=1, tiled=True)
        half_lanes = head_dim // 2
        turned = own_sum * cosine - jnp.roll(own_sum, half_lanes, axis=-1) * sine
        own_grad = jnp.where(parity == 0, turned, own_sum).astype(LOW).reshape(token_count, head_dim)
        line_grad = jnp.concatenate([grad_query.reshape(token_count, query_cols), own_grad], axis=1)
    def scatter_units(grad):
        if not split:
            return scatter_sum(grad, ctx_rank, LOW)
        return lax.psum_scatter(grad, "fsdp", scatter_dimension=0, tiled=True)

    unit_grads = (grad_a, down_b, up_grad_b, gate_grad_b) if split else (down_grad, gate_grad, up_grad)
    unit_sums = [scatter_units(unit_grads[0])]
    if split:
        unit_sums += [scatter_units(after(g, unit_sums[0])) for g in unit_grads[1:3]]
        unit_sums += [scatter_units(after(unit_grads[3], unit_sums[0]))]
    else:
        unit_sums += [scatter_units(g) for g in unit_grads[1:]]

    normed_flat = normed_one.reshape(token_count, model_width)
    if split:
        input_share, gain_grad, attn_grad, bias_grad, block_home = finish_rows(
            line_grad,
            after(back_full, *unit_sums),
            own_in,
            grad_middle,
            gains_now[0:1],
            gain_two,
            normed_flat,
            block_share,
        )
        attn_grad = jnp.concatenate([attn_grad, output_grad], axis=1)
    else:
        half = token_count // 2
        line_far = contract_cols(line_grad[half:], back_full, LOW).reshape(2, local_len, model_width)
        line_near = contract_cols(line_grad[:half], back_full, LOW).reshape(2, local_len, model_width)
        line_wide = collect_far(line_far[0], line_far[1])
        line_got = from_partner(line_wide, "tp", 2)
        line_core = from_partner(line_near[1], "tp", 1)
        first_mlp, finish_mlp = collect_all((hidden_act,), ((down_full, 0, 1),), up_grad, branch_far)
        block_share = (middle_share + finish_mlp()).astype(LOW)
        grad_one_share = line_near[0].astype(WIDE) + line_core.astype(WIDE) + line_got.astype(WIDE)
        inv_one = lax.rsqrt(jnp.mean(in_share * in_share, axis=-1, keepdims=True) + EPS)
        grad_norm_one, gain_one = norm_backward(in_share, inv_one, gains_now[0], grad_one_share)
        input_share = (grad_middle + grad_norm_one).astype(LOW)
        attn_grad = jnp.concatenate(
            [contract_rows(normed_flat, line_grad, LOW), contract_rows(grad_branch, mixed_flat, LOW)],
            axis=1,
        )
        bias_grad = jnp.sum(line_grad.astype(WIDE), axis=0)

    shard_count = fsdp_count * ctx_count
    share = head_dim // shard_count
    if not split:
        gain_grad = jnp.concatenate([gain_one, gain_two], axis=0)
        gain_grad = gain_grad + from_partner(gain_grad, "tp", 1)
        gain_grad = gain_grad + from_partner(gain_grad, "tp", 2)
    bias_cols = jnp.transpose(bias_grad.reshape(heads + 1, shard_count, share), (1, 2, 0))
    bias_cols = jnp.pad(bias_cols, ((0, 0), (0, (model_width - head_dim) // shard_count), (0, 0)))
    tiny = jnp.concatenate([gain_grad.T, bias_cols.reshape(model_width, heads + 1)], axis=1)
    tiny = jnp.pad(tiny, ((0, 0), (0, 128 - tiny.shape[1]))).astype(LOW)
    attn_grad = jnp.concatenate([attn_grad, tiny], axis=1)
    if split:
        attn_blocks = attn_grad.reshape(fsdp_count, ctx_count, -1, attn_grad.shape[1])
        kept, sent = scatter_ctx(attn_blocks, ctx_rank)
        attn_held = (kept.astype(WIDE) + from_partner(sent, "ctx", 1).astype(WIDE)).astype(LOW)
        attn_held = attn_held.reshape(-1, attn_grad.shape[1])
        attn_end = lax.psum_scatter(after(attn_held, *unit_sums), "fsdp", scatter_dimension=0, tiled=True)
    else:
        attn_end = scatter_sum(attn_grad, ctx_rank, LOW, *unit_sums)


    def leave(share):
        return lax.ppermute(share, ("fsdp", "tp"), back)

    def arrive(own, order):
        far = from_partner(own, "tp", 2)
        near = from_partner(own, "tp", 1)
        return place_rows((own, near, far, from_partner(far, "tp", 1)), order)

    input_home = leave(input_share)
    if not split:
        block_home = leave(block_share)
    block_out = arrive(block_home, home_order)
    if split:

        def unit_end(total, *earlier):
            kept, sent = scatter_ctx(total.reshape(1, ctx_count, -1, total.shape[1]), ctx_rank)
            return kept[0], from_partner(after(sent[0], *earlier), "ctx", 1)

        own_a, got_a = unit_end(unit_sums[0], grad_branch)
        ends = [unit_end(t, line_grad) for t in unit_sums[1:]]
        input_home = after(input_home, attn_held)
        home_order = after(home_order, got_a, *[end[1] for end in ends])
    input_grad = arrive(input_home, home_order)

    small_at = query_cols + head_dim + query_cols
    tiny_grad = attn_end[:, small_at:].astype(WIDE)

    if split:

        def joined(part, end):
            cols = slice(part * first_units, (part + 1) * first_units)
            own = jnp.concatenate([own_a[:, cols], end[0]], axis=1)
            got = jnp.concatenate([got_a[:, cols], end[1]], axis=1)
            first, second = jnp.where(ctx_rank == 0, own, got), jnp.where(ctx_rank == 0, got, own)
            return jnp.concatenate([first, second], axis=1)[:, :units].astype(WIDE)

        down_end, gate_end, up_end = joined(0, ends[0]), joined(1, ends[2]), joined(2, ends[1])
    else:
        down_end, gate_end, up_end = (t[:, :units].astype(WIDE) for t in unit_sums)
    return (
        block_out,
        input_grad,
        attn_end[:, :query_cols].astype(WIDE),
        attn_end[:, query_cols : query_cols + head_dim].astype(WIDE),
        attn_end[:, query_cols + head_dim : small_at].astype(WIDE).T,
        tiny_grad[:, :2].T,
        tiny_grad[:share, 2 : 2 + heads].T,
        tiny_grad[:share, 2 + heads : 3 + heads].T,
        gate_end,
        up_end,
        down_end.T,
    )


def solution(mesh):
    placed = (
        P("fsdp", "ctx", None),
        P("fsdp", "ctx", None),
        P(),
        P(None, "ctx"),
        P(),
        P(("fsdp", "ctx"), "tp"),
        P(("fsdp", "ctx"), None),
        P("tp", ("fsdp", "ctx")),
        P(None, ("fsdp", "ctx")),
        P("tp", None),
        P(),
        P(("fsdp", "ctx"), "tp"),
        P(("fsdp", "ctx"), "tp"),
        P("tp", ("fsdp", "ctx")),
    )
    return jax.shard_map(
        local,
        mesh=mesh,
        in_specs=placed,
        out_specs=(
            P("fsdp", "ctx", None),
            P("fsdp", "ctx", None),
            P(("fsdp", "ctx"), "tp"),
            P(("fsdp", "ctx"), "tp"),
            P("tp", ("fsdp", "ctx")),
            P(None, ("fsdp", "ctx")),
            P("tp", ("fsdp", "ctx")),
            P("tp", ("fsdp", "ctx")),
            P(("fsdp", "ctx"), "tp"),
            P(("fsdp", "ctx"), "tp"),
            P("tp", ("fsdp", "ctx")),
        ),
        check_vma=False,
    )
```

```python
import functools
import math

import jax
import jax.numpy as jnp
from jax import lax
from jax.experimental import pallas as pl
from jax.experimental.pallas import tpu as pltpu
from jax.sharding import PartitionSpec as P

EPS = 1e-06
ROPE_BASE = 10000.0
NEG_FILL = -1e30
LOW = jnp.bfloat16
WIDE = jnp.float32
DEAL_SHIFT = (0, 2, 1, 3)


def from_partner(value, axis, apart):
    pairs = [(source, source ^ apart) for source in range(lax.axis_size(axis))]
    return lax.ppermute(value, axis, pairs)


def product(left_side, right_side, kind=WIDE):
    return jnp.dot(left_side, right_side, preferred_element_type=WIDE).astype(kind)


def contract_rows(left_side, right_side, kind=WIDE):
    return lax.dot_general(
        left_side, right_side, (((0,), (0,)), ((), ())), preferred_element_type=WIDE
    ).astype(kind)


def contract_cols(left_side, right_side, kind=WIDE):
    return lax.dot_general(
        left_side, right_side, (((1,), (1,)), ((), ())), preferred_element_type=WIDE
    ).astype(kind)


def norm_backward(values, scale_inv, gain_row, upstream):
    scaled = gain_row * upstream
    inner_mean = jnp.mean(values * scaled, axis=-1, keepdims=True)
    grad_in = scale_inv * scaled - values * (scale_inv * scale_inv * scale_inv) * inner_mean
    gain_grad = jnp.sum(upstream * values * scale_inv, axis=0, keepdims=True)
    return (grad_in, gain_grad)


def after(value, *earlier):
    return lax.optimization_barrier((value, *earlier))[0]


def collect_far(far_part, cross_part):
    wide = far_part.astype(WIDE) + from_partner(cross_part, "tp", 1).astype(WIDE)
    return wide.astype(LOW)


def units_split():
    return lax.axis_size("ctx") == 2


def all_rows(shard):
    return lax.all_gather(shard, "fsdp", axis=0, tiled=True)


def scatter_ctx(blocks, ctx_rank):
    kept = lax.dynamic_index_in_dim(blocks, ctx_rank, 1, keepdims=False)
    sent = lax.dynamic_index_in_dim(blocks, 1 - ctx_rank, 1, keepdims=False)
    return kept, sent


def scatter_sum(grad, ctx_rank, kind, *earlier):
    fsdp_count, ctx_count = lax.axis_size("fsdp"), lax.axis_size("ctx")
    rows, cols = grad.shape
    blocks = grad.reshape(fsdp_count, ctx_count, rows // (fsdp_count * ctx_count), cols)
    if ctx_count == 2:
        kept, sent = scatter_ctx(blocks, ctx_rank)
        got = from_partner(sent, "ctx", 1)
        held = (after(kept, *earlier).astype(WIDE) + got.astype(WIDE)).astype(kind)
    else:
        swapped = jnp.swapaxes(blocks, 0, 1).reshape(rows, cols)
        held = lax.psum_scatter(swapped, "ctx", scatter_dimension=0, tiled=True)
    held = held.reshape(rows // ctx_count, cols)
    return lax.psum_scatter(held, "fsdp", scatter_dimension=0, tiled=True)


def estimate(flops, moved, transcendentals=0):
    return pl.CostEstimate(flops=flops, bytes_accessed=moved, transcendentals=transcendentals)


def part_spec(rows, cols, part):
    return pl.BlockSpec((rows, cols), lambda *_: (0, part), pipeline_mode=pl.Buffered(1))


def whole_spec(*shape, once=False):
    mode = {"pipeline_mode": pl.Buffered(1)} if once else {}
    return pl.BlockSpec(shape, lambda *_: (0,) * len(shape), **mode)


def rows_kernel(groups, *refs):
    slot = pl.program_id(0)
    weight, (lin, stacked) = refs[sum(groups)], refs[-2:]

    def run(pieces):
        start = 0
        for piece in pieces:
            stacked[start : start + piece.shape[0]] = piece[...]
            start += piece.shape[0]
        lin[...] = jnp.dot(stacked[...], weight[...], preferred_element_type=WIDE).astype(LOW)

    first = 0
    for r, pieces in enumerate(groups):
        pl.when(slot == r)(functools.partial(run, refs[first : first + pieces]))
        first += pieces


def stack_rows(slots, weight, part, parts, into=None, first=0, total=None):
    groups = [len(s) for s in slots]
    rows = [piece for s in slots for piece in s]
    width, length = rows[0].shape[1], sum(piece.shape[0] for piece in slots[0])
    count, cols = len(slots), weight.shape[1] // parts
    total = total or count
    into = into or ()
    return pl.pallas_call(
        functools.partial(rows_kernel, groups),
        grid=(count,),
        in_specs=[whole_spec(*piece.shape, once=True) for piece in rows]
        + [part_spec(width, cols, part)]
        + [pl.BlockSpec(memory_space=pl.ANY)] * len(into),
        out_specs=[
            pl.BlockSpec((length, cols), lambda s: (first + s, 0)),
            pl.BlockSpec((length, width), lambda s: (first + s, 0)),
        ],
        out_shape=[
            jax.ShapeDtypeStruct((total * length, cols), LOW),
            jax.ShapeDtypeStruct((total * length, width), LOW),
        ],
        input_output_aliases={len(rows) + 1 + i: i for i in range(len(into))},
        compiler_params=pltpu.CompilerParams(vmem_limit_bytes=60 << 20),
        cost_estimate=estimate(
            2 * count * length * width * cols, 2 * (count * length * (2 * width + cols) + width * cols)
        ),
    )(*rows, weight, *into)


def units_kernel(h, up, gate, grad, hid, grad_gate, grad_up):
    up_lin = jnp.dot(h[...], up[...], preferred_element_type=WIDE)
    gate_lin = gate[...].astype(WIDE)
    grad_hidden = grad[...].astype(WIDE)
    sigmoid = 1.0 / (1.0 + jnp.exp(-gate_lin))
    silu = gate_lin * sigmoid
    hid[...] = (silu * up_lin).astype(LOW)
    grad_gate[...] = (grad_hidden * up_lin * sigmoid * (1.0 + gate_lin * (1.0 - sigmoid))).astype(LOW)
    grad_up[...] = (grad_hidden * silu).astype(LOW)


def hidden_units(h, up, part, parts, gate_lin, grad_hidden):
    tokens, width = h.shape
    cols = up.shape[1] // parts
    step = math.gcd(512, tokens)
    by_row = lambda n: pl.BlockSpec((step, n), lambda i: (i, 0))
    return pl.pallas_call(
        units_kernel,
        grid=(tokens // step,),
        in_specs=[by_row(width), part_spec(width, cols, part), by_row(cols), by_row(cols)],
        out_specs=[by_row(cols)] * 3,
        out_shape=[jax.ShapeDtypeStruct((tokens, cols), LOW)] * 3,
        compiler_params=pltpu.CompilerParams(vmem_limit_bytes=60 << 20),
        cost_estimate=estimate(
            2 * tokens * width * cols, 2 * (tokens * width + width * cols + 5 * tokens * cols)
        ),
    )(h, up, gate_lin, grad_hidden)


def back_kernel(terms, *refs):
    lefts, weights, outs = refs[:terms], refs[terms : 2 * terms], refs[2 * terms :]
    total = None
    for left, weight in zip(lefts, weights):
        term = dot_cols(left[...], weight[...])
        total = term if total is None else total + term
    for i, out in enumerate(outs):

        @pl.when(pl.program_id(0) == i)
        def _():
            out[...] = total.astype(LOW)


def back_rows(lefts, weights, first_slot, slots, length):
    width = weights[0][0].shape[0]
    depth = sum(left.shape[1] for left in lefts)
    return pl.pallas_call(
        functools.partial(back_kernel, len(lefts)),
        grid=(slots,),
        in_specs=[
            pl.BlockSpec((length, left.shape[1]), lambda s: (first_slot + s, 0)) for left in lefts
        ]
        + [part_spec(width, w.shape[1] // parts, part) for w, part, parts in weights],
        out_specs=[whole_spec(length, width)] * slots,
        out_shape=[jax.ShapeDtypeStruct((length, width), LOW)] * slots,
        compiler_params=pltpu.CompilerParams(vmem_limit_bytes=60 << 20),
        cost_estimate=estimate(
            2 * slots * length * width * depth,
            2 * (slots * length * (width + depth) + width * depth),
        ),
    )(*lefts, *[w for w, _, _ in weights])


def chosen_kernel(near, count, info, cotangent, *refs):
    slot = pl.program_id(0)
    others, (weight, lin, stacked) = refs[:count], refs[count:]

    @pl.when(slot < near)
    def _():
        stacked[...] = cotangent[0]

    for k, other in enumerate(others):

        @pl.when((slot >= near) & (info[slot] == k))
        def _():
            stacked[...] = other[...]

    lin[...] = jnp.dot(stacked[...], weight[...], preferred_element_type=WIDE).astype(LOW)


def chosen_rows(info, cotangent, others, weight, part, parts):
    near, length, width = cotangent.shape
    slots, cols = near + len(others), weight.shape[1] // parts
    held = lambda rows, n, at: pl.BlockSpec(
        (rows, n), lambda s, info: (0, at), pipeline_mode=pl.Buffered(1)
    )
    return pl.pallas_call(
        functools.partial(chosen_kernel, near, len(others)),
        grid_spec=pltpu.PrefetchScalarGridSpec(
            num_scalar_prefetch=1,
            grid=(slots,),
            in_specs=[
                pl.BlockSpec((1, length, width), lambda s, info: (info[jnp.minimum(s, near - 1)], 0, 0))
            ]
            + [held(length, width, 0)] * len(others)
            + [held(width, cols, part)],
            out_specs=[
                pl.BlockSpec((length, cols), lambda s, info: (s, 0)),
                pl.BlockSpec((length, width), lambda s, info: (s, 0)),
            ],
        ),
        out_shape=[
            jax.ShapeDtypeStruct((slots * length, cols), LOW),
            jax.ShapeDtypeStruct((slots * length, width), LOW),
        ],
        compiler_params=pltpu.CompilerParams(vmem_limit_bytes=60 << 20),
        cost_estimate=estimate(
            2 * slots * length * width * cols, 2 * (slots * length * (2 * width + cols) + width * cols)
        ),
    )(info, cotangent, *others, weight)


def full_units_kernel(h, g, down, gate, up, hid, grad_gate, grad_up):
    gate_lin = jnp.dot(h[...], gate[...], preferred_element_type=WIDE)
    up_lin = jnp.dot(h[...], up[...], preferred_element_type=WIDE)
    grad_hidden = jnp.dot(g[...], down[...], preferred_element_type=WIDE)
    sigmoid = 1.0 / (1.0 + jnp.exp(-gate_lin))
    silu = gate_lin * sigmoid
    hid[...] = (silu * up_lin).astype(LOW)
    grad_gate[...] = (grad_hidden * up_lin * sigmoid * (1.0 + gate_lin * (1.0 - sigmoid))).astype(LOW)
    grad_up[...] = (grad_hidden * silu).astype(LOW)


def full_units(h, g, weight):
    tokens, width = h.shape
    cols = weight.shape[1] // 3
    step = math.gcd(512, tokens)
    by_row = lambda n: pl.BlockSpec((step, n), lambda i: (i, 0))
    return pl.pallas_call(
        full_units_kernel,
        grid=(tokens // step,),
        in_specs=[by_row(width)] * 2 + [part_spec(width, cols, i) for i in range(3)],
        out_specs=[by_row(cols)] * 3,
        out_shape=[jax.ShapeDtypeStruct((tokens, cols), LOW)] * 3,
        compiler_params=pltpu.CompilerParams(vmem_limit_bytes=60 << 20),
        cost_estimate=estimate(
            6 * tokens * width * cols, 2 * (2 * tokens * width + 3 * width * cols + 3 * tokens * cols)
        ),
    )(h, g, weight, weight, weight)


def first_grads_kernel(g, h, hid, gate, up, out):
    part = pl.program_id(0)
    for i, (left, right) in enumerate(((g, hid), (h, gate), (h, up))):

        @pl.when(part == i)
        def _():
            out[...] = dot_rows(left[...], right[...]).astype(LOW)


def first_grads(grad_rows, rows, hid, grad_gate, grad_up):
    tokens, width = rows.shape
    cols, tile = hid.shape[1], 256
    tiles = width // tile
    return pl.pallas_call(
        first_grads_kernel,
        grid=(3, tiles),
        in_specs=[
            pl.BlockSpec((tokens, tile), lambda p, i: (0, jnp.where(p == 0, i, tiles - 1))),
            pl.BlockSpec((tokens, tile), lambda p, i: (0, jnp.where(p == 0, 0, i))),
        ]
        + [whole_spec(tokens, cols, once=True)] * 3,
        out_specs=pl.BlockSpec((tile, cols), lambda p, i: (i, p)),
        out_shape=jax.ShapeDtypeStruct((width, 3 * cols), LOW),
        compiler_params=pltpu.CompilerParams(vmem_limit_bytes=60 << 20),
        cost_estimate=estimate(6 * tokens * width * cols, 6 * tokens * cols + 6 * width * cols),
    )(grad_rows, rows, hid, grad_gate, grad_up)


MESH_ID = pl.DeviceIdType.MESH


def meet(partners):
    barrier = pltpu.get_barrier_semaphore()
    for partner in partners:
        pl.semaphore_signal(barrier, inc=1, device_id=partner, device_id_type=MESH_ID)
    pl.semaphore_wait(barrier, len(partners))


def partners_of():
    tensor_rank, ctx_rank = lax.axis_index("tp"), lax.axis_index("ctx")
    return {"tp": tensor_rank ^ 1}, {"tp": tensor_rank ^ 2}, {"ctx": ctx_rank ^ 1}


def collect_kernel(
    slots, tiles, gate_a, up_a, gate_b, up_b, w_gate_a, w_up_a, w_gate_b, w_up_b, left, right, hid, up, total,
    down_out, up_out, parts, sent, core_in, across_in, last_in, held, send, recv, load
):
    step = pl.program_id(0)
    steps = pl.num_programs(0)
    core, far, side = partners_of()
    half = total.shape[0] // 2
    remote = remote_copy(send, recv)
    cores = [remote(sent.at[k % 2], core_in.at[k], k, core) for k in range(4)]
    across = [
        remote(parts.at[3, pl.ds(0, half)], across_in.at[0], 4, far),
        remote(parts.at[3, pl.ds(half, half)], across_in.at[1], 5, side),
    ]
    lasts = [
        remote(parts.at[1], last_in.at[0], 6, far),
        remote(parts.at[2, pl.ds(half, half)], last_in.at[1, pl.ds(half, half)], 7, side),
        remote(parts.at[2, pl.ds(0, half)], last_in.at[1, pl.ds(0, half)], 8, side),
    ]
    loading = [
        pltpu.make_async_copy(source, held.at[i], load.at[i]) for i, source in enumerate((hid, up))
    ]

    @pl.when(step == 0)
    def _():
        for copy in loading:
            copy.start()
        meet((core, far, side))

    for k in (2, 3):
        pl.when(step == 2 * k)(cores[k - 2].wait_send)

    @pl.when(step < slots)
    def _():
        part = (
            dot_cols(gate_a[...], w_gate_a[...])
            + dot_cols(up_a[...], w_up_a[...])
            + dot_cols(gate_b[...], w_gate_b[...])
            + dot_cols(up_b[...], w_up_b[...])
        )

        @pl.when(step == slots - 1)
        def _():
            total[...] = part

        for k in range(4):

            @pl.when(step == 2 * k)
            def _():
                sent[k % 2] = part.astype(LOW)
                cores[k].start()

            if k < 3:

                @pl.when(step == 2 * k + 1)
                def _():
                    cores[k].wait_recv()
                    parts[3 - k] = (part + core_in[k].astype(WIDE)).astype(LOW)

    def add(slot, rows, value):
        parts[slot, rows] = (parts[slot, rows].astype(WIDE) + value.astype(WIDE)).astype(LOW)

    low, high = pl.ds(0, half), pl.ds(half, half)

    @pl.when(step == 1)
    def _():
        for copy in across:
            copy.start()

    pl.when(step == 3)(lasts[1].start)

    @pl.when(step == 5)
    def _():
        across[1].wait_recv()
        add(1, high, across_in[1])
        lasts[0].start()
        across[0].wait_recv()
        add(2, low, across_in[0])
        lasts[2].start()

    @pl.when((step >= slots) & (step < slots + tiles))
    def _():
        pl.when(step == slots)(loading[0].wait)
        down_out[...] = dot_rows(left[...], held[0]).astype(LOW)

    @pl.when(step >= slots + tiles)
    def _():
        pl.when(step == slots + tiles)(loading[1].wait)
        up_out[...] = dot_rows(right[...], held[1]).astype(LOW)

    @pl.when(step == steps - 1)
    def _():
        cores[3].wait_recv()
        for copy in lasts:
            copy.wait_recv()
        total[...] += (
            core_in[3].astype(WIDE) + last_in[0].astype(WIDE) + last_in[1].astype(WIDE)
        )
        for copy in (*cores[2:], *across, *lasts):
            copy.wait_send()


def collect_back(first, second, weight_a, weight_b, grad_rows, rows, hid, length):
    tokens, cols_a = first[0].shape
    cols = second[0].shape[1]
    width = weight_a.shape[0]
    slots, tile = tokens // length, 256
    tiles = width // tile
    row = lambda n: pl.BlockSpec((length, n), lambda i: (jnp.maximum(slots - 1 - i, 0), 0))
    column = lambda i, start: jnp.clip(i - start, 0, tiles - 1)
    down_at, up_at = (lambda i: column(i, slots)), (lambda i: column(i, slots + tiles))
    return pl.pallas_call(
        functools.partial(collect_kernel, slots, tiles),
        grid=(slots + 2 * tiles,),
        in_specs=[row(cols_a), row(cols_a), row(cols), row(cols)]
        + [part_spec(width, cols_a, 1), part_spec(width, cols_a, 2)]
        + [part_spec(width, cols, 1), part_spec(width, cols, 2)]
        + [
            pl.BlockSpec((tokens, tile), lambda i: (0, down_at(i))),
            pl.BlockSpec((tokens, tile), lambda i: (0, up_at(i))),
            ANYWHERE,
            ANYWHERE,
        ],
        out_specs=[
            whole_spec(length, width, once=True),
            pl.BlockSpec((tile, cols), lambda i: (down_at(i), 0)),
            pl.BlockSpec((tile, cols), lambda i: (up_at(i), 0)),
        ],
        out_shape=[
            jax.ShapeDtypeStruct((length, width), WIDE),
            jax.ShapeDtypeStruct((width, cols), LOW),
            jax.ShapeDtypeStruct((width, cols), LOW),
        ],
        scratch_shapes=[
            pltpu.VMEM((4, length, width), LOW),
            pltpu.VMEM((2, length, width), LOW),
            pltpu.VMEM((4, length, width), LOW),
            pltpu.VMEM((2, length // 2, width), LOW),
            pltpu.VMEM((2, length, width), LOW),
            pltpu.VMEM((2, tokens, cols), LOW),
            pltpu.SemaphoreType.DMA((9,)),
            pltpu.SemaphoreType.DMA((9,)),
            pltpu.SemaphoreType.DMA((2,)),
        ],
        compiler_params=pltpu.CompilerParams(
            vmem_limit_bytes=63 << 20, collective_id=1, has_side_effects=True
        ),
        cost_estimate=estimate(6 * tokens * width * cols, 10 * tokens * cols),
    )(*first, *second, weight_a, weight_a, weight_b, weight_b, grad_rows, rows, hid, second[1])


def remote_copy(send, recv):
    def make(source, target, index, partner):
        return pltpu.make_async_remote_copy(
            source, target, send.at[index], recv.at[index], device_id=partner, device_id_type=MESH_ID
        )

    return make


def branch_kernel(
    slots, tiles, total, middle, own_grad, gain, hid_a, hid_b, w_a, w_b, turned, gate, grad_middle, gain_grad,
    gate_out, branch, mlp_own, mlp_far, mlp_side, own, parts, core_in, across_in, held, send, recv, load
):
    step = pl.program_id(0)
    core, far, side = partners_of()
    remote = remote_copy(send, recv)
    to_far = remote(own, branch.at[2], 0, far)
    to_near = remote(own, branch.at[1], 1, core)
    to_cross = remote(branch.at[2], branch.at[3], 2, core)
    keep = pltpu.make_async_copy(own, branch.at[0], load.at[0])
    loading = pltpu.make_async_copy(gate, held, load.at[1])
    cores = [remote(parts.at[7 - 2 * k], core_in.at[k], 3 + k, core) for k in range(4)]
    across = remote(parts.at[6], across_in, 7, side)
    stores = [
        pltpu.make_async_copy(parts.at[4], mlp_side, load.at[2]),
        pltpu.make_async_copy(parts.at[2], mlp_far, load.at[3]),
        pltpu.make_async_copy(parts.at[0], mlp_own, load.at[4]),
    ]

    @pl.when(step == 0)
    def _():
        loading.start()
        meet((core, far, side))
        values, upstream = middle[...], total[...]
        inverse = lax.rsqrt(jnp.mean(values * values, axis=-1, keepdims=True) + EPS)
        grad_in, gain_grad[...] = norm_backward(values, inverse, gain[...], upstream)
        grad_in = own_grad[...].astype(WIDE) + grad_in
        grad_middle[...] = grad_in
        own[...] = grad_in.astype(LOW)
        for copy in (to_far, to_near, keep):
            copy.start()

    @pl.when(step < slots)
    def _():
        part = dot_cols(hid_a[...], w_a[...]) + dot_cols(hid_b[...], w_b[...])
        parts[slots - 1 - step] = part.astype(LOW)

    for k in range(4):
        pl.when(step == 2 * k)(cores[k].start)

        def finish(k=k):
            slot = 6 - 2 * k
            cores[k].wait_recv()
            parts[slot] = (parts[slot].astype(WIDE) + core_in[k].astype(WIDE)).astype(LOW)
            if k == 0:
                across.start()
            if k == 1:
                stores[0].start()
            if k == 3:
                stores[2].start()

        pl.when(step == 2 * k + 1)(finish)

    @pl.when(step >= slots)
    def _():
        pl.when(step == slots)(loading.wait)
        gate_out[...] = dot_rows(turned[...], held[...]).astype(LOW)

    @pl.when(step == slots + tiles - 2)
    def _():
        to_far.wait_recv()
        to_cross.start()

    @pl.when(step == slots + tiles - 1)
    def _():
        to_near.wait_recv()
        to_cross.wait_recv()
        across.wait_recv()
        parts[2] = (parts[2].astype(WIDE) + across_in[...].astype(WIDE)).astype(LOW)
        stores[1].start()
        keep.wait()
        for copy in stores:
            copy.wait()
        for copy in (to_far, to_near, to_cross, *cores, across):
            copy.wait_send()


ANYWHERE = pl.BlockSpec(memory_space=pl.ANY)


def spread_branch(total, middle, own_grad, gain, hid_a, hid_b, weight_a, weight_b, rows, grad_gate):
    length, width = total.shape
    tokens, cols = grad_gate.shape
    slots, tile = tokens // length, 256
    tiles = width // tile
    once = whole_spec(length, width, once=True)
    column = lambda i: jnp.clip(i - slots, 0, tiles - 1)
    part = jax.ShapeDtypeStruct((length, width), LOW)
    return pl.pallas_call(
        functools.partial(branch_kernel, slots, tiles),
        grid=(slots + tiles,),
        in_specs=[
            once,
            once,
            once,
            whole_spec(1, width),
            pl.BlockSpec((length, hid_a.shape[1]), lambda i: (jnp.maximum(slots - 1 - i, 0), 0)),
            pl.BlockSpec((length, cols), lambda i: (jnp.maximum(slots - 1 - i, 0), 0)),
            part_spec(width, hid_a.shape[1], 0),
            part_spec(width, cols, 0),
            pl.BlockSpec((tokens, tile), lambda i: (0, column(i))),
            ANYWHERE,
        ],
        out_specs=[
            whole_spec(length, width, once=True),
            whole_spec(1, width),
            pl.BlockSpec((tile, cols), lambda i: (column(i), 0)),
        ]
        + [ANYWHERE] * 4,
        out_shape=[
            jax.ShapeDtypeStruct((length, width), WIDE),
            jax.ShapeDtypeStruct((1, width), WIDE),
            jax.ShapeDtypeStruct((width, cols), LOW),
            jax.ShapeDtypeStruct((4, length, width), LOW),
            part,
            part,
            part,
        ],
        scratch_shapes=[
            pltpu.VMEM((length, width), LOW),
            pltpu.VMEM((slots, length, width), LOW),
            pltpu.VMEM((4, length, width), LOW),
            pltpu.VMEM((length, width), LOW),
            pltpu.VMEM((tokens, cols), LOW),
            pltpu.SemaphoreType.DMA((8,)),
            pltpu.SemaphoreType.DMA((8,)),
            pltpu.SemaphoreType.DMA((5,)),
        ],
        compiler_params=pltpu.CompilerParams(
            vmem_limit_bytes=63 << 20, collective_id=2, has_side_effects=True
        ),
        cost_estimate=estimate(4 * tokens * width * cols, 10 * tokens * cols),
    )(total, middle, own_grad, gain, hid_a, hid_b, weight_a, weight_b, rows, grad_gate)


def line_kernel(
    slots, tiles, line, weight, own_in, grad_middle, gain, gain_two, rows_one, line_all, block, share,
    gain_grad, attn_out, bias_out, home, parts, core_in, far_in, total, gains, gains_in, send, recv, load
):
    step = pl.program_id(0)
    core, far, _ = partners_of()
    tensor_rank, group = lax.axis_index("tp"), lax.axis_index("fsdp")
    shift = (tensor_rank % 2) * 2 + tensor_rank // 2
    target = {"fsdp": (group + slots - shift) % slots}
    source = {"fsdp": (group + shift) % slots}
    stays = shift == 0
    remote = remote_copy(send, recv)
    cores = [remote(parts.at[3 - 2 * k], core_in.at[k], k, core) for k in range(2)]
    to_far = remote(parts.at[2], far_in, 2, far)
    leave = remote(block, home, 3, target)
    keep = pltpu.make_async_copy(block, home, load)
    cross = {"tp": tensor_rank ^ 3}
    gain_copies = [
        remote(gains, gains_in.at[i], 4 + i, partner) for i, partner in enumerate((core, far, cross))
    ]

    @pl.when(step == 0)
    def _():
        barrier = pltpu.get_barrier_semaphore()
        for partner in (core, far, cross):
            pl.semaphore_signal(barrier, inc=1, device_id=partner, device_id_type=MESH_ID)

        @pl.when(stays)
        def _():
            pl.semaphore_wait(barrier, 3)
            keep.start()

        @pl.when(jnp.logical_not(stays))
        def _():
            for partner in (target, source):
                pl.semaphore_signal(barrier, inc=1, device_id=partner, device_id_type=MESH_ID)
            pl.semaphore_wait(barrier, 5)
            leave.start()

    @pl.when(step < slots)
    def _():
        part = dot_cols(line[...], weight[...])
        parts[slots - 1 - step] = part.astype(LOW)

        @pl.when(step == slots - 1)
        def _():
            total[...] = part

    for k in range(2):
        pl.when(step == 2 * k)(cores[k].start)

    @pl.when(step == 1)
    def _():
        cores[0].wait_recv()
        parts[2] = (parts[2].astype(WIDE) + core_in[0].astype(WIDE)).astype(LOW)
        to_far.start()

    @pl.when(step == slots - 1)
    def _():
        bias_out[...] = jnp.sum(line_all[...].astype(WIDE), axis=0, keepdims=True)

    @pl.when(step >= slots)
    def _():
        attn_out[...] = dot_rows(rows_one[...], line_all[...]).astype(LOW)

    @pl.when(step == slots + tiles - 1)
    def _():
        cores[1].wait_recv()
        to_far.wait_recv()
        upstream = total[...] + core_in[1].astype(WIDE) + far_in[...].astype(WIDE)
        values = own_in[...].astype(WIDE)
        inverse = lax.rsqrt(jnp.mean(values * values, axis=-1, keepdims=True) + EPS)
        grad_in, gain_one = norm_backward(values, inverse, gain[...], upstream)
        gains[0:1] = gain_one
        gains[1:2] = gain_two[...]
        for copy in gain_copies:
            copy.start()
        share[...] = (grad_middle[...] + grad_in).astype(LOW)
        for copy in gain_copies:
            copy.wait_recv()
        gain_grad[...] = (gains[...] + gains_in[0]) + (gains_in[1] + gains_in[2])
        for copy in (*cores, to_far, *gain_copies):
            copy.wait_send()
        pl.when(stays)(keep.wait)

        @pl.when(jnp.logical_not(stays))
        def _():
            leave.wait_recv()
            leave.wait_send()


def finish_rows(line, weight, own_in, grad_middle, gain, gain_two, rows_one, block):
    length, width = own_in.shape
    near_tokens, line_cols = line.shape
    slots, tile = near_tokens // length, 256
    tiles = width // tile
    once = whole_spec(length, width, once=True)
    column = lambda i: jnp.clip(i - slots, 0, tiles - 1)
    by_column = lambda n: pl.BlockSpec((n, tile), lambda i: (0, column(i)))
    attn_cols = line_cols
    return pl.pallas_call(
        functools.partial(line_kernel, slots, tiles),
        grid=(slots + tiles,),
        in_specs=[
            pl.BlockSpec((length, line_cols), lambda i: (jnp.maximum(slots - 1 - i, 0), 0)),
            whole_spec(width, line_cols, once=True),
            once,
            once,
            whole_spec(1, width),
            whole_spec(1, width),
            by_column(near_tokens),
            whole_spec(near_tokens, line_cols, once=True),
            ANYWHERE,
        ],
        out_specs=[
            whole_spec(length, width),
            whole_spec(2, width),
            pl.BlockSpec((tile, attn_cols), lambda i: (column(i), 0)),
            whole_spec(1, line_cols),
            ANYWHERE,
        ],
        out_shape=[
            jax.ShapeDtypeStruct((length, width), LOW),
            jax.ShapeDtypeStruct((2, width), WIDE),
            jax.ShapeDtypeStruct((width, attn_cols), LOW),
            jax.ShapeDtypeStruct((1, line_cols), WIDE),
            jax.ShapeDtypeStruct((length, width), LOW),
        ],
        scratch_shapes=[
            pltpu.VMEM((slots, length, width), LOW),
            pltpu.VMEM((2, length, width), LOW),
            pltpu.VMEM((length, width), LOW),
            pltpu.VMEM((length, width), WIDE),
            pltpu.VMEM((2, width), WIDE),
            pltpu.VMEM((3, 2, width), WIDE),
            pltpu.SemaphoreType.DMA((7,)),
            pltpu.SemaphoreType.DMA((7,)),
            pltpu.SemaphoreType.DMA,
        ],
        compiler_params=pltpu.CompilerParams(
            vmem_limit_bytes=63 << 20, collective_id=3, has_side_effects=True
        ),
        cost_estimate=estimate(2 * near_tokens * width * attn_cols, 10 * near_tokens * width),
    )(line, weight, own_in, grad_middle, gain, gain_two, rows_one, line, block)


def place_kernel(count, info, *refs):
    out = refs[count]
    for r in range(count):

        @pl.when(pl.program_id(0) == r)
        def _():
            out[0] = refs[r][...]


def place_rows(rows, order):
    length, width = rows[0].shape
    count = len(rows)
    held = pl.BlockSpec((length, width), lambda s, info: (0, 0), pipeline_mode=pl.Buffered(1))
    return pl.pallas_call(
        functools.partial(place_kernel, count),
        grid_spec=pltpu.PrefetchScalarGridSpec(
            num_scalar_prefetch=1,
            grid=(count,),
            in_specs=[held] * count,
            out_specs=pl.BlockSpec((1, length, width), lambda s, info: (info[s], 0, 0)),
        ),
        out_shape=jax.ShapeDtypeStruct((count, length, width), LOW),
        compiler_params=pltpu.CompilerParams(vmem_limit_bytes=32 << 20),
        cost_estimate=estimate(0, 4 * count * length * width),
    )(order, *rows)


def turn(values, cosine, sine_signed):
    return values * cosine + pltpu.roll(values, values.shape[-1] // 2, 1) * sine_signed


def turn_back(values, cosine, sine_signed):
    return values * cosine - pltpu.roll(values, values.shape[-1] // 2, 1) * sine_signed


def project_kernel(
    heads, head_dim, x0, x1, x2, x3, gains, weight, bias, cosine, sine, h_out, q_out, k_out, v_out, gain
):
    slot = pl.program_id(0)

    @pl.when(slot == 0)
    def _():
        gain[...] = gains[...].astype(WIDE).T[:8]


    def run(x_ref):
        x = x_ref[...].astype(WIDE)
        scale_inv = lax.rsqrt(jnp.mean(x * x, axis=-1, keepdims=True) + EPS)
        normed = (x * scale_inv * gain[0:1]).astype(LOW)
        h_out[0] = normed
        lin = jnp.dot(normed, weight[...], preferred_element_type=WIDE) + bias[...]
        cos, sin = cosine[0], sine[0]
        for h in range(heads + 1):
            part = turn(lin[:, h * head_dim : (h + 1) * head_dim], cos, sin).astype(LOW)
            if h < heads:
                q_out[0, :, h * head_dim : (h + 1) * head_dim] = part
            else:
                k_out[0] = part
        v_out[0] = lin[:, (heads + 1) * head_dim :].astype(LOW)

    for r, x_ref in enumerate((x0, x1, x2, x3)):
        pl.when(slot == r)(functools.partial(run, x_ref))


def project(rows, held, bias, cosine, sine, heads, head_dim):
    length, width = rows[0].shape
    count = len(rows)
    cols = (heads + 2) * head_dim
    whole = whole_spec
    by_slot = lambda *shape: pl.BlockSpec((1, *shape), lambda s: (s,) + (0,) * len(shape))
    return pl.pallas_call(
        functools.partial(project_kernel, heads, head_dim),
        grid=(count,),
        in_specs=[whole(length, width)] * count
        + [part_spec(width, 128, cols // 128), part_spec(width, cols, 0), whole(1, cols)]
        + [by_slot(length, head_dim)] * 2,
        out_specs=[
            by_slot(length, width),
            by_slot(length, heads * head_dim),
            by_slot(length, head_dim),
            by_slot(length, head_dim),
        ],
        out_shape=[
            jax.ShapeDtypeStruct((count, length, width), LOW),
            jax.ShapeDtypeStruct((count, length, heads * head_dim), LOW),
            jax.ShapeDtypeStruct((count, length, head_dim), LOW),
            jax.ShapeDtypeStruct((count, length, head_dim), LOW),
        ],
        scratch_shapes=[pltpu.VMEM((8, width), WIDE)],
        compiler_params=pltpu.CompilerParams(vmem_limit_bytes=56 << 20),
        cost_estimate=pl.CostEstimate(
            flops=2 * count * length * width * cols,
            bytes_accessed=count * length * (2 * width + cols) * 2 + width * cols * 2,
            transcendentals=0,
        ),
    )(*rows, held, held, bias, cosine, sine)


def row_blocks(length):
    return [(i, min(256, length)) for i in range(0, length, min(256, length))]


def key_biases(length, offset, start, rows, past, keys):
    past_pos = lax.broadcasted_iota(jnp.int32, (1, past), 1)
    past_bias = jnp.where((past_pos < offset) & (past_pos < length), 0.0, NEG_FILL)
    query_pos = offset + start + lax.broadcasted_iota(jnp.int32, (rows, keys), 0)
    own_pos = offset + lax.broadcasted_iota(jnp.int32, (rows, keys), 1)
    own_bias = jnp.where((own_pos <= query_pos) & (own_pos < length), 0.0, NEG_FILL)
    return past_bias, own_bias


def dot_cols(left, right):
    return lax.dot_general(left, right, (((1,), (1,)), ((), ())), preferred_element_type=WIDE)


def dot_rows(left, right):
    return lax.dot_general(left, right, (((0,), (0,)), ((), ())), preferred_element_type=WIDE)


def attend_rows(
    heads, head_dim, scale, length, offset, q, k_past, v_past, k_own, v_own, weight, out, lse, put
):
    past = k_past.shape[1]
    for start, rows in row_blocks(q.shape[1]):
        keys = start + rows
        past_bias, own_bias = key_biases(length, offset, start, rows, past, keys)
        here = slice(start, start + rows)
        for h in range(heads):
            cols = slice(h * head_dim, (h + 1) * head_dim)
            query = q[0, here, cols]
            s_past = dot_cols(query, k_past[0]) * scale + past_bias
            s_own = dot_cols(query, k_own[0, :keys]) * scale + own_bias
            top = jnp.maximum(
                jnp.max(s_past, axis=1, keepdims=True), jnp.max(s_own, axis=1, keepdims=True)
            )
            e_past, e_own = jnp.exp(s_past - top), jnp.exp(s_own - top)
            total = jnp.sum(e_past, axis=1, keepdims=True) + jnp.sum(e_own, axis=1, keepdims=True)
            inverse = 1.0 / total
            mixed = jnp.dot(
                (e_past * inverse).astype(LOW), v_past[0], preferred_element_type=WIDE
            ) + jnp.dot((e_own * inverse).astype(LOW), v_own[0, :keys], preferred_element_type=WIDE)
            out[0, here, cols] = mixed.astype(LOW)
            lse[0, here, h : h + 1] = top + jnp.log(total)
        rows_out = dot_cols(out[0, here], weight[...]).astype(LOW)
        put(here, rows_out)


def attend_kernel(
    heads, head_dim, scale, first, total_slots, info, q, k_past, v_past, k_own, v_own, weight, out, lse, *parts
):
    length, offset = info[first + pl.program_id(0)], info[total_slots]

    def put(here, value):
        for i, part in enumerate(parts):

            @pl.when(pl.program_id(0) == i)
            def _():
                part[here] = value

    attend_rows(heads, head_dim, scale, length, offset, q, k_past, v_past, k_own, v_own, weight, out, lse, put)


def attend_forward(info, q, k_past, v_past, k_own, v_own, weight, heads, head_dim, scale, first, count):
    _, length, width = q.shape
    past = k_past.shape[1]
    by_slot = lambda *shape: pl.BlockSpec((1, *shape), lambda s, info: (first + s,) + (0,) * len(shape))
    out_slot = lambda *shape: pl.BlockSpec((1, *shape), lambda s, info: (s,) + (0,) * len(shape))
    keys = count * length * (past + length) * heads
    return pl.pallas_call(
        functools.partial(attend_kernel, heads, head_dim, scale, first, q.shape[0]),
        grid_spec=pltpu.PrefetchScalarGridSpec(
            num_scalar_prefetch=1,
            grid=(count,),
            in_specs=[
                by_slot(length, width),
                by_slot(past, head_dim),
                by_slot(past, head_dim),
                by_slot(length, head_dim),
                by_slot(length, head_dim),
                whole_spec(*weight.shape, once=True),
            ],
            out_specs=[out_slot(length, width), out_slot(length, 128)]
            + [whole_spec(length, weight.shape[0])] * count,
        ),
        out_shape=[
            jax.ShapeDtypeStruct((count, length, width), LOW),
            jax.ShapeDtypeStruct((count, length, 128), WIDE),
        ]
        + [jax.ShapeDtypeStruct((length, weight.shape[0]), LOW)] * count,
        compiler_params=pltpu.CompilerParams(vmem_limit_bytes=56 << 20),
        cost_estimate=estimate(4 * keys * head_dim, 4 * count * length * width, keys),
    )(info, q, k_past, v_past, k_own, v_own, weight)


def attend_back_rows(
    heads, head_dim, scale, length, offset, q, k_past, v_past, k_own, v_own, grad, lse, cosine, sine, put,
    dk_past, dk_own, dv_past, dv_own
):
    past = k_past.shape[1]
    for start, rows in row_blocks(q.shape[1]):
        keys = start + rows
        past_bias, own_bias = key_biases(length, offset, start, rows, past, keys)
        here = slice(start, start + rows)
        cos, sin = cosine[0, here], sine[0, here]
        for h in range(heads):
            cols = slice(h * head_dim, (h + 1) * head_dim)
            query, upstream = q[0, here, cols], grad[0, here, cols]
            log_total = lse[0, here, h : h + 1]
            p_past = jnp.exp(dot_cols(query, k_past[0]) * scale + past_bias - log_total)
            p_own = jnp.exp(dot_cols(query, k_own[0, :keys]) * scale + own_bias - log_total)
            g_past = dot_cols(upstream, v_past[0])
            g_own = dot_cols(upstream, v_own[0, :keys])
            row_dot = jnp.sum(p_past * g_past, axis=1, keepdims=True) + jnp.sum(
                p_own * g_own, axis=1, keepdims=True
            )
            s_past = (p_past * (g_past - row_dot)).astype(LOW)
            s_own = (p_own * (g_own - row_dot)).astype(LOW)
            dq = (
                jnp.dot(s_past, k_past[0], preferred_element_type=WIDE)
                + jnp.dot(s_own, k_own[0, :keys], preferred_element_type=WIDE)
            ) * scale
            put(here, cols, turn_back(dq, cos, sin).astype(LOW))
            dk_past[...] += dot_rows(s_past, query)
            dk_own[:keys] += dot_rows(s_own, query)
            dv_past[...] += dot_rows(p_past.astype(LOW), upstream)
            dv_own[:keys] += dot_rows(p_own.astype(LOW), upstream)


def attend_back_kernel(
    heads,
    head_dim,
    scale,
    info,
    q,
    k_past,
    v_past,
    k_own,
    v_own,
    grad,
    lse,
    cosine,
    sine,
    dq_out,
    mine_past,
    mine_own,
    other_past,
    other_own,
    dk_past,
    dk_own,
    dv_past,
    dv_own,
):
    slot = pl.program_id(0)
    length, offset = info[slot], info[pl.num_programs(0)]
    parity = info[pl.num_programs(0) + 1]
    for total in (dk_past, dk_own, dv_past, dv_own):
        total[...] = jnp.zeros_like(total)
    attend_back_rows(
        heads, head_dim, scale, length, offset, q, k_past, v_past, k_own, v_own, grad, lse, cosine, sine,
        lambda here, cols, value: dq_out.__setitem__((0, here, cols), value),
        dk_past, dk_own, dv_past, dv_own,
    )

    @pl.when(parity == 0)
    def _():
        mine_past[0] = dk_past[...] * scale
        mine_own[0] = dk_own[...] * scale
        other_past[0] = dv_past[...]
        other_own[0] = dv_own[...]

    @pl.when(parity != 0)
    def _():
        mine_past[0] = dv_past[...]
        mine_own[0] = dv_own[...]
        other_past[0] = dk_past[...] * scale
        other_own[0] = dk_own[...] * scale


def attend_backward(
    info, q, k_past, v_past, k_own, v_own, grad, lse, cosine, sine, heads, head_dim, scale
):
    count, length, width = q.shape
    past = k_past.shape[1]
    by_slot = lambda *shape: pl.BlockSpec((1, *shape), lambda s, info: (s,) + (0,) * len(shape))
    keys = count * length * (past + length) * heads
    return pl.pallas_call(
        functools.partial(attend_back_kernel, heads, head_dim, scale),
        grid_spec=pltpu.PrefetchScalarGridSpec(
            num_scalar_prefetch=1,
            grid=(count,),
            in_specs=[
                by_slot(length, width),
                by_slot(past, head_dim),
                by_slot(past, head_dim),
                by_slot(length, head_dim),
                by_slot(length, head_dim),
                by_slot(length, width),
                by_slot(length, 128),
                by_slot(length, head_dim),
                by_slot(length, head_dim),
            ],
            out_specs=[
                by_slot(length, width),
                by_slot(past, head_dim),
                by_slot(length, head_dim),
                by_slot(past, head_dim),
                by_slot(length, head_dim),
            ],
            scratch_shapes=[
                pltpu.VMEM((past, head_dim), WIDE),
                pltpu.VMEM((length, head_dim), WIDE),
                pltpu.VMEM((past, head_dim), WIDE),
                pltpu.VMEM((length, head_dim), WIDE),
            ],
        ),
        out_shape=[
            jax.ShapeDtypeStruct((count, length, width), LOW),
            jax.ShapeDtypeStruct((count, past, head_dim), WIDE),
            jax.ShapeDtypeStruct((count, length, head_dim), WIDE),
            jax.ShapeDtypeStruct((count, past, head_dim), WIDE),
            jax.ShapeDtypeStruct((count, length, head_dim), WIDE),
        ],
        compiler_params=pltpu.CompilerParams(vmem_limit_bytes=56 << 20),
        cost_estimate=estimate(10 * keys * head_dim, 8 * count * length * width, keys),
    )(info, q, k_past, v_past, k_own, v_own, grad, lse, cosine, sine)


def attend_sum_kernel(
    heads, head_dim, scale, slots, info, q, k_past, v_past, k_own, v_own, weight, own_in, gain, out, lse, middle,
    normed, parts, core_in, far_in, send, recv
):
    step = pl.program_id(0)
    slot = slots - 1 - step
    core, far, _ = partners_of()
    remote = remote_copy(send, recv)
    cores = [remote(parts.at[3 - 2 * k], core_in.at[k], k, core) for k in range(2)]
    to_far = remote(parts.at[2], far_in, 2, far)

    @pl.when(step == 0)
    def _():
        meet((core, far))

    def put(here, value):
        parts[slot, here] = value

    offset = lax.axis_index("ctx") * q.shape[1]
    attend_rows(
        heads, head_dim, scale, info[slot], offset, q, k_past, v_past, k_own, v_own, weight, out, lse, put
    )
    for k in range(2):
        pl.when(step == 2 * k)(cores[k].start)

    @pl.when(step == 1)
    def _():
        cores[0].wait_recv()
        parts[2] = (parts[2].astype(WIDE) + core_in[0].astype(WIDE)).astype(LOW)
        to_far.start()

    @pl.when(step == slots - 1)
    def _():
        cores[1].wait_recv()
        to_far.wait_recv()
        rows = own_in[...].astype(WIDE) + parts[0].astype(WIDE)
        rows = rows + core_in[1].astype(WIDE) + far_in[...].astype(WIDE)
        middle[...] = rows
        inverse = lax.rsqrt(jnp.mean(rows * rows, axis=-1, keepdims=True) + EPS)
        normed[...] = (rows * inverse * gain[...]).astype(LOW)
        for copy in (*cores, to_far):
            copy.wait_send()


def attend_sum(info, q, k_past, v_past, k_own, v_own, weight, own_in, gain, heads, head_dim, scale):
    count, length, width = q.shape
    past, model_width = k_past.shape[1], own_in.shape[1]
    by_slot = lambda *shape: pl.BlockSpec(
        (1, *shape), lambda i, info: (count - 1 - i,) + (0,) * len(shape)
    )
    keys = count * length * (past + length) * heads
    return pl.pallas_call(
        functools.partial(attend_sum_kernel, heads, head_dim, scale, count),
        grid_spec=pltpu.PrefetchScalarGridSpec(
            num_scalar_prefetch=1,
            grid=(count,),
            in_specs=[
                by_slot(length, width),
                by_slot(past, head_dim),
                by_slot(past, head_dim),
                by_slot(length, head_dim),
                by_slot(length, head_dim),
                whole_spec(*weight.shape, once=True),
                whole_spec(length, model_width, once=True),
                whole_spec(1, model_width),
            ],
            out_specs=[
                by_slot(length, width),
                by_slot(length, 128),
                whole_spec(length, model_width, once=True),
                whole_spec(length, model_width, once=True),
            ],
            scratch_shapes=[
                pltpu.VMEM((count, length, model_width), LOW),
                pltpu.VMEM((2, length, model_width), LOW),
                pltpu.VMEM((length, model_width), LOW),
                pltpu.SemaphoreType.DMA((3,)),
                pltpu.SemaphoreType.DMA((3,)),
            ],
        ),
        out_shape=[
            jax.ShapeDtypeStruct((count, length, width), LOW),
            jax.ShapeDtypeStruct((count, length, 128), WIDE),
            jax.ShapeDtypeStruct((length, model_width), WIDE),
            jax.ShapeDtypeStruct((length, model_width), LOW),
        ],
        compiler_params=pltpu.CompilerParams(
            vmem_limit_bytes=56 << 20, collective_id=5, has_side_effects=True
        ),
        cost_estimate=estimate(4 * keys * head_dim, 4 * count * length * width, keys),
    )(info, q, k_past, v_past, k_own, v_own, weight, own_in, gain)


def exchange_kernel(
    heads, head_dim, scale, slots, tiles, info, q, k_past, v_past, k_own, v_own, rows, weight, lse, cosine, sine,
    cosine_all, sine_all, branch, mixed, mlp_far, mlp_side, mlp_own, middle, line, out_grad, block, mine_past,
    mine_own, other_past, other_own, got_past, got_own, side_out, side_in, dk_past, dk_own, dv_past, dv_own,
    own_rows, last_in, grad, send, recv, load
):
    step = pl.program_id(0)
    tensor_rank = lax.axis_index("tp")
    core, far, side = partners_of()
    parity = lax.rem(tensor_rank, 2)
    offset = lax.axis_index("ctx") * q.shape[1]
    remote = remote_copy(send, recv)
    pasts = [remote(other_past.at[r], got_past.at[r ^ 1], r, core) for r in range(slots)]
    owns = [remote(other_own.at[r], got_own.at[r ^ 1], slots + r, core) for r in range(slots)]
    sides = [remote(side_out.at[r], side_in.at[r], 2 * slots + r, side) for r in range(slots)]
    lasts = [
        remote(mlp_far, last_in.at[0], 3 * slots, far),
        remote(mlp_side, last_in.at[1], 3 * slots + 1, side),
    ]
    loading = pltpu.make_async_copy(mlp_own, own_rows, load)

    @pl.when(step == 0)
    def _():
        loading.start()
        meet((core, far, side))
        for copy in lasts:
            copy.start()

    @pl.when(step < slots)
    def _():
        length = info[jnp.minimum(step, slots - 1)]
        for total in (dk_past, dk_own, dv_past, dv_own):
            total[...] = jnp.zeros_like(total)
        grad[0] = jnp.dot(rows[...], weight[...], preferred_element_type=WIDE).astype(LOW)
        attend_back_rows(
            heads, head_dim, scale, length, offset, q, k_past, v_past, k_own, v_own, grad, lse, cosine,
            sine, lambda here, cols, value: line.__setitem__((step, here, cols), value),
            dk_past, dk_own, dv_past, dv_own,
        )

        @pl.when(parity == 0)
        def _():
            mine_past[step] = dk_past[...] * scale
            mine_own[step] = dk_own[...] * scale
            other_past[step] = dv_past[...]
            other_own[step] = dv_own[...]

        @pl.when(parity != 0)
        def _():
            mine_past[step] = dv_past[...]
            mine_own[step] = dv_own[...]
            other_past[step] = dk_past[...] * scale
            other_own[step] = dk_own[...] * scale

    for r in range(slots):

        def start(r=r):
            pasts[r].start()
            owns[r].start()

        pl.when(step == r)(start)

    for pair in range(0, slots, 2):

        def merge(pair=pair):
            for r in (pair, pair + 1):
                pasts[r ^ 1].wait_recv()
                side_out[r] = (mine_past[r] + got_past[r]).astype(LOW)
                sides[r].start()

        pl.when(step == pair + 1)(merge)

    @pl.when(step >= slots)
    def _():
        out_grad[...] = dot_rows(branch[...], mixed[...]).astype(LOW)

    @pl.when(step == slots + tiles - 1)
    def _():
        for r in range(slots):
            owns[r ^ 1].wait_recv()
            sides[r].wait_recv()
            total = mine_own[r] + got_own[r] + side_in[r].astype(WIDE)
            back = turn_back(total, cosine_all[r], sine_all[r])
            line[r, :, heads * head_dim :] = jnp.where(parity == 0, back, total).astype(LOW)
        loading.wait()
        for copy in lasts:
            copy.wait_recv()
        block[...] = (
            middle[...] + own_rows[...].astype(WIDE) + last_in[0].astype(WIDE) + last_in[1].astype(WIDE)
        ).astype(LOW)
        for copy in (*pasts, *owns, *sides, *lasts):
            copy.wait_send()


def attend_exchange(
    info, q, k_past, v_past, k_own, v_own, weight, lse, cosine, sine, heads, head_dim, scale, branch, mixed, mlp,
    middle
):
    count, length, width = q.shape
    past = k_past.shape[1]
    tokens, model_width = branch.shape
    tile = 256
    tiles = model_width // tile
    slot = lambda i: jnp.minimum(i, count - 1)
    by_slot = lambda *shape: pl.BlockSpec((1, *shape), lambda i, info: (slot(i),) + (0,) * len(shape))
    column = lambda i: jnp.clip(i - count, 0, tiles - 1)
    held = lambda *shape: pl.BlockSpec(
        shape, lambda i, info: (0,) * len(shape), pipeline_mode=pl.Buffered(1)
    )
    line_cols = width + head_dim
    return pl.pallas_call(
        functools.partial(exchange_kernel, heads, head_dim, scale, count, tiles),
        grid_spec=pltpu.PrefetchScalarGridSpec(
            num_scalar_prefetch=1,
            grid=(count + tiles,),
            in_specs=[
                by_slot(length, width),
                by_slot(past, head_dim),
                by_slot(past, head_dim),
                by_slot(length, head_dim),
                by_slot(length, head_dim),
                pl.BlockSpec((length, model_width), lambda i, info: (slot(i), 0)),
                held(*weight.shape),
                by_slot(length, 128),
                by_slot(length, head_dim),
                by_slot(length, head_dim),
                held(count, length, head_dim),
                held(count, length, head_dim),
                pl.BlockSpec((tokens, tile), lambda i, info: (0, column(i))),
                held(*mixed.shape),
            ]
            + [ANYWHERE] * 3
            + [held(length, model_width)],
            out_specs=[
                held(count, length, line_cols),
                pl.BlockSpec((tile, width), lambda i, info: (column(i), 0)),
                held(length, model_width),
            ],
            scratch_shapes=[pltpu.VMEM((count, length, head_dim), WIDE)] * 6
            + [pltpu.VMEM((count, length, head_dim), LOW)] * 2
            + [pltpu.VMEM((length, head_dim), WIDE)] * 4
            + [
                pltpu.VMEM((length, model_width), LOW),
                pltpu.VMEM((2, length, model_width), LOW),
                pltpu.VMEM((1, length, width), LOW),
                pltpu.SemaphoreType.DMA((3 * count + 2,)),
                pltpu.SemaphoreType.DMA((3 * count + 2,)),
                pltpu.SemaphoreType.DMA,
            ],
        ),
        out_shape=[
            jax.ShapeDtypeStruct((count, length, line_cols), LOW),
            jax.ShapeDtypeStruct((model_width, width), LOW),
            jax.ShapeDtypeStruct((length, model_width), LOW),
        ],
        compiler_params=pltpu.CompilerParams(
            vmem_limit_bytes=63 << 20, collective_id=4, has_side_effects=True
        ),
        cost_estimate=estimate(2 * tokens * model_width * width, 10 * tokens * width),
    )(info, q, k_past, v_past, k_own, v_own, branch, weight, lse, cosine, sine, cosine, sine, branch, mixed, *mlp, middle)


def local(
    hidden_in,
    cotangent,
    seq_lengths,
    positions,
    permutation,
    query_weight,
    keyval_weight,
    output_weight,
    norm_gains,
    bias_query,
    bias_keyval,
    gate_weight,
    up_weight,
    down_weight,
):
    group_rank = lax.axis_index("fsdp")
    ctx_rank = lax.axis_index("ctx")
    tensor_rank = lax.axis_index("tp")
    fsdp_count = lax.axis_size("fsdp")
    ctx_count = lax.axis_size("ctx")
    tensor_count = lax.axis_size("tp")
    seq_grp, local_len, model_width = hidden_in.shape
    heads, head_dim = bias_query.shape
    keyval_heads = bias_keyval.shape[0] // 2
    assert seq_grp == tensor_count == fsdp_count == len(DEAL_SHIFT)
    token_count = seq_grp * local_len
    scale = 1.0 / math.sqrt(head_dim)
    offset = ctx_rank * local_len
    head_pair = tensor_rank // (tensor_count // keyval_heads)
    parity = tensor_rank % 2
    assert DEAL_SHIFT == tuple((t % 2) * 2 + t // 2 for t in range(tensor_count))

    entry = jnp.arange(permutation.shape[0])
    entry_group, entry_slot = entry // seq_grp, entry % seq_grp
    home_group, home_slot = lax.div(permutation, seq_grp), lax.rem(permutation, seq_grp)
    places = jnp.arange(2 * seq_grp)
    near_places = places < seq_grp
    slot_rank = tensor_rank ^ (places % seq_grp)
    shift_of = lambda rank: lax.rem(rank, 2) * 2 + lax.div(rank, 2)
    target = lax.rem(group_rank + shift_of(tensor_rank), fsdp_count)
    leaving = jnp.sum(jnp.where((entry_group == target) & (home_group == group_rank), home_slot, 0))
    source = lax.rem(group_rank + fsdp_count - shift_of(slot_rank), fsdp_count)
    hit = (entry_group == group_rank)[None] & (home_group[None] == source[:, None])
    slot_now = jnp.sum(jnp.where(hit, entry_slot[None], 0), axis=1)
    seq_now = jnp.sum(jnp.where(hit, permutation[None], 0), axis=1)
    targets = lax.rem(group_rank + shift_of(slot_rank), fsdp_count)
    back_hit = (entry_group[None] == targets[:, None]) & (home_group == group_rank)[None]
    home_order = jnp.sum(jnp.where(back_hit, home_slot[None], 0), axis=1)[:seq_grp]
    there = [
        (f * tensor_count + t, (f + DEAL_SHIFT[t]) % fsdp_count * tensor_count + t)
        for f in range(fsdp_count)
        for t in range(tensor_count)
    ]
    back = [(target, source) for source, target in there]

    split = units_split()
    head_width = 2 * head_dim
    query_cols = heads * head_dim
    near_cols = query_cols + head_width + 128

    outgoing = lax.dynamic_index_in_dim(hidden_in, leaving, 0, keepdims=False)
    own_in = lax.ppermute(outgoing, ("fsdp", "tp"), there)
    small = jnp.concatenate(
        [
            query_weight,
            lax.dynamic_slice_in_dim(keyval_weight, head_pair * head_width, head_width, axis=1),
            jnp.pad(norm_gains.T, ((0, 0), (0, 128 - norm_gains.shape[0]))),
            output_weight.T,
        ],
        axis=1,
    )
    seq_hit = seq_now[:, None] == entry[None]
    lengths_now = jnp.sum(jnp.where(seq_hit, seq_lengths[None], 0), axis=1)
    more = jnp.where(places == seq_grp, offset, jnp.where(places == seq_grp + 1, parity, 0))
    info = jnp.where(near_places, lengths_now, more).astype(jnp.int32)
    positions_now = jnp.sum(
        jnp.where(seq_hit[:seq_grp, :, None], positions[None], 0), axis=1
    )
    lane = jnp.arange(head_dim)
    frequency = 1.0 / ROPE_BASE ** ((lane % (head_dim // 2)).astype(WIDE) * 2.0 / head_dim)
    angles = positions_now.astype(WIDE)[..., None] * frequency
    cosine = jnp.cos(angles)
    sine = jnp.sin(angles) * jnp.where(lane < head_dim // 2, -1.0, 1.0)
    pick_info = jnp.where(near_places, slot_now, slot_now ^ tensor_rank).astype(jnp.int32)
    units = gate_weight.shape[1]
    units_pad = -(-units // 256) * 256
    widen = lambda w: jnp.pad(w, ((0, 0), (0, units_pad - units)))
    shards = [widen(w) for w in (down_weight.T, gate_weight, up_weight)]
    if split:
        half_units = units_pad // 2
        cut = lambda w, c: lax.dynamic_slice_in_dim(w, c * half_units, half_units, axis=1)

        def in_order(own, other):
            return jnp.stack(
                [jnp.where(ctx_rank == 0, own, other), jnp.where(ctx_rank == 0, other, own)]
            )

        def all_rows(both, *earlier):
            full = lax.all_gather(after(both, *earlier), "fsdp", axis=0, tiled=False)
            return full.reshape(-1, both.shape[-1])

        first_units = half_units - half_units // 2 // 256 * 256
        first_cols = 3 * first_units

        def in_parts(c):
            halves = [cut(w, c) for w in shards]
            return jnp.concatenate(
                [w[:, :first_units] for w in halves] + [w[:, first_units:] for w in halves], axis=1
            )

        leaving_units, own_units = in_parts(1 - ctx_rank), in_parts(ctx_rank)
        slot_pick = lax.dynamic_index_in_dim(cotangent, tensor_rank, 0, keepdims=False)
        small = after(small, outgoing, leaving_units, cosine, sine, slot_pick)
        small_both = in_order(small, from_partner(small, "ctx", 1))
        arriving_units = from_partner(after(leaving_units, small_both), "ctx", 1)
        other_own = from_partner(after(slot_pick, arriving_units), "ctx", 1)
        both_a = in_order(own_units[:, :first_cols], arriving_units[:, :first_cols])
        both_b = in_order(own_units[:, first_cols:], arriving_units[:, first_cols:])
    else:
        all_rows = lambda shard, *earlier: lax.all_gather(
            shard, ("fsdp", "ctx"), axis=0, tiled=True
        )
        small_both, unit_both, half_units = small, jnp.concatenate(shards, axis=1), units_pad
    far_in = from_partner(own_in, "tp", 2)
    near_in = from_partner(own_in, "tp", 1)
    ready = (info, pick_info, own_units, home_order) if split else (cosine, sine, info)
    cross_in = from_partner(after(far_in, *ready), "tp", 1)

    near_full = all_rows(small_both, own_in)
    if split:
        units_a = all_rows(both_a, cross_in)
        units_b = all_rows(both_b, cross_in)
    else:
        down_full = all_rows(unit_both[..., :half_units], cross_in)
        gate_up_full = all_rows(unit_both[..., half_units:], cross_in)
    project_full = near_full[:, : query_cols + head_width]
    output_full = near_full[:, near_cols:]
    bias_head = lax.dynamic_slice_in_dim(bias_keyval, head_pair * 2, 2, axis=0)
    bias_row = jnp.concatenate([bias_query.reshape(1, -1), bias_head.reshape(1, -1)], axis=1).astype(WIDE)
    normed_one, query_rot, key_own, value_own = project(
        (own_in, near_in, far_in, cross_in),
        near_full,
        bias_row,
        after(cosine, other_own, both_a, both_b, info, pick_info) if split else cosine,
        sine,
        heads,
        head_dim,
    )
    gains_now = near_full[:, query_cols + head_width : near_cols][:, :2].astype(WIDE).T
    if split:
        key_past, value_past = lax.ppermute((key_own, value_own), "ctx", [(0, 1)])
        other_far = from_partner(other_own, "tp", 2)
        other_near = from_partner(after(other_own, key_past), "tp", 1)
        other_cross = from_partner(after(other_far, key_past), "tp", 1)
        other_rows = (other_own, other_near, other_far, other_cross)
        key_past = after(key_past, other_far)
    else:
        key_past = lax.all_gather(key_own, "ctx", axis=1, tiled=True)
        value_past = lax.all_gather(value_own, "ctx", axis=1, tiled=True)
    in_share = own_in.astype(WIDE)
    if split:
        mixed, lse, middle_share, normed_share = attend_sum(
            info,
            query_rot,
            key_past,
            value_past,
            key_own,
            value_own,
            output_full,
            own_in,
            gains_now[1:2],
            heads,
            head_dim,
            scale,
        )
    else:
        attend = lambda first, *held: attend_forward(
            info, query_rot, *held, key_own, value_own, output_full, heads, head_dim, scale, first, 2
        )

        mixed_far, lse_far, *attn_far = attend(2, key_past, value_past)
        attn_wide = collect_far(attn_far[0], attn_far[1])
        attn_got = from_partner(attn_wide, "tp", 2)
        mixed_near, lse_near, *attn_near = attend(0, after(key_past, attn_wide), value_past)
        attn_core = from_partner(attn_near[1], "tp", 1)
        middle_share = (
            in_share
            + attn_near[0].astype(WIDE)
            + attn_core.astype(WIDE)
            + attn_got.astype(WIDE)
        )
        inv_two = lax.rsqrt(jnp.mean(middle_share * middle_share, axis=-1, keepdims=True) + EPS)
        normed_share = (middle_share * inv_two * gains_now[1]).astype(LOW)
        mixed = jnp.concatenate([mixed_near, mixed_far], axis=0)
        lse = jnp.concatenate([lse_near, lse_far], axis=0)
    half_len = local_len // 2

    if split:
        grad_hidden, grad_rows = chosen_rows(
            pick_info,
            after(cotangent, normed_share),
            other_rows,
            units_a,
            0,
            3,
        )
    else:
        grad_slots = [
            lax.dynamic_index_in_dim(cotangent, slot_now[r], 0, keepdims=False) for r in range(seq_grp)
        ]
        grad_hidden, grad_rows = stack_rows([(g,) for g in grad_slots], down_full, 0, 1)

    def spread_all(own):
        far = from_partner(own, "tp", 2)
        near = from_partner(own, "tp", 1)
        if not split:
            return (own, near, far, from_partner(far, "tp", 1))
        side = from_partner(own, "ctx", 1)
        held = after(far, grad_hidden), after(side, grad_hidden)
        across = from_partner(held[0][:half_len], "ctx", 1), from_partner(held[1][half_len:], "tp", 2)
        cores = [from_partner(v, "tp", 1) for v in held]
        return (own, near, far, cores[0], side, cores[1], *across)

    def in_slots(rows):
        if not split:
            return [(row,) for row in rows]
        return [(row,) for row in rows[:6]] + [rows[6:]]

    mixed_flat = mixed.reshape(token_count, query_cols)
    own_weight = lax.dynamic_slice_in_dim(
        project_full, query_cols + parity * head_dim, head_dim, axis=1
    )
    back_full = jnp.concatenate([project_full[:, :query_cols], own_weight], axis=1)
    normed_slots = in_slots(spread_all(normed_share))
    if split:
        early = after(units_a, back_full)
        ahead = stack_rows(normed_slots[:6], early, 1, 3, total=8)
        last = [normed_slots[6], tuple(from_partner(after(v, ahead[0]), "tp", 1) for v in normed_slots[6])]
        gate_lin, normed_two = stack_rows(last, units_a, 1, 3, into=ahead, first=6, total=8)
        hidden_a, gate_a, up_a = hidden_units(normed_two, units_a, 2, 3, gate_lin, grad_hidden)
        grad_a = first_grads(grad_rows, normed_two, hidden_a, gate_a, up_a)
        hidden_b, gate_b, up_b = full_units(after(normed_two, grad_a), grad_rows, units_b)
    else:
        gate_lin, normed_two = stack_rows(normed_slots, gate_up_full, 0, 2)
        hidden_act, grad_gate, grad_up = hidden_units(
            normed_two, gate_up_full, 1, 2, gate_lin, grad_hidden
        )

    def collect_all(lefts, weights, *earlier):
        lefts = list(lefts)
        lefts[0] = after(lefts[0], *earlier)
        last = back_rows(lefts, weights, 2, 2, local_len)
        got = [from_partner(collect_far(last[0], last[1]), "tp", 2)]
        first = back_rows(lefts, weights, 0, 2, local_len)
        got.append(from_partner(first[1], "tp", 1))

        def finish():
            return sum((v.astype(WIDE) for v in got), first[0].astype(WIDE))

        return first[0], finish

    if split:
        grad_two_share, down_b, up_grad_b = collect_back(
            (gate_a, up_a),
            (gate_b, up_b),
            units_a,
            units_b,
            grad_rows,
            normed_two,
            hidden_b,
            local_len,
        )
        grad_middle, gain_two, gate_grad_b, grad_branch, *mlp = spread_branch(
            grad_two_share,
            middle_share,
            grad_rows,
            gains_now[1:2],
            hidden_a,
            hidden_b,
            units_a,
            units_b,
            normed_two,
            gate_b,
        )
        mlp_own, mlp_far, mlp_side = mlp
        grad_branch = grad_branch.reshape(token_count, model_width)
    else:
        first_back, finish_back = collect_all(
            (grad_gate, grad_up), ((gate_up_full, 0, 2), (gate_up_full, 1, 2))
        )
        down_grad = contract_rows(after(grad_rows, first_back), hidden_act, LOW)
        gate_grad = contract_rows(normed_two, after(grad_gate, down_grad), LOW)
        grad_two_share = finish_back()
        grad_norm_two, gain_two = norm_backward(
            middle_share, inv_two, gains_now[1], grad_two_share
        )
        grad_middle = grad_slots[0].astype(WIDE) + grad_norm_two
        branch_own = grad_middle.astype(LOW)
        branch_far = from_partner(branch_own, "tp", 2)
        branch_near = from_partner(branch_own, "tp", 1)
        branch_cross = from_partner(branch_far, "tp", 1)
        grad_branch = jnp.concatenate([branch_own, branch_near, branch_far, branch_cross], axis=0)
        up_grad = contract_rows(normed_two, after(grad_up, branch_own), LOW)

    grad_mixed = None if split else product(grad_branch, output_full, LOW)
    attend_args = (
        info,
        query_rot,
        key_past,
        value_past,
        key_own,
        value_own,
        output_full if split else grad_mixed.reshape(seq_grp, local_len, query_cols),
        lse,
        cosine,
        sine,
        heads,
        head_dim,
        scale,
    )
    if split:
        line_grad, output_grad, block_share = attend_exchange(
            *attend_args,
            grad_branch,
            mixed_flat,
            (mlp_far, mlp_side, mlp_own),
            middle_share,
        )
        line_grad = line_grad.reshape(token_count, -1)
    else:
        grad_query, mine_past, mine_own, other_past, other_own = attend_backward(*attend_args)
        swap = lambda value: jnp.stack([value[r ^ 1] for r in range(seq_grp)])
        got_past, got_own = from_partner((other_past, other_own), "tp", 1)
        past_sum = mine_past + swap(got_past)
        own_sum = mine_own + swap(got_own)
        own_sum = own_sum + lax.psum_scatter(past_sum, "ctx", scatter_dimension=1, tiled=True)
        half_lanes = head_dim // 2
        turned = own_sum * cosine - jnp.roll(own_sum, half_lanes, axis=-1) * sine
        own_grad = jnp.where(parity == 0, turned, own_sum).astype(LOW).reshape(token_count, head_dim)
        line_grad = jnp.concatenate([grad_query.reshape(token_count, query_cols), own_grad], axis=1)
    def scatter_units(grad):
        if not split:
            return scatter_sum(grad, ctx_rank, LOW)
        return lax.psum_scatter(grad, "fsdp", scatter_dimension=0, tiled=True)

    unit_grads = (grad_a, down_b, up_grad_b, gate_grad_b) if split else (down_grad, gate_grad, up_grad)
    unit_sums = [scatter_units(unit_grads[0])]
    if split:
        unit_sums += [scatter_units(after(g, unit_sums[0])) for g in unit_grads[1:3]]
        unit_sums += [scatter_units(after(unit_grads[3], unit_sums[0]))]
    else:
        unit_sums += [scatter_units(g) for g in unit_grads[1:]]

    normed_flat = normed_one.reshape(token_count, model_width)
    if split:
        input_share, gain_grad, attn_grad, bias_grad, block_home = finish_rows(
            line_grad,
            after(back_full, *unit_sums),
            own_in,
            grad_middle,
            gains_now[0:1],
            gain_two,
            normed_flat,
            block_share,
        )
        attn_grad = jnp.concatenate([attn_grad, output_grad], axis=1)
    else:
        half = token_count // 2
        line_far = contract_cols(line_grad[half:], back_full, LOW).reshape(2, local_len, model_width)
        line_near = contract_cols(line_grad[:half], back_full, LOW).reshape(2, local_len, model_width)
        line_wide = collect_far(line_far[0], line_far[1])
        line_got = from_partner(line_wide, "tp", 2)
        line_core = from_partner(line_near[1], "tp", 1)
        first_mlp, finish_mlp = collect_all((hidden_act,), ((down_full, 0, 1),), up_grad, branch_far)
        block_share = (middle_share + finish_mlp()).astype(LOW)
        grad_one_share = line_near[0].astype(WIDE) + line_core.astype(WIDE) + line_got.astype(WIDE)
        inv_one = lax.rsqrt(jnp.mean(in_share * in_share, axis=-1, keepdims=True) + EPS)
        grad_norm_one, gain_one = norm_backward(in_share, inv_one, gains_now[0], grad_one_share)
        input_share = (grad_middle + grad_norm_one).astype(LOW)
        attn_grad = jnp.concatenate(
            [contract_rows(normed_flat, line_grad, LOW), contract_rows(grad_branch, mixed_flat, LOW)],
            axis=1,
        )
        bias_grad = jnp.sum(line_grad.astype(WIDE), axis=0)

    shard_count = fsdp_count * ctx_count
    share = head_dim // shard_count
    if not split:
        gain_grad = jnp.concatenate([gain_one, gain_two], axis=0)
        gain_grad = gain_grad + from_partner(gain_grad, "tp", 1)
        gain_grad = gain_grad + from_partner(gain_grad, "tp", 2)
    bias_cols = jnp.transpose(bias_grad.reshape(heads + 1, shard_count, share), (1, 2, 0))
    bias_cols = jnp.pad(bias_cols, ((0, 0), (0, (model_width - head_dim) // shard_count), (0, 0)))
    tiny = jnp.concatenate([gain_grad.T, bias_cols.reshape(model_width, heads + 1)], axis=1)
    tiny = jnp.pad(tiny, ((0, 0), (0, 128 - tiny.shape[1]))).astype(LOW)
    attn_grad = jnp.concatenate([attn_grad, tiny], axis=1)
    if split:
        attn_blocks = attn_grad.reshape(fsdp_count, ctx_count, -1, attn_grad.shape[1])
        kept, sent = scatter_ctx(attn_blocks, ctx_rank)
        attn_held = (kept.astype(WIDE) + from_partner(sent, "ctx", 1).astype(WIDE)).astype(LOW)
        attn_held = attn_held.reshape(-1, attn_grad.shape[1])
        attn_end = lax.psum_scatter(after(attn_held, *unit_sums), "fsdp", scatter_dimension=0, tiled=True)
    else:
        attn_end = scatter_sum(attn_grad, ctx_rank, LOW, *unit_sums)


    def leave(share):
        return lax.ppermute(share, ("fsdp", "tp"), back)

    def arrive(own):
        far = from_partner(own, "tp", 2)
        near = from_partner(own, "tp", 1)
        return (own, near, far, from_partner(far, "tp", 1))

    input_home = leave(input_share)
    if not split:
        block_home = leave(block_share)
    block_out = place_rows(arrive(block_home), home_order)
    if split:

        def unit_end(total, *earlier):
            kept, sent = scatter_ctx(total.reshape(1, ctx_count, -1, total.shape[1]), ctx_rank)
            return kept[0], from_partner(after(sent[0], *earlier), "ctx", 1)

        input_home = after(input_home, attn_held)
        input_rows = arrive(input_home)
        own_a, got_a = unit_end(unit_sums[0], input_rows[1])
        ends = [unit_end(t, input_rows[1]) for t in unit_sums[1:]]
        home_order = after(home_order, got_a, *[end[1] for end in ends])
    else:
        input_rows = arrive(input_home)
    input_grad = place_rows(input_rows, home_order)

    small_at = query_cols + head_dim + query_cols
    tiny_grad = attn_end[:, small_at:].astype(WIDE)

    if split:

        def joined(part, end):
            cols = slice(part * first_units, (part + 1) * first_units)
            own = jnp.concatenate([own_a[:, cols], end[0]], axis=1)
            got = jnp.concatenate([got_a[:, cols], end[1]], axis=1)
            first, second = jnp.where(ctx_rank == 0, own, got), jnp.where(ctx_rank == 0, got, own)
            return jnp.concatenate([first, second], axis=1)[:, :units].astype(WIDE)

        down_end, gate_end, up_end = joined(0, ends[0]), joined(1, ends[2]), joined(2, ends[1])
    else:
        down_end, gate_end, up_end = (t[:, :units].astype(WIDE) for t in unit_sums)
    return (
        block_out,
        input_grad,
        attn_end[:, :query_cols].astype(WIDE),
        attn_end[:, query_cols : query_cols + head_dim].astype(WIDE),
        attn_end[:, query_cols + head_dim : small_at].astype(WIDE).T,
        tiny_grad[:, :2].T,
        tiny_grad[:share, 2 : 2 + heads].T,
        tiny_grad[:share, 2 + heads : 3 + heads].T,
        gate_end,
        up_end,
        down_end.T,
    )


def solution(mesh):
    placed = (
        P("fsdp", "ctx", None),
        P("fsdp", "ctx", None),
        P(),
        P(None, "ctx"),
        P(),
        P(("fsdp", "ctx"), "tp"),
        P(("fsdp", "ctx"), None),
        P("tp", ("fsdp", "ctx")),
        P(None, ("fsdp", "ctx")),
        P("tp", None),
        P(),
        P(("fsdp", "ctx"), "tp"),
        P(("fsdp", "ctx"), "tp"),
        P("tp", ("fsdp", "ctx")),
    )
    return jax.shard_map(
        local,
        mesh=mesh,
        in_specs=placed,
        out_specs=(
            P("fsdp", "ctx", None),
            P("fsdp", "ctx", None),
            P(("fsdp", "ctx"), "tp"),
            P(("fsdp", "ctx"), "tp"),
            P("tp", ("fsdp", "ctx")),
            P(None, ("fsdp", "ctx")),
            P("tp", ("fsdp", "ctx")),
            P("tp", ("fsdp", "ctx")),
            P(("fsdp", "ctx"), "tp"),
            P(("fsdp", "ctx"), "tp"),
            P("tp", ("fsdp", "ctx")),
        ),
        check_vma=False,
    )
```

```python
import functools
import math

import jax
import jax.numpy as jnp
from jax import lax
from jax.experimental import pallas as pl
from jax.experimental.pallas import tpu as pltpu
from jax.sharding import PartitionSpec as P

EPS = 1e-06
ROPE_BASE = 10000.0
NEG_FILL = -1e30
LOW = jnp.bfloat16
WIDE = jnp.float32
DEAL_SHIFT = (0, 2, 1, 3)


def from_partner(value, axis, apart):
    pairs = [(source, source ^ apart) for source in range(lax.axis_size(axis))]
    return lax.ppermute(value, axis, pairs)


def product(left_side, right_side, kind=WIDE):
    return jnp.dot(left_side, right_side, preferred_element_type=WIDE).astype(kind)


def contract_rows(left_side, right_side, kind=WIDE):
    return lax.dot_general(
        left_side, right_side, (((0,), (0,)), ((), ())), preferred_element_type=WIDE
    ).astype(kind)


def contract_cols(left_side, right_side, kind=WIDE):
    return lax.dot_general(
        left_side, right_side, (((1,), (1,)), ((), ())), preferred_element_type=WIDE
    ).astype(kind)


def norm_backward(values, scale_inv, gain_row, upstream):
    scaled = gain_row * upstream
    inner_mean = jnp.mean(values * scaled, axis=-1, keepdims=True)
    grad_in = scale_inv * scaled - values * (scale_inv * scale_inv * scale_inv) * inner_mean
    gain_grad = jnp.sum(upstream * values * scale_inv, axis=0, keepdims=True)
    return (grad_in, gain_grad)


def after(value, *earlier):
    return lax.optimization_barrier((value, *earlier))[0]


def collect_far(far_part, cross_part):
    wide = far_part.astype(WIDE) + from_partner(cross_part, "tp", 1).astype(WIDE)
    return wide.astype(LOW)


def units_split():
    return lax.axis_size("ctx") == 2


def all_rows(shard):
    return lax.all_gather(shard, "fsdp", axis=0, tiled=True)


def scatter_ctx(blocks, ctx_rank):
    kept = lax.dynamic_index_in_dim(blocks, ctx_rank, 1, keepdims=False)
    sent = lax.dynamic_index_in_dim(blocks, 1 - ctx_rank, 1, keepdims=False)
    return kept, sent


def scatter_sum(grad, ctx_rank, kind, *earlier):
    fsdp_count, ctx_count = lax.axis_size("fsdp"), lax.axis_size("ctx")
    rows, cols = grad.shape
    blocks = grad.reshape(fsdp_count, ctx_count, rows // (fsdp_count * ctx_count), cols)
    if ctx_count == 2:
        kept, sent = scatter_ctx(blocks, ctx_rank)
        got = from_partner(sent, "ctx", 1)
        held = (after(kept, *earlier).astype(WIDE) + got.astype(WIDE)).astype(kind)
    else:
        swapped = jnp.swapaxes(blocks, 0, 1).reshape(rows, cols)
        held = lax.psum_scatter(swapped, "ctx", scatter_dimension=0, tiled=True)
    held = held.reshape(rows // ctx_count, cols)
    return lax.psum_scatter(held, "fsdp", scatter_dimension=0, tiled=True)


def estimate(flops, moved, transcendentals=0):
    return pl.CostEstimate(flops=flops, bytes_accessed=moved, transcendentals=transcendentals)


def part_spec(rows, cols, part):
    return pl.BlockSpec((rows, cols), lambda *_: (0, part), pipeline_mode=pl.Buffered(1))


def whole_spec(*shape, once=False):
    mode = {"pipeline_mode": pl.Buffered(1)} if once else {}
    return pl.BlockSpec(shape, lambda *_: (0,) * len(shape), **mode)


def rows_kernel(groups, *refs):
    slot = pl.program_id(0)
    weight, (lin, stacked) = refs[sum(groups)], refs[-2:]

    def run(pieces):
        start = 0
        for piece in pieces:
            stacked[start : start + piece.shape[0]] = piece[...]
            start += piece.shape[0]
        lin[...] = jnp.dot(stacked[...], weight[...], preferred_element_type=WIDE).astype(LOW)

    first = 0
    for r, pieces in enumerate(groups):
        pl.when(slot == r)(functools.partial(run, refs[first : first + pieces]))
        first += pieces


def stack_rows(slots, weight, part, parts, into=None, first=0, total=None):
    groups = [len(s) for s in slots]
    rows = [piece for s in slots for piece in s]
    width, length = rows[0].shape[1], sum(piece.shape[0] for piece in slots[0])
    count, cols = len(slots), weight.shape[1] // parts
    total = total or count
    into = into or ()
    return pl.pallas_call(
        functools.partial(rows_kernel, groups),
        grid=(count,),
        in_specs=[whole_spec(*piece.shape, once=True) for piece in rows]
        + [part_spec(width, cols, part)]
        + [pl.BlockSpec(memory_space=pl.ANY)] * len(into),
        out_specs=[
            pl.BlockSpec((length, cols), lambda s: (first + s, 0)),
            pl.BlockSpec((length, width), lambda s: (first + s, 0)),
        ],
        out_shape=[
            jax.ShapeDtypeStruct((total * length, cols), LOW),
            jax.ShapeDtypeStruct((total * length, width), LOW),
        ],
        input_output_aliases={len(rows) + 1 + i: i for i in range(len(into))},
        compiler_params=pltpu.CompilerParams(vmem_limit_bytes=60 << 20),
        cost_estimate=estimate(
            2 * count * length * width * cols, 2 * (count * length * (2 * width + cols) + width * cols)
        ),
    )(*rows, weight, *into)


def units_kernel(h, up, gate, grad, hid, grad_gate, grad_up):
    up_lin = jnp.dot(h[...], up[...], preferred_element_type=WIDE)
    gate_lin = gate[...].astype(WIDE)
    grad_hidden = grad[...].astype(WIDE)
    sigmoid = 1.0 / (1.0 + jnp.exp(-gate_lin))
    silu = gate_lin * sigmoid
    hid[...] = (silu * up_lin).astype(LOW)
    grad_gate[...] = (grad_hidden * up_lin * sigmoid * (1.0 + gate_lin * (1.0 - sigmoid))).astype(LOW)
    grad_up[...] = (grad_hidden * silu).astype(LOW)


def hidden_units(h, up, part, parts, gate_lin, grad_hidden):
    tokens, width = h.shape
    cols = up.shape[1] // parts
    step = math.gcd(512, tokens)
    by_row = lambda n: pl.BlockSpec((step, n), lambda i: (i, 0))
    return pl.pallas_call(
        units_kernel,
        grid=(tokens // step,),
        in_specs=[by_row(width), part_spec(width, cols, part), by_row(cols), by_row(cols)],
        out_specs=[by_row(cols)] * 3,
        out_shape=[jax.ShapeDtypeStruct((tokens, cols), LOW)] * 3,
        compiler_params=pltpu.CompilerParams(vmem_limit_bytes=60 << 20),
        cost_estimate=estimate(
            2 * tokens * width * cols, 2 * (tokens * width + width * cols + 5 * tokens * cols)
        ),
    )(h, up, gate_lin, grad_hidden)


def back_kernel(terms, *refs):
    lefts, weights, outs = refs[:terms], refs[terms : 2 * terms], refs[2 * terms :]
    total = None
    for left, weight in zip(lefts, weights):
        term = dot_cols(left[...], weight[...])
        total = term if total is None else total + term
    for i, out in enumerate(outs):

        @pl.when(pl.program_id(0) == i)
        def _():
            out[...] = total.astype(LOW)


def back_rows(lefts, weights, first_slot, slots, length):
    width = weights[0][0].shape[0]
    depth = sum(left.shape[1] for left in lefts)
    return pl.pallas_call(
        functools.partial(back_kernel, len(lefts)),
        grid=(slots,),
        in_specs=[
            pl.BlockSpec((length, left.shape[1]), lambda s: (first_slot + s, 0)) for left in lefts
        ]
        + [part_spec(width, w.shape[1] // parts, part) for w, part, parts in weights],
        out_specs=[whole_spec(length, width)] * slots,
        out_shape=[jax.ShapeDtypeStruct((length, width), LOW)] * slots,
        compiler_params=pltpu.CompilerParams(vmem_limit_bytes=60 << 20),
        cost_estimate=estimate(
            2 * slots * length * width * depth,
            2 * (slots * length * (width + depth) + width * depth),
        ),
    )(*lefts, *[w for w, _, _ in weights])


def chosen_kernel(near, count, info, cotangent, *refs):
    slot = pl.program_id(0)
    others, (weight, lin, stacked) = refs[:count], refs[count:]

    @pl.when(slot < near)
    def _():
        stacked[...] = cotangent[0]

    for k, other in enumerate(others):

        @pl.when((slot >= near) & (info[slot] == k))
        def _():
            stacked[...] = other[...]

    lin[...] = jnp.dot(stacked[...], weight[...], preferred_element_type=WIDE).astype(LOW)


def chosen_rows(info, cotangent, others, weight, part, parts):
    near, length, width = cotangent.shape
    slots, cols = near + len(others), weight.shape[1] // parts
    held = lambda rows, n, at: pl.BlockSpec(
        (rows, n), lambda s, info: (0, at), pipeline_mode=pl.Buffered(1)
    )
    return pl.pallas_call(
        functools.partial(chosen_kernel, near, len(others)),
        grid_spec=pltpu.PrefetchScalarGridSpec(
            num_scalar_prefetch=1,
            grid=(slots,),
            in_specs=[
                pl.BlockSpec((1, length, width), lambda s, info: (info[jnp.minimum(s, near - 1)], 0, 0))
            ]
            + [held(length, width, 0)] * len(others)
            + [held(width, cols, part)],
            out_specs=[
                pl.BlockSpec((length, cols), lambda s, info: (s, 0)),
                pl.BlockSpec((length, width), lambda s, info: (s, 0)),
            ],
        ),
        out_shape=[
            jax.ShapeDtypeStruct((slots * length, cols), LOW),
            jax.ShapeDtypeStruct((slots * length, width), LOW),
        ],
        compiler_params=pltpu.CompilerParams(vmem_limit_bytes=60 << 20),
        cost_estimate=estimate(
            2 * slots * length * width * cols, 2 * (slots * length * (2 * width + cols) + width * cols)
        ),
    )(info, cotangent, *others, weight)


def full_units_kernel(h, g, down, gate, up, hid, grad_gate, grad_up):
    gate_lin = jnp.dot(h[...], gate[...], preferred_element_type=WIDE)
    up_lin = jnp.dot(h[...], up[...], preferred_element_type=WIDE)
    grad_hidden = jnp.dot(g[...], down[...], preferred_element_type=WIDE)
    sigmoid = 1.0 / (1.0 + jnp.exp(-gate_lin))
    silu = gate_lin * sigmoid
    hid[...] = (silu * up_lin).astype(LOW)
    grad_gate[...] = (grad_hidden * up_lin * sigmoid * (1.0 + gate_lin * (1.0 - sigmoid))).astype(LOW)
    grad_up[...] = (grad_hidden * silu).astype(LOW)


def full_units(h, g, weight):
    tokens, width = h.shape
    cols = weight.shape[1] // 3
    step = math.gcd(512, tokens)
    by_row = lambda n: pl.BlockSpec((step, n), lambda i: (i, 0))
    return pl.pallas_call(
        full_units_kernel,
        grid=(tokens // step,),
        in_specs=[by_row(width)] * 2 + [part_spec(width, cols, i) for i in range(3)],
        out_specs=[by_row(cols)] * 3,
        out_shape=[jax.ShapeDtypeStruct((tokens, cols), LOW)] * 3,
        compiler_params=pltpu.CompilerParams(vmem_limit_bytes=60 << 20),
        cost_estimate=estimate(
            6 * tokens * width * cols, 2 * (2 * tokens * width + 3 * width * cols + 3 * tokens * cols)
        ),
    )(h, g, weight, weight, weight)


def first_grads_kernel(g, h, hid, gate, up, out):
    part = pl.program_id(0)
    for i, (left, right) in enumerate(((g, hid), (h, gate), (h, up))):

        @pl.when(part == i)
        def _():
            out[...] = dot_rows(left[...], right[...]).astype(LOW)


def first_grads(grad_rows, rows, hid, grad_gate, grad_up):
    tokens, width = rows.shape
    cols, tile = hid.shape[1], 256
    tiles = width // tile
    return pl.pallas_call(
        first_grads_kernel,
        grid=(3, tiles),
        in_specs=[
            pl.BlockSpec((tokens, tile), lambda p, i: (0, jnp.where(p == 0, i, tiles - 1))),
            pl.BlockSpec((tokens, tile), lambda p, i: (0, jnp.where(p == 0, 0, i))),
        ]
        + [whole_spec(tokens, cols, once=True)] * 3,
        out_specs=pl.BlockSpec((tile, cols), lambda p, i: (i, p)),
        out_shape=jax.ShapeDtypeStruct((width, 3 * cols), LOW),
        compiler_params=pltpu.CompilerParams(vmem_limit_bytes=60 << 20),
        cost_estimate=estimate(6 * tokens * width * cols, 6 * tokens * cols + 6 * width * cols),
    )(grad_rows, rows, hid, grad_gate, grad_up)


MESH_ID = pl.DeviceIdType.MESH


def meet(partners):
    barrier = pltpu.get_barrier_semaphore()
    for partner in partners:
        pl.semaphore_signal(barrier, inc=1, device_id=partner, device_id_type=MESH_ID)
    pl.semaphore_wait(barrier, len(partners))


def partners_of():
    tensor_rank, ctx_rank = lax.axis_index("tp"), lax.axis_index("ctx")
    return {"tp": tensor_rank ^ 1}, {"tp": tensor_rank ^ 2}, {"ctx": ctx_rank ^ 1}


def collect_kernel(
    slots, tiles, gate_a, up_a, gate_b, up_b, w_gate_a, w_up_a, w_gate_b, w_up_b, left, right, hid, up, total,
    down_out, up_out, parts, sent, core_in, across_in, last_in, held, send, recv, load
):
    step = pl.program_id(0)
    steps = pl.num_programs(0)
    core, far, side = partners_of()
    half = total.shape[0] // 2
    remote = remote_copy(send, recv)
    cores = [remote(sent.at[k % 2], core_in.at[k], k, core) for k in range(4)]
    across = [
        remote(parts.at[3, pl.ds(0, half)], across_in.at[0], 4, far),
        remote(parts.at[3, pl.ds(half, half)], across_in.at[1], 5, side),
    ]
    lasts = [
        remote(parts.at[1], last_in.at[0], 6, far),
        remote(parts.at[2, pl.ds(half, half)], last_in.at[1, pl.ds(half, half)], 7, side),
        remote(parts.at[2, pl.ds(0, half)], last_in.at[1, pl.ds(0, half)], 8, side),
    ]
    loading = [
        pltpu.make_async_copy(source, held.at[i], load.at[i]) for i, source in enumerate((hid, up))
    ]

    @pl.when(step == 0)
    def _():
        for copy in loading:
            copy.start()
        meet((core, far, side))

    for k in (2, 3):
        pl.when(step == 2 * k)(cores[k - 2].wait_send)

    @pl.when(step < slots)
    def _():
        part = (
            dot_cols(gate_a[...], w_gate_a[...])
            + dot_cols(up_a[...], w_up_a[...])
            + dot_cols(gate_b[...], w_gate_b[...])
            + dot_cols(up_b[...], w_up_b[...])
        )

        @pl.when(step == slots - 1)
        def _():
            total[...] = part

        for k in range(4):

            @pl.when(step == 2 * k)
            def _():
                sent[k % 2] = part.astype(LOW)
                cores[k].start()

            if k < 3:

                @pl.when(step == 2 * k + 1)
                def _():
                    cores[k].wait_recv()
                    parts[3 - k] = (part + core_in[k].astype(WIDE)).astype(LOW)

    def add(slot, rows, value):
        parts[slot, rows] = (parts[slot, rows].astype(WIDE) + value.astype(WIDE)).astype(LOW)

    low, high = pl.ds(0, half), pl.ds(half, half)

    @pl.when(step == 1)
    def _():
        for copy in across:
            copy.start()

    pl.when(step == 3)(lasts[1].start)

    @pl.when(step == 5)
    def _():
        across[1].wait_recv()
        add(1, high, across_in[1])
        lasts[0].start()
        across[0].wait_recv()
        add(2, low, across_in[0])
        lasts[2].start()

    @pl.when((step >= slots) & (step < slots + tiles))
    def _():
        pl.when(step == slots)(loading[0].wait)
        down_out[...] = dot_rows(left[...], held[0]).astype(LOW)

    @pl.when(step >= slots + tiles)
    def _():
        pl.when(step == slots + tiles)(loading[1].wait)
        up_out[...] = dot_rows(right[...], held[1]).astype(LOW)

    @pl.when(step == steps - 1)
    def _():
        cores[3].wait_recv()
        for copy in lasts:
            copy.wait_recv()
        total[...] += (
            core_in[3].astype(WIDE) + last_in[0].astype(WIDE) + last_in[1].astype(WIDE)
        )
        for copy in (*cores[2:], *across, *lasts):
            copy.wait_send()


def collect_back(first, second, weight_a, weight_b, grad_rows, rows, hid, length):
    tokens, cols_a = first[0].shape
    cols = second[0].shape[1]
    width = weight_a.shape[0]
    slots, tile = tokens // length, 256
    tiles = width // tile
    row = lambda n: pl.BlockSpec((length, n), lambda i: (jnp.maximum(slots - 1 - i, 0), 0))
    column = lambda i, start: jnp.clip(i - start, 0, tiles - 1)
    down_at, up_at = (lambda i: column(i, slots)), (lambda i: column(i, slots + tiles))
    return pl.pallas_call(
        functools.partial(collect_kernel, slots, tiles),
        grid=(slots + 2 * tiles,),
        in_specs=[row(cols_a), row(cols_a), row(cols), row(cols)]
        + [part_spec(width, cols_a, 1), part_spec(width, cols_a, 2)]
        + [part_spec(width, cols, 1), part_spec(width, cols, 2)]
        + [
            pl.BlockSpec((tokens, tile), lambda i: (0, down_at(i))),
            pl.BlockSpec((tokens, tile), lambda i: (0, up_at(i))),
            ANYWHERE,
            ANYWHERE,
        ],
        out_specs=[
            whole_spec(length, width, once=True),
            pl.BlockSpec((tile, cols), lambda i: (down_at(i), 0)),
            pl.BlockSpec((tile, cols), lambda i: (up_at(i), 0)),
        ],
        out_shape=[
            jax.ShapeDtypeStruct((length, width), WIDE),
            jax.ShapeDtypeStruct((width, cols), LOW),
            jax.ShapeDtypeStruct((width, cols), LOW),
        ],
        scratch_shapes=[
            pltpu.VMEM((4, length, width), LOW),
            pltpu.VMEM((2, length, width), LOW),
            pltpu.VMEM((4, length, width), LOW),
            pltpu.VMEM((2, length // 2, width), LOW),
            pltpu.VMEM((2, length, width), LOW),
            pltpu.VMEM((2, tokens, cols), LOW),
            pltpu.SemaphoreType.DMA((9,)),
            pltpu.SemaphoreType.DMA((9,)),
            pltpu.SemaphoreType.DMA((2,)),
        ],
        compiler_params=pltpu.CompilerParams(
            vmem_limit_bytes=63 << 20, collective_id=1, has_side_effects=True
        ),
        cost_estimate=estimate(6 * tokens * width * cols, 10 * tokens * cols),
    )(*first, *second, weight_a, weight_a, weight_b, weight_b, grad_rows, rows, hid, second[1])


def remote_copy(send, recv):
    def make(source, target, index, partner):
        return pltpu.make_async_remote_copy(
            source, target, send.at[index], recv.at[index], device_id=partner, device_id_type=MESH_ID
        )

    return make


def branch_kernel(
    slots, tiles, total, middle, own_grad, gain, hid_a, hid_b, w_a, w_b, turned, gate, grad_middle, gain_grad,
    gate_out, branch, mlp_own, mlp_far, mlp_side, own, parts, core_in, across_in, held, send, recv, load
):
    step = pl.program_id(0)
    core, far, side = partners_of()
    remote = remote_copy(send, recv)
    to_far = remote(own, branch.at[2], 0, far)
    to_near = remote(own, branch.at[1], 1, core)
    to_cross = remote(branch.at[2], branch.at[3], 2, core)
    keep = pltpu.make_async_copy(own, branch.at[0], load.at[0])
    loading = pltpu.make_async_copy(gate, held, load.at[1])
    cores = [remote(parts.at[7 - 2 * k], core_in.at[k], 3 + k, core) for k in range(4)]
    across = remote(parts.at[6], across_in, 7, side)
    stores = [
        pltpu.make_async_copy(parts.at[4], mlp_side, load.at[2]),
        pltpu.make_async_copy(parts.at[2], mlp_far, load.at[3]),
        pltpu.make_async_copy(parts.at[0], mlp_own, load.at[4]),
    ]

    @pl.when(step == 0)
    def _():
        loading.start()
        meet((core, far, side))
        values, upstream = middle[...], total[...]
        inverse = lax.rsqrt(jnp.mean(values * values, axis=-1, keepdims=True) + EPS)
        grad_in, gain_grad[...] = norm_backward(values, inverse, gain[...], upstream)
        grad_in = own_grad[...].astype(WIDE) + grad_in
        grad_middle[...] = grad_in
        own[...] = grad_in.astype(LOW)
        for copy in (to_far, to_near, keep):
            copy.start()

    @pl.when(step < slots)
    def _():
        part = dot_cols(hid_a[...], w_a[...]) + dot_cols(hid_b[...], w_b[...])
        parts[slots - 1 - step] = part.astype(LOW)

    for k in range(4):
        pl.when(step == 2 * k)(cores[k].start)

        def finish(k=k):
            slot = 6 - 2 * k
            cores[k].wait_recv()
            parts[slot] = (parts[slot].astype(WIDE) + core_in[k].astype(WIDE)).astype(LOW)
            if k == 0:
                across.start()
            if k == 1:
                stores[0].start()
            if k == 3:
                stores[2].start()

        pl.when(step == 2 * k + 1)(finish)

    @pl.when(step >= slots)
    def _():
        pl.when(step == slots)(loading.wait)
        gate_out[...] = dot_rows(turned[...], held[...]).astype(LOW)

    @pl.when(step == slots + tiles - 2)
    def _():
        to_far.wait_recv()
        to_cross.start()

    @pl.when(step == slots + tiles - 1)
    def _():
        to_near.wait_recv()
        to_cross.wait_recv()
        across.wait_recv()
        parts[2] = (parts[2].astype(WIDE) + across_in[...].astype(WIDE)).astype(LOW)
        stores[1].start()
        keep.wait()
        for copy in stores:
            copy.wait()
        for copy in (to_far, to_near, to_cross, *cores, across):
            copy.wait_send()


ANYWHERE = pl.BlockSpec(memory_space=pl.ANY)


def spread_branch(total, middle, own_grad, gain, hid_a, hid_b, weight_a, weight_b, rows, grad_gate):
    length, width = total.shape
    tokens, cols = grad_gate.shape
    slots, tile = tokens // length, 256
    tiles = width // tile
    once = whole_spec(length, width, once=True)
    column = lambda i: jnp.clip(i - slots, 0, tiles - 1)
    part = jax.ShapeDtypeStruct((length, width), LOW)
    return pl.pallas_call(
        functools.partial(branch_kernel, slots, tiles),
        grid=(slots + tiles,),
        in_specs=[
            once,
            once,
            once,
            whole_spec(1, width),
            pl.BlockSpec((length, hid_a.shape[1]), lambda i: (jnp.maximum(slots - 1 - i, 0), 0)),
            pl.BlockSpec((length, cols), lambda i: (jnp.maximum(slots - 1 - i, 0), 0)),
            part_spec(width, hid_a.shape[1], 0),
            part_spec(width, cols, 0),
            pl.BlockSpec((tokens, tile), lambda i: (0, column(i))),
            ANYWHERE,
        ],
        out_specs=[
            whole_spec(length, width, once=True),
            whole_spec(1, width),
            pl.BlockSpec((tile, cols), lambda i: (column(i), 0)),
        ]
        + [ANYWHERE] * 4,
        out_shape=[
            jax.ShapeDtypeStruct((length, width), WIDE),
            jax.ShapeDtypeStruct((1, width), WIDE),
            jax.ShapeDtypeStruct((width, cols), LOW),
            jax.ShapeDtypeStruct((4, length, width), LOW),
            part,
            part,
            part,
        ],
        scratch_shapes=[
            pltpu.VMEM((length, width), LOW),
            pltpu.VMEM((slots, length, width), LOW),
            pltpu.VMEM((4, length, width), LOW),
            pltpu.VMEM((length, width), LOW),
            pltpu.VMEM((tokens, cols), LOW),
            pltpu.SemaphoreType.DMA((8,)),
            pltpu.SemaphoreType.DMA((8,)),
            pltpu.SemaphoreType.DMA((5,)),
        ],
        compiler_params=pltpu.CompilerParams(
            vmem_limit_bytes=63 << 20, collective_id=2, has_side_effects=True
        ),
        cost_estimate=estimate(4 * tokens * width * cols, 10 * tokens * cols),
    )(total, middle, own_grad, gain, hid_a, hid_b, weight_a, weight_b, rows, grad_gate)


def line_kernel(
    slots, tiles, count, line, weight, own_in, grad_middle, gain, gain_two, rows_one, line_all, block, *refs
):
    sums, (share, gain_grad, attn_out, bias_out, home) = refs[:count], refs[count : count + 5]
    gots = refs[count + 5 : 2 * count + 5]
    parts, core_in, far_in, total, gains, gains_in, send, recv, load = refs[2 * count + 5 :]
    step = pl.program_id(0)
    core, far, side = partners_of()
    tensor_rank, group = lax.axis_index("tp"), lax.axis_index("fsdp")
    shift = (tensor_rank % 2) * 2 + tensor_rank // 2
    target = {"fsdp": (group + slots - shift) % slots}
    source = {"fsdp": (group + shift) % slots}
    stays = shift == 0
    remote = remote_copy(send, recv)
    cores = [remote(parts.at[3 - 2 * k], core_in.at[k], k, core) for k in range(2)]
    to_far = remote(parts.at[2], far_in, 2, far)
    leave = remote(block, home, 3, target)
    keep = pltpu.make_async_copy(block, home, load)
    cross = {"tp": tensor_rank ^ 3}
    gain_copies = [
        remote(gains, gains_in.at[i], 4 + i, partner) for i, partner in enumerate((core, far, cross))
    ]
    rows = gots[0].shape[0]
    there = pl.multiple_of((1 - lax.axis_index("ctx")) * rows, rows)
    sides = [
        remote(held.at[pl.ds(there, rows)], got, 7 + i, side) for i, (held, got) in enumerate(zip(sums, gots))
    ]

    @pl.when(step == 0)
    def _():
        barrier = pltpu.get_barrier_semaphore()
        for partner in (core, far, cross, side):
            pl.semaphore_signal(barrier, inc=1, device_id=partner, device_id_type=MESH_ID)

        @pl.when(stays)
        def _():
            pl.semaphore_wait(barrier, 4)
            keep.start()

        @pl.when(jnp.logical_not(stays))
        def _():
            for partner in (target, source):
                pl.semaphore_signal(barrier, inc=1, device_id=partner, device_id_type=MESH_ID)
            pl.semaphore_wait(barrier, 6)
            leave.start()

        for copy in sides:
            copy.start()

    @pl.when(step < slots)
    def _():
        part = dot_cols(line[...], weight[...])
        parts[slots - 1 - step] = part.astype(LOW)

        @pl.when(step == slots - 1)
        def _():
            total[...] = part

    for k in range(2):
        pl.when(step == 2 * k)(cores[k].start)

    @pl.when(step == 1)
    def _():
        cores[0].wait_recv()
        parts[2] = (parts[2].astype(WIDE) + core_in[0].astype(WIDE)).astype(LOW)
        to_far.start()

    @pl.when(step == slots - 1)
    def _():
        bias_out[...] = jnp.sum(line_all[...].astype(WIDE), axis=0, keepdims=True)

    @pl.when(step >= slots)
    def _():
        attn_out[...] = dot_rows(rows_one[...], line_all[...]).astype(LOW)

    @pl.when(step == slots + tiles - 1)
    def _():
        cores[1].wait_recv()
        to_far.wait_recv()
        upstream = total[...] + core_in[1].astype(WIDE) + far_in[...].astype(WIDE)
        values = own_in[...].astype(WIDE)
        inverse = lax.rsqrt(jnp.mean(values * values, axis=-1, keepdims=True) + EPS)
        grad_in, gain_one = norm_backward(values, inverse, gain[...], upstream)
        gains[0:1] = gain_one
        gains[1:2] = gain_two[...]
        for copy in gain_copies:
            copy.start()
        share[...] = (grad_middle[...] + grad_in).astype(LOW)
        for copy in gain_copies:
            copy.wait_recv()
        gain_grad[...] = (gains[...] + gains_in[0]) + (gains_in[1] + gains_in[2])
        for copy in sides:
            copy.wait_recv()
        for copy in (*cores, to_far, *gain_copies, *sides):
            copy.wait_send()
        pl.when(stays)(keep.wait)

        @pl.when(jnp.logical_not(stays))
        def _():
            leave.wait_recv()
            leave.wait_send()


def finish_rows(line, weight, own_in, grad_middle, gain, gain_two, rows_one, block, sums):
    length, width = own_in.shape
    near_tokens, line_cols = line.shape
    slots, tile = near_tokens // length, 256
    tiles = width // tile
    once = whole_spec(length, width, once=True)
    column = lambda i: jnp.clip(i - slots, 0, tiles - 1)
    by_column = lambda n: pl.BlockSpec((n, tile), lambda i: (0, column(i)))
    attn_cols = line_cols
    return pl.pallas_call(
        functools.partial(line_kernel, slots, tiles, len(sums)),
        grid=(slots + tiles,),
        in_specs=[
            pl.BlockSpec((length, line_cols), lambda i: (jnp.maximum(slots - 1 - i, 0), 0)),
            whole_spec(width, line_cols, once=True),
            once,
            once,
            whole_spec(1, width),
            whole_spec(1, width),
            by_column(near_tokens),
            whole_spec(near_tokens, line_cols, once=True),
            ANYWHERE,
        ]
        + [ANYWHERE] * len(sums),
        out_specs=[
            whole_spec(length, width),
            whole_spec(2, width),
            pl.BlockSpec((tile, attn_cols), lambda i: (column(i), 0)),
            whole_spec(1, line_cols),
            ANYWHERE,
        ]
        + [ANYWHERE] * len(sums),
        out_shape=[
            jax.ShapeDtypeStruct((length, width), LOW),
            jax.ShapeDtypeStruct((2, width), WIDE),
            jax.ShapeDtypeStruct((width, attn_cols), LOW),
            jax.ShapeDtypeStruct((1, line_cols), WIDE),
            jax.ShapeDtypeStruct((length, width), LOW),
        ]
        + [jax.ShapeDtypeStruct((t.shape[0] // 2, t.shape[1]), LOW) for t in sums],
        scratch_shapes=[
            pltpu.VMEM((slots, length, width), LOW),
            pltpu.VMEM((2, length, width), LOW),
            pltpu.VMEM((length, width), LOW),
            pltpu.VMEM((length, width), WIDE),
            pltpu.VMEM((2, width), WIDE),
            pltpu.VMEM((3, 2, width), WIDE),
            pltpu.SemaphoreType.DMA((7 + len(sums),)),
            pltpu.SemaphoreType.DMA((7 + len(sums),)),
            pltpu.SemaphoreType.DMA,
        ],
        compiler_params=pltpu.CompilerParams(
            vmem_limit_bytes=63 << 20, collective_id=3, has_side_effects=True
        ),
        cost_estimate=estimate(2 * near_tokens * width * attn_cols, 10 * near_tokens * width),
    )(line, weight, own_in, grad_middle, gain, gain_two, rows_one, line, block, *sums)


def place_kernel(count, info, *refs):
    out = refs[count]
    for r in range(count):

        @pl.when(pl.program_id(0) == r)
        def _():
            out[0] = refs[r][...]


def place_rows(rows, order):
    length, width = rows[0].shape
    count = len(rows)
    held = pl.BlockSpec((length, width), lambda s, info: (0, 0), pipeline_mode=pl.Buffered(1))
    return pl.pallas_call(
        functools.partial(place_kernel, count),
        grid_spec=pltpu.PrefetchScalarGridSpec(
            num_scalar_prefetch=1,
            grid=(count,),
            in_specs=[held] * count,
            out_specs=pl.BlockSpec((1, length, width), lambda s, info: (info[s], 0, 0)),
        ),
        out_shape=jax.ShapeDtypeStruct((count, length, width), LOW),
        compiler_params=pltpu.CompilerParams(vmem_limit_bytes=32 << 20),
        cost_estimate=estimate(0, 4 * count * length * width),
    )(order, *rows)


def turn(values, cosine, sine_signed):
    return values * cosine + pltpu.roll(values, values.shape[-1] // 2, 1) * sine_signed


def turn_back(values, cosine, sine_signed):
    return values * cosine - pltpu.roll(values, values.shape[-1] // 2, 1) * sine_signed


def project_kernel(
    heads, head_dim, x0, x1, x2, x3, gains, weight, bias, cosine, sine, h_out, q_out, k_out, v_out, gain
):
    slot = pl.program_id(0)

    @pl.when(slot == 0)
    def _():
        gain[...] = gains[...].astype(WIDE).T[:8]


    def run(x_ref):
        x = x_ref[...].astype(WIDE)
        scale_inv = lax.rsqrt(jnp.mean(x * x, axis=-1, keepdims=True) + EPS)
        normed = (x * scale_inv * gain[0:1]).astype(LOW)
        h_out[0] = normed
        lin = jnp.dot(normed, weight[...], preferred_element_type=WIDE) + bias[...]
        cos, sin = cosine[0], sine[0]
        for h in range(heads + 1):
            part = turn(lin[:, h * head_dim : (h + 1) * head_dim], cos, sin).astype(LOW)
            if h < heads:
                q_out[0, :, h * head_dim : (h + 1) * head_dim] = part
            else:
                k_out[0] = part
        v_out[0] = lin[:, (heads + 1) * head_dim :].astype(LOW)

    for r, x_ref in enumerate((x0, x1, x2, x3)):
        pl.when(slot == r)(functools.partial(run, x_ref))


def project(rows, held, bias, cosine, sine, heads, head_dim):
    length, width = rows[0].shape
    count = len(rows)
    cols = (heads + 2) * head_dim
    whole = whole_spec
    by_slot = lambda *shape: pl.BlockSpec((1, *shape), lambda s: (s,) + (0,) * len(shape))
    return pl.pallas_call(
        functools.partial(project_kernel, heads, head_dim),
        grid=(count,),
        in_specs=[whole(length, width)] * count
        + [part_spec(width, 128, cols // 128), part_spec(width, cols, 0), whole(1, cols)]
        + [by_slot(length, head_dim)] * 2,
        out_specs=[
            by_slot(length, width),
            by_slot(length, heads * head_dim),
            by_slot(length, head_dim),
            by_slot(length, head_dim),
        ],
        out_shape=[
            jax.ShapeDtypeStruct((count, length, width), LOW),
            jax.ShapeDtypeStruct((count, length, heads * head_dim), LOW),
            jax.ShapeDtypeStruct((count, length, head_dim), LOW),
            jax.ShapeDtypeStruct((count, length, head_dim), LOW),
        ],
        scratch_shapes=[pltpu.VMEM((8, width), WIDE)],
        compiler_params=pltpu.CompilerParams(vmem_limit_bytes=56 << 20),
        cost_estimate=pl.CostEstimate(
            flops=2 * count * length * width * cols,
            bytes_accessed=count * length * (2 * width + cols) * 2 + width * cols * 2,
            transcendentals=0,
        ),
    )(*rows, held, held, bias, cosine, sine)


def row_blocks(length):
    return [(i, min(256, length)) for i in range(0, length, min(256, length))]


def key_biases(length, offset, start, rows, past, keys):
    past_pos = lax.broadcasted_iota(jnp.int32, (1, past), 1)
    past_bias = jnp.where((past_pos < offset) & (past_pos < length), 0.0, NEG_FILL)
    query_pos = offset + start + lax.broadcasted_iota(jnp.int32, (rows, keys), 0)
    own_pos = offset + lax.broadcasted_iota(jnp.int32, (rows, keys), 1)
    own_bias = jnp.where((own_pos <= query_pos) & (own_pos < length), 0.0, NEG_FILL)
    return past_bias, own_bias


def dot_cols(left, right):
    return lax.dot_general(left, right, (((1,), (1,)), ((), ())), preferred_element_type=WIDE)


def dot_rows(left, right):
    return lax.dot_general(left, right, (((0,), (0,)), ((), ())), preferred_element_type=WIDE)


def attend_rows(
    heads, head_dim, scale, length, offset, q, k_past, v_past, k_own, v_own, weight, out, lse, put
):
    past = k_past.shape[1]
    for start, rows in row_blocks(q.shape[1]):
        keys = start + rows
        past_bias, own_bias = key_biases(length, offset, start, rows, past, keys)
        here = slice(start, start + rows)
        for h in range(heads):
            cols = slice(h * head_dim, (h + 1) * head_dim)
            query = q[0, here, cols]
            s_past = dot_cols(query, k_past[0]) * scale + past_bias
            s_own = dot_cols(query, k_own[0, :keys]) * scale + own_bias
            top = jnp.maximum(
                jnp.max(s_past, axis=1, keepdims=True), jnp.max(s_own, axis=1, keepdims=True)
            )
            e_past, e_own = jnp.exp(s_past - top), jnp.exp(s_own - top)
            total = jnp.sum(e_past, axis=1, keepdims=True) + jnp.sum(e_own, axis=1, keepdims=True)
            inverse = 1.0 / total
            mixed = jnp.dot(
                (e_past * inverse).astype(LOW), v_past[0], preferred_element_type=WIDE
            ) + jnp.dot((e_own * inverse).astype(LOW), v_own[0, :keys], preferred_element_type=WIDE)
            out[0, here, cols] = mixed.astype(LOW)
            lse[0, here, h : h + 1] = top + jnp.log(total)
        rows_out = dot_cols(out[0, here], weight[...]).astype(LOW)
        put(here, rows_out)


def attend_kernel(
    heads, head_dim, scale, first, total_slots, info, q, k_past, v_past, k_own, v_own, weight, out, lse, *parts
):
    length, offset = info[first + pl.program_id(0)], info[total_slots]

    def put(here, value):
        for i, part in enumerate(parts):

            @pl.when(pl.program_id(0) == i)
            def _():
                part[here] = value

    attend_rows(heads, head_dim, scale, length, offset, q, k_past, v_past, k_own, v_own, weight, out, lse, put)


def attend_forward(info, q, k_past, v_past, k_own, v_own, weight, heads, head_dim, scale, first, count):
    _, length, width = q.shape
    past = k_past.shape[1]
    by_slot = lambda *shape: pl.BlockSpec((1, *shape), lambda s, info: (first + s,) + (0,) * len(shape))
    out_slot = lambda *shape: pl.BlockSpec((1, *shape), lambda s, info: (s,) + (0,) * len(shape))
    keys = count * length * (past + length) * heads
    return pl.pallas_call(
        functools.partial(attend_kernel, heads, head_dim, scale, first, q.shape[0]),
        grid_spec=pltpu.PrefetchScalarGridSpec(
            num_scalar_prefetch=1,
            grid=(count,),
            in_specs=[
                by_slot(length, width),
                by_slot(past, head_dim),
                by_slot(past, head_dim),
                by_slot(length, head_dim),
                by_slot(length, head_dim),
                whole_spec(*weight.shape, once=True),
            ],
            out_specs=[out_slot(length, width), out_slot(length, 128)]
            + [whole_spec(length, weight.shape[0])] * count,
        ),
        out_shape=[
            jax.ShapeDtypeStruct((count, length, width), LOW),
            jax.ShapeDtypeStruct((count, length, 128), WIDE),
        ]
        + [jax.ShapeDtypeStruct((length, weight.shape[0]), LOW)] * count,
        compiler_params=pltpu.CompilerParams(vmem_limit_bytes=56 << 20),
        cost_estimate=estimate(4 * keys * head_dim, 4 * count * length * width, keys),
    )(info, q, k_past, v_past, k_own, v_own, weight)


def attend_back_rows(
    heads, head_dim, scale, length, offset, q, k_past, v_past, k_own, v_own, grad, lse, cosine, sine, put,
    dk_past, dk_own, dv_past, dv_own
):
    past = k_past.shape[1]
    for start, rows in row_blocks(q.shape[1]):
        keys = start + rows
        past_bias, own_bias = key_biases(length, offset, start, rows, past, keys)
        here = slice(start, start + rows)
        cos, sin = cosine[0, here], sine[0, here]
        for h in range(heads):
            cols = slice(h * head_dim, (h + 1) * head_dim)
            query, upstream = q[0, here, cols], grad[0, here, cols]
            log_total = lse[0, here, h : h + 1]
            p_past = jnp.exp(dot_cols(query, k_past[0]) * scale + past_bias - log_total)
            p_own = jnp.exp(dot_cols(query, k_own[0, :keys]) * scale + own_bias - log_total)
            g_past = dot_cols(upstream, v_past[0])
            g_own = dot_cols(upstream, v_own[0, :keys])
            row_dot = jnp.sum(p_past * g_past, axis=1, keepdims=True) + jnp.sum(
                p_own * g_own, axis=1, keepdims=True
            )
            s_past = (p_past * (g_past - row_dot)).astype(LOW)
            s_own = (p_own * (g_own - row_dot)).astype(LOW)
            dq = (
                jnp.dot(s_past, k_past[0], preferred_element_type=WIDE)
                + jnp.dot(s_own, k_own[0, :keys], preferred_element_type=WIDE)
            ) * scale
            put(here, cols, turn_back(dq, cos, sin).astype(LOW))
            dk_past[...] += dot_rows(s_past, query)
            dk_own[:keys] += dot_rows(s_own, query)
            dv_past[...] += dot_rows(p_past.astype(LOW), upstream)
            dv_own[:keys] += dot_rows(p_own.astype(LOW), upstream)


def attend_back_kernel(
    heads,
    head_dim,
    scale,
    info,
    q,
    k_past,
    v_past,
    k_own,
    v_own,
    grad,
    lse,
    cosine,
    sine,
    dq_out,
    mine_past,
    mine_own,
    other_past,
    other_own,
    dk_past,
    dk_own,
    dv_past,
    dv_own,
):
    slot = pl.program_id(0)
    length, offset = info[slot], info[pl.num_programs(0)]
    parity = info[pl.num_programs(0) + 1]
    for total in (dk_past, dk_own, dv_past, dv_own):
        total[...] = jnp.zeros_like(total)
    attend_back_rows(
        heads, head_dim, scale, length, offset, q, k_past, v_past, k_own, v_own, grad, lse, cosine, sine,
        lambda here, cols, value: dq_out.__setitem__((0, here, cols), value),
        dk_past, dk_own, dv_past, dv_own,
    )

    @pl.when(parity == 0)
    def _():
        mine_past[0] = dk_past[...] * scale
        mine_own[0] = dk_own[...] * scale
        other_past[0] = dv_past[...]
        other_own[0] = dv_own[...]

    @pl.when(parity != 0)
    def _():
        mine_past[0] = dv_past[...]
        mine_own[0] = dv_own[...]
        other_past[0] = dk_past[...] * scale
        other_own[0] = dk_own[...] * scale


def attend_backward(
    info, q, k_past, v_past, k_own, v_own, grad, lse, cosine, sine, heads, head_dim, scale
):
    count, length, width = q.shape
    past = k_past.shape[1]
    by_slot = lambda *shape: pl.BlockSpec((1, *shape), lambda s, info: (s,) + (0,) * len(shape))
    keys = count * length * (past + length) * heads
    return pl.pallas_call(
        functools.partial(attend_back_kernel, heads, head_dim, scale),
        grid_spec=pltpu.PrefetchScalarGridSpec(
            num_scalar_prefetch=1,
            grid=(count,),
            in_specs=[
                by_slot(length, width),
                by_slot(past, head_dim),
                by_slot(past, head_dim),
                by_slot(length, head_dim),
                by_slot(length, head_dim),
                by_slot(length, width),
                by_slot(length, 128),
                by_slot(length, head_dim),
                by_slot(length, head_dim),
            ],
            out_specs=[
                by_slot(length, width),
                by_slot(past, head_dim),
                by_slot(length, head_dim),
                by_slot(past, head_dim),
                by_slot(length, head_dim),
            ],
            scratch_shapes=[
                pltpu.VMEM((past, head_dim), WIDE),
                pltpu.VMEM((length, head_dim), WIDE),
                pltpu.VMEM((past, head_dim), WIDE),
                pltpu.VMEM((length, head_dim), WIDE),
            ],
        ),
        out_shape=[
            jax.ShapeDtypeStruct((count, length, width), LOW),
            jax.ShapeDtypeStruct((count, past, head_dim), WIDE),
            jax.ShapeDtypeStruct((count, length, head_dim), WIDE),
            jax.ShapeDtypeStruct((count, past, head_dim), WIDE),
            jax.ShapeDtypeStruct((count, length, head_dim), WIDE),
        ],
        compiler_params=pltpu.CompilerParams(vmem_limit_bytes=56 << 20),
        cost_estimate=estimate(10 * keys * head_dim, 8 * count * length * width, keys),
    )(info, q, k_past, v_past, k_own, v_own, grad, lse, cosine, sine)


def attend_sum_kernel(
    heads, head_dim, scale, slots, info, q, k_past, v_past, k_own, v_own, weight, own_in, gain, out, lse, middle,
    normed, parts, core_in, far_in, send, recv
):
    step = pl.program_id(0)
    slot = slots - 1 - step
    core, far, _ = partners_of()
    remote = remote_copy(send, recv)
    cores = [remote(parts.at[3 - 2 * k], core_in.at[k], k, core) for k in range(2)]
    to_far = remote(parts.at[2], far_in, 2, far)

    @pl.when(step == 0)
    def _():
        meet((core, far))

    def put(here, value):
        parts[slot, here] = value

    offset = lax.axis_index("ctx") * q.shape[1]
    attend_rows(
        heads, head_dim, scale, info[slot], offset, q, k_past, v_past, k_own, v_own, weight, out, lse, put
    )
    for k in range(2):
        pl.when(step == 2 * k)(cores[k].start)

    @pl.when(step == 1)
    def _():
        cores[0].wait_recv()
        parts[2] = (parts[2].astype(WIDE) + core_in[0].astype(WIDE)).astype(LOW)
        to_far.start()

    @pl.when(step == slots - 1)
    def _():
        cores[1].wait_recv()
        to_far.wait_recv()
        rows = own_in[...].astype(WIDE) + parts[0].astype(WIDE)
        rows = rows + core_in[1].astype(WIDE) + far_in[...].astype(WIDE)
        middle[...] = rows
        inverse = lax.rsqrt(jnp.mean(rows * rows, axis=-1, keepdims=True) + EPS)
        normed[...] = (rows * inverse * gain[...]).astype(LOW)
        for copy in (*cores, to_far):
            copy.wait_send()


def attend_sum(info, q, k_past, v_past, k_own, v_own, weight, own_in, gain, heads, head_dim, scale):
    count, length, width = q.shape
    past, model_width = k_past.shape[1], own_in.shape[1]
    by_slot = lambda *shape: pl.BlockSpec(
        (1, *shape), lambda i, info: (count - 1 - i,) + (0,) * len(shape)
    )
    keys = count * length * (past + length) * heads
    return pl.pallas_call(
        functools.partial(attend_sum_kernel, heads, head_dim, scale, count),
        grid_spec=pltpu.PrefetchScalarGridSpec(
            num_scalar_prefetch=1,
            grid=(count,),
            in_specs=[
                by_slot(length, width),
                by_slot(past, head_dim),
                by_slot(past, head_dim),
                by_slot(length, head_dim),
                by_slot(length, head_dim),
                whole_spec(*weight.shape, once=True),
                whole_spec(length, model_width, once=True),
                whole_spec(1, model_width),
            ],
            out_specs=[
                by_slot(length, width),
                by_slot(length, 128),
                whole_spec(length, model_width, once=True),
                whole_spec(length, model_width, once=True),
            ],
            scratch_shapes=[
                pltpu.VMEM((count, length, model_width), LOW),
                pltpu.VMEM((2, length, model_width), LOW),
                pltpu.VMEM((length, model_width), LOW),
                pltpu.SemaphoreType.DMA((3,)),
                pltpu.SemaphoreType.DMA((3,)),
            ],
        ),
        out_shape=[
            jax.ShapeDtypeStruct((count, length, width), LOW),
            jax.ShapeDtypeStruct((count, length, 128), WIDE),
            jax.ShapeDtypeStruct((length, model_width), WIDE),
            jax.ShapeDtypeStruct((length, model_width), LOW),
        ],
        compiler_params=pltpu.CompilerParams(
            vmem_limit_bytes=56 << 20, collective_id=5, has_side_effects=True
        ),
        cost_estimate=estimate(4 * keys * head_dim, 4 * count * length * width, keys),
    )(info, q, k_past, v_past, k_own, v_own, weight, own_in, gain)


def exchange_kernel(
    heads, head_dim, scale, slots, tiles, info, q, k_past, v_past, k_own, v_own, rows, weight, lse, cosine, sine,
    cosine_all, sine_all, branch, mixed, mlp_far, mlp_side, mlp_own, middle, line, out_grad, block, mine_past,
    mine_own, other_past, other_own, got_past, got_own, side_out, side_in, dk_past, dk_own, dv_past, dv_own,
    own_rows, last_in, grad, send, recv, load
):
    step = pl.program_id(0)
    tensor_rank = lax.axis_index("tp")
    core, far, side = partners_of()
    parity = lax.rem(tensor_rank, 2)
    offset = lax.axis_index("ctx") * q.shape[1]
    remote = remote_copy(send, recv)
    pasts = [remote(other_past.at[r], got_past.at[r ^ 1], r, core) for r in range(slots)]
    owns = [remote(other_own.at[r], got_own.at[r ^ 1], slots + r, core) for r in range(slots)]
    sides = [remote(side_out.at[r], side_in.at[r], 2 * slots + r, side) for r in range(slots)]
    lasts = [
        remote(mlp_far, last_in.at[0], 3 * slots, far),
        remote(mlp_side, last_in.at[1], 3 * slots + 1, side),
    ]
    loading = pltpu.make_async_copy(mlp_own, own_rows, load)

    @pl.when(step == 0)
    def _():
        loading.start()
        meet((core, far, side))
        for copy in lasts:
            copy.start()

    @pl.when(step < slots)
    def _():
        length = info[jnp.minimum(step, slots - 1)]
        for total in (dk_past, dk_own, dv_past, dv_own):
            total[...] = jnp.zeros_like(total)
        grad[0] = jnp.dot(rows[...], weight[...], preferred_element_type=WIDE).astype(LOW)
        attend_back_rows(
            heads, head_dim, scale, length, offset, q, k_past, v_past, k_own, v_own, grad, lse, cosine,
            sine, lambda here, cols, value: line.__setitem__((step, here, cols), value),
            dk_past, dk_own, dv_past, dv_own,
        )

        @pl.when(parity == 0)
        def _():
            mine_past[step] = dk_past[...] * scale
            mine_own[step] = dk_own[...] * scale
            other_past[step] = dv_past[...]
            other_own[step] = dv_own[...]

        @pl.when(parity != 0)
        def _():
            mine_past[step] = dv_past[...]
            mine_own[step] = dv_own[...]
            other_past[step] = dk_past[...] * scale
            other_own[step] = dk_own[...] * scale

    for r in range(slots):

        def start(r=r):
            pasts[r].start()
            owns[r].start()

        pl.when(step == r)(start)

    for pair in range(0, slots, 2):

        def merge(pair=pair):
            for r in (pair, pair + 1):
                pasts[r ^ 1].wait_recv()
                side_out[r] = (mine_past[r] + got_past[r]).astype(LOW)
                sides[r].start()

        pl.when(step == pair + 1)(merge)

    @pl.when(step >= slots)
    def _():
        out_grad[...] = dot_rows(branch[...], mixed[...]).astype(LOW)

    @pl.when(step == slots + tiles - 1)
    def _():
        for r in range(slots):
            owns[r ^ 1].wait_recv()
            sides[r].wait_recv()
            total = mine_own[r] + got_own[r] + side_in[r].astype(WIDE)
            back = turn_back(total, cosine_all[r], sine_all[r])
            line[r, :, heads * head_dim :] = jnp.where(parity == 0, back, total).astype(LOW)
        loading.wait()
        for copy in lasts:
            copy.wait_recv()
        block[...] = (
            middle[...] + own_rows[...].astype(WIDE) + last_in[0].astype(WIDE) + last_in[1].astype(WIDE)
        ).astype(LOW)
        for copy in (*pasts, *owns, *sides, *lasts):
            copy.wait_send()


def attend_exchange(
    info, q, k_past, v_past, k_own, v_own, weight, lse, cosine, sine, heads, head_dim, scale, branch, mixed, mlp,
    middle
):
    count, length, width = q.shape
    past = k_past.shape[1]
    tokens, model_width = branch.shape
    tile = 256
    tiles = model_width // tile
    slot = lambda i: jnp.minimum(i, count - 1)
    by_slot = lambda *shape: pl.BlockSpec((1, *shape), lambda i, info: (slot(i),) + (0,) * len(shape))
    column = lambda i: jnp.clip(i - count, 0, tiles - 1)
    held = lambda *shape: pl.BlockSpec(
        shape, lambda i, info: (0,) * len(shape), pipeline_mode=pl.Buffered(1)
    )
    line_cols = width + head_dim
    return pl.pallas_call(
        functools.partial(exchange_kernel, heads, head_dim, scale, count, tiles),
        grid_spec=pltpu.PrefetchScalarGridSpec(
            num_scalar_prefetch=1,
            grid=(count + tiles,),
            in_specs=[
                by_slot(length, width),
                by_slot(past, head_dim),
                by_slot(past, head_dim),
                by_slot(length, head_dim),
                by_slot(length, head_dim),
                pl.BlockSpec((length, model_width), lambda i, info: (slot(i), 0)),
                held(*weight.shape),
                by_slot(length, 128),
                by_slot(length, head_dim),
                by_slot(length, head_dim),
                held(count, length, head_dim),
                held(count, length, head_dim),
                pl.BlockSpec((tokens, tile), lambda i, info: (0, column(i))),
                held(*mixed.shape),
            ]
            + [ANYWHERE] * 3
            + [held(length, model_width)],
            out_specs=[
                held(count, length, line_cols),
                pl.BlockSpec((tile, width), lambda i, info: (column(i), 0)),
                held(length, model_width),
            ],
            scratch_shapes=[pltpu.VMEM((count, length, head_dim), WIDE)] * 6
            + [pltpu.VMEM((count, length, head_dim), LOW)] * 2
            + [pltpu.VMEM((length, head_dim), WIDE)] * 4
            + [
                pltpu.VMEM((length, model_width), LOW),
                pltpu.VMEM((2, length, model_width), LOW),
                pltpu.VMEM((1, length, width), LOW),
                pltpu.SemaphoreType.DMA((3 * count + 2,)),
                pltpu.SemaphoreType.DMA((3 * count + 2,)),
                pltpu.SemaphoreType.DMA,
            ],
        ),
        out_shape=[
            jax.ShapeDtypeStruct((count, length, line_cols), LOW),
            jax.ShapeDtypeStruct((model_width, width), LOW),
            jax.ShapeDtypeStruct((length, model_width), LOW),
        ],
        compiler_params=pltpu.CompilerParams(
            vmem_limit_bytes=63 << 20, collective_id=4, has_side_effects=True
        ),
        cost_estimate=estimate(2 * tokens * model_width * width, 10 * tokens * width),
    )(info, q, k_past, v_past, k_own, v_own, branch, weight, lse, cosine, sine, cosine, sine, branch, mixed, *mlp, middle)


def local(
    hidden_in,
    cotangent,
    seq_lengths,
    positions,
    permutation,
    query_weight,
    keyval_weight,
    output_weight,
    norm_gains,
    bias_query,
    bias_keyval,
    gate_weight,
    up_weight,
    down_weight,
):
    group_rank = lax.axis_index("fsdp")
    ctx_rank = lax.axis_index("ctx")
    tensor_rank = lax.axis_index("tp")
    fsdp_count = lax.axis_size("fsdp")
    ctx_count = lax.axis_size("ctx")
    tensor_count = lax.axis_size("tp")
    seq_grp, local_len, model_width = hidden_in.shape
    heads, head_dim = bias_query.shape
    keyval_heads = bias_keyval.shape[0] // 2
    assert seq_grp == tensor_count == fsdp_count == len(DEAL_SHIFT)
    token_count = seq_grp * local_len
    scale = 1.0 / math.sqrt(head_dim)
    offset = ctx_rank * local_len
    head_pair = tensor_rank // (tensor_count // keyval_heads)
    parity = tensor_rank % 2
    assert DEAL_SHIFT == tuple((t % 2) * 2 + t // 2 for t in range(tensor_count))

    entry = jnp.arange(permutation.shape[0])
    entry_group, entry_slot = entry // seq_grp, entry % seq_grp
    home_group, home_slot = lax.div(permutation, seq_grp), lax.rem(permutation, seq_grp)
    places = jnp.arange(2 * seq_grp)
    near_places = places < seq_grp
    slot_rank = tensor_rank ^ (places % seq_grp)
    shift_of = lambda rank: lax.rem(rank, 2) * 2 + lax.div(rank, 2)
    target = lax.rem(group_rank + shift_of(tensor_rank), fsdp_count)
    leaving = jnp.sum(jnp.where((entry_group == target) & (home_group == group_rank), home_slot, 0))
    source = lax.rem(group_rank + fsdp_count - shift_of(slot_rank), fsdp_count)
    hit = (entry_group == group_rank)[None] & (home_group[None] == source[:, None])
    slot_now = jnp.sum(jnp.where(hit, entry_slot[None], 0), axis=1)
    seq_now = jnp.sum(jnp.where(hit, permutation[None], 0), axis=1)
    targets = lax.rem(group_rank + shift_of(slot_rank), fsdp_count)
    back_hit = (entry_group[None] == targets[:, None]) & (home_group == group_rank)[None]
    home_order = jnp.sum(jnp.where(back_hit, home_slot[None], 0), axis=1)[:seq_grp]
    there = [
        (f * tensor_count + t, (f + DEAL_SHIFT[t]) % fsdp_count * tensor_count + t)
        for f in range(fsdp_count)
        for t in range(tensor_count)
    ]
    back = [(target, source) for source, target in there]

    split = units_split()
    head_width = 2 * head_dim
    query_cols = heads * head_dim
    near_cols = query_cols + head_width + 128

    outgoing = lax.dynamic_index_in_dim(hidden_in, leaving, 0, keepdims=False)
    own_in = lax.ppermute(outgoing, ("fsdp", "tp"), there)
    small = jnp.concatenate(
        [
            query_weight,
            lax.dynamic_slice_in_dim(keyval_weight, head_pair * head_width, head_width, axis=1),
            jnp.pad(norm_gains.T, ((0, 0), (0, 128 - norm_gains.shape[0]))),
            output_weight.T,
        ],
        axis=1,
    )
    seq_hit = seq_now[:, None] == entry[None]
    lengths_now = jnp.sum(jnp.where(seq_hit, seq_lengths[None], 0), axis=1)
    more = jnp.where(places == seq_grp, offset, jnp.where(places == seq_grp + 1, parity, 0))
    info = jnp.where(near_places, lengths_now, more).astype(jnp.int32)
    positions_now = jnp.sum(
        jnp.where(seq_hit[:seq_grp, :, None], positions[None], 0), axis=1
    )
    lane = jnp.arange(head_dim)
    frequency = 1.0 / ROPE_BASE ** ((lane % (head_dim // 2)).astype(WIDE) * 2.0 / head_dim)
    angles = positions_now.astype(WIDE)[..., None] * frequency
    cosine = jnp.cos(angles)
    sine = jnp.sin(angles) * jnp.where(lane < head_dim // 2, -1.0, 1.0)
    pick_info = jnp.where(near_places, slot_now, slot_now ^ tensor_rank).astype(jnp.int32)
    units = gate_weight.shape[1]
    units_pad = -(-units // 256) * 256
    widen = lambda w: jnp.pad(w, ((0, 0), (0, units_pad - units)))
    shards = [widen(w) for w in (down_weight.T, gate_weight, up_weight)]
    if split:
        half_units = units_pad // 2
        cut = lambda w, c: lax.dynamic_slice_in_dim(w, c * half_units, half_units, axis=1)

        def in_order(own, other):
            return jnp.stack(
                [jnp.where(ctx_rank == 0, own, other), jnp.where(ctx_rank == 0, other, own)]
            )

        def all_rows(both, *earlier):
            full = lax.all_gather(after(both, *earlier), "fsdp", axis=0, tiled=False)
            return full.reshape(-1, both.shape[-1])

        first_units = half_units - half_units // 2 // 256 * 256
        first_cols = 3 * first_units

        def in_parts(c):
            halves = [cut(w, c) for w in shards]
            return jnp.concatenate(
                [w[:, :first_units] for w in halves] + [w[:, first_units:] for w in halves], axis=1
            )

        leaving_units, own_units = in_parts(1 - ctx_rank), in_parts(ctx_rank)
        slot_pick = lax.dynamic_index_in_dim(cotangent, tensor_rank, 0, keepdims=False)
        small = after(small, outgoing, leaving_units, cosine, sine, slot_pick)
        small_both = in_order(small, from_partner(small, "ctx", 1))
        arriving_units = from_partner(after(leaving_units, small_both), "ctx", 1)
        other_own = from_partner(after(slot_pick, arriving_units), "ctx", 1)
        both_a = in_order(own_units[:, :first_cols], arriving_units[:, :first_cols])
        both_b = in_order(own_units[:, first_cols:], arriving_units[:, first_cols:])
    else:
        all_rows = lambda shard, *earlier: lax.all_gather(
            shard, ("fsdp", "ctx"), axis=0, tiled=True
        )
        small_both, unit_both, half_units = small, jnp.concatenate(shards, axis=1), units_pad
    far_in = from_partner(own_in, "tp", 2)
    near_in = from_partner(own_in, "tp", 1)
    ready = (info, pick_info, own_units, home_order) if split else (cosine, sine, info)
    cross_in = from_partner(after(far_in, *ready), "tp", 1)

    near_full = all_rows(small_both, own_in)
    if split:
        units_a = all_rows(both_a, cross_in)
        units_b = all_rows(both_b, cross_in)
    else:
        down_full = all_rows(unit_both[..., :half_units], cross_in)
        gate_up_full = all_rows(unit_both[..., half_units:], cross_in)
    project_full = near_full[:, : query_cols + head_width]
    output_full = near_full[:, near_cols:]
    bias_head = lax.dynamic_slice_in_dim(bias_keyval, head_pair * 2, 2, axis=0)
    bias_row = jnp.concatenate([bias_query.reshape(1, -1), bias_head.reshape(1, -1)], axis=1).astype(WIDE)
    normed_one, query_rot, key_own, value_own = project(
        (own_in, near_in, far_in, cross_in),
        near_full,
        bias_row,
        after(cosine, other_own, both_a, both_b, info, pick_info) if split else cosine,
        sine,
        heads,
        head_dim,
    )
    gains_now = near_full[:, query_cols + head_width : near_cols][:, :2].astype(WIDE).T
    if split:
        key_past, value_past = lax.ppermute((key_own, value_own), "ctx", [(0, 1)])
        other_far = from_partner(other_own, "tp", 2)
        other_near = from_partner(after(other_own, key_past), "tp", 1)
        other_cross = from_partner(after(other_far, key_past), "tp", 1)
        other_rows = (other_own, other_near, other_far, other_cross)
        key_past = after(key_past, other_far)
    else:
        key_past = lax.all_gather(key_own, "ctx", axis=1, tiled=True)
        value_past = lax.all_gather(value_own, "ctx", axis=1, tiled=True)
    in_share = own_in.astype(WIDE)
    if split:
        mixed, lse, middle_share, normed_share = attend_sum(
            info,
            query_rot,
            key_past,
            value_past,
            key_own,
            value_own,
            output_full,
            own_in,
            gains_now[1:2],
            heads,
            head_dim,
            scale,
        )
    else:
        attend = lambda first, *held: attend_forward(
            info, query_rot, *held, key_own, value_own, output_full, heads, head_dim, scale, first, 2
        )

        mixed_far, lse_far, *attn_far = attend(2, key_past, value_past)
        attn_wide = collect_far(attn_far[0], attn_far[1])
        attn_got = from_partner(attn_wide, "tp", 2)
        mixed_near, lse_near, *attn_near = attend(0, after(key_past, attn_wide), value_past)
        attn_core = from_partner(attn_near[1], "tp", 1)
        middle_share = (
            in_share
            + attn_near[0].astype(WIDE)
            + attn_core.astype(WIDE)
            + attn_got.astype(WIDE)
        )
        inv_two = lax.rsqrt(jnp.mean(middle_share * middle_share, axis=-1, keepdims=True) + EPS)
        normed_share = (middle_share * inv_two * gains_now[1]).astype(LOW)
        mixed = jnp.concatenate([mixed_near, mixed_far], axis=0)
        lse = jnp.concatenate([lse_near, lse_far], axis=0)
    half_len = local_len // 2

    if split:
        grad_hidden, grad_rows = chosen_rows(
            pick_info,
            after(cotangent, normed_share),
            other_rows,
            units_a,
            0,
            3,
        )
    else:
        grad_slots = [
            lax.dynamic_index_in_dim(cotangent, slot_now[r], 0, keepdims=False) for r in range(seq_grp)
        ]
        grad_hidden, grad_rows = stack_rows([(g,) for g in grad_slots], down_full, 0, 1)

    def spread_all(own):
        far = from_partner(own, "tp", 2)
        near = from_partner(own, "tp", 1)
        if not split:
            return (own, near, far, from_partner(far, "tp", 1))
        side = from_partner(own, "ctx", 1)
        held = after(far, grad_hidden), after(side, grad_hidden)
        across = from_partner(held[0][:half_len], "ctx", 1), from_partner(held[1][half_len:], "tp", 2)
        cores = [from_partner(v, "tp", 1) for v in held]
        return (own, near, far, cores[0], side, cores[1], *across)

    def in_slots(rows):
        if not split:
            return [(row,) for row in rows]
        return [(row,) for row in rows[:6]] + [rows[6:]]

    mixed_flat = mixed.reshape(token_count, query_cols)
    own_weight = lax.dynamic_slice_in_dim(
        project_full, query_cols + parity * head_dim, head_dim, axis=1
    )
    back_full = jnp.concatenate([project_full[:, :query_cols], own_weight], axis=1)
    normed_slots = in_slots(spread_all(normed_share))
    if split:
        early = after(units_a, back_full)
        ahead = stack_rows(normed_slots[:6], early, 1, 3, total=8)
        last = [normed_slots[6], tuple(from_partner(after(v, ahead[0]), "tp", 1) for v in normed_slots[6])]
        gate_lin, normed_two = stack_rows(last, units_a, 1, 3, into=ahead, first=6, total=8)
        hidden_a, gate_a, up_a = hidden_units(normed_two, units_a, 2, 3, gate_lin, grad_hidden)
        grad_a = first_grads(grad_rows, normed_two, hidden_a, gate_a, up_a)
        hidden_b, gate_b, up_b = full_units(after(normed_two, grad_a), grad_rows, units_b)
    else:
        gate_lin, normed_two = stack_rows(normed_slots, gate_up_full, 0, 2)
        hidden_act, grad_gate, grad_up = hidden_units(
            normed_two, gate_up_full, 1, 2, gate_lin, grad_hidden
        )

    def collect_all(lefts, weights, *earlier):
        lefts = list(lefts)
        lefts[0] = after(lefts[0], *earlier)
        last = back_rows(lefts, weights, 2, 2, local_len)
        got = [from_partner(collect_far(last[0], last[1]), "tp", 2)]
        first = back_rows(lefts, weights, 0, 2, local_len)
        got.append(from_partner(first[1], "tp", 1))

        def finish():
            return sum((v.astype(WIDE) for v in got), first[0].astype(WIDE))

        return first[0], finish

    if split:
        grad_two_share, down_b, up_grad_b = collect_back(
            (gate_a, up_a),
            (gate_b, up_b),
            units_a,
            units_b,
            grad_rows,
            normed_two,
            hidden_b,
            local_len,
        )
        grad_middle, gain_two, gate_grad_b, grad_branch, *mlp = spread_branch(
            grad_two_share,
            middle_share,
            grad_rows,
            gains_now[1:2],
            hidden_a,
            hidden_b,
            units_a,
            units_b,
            normed_two,
            gate_b,
        )
        mlp_own, mlp_far, mlp_side = mlp
        grad_branch = grad_branch.reshape(token_count, model_width)
    else:
        first_back, finish_back = collect_all(
            (grad_gate, grad_up), ((gate_up_full, 0, 2), (gate_up_full, 1, 2))
        )
        down_grad = contract_rows(after(grad_rows, first_back), hidden_act, LOW)
        gate_grad = contract_rows(normed_two, after(grad_gate, down_grad), LOW)
        grad_two_share = finish_back()
        grad_norm_two, gain_two = norm_backward(
            middle_share, inv_two, gains_now[1], grad_two_share
        )
        grad_middle = grad_slots[0].astype(WIDE) + grad_norm_two
        branch_own = grad_middle.astype(LOW)
        branch_far = from_partner(branch_own, "tp", 2)
        branch_near = from_partner(branch_own, "tp", 1)
        branch_cross = from_partner(branch_far, "tp", 1)
        grad_branch = jnp.concatenate([branch_own, branch_near, branch_far, branch_cross], axis=0)
        up_grad = contract_rows(normed_two, after(grad_up, branch_own), LOW)

    grad_mixed = None if split else product(grad_branch, output_full, LOW)
    attend_args = (
        info,
        query_rot,
        key_past,
        value_past,
        key_own,
        value_own,
        output_full if split else grad_mixed.reshape(seq_grp, local_len, query_cols),
        lse,
        cosine,
        sine,
        heads,
        head_dim,
        scale,
    )
    if split:
        line_grad, output_grad, block_share = attend_exchange(
            *attend_args,
            grad_branch,
            mixed_flat,
            (mlp_far, mlp_side, mlp_own),
            middle_share,
        )
        line_grad = line_grad.reshape(token_count, -1)
    else:
        grad_query, mine_past, mine_own, other_past, other_own = attend_backward(*attend_args)
        swap = lambda value: jnp.stack([value[r ^ 1] for r in range(seq_grp)])
        got_past, got_own = from_partner((other_past, other_own), "tp", 1)
        past_sum = mine_past + swap(got_past)
        own_sum = mine_own + swap(got_own)
        own_sum = own_sum + lax.psum_scatter(past_sum, "ctx", scatter_dimension=1, tiled=True)
        half_lanes = head_dim // 2
        turned = own_sum * cosine - jnp.roll(own_sum, half_lanes, axis=-1) * sine
        own_grad = jnp.where(parity == 0, turned, own_sum).astype(LOW).reshape(token_count, head_dim)
        line_grad = jnp.concatenate([grad_query.reshape(token_count, query_cols), own_grad], axis=1)
    def scatter_units(grad):
        if not split:
            return scatter_sum(grad, ctx_rank, LOW)
        return lax.psum_scatter(grad, "fsdp", scatter_dimension=0, tiled=True)

    unit_grads = (grad_a, down_b, up_grad_b, gate_grad_b) if split else (down_grad, gate_grad, up_grad)
    unit_sums = [scatter_units(unit_grads[0])]
    if split:
        unit_sums += [scatter_units(after(g, unit_sums[0])) for g in unit_grads[1:3]]
        unit_sums += [scatter_units(after(unit_grads[3], unit_sums[0]))]
    else:
        unit_sums += [scatter_units(g) for g in unit_grads[1:]]

    normed_flat = normed_one.reshape(token_count, model_width)
    if split:
        input_share, gain_grad, attn_grad, bias_grad, block_home, *unit_gots = finish_rows(
            line_grad,
            back_full,
            own_in,
            grad_middle,
            gains_now[0:1],
            gain_two,
            normed_flat,
            block_share,
            unit_sums,
        )
        attn_grad = jnp.concatenate([attn_grad, output_grad], axis=1)
    else:
        half = token_count // 2
        line_far = contract_cols(line_grad[half:], back_full, LOW).reshape(2, local_len, model_width)
        line_near = contract_cols(line_grad[:half], back_full, LOW).reshape(2, local_len, model_width)
        line_wide = collect_far(line_far[0], line_far[1])
        line_got = from_partner(line_wide, "tp", 2)
        line_core = from_partner(line_near[1], "tp", 1)
        first_mlp, finish_mlp = collect_all((hidden_act,), ((down_full, 0, 1),), up_grad, branch_far)
        block_share = (middle_share + finish_mlp()).astype(LOW)
        grad_one_share = line_near[0].astype(WIDE) + line_core.astype(WIDE) + line_got.astype(WIDE)
        inv_one = lax.rsqrt(jnp.mean(in_share * in_share, axis=-1, keepdims=True) + EPS)
        grad_norm_one, gain_one = norm_backward(in_share, inv_one, gains_now[0], grad_one_share)
        input_share = (grad_middle + grad_norm_one).astype(LOW)
        attn_grad = jnp.concatenate(
            [contract_rows(normed_flat, line_grad, LOW), contract_rows(grad_branch, mixed_flat, LOW)],
            axis=1,
        )
        bias_grad = jnp.sum(line_grad.astype(WIDE), axis=0)

    shard_count = fsdp_count * ctx_count
    share = head_dim // shard_count
    if not split:
        gain_grad = jnp.concatenate([gain_one, gain_two], axis=0)
        gain_grad = gain_grad + from_partner(gain_grad, "tp", 1)
        gain_grad = gain_grad + from_partner(gain_grad, "tp", 2)
    bias_cols = jnp.transpose(bias_grad.reshape(heads + 1, shard_count, share), (1, 2, 0))
    bias_cols = jnp.pad(bias_cols, ((0, 0), (0, (model_width - head_dim) // shard_count), (0, 0)))
    tiny = jnp.concatenate([gain_grad.T, bias_cols.reshape(model_width, heads + 1)], axis=1)
    tiny = jnp.pad(tiny, ((0, 0), (0, 128 - tiny.shape[1]))).astype(LOW)
    attn_grad = jnp.concatenate([attn_grad, tiny], axis=1)
    if split:
        attn_blocks = attn_grad.reshape(fsdp_count, ctx_count, -1, attn_grad.shape[1])
        kept, sent = scatter_ctx(attn_blocks, ctx_rank)
        attn_held = (kept.astype(WIDE) + from_partner(sent, "ctx", 1).astype(WIDE)).astype(LOW)
        attn_held = attn_held.reshape(-1, attn_grad.shape[1])
        attn_end = lax.psum_scatter(after(attn_held, *unit_sums), "fsdp", scatter_dimension=0, tiled=True)
    else:
        attn_end = scatter_sum(attn_grad, ctx_rank, LOW, *unit_sums)


    def leave(share):
        return lax.ppermute(share, ("fsdp", "tp"), back)

    def arrive(own):
        far = from_partner(own, "tp", 2)
        near = from_partner(own, "tp", 1)
        return (own, near, far, from_partner(far, "tp", 1))

    input_home = leave(input_share)
    if not split:
        block_home = leave(block_share)
    block_out = place_rows(arrive(block_home), home_order)
    if split:
        input_home = after(input_home, attn_held)
        input_rows = arrive(input_home)
    else:
        input_rows = arrive(input_home)
    input_grad = place_rows(input_rows, home_order)

    small_at = query_cols + head_dim + query_cols
    tiny_grad = attn_end[:, small_at:].astype(WIDE)

    if split:

        def own_half(total):
            rows = total.shape[0] // 2
            return lax.dynamic_slice_in_dim(total, ctx_rank * rows, rows, axis=0)

        (own_a, got_a), *ends = [(own_half(t), got) for t, got in zip(unit_sums, unit_gots)]

        def joined(part, end):
            cols = slice(part * first_units, (part + 1) * first_units)
            own = jnp.concatenate([own_a[:, cols], end[0]], axis=1)
            got = jnp.concatenate([got_a[:, cols], end[1]], axis=1)
            first, second = jnp.where(ctx_rank == 0, own, got), jnp.where(ctx_rank == 0, got, own)
            return jnp.concatenate([first, second], axis=1)[:, :units].astype(WIDE)

        down_end, gate_end, up_end = joined(0, ends[0]), joined(1, ends[2]), joined(2, ends[1])
    else:
        down_end, gate_end, up_end = (t[:, :units].astype(WIDE) for t in unit_sums)
    return (
        block_out,
        input_grad,
        attn_end[:, :query_cols].astype(WIDE),
        attn_end[:, query_cols : query_cols + head_dim].astype(WIDE),
        attn_end[:, query_cols + head_dim : small_at].astype(WIDE).T,
        tiny_grad[:, :2].T,
        tiny_grad[:share, 2 : 2 + heads].T,
        tiny_grad[:share, 2 + heads : 3 + heads].T,
        gate_end,
        up_end,
        down_end.T,
    )


def solution(mesh):
    placed = (
        P("fsdp", "ctx", None),
        P("fsdp", "ctx", None),
        P(),
        P(None, "ctx"),
        P(),
        P(("fsdp", "ctx"), "tp"),
        P(("fsdp", "ctx"), None),
        P("tp", ("fsdp", "ctx")),
        P(None, ("fsdp", "ctx")),
        P("tp", None),
        P(),
        P(("fsdp", "ctx"), "tp"),
        P(("fsdp", "ctx"), "tp"),
        P("tp", ("fsdp", "ctx")),
    )
    return jax.shard_map(
        local,
        mesh=mesh,
        in_specs=placed,
        out_specs=(
            P("fsdp", "ctx", None),
            P("fsdp", "ctx", None),
            P(("fsdp", "ctx"), "tp"),
            P(("fsdp", "ctx"), "tp"),
            P("tp", ("fsdp", "ctx")),
            P(None, ("fsdp", "ctx")),
            P("tp", ("fsdp", "ctx")),
            P("tp", ("fsdp", "ctx")),
            P(("fsdp", "ctx"), "tp"),
            P(("fsdp", "ctx"), "tp"),
            P("tp", ("fsdp", "ctx")),
        ),
        check_vma=False,
    )
```

```python
import functools
import math

import jax
import jax.numpy as jnp
from jax import lax
from jax.experimental import pallas as pl
from jax.experimental.pallas import tpu as pltpu
from jax.sharding import PartitionSpec as P

EPS = 1e-06
ROPE_BASE = 10000.0
NEG_FILL = -1e30
LOW = jnp.bfloat16
WIDE = jnp.float32
DEAL_SHIFT = (0, 2, 1, 3)


def from_partner(value, axis, apart):
    pairs = [(source, source ^ apart) for source in range(lax.axis_size(axis))]
    return lax.ppermute(value, axis, pairs)


def product(left_side, right_side, kind=WIDE):
    return jnp.dot(left_side, right_side, preferred_element_type=WIDE).astype(kind)


def contract_rows(left_side, right_side, kind=WIDE):
    return lax.dot_general(
        left_side, right_side, (((0,), (0,)), ((), ())), preferred_element_type=WIDE
    ).astype(kind)


def contract_cols(left_side, right_side, kind=WIDE):
    return lax.dot_general(
        left_side, right_side, (((1,), (1,)), ((), ())), preferred_element_type=WIDE
    ).astype(kind)


def norm_backward(values, scale_inv, gain_row, upstream):
    scaled = gain_row * upstream
    inner_mean = jnp.mean(values * scaled, axis=-1, keepdims=True)
    grad_in = scale_inv * scaled - values * (scale_inv * scale_inv * scale_inv) * inner_mean
    gain_grad = jnp.sum(upstream * values * scale_inv, axis=0, keepdims=True)
    return (grad_in, gain_grad)


def after(value, *earlier):
    return lax.optimization_barrier((value, *earlier))[0]


def collect_far(far_part, cross_part):
    wide = far_part.astype(WIDE) + from_partner(cross_part, "tp", 1).astype(WIDE)
    return wide.astype(LOW)


def units_split():
    return lax.axis_size("ctx") == 2


def all_rows(shard):
    return lax.all_gather(shard, "fsdp", axis=0, tiled=True)


def scatter_ctx(blocks, ctx_rank):
    kept = lax.dynamic_index_in_dim(blocks, ctx_rank, 1, keepdims=False)
    sent = lax.dynamic_index_in_dim(blocks, 1 - ctx_rank, 1, keepdims=False)
    return kept, sent


def scatter_sum(grad, ctx_rank, kind, *earlier):
    fsdp_count, ctx_count = lax.axis_size("fsdp"), lax.axis_size("ctx")
    rows, cols = grad.shape
    blocks = grad.reshape(fsdp_count, ctx_count, rows // (fsdp_count * ctx_count), cols)
    if ctx_count == 2:
        kept, sent = scatter_ctx(blocks, ctx_rank)
        got = from_partner(sent, "ctx", 1)
        held = (after(kept, *earlier).astype(WIDE) + got.astype(WIDE)).astype(kind)
    else:
        swapped = jnp.swapaxes(blocks, 0, 1).reshape(rows, cols)
        held = lax.psum_scatter(swapped, "ctx", scatter_dimension=0, tiled=True)
    held = held.reshape(rows // ctx_count, cols)
    return lax.psum_scatter(held, "fsdp", scatter_dimension=0, tiled=True)


def estimate(flops, moved, transcendentals=0):
    return pl.CostEstimate(flops=flops, bytes_accessed=moved, transcendentals=transcendentals)


def part_spec(rows, cols, part):
    return pl.BlockSpec((rows, cols), lambda *_: (0, part), pipeline_mode=pl.Buffered(1))


def whole_spec(*shape, once=False):
    mode = {"pipeline_mode": pl.Buffered(1)} if once else {}
    return pl.BlockSpec(shape, lambda *_: (0,) * len(shape), **mode)


def rows_kernel(groups, *refs):
    slot = pl.program_id(0)
    weight, (lin, stacked) = refs[sum(groups)], refs[-2:]

    def run(pieces):
        start = 0
        for piece in pieces:
            stacked[start : start + piece.shape[0]] = piece[...]
            start += piece.shape[0]
        lin[...] = jnp.dot(stacked[...], weight[...], preferred_element_type=WIDE).astype(LOW)

    first = 0
    for r, pieces in enumerate(groups):
        pl.when(slot == r)(functools.partial(run, refs[first : first + pieces]))
        first += pieces


def stack_rows(slots, weight, part, parts, into=None, first=0, total=None):
    groups = [len(s) for s in slots]
    rows = [piece for s in slots for piece in s]
    width, length = rows[0].shape[1], sum(piece.shape[0] for piece in slots[0])
    count, cols = len(slots), weight.shape[1] // parts
    total = total or count
    into = into or ()
    return pl.pallas_call(
        functools.partial(rows_kernel, groups),
        grid=(count,),
        in_specs=[whole_spec(*piece.shape, once=True) for piece in rows]
        + [part_spec(width, cols, part)]
        + [pl.BlockSpec(memory_space=pl.ANY)] * len(into),
        out_specs=[
            pl.BlockSpec((length, cols), lambda s: (first + s, 0)),
            pl.BlockSpec((length, width), lambda s: (first + s, 0)),
        ],
        out_shape=[
            jax.ShapeDtypeStruct((total * length, cols), LOW),
            jax.ShapeDtypeStruct((total * length, width), LOW),
        ],
        input_output_aliases={len(rows) + 1 + i: i for i in range(len(into))},
        compiler_params=pltpu.CompilerParams(vmem_limit_bytes=60 << 20),
        cost_estimate=estimate(
            2 * count * length * width * cols, 2 * (count * length * (2 * width + cols) + width * cols)
        ),
    )(*rows, weight, *into)


def units_kernel(h, up, gate, grad, hid, grad_gate, grad_up):
    up_lin = jnp.dot(h[...], up[...], preferred_element_type=WIDE)
    gate_lin = gate[...].astype(WIDE)
    grad_hidden = grad[...].astype(WIDE)
    sigmoid = 1.0 / (1.0 + jnp.exp(-gate_lin))
    silu = gate_lin * sigmoid
    hid[...] = (silu * up_lin).astype(LOW)
    grad_gate[...] = (grad_hidden * up_lin * sigmoid * (1.0 + gate_lin * (1.0 - sigmoid))).astype(LOW)
    grad_up[...] = (grad_hidden * silu).astype(LOW)


def hidden_units(h, up, part, parts, gate_lin, grad_hidden):
    tokens, width = h.shape
    cols = up.shape[1] // parts
    step = math.gcd(512, tokens)
    by_row = lambda n: pl.BlockSpec((step, n), lambda i: (i, 0))
    return pl.pallas_call(
        units_kernel,
        grid=(tokens // step,),
        in_specs=[by_row(width), part_spec(width, cols, part), by_row(cols), by_row(cols)],
        out_specs=[by_row(cols)] * 3,
        out_shape=[jax.ShapeDtypeStruct((tokens, cols), LOW)] * 3,
        compiler_params=pltpu.CompilerParams(vmem_limit_bytes=60 << 20),
        cost_estimate=estimate(
            2 * tokens * width * cols, 2 * (tokens * width + width * cols + 5 * tokens * cols)
        ),
    )(h, up, gate_lin, grad_hidden)


def back_kernel(terms, *refs):
    lefts, weights, outs = refs[:terms], refs[terms : 2 * terms], refs[2 * terms :]
    total = None
    for left, weight in zip(lefts, weights):
        term = dot_cols(left[...], weight[...])
        total = term if total is None else total + term
    for i, out in enumerate(outs):

        @pl.when(pl.program_id(0) == i)
        def _():
            out[...] = total.astype(LOW)


def back_rows(lefts, weights, first_slot, slots, length):
    width = weights[0][0].shape[0]
    depth = sum(left.shape[1] for left in lefts)
    return pl.pallas_call(
        functools.partial(back_kernel, len(lefts)),
        grid=(slots,),
        in_specs=[
            pl.BlockSpec((length, left.shape[1]), lambda s: (first_slot + s, 0)) for left in lefts
        ]
        + [part_spec(width, w.shape[1] // parts, part) for w, part, parts in weights],
        out_specs=[whole_spec(length, width)] * slots,
        out_shape=[jax.ShapeDtypeStruct((length, width), LOW)] * slots,
        compiler_params=pltpu.CompilerParams(vmem_limit_bytes=60 << 20),
        cost_estimate=estimate(
            2 * slots * length * width * depth,
            2 * (slots * length * (width + depth) + width * depth),
        ),
    )(*lefts, *[w for w, _, _ in weights])


def chosen_kernel(near, count, info, cotangent, *refs):
    slot = pl.program_id(0)
    others, (weight, lin, stacked) = refs[:count], refs[count:]

    @pl.when(slot < near)
    def _():
        stacked[...] = cotangent[0]

    for k, other in enumerate(others):

        @pl.when((slot >= near) & (info[slot] == k))
        def _():
            stacked[...] = other[...]

    lin[...] = jnp.dot(stacked[...], weight[...], preferred_element_type=WIDE).astype(LOW)


def chosen_rows(info, cotangent, others, weight, part, parts):
    near, length, width = cotangent.shape
    slots, cols = near + len(others), weight.shape[1] // parts
    held = lambda rows, n, at: pl.BlockSpec(
        (rows, n), lambda s, info: (0, at), pipeline_mode=pl.Buffered(1)
    )
    return pl.pallas_call(
        functools.partial(chosen_kernel, near, len(others)),
        grid_spec=pltpu.PrefetchScalarGridSpec(
            num_scalar_prefetch=1,
            grid=(slots,),
            in_specs=[
                pl.BlockSpec((1, length, width), lambda s, info: (info[jnp.minimum(s, near - 1)], 0, 0))
            ]
            + [held(length, width, 0)] * len(others)
            + [held(width, cols, part)],
            out_specs=[
                pl.BlockSpec((length, cols), lambda s, info: (s, 0)),
                pl.BlockSpec((length, width), lambda s, info: (s, 0)),
            ],
        ),
        out_shape=[
            jax.ShapeDtypeStruct((slots * length, cols), LOW),
            jax.ShapeDtypeStruct((slots * length, width), LOW),
        ],
        compiler_params=pltpu.CompilerParams(vmem_limit_bytes=60 << 20),
        cost_estimate=estimate(
            2 * slots * length * width * cols, 2 * (slots * length * (2 * width + cols) + width * cols)
        ),
    )(info, cotangent, *others, weight)


def full_units_kernel(h, g, down, gate, up, hid, grad_gate, grad_up):
    gate_lin = jnp.dot(h[...], gate[...], preferred_element_type=WIDE)
    up_lin = jnp.dot(h[...], up[...], preferred_element_type=WIDE)
    grad_hidden = jnp.dot(g[...], down[...], preferred_element_type=WIDE)
    sigmoid = 1.0 / (1.0 + jnp.exp(-gate_lin))
    silu = gate_lin * sigmoid
    hid[...] = (silu * up_lin).astype(LOW)
    grad_gate[...] = (grad_hidden * up_lin * sigmoid * (1.0 + gate_lin * (1.0 - sigmoid))).astype(LOW)
    grad_up[...] = (grad_hidden * silu).astype(LOW)


def full_units(h, g, weight):
    tokens, width = h.shape
    cols = weight.shape[1] // 3
    step = math.gcd(512, tokens)
    by_row = lambda n: pl.BlockSpec((step, n), lambda i: (i, 0))
    return pl.pallas_call(
        full_units_kernel,
        grid=(tokens // step,),
        in_specs=[by_row(width)] * 2 + [part_spec(width, cols, i) for i in range(3)],
        out_specs=[by_row(cols)] * 3,
        out_shape=[jax.ShapeDtypeStruct((tokens, cols), LOW)] * 3,
        compiler_params=pltpu.CompilerParams(vmem_limit_bytes=60 << 20),
        cost_estimate=estimate(
            6 * tokens * width * cols, 2 * (2 * tokens * width + 3 * width * cols + 3 * tokens * cols)
        ),
    )(h, g, weight, weight, weight)


def first_grads_kernel(g, h, hid, gate, up, out):
    part = pl.program_id(0)
    for i, (left, right) in enumerate(((g, hid), (h, gate), (h, up))):

        @pl.when(part == i)
        def _():
            out[...] = dot_rows(left[...], right[...]).astype(LOW)


def first_grads(grad_rows, rows, hid, grad_gate, grad_up):
    tokens, width = rows.shape
    cols, tile = hid.shape[1], 256
    tiles = width // tile
    return pl.pallas_call(
        first_grads_kernel,
        grid=(3, tiles),
        in_specs=[
            pl.BlockSpec((tokens, tile), lambda p, i: (0, jnp.where(p == 0, i, tiles - 1))),
            pl.BlockSpec((tokens, tile), lambda p, i: (0, jnp.where(p == 0, 0, i))),
        ]
        + [whole_spec(tokens, cols, once=True)] * 3,
        out_specs=pl.BlockSpec((tile, cols), lambda p, i: (i, p)),
        out_shape=jax.ShapeDtypeStruct((width, 3 * cols), LOW),
        compiler_params=pltpu.CompilerParams(vmem_limit_bytes=60 << 20),
        cost_estimate=estimate(6 * tokens * width * cols, 6 * tokens * cols + 6 * width * cols),
    )(grad_rows, rows, hid, grad_gate, grad_up)


MESH_ID = pl.DeviceIdType.MESH


def meet(partners):
    barrier = pltpu.get_barrier_semaphore()
    for partner in partners:
        pl.semaphore_signal(barrier, inc=1, device_id=partner, device_id_type=MESH_ID)
    pl.semaphore_wait(barrier, len(partners))


def partners_of():
    tensor_rank, ctx_rank = lax.axis_index("tp"), lax.axis_index("ctx")
    return {"tp": tensor_rank ^ 1}, {"tp": tensor_rank ^ 2}, {"ctx": ctx_rank ^ 1}


def collect_kernel(
    slots, tiles, gate_a, up_a, gate_b, up_b, w_gate_a, w_up_a, w_gate_b, w_up_b, left, right, hid, up, total,
    down_out, up_out, parts, sent, core_in, across_in, last_in, held, send, recv, load
):
    step = pl.program_id(0)
    steps = pl.num_programs(0)
    core, far, side = partners_of()
    half = total.shape[0] // 2
    remote = remote_copy(send, recv)
    cores = [remote(sent.at[k % 2], core_in.at[k], k, core) for k in range(4)]
    across = [
        remote(parts.at[3, pl.ds(0, half)], across_in.at[0], 4, far),
        remote(parts.at[3, pl.ds(half, half)], across_in.at[1], 5, side),
    ]
    lasts = [
        remote(parts.at[1], last_in.at[0], 6, far),
        remote(parts.at[2, pl.ds(half, half)], last_in.at[1, pl.ds(half, half)], 7, side),
        remote(parts.at[2, pl.ds(0, half)], last_in.at[1, pl.ds(0, half)], 8, side),
    ]
    loading = [
        pltpu.make_async_copy(source, held.at[i], load.at[i]) for i, source in enumerate((hid, up))
    ]

    @pl.when(step == 0)
    def _():
        for copy in loading:
            copy.start()
        meet((core, far, side))

    for k in (2, 3):
        pl.when(step == 2 * k)(cores[k - 2].wait_send)

    @pl.when(step < slots)
    def _():
        part = (
            dot_cols(gate_a[...], w_gate_a[...])
            + dot_cols(up_a[...], w_up_a[...])
            + dot_cols(gate_b[...], w_gate_b[...])
            + dot_cols(up_b[...], w_up_b[...])
        )

        @pl.when(step == slots - 1)
        def _():
            total[...] = part

        for k in range(4):

            @pl.when(step == 2 * k)
            def _():
                sent[k % 2] = part.astype(LOW)
                cores[k].start()

            if k < 3:

                @pl.when(step == 2 * k + 1)
                def _():
                    cores[k].wait_recv()
                    parts[3 - k] = (part + core_in[k].astype(WIDE)).astype(LOW)

    def add(slot, rows, value):
        parts[slot, rows] = (parts[slot, rows].astype(WIDE) + value.astype(WIDE)).astype(LOW)

    low, high = pl.ds(0, half), pl.ds(half, half)

    @pl.when(step == 1)
    def _():
        for copy in across:
            copy.start()

    pl.when(step == 3)(lasts[1].start)

    @pl.when(step == 5)
    def _():
        across[1].wait_recv()
        add(1, high, across_in[1])
        lasts[0].start()
        across[0].wait_recv()
        add(2, low, across_in[0])
        lasts[2].start()

    @pl.when((step >= slots) & (step < slots + tiles))
    def _():
        pl.when(step == slots)(loading[0].wait)
        down_out[...] = dot_rows(left[...], held[0]).astype(LOW)

    @pl.when(step >= slots + tiles)
    def _():
        pl.when(step == slots + tiles)(loading[1].wait)
        up_out[...] = dot_rows(right[...], held[1]).astype(LOW)

    @pl.when(step == steps - 1)
    def _():
        cores[3].wait_recv()
        for copy in lasts:
            copy.wait_recv()
        total[...] += (
            core_in[3].astype(WIDE) + last_in[0].astype(WIDE) + last_in[1].astype(WIDE)
        )
        for copy in (*cores[2:], *across, *lasts):
            copy.wait_send()


def collect_back(first, second, weight_a, weight_b, grad_rows, rows, hid, length):
    tokens, cols_a = first[0].shape
    cols = second[0].shape[1]
    width = weight_a.shape[0]
    slots, tile = tokens // length, 256
    tiles = width // tile
    row = lambda n: pl.BlockSpec((length, n), lambda i: (jnp.maximum(slots - 1 - i, 0), 0))
    column = lambda i, start: jnp.clip(i - start, 0, tiles - 1)
    down_at, up_at = (lambda i: column(i, slots)), (lambda i: column(i, slots + tiles))
    return pl.pallas_call(
        functools.partial(collect_kernel, slots, tiles),
        grid=(slots + 2 * tiles,),
        in_specs=[row(cols_a), row(cols_a), row(cols), row(cols)]
        + [part_spec(width, cols_a, 1), part_spec(width, cols_a, 2)]
        + [part_spec(width, cols, 1), part_spec(width, cols, 2)]
        + [
            pl.BlockSpec((tokens, tile), lambda i: (0, down_at(i))),
            pl.BlockSpec((tokens, tile), lambda i: (0, up_at(i))),
            ANYWHERE,
            ANYWHERE,
        ],
        out_specs=[
            whole_spec(length, width, once=True),
            pl.BlockSpec((tile, cols), lambda i: (down_at(i), 0)),
            pl.BlockSpec((tile, cols), lambda i: (up_at(i), 0)),
        ],
        out_shape=[
            jax.ShapeDtypeStruct((length, width), WIDE),
            jax.ShapeDtypeStruct((width, cols), LOW),
            jax.ShapeDtypeStruct((width, cols), LOW),
        ],
        scratch_shapes=[
            pltpu.VMEM((4, length, width), LOW),
            pltpu.VMEM((2, length, width), LOW),
            pltpu.VMEM((4, length, width), LOW),
            pltpu.VMEM((2, length // 2, width), LOW),
            pltpu.VMEM((2, length, width), LOW),
            pltpu.VMEM((2, tokens, cols), LOW),
            pltpu.SemaphoreType.DMA((9,)),
            pltpu.SemaphoreType.DMA((9,)),
            pltpu.SemaphoreType.DMA((2,)),
        ],
        compiler_params=pltpu.CompilerParams(
            vmem_limit_bytes=63 << 20, collective_id=1, has_side_effects=True
        ),
        cost_estimate=estimate(6 * tokens * width * cols, 10 * tokens * cols),
    )(*first, *second, weight_a, weight_a, weight_b, weight_b, grad_rows, rows, hid, second[1])


def remote_copy(send, recv):
    def make(source, target, index, partner):
        return pltpu.make_async_remote_copy(
            source, target, send.at[index], recv.at[index], device_id=partner, device_id_type=MESH_ID
        )

    return make


def branch_kernel(
    slots, tiles, total, middle, own_grad, gain, hid_a, hid_b, w_a, w_b, turned, gate, grad_middle, gain_grad,
    gate_out, branch, mlp_own, mlp_far, mlp_side, own, parts, core_in, across_in, held, send, recv, load
):
    step = pl.program_id(0)
    core, far, side = partners_of()
    remote = remote_copy(send, recv)
    to_far = remote(own, branch.at[2], 0, far)
    to_near = remote(own, branch.at[1], 1, core)
    to_cross = remote(branch.at[2], branch.at[3], 2, core)
    keep = pltpu.make_async_copy(own, branch.at[0], load.at[0])
    loading = pltpu.make_async_copy(gate, held, load.at[1])
    cores = [remote(parts.at[7 - 2 * k], core_in.at[k], 3 + k, core) for k in range(4)]
    across = remote(parts.at[6], across_in, 7, side)
    stores = [
        pltpu.make_async_copy(parts.at[4], mlp_side, load.at[2]),
        pltpu.make_async_copy(parts.at[2], mlp_far, load.at[3]),
        pltpu.make_async_copy(parts.at[0], mlp_own, load.at[4]),
    ]

    @pl.when(step == 0)
    def _():
        loading.start()
        meet((core, far, side))
        values, upstream = middle[...], total[...]
        inverse = lax.rsqrt(jnp.mean(values * values, axis=-1, keepdims=True) + EPS)
        grad_in, gain_grad[...] = norm_backward(values, inverse, gain[...], upstream)
        grad_in = own_grad[...].astype(WIDE) + grad_in
        grad_middle[...] = grad_in
        own[...] = grad_in.astype(LOW)
        for copy in (to_far, to_near, keep):
            copy.start()

    @pl.when(step < slots)
    def _():
        part = dot_cols(hid_a[...], w_a[...]) + dot_cols(hid_b[...], w_b[...])
        parts[slots - 1 - step] = part.astype(LOW)

    for k in range(4):
        pl.when(step == 2 * k)(cores[k].start)

        def finish(k=k):
            slot = 6 - 2 * k
            cores[k].wait_recv()
            parts[slot] = (parts[slot].astype(WIDE) + core_in[k].astype(WIDE)).astype(LOW)
            if k == 0:
                across.start()
            if k == 1:
                stores[0].start()
            if k == 3:
                stores[2].start()

        pl.when(step == 2 * k + 1)(finish)

    @pl.when(step >= slots)
    def _():
        pl.when(step == slots)(loading.wait)
        gate_out[...] = dot_rows(turned[...], held[...]).astype(LOW)

    @pl.when(step == slots + tiles - 2)
    def _():
        to_far.wait_recv()
        to_cross.start()

    @pl.when(step == slots + tiles - 1)
    def _():
        to_near.wait_recv()
        to_cross.wait_recv()
        across.wait_recv()
        parts[2] = (parts[2].astype(WIDE) + across_in[...].astype(WIDE)).astype(LOW)
        stores[1].start()
        keep.wait()
        for copy in stores:
            copy.wait()
        for copy in (to_far, to_near, to_cross, *cores, across):
            copy.wait_send()


ANYWHERE = pl.BlockSpec(memory_space=pl.ANY)


def spread_branch(total, middle, own_grad, gain, hid_a, hid_b, weight_a, weight_b, rows, grad_gate):
    length, width = total.shape
    tokens, cols = grad_gate.shape
    slots, tile = tokens // length, 256
    tiles = width // tile
    once = whole_spec(length, width, once=True)
    column = lambda i: jnp.clip(i - slots, 0, tiles - 1)
    part = jax.ShapeDtypeStruct((length, width), LOW)
    return pl.pallas_call(
        functools.partial(branch_kernel, slots, tiles),
        grid=(slots + tiles,),
        in_specs=[
            once,
            once,
            once,
            whole_spec(1, width),
            pl.BlockSpec((length, hid_a.shape[1]), lambda i: (jnp.maximum(slots - 1 - i, 0), 0)),
            pl.BlockSpec((length, cols), lambda i: (jnp.maximum(slots - 1 - i, 0), 0)),
            part_spec(width, hid_a.shape[1], 0),
            part_spec(width, cols, 0),
            pl.BlockSpec((tokens, tile), lambda i: (0, column(i))),
            ANYWHERE,
        ],
        out_specs=[
            whole_spec(length, width, once=True),
            whole_spec(1, width),
            pl.BlockSpec((tile, cols), lambda i: (column(i), 0)),
        ]
        + [ANYWHERE] * 4,
        out_shape=[
            jax.ShapeDtypeStruct((length, width), WIDE),
            jax.ShapeDtypeStruct((1, width), WIDE),
            jax.ShapeDtypeStruct((width, cols), LOW),
            jax.ShapeDtypeStruct((4, length, width), LOW),
            part,
            part,
            part,
        ],
        scratch_shapes=[
            pltpu.VMEM((length, width), LOW),
            pltpu.VMEM((slots, length, width), LOW),
            pltpu.VMEM((4, length, width), LOW),
            pltpu.VMEM((length, width), LOW),
            pltpu.VMEM((tokens, cols), LOW),
            pltpu.SemaphoreType.DMA((8,)),
            pltpu.SemaphoreType.DMA((8,)),
            pltpu.SemaphoreType.DMA((5,)),
        ],
        compiler_params=pltpu.CompilerParams(
            vmem_limit_bytes=63 << 20, collective_id=2, has_side_effects=True
        ),
        cost_estimate=estimate(4 * tokens * width * cols, 10 * tokens * cols),
    )(total, middle, own_grad, gain, hid_a, hid_b, weight_a, weight_b, rows, grad_gate)


def line_kernel(
    slots, tiles, count, line, weight, own_in, grad_middle, gain, gain_two, rows_one, line_all, block, *refs
):
    sums, (share, gain_grad, attn_out, bias_out, home) = refs[:count], refs[count : count + 5]
    gots = refs[count + 5 : 2 * count + 5]
    parts, core_in, far_in, total, gains, gains_in, send, recv, load = refs[2 * count + 5 :]
    step = pl.program_id(0)
    core, far, side = partners_of()
    tensor_rank, group = lax.axis_index("tp"), lax.axis_index("fsdp")
    shift = (tensor_rank % 2) * 2 + tensor_rank // 2
    target = {"fsdp": (group + slots - shift) % slots}
    source = {"fsdp": (group + shift) % slots}
    stays = shift == 0
    remote = remote_copy(send, recv)
    cores = [remote(parts.at[3 - 2 * k], core_in.at[k], k, core) for k in range(2)]
    to_far = remote(parts.at[2], far_in, 2, far)
    leave = remote(block, home, 3, target)
    keep = pltpu.make_async_copy(block, home, load)
    cross = {"tp": tensor_rank ^ 3}
    gain_copies = [
        remote(gains, gains_in.at[i], 4 + i, partner) for i, partner in enumerate((core, far, cross))
    ]
    rows = gots[0].shape[0]
    there = pl.multiple_of((1 - lax.axis_index("ctx")) * rows, rows)
    sides = [
        remote(held.at[pl.ds(there, rows)], got, 7 + i, side) for i, (held, got) in enumerate(zip(sums, gots))
    ]

    @pl.when(step == 0)
    def _():
        barrier = pltpu.get_barrier_semaphore()
        for partner in (core, far, cross, side):
            pl.semaphore_signal(barrier, inc=1, device_id=partner, device_id_type=MESH_ID)

        @pl.when(stays)
        def _():
            pl.semaphore_wait(barrier, 4)
            keep.start()

        @pl.when(jnp.logical_not(stays))
        def _():
            for partner in (target, source):
                pl.semaphore_signal(barrier, inc=1, device_id=partner, device_id_type=MESH_ID)
            pl.semaphore_wait(barrier, 6)
            leave.start()

        for copy in sides:
            copy.start()

    @pl.when(step < slots)
    def _():
        part = dot_cols(line[...], weight[...])
        parts[slots - 1 - step] = part.astype(LOW)

        @pl.when(step == slots - 1)
        def _():
            total[...] = part

    for k in range(2):
        pl.when(step == 2 * k)(cores[k].start)

    @pl.when(step == 1)
    def _():
        cores[0].wait_recv()
        parts[2] = (parts[2].astype(WIDE) + core_in[0].astype(WIDE)).astype(LOW)
        to_far.start()

    @pl.when(step == slots - 1)
    def _():
        bias_out[...] = jnp.sum(line_all[...].astype(WIDE), axis=0, keepdims=True)

    @pl.when(step >= slots)
    def _():
        attn_out[...] = dot_rows(rows_one[...], line_all[...]).astype(LOW)

    @pl.when(step == slots + tiles - 1)
    def _():
        cores[1].wait_recv()
        to_far.wait_recv()
        upstream = total[...] + core_in[1].astype(WIDE) + far_in[...].astype(WIDE)
        values = own_in[...].astype(WIDE)
        inverse = lax.rsqrt(jnp.mean(values * values, axis=-1, keepdims=True) + EPS)
        grad_in, gain_one = norm_backward(values, inverse, gain[...], upstream)
        gains[0:1] = gain_one
        gains[1:2] = gain_two[...]
        for copy in gain_copies:
            copy.start()
        share[...] = (grad_middle[...] + grad_in).astype(LOW)
        for copy in gain_copies:
            copy.wait_recv()
        gain_grad[...] = (gains[...] + gains_in[0]) + (gains_in[1] + gains_in[2])
        for copy in sides:
            copy.wait_recv()
        for copy in (*cores, to_far, *gain_copies, *sides):
            copy.wait_send()
        pl.when(stays)(keep.wait)

        @pl.when(jnp.logical_not(stays))
        def _():
            leave.wait_recv()
            leave.wait_send()


def finish_rows(line, weight, own_in, grad_middle, gain, gain_two, rows_one, block, sums):
    length, width = own_in.shape
    near_tokens, line_cols = line.shape
    slots, tile = near_tokens // length, 256
    tiles = width // tile
    once = whole_spec(length, width, once=True)
    column = lambda i: jnp.clip(i - slots, 0, tiles - 1)
    by_column = lambda n: pl.BlockSpec((n, tile), lambda i: (0, column(i)))
    attn_cols = line_cols
    return pl.pallas_call(
        functools.partial(line_kernel, slots, tiles, len(sums)),
        grid=(slots + tiles,),
        in_specs=[
            pl.BlockSpec((length, line_cols), lambda i: (jnp.maximum(slots - 1 - i, 0), 0)),
            whole_spec(width, line_cols, once=True),
            once,
            once,
            whole_spec(1, width),
            whole_spec(1, width),
            by_column(near_tokens),
            whole_spec(near_tokens, line_cols, once=True),
            ANYWHERE,
        ]
        + [ANYWHERE] * len(sums),
        out_specs=[
            whole_spec(length, width),
            whole_spec(2, width),
            pl.BlockSpec((tile, attn_cols), lambda i: (column(i), 0)),
            whole_spec(1, line_cols),
            ANYWHERE,
        ]
        + [ANYWHERE] * len(sums),
        out_shape=[
            jax.ShapeDtypeStruct((length, width), LOW),
            jax.ShapeDtypeStruct((2, width), WIDE),
            jax.ShapeDtypeStruct((width, attn_cols), LOW),
            jax.ShapeDtypeStruct((1, line_cols), WIDE),
            jax.ShapeDtypeStruct((length, width), LOW),
        ]
        + [jax.ShapeDtypeStruct((t.shape[0] // 2, t.shape[1]), LOW) for t in sums],
        scratch_shapes=[
            pltpu.VMEM((slots, length, width), LOW),
            pltpu.VMEM((2, length, width), LOW),
            pltpu.VMEM((length, width), LOW),
            pltpu.VMEM((length, width), WIDE),
            pltpu.VMEM((2, width), WIDE),
            pltpu.VMEM((3, 2, width), WIDE),
            pltpu.SemaphoreType.DMA((7 + len(sums),)),
            pltpu.SemaphoreType.DMA((7 + len(sums),)),
            pltpu.SemaphoreType.DMA,
        ],
        compiler_params=pltpu.CompilerParams(
            vmem_limit_bytes=63 << 20, collective_id=3, has_side_effects=True
        ),
        cost_estimate=estimate(2 * near_tokens * width * attn_cols, 10 * near_tokens * width),
    )(line, weight, own_in, grad_middle, gain, gain_two, rows_one, line, block, *sums)


def place_kernel(count, info, *refs):
    out = refs[count]
    for r in range(count):

        @pl.when(pl.program_id(0) == r)
        def _():
            out[0] = refs[r][...]


def place_rows(rows, order):
    length, width = rows[0].shape
    count = len(rows)
    held = pl.BlockSpec((length, width), lambda s, info: (0, 0), pipeline_mode=pl.Buffered(1))
    return pl.pallas_call(
        functools.partial(place_kernel, count),
        grid_spec=pltpu.PrefetchScalarGridSpec(
            num_scalar_prefetch=1,
            grid=(count,),
            in_specs=[held] * count,
            out_specs=pl.BlockSpec((1, length, width), lambda s, info: (info[s], 0, 0)),
        ),
        out_shape=jax.ShapeDtypeStruct((count, length, width), LOW),
        compiler_params=pltpu.CompilerParams(vmem_limit_bytes=32 << 20),
        cost_estimate=estimate(0, 4 * count * length * width),
    )(order, *rows)


def turn(values, cosine, sine_signed):
    return values * cosine + pltpu.roll(values, values.shape[-1] // 2, 1) * sine_signed


def turn_back(values, cosine, sine_signed):
    return values * cosine - pltpu.roll(values, values.shape[-1] // 2, 1) * sine_signed


def project_kernel(
    heads, head_dim, x0, x1, x2, x3, gains, weight, bias, cosine, sine, h_out, q_out, k_out, v_out, gain
):
    slot = pl.program_id(0)

    @pl.when(slot == 0)
    def _():
        gain[...] = gains[...].astype(WIDE).T[:8]


    def run(x_ref):
        x = x_ref[...].astype(WIDE)
        scale_inv = lax.rsqrt(jnp.mean(x * x, axis=-1, keepdims=True) + EPS)
        normed = (x * scale_inv * gain[0:1]).astype(LOW)
        h_out[0] = normed
        lin = jnp.dot(normed, weight[...], preferred_element_type=WIDE) + bias[...]
        cos, sin = cosine[0], sine[0]
        for h in range(heads + 1):
            part = turn(lin[:, h * head_dim : (h + 1) * head_dim], cos, sin).astype(LOW)
            if h < heads:
                q_out[0, :, h * head_dim : (h + 1) * head_dim] = part
            else:
                k_out[0] = part
        v_out[0] = lin[:, (heads + 1) * head_dim :].astype(LOW)

    for r, x_ref in enumerate((x0, x1, x2, x3)):
        pl.when(slot == r)(functools.partial(run, x_ref))


def project(rows, held, bias, cosine, sine, heads, head_dim):
    length, width = rows[0].shape
    count = len(rows)
    cols = (heads + 2) * head_dim
    whole = whole_spec
    by_slot = lambda *shape: pl.BlockSpec((1, *shape), lambda s: (s,) + (0,) * len(shape))
    return pl.pallas_call(
        functools.partial(project_kernel, heads, head_dim),
        grid=(count,),
        in_specs=[whole(length, width)] * count
        + [part_spec(width, 128, cols // 128), part_spec(width, cols, 0), whole(1, cols)]
        + [by_slot(length, head_dim)] * 2,
        out_specs=[
            by_slot(length, width),
            by_slot(length, heads * head_dim),
            by_slot(length, head_dim),
            by_slot(length, head_dim),
        ],
        out_shape=[
            jax.ShapeDtypeStruct((count, length, width), LOW),
            jax.ShapeDtypeStruct((count, length, heads * head_dim), LOW),
            jax.ShapeDtypeStruct((count, length, head_dim), LOW),
            jax.ShapeDtypeStruct((count, length, head_dim), LOW),
        ],
        scratch_shapes=[pltpu.VMEM((8, width), WIDE)],
        compiler_params=pltpu.CompilerParams(vmem_limit_bytes=56 << 20),
        cost_estimate=pl.CostEstimate(
            flops=2 * count * length * width * cols,
            bytes_accessed=count * length * (2 * width + cols) * 2 + width * cols * 2,
            transcendentals=0,
        ),
    )(*rows, held, held, bias, cosine, sine)


def row_blocks(length):
    return [(i, min(256, length)) for i in range(0, length, min(256, length))]


def key_biases(length, offset, start, rows, past, keys):
    past_pos = lax.broadcasted_iota(jnp.int32, (1, past), 1)
    past_bias = jnp.where((past_pos < offset) & (past_pos < length), 0.0, NEG_FILL)
    query_pos = offset + start + lax.broadcasted_iota(jnp.int32, (rows, keys), 0)
    own_pos = offset + lax.broadcasted_iota(jnp.int32, (rows, keys), 1)
    own_bias = jnp.where((own_pos <= query_pos) & (own_pos < length), 0.0, NEG_FILL)
    return past_bias, own_bias


def dot_cols(left, right):
    return lax.dot_general(left, right, (((1,), (1,)), ((), ())), preferred_element_type=WIDE)


def dot_rows(left, right):
    return lax.dot_general(left, right, (((0,), (0,)), ((), ())), preferred_element_type=WIDE)


def attend_rows(
    heads, head_dim, scale, length, offset, q, k_past, v_past, k_own, v_own, weight, out, lse, put
):
    past = k_past.shape[1]
    for start, rows in row_blocks(q.shape[1]):
        keys = start + rows
        past_bias, own_bias = key_biases(length, offset, start, rows, past, keys)
        here = slice(start, start + rows)
        for h in range(heads):
            cols = slice(h * head_dim, (h + 1) * head_dim)
            query = q[0, here, cols]
            s_past = dot_cols(query, k_past[0]) * scale + past_bias
            s_own = dot_cols(query, k_own[0, :keys]) * scale + own_bias
            top = jnp.maximum(
                jnp.max(s_past, axis=1, keepdims=True), jnp.max(s_own, axis=1, keepdims=True)
            )
            e_past, e_own = jnp.exp(s_past - top), jnp.exp(s_own - top)
            total = jnp.sum(e_past, axis=1, keepdims=True) + jnp.sum(e_own, axis=1, keepdims=True)
            inverse = 1.0 / total
            mixed = jnp.dot(
                (e_past * inverse).astype(LOW), v_past[0], preferred_element_type=WIDE
            ) + jnp.dot((e_own * inverse).astype(LOW), v_own[0, :keys], preferred_element_type=WIDE)
            out[0, here, cols] = mixed.astype(LOW)
            lse[0, here, h : h + 1] = top + jnp.log(total)
        rows_out = dot_cols(out[0, here], weight[...]).astype(LOW)
        put(here, rows_out)


def attend_kernel(
    heads, head_dim, scale, first, total_slots, info, q, k_past, v_past, k_own, v_own, weight, out, lse, *parts
):
    length, offset = info[first + pl.program_id(0)], info[total_slots]

    def put(here, value):
        for i, part in enumerate(parts):

            @pl.when(pl.program_id(0) == i)
            def _():
                part[here] = value

    attend_rows(heads, head_dim, scale, length, offset, q, k_past, v_past, k_own, v_own, weight, out, lse, put)


def attend_forward(info, q, k_past, v_past, k_own, v_own, weight, heads, head_dim, scale, first, count):
    _, length, width = q.shape
    past = k_past.shape[1]
    by_slot = lambda *shape: pl.BlockSpec((1, *shape), lambda s, info: (first + s,) + (0,) * len(shape))
    out_slot = lambda *shape: pl.BlockSpec((1, *shape), lambda s, info: (s,) + (0,) * len(shape))
    keys = count * length * (past + length) * heads
    return pl.pallas_call(
        functools.partial(attend_kernel, heads, head_dim, scale, first, q.shape[0]),
        grid_spec=pltpu.PrefetchScalarGridSpec(
            num_scalar_prefetch=1,
            grid=(count,),
            in_specs=[
                by_slot(length, width),
                by_slot(past, head_dim),
                by_slot(past, head_dim),
                by_slot(length, head_dim),
                by_slot(length, head_dim),
                whole_spec(*weight.shape, once=True),
            ],
            out_specs=[out_slot(length, width), out_slot(length, 128)]
            + [whole_spec(length, weight.shape[0])] * count,
        ),
        out_shape=[
            jax.ShapeDtypeStruct((count, length, width), LOW),
            jax.ShapeDtypeStruct((count, length, 128), WIDE),
        ]
        + [jax.ShapeDtypeStruct((length, weight.shape[0]), LOW)] * count,
        compiler_params=pltpu.CompilerParams(vmem_limit_bytes=56 << 20),
        cost_estimate=estimate(4 * keys * head_dim, 4 * count * length * width, keys),
    )(info, q, k_past, v_past, k_own, v_own, weight)


def attend_back_rows(
    heads, head_dim, scale, length, offset, q, k_past, v_past, k_own, v_own, grad, lse, cosine, sine, put,
    dk_past, dk_own, dv_past, dv_own
):
    past = k_past.shape[1]
    for start, rows in row_blocks(q.shape[1]):
        keys = start + rows
        past_bias, own_bias = key_biases(length, offset, start, rows, past, keys)
        here = slice(start, start + rows)
        cos, sin = cosine[0, here], sine[0, here]
        for h in range(heads):
            cols = slice(h * head_dim, (h + 1) * head_dim)
            query, upstream = q[0, here, cols], grad[0, here, cols]
            log_total = lse[0, here, h : h + 1]
            p_past = jnp.exp(dot_cols(query, k_past[0]) * scale + past_bias - log_total)
            p_own = jnp.exp(dot_cols(query, k_own[0, :keys]) * scale + own_bias - log_total)
            g_past = dot_cols(upstream, v_past[0])
            g_own = dot_cols(upstream, v_own[0, :keys])
            row_dot = jnp.sum(p_past * g_past, axis=1, keepdims=True) + jnp.sum(
                p_own * g_own, axis=1, keepdims=True
            )
            s_past = (p_past * (g_past - row_dot)).astype(LOW)
            s_own = (p_own * (g_own - row_dot)).astype(LOW)
            dq = (
                jnp.dot(s_past, k_past[0], preferred_element_type=WIDE)
                + jnp.dot(s_own, k_own[0, :keys], preferred_element_type=WIDE)
            ) * scale
            put(here, cols, turn_back(dq, cos, sin).astype(LOW))
            dk_past[...] += dot_rows(s_past, query)
            dk_own[:keys] += dot_rows(s_own, query)
            dv_past[...] += dot_rows(p_past.astype(LOW), upstream)
            dv_own[:keys] += dot_rows(p_own.astype(LOW), upstream)


def attend_back_kernel(
    heads,
    head_dim,
    scale,
    info,
    q,
    k_past,
    v_past,
    k_own,
    v_own,
    grad,
    lse,
    cosine,
    sine,
    dq_out,
    mine_past,
    mine_own,
    other_past,
    other_own,
    dk_past,
    dk_own,
    dv_past,
    dv_own,
):
    slot = pl.program_id(0)
    length, offset = info[slot], info[pl.num_programs(0)]
    parity = info[pl.num_programs(0) + 1]
    for total in (dk_past, dk_own, dv_past, dv_own):
        total[...] = jnp.zeros_like(total)
    attend_back_rows(
        heads, head_dim, scale, length, offset, q, k_past, v_past, k_own, v_own, grad, lse, cosine, sine,
        lambda here, cols, value: dq_out.__setitem__((0, here, cols), value),
        dk_past, dk_own, dv_past, dv_own,
    )

    @pl.when(parity == 0)
    def _():
        mine_past[0] = dk_past[...] * scale
        mine_own[0] = dk_own[...] * scale
        other_past[0] = dv_past[...]
        other_own[0] = dv_own[...]

    @pl.when(parity != 0)
    def _():
        mine_past[0] = dv_past[...]
        mine_own[0] = dv_own[...]
        other_past[0] = dk_past[...] * scale
        other_own[0] = dk_own[...] * scale


def attend_backward(
    info, q, k_past, v_past, k_own, v_own, grad, lse, cosine, sine, heads, head_dim, scale
):
    count, length, width = q.shape
    past = k_past.shape[1]
    by_slot = lambda *shape: pl.BlockSpec((1, *shape), lambda s, info: (s,) + (0,) * len(shape))
    keys = count * length * (past + length) * heads
    return pl.pallas_call(
        functools.partial(attend_back_kernel, heads, head_dim, scale),
        grid_spec=pltpu.PrefetchScalarGridSpec(
            num_scalar_prefetch=1,
            grid=(count,),
            in_specs=[
                by_slot(length, width),
                by_slot(past, head_dim),
                by_slot(past, head_dim),
                by_slot(length, head_dim),
                by_slot(length, head_dim),
                by_slot(length, width),
                by_slot(length, 128),
                by_slot(length, head_dim),
                by_slot(length, head_dim),
            ],
            out_specs=[
                by_slot(length, width),
                by_slot(past, head_dim),
                by_slot(length, head_dim),
                by_slot(past, head_dim),
                by_slot(length, head_dim),
            ],
            scratch_shapes=[
                pltpu.VMEM((past, head_dim), WIDE),
                pltpu.VMEM((length, head_dim), WIDE),
                pltpu.VMEM((past, head_dim), WIDE),
                pltpu.VMEM((length, head_dim), WIDE),
            ],
        ),
        out_shape=[
            jax.ShapeDtypeStruct((count, length, width), LOW),
            jax.ShapeDtypeStruct((count, past, head_dim), WIDE),
            jax.ShapeDtypeStruct((count, length, head_dim), WIDE),
            jax.ShapeDtypeStruct((count, past, head_dim), WIDE),
            jax.ShapeDtypeStruct((count, length, head_dim), WIDE),
        ],
        compiler_params=pltpu.CompilerParams(vmem_limit_bytes=56 << 20),
        cost_estimate=estimate(10 * keys * head_dim, 8 * count * length * width, keys),
    )(info, q, k_past, v_past, k_own, v_own, grad, lse, cosine, sine)


def attend_sum_kernel(
    heads, head_dim, scale, slots, info, q, k_past, v_past, k_own, v_own, weight, own_in, gain, out, lse, middle,
    normed, parts, core_in, far_in, send, recv
):
    step = pl.program_id(0)
    slot = slots - 1 - step
    core, far, _ = partners_of()
    remote = remote_copy(send, recv)
    cores = [remote(parts.at[3 - 2 * k], core_in.at[k], k, core) for k in range(2)]
    to_far = remote(parts.at[2], far_in, 2, far)

    @pl.when(step == 0)
    def _():
        meet((core, far))

    def put(here, value):
        parts[slot, here] = value

    offset = lax.axis_index("ctx") * q.shape[1]
    attend_rows(
        heads, head_dim, scale, info[slot], offset, q, k_past, v_past, k_own, v_own, weight, out, lse, put
    )
    for k in range(2):
        pl.when(step == 2 * k)(cores[k].start)

    @pl.when(step == 1)
    def _():
        cores[0].wait_recv()
        parts[2] = (parts[2].astype(WIDE) + core_in[0].astype(WIDE)).astype(LOW)
        to_far.start()

    @pl.when(step == slots - 1)
    def _():
        cores[1].wait_recv()
        to_far.wait_recv()
        rows = own_in[...].astype(WIDE) + parts[0].astype(WIDE)
        rows = rows + core_in[1].astype(WIDE) + far_in[...].astype(WIDE)
        middle[...] = rows
        inverse = lax.rsqrt(jnp.mean(rows * rows, axis=-1, keepdims=True) + EPS)
        normed[...] = (rows * inverse * gain[...]).astype(LOW)
        for copy in (*cores, to_far):
            copy.wait_send()


def attend_sum(info, q, k_past, v_past, k_own, v_own, weight, own_in, gain, heads, head_dim, scale):
    count, length, width = q.shape
    past, model_width = k_past.shape[1], own_in.shape[1]
    by_slot = lambda *shape: pl.BlockSpec(
        (1, *shape), lambda i, info: (count - 1 - i,) + (0,) * len(shape)
    )
    keys = count * length * (past + length) * heads
    return pl.pallas_call(
        functools.partial(attend_sum_kernel, heads, head_dim, scale, count),
        grid_spec=pltpu.PrefetchScalarGridSpec(
            num_scalar_prefetch=1,
            grid=(count,),
            in_specs=[
                by_slot(length, width),
                by_slot(past, head_dim),
                by_slot(past, head_dim),
                by_slot(length, head_dim),
                by_slot(length, head_dim),
                whole_spec(*weight.shape, once=True),
                whole_spec(length, model_width, once=True),
                whole_spec(1, model_width),
            ],
            out_specs=[
                by_slot(length, width),
                by_slot(length, 128),
                whole_spec(length, model_width, once=True),
                whole_spec(length, model_width, once=True),
            ],
            scratch_shapes=[
                pltpu.VMEM((count, length, model_width), LOW),
                pltpu.VMEM((2, length, model_width), LOW),
                pltpu.VMEM((length, model_width), LOW),
                pltpu.SemaphoreType.DMA((3,)),
                pltpu.SemaphoreType.DMA((3,)),
            ],
        ),
        out_shape=[
            jax.ShapeDtypeStruct((count, length, width), LOW),
            jax.ShapeDtypeStruct((count, length, 128), WIDE),
            jax.ShapeDtypeStruct((length, model_width), WIDE),
            jax.ShapeDtypeStruct((length, model_width), LOW),
        ],
        compiler_params=pltpu.CompilerParams(
            vmem_limit_bytes=56 << 20, collective_id=5, has_side_effects=True
        ),
        cost_estimate=estimate(4 * keys * head_dim, 4 * count * length * width, keys),
    )(info, q, k_past, v_past, k_own, v_own, weight, own_in, gain)


def exchange_kernel(
    heads, head_dim, scale, slots, tiles, info, q, k_past, v_past, k_own, v_own, rows, weight, lse, cosine, sine,
    cosine_all, sine_all, branch, mixed, mlp_far, mlp_side, mlp_own, middle, line, out_grad, block, mine_past,
    mine_own, other_past, other_own, got_past, got_own, side_out, side_in, dk_past, dk_own, dv_past, dv_own,
    own_rows, last_in, grad, send, recv, load
):
    step = pl.program_id(0)
    tensor_rank = lax.axis_index("tp")
    core, far, side = partners_of()
    parity = lax.rem(tensor_rank, 2)
    offset = lax.axis_index("ctx") * q.shape[1]
    remote = remote_copy(send, recv)
    pasts = [remote(other_past.at[r], got_past.at[r ^ 1], r, core) for r in range(slots)]
    owns = [remote(other_own.at[r], got_own.at[r ^ 1], slots + r, core) for r in range(slots)]
    sides = [remote(side_out.at[r], side_in.at[r], 2 * slots + r, side) for r in range(slots)]
    lasts = [
        remote(mlp_far, last_in.at[0], 3 * slots, far),
        remote(mlp_side, last_in.at[1], 3 * slots + 1, side),
    ]
    loading = pltpu.make_async_copy(mlp_own, own_rows, load)

    @pl.when(step == 0)
    def _():
        loading.start()
        meet((core, far, side))
        for copy in lasts:
            copy.start()

    @pl.when(step < slots)
    def _():
        length = info[jnp.minimum(step, slots - 1)]
        for total in (dk_past, dk_own, dv_past, dv_own):
            total[...] = jnp.zeros_like(total)
        grad[0] = jnp.dot(rows[...], weight[...], preferred_element_type=WIDE).astype(LOW)
        attend_back_rows(
            heads, head_dim, scale, length, offset, q, k_past, v_past, k_own, v_own, grad, lse, cosine,
            sine, lambda here, cols, value: line.__setitem__((step, here, cols), value),
            dk_past, dk_own, dv_past, dv_own,
        )

        @pl.when(parity == 0)
        def _():
            mine_past[step] = dk_past[...] * scale
            mine_own[step] = dk_own[...] * scale
            other_past[step] = dv_past[...]
            other_own[step] = dv_own[...]

        @pl.when(parity != 0)
        def _():
            mine_past[step] = dv_past[...]
            mine_own[step] = dv_own[...]
            other_past[step] = dk_past[...] * scale
            other_own[step] = dk_own[...] * scale

    for r in range(slots):

        def start(r=r):
            pasts[r].start()
            owns[r].start()

        pl.when(step == r)(start)

    for pair in range(0, slots, 2):

        def merge(pair=pair):
            for r in (pair, pair + 1):
                pasts[r ^ 1].wait_recv()
                side_out[r] = (mine_past[r] + got_past[r]).astype(LOW)
                sides[r].start()

        pl.when(step == pair + 1)(merge)

    @pl.when(step >= slots)
    def _():
        out_grad[...] = dot_rows(branch[...], mixed[...]).astype(LOW)

    @pl.when(step == slots + tiles - 1)
    def _():
        for r in range(slots):
            owns[r ^ 1].wait_recv()
            sides[r].wait_recv()
            total = mine_own[r] + got_own[r] + side_in[r].astype(WIDE)
            back = turn_back(total, cosine_all[r], sine_all[r])
            line[r, :, heads * head_dim :] = jnp.where(parity == 0, back, total).astype(LOW)
        loading.wait()
        for copy in lasts:
            copy.wait_recv()
        block[...] = (
            middle[...] + own_rows[...].astype(WIDE) + last_in[0].astype(WIDE) + last_in[1].astype(WIDE)
        ).astype(LOW)
        for copy in (*pasts, *owns, *sides, *lasts):
            copy.wait_send()


def attend_exchange(
    info, q, k_past, v_past, k_own, v_own, weight, lse, cosine, sine, heads, head_dim, scale, branch, mixed, mlp,
    middle
):
    count, length, width = q.shape
    past = k_past.shape[1]
    tokens, model_width = branch.shape
    tile = 256
    tiles = model_width // tile
    slot = lambda i: jnp.minimum(i, count - 1)
    by_slot = lambda *shape: pl.BlockSpec((1, *shape), lambda i, info: (slot(i),) + (0,) * len(shape))
    column = lambda i: jnp.clip(i - count, 0, tiles - 1)
    held = lambda *shape: pl.BlockSpec(
        shape, lambda i, info: (0,) * len(shape), pipeline_mode=pl.Buffered(1)
    )
    line_cols = width + head_dim
    return pl.pallas_call(
        functools.partial(exchange_kernel, heads, head_dim, scale, count, tiles),
        grid_spec=pltpu.PrefetchScalarGridSpec(
            num_scalar_prefetch=1,
            grid=(count + tiles,),
            in_specs=[
                by_slot(length, width),
                by_slot(past, head_dim),
                by_slot(past, head_dim),
                by_slot(length, head_dim),
                by_slot(length, head_dim),
                pl.BlockSpec((length, model_width), lambda i, info: (slot(i), 0)),
                held(*weight.shape),
                by_slot(length, 128),
                by_slot(length, head_dim),
                by_slot(length, head_dim),
                held(count, length, head_dim),
                held(count, length, head_dim),
                pl.BlockSpec((tokens, tile), lambda i, info: (0, column(i))),
                held(*mixed.shape),
            ]
            + [ANYWHERE] * 3
            + [held(length, model_width)],
            out_specs=[
                held(count, length, line_cols),
                pl.BlockSpec((tile, width), lambda i, info: (column(i), 0)),
                held(length, model_width),
            ],
            scratch_shapes=[pltpu.VMEM((count, length, head_dim), WIDE)] * 6
            + [pltpu.VMEM((count, length, head_dim), LOW)] * 2
            + [pltpu.VMEM((length, head_dim), WIDE)] * 4
            + [
                pltpu.VMEM((length, model_width), LOW),
                pltpu.VMEM((2, length, model_width), LOW),
                pltpu.VMEM((1, length, width), LOW),
                pltpu.SemaphoreType.DMA((3 * count + 2,)),
                pltpu.SemaphoreType.DMA((3 * count + 2,)),
                pltpu.SemaphoreType.DMA,
            ],
        ),
        out_shape=[
            jax.ShapeDtypeStruct((count, length, line_cols), LOW),
            jax.ShapeDtypeStruct((model_width, width), LOW),
            jax.ShapeDtypeStruct((length, model_width), LOW),
        ],
        compiler_params=pltpu.CompilerParams(
            vmem_limit_bytes=63 << 20, collective_id=4, has_side_effects=True
        ),
        cost_estimate=estimate(2 * tokens * model_width * width, 10 * tokens * width),
    )(info, q, k_past, v_past, k_own, v_own, branch, weight, lse, cosine, sine, cosine, sine, branch, mixed, *mlp, middle)


def local(
    hidden_in,
    cotangent,
    seq_lengths,
    positions,
    permutation,
    query_weight,
    keyval_weight,
    output_weight,
    norm_gains,
    bias_query,
    bias_keyval,
    gate_weight,
    up_weight,
    down_weight,
):
    group_rank = lax.axis_index("fsdp")
    ctx_rank = lax.axis_index("ctx")
    tensor_rank = lax.axis_index("tp")
    fsdp_count = lax.axis_size("fsdp")
    ctx_count = lax.axis_size("ctx")
    tensor_count = lax.axis_size("tp")
    seq_grp, local_len, model_width = hidden_in.shape
    heads, head_dim = bias_query.shape
    keyval_heads = bias_keyval.shape[0] // 2
    assert seq_grp == tensor_count == fsdp_count == len(DEAL_SHIFT)
    token_count = seq_grp * local_len
    scale = 1.0 / math.sqrt(head_dim)
    offset = ctx_rank * local_len
    head_pair = tensor_rank // (tensor_count // keyval_heads)
    parity = tensor_rank % 2
    assert DEAL_SHIFT == tuple((t % 2) * 2 + t // 2 for t in range(tensor_count))

    entry = jnp.arange(permutation.shape[0])
    entry_group, entry_slot = entry // seq_grp, entry % seq_grp
    home_group, home_slot = lax.div(permutation, seq_grp), lax.rem(permutation, seq_grp)
    places = jnp.arange(2 * seq_grp)
    near_places = places < seq_grp
    slot_rank = tensor_rank ^ (places % seq_grp)
    shift_of = lambda rank: lax.rem(rank, 2) * 2 + lax.div(rank, 2)
    target = lax.rem(group_rank + shift_of(tensor_rank), fsdp_count)
    leaving = jnp.sum(jnp.where((entry_group == target) & (home_group == group_rank), home_slot, 0))
    source = lax.rem(group_rank + fsdp_count - shift_of(slot_rank), fsdp_count)
    hit = (entry_group == group_rank)[None] & (home_group[None] == source[:, None])
    slot_now = jnp.sum(jnp.where(hit, entry_slot[None], 0), axis=1)
    seq_now = jnp.sum(jnp.where(hit, permutation[None], 0), axis=1)
    targets = lax.rem(group_rank + shift_of(slot_rank), fsdp_count)
    back_hit = (entry_group[None] == targets[:, None]) & (home_group == group_rank)[None]
    home_order = jnp.sum(jnp.where(back_hit, home_slot[None], 0), axis=1)[:seq_grp]
    there = [
        (f * tensor_count + t, (f + DEAL_SHIFT[t]) % fsdp_count * tensor_count + t)
        for f in range(fsdp_count)
        for t in range(tensor_count)
    ]
    back = [(target, source) for source, target in there]

    split = units_split()
    head_width = 2 * head_dim
    query_cols = heads * head_dim
    near_cols = query_cols + head_width + 128

    outgoing = lax.dynamic_index_in_dim(hidden_in, leaving, 0, keepdims=False)
    own_in = lax.ppermute(outgoing, ("fsdp", "tp"), there)
    small = jnp.concatenate(
        [
            query_weight,
            lax.dynamic_slice_in_dim(keyval_weight, head_pair * head_width, head_width, axis=1),
            jnp.pad(norm_gains.T, ((0, 0), (0, 128 - norm_gains.shape[0]))),
            output_weight.T,
        ],
        axis=1,
    )
    seq_hit = seq_now[:, None] == entry[None]
    lengths_now = jnp.sum(jnp.where(seq_hit, seq_lengths[None], 0), axis=1)
    more = jnp.where(places == seq_grp, offset, jnp.where(places == seq_grp + 1, parity, 0))
    info = jnp.where(near_places, lengths_now, more).astype(jnp.int32)
    positions_now = jnp.sum(
        jnp.where(seq_hit[:seq_grp, :, None], positions[None], 0), axis=1
    )
    lane = jnp.arange(head_dim)
    frequency = 1.0 / ROPE_BASE ** ((lane % (head_dim // 2)).astype(WIDE) * 2.0 / head_dim)
    angles = positions_now.astype(WIDE)[..., None] * frequency
    cosine = jnp.cos(angles)
    sine = jnp.sin(angles) * jnp.where(lane < head_dim // 2, -1.0, 1.0)
    pick_info = jnp.where(near_places, slot_now, slot_now ^ tensor_rank).astype(jnp.int32)
    units = gate_weight.shape[1]
    units_pad = -(-units // 256) * 256
    widen = lambda w: jnp.pad(w, ((0, 0), (0, units_pad - units)))
    shards = [widen(w) for w in (down_weight.T, gate_weight, up_weight)]
    if split:
        half_units = units_pad // 2
        cut = lambda w, c: lax.dynamic_slice_in_dim(w, c * half_units, half_units, axis=1)

        def in_order(own, other):
            return jnp.stack(
                [jnp.where(ctx_rank == 0, own, other), jnp.where(ctx_rank == 0, other, own)]
            )

        def all_rows(both, *earlier):
            full = lax.all_gather(after(both, *earlier), "fsdp", axis=0, tiled=False)
            return full.reshape(-1, both.shape[-1])

        first_units = half_units - half_units // 2 // 256 * 256
        first_cols = 3 * first_units

        def in_parts(c):
            halves = [cut(w, c) for w in shards]
            return jnp.concatenate(
                [w[:, :first_units] for w in halves] + [w[:, first_units:] for w in halves], axis=1
            )

        leaving_units, own_units = in_parts(1 - ctx_rank), in_parts(ctx_rank)
        slot_pick = lax.dynamic_index_in_dim(cotangent, tensor_rank, 0, keepdims=False)
        small = after(small, outgoing, leaving_units, cosine, sine, slot_pick)
        small_both = in_order(small, from_partner(small, "ctx", 1))
        arriving_units = from_partner(after(leaving_units, small_both), "ctx", 1)
        other_own = from_partner(after(slot_pick, arriving_units), "ctx", 1)
        both_a = in_order(own_units[:, :first_cols], arriving_units[:, :first_cols])
        both_b = in_order(own_units[:, first_cols:], arriving_units[:, first_cols:])
    else:
        all_rows = lambda shard, *earlier: lax.all_gather(
            shard, ("fsdp", "ctx"), axis=0, tiled=True
        )
        small_both, unit_both, half_units = small, jnp.concatenate(shards, axis=1), units_pad
    far_in = from_partner(own_in, "tp", 2)
    near_in = from_partner(own_in, "tp", 1)
    ready = (info, pick_info, own_units, home_order) if split else (cosine, sine, info)
    cross_in = from_partner(after(far_in, *ready), "tp", 1)

    near_full = all_rows(small_both, own_in)
    if split:
        units_a = all_rows(both_a, cross_in)
        units_b = all_rows(both_b, cross_in)
    else:
        down_full = all_rows(unit_both[..., :half_units], cross_in)
        gate_up_full = all_rows(unit_both[..., half_units:], cross_in)
    project_full = near_full[:, : query_cols + head_width]
    output_full = near_full[:, near_cols:]
    bias_head = lax.dynamic_slice_in_dim(bias_keyval, head_pair * 2, 2, axis=0)
    bias_row = jnp.concatenate([bias_query.reshape(1, -1), bias_head.reshape(1, -1)], axis=1).astype(WIDE)
    normed_one, query_rot, key_own, value_own = project(
        (own_in, near_in, far_in, cross_in),
        near_full,
        bias_row,
        after(cosine, other_own, both_a, both_b, info, pick_info) if split else cosine,
        sine,
        heads,
        head_dim,
    )
    gains_now = near_full[:, query_cols + head_width : near_cols][:, :2].astype(WIDE).T
    if split:
        key_past, value_past = lax.ppermute((key_own, value_own), "ctx", [(0, 1)])
        other_far = from_partner(other_own, "tp", 2)
        other_near = from_partner(after(other_own, key_past), "tp", 1)
        other_cross = from_partner(after(other_far, key_past), "tp", 1)
        other_rows = (other_own, other_near, other_far, other_cross)
        key_past = after(key_past, other_far)
    else:
        key_past = lax.all_gather(key_own, "ctx", axis=1, tiled=True)
        value_past = lax.all_gather(value_own, "ctx", axis=1, tiled=True)
    own_weight = lax.dynamic_slice_in_dim(
        project_full, query_cols + parity * head_dim, head_dim, axis=1
    )
    back_full = jnp.concatenate([project_full[:, :query_cols], own_weight], axis=1)
    in_share = own_in.astype(WIDE)
    if split:
        mixed, lse, middle_share, normed_share = attend_sum(
            info,
            query_rot,
            key_past,
            value_past,
            key_own,
            value_own,
            after(output_full, back_full),
            own_in,
            gains_now[1:2],
            heads,
            head_dim,
            scale,
        )
    else:
        attend = lambda first, *held: attend_forward(
            info, query_rot, *held, key_own, value_own, output_full, heads, head_dim, scale, first, 2
        )

        mixed_far, lse_far, *attn_far = attend(2, key_past, value_past)
        attn_wide = collect_far(attn_far[0], attn_far[1])
        attn_got = from_partner(attn_wide, "tp", 2)
        mixed_near, lse_near, *attn_near = attend(0, after(key_past, attn_wide), value_past)
        attn_core = from_partner(attn_near[1], "tp", 1)
        middle_share = (
            in_share
            + attn_near[0].astype(WIDE)
            + attn_core.astype(WIDE)
            + attn_got.astype(WIDE)
        )
        inv_two = lax.rsqrt(jnp.mean(middle_share * middle_share, axis=-1, keepdims=True) + EPS)
        normed_share = (middle_share * inv_two * gains_now[1]).astype(LOW)
        mixed = jnp.concatenate([mixed_near, mixed_far], axis=0)
        lse = jnp.concatenate([lse_near, lse_far], axis=0)
    half_len = local_len // 2

    if split:
        grad_hidden, grad_rows = chosen_rows(
            pick_info,
            after(cotangent, normed_share),
            other_rows,
            units_a,
            0,
            3,
        )
    else:
        grad_slots = [
            lax.dynamic_index_in_dim(cotangent, slot_now[r], 0, keepdims=False) for r in range(seq_grp)
        ]
        grad_hidden, grad_rows = stack_rows([(g,) for g in grad_slots], down_full, 0, 1)

    def spread_all(own):
        far = from_partner(own, "tp", 2)
        near = from_partner(own, "tp", 1)
        if not split:
            return (own, near, far, from_partner(far, "tp", 1))
        side = from_partner(own, "ctx", 1)
        held = after(far, grad_hidden), after(side, grad_hidden)
        across = from_partner(held[0][:half_len], "ctx", 1), from_partner(held[1][half_len:], "tp", 2)
        cores = [from_partner(v, "tp", 1) for v in held]
        return (own, near, far, cores[0], side, cores[1], *across)

    def in_slots(rows):
        if not split:
            return [(row,) for row in rows]
        return [(row,) for row in rows[:6]] + [rows[6:]]

    mixed_flat = mixed.reshape(token_count, query_cols)
    normed_slots = in_slots(spread_all(normed_share))
    if split:
        ahead = stack_rows(normed_slots[:6], units_a, 1, 3, total=8)
        last = [normed_slots[6], tuple(from_partner(after(v, ahead[0]), "tp", 1) for v in normed_slots[6])]
        gate_lin, normed_two = stack_rows(last, units_a, 1, 3, into=ahead, first=6, total=8)
        hidden_a, gate_a, up_a = hidden_units(normed_two, units_a, 2, 3, gate_lin, grad_hidden)
        grad_a = first_grads(grad_rows, normed_two, hidden_a, gate_a, up_a)
        hidden_b, gate_b, up_b = full_units(after(normed_two, grad_a), grad_rows, units_b)
    else:
        gate_lin, normed_two = stack_rows(normed_slots, gate_up_full, 0, 2)
        hidden_act, grad_gate, grad_up = hidden_units(
            normed_two, gate_up_full, 1, 2, gate_lin, grad_hidden
        )

    def collect_all(lefts, weights, *earlier):
        lefts = list(lefts)
        lefts[0] = after(lefts[0], *earlier)
        last = back_rows(lefts, weights, 2, 2, local_len)
        got = [from_partner(collect_far(last[0], last[1]), "tp", 2)]
        first = back_rows(lefts, weights, 0, 2, local_len)
        got.append(from_partner(first[1], "tp", 1))

        def finish():
            return sum((v.astype(WIDE) for v in got), first[0].astype(WIDE))

        return first[0], finish

    if split:
        grad_two_share, down_b, up_grad_b = collect_back(
            (gate_a, up_a),
            (gate_b, up_b),
            units_a,
            units_b,
            grad_rows,
            normed_two,
            hidden_b,
            local_len,
        )
        grad_middle, gain_two, gate_grad_b, grad_branch, *mlp = spread_branch(
            grad_two_share,
            middle_share,
            grad_rows,
            gains_now[1:2],
            hidden_a,
            hidden_b,
            units_a,
            units_b,
            normed_two,
            gate_b,
        )
        mlp_own, mlp_far, mlp_side = mlp
        grad_branch = grad_branch.reshape(token_count, model_width)
    else:
        first_back, finish_back = collect_all(
            (grad_gate, grad_up), ((gate_up_full, 0, 2), (gate_up_full, 1, 2))
        )
        down_grad = contract_rows(after(grad_rows, first_back), hidden_act, LOW)
        gate_grad = contract_rows(normed_two, after(grad_gate, down_grad), LOW)
        grad_two_share = finish_back()
        grad_norm_two, gain_two = norm_backward(
            middle_share, inv_two, gains_now[1], grad_two_share
        )
        grad_middle = grad_slots[0].astype(WIDE) + grad_norm_two
        branch_own = grad_middle.astype(LOW)
        branch_far = from_partner(branch_own, "tp", 2)
        branch_near = from_partner(branch_own, "tp", 1)
        branch_cross = from_partner(branch_far, "tp", 1)
        grad_branch = jnp.concatenate([branch_own, branch_near, branch_far, branch_cross], axis=0)
        up_grad = contract_rows(normed_two, after(grad_up, branch_own), LOW)

    grad_mixed = None if split else product(grad_branch, output_full, LOW)
    attend_args = (
        info,
        query_rot,
        key_past,
        value_past,
        key_own,
        value_own,
        output_full if split else grad_mixed.reshape(seq_grp, local_len, query_cols),
        lse,
        cosine,
        sine,
        heads,
        head_dim,
        scale,
    )
    if split:
        line_grad, output_grad, block_share = attend_exchange(
            *attend_args,
            grad_branch,
            mixed_flat,
            (mlp_far, mlp_side, mlp_own),
            middle_share,
        )
        line_grad = line_grad.reshape(token_count, -1)
    else:
        grad_query, mine_past, mine_own, other_past, other_own = attend_backward(*attend_args)
        swap = lambda value: jnp.stack([value[r ^ 1] for r in range(seq_grp)])
        got_past, got_own = from_partner((other_past, other_own), "tp", 1)
        past_sum = mine_past + swap(got_past)
        own_sum = mine_own + swap(got_own)
        own_sum = own_sum + lax.psum_scatter(past_sum, "ctx", scatter_dimension=1, tiled=True)
        half_lanes = head_dim // 2
        turned = own_sum * cosine - jnp.roll(own_sum, half_lanes, axis=-1) * sine
        own_grad = jnp.where(parity == 0, turned, own_sum).astype(LOW).reshape(token_count, head_dim)
        line_grad = jnp.concatenate([grad_query.reshape(token_count, query_cols), own_grad], axis=1)
    def scatter_units(grad):
        if not split:
            return scatter_sum(grad, ctx_rank, LOW)
        return lax.psum_scatter(grad, "fsdp", scatter_dimension=0, tiled=True)

    unit_grads = (grad_a, down_b, up_grad_b, gate_grad_b) if split else (down_grad, gate_grad, up_grad)
    unit_sums = [scatter_units(unit_grads[0])]
    if split:
        unit_sums += [scatter_units(after(g, unit_sums[0])) for g in unit_grads[1:3]]
        unit_sums += [scatter_units(after(unit_grads[3], unit_sums[0]))]
    else:
        unit_sums += [scatter_units(g) for g in unit_grads[1:]]

    normed_flat = normed_one.reshape(token_count, model_width)
    if split:
        input_share, gain_grad, attn_grad, bias_grad, block_home, *unit_gots = finish_rows(
            line_grad,
            back_full,
            own_in,
            grad_middle,
            gains_now[0:1],
            gain_two,
            normed_flat,
            block_share,
            unit_sums,
        )
        attn_grad = jnp.concatenate([attn_grad, output_grad], axis=1)
    else:
        half = token_count // 2
        line_far = contract_cols(line_grad[half:], back_full, LOW).reshape(2, local_len, model_width)
        line_near = contract_cols(line_grad[:half], back_full, LOW).reshape(2, local_len, model_width)
        line_wide = collect_far(line_far[0], line_far[1])
        line_got = from_partner(line_wide, "tp", 2)
        line_core = from_partner(line_near[1], "tp", 1)
        first_mlp, finish_mlp = collect_all((hidden_act,), ((down_full, 0, 1),), up_grad, branch_far)
        block_share = (middle_share + finish_mlp()).astype(LOW)
        grad_one_share = line_near[0].astype(WIDE) + line_core.astype(WIDE) + line_got.astype(WIDE)
        inv_one = lax.rsqrt(jnp.mean(in_share * in_share, axis=-1, keepdims=True) + EPS)
        grad_norm_one, gain_one = norm_backward(in_share, inv_one, gains_now[0], grad_one_share)
        input_share = (grad_middle + grad_norm_one).astype(LOW)
        attn_grad = jnp.concatenate(
            [contract_rows(normed_flat, line_grad, LOW), contract_rows(grad_branch, mixed_flat, LOW)],
            axis=1,
        )
        bias_grad = jnp.sum(line_grad.astype(WIDE), axis=0)

    shard_count = fsdp_count * ctx_count
    share = head_dim // shard_count
    if not split:
        gain_grad = jnp.concatenate([gain_one, gain_two], axis=0)
        gain_grad = gain_grad + from_partner(gain_grad, "tp", 1)
        gain_grad = gain_grad + from_partner(gain_grad, "tp", 2)
    bias_cols = jnp.transpose(bias_grad.reshape(heads + 1, shard_count, share), (1, 2, 0))
    bias_cols = jnp.pad(bias_cols, ((0, 0), (0, (model_width - head_dim) // shard_count), (0, 0)))
    tiny = jnp.concatenate([gain_grad.T, bias_cols.reshape(model_width, heads + 1)], axis=1)
    tiny = jnp.pad(tiny, ((0, 0), (0, 128 - tiny.shape[1]))).astype(LOW)
    attn_grad = jnp.concatenate([attn_grad, tiny], axis=1)
    if split:
        attn_blocks = attn_grad.reshape(fsdp_count, ctx_count, -1, attn_grad.shape[1])
        kept, sent = scatter_ctx(attn_blocks, ctx_rank)
        attn_held = (kept.astype(WIDE) + from_partner(sent, "ctx", 1).astype(WIDE)).astype(LOW)
        attn_held = attn_held.reshape(-1, attn_grad.shape[1])
        attn_end = lax.psum_scatter(after(attn_held, *unit_sums), "fsdp", scatter_dimension=0, tiled=True)
    else:
        attn_end = scatter_sum(attn_grad, ctx_rank, LOW, *unit_sums)


    def leave(share):
        return lax.ppermute(share, ("fsdp", "tp"), back)

    def arrive(own, *earlier):
        far = from_partner(own, "tp", 2)
        near = from_partner(own, "tp", 1)
        return (own, near, far, from_partner(after(far, *earlier), "tp", 1))

    input_home = leave(input_share)
    if not split:
        block_home = leave(block_share)
    block_out = place_rows(arrive(block_home), home_order)
    if split:
        input_home = after(input_home, attn_held)
        input_rows = arrive(input_home, block_out)
    else:
        input_rows = arrive(input_home)
    input_grad = place_rows(input_rows, home_order)

    small_at = query_cols + head_dim + query_cols
    tiny_grad = attn_end[:, small_at:].astype(WIDE)

    if split:

        def own_half(total):
            rows = total.shape[0] // 2
            return lax.dynamic_slice_in_dim(total, ctx_rank * rows, rows, axis=0)

        (own_a, got_a), *ends = [(own_half(t), got) for t, got in zip(unit_sums, unit_gots)]

        def joined(part, end):
            cols = slice(part * first_units, (part + 1) * first_units)
            own = jnp.concatenate([own_a[:, cols], end[0]], axis=1)
            got = jnp.concatenate([got_a[:, cols], end[1]], axis=1)
            first, second = jnp.where(ctx_rank == 0, own, got), jnp.where(ctx_rank == 0, got, own)
            return jnp.concatenate([first, second], axis=1)[:, :units].astype(WIDE)

        down_end, gate_end, up_end = joined(0, ends[0]), joined(1, ends[2]), joined(2, ends[1])
    else:
        down_end, gate_end, up_end = (t[:, :units].astype(WIDE) for t in unit_sums)
    return (
        block_out,
        input_grad,
        attn_end[:, :query_cols].astype(WIDE),
        attn_end[:, query_cols : query_cols + head_dim].astype(WIDE),
        attn_end[:, query_cols + head_dim : small_at].astype(WIDE).T,
        tiny_grad[:, :2].T,
        tiny_grad[:share, 2 : 2 + heads].T,
        tiny_grad[:share, 2 + heads : 3 + heads].T,
        gate_end,
        up_end,
        down_end.T,
    )


def solution(mesh):
    placed = (
        P("fsdp", "ctx", None),
        P("fsdp", "ctx", None),
        P(),
        P(None, "ctx"),
        P(),
        P(("fsdp", "ctx"), "tp"),
        P(("fsdp", "ctx"), None),
        P("tp", ("fsdp", "ctx")),
        P(None, ("fsdp", "ctx")),
        P("tp", None),
        P(),
        P(("fsdp", "ctx"), "tp"),
        P(("fsdp", "ctx"), "tp"),
        P("tp", ("fsdp", "ctx")),
    )
    return jax.shard_map(
        local,
        mesh=mesh,
        in_specs=placed,
        out_specs=(
            P("fsdp", "ctx", None),
            P("fsdp", "ctx", None),
            P(("fsdp", "ctx"), "tp"),
            P(("fsdp", "ctx"), "tp"),
            P("tp", ("fsdp", "ctx")),
            P(None, ("fsdp", "ctx")),
            P("tp", ("fsdp", "ctx")),
            P("tp", ("fsdp", "ctx")),
            P(("fsdp", "ctx"), "tp"),
            P(("fsdp", "ctx"), "tp"),
            P("tp", ("fsdp", "ctx")),
        ),
        check_vma=False,
    )
```

```python
import functools
import math

import jax
import jax.numpy as jnp
from jax import lax
from jax.experimental import pallas as pl
from jax.experimental.pallas import tpu as pltpu
from jax.sharding import PartitionSpec as P

EPS = 1e-06
ROPE_BASE = 10000.0
NEG_FILL = -1e30
LOW = jnp.bfloat16
WIDE = jnp.float32
DEAL_SHIFT = (0, 2, 1, 3)


def from_partner(value, axis, apart):
    pairs = [(source, source ^ apart) for source in range(lax.axis_size(axis))]
    return lax.ppermute(value, axis, pairs)


def product(left_side, right_side, kind=WIDE):
    return jnp.dot(left_side, right_side, preferred_element_type=WIDE).astype(kind)


def contract_rows(left_side, right_side, kind=WIDE):
    return lax.dot_general(
        left_side, right_side, (((0,), (0,)), ((), ())), preferred_element_type=WIDE
    ).astype(kind)


def contract_cols(left_side, right_side, kind=WIDE):
    return lax.dot_general(
        left_side, right_side, (((1,), (1,)), ((), ())), preferred_element_type=WIDE
    ).astype(kind)


def norm_backward(values, scale_inv, gain_row, upstream):
    scaled = gain_row * upstream
    inner_mean = jnp.mean(values * scaled, axis=-1, keepdims=True)
    grad_in = scale_inv * scaled - values * (scale_inv * scale_inv * scale_inv) * inner_mean
    gain_grad = jnp.sum(upstream * values * scale_inv, axis=0, keepdims=True)
    return (grad_in, gain_grad)


def after(value, *earlier):
    return lax.optimization_barrier((value, *earlier))[0]


def collect_far(far_part, cross_part):
    wide = far_part.astype(WIDE) + from_partner(cross_part, "tp", 1).astype(WIDE)
    return wide.astype(LOW)


def units_split():
    return lax.axis_size("ctx") == 2


def all_rows(shard):
    return lax.all_gather(shard, "fsdp", axis=0, tiled=True)


def scatter_ctx(blocks, ctx_rank):
    kept = lax.dynamic_index_in_dim(blocks, ctx_rank, 1, keepdims=False)
    sent = lax.dynamic_index_in_dim(blocks, 1 - ctx_rank, 1, keepdims=False)
    return kept, sent


def scatter_sum(grad, ctx_rank, kind, *earlier):
    fsdp_count, ctx_count = lax.axis_size("fsdp"), lax.axis_size("ctx")
    rows, cols = grad.shape
    blocks = grad.reshape(fsdp_count, ctx_count, rows // (fsdp_count * ctx_count), cols)
    if ctx_count == 2:
        kept, sent = scatter_ctx(blocks, ctx_rank)
        got = from_partner(sent, "ctx", 1)
        held = (after(kept, *earlier).astype(WIDE) + got.astype(WIDE)).astype(kind)
    else:
        swapped = jnp.swapaxes(blocks, 0, 1).reshape(rows, cols)
        held = lax.psum_scatter(swapped, "ctx", scatter_dimension=0, tiled=True)
    held = held.reshape(rows // ctx_count, cols)
    return lax.psum_scatter(held, "fsdp", scatter_dimension=0, tiled=True)


def estimate(flops, moved, transcendentals=0):
    return pl.CostEstimate(flops=flops, bytes_accessed=moved, transcendentals=transcendentals)


def part_spec(rows, cols, part):
    return pl.BlockSpec((rows, cols), lambda *_: (0, part), pipeline_mode=pl.Buffered(1))


def whole_spec(*shape, once=False):
    mode = {"pipeline_mode": pl.Buffered(1)} if once else {}
    return pl.BlockSpec(shape, lambda *_: (0,) * len(shape), **mode)


def rows_kernel(groups, *refs):
    slot = pl.program_id(0)
    weight, (lin, stacked) = refs[sum(groups)], refs[-2:]

    def run(pieces):
        start = 0
        for piece in pieces:
            stacked[start : start + piece.shape[0]] = piece[...]
            start += piece.shape[0]
        lin[...] = jnp.dot(stacked[...], weight[...], preferred_element_type=WIDE).astype(LOW)

    first = 0
    for r, pieces in enumerate(groups):
        pl.when(slot == r)(functools.partial(run, refs[first : first + pieces]))
        first += pieces


def stack_rows(slots, weight, part, parts, into=None, first=0, total=None):
    groups = [len(s) for s in slots]
    rows = [piece for s in slots for piece in s]
    width, length = rows[0].shape[1], sum(piece.shape[0] for piece in slots[0])
    count, cols = len(slots), weight.shape[1] // parts
    total = total or count
    into = into or ()
    return pl.pallas_call(
        functools.partial(rows_kernel, groups),
        grid=(count,),
        in_specs=[whole_spec(*piece.shape, once=True) for piece in rows]
        + [part_spec(width, cols, part)]
        + [pl.BlockSpec(memory_space=pl.ANY)] * len(into),
        out_specs=[
            pl.BlockSpec((length, cols), lambda s: (first + s, 0)),
            pl.BlockSpec((length, width), lambda s: (first + s, 0)),
        ],
        out_shape=[
            jax.ShapeDtypeStruct((total * length, cols), LOW),
            jax.ShapeDtypeStruct((total * length, width), LOW),
        ],
        input_output_aliases={len(rows) + 1 + i: i for i in range(len(into))},
        compiler_params=pltpu.CompilerParams(vmem_limit_bytes=60 << 20),
        cost_estimate=estimate(
            2 * count * length * width * cols, 2 * (count * length * (2 * width + cols) + width * cols)
        ),
    )(*rows, weight, *into)


def units_kernel(h, up, gate, grad, hid, grad_gate, grad_up):
    up_lin = jnp.dot(h[...], up[...], preferred_element_type=WIDE)
    gate_lin = gate[...].astype(WIDE)
    grad_hidden = grad[...].astype(WIDE)
    sigmoid = 1.0 / (1.0 + jnp.exp(-gate_lin))
    silu = gate_lin * sigmoid
    hid[...] = (silu * up_lin).astype(LOW)
    grad_gate[...] = (grad_hidden * up_lin * sigmoid * (1.0 + gate_lin * (1.0 - sigmoid))).astype(LOW)
    grad_up[...] = (grad_hidden * silu).astype(LOW)


def hidden_units(h, up, part, parts, gate_lin, grad_hidden):
    tokens, width = h.shape
    cols = up.shape[1] // parts
    step = math.gcd(512, tokens)
    by_row = lambda n: pl.BlockSpec((step, n), lambda i: (i, 0))
    return pl.pallas_call(
        units_kernel,
        grid=(tokens // step,),
        in_specs=[by_row(width), part_spec(width, cols, part), by_row(cols), by_row(cols)],
        out_specs=[by_row(cols)] * 3,
        out_shape=[jax.ShapeDtypeStruct((tokens, cols), LOW)] * 3,
        compiler_params=pltpu.CompilerParams(vmem_limit_bytes=60 << 20),
        cost_estimate=estimate(
            2 * tokens * width * cols, 2 * (tokens * width + width * cols + 5 * tokens * cols)
        ),
    )(h, up, gate_lin, grad_hidden)


def back_kernel(terms, *refs):
    lefts, weights, outs = refs[:terms], refs[terms : 2 * terms], refs[2 * terms :]
    total = None
    for left, weight in zip(lefts, weights):
        term = dot_cols(left[...], weight[...])
        total = term if total is None else total + term
    for i, out in enumerate(outs):

        @pl.when(pl.program_id(0) == i)
        def _():
            out[...] = total.astype(LOW)


def back_rows(lefts, weights, first_slot, slots, length):
    width = weights[0][0].shape[0]
    depth = sum(left.shape[1] for left in lefts)
    return pl.pallas_call(
        functools.partial(back_kernel, len(lefts)),
        grid=(slots,),
        in_specs=[
            pl.BlockSpec((length, left.shape[1]), lambda s: (first_slot + s, 0)) for left in lefts
        ]
        + [part_spec(width, w.shape[1] // parts, part) for w, part, parts in weights],
        out_specs=[whole_spec(length, width)] * slots,
        out_shape=[jax.ShapeDtypeStruct((length, width), LOW)] * slots,
        compiler_params=pltpu.CompilerParams(vmem_limit_bytes=60 << 20),
        cost_estimate=estimate(
            2 * slots * length * width * depth,
            2 * (slots * length * (width + depth) + width * depth),
        ),
    )(*lefts, *[w for w, _, _ in weights])


def chosen_kernel(near, count, info, cotangent, *refs):
    slot = pl.program_id(0)
    others, (weight, lin, stacked) = refs[:count], refs[count:]

    @pl.when(slot < near)
    def _():
        stacked[...] = cotangent[0]

    for k, other in enumerate(others):

        @pl.when((slot >= near) & (info[slot] == k))
        def _():
            stacked[...] = other[...]

    lin[...] = jnp.dot(stacked[...], weight[...], preferred_element_type=WIDE).astype(LOW)


def chosen_rows(info, cotangent, others, weight, part, parts):
    near, length, width = cotangent.shape
    slots, cols = near + len(others), weight.shape[1] // parts
    held = lambda rows, n, at: pl.BlockSpec(
        (rows, n), lambda s, info: (0, at), pipeline_mode=pl.Buffered(1)
    )
    return pl.pallas_call(
        functools.partial(chosen_kernel, near, len(others)),
        grid_spec=pltpu.PrefetchScalarGridSpec(
            num_scalar_prefetch=1,
            grid=(slots,),
            in_specs=[
                pl.BlockSpec((1, length, width), lambda s, info: (info[jnp.minimum(s, near - 1)], 0, 0))
            ]
            + [held(length, width, 0)] * len(others)
            + [held(width, cols, part)],
            out_specs=[
                pl.BlockSpec((length, cols), lambda s, info: (s, 0)),
                pl.BlockSpec((length, width), lambda s, info: (s, 0)),
            ],
        ),
        out_shape=[
            jax.ShapeDtypeStruct((slots * length, cols), LOW),
            jax.ShapeDtypeStruct((slots * length, width), LOW),
        ],
        compiler_params=pltpu.CompilerParams(vmem_limit_bytes=60 << 20),
        cost_estimate=estimate(
            2 * slots * length * width * cols, 2 * (slots * length * (2 * width + cols) + width * cols)
        ),
    )(info, cotangent, *others, weight)


def full_units_kernel(h, g, down, gate, up, hid, grad_gate, grad_up):
    gate_lin = jnp.dot(h[...], gate[...], preferred_element_type=WIDE)
    up_lin = jnp.dot(h[...], up[...], preferred_element_type=WIDE)
    grad_hidden = jnp.dot(g[...], down[...], preferred_element_type=WIDE)
    sigmoid = 1.0 / (1.0 + jnp.exp(-gate_lin))
    silu = gate_lin * sigmoid
    hid[...] = (silu * up_lin).astype(LOW)
    grad_gate[...] = (grad_hidden * up_lin * sigmoid * (1.0 + gate_lin * (1.0 - sigmoid))).astype(LOW)
    grad_up[...] = (grad_hidden * silu).astype(LOW)


def full_units(h, g, weight):
    tokens, width = h.shape
    cols = weight.shape[1] // 3
    step = math.gcd(512, tokens)
    by_row = lambda n: pl.BlockSpec((step, n), lambda i: (i, 0))
    return pl.pallas_call(
        full_units_kernel,
        grid=(tokens // step,),
        in_specs=[by_row(width)] * 2 + [part_spec(width, cols, i) for i in range(3)],
        out_specs=[by_row(cols)] * 3,
        out_shape=[jax.ShapeDtypeStruct((tokens, cols), LOW)] * 3,
        compiler_params=pltpu.CompilerParams(vmem_limit_bytes=60 << 20),
        cost_estimate=estimate(
            6 * tokens * width * cols, 2 * (2 * tokens * width + 3 * width * cols + 3 * tokens * cols)
        ),
    )(h, g, weight, weight, weight)


def first_grads_kernel(g, h, hid, gate, up, out):
    part = pl.program_id(0)
    for i, (left, right) in enumerate(((g, hid), (h, gate), (h, up))):

        @pl.when(part == i)
        def _():
            out[...] = dot_rows(left[...], right[...]).astype(LOW)


def first_grads(grad_rows, rows, hid, grad_gate, grad_up):
    tokens, width = rows.shape
    cols, tile = hid.shape[1], 256
    tiles = width // tile
    return pl.pallas_call(
        first_grads_kernel,
        grid=(3, tiles),
        in_specs=[
            pl.BlockSpec((tokens, tile), lambda p, i: (0, jnp.where(p == 0, i, tiles - 1))),
            pl.BlockSpec((tokens, tile), lambda p, i: (0, jnp.where(p == 0, 0, i))),
        ]
        + [whole_spec(tokens, cols, once=True)] * 3,
        out_specs=pl.BlockSpec((tile, cols), lambda p, i: (i, p)),
        out_shape=jax.ShapeDtypeStruct((width, 3 * cols), LOW),
        compiler_params=pltpu.CompilerParams(vmem_limit_bytes=60 << 20),
        cost_estimate=estimate(6 * tokens * width * cols, 6 * tokens * cols + 6 * width * cols),
    )(grad_rows, rows, hid, grad_gate, grad_up)


MESH_ID = pl.DeviceIdType.MESH


def meet(partners):
    barrier = pltpu.get_barrier_semaphore()
    for partner in partners:
        pl.semaphore_signal(barrier, inc=1, device_id=partner, device_id_type=MESH_ID)
    pl.semaphore_wait(barrier, len(partners))


def partners_of():
    tensor_rank, ctx_rank = lax.axis_index("tp"), lax.axis_index("ctx")
    return {"tp": tensor_rank ^ 1}, {"tp": tensor_rank ^ 2}, {"ctx": ctx_rank ^ 1}


def collect_kernel(
    slots, tiles, gate_a, up_a, gate_b, up_b, w_gate_a, w_up_a, w_gate_b, w_up_b, left, right, hid, up, total,
    down_out, up_out, parts, sent, core_in, across_in, last_in, held, send, recv, load
):
    step = pl.program_id(0)
    steps = pl.num_programs(0)
    core, far, side = partners_of()
    half = total.shape[0] // 2
    remote = remote_copy(send, recv)
    cores = [remote(sent.at[k % 2], core_in.at[k], k, core) for k in range(4)]
    across = [
        remote(parts.at[3, pl.ds(0, half)], across_in.at[0], 4, far),
        remote(parts.at[3, pl.ds(half, half)], across_in.at[1], 5, side),
    ]
    lasts = [
        remote(parts.at[1], last_in.at[0], 6, far),
        remote(parts.at[2, pl.ds(half, half)], last_in.at[1, pl.ds(half, half)], 7, side),
        remote(parts.at[2, pl.ds(0, half)], last_in.at[1, pl.ds(0, half)], 8, side),
    ]
    loading = [
        pltpu.make_async_copy(source, held.at[i], load.at[i]) for i, source in enumerate((hid, up))
    ]

    @pl.when(step == 0)
    def _():
        for copy in loading:
            copy.start()
        meet((core, far, side))

    for k in (2, 3):
        pl.when(step == 2 * k)(cores[k - 2].wait_send)

    @pl.when(step < slots)
    def _():
        part = (
            dot_cols(gate_a[...], w_gate_a[...])
            + dot_cols(up_a[...], w_up_a[...])
            + dot_cols(gate_b[...], w_gate_b[...])
            + dot_cols(up_b[...], w_up_b[...])
        )

        @pl.when(step == slots - 1)
        def _():
            total[...] = part

        for k in range(4):

            @pl.when(step == 2 * k)
            def _():
                sent[k % 2] = part.astype(LOW)
                cores[k].start()

            if k < 3:

                @pl.when(step == 2 * k + 1)
                def _():
                    cores[k].wait_recv()
                    parts[3 - k] = (part + core_in[k].astype(WIDE)).astype(LOW)

    def add(slot, rows, value):
        parts[slot, rows] = (parts[slot, rows].astype(WIDE) + value.astype(WIDE)).astype(LOW)

    low, high = pl.ds(0, half), pl.ds(half, half)

    @pl.when(step == 1)
    def _():
        for copy in across:
            copy.start()

    pl.when(step == 3)(lasts[1].start)

    @pl.when(step == 5)
    def _():
        across[1].wait_recv()
        add(1, high, across_in[1])
        lasts[0].start()
        across[0].wait_recv()
        add(2, low, across_in[0])
        lasts[2].start()

    @pl.when((step >= slots) & (step < slots + tiles))
    def _():
        pl.when(step == slots)(loading[0].wait)
        down_out[...] = dot_rows(left[...], held[0]).astype(LOW)

    @pl.when(step >= slots + tiles)
    def _():
        pl.when(step == slots + tiles)(loading[1].wait)
        up_out[...] = dot_rows(right[...], held[1]).astype(LOW)

    @pl.when(step == steps - 1)
    def _():
        cores[3].wait_recv()
        for copy in lasts:
            copy.wait_recv()
        total[...] += (
            core_in[3].astype(WIDE) + last_in[0].astype(WIDE) + last_in[1].astype(WIDE)
        )
        for copy in (*cores[2:], *across, *lasts):
            copy.wait_send()


def collect_back(first, second, weight_a, weight_b, grad_rows, rows, hid, length):
    tokens, cols_a = first[0].shape
    cols = second[0].shape[1]
    width = weight_a.shape[0]
    slots, tile = tokens // length, 256
    tiles = width // tile
    row = lambda n: pl.BlockSpec((length, n), lambda i: (jnp.maximum(slots - 1 - i, 0), 0))
    column = lambda i, start: jnp.clip(i - start, 0, tiles - 1)
    down_at, up_at = (lambda i: column(i, slots)), (lambda i: column(i, slots + tiles))
    return pl.pallas_call(
        functools.partial(collect_kernel, slots, tiles),
        grid=(slots + 2 * tiles,),
        in_specs=[row(cols_a), row(cols_a), row(cols), row(cols)]
        + [part_spec(width, cols_a, 1), part_spec(width, cols_a, 2)]
        + [part_spec(width, cols, 1), part_spec(width, cols, 2)]
        + [
            pl.BlockSpec((tokens, tile), lambda i: (0, down_at(i))),
            pl.BlockSpec((tokens, tile), lambda i: (0, up_at(i))),
            ANYWHERE,
            ANYWHERE,
        ],
        out_specs=[
            whole_spec(length, width, once=True),
            pl.BlockSpec((tile, cols), lambda i: (down_at(i), 0)),
            pl.BlockSpec((tile, cols), lambda i: (up_at(i), 0)),
        ],
        out_shape=[
            jax.ShapeDtypeStruct((length, width), WIDE),
            jax.ShapeDtypeStruct((width, cols), LOW),
            jax.ShapeDtypeStruct((width, cols), LOW),
        ],
        scratch_shapes=[
            pltpu.VMEM((4, length, width), LOW),
            pltpu.VMEM((2, length, width), LOW),
            pltpu.VMEM((4, length, width), LOW),
            pltpu.VMEM((2, length // 2, width), LOW),
            pltpu.VMEM((2, length, width), LOW),
            pltpu.VMEM((2, tokens, cols), LOW),
            pltpu.SemaphoreType.DMA((9,)),
            pltpu.SemaphoreType.DMA((9,)),
            pltpu.SemaphoreType.DMA((2,)),
        ],
        compiler_params=pltpu.CompilerParams(
            vmem_limit_bytes=63 << 20, collective_id=1, has_side_effects=True
        ),
        cost_estimate=estimate(6 * tokens * width * cols, 10 * tokens * cols),
    )(*first, *second, weight_a, weight_a, weight_b, weight_b, grad_rows, rows, hid, second[1])


def remote_copy(send, recv):
    def make(source, target, index, partner):
        return pltpu.make_async_remote_copy(
            source, target, send.at[index], recv.at[index], device_id=partner, device_id_type=MESH_ID
        )

    return make


def branch_kernel(
    slots, tiles, total, middle, own_grad, gain, hid_a, hid_b, w_a, w_b, turned, gate, grad_middle, gain_grad,
    gate_out, branch, mlp_own, mlp_far, mlp_side, own, parts, core_in, across_in, held, send, recv, load
):
    step = pl.program_id(0)
    core, far, side = partners_of()
    remote = remote_copy(send, recv)
    to_far = remote(own, branch.at[2], 0, far)
    to_near = remote(own, branch.at[1], 1, core)
    to_cross = remote(branch.at[2], branch.at[3], 2, core)
    keep = pltpu.make_async_copy(own, branch.at[0], load.at[0])
    loading = pltpu.make_async_copy(gate, held, load.at[1])
    cores = [remote(parts.at[7 - 2 * k], core_in.at[k], 3 + k, core) for k in range(4)]
    across = remote(parts.at[6], across_in, 7, side)
    stores = [
        pltpu.make_async_copy(parts.at[4], mlp_side, load.at[2]),
        pltpu.make_async_copy(parts.at[2], mlp_far, load.at[3]),
        pltpu.make_async_copy(parts.at[0], mlp_own, load.at[4]),
    ]

    @pl.when(step == 0)
    def _():
        loading.start()
        meet((core, far, side))
        values, upstream = middle[...], total[...]
        inverse = lax.rsqrt(jnp.mean(values * values, axis=-1, keepdims=True) + EPS)
        grad_in, gain_grad[...] = norm_backward(values, inverse, gain[...], upstream)
        grad_in = own_grad[...].astype(WIDE) + grad_in
        grad_middle[...] = grad_in
        own[...] = grad_in.astype(LOW)
        for copy in (to_far, to_near, keep):
            copy.start()

    @pl.when(step < slots)
    def _():
        part = dot_cols(hid_a[...], w_a[...]) + dot_cols(hid_b[...], w_b[...])
        parts[slots - 1 - step] = part.astype(LOW)

    for k in range(4):
        pl.when(step == 2 * k)(cores[k].start)

        def finish(k=k):
            slot = 6 - 2 * k
            cores[k].wait_recv()
            parts[slot] = (parts[slot].astype(WIDE) + core_in[k].astype(WIDE)).astype(LOW)
            if k == 0:
                across.start()
            if k == 1:
                stores[0].start()
            if k == 3:
                stores[2].start()

        pl.when(step == 2 * k + 1)(finish)

    @pl.when(step >= slots)
    def _():
        pl.when(step == slots)(loading.wait)
        gate_out[...] = dot_rows(turned[...], held[...]).astype(LOW)

    @pl.when(step == slots + tiles - 2)
    def _():
        to_far.wait_recv()
        to_cross.start()

    @pl.when(step == slots + tiles - 1)
    def _():
        to_near.wait_recv()
        to_cross.wait_recv()
        across.wait_recv()
        parts[2] = (parts[2].astype(WIDE) + across_in[...].astype(WIDE)).astype(LOW)
        stores[1].start()
        keep.wait()
        for copy in stores:
            copy.wait()
        for copy in (to_far, to_near, to_cross, *cores, across):
            copy.wait_send()


ANYWHERE = pl.BlockSpec(memory_space=pl.ANY)


def spread_branch(total, middle, own_grad, gain, hid_a, hid_b, weight_a, weight_b, rows, grad_gate):
    length, width = total.shape
    tokens, cols = grad_gate.shape
    slots, tile = tokens // length, 256
    tiles = width // tile
    once = whole_spec(length, width, once=True)
    column = lambda i: jnp.clip(i - slots, 0, tiles - 1)
    part = jax.ShapeDtypeStruct((length, width), LOW)
    return pl.pallas_call(
        functools.partial(branch_kernel, slots, tiles),
        grid=(slots + tiles,),
        in_specs=[
            once,
            once,
            once,
            whole_spec(1, width),
            pl.BlockSpec((length, hid_a.shape[1]), lambda i: (jnp.maximum(slots - 1 - i, 0), 0)),
            pl.BlockSpec((length, cols), lambda i: (jnp.maximum(slots - 1 - i, 0), 0)),
            part_spec(width, hid_a.shape[1], 0),
            part_spec(width, cols, 0),
            pl.BlockSpec((tokens, tile), lambda i: (0, column(i))),
            ANYWHERE,
        ],
        out_specs=[
            whole_spec(length, width, once=True),
            whole_spec(1, width),
            pl.BlockSpec((tile, cols), lambda i: (column(i), 0)),
        ]
        + [ANYWHERE] * 4,
        out_shape=[
            jax.ShapeDtypeStruct((length, width), WIDE),
            jax.ShapeDtypeStruct((1, width), WIDE),
            jax.ShapeDtypeStruct((width, cols), LOW),
            jax.ShapeDtypeStruct((4, length, width), LOW),
            part,
            part,
            part,
        ],
        scratch_shapes=[
            pltpu.VMEM((length, width), LOW),
            pltpu.VMEM((slots, length, width), LOW),
            pltpu.VMEM((4, length, width), LOW),
            pltpu.VMEM((length, width), LOW),
            pltpu.VMEM((tokens, cols), LOW),
            pltpu.SemaphoreType.DMA((8,)),
            pltpu.SemaphoreType.DMA((8,)),
            pltpu.SemaphoreType.DMA((5,)),
        ],
        compiler_params=pltpu.CompilerParams(
            vmem_limit_bytes=63 << 20, collective_id=2, has_side_effects=True
        ),
        cost_estimate=estimate(4 * tokens * width * cols, 10 * tokens * cols),
    )(total, middle, own_grad, gain, hid_a, hid_b, weight_a, weight_b, rows, grad_gate)


def line_kernel(
    slots, tiles, count, line, weight, own_in, grad_middle, gain, gain_two, rows_one, line_all, block, *refs
):
    sums, (share, gain_grad, attn_out, bias_out, home) = refs[:count], refs[count : count + 5]
    gots = refs[count + 5 : 2 * count + 5]
    parts, core_in, far_in, total, gains, gains_in, send, recv, load = refs[2 * count + 5 :]
    step = pl.program_id(0)
    core, far, side = partners_of()
    tensor_rank, group = lax.axis_index("tp"), lax.axis_index("fsdp")
    shift = (tensor_rank % 2) * 2 + tensor_rank // 2
    target = {"fsdp": (group + slots - shift) % slots}
    source = {"fsdp": (group + shift) % slots}
    stays = shift == 0
    remote = remote_copy(send, recv)
    cores = [remote(parts.at[3 - 2 * k], core_in.at[k], k, core) for k in range(2)]
    to_far = remote(parts.at[2], far_in, 2, far)
    leave = remote(block, home, 3, target)
    keep = pltpu.make_async_copy(block, home, load)
    cross = {"tp": tensor_rank ^ 3}
    gain_copies = [
        remote(gains, gains_in.at[i], 4 + i, partner) for i, partner in enumerate((core, far, cross))
    ]
    rows = gots[0].shape[0]
    there = pl.multiple_of((1 - lax.axis_index("ctx")) * rows, rows)
    sides = [
        remote(held.at[pl.ds(there, rows)], got, 7 + i, side) for i, (held, got) in enumerate(zip(sums, gots))
    ]

    @pl.when(step == 0)
    def _():
        barrier = pltpu.get_barrier_semaphore()
        for partner in (core, far, cross, side):
            pl.semaphore_signal(barrier, inc=1, device_id=partner, device_id_type=MESH_ID)

        @pl.when(stays)
        def _():
            pl.semaphore_wait(barrier, 4)
            keep.start()

        @pl.when(jnp.logical_not(stays))
        def _():
            for partner in (target, source):
                pl.semaphore_signal(barrier, inc=1, device_id=partner, device_id_type=MESH_ID)
            pl.semaphore_wait(barrier, 6)
            leave.start()

        for copy in sides:
            copy.start()

    @pl.when(step < slots)
    def _():
        part = dot_cols(line[...], weight[...])
        parts[slots - 1 - step] = part.astype(LOW)

        @pl.when(step == slots - 1)
        def _():
            total[...] = part

    for k in range(2):
        pl.when(step == 2 * k)(cores[k].start)

    @pl.when(step == 1)
    def _():
        cores[0].wait_recv()
        parts[2] = (parts[2].astype(WIDE) + core_in[0].astype(WIDE)).astype(LOW)
        to_far.start()

    @pl.when(step == slots - 1)
    def _():
        bias_out[...] = jnp.sum(line_all[...].astype(WIDE), axis=0, keepdims=True)

    @pl.when(step >= slots)
    def _():
        attn_out[...] = dot_rows(rows_one[...], line_all[...]).astype(LOW)

    @pl.when(step == slots + tiles - 1)
    def _():
        cores[1].wait_recv()
        to_far.wait_recv()
        upstream = total[...] + core_in[1].astype(WIDE) + far_in[...].astype(WIDE)
        values = own_in[...].astype(WIDE)
        inverse = lax.rsqrt(jnp.mean(values * values, axis=-1, keepdims=True) + EPS)
        grad_in, gain_one = norm_backward(values, inverse, gain[...], upstream)
        gains[0:1] = gain_one
        gains[1:2] = gain_two[...]
        for copy in gain_copies:
            copy.start()
        share[...] = (grad_middle[...] + grad_in).astype(LOW)
        for copy in gain_copies:
            copy.wait_recv()
        gain_grad[...] = (gains[...] + gains_in[0]) + (gains_in[1] + gains_in[2])
        for copy in sides:
            copy.wait_recv()
        for copy in (*cores, to_far, *gain_copies, *sides):
            copy.wait_send()
        pl.when(stays)(keep.wait)

        @pl.when(jnp.logical_not(stays))
        def _():
            leave.wait_recv()
            leave.wait_send()


def finish_rows(line, weight, own_in, grad_middle, gain, gain_two, rows_one, block, sums):
    length, width = own_in.shape
    near_tokens, line_cols = line.shape
    slots, tile = near_tokens // length, 256
    tiles = width // tile
    once = whole_spec(length, width, once=True)
    column = lambda i: jnp.clip(i - slots, 0, tiles - 1)
    by_column = lambda n: pl.BlockSpec((n, tile), lambda i: (0, column(i)))
    attn_cols = line_cols
    return pl.pallas_call(
        functools.partial(line_kernel, slots, tiles, len(sums)),
        grid=(slots + tiles,),
        in_specs=[
            pl.BlockSpec((length, line_cols), lambda i: (jnp.maximum(slots - 1 - i, 0), 0)),
            whole_spec(width, line_cols, once=True),
            once,
            once,
            whole_spec(1, width),
            whole_spec(1, width),
            by_column(near_tokens),
            whole_spec(near_tokens, line_cols, once=True),
            ANYWHERE,
        ]
        + [ANYWHERE] * len(sums),
        out_specs=[
            whole_spec(length, width),
            whole_spec(2, width),
            pl.BlockSpec((tile, attn_cols), lambda i: (column(i), 0)),
            whole_spec(1, line_cols),
            ANYWHERE,
        ]
        + [ANYWHERE] * len(sums),
        out_shape=[
            jax.ShapeDtypeStruct((length, width), LOW),
            jax.ShapeDtypeStruct((2, width), WIDE),
            jax.ShapeDtypeStruct((width, attn_cols), LOW),
            jax.ShapeDtypeStruct((1, line_cols), WIDE),
            jax.ShapeDtypeStruct((length, width), LOW),
        ]
        + [jax.ShapeDtypeStruct((t.shape[0] // 2, t.shape[1]), LOW) for t in sums],
        scratch_shapes=[
            pltpu.VMEM((slots, length, width), LOW),
            pltpu.VMEM((2, length, width), LOW),
            pltpu.VMEM((length, width), LOW),
            pltpu.VMEM((length, width), WIDE),
            pltpu.VMEM((2, width), WIDE),
            pltpu.VMEM((3, 2, width), WIDE),
            pltpu.SemaphoreType.DMA((7 + len(sums),)),
            pltpu.SemaphoreType.DMA((7 + len(sums),)),
            pltpu.SemaphoreType.DMA,
        ],
        compiler_params=pltpu.CompilerParams(
            vmem_limit_bytes=63 << 20, collective_id=3, has_side_effects=True
        ),
        cost_estimate=estimate(2 * near_tokens * width * attn_cols, 10 * near_tokens * width),
    )(line, weight, own_in, grad_middle, gain, gain_two, rows_one, line, block, *sums)


def place_kernel(count, info, *refs):
    out = refs[count]
    for r in range(count):

        @pl.when(pl.program_id(0) == r)
        def _():
            out[0] = refs[r][...]


def place_rows(rows, order):
    length, width = rows[0].shape
    count = len(rows)
    held = pl.BlockSpec((length, width), lambda s, info: (0, 0), pipeline_mode=pl.Buffered(1))
    return pl.pallas_call(
        functools.partial(place_kernel, count),
        grid_spec=pltpu.PrefetchScalarGridSpec(
            num_scalar_prefetch=1,
            grid=(count,),
            in_specs=[held] * count,
            out_specs=pl.BlockSpec((1, length, width), lambda s, info: (info[s], 0, 0)),
        ),
        out_shape=jax.ShapeDtypeStruct((count, length, width), LOW),
        compiler_params=pltpu.CompilerParams(vmem_limit_bytes=32 << 20),
        cost_estimate=estimate(0, 4 * count * length * width),
    )(order, *rows)


def turn(values, cosine, sine_signed):
    return values * cosine + pltpu.roll(values, values.shape[-1] // 2, 1) * sine_signed


def turn_back(values, cosine, sine_signed):
    return values * cosine - pltpu.roll(values, values.shape[-1] // 2, 1) * sine_signed


def project_kernel(
    heads, head_dim, x0, x1, x2, x3, gains, weight, bias, cosine, sine, h_out, q_out, k_out, v_out, gain
):
    slot = pl.program_id(0)

    @pl.when(slot == 0)
    def _():
        gain[...] = gains[...].astype(WIDE).T[:8]


    def run(x_ref):
        x = x_ref[...].astype(WIDE)
        scale_inv = lax.rsqrt(jnp.mean(x * x, axis=-1, keepdims=True) + EPS)
        normed = (x * scale_inv * gain[0:1]).astype(LOW)
        h_out[0] = normed
        lin = jnp.dot(normed, weight[...], preferred_element_type=WIDE) + bias[...]
        cos, sin = cosine[0], sine[0]
        for h in range(heads + 1):
            part = turn(lin[:, h * head_dim : (h + 1) * head_dim], cos, sin).astype(LOW)
            if h < heads:
                q_out[0, :, h * head_dim : (h + 1) * head_dim] = part
            else:
                k_out[0] = part
        v_out[0] = lin[:, (heads + 1) * head_dim :].astype(LOW)

    for r, x_ref in enumerate((x0, x1, x2, x3)):
        pl.when(slot == r)(functools.partial(run, x_ref))


def project(rows, held, bias, cosine, sine, heads, head_dim):
    length, width = rows[0].shape
    count = len(rows)
    cols = (heads + 2) * head_dim
    whole = whole_spec
    by_slot = lambda *shape: pl.BlockSpec((1, *shape), lambda s: (s,) + (0,) * len(shape))
    return pl.pallas_call(
        functools.partial(project_kernel, heads, head_dim),
        grid=(count,),
        in_specs=[whole(length, width)] * count
        + [part_spec(width, 128, cols // 128), part_spec(width, cols, 0), whole(1, cols)]
        + [by_slot(length, head_dim)] * 2,
        out_specs=[
            by_slot(length, width),
            by_slot(length, heads * head_dim),
            by_slot(length, head_dim),
            by_slot(length, head_dim),
        ],
        out_shape=[
            jax.ShapeDtypeStruct((count, length, width), LOW),
            jax.ShapeDtypeStruct((count, length, heads * head_dim), LOW),
            jax.ShapeDtypeStruct((count, length, head_dim), LOW),
            jax.ShapeDtypeStruct((count, length, head_dim), LOW),
        ],
        scratch_shapes=[pltpu.VMEM((8, width), WIDE)],
        compiler_params=pltpu.CompilerParams(vmem_limit_bytes=56 << 20),
        cost_estimate=pl.CostEstimate(
            flops=2 * count * length * width * cols,
            bytes_accessed=count * length * (2 * width + cols) * 2 + width * cols * 2,
            transcendentals=0,
        ),
    )(*rows, held, held, bias, cosine, sine)


def row_blocks(length):
    return [(i, min(256, length)) for i in range(0, length, min(256, length))]


def key_biases(length, offset, start, rows, past, keys):
    past_pos = lax.broadcasted_iota(jnp.int32, (1, past), 1)
    past_bias = jnp.where((past_pos < offset) & (past_pos < length), 0.0, NEG_FILL)
    query_pos = offset + start + lax.broadcasted_iota(jnp.int32, (rows, keys), 0)
    own_pos = offset + lax.broadcasted_iota(jnp.int32, (rows, keys), 1)
    own_bias = jnp.where((own_pos <= query_pos) & (own_pos < length), 0.0, NEG_FILL)
    return past_bias, own_bias


def dot_cols(left, right):
    return lax.dot_general(left, right, (((1,), (1,)), ((), ())), preferred_element_type=WIDE)


def dot_rows(left, right):
    return lax.dot_general(left, right, (((0,), (0,)), ((), ())), preferred_element_type=WIDE)


def attend_rows(
    heads, head_dim, scale, length, offset, q, k_past, v_past, k_own, v_own, weight, out, lse, put
):
    past = k_past.shape[1]
    for start, rows in row_blocks(q.shape[1]):
        keys = start + rows
        past_bias, own_bias = key_biases(length, offset, start, rows, past, keys)
        here = slice(start, start + rows)
        for h in range(heads):
            cols = slice(h * head_dim, (h + 1) * head_dim)
            query = q[0, here, cols]
            s_past = dot_cols(query, k_past[0]) * scale + past_bias
            s_own = dot_cols(query, k_own[0, :keys]) * scale + own_bias
            top = jnp.maximum(
                jnp.max(s_past, axis=1, keepdims=True), jnp.max(s_own, axis=1, keepdims=True)
            )
            e_past, e_own = jnp.exp(s_past - top), jnp.exp(s_own - top)
            total = jnp.sum(e_past, axis=1, keepdims=True) + jnp.sum(e_own, axis=1, keepdims=True)
            inverse = 1.0 / total
            mixed = jnp.dot(
                (e_past * inverse).astype(LOW), v_past[0], preferred_element_type=WIDE
            ) + jnp.dot((e_own * inverse).astype(LOW), v_own[0, :keys], preferred_element_type=WIDE)
            out[0, here, cols] = mixed.astype(LOW)
            lse[0, here, h : h + 1] = top + jnp.log(total)
        rows_out = dot_cols(out[0, here], weight[...]).astype(LOW)
        put(here, rows_out)


def attend_kernel(
    heads, head_dim, scale, first, total_slots, info, q, k_past, v_past, k_own, v_own, weight, out, lse, *parts
):
    length, offset = info[first + pl.program_id(0)], info[total_slots]

    def put(here, value):
        for i, part in enumerate(parts):

            @pl.when(pl.program_id(0) == i)
            def _():
                part[here] = value

    attend_rows(heads, head_dim, scale, length, offset, q, k_past, v_past, k_own, v_own, weight, out, lse, put)


def attend_forward(info, q, k_past, v_past, k_own, v_own, weight, heads, head_dim, scale, first, count):
    _, length, width = q.shape
    past = k_past.shape[1]
    by_slot = lambda *shape: pl.BlockSpec((1, *shape), lambda s, info: (first + s,) + (0,) * len(shape))
    out_slot = lambda *shape: pl.BlockSpec((1, *shape), lambda s, info: (s,) + (0,) * len(shape))
    keys = count * length * (past + length) * heads
    return pl.pallas_call(
        functools.partial(attend_kernel, heads, head_dim, scale, first, q.shape[0]),
        grid_spec=pltpu.PrefetchScalarGridSpec(
            num_scalar_prefetch=1,
            grid=(count,),
            in_specs=[
                by_slot(length, width),
                by_slot(past, head_dim),
                by_slot(past, head_dim),
                by_slot(length, head_dim),
                by_slot(length, head_dim),
                whole_spec(*weight.shape, once=True),
            ],
            out_specs=[out_slot(length, width), out_slot(length, 128)]
            + [whole_spec(length, weight.shape[0])] * count,
        ),
        out_shape=[
            jax.ShapeDtypeStruct((count, length, width), LOW),
            jax.ShapeDtypeStruct((count, length, 128), WIDE),
        ]
        + [jax.ShapeDtypeStruct((length, weight.shape[0]), LOW)] * count,
        compiler_params=pltpu.CompilerParams(vmem_limit_bytes=56 << 20),
        cost_estimate=estimate(4 * keys * head_dim, 4 * count * length * width, keys),
    )(info, q, k_past, v_past, k_own, v_own, weight)


def attend_back_rows(
    heads, head_dim, scale, length, offset, q, k_past, v_past, k_own, v_own, grad, lse, cosine, sine, put,
    dk_past, dk_own, dv_past, dv_own
):
    past = k_past.shape[1]
    for start, rows in row_blocks(q.shape[1]):
        keys = start + rows
        past_bias, own_bias = key_biases(length, offset, start, rows, past, keys)
        here = slice(start, start + rows)
        cos, sin = cosine[0, here], sine[0, here]
        for h in range(heads):
            cols = slice(h * head_dim, (h + 1) * head_dim)
            query, upstream = q[0, here, cols], grad[0, here, cols]
            log_total = lse[0, here, h : h + 1]
            p_past = jnp.exp(dot_cols(query, k_past[0]) * scale + past_bias - log_total)
            p_own = jnp.exp(dot_cols(query, k_own[0, :keys]) * scale + own_bias - log_total)
            g_past = dot_cols(upstream, v_past[0])
            g_own = dot_cols(upstream, v_own[0, :keys])
            row_dot = jnp.sum(p_past * g_past, axis=1, keepdims=True) + jnp.sum(
                p_own * g_own, axis=1, keepdims=True
            )
            s_past = (p_past * (g_past - row_dot)).astype(LOW)
            s_own = (p_own * (g_own - row_dot)).astype(LOW)
            dq = (
                jnp.dot(s_past, k_past[0], preferred_element_type=WIDE)
                + jnp.dot(s_own, k_own[0, :keys], preferred_element_type=WIDE)
            ) * scale
            put(here, cols, turn_back(dq, cos, sin).astype(LOW))
            dk_past[...] += dot_rows(s_past, query)
            dk_own[:keys] += dot_rows(s_own, query)
            dv_past[...] += dot_rows(p_past.astype(LOW), upstream)
            dv_own[:keys] += dot_rows(p_own.astype(LOW), upstream)


def attend_back_kernel(
    heads,
    head_dim,
    scale,
    info,
    q,
    k_past,
    v_past,
    k_own,
    v_own,
    grad,
    lse,
    cosine,
    sine,
    dq_out,
    mine_past,
    mine_own,
    other_past,
    other_own,
    dk_past,
    dk_own,
    dv_past,
    dv_own,
):
    slot = pl.program_id(0)
    length, offset = info[slot], info[pl.num_programs(0)]
    parity = info[pl.num_programs(0) + 1]
    for total in (dk_past, dk_own, dv_past, dv_own):
        total[...] = jnp.zeros_like(total)
    attend_back_rows(
        heads, head_dim, scale, length, offset, q, k_past, v_past, k_own, v_own, grad, lse, cosine, sine,
        lambda here, cols, value: dq_out.__setitem__((0, here, cols), value),
        dk_past, dk_own, dv_past, dv_own,
    )

    @pl.when(parity == 0)
    def _():
        mine_past[0] = dk_past[...] * scale
        mine_own[0] = dk_own[...] * scale
        other_past[0] = dv_past[...]
        other_own[0] = dv_own[...]

    @pl.when(parity != 0)
    def _():
        mine_past[0] = dv_past[...]
        mine_own[0] = dv_own[...]
        other_past[0] = dk_past[...] * scale
        other_own[0] = dk_own[...] * scale


def attend_backward(
    info, q, k_past, v_past, k_own, v_own, grad, lse, cosine, sine, heads, head_dim, scale
):
    count, length, width = q.shape
    past = k_past.shape[1]
    by_slot = lambda *shape: pl.BlockSpec((1, *shape), lambda s, info: (s,) + (0,) * len(shape))
    keys = count * length * (past + length) * heads
    return pl.pallas_call(
        functools.partial(attend_back_kernel, heads, head_dim, scale),
        grid_spec=pltpu.PrefetchScalarGridSpec(
            num_scalar_prefetch=1,
            grid=(count,),
            in_specs=[
                by_slot(length, width),
                by_slot(past, head_dim),
                by_slot(past, head_dim),
                by_slot(length, head_dim),
                by_slot(length, head_dim),
                by_slot(length, width),
                by_slot(length, 128),
                by_slot(length, head_dim),
                by_slot(length, head_dim),
            ],
            out_specs=[
                by_slot(length, width),
                by_slot(past, head_dim),
                by_slot(length, head_dim),
                by_slot(past, head_dim),
                by_slot(length, head_dim),
            ],
            scratch_shapes=[
                pltpu.VMEM((past, head_dim), WIDE),
                pltpu.VMEM((length, head_dim), WIDE),
                pltpu.VMEM((past, head_dim), WIDE),
                pltpu.VMEM((length, head_dim), WIDE),
            ],
        ),
        out_shape=[
            jax.ShapeDtypeStruct((count, length, width), LOW),
            jax.ShapeDtypeStruct((count, past, head_dim), WIDE),
            jax.ShapeDtypeStruct((count, length, head_dim), WIDE),
            jax.ShapeDtypeStruct((count, past, head_dim), WIDE),
            jax.ShapeDtypeStruct((count, length, head_dim), WIDE),
        ],
        compiler_params=pltpu.CompilerParams(vmem_limit_bytes=56 << 20),
        cost_estimate=estimate(10 * keys * head_dim, 8 * count * length * width, keys),
    )(info, q, k_past, v_past, k_own, v_own, grad, lse, cosine, sine)


def attend_sum_kernel(
    heads, head_dim, scale, slots, info, q, k_past, v_past, k_own, v_own, weight, own_in, gain, out, lse, middle,
    normed, parts, core_in, far_in, send, recv
):
    step = pl.program_id(0)
    slot = slots - 1 - step
    core, far, _ = partners_of()
    remote = remote_copy(send, recv)
    cores = [remote(parts.at[3 - 2 * k], core_in.at[k], k, core) for k in range(2)]
    to_far = remote(parts.at[2], far_in, 2, far)

    @pl.when(step == 0)
    def _():
        meet((core, far))

    def put(here, value):
        parts[slot, here] = value

    offset = lax.axis_index("ctx") * q.shape[1]
    attend_rows(
        heads, head_dim, scale, info[slot], offset, q, k_past, v_past, k_own, v_own, weight, out, lse, put
    )
    for k in range(2):
        pl.when(step == 2 * k)(cores[k].start)

    @pl.when(step == 1)
    def _():
        cores[0].wait_recv()
        parts[2] = (parts[2].astype(WIDE) + core_in[0].astype(WIDE)).astype(LOW)
        to_far.start()

    @pl.when(step == slots - 1)
    def _():
        cores[1].wait_recv()
        to_far.wait_recv()
        rows = own_in[...].astype(WIDE) + parts[0].astype(WIDE)
        rows = rows + core_in[1].astype(WIDE) + far_in[...].astype(WIDE)
        middle[...] = rows
        inverse = lax.rsqrt(jnp.mean(rows * rows, axis=-1, keepdims=True) + EPS)
        normed[...] = (rows * inverse * gain[...]).astype(LOW)
        for copy in (*cores, to_far):
            copy.wait_send()


def attend_sum(info, q, k_past, v_past, k_own, v_own, weight, own_in, gain, heads, head_dim, scale):
    count, length, width = q.shape
    past, model_width = k_past.shape[1], own_in.shape[1]
    by_slot = lambda *shape: pl.BlockSpec(
        (1, *shape), lambda i, info: (count - 1 - i,) + (0,) * len(shape)
    )
    keys = count * length * (past + length) * heads
    return pl.pallas_call(
        functools.partial(attend_sum_kernel, heads, head_dim, scale, count),
        grid_spec=pltpu.PrefetchScalarGridSpec(
            num_scalar_prefetch=1,
            grid=(count,),
            in_specs=[
                by_slot(length, width),
                by_slot(past, head_dim),
                by_slot(past, head_dim),
                by_slot(length, head_dim),
                by_slot(length, head_dim),
                whole_spec(*weight.shape, once=True),
                whole_spec(length, model_width, once=True),
                whole_spec(1, model_width),
            ],
            out_specs=[
                by_slot(length, width),
                by_slot(length, 128),
                whole_spec(length, model_width, once=True),
                whole_spec(length, model_width, once=True),
            ],
            scratch_shapes=[
                pltpu.VMEM((count, length, model_width), LOW),
                pltpu.VMEM((2, length, model_width), LOW),
                pltpu.VMEM((length, model_width), LOW),
                pltpu.SemaphoreType.DMA((3,)),
                pltpu.SemaphoreType.DMA((3,)),
            ],
        ),
        out_shape=[
            jax.ShapeDtypeStruct((count, length, width), LOW),
            jax.ShapeDtypeStruct((count, length, 128), WIDE),
            jax.ShapeDtypeStruct((length, model_width), WIDE),
            jax.ShapeDtypeStruct((length, model_width), LOW),
        ],
        compiler_params=pltpu.CompilerParams(
            vmem_limit_bytes=56 << 20, collective_id=5, has_side_effects=True
        ),
        cost_estimate=estimate(4 * keys * head_dim, 4 * count * length * width, keys),
    )(info, q, k_past, v_past, k_own, v_own, weight, own_in, gain)


def exchange_kernel(
    heads, head_dim, scale, slots, tiles, info, q, k_past, v_past, k_own, v_own, rows, weight, lse, cosine, sine,
    cosine_all, sine_all, branch, mixed, mlp_far, mlp_side, mlp_own, middle, line, out_grad, block, mine_past,
    mine_own, other_past, other_own, got_past, got_own, side_out, side_in, dk_past, dk_own, dv_past, dv_own,
    own_rows, last_in, grad, send, recv, load
):
    step = pl.program_id(0)
    tensor_rank = lax.axis_index("tp")
    core, far, side = partners_of()
    parity = lax.rem(tensor_rank, 2)
    offset = lax.axis_index("ctx") * q.shape[1]
    remote = remote_copy(send, recv)
    pasts = [remote(other_past.at[r], got_past.at[r ^ 1], r, core) for r in range(slots)]
    owns = [remote(other_own.at[r], got_own.at[r ^ 1], slots + r, core) for r in range(slots)]
    sides = [remote(side_out.at[r], side_in.at[r], 2 * slots + r, side) for r in range(slots)]
    lasts = [
        remote(mlp_far, last_in.at[0], 3 * slots, far),
        remote(mlp_side, last_in.at[1], 3 * slots + 1, side),
    ]
    loading = pltpu.make_async_copy(mlp_own, own_rows, load)

    @pl.when(step == 0)
    def _():
        loading.start()
        meet((core, far, side))
        for copy in lasts:
            copy.start()

    @pl.when(step < slots)
    def _():
        length = info[jnp.minimum(step, slots - 1)]
        for total in (dk_past, dk_own, dv_past, dv_own):
            total[...] = jnp.zeros_like(total)
        grad[0] = jnp.dot(rows[...], weight[...], preferred_element_type=WIDE).astype(LOW)
        attend_back_rows(
            heads, head_dim, scale, length, offset, q, k_past, v_past, k_own, v_own, grad, lse, cosine,
            sine, lambda here, cols, value: line.__setitem__((step, here, cols), value),
            dk_past, dk_own, dv_past, dv_own,
        )

        @pl.when(parity == 0)
        def _():
            mine_past[step] = dk_past[...] * scale
            mine_own[step] = dk_own[...] * scale
            other_past[step] = dv_past[...]
            other_own[step] = dv_own[...]

        @pl.when(parity != 0)
        def _():
            mine_past[step] = dv_past[...]
            mine_own[step] = dv_own[...]
            other_past[step] = dk_past[...] * scale
            other_own[step] = dk_own[...] * scale

    for r in range(slots):

        def start(r=r):
            pasts[r].start()
            owns[r].start()

        pl.when(step == r)(start)

    for pair in range(0, slots, 2):

        def merge(pair=pair):
            for r in (pair, pair + 1):
                pasts[r ^ 1].wait_recv()
                side_out[r] = (mine_past[r] + got_past[r]).astype(LOW)
                sides[r].start()

        pl.when(step == pair + 1)(merge)

    @pl.when(step >= slots)
    def _():
        out_grad[...] = dot_rows(branch[...], mixed[...]).astype(LOW)

    @pl.when(step == slots + tiles - 1)
    def _():
        for r in range(slots):
            owns[r ^ 1].wait_recv()
            sides[r].wait_recv()
            total = mine_own[r] + got_own[r] + side_in[r].astype(WIDE)
            back = turn_back(total, cosine_all[r], sine_all[r])
            line[r, :, heads * head_dim :] = jnp.where(parity == 0, back, total).astype(LOW)
        loading.wait()
        for copy in lasts:
            copy.wait_recv()
        block[...] = (
            middle[...] + own_rows[...].astype(WIDE) + last_in[0].astype(WIDE) + last_in[1].astype(WIDE)
        ).astype(LOW)
        for copy in (*pasts, *owns, *sides, *lasts):
            copy.wait_send()


def attend_exchange(
    info, q, k_past, v_past, k_own, v_own, weight, lse, cosine, sine, heads, head_dim, scale, branch, mixed, mlp,
    middle
):
    count, length, width = q.shape
    past = k_past.shape[1]
    tokens, model_width = branch.shape
    tile = 256
    tiles = model_width // tile
    slot = lambda i: jnp.minimum(i, count - 1)
    by_slot = lambda *shape: pl.BlockSpec((1, *shape), lambda i, info: (slot(i),) + (0,) * len(shape))
    column = lambda i: jnp.clip(i - count, 0, tiles - 1)
    held = lambda *shape: pl.BlockSpec(
        shape, lambda i, info: (0,) * len(shape), pipeline_mode=pl.Buffered(1)
    )
    line_cols = width + head_dim
    return pl.pallas_call(
        functools.partial(exchange_kernel, heads, head_dim, scale, count, tiles),
        grid_spec=pltpu.PrefetchScalarGridSpec(
            num_scalar_prefetch=1,
            grid=(count + tiles,),
            in_specs=[
                by_slot(length, width),
                by_slot(past, head_dim),
                by_slot(past, head_dim),
                by_slot(length, head_dim),
                by_slot(length, head_dim),
                pl.BlockSpec((length, model_width), lambda i, info: (slot(i), 0)),
                held(*weight.shape),
                by_slot(length, 128),
                by_slot(length, head_dim),
                by_slot(length, head_dim),
                held(count, length, head_dim),
                held(count, length, head_dim),
                pl.BlockSpec((tokens, tile), lambda i, info: (0, column(i))),
                held(*mixed.shape),
            ]
            + [ANYWHERE] * 3
            + [held(length, model_width)],
            out_specs=[
                held(count, length, line_cols),
                pl.BlockSpec((tile, width), lambda i, info: (column(i), 0)),
                held(length, model_width),
            ],
            scratch_shapes=[pltpu.VMEM((count, length, head_dim), WIDE)] * 6
            + [pltpu.VMEM((count, length, head_dim), LOW)] * 2
            + [pltpu.VMEM((length, head_dim), WIDE)] * 4
            + [
                pltpu.VMEM((length, model_width), LOW),
                pltpu.VMEM((2, length, model_width), LOW),
                pltpu.VMEM((1, length, width), LOW),
                pltpu.SemaphoreType.DMA((3 * count + 2,)),
                pltpu.SemaphoreType.DMA((3 * count + 2,)),
                pltpu.SemaphoreType.DMA,
            ],
        ),
        out_shape=[
            jax.ShapeDtypeStruct((count, length, line_cols), LOW),
            jax.ShapeDtypeStruct((model_width, width), LOW),
            jax.ShapeDtypeStruct((length, model_width), LOW),
        ],
        compiler_params=pltpu.CompilerParams(
            vmem_limit_bytes=63 << 20, collective_id=4, has_side_effects=True
        ),
        cost_estimate=estimate(2 * tokens * model_width * width, 10 * tokens * width),
    )(info, q, k_past, v_past, k_own, v_own, branch, weight, lse, cosine, sine, cosine, sine, branch, mixed, *mlp, middle)


def local(
    hidden_in,
    cotangent,
    seq_lengths,
    positions,
    permutation,
    query_weight,
    keyval_weight,
    output_weight,
    norm_gains,
    bias_query,
    bias_keyval,
    gate_weight,
    up_weight,
    down_weight,
):
    group_rank = lax.axis_index("fsdp")
    ctx_rank = lax.axis_index("ctx")
    tensor_rank = lax.axis_index("tp")
    fsdp_count = lax.axis_size("fsdp")
    ctx_count = lax.axis_size("ctx")
    tensor_count = lax.axis_size("tp")
    seq_grp, local_len, model_width = hidden_in.shape
    heads, head_dim = bias_query.shape
    keyval_heads = bias_keyval.shape[0] // 2
    assert seq_grp == tensor_count == fsdp_count == len(DEAL_SHIFT)
    token_count = seq_grp * local_len
    scale = 1.0 / math.sqrt(head_dim)
    offset = ctx_rank * local_len
    head_pair = tensor_rank // (tensor_count // keyval_heads)
    parity = tensor_rank % 2
    assert DEAL_SHIFT == tuple((t % 2) * 2 + t // 2 for t in range(tensor_count))

    entry = jnp.arange(permutation.shape[0])
    entry_group, entry_slot = entry // seq_grp, entry % seq_grp
    home_group, home_slot = lax.div(permutation, seq_grp), lax.rem(permutation, seq_grp)
    places = jnp.arange(2 * seq_grp)
    near_places = places < seq_grp
    slot_rank = tensor_rank ^ (places % seq_grp)
    shift_of = lambda rank: lax.rem(rank, 2) * 2 + lax.div(rank, 2)
    target = lax.rem(group_rank + shift_of(tensor_rank), fsdp_count)
    leaving = jnp.sum(jnp.where((entry_group == target) & (home_group == group_rank), home_slot, 0))
    source = lax.rem(group_rank + fsdp_count - shift_of(slot_rank), fsdp_count)
    hit = (entry_group == group_rank)[None] & (home_group[None] == source[:, None])
    slot_now = jnp.sum(jnp.where(hit, entry_slot[None], 0), axis=1)
    seq_now = jnp.sum(jnp.where(hit, permutation[None], 0), axis=1)
    targets = lax.rem(group_rank + shift_of(slot_rank), fsdp_count)
    back_hit = (entry_group[None] == targets[:, None]) & (home_group == group_rank)[None]
    home_order = jnp.sum(jnp.where(back_hit, home_slot[None], 0), axis=1)[:seq_grp]
    there = [
        (f * tensor_count + t, (f + DEAL_SHIFT[t]) % fsdp_count * tensor_count + t)
        for f in range(fsdp_count)
        for t in range(tensor_count)
    ]
    back = [(target, source) for source, target in there]

    split = units_split()
    head_width = 2 * head_dim
    query_cols = heads * head_dim
    near_cols = query_cols + head_width + 128

    outgoing = lax.dynamic_index_in_dim(hidden_in, leaving, 0, keepdims=False)
    own_in = lax.ppermute(outgoing, ("fsdp", "tp"), there)
    small = jnp.concatenate(
        [
            query_weight,
            lax.dynamic_slice_in_dim(keyval_weight, head_pair * head_width, head_width, axis=1),
            jnp.pad(norm_gains.T, ((0, 0), (0, 128 - norm_gains.shape[0]))),
            output_weight.T,
        ],
        axis=1,
    )
    seq_hit = seq_now[:, None] == entry[None]
    lengths_now = jnp.sum(jnp.where(seq_hit, seq_lengths[None], 0), axis=1)
    more = jnp.where(places == seq_grp, offset, jnp.where(places == seq_grp + 1, parity, 0))
    info = jnp.where(near_places, lengths_now, more).astype(jnp.int32)
    positions_now = jnp.sum(
        jnp.where(seq_hit[:seq_grp, :, None], positions[None], 0), axis=1
    )
    lane = jnp.arange(head_dim)
    frequency = 1.0 / ROPE_BASE ** ((lane % (head_dim // 2)).astype(WIDE) * 2.0 / head_dim)
    angles = positions_now.astype(WIDE)[..., None] * frequency
    cosine = jnp.cos(angles)
    sine = jnp.sin(angles) * jnp.where(lane < head_dim // 2, -1.0, 1.0)
    pick_info = jnp.where(near_places, slot_now, slot_now ^ tensor_rank).astype(jnp.int32)
    units = gate_weight.shape[1]
    units_pad = -(-units // 256) * 256
    widen = lambda w: jnp.pad(w, ((0, 0), (0, units_pad - units)))
    shards = [widen(w) for w in (down_weight.T, gate_weight, up_weight)]
    if split:
        half_units = units_pad // 2
        cut = lambda w, c: lax.dynamic_slice_in_dim(w, c * half_units, half_units, axis=1)

        def in_order(own, other):
            return jnp.stack(
                [jnp.where(ctx_rank == 0, own, other), jnp.where(ctx_rank == 0, other, own)]
            )

        def all_rows(both, *earlier):
            full = lax.all_gather(after(both, *earlier), "fsdp", axis=0, tiled=False)
            return full.reshape(-1, both.shape[-1])

        first_units = half_units - half_units // 2 // 256 * 256
        first_cols = 3 * first_units

        def in_parts(c):
            halves = [cut(w, c) for w in shards]
            return jnp.concatenate(
                [w[:, :first_units] for w in halves] + [w[:, first_units:] for w in halves], axis=1
            )

        leaving_units, own_units = in_parts(1 - ctx_rank), in_parts(ctx_rank)
        slot_pick = lax.dynamic_index_in_dim(cotangent, tensor_rank, 0, keepdims=False)
        small = after(small, outgoing, leaving_units, cosine, sine, slot_pick)
        small_both = in_order(small, from_partner(small, "ctx", 1))
        arriving_units = from_partner(after(leaving_units, small_both), "ctx", 1)
        other_own = from_partner(after(slot_pick, arriving_units), "ctx", 1)
        both_a = in_order(own_units[:, :first_cols], arriving_units[:, :first_cols])
        both_b = in_order(own_units[:, first_cols:], arriving_units[:, first_cols:])
    else:
        all_rows = lambda shard, *earlier: lax.all_gather(
            shard, ("fsdp", "ctx"), axis=0, tiled=True
        )
        small_both, unit_both, half_units = small, jnp.concatenate(shards, axis=1), units_pad
    far_in = from_partner(own_in, "tp", 2)
    near_in = from_partner(own_in, "tp", 1)
    ready = (info, pick_info, own_units, home_order) if split else (cosine, sine, info)
    cross_in = from_partner(after(far_in, *ready), "tp", 1)

    near_full = all_rows(small_both, own_in)
    if split:
        units_a = all_rows(both_a, cross_in)
        units_b = all_rows(both_b, cross_in)
    else:
        down_full = all_rows(unit_both[..., :half_units], cross_in)
        gate_up_full = all_rows(unit_both[..., half_units:], cross_in)
    output_full = near_full[:, near_cols:]
    bias_head = lax.dynamic_slice_in_dim(bias_keyval, head_pair * 2, 2, axis=0)
    bias_row = jnp.concatenate([bias_query.reshape(1, -1), bias_head.reshape(1, -1)], axis=1).astype(WIDE)
    normed_one, query_rot, key_own, value_own = project(
        (own_in, near_in, far_in, cross_in),
        near_full,
        bias_row,
        after(cosine, other_own, both_a, both_b, info, pick_info) if split else cosine,
        sine,
        heads,
        head_dim,
    )
    gains_now = near_full[:, query_cols + head_width : near_cols][:, :2].astype(WIDE).T
    if split:
        key_past, value_past = lax.ppermute((key_own, value_own), "ctx", [(0, 1)])
        other_far = from_partner(other_own, "tp", 2)
        other_near = from_partner(after(other_own, key_past), "tp", 1)
        other_cross = from_partner(after(other_far, key_past), "tp", 1)
        other_rows = (other_own, other_near, other_far, other_cross)
        key_past = after(key_past, other_far)
    else:
        key_past = lax.all_gather(key_own, "ctx", axis=1, tiled=True)
        value_past = lax.all_gather(value_own, "ctx", axis=1, tiled=True)
    project_full = after(near_full, query_rot)[:, : query_cols + head_width]
    own_weight = lax.dynamic_slice_in_dim(
        project_full, query_cols + parity * head_dim, head_dim, axis=1
    )
    back_full = jnp.concatenate([project_full[:, :query_cols], own_weight], axis=1)
    in_share = own_in.astype(WIDE)
    if split:
        mixed, lse, middle_share, normed_share = attend_sum(
            info,
            query_rot,
            key_past,
            value_past,
            key_own,
            value_own,
            after(output_full, back_full),
            own_in,
            gains_now[1:2],
            heads,
            head_dim,
            scale,
        )
    else:
        attend = lambda first, *held: attend_forward(
            info, query_rot, *held, key_own, value_own, output_full, heads, head_dim, scale, first, 2
        )

        mixed_far, lse_far, *attn_far = attend(2, key_past, value_past)
        attn_wide = collect_far(attn_far[0], attn_far[1])
        attn_got = from_partner(attn_wide, "tp", 2)
        mixed_near, lse_near, *attn_near = attend(0, after(key_past, attn_wide), value_past)
        attn_core = from_partner(attn_near[1], "tp", 1)
        middle_share = (
            in_share
            + attn_near[0].astype(WIDE)
            + attn_core.astype(WIDE)
            + attn_got.astype(WIDE)
        )
        inv_two = lax.rsqrt(jnp.mean(middle_share * middle_share, axis=-1, keepdims=True) + EPS)
        normed_share = (middle_share * inv_two * gains_now[1]).astype(LOW)
        mixed = jnp.concatenate([mixed_near, mixed_far], axis=0)
        lse = jnp.concatenate([lse_near, lse_far], axis=0)
    half_len = local_len // 2

    if split:
        grad_hidden, grad_rows = chosen_rows(
            pick_info,
            after(cotangent, normed_share),
            other_rows,
            units_a,
            0,
            3,
        )
    else:
        grad_slots = [
            lax.dynamic_index_in_dim(cotangent, slot_now[r], 0, keepdims=False) for r in range(seq_grp)
        ]
        grad_hidden, grad_rows = stack_rows([(g,) for g in grad_slots], down_full, 0, 1)

    def spread_all(own):
        far = from_partner(own, "tp", 2)
        near = from_partner(own, "tp", 1)
        if not split:
            return (own, near, far, from_partner(far, "tp", 1))
        side = from_partner(own, "ctx", 1)
        held = after(far, grad_hidden), after(side, grad_hidden)
        across = from_partner(held[0][:half_len], "ctx", 1), from_partner(held[1][half_len:], "tp", 2)
        cores = [from_partner(v, "tp", 1) for v in held]
        return (own, near, far, cores[0], side, cores[1], *across)

    def in_slots(rows):
        if not split:
            return [(row,) for row in rows]
        return [(row,) for row in rows[:6]] + [rows[6:]]

    mixed_flat = mixed.reshape(token_count, query_cols)
    normed_slots = in_slots(spread_all(normed_share))
    if split:
        ahead = stack_rows(normed_slots[:6], units_a, 1, 3, total=8)
        last = [normed_slots[6], tuple(from_partner(after(v, ahead[0]), "tp", 1) for v in normed_slots[6])]
        gate_lin, normed_two = stack_rows(last, units_a, 1, 3, into=ahead, first=6, total=8)
        hidden_a, gate_a, up_a = hidden_units(normed_two, units_a, 2, 3, gate_lin, grad_hidden)
        grad_a = first_grads(grad_rows, normed_two, hidden_a, gate_a, up_a)
        hidden_b, gate_b, up_b = full_units(after(normed_two, grad_a), grad_rows, units_b)
    else:
        gate_lin, normed_two = stack_rows(normed_slots, gate_up_full, 0, 2)
        hidden_act, grad_gate, grad_up = hidden_units(
            normed_two, gate_up_full, 1, 2, gate_lin, grad_hidden
        )

    def collect_all(lefts, weights, *earlier):
        lefts = list(lefts)
        lefts[0] = after(lefts[0], *earlier)
        last = back_rows(lefts, weights, 2, 2, local_len)
        got = [from_partner(collect_far(last[0], last[1]), "tp", 2)]
        first = back_rows(lefts, weights, 0, 2, local_len)
        got.append(from_partner(first[1], "tp", 1))

        def finish():
            return sum((v.astype(WIDE) for v in got), first[0].astype(WIDE))

        return first[0], finish

    if split:
        grad_two_share, down_b, up_grad_b = collect_back(
            (gate_a, up_a),
            (gate_b, up_b),
            units_a,
            units_b,
            grad_rows,
            normed_two,
            hidden_b,
            local_len,
        )
        grad_middle, gain_two, gate_grad_b, grad_branch, *mlp = spread_branch(
            grad_two_share,
            middle_share,
            grad_rows,
            gains_now[1:2],
            hidden_a,
            hidden_b,
            units_a,
            units_b,
            normed_two,
            gate_b,
        )
        mlp_own, mlp_far, mlp_side = mlp
        grad_branch = grad_branch.reshape(token_count, model_width)
    else:
        first_back, finish_back = collect_all(
            (grad_gate, grad_up), ((gate_up_full, 0, 2), (gate_up_full, 1, 2))
        )
        down_grad = contract_rows(after(grad_rows, first_back), hidden_act, LOW)
        gate_grad = contract_rows(normed_two, after(grad_gate, down_grad), LOW)
        grad_two_share = finish_back()
        grad_norm_two, gain_two = norm_backward(
            middle_share, inv_two, gains_now[1], grad_two_share
        )
        grad_middle = grad_slots[0].astype(WIDE) + grad_norm_two
        branch_own = grad_middle.astype(LOW)
        branch_far = from_partner(branch_own, "tp", 2)
        branch_near = from_partner(branch_own, "tp", 1)
        branch_cross = from_partner(branch_far, "tp", 1)
        grad_branch = jnp.concatenate([branch_own, branch_near, branch_far, branch_cross], axis=0)
        up_grad = contract_rows(normed_two, after(grad_up, branch_own), LOW)

    grad_mixed = None if split else product(grad_branch, output_full, LOW)
    attend_args = (
        info,
        query_rot,
        key_past,
        value_past,
        key_own,
        value_own,
        output_full if split else grad_mixed.reshape(seq_grp, local_len, query_cols),
        lse,
        cosine,
        sine,
        heads,
        head_dim,
        scale,
    )
    if split:
        line_grad, output_grad, block_share = attend_exchange(
            *attend_args,
            grad_branch,
            mixed_flat,
            (mlp_far, mlp_side, mlp_own),
            middle_share,
        )
        line_grad = line_grad.reshape(token_count, -1)
    else:
        grad_query, mine_past, mine_own, other_past, other_own = attend_backward(*attend_args)
        swap = lambda value: jnp.stack([value[r ^ 1] for r in range(seq_grp)])
        got_past, got_own = from_partner((other_past, other_own), "tp", 1)
        past_sum = mine_past + swap(got_past)
        own_sum = mine_own + swap(got_own)
        own_sum = own_sum + lax.psum_scatter(past_sum, "ctx", scatter_dimension=1, tiled=True)
        half_lanes = head_dim // 2
        turned = own_sum * cosine - jnp.roll(own_sum, half_lanes, axis=-1) * sine
        own_grad = jnp.where(parity == 0, turned, own_sum).astype(LOW).reshape(token_count, head_dim)
        line_grad = jnp.concatenate([grad_query.reshape(token_count, query_cols), own_grad], axis=1)
    def scatter_units(grad):
        if not split:
            return scatter_sum(grad, ctx_rank, LOW)
        return lax.psum_scatter(grad, "fsdp", scatter_dimension=0, tiled=True)

    unit_grads = (grad_a, down_b, up_grad_b, gate_grad_b) if split else (down_grad, gate_grad, up_grad)
    unit_sums = [scatter_units(unit_grads[0])]
    if split:
        unit_sums += [scatter_units(after(g, unit_sums[0])) for g in unit_grads[1:3]]
        unit_sums += [scatter_units(after(unit_grads[3], unit_sums[0]))]
    else:
        unit_sums += [scatter_units(g) for g in unit_grads[1:]]

    normed_flat = normed_one.reshape(token_count, model_width)
    if split:
        input_share, gain_grad, attn_grad, bias_grad, block_home, *unit_gots = finish_rows(
            line_grad,
            back_full,
            own_in,
            grad_middle,
            gains_now[0:1],
            gain_two,
            normed_flat,
            block_share,
            unit_sums,
        )
        attn_grad = jnp.concatenate([attn_grad, output_grad], axis=1)
    else:
        half = token_count // 2
        line_far = contract_cols(line_grad[half:], back_full, LOW).reshape(2, local_len, model_width)
        line_near = contract_cols(line_grad[:half], back_full, LOW).reshape(2, local_len, model_width)
        line_wide = collect_far(line_far[0], line_far[1])
        line_got = from_partner(line_wide, "tp", 2)
        line_core = from_partner(line_near[1], "tp", 1)
        first_mlp, finish_mlp = collect_all((hidden_act,), ((down_full, 0, 1),), up_grad, branch_far)
        block_share = (middle_share + finish_mlp()).astype(LOW)
        grad_one_share = line_near[0].astype(WIDE) + line_core.astype(WIDE) + line_got.astype(WIDE)
        inv_one = lax.rsqrt(jnp.mean(in_share * in_share, axis=-1, keepdims=True) + EPS)
        grad_norm_one, gain_one = norm_backward(in_share, inv_one, gains_now[0], grad_one_share)
        input_share = (grad_middle + grad_norm_one).astype(LOW)
        attn_grad = jnp.concatenate(
            [contract_rows(normed_flat, line_grad, LOW), contract_rows(grad_branch, mixed_flat, LOW)],
            axis=1,
        )
        bias_grad = jnp.sum(line_grad.astype(WIDE), axis=0)

    shard_count = fsdp_count * ctx_count
    share = head_dim // shard_count
    if not split:
        gain_grad = jnp.concatenate([gain_one, gain_two], axis=0)
        gain_grad = gain_grad + from_partner(gain_grad, "tp", 1)
        gain_grad = gain_grad + from_partner(gain_grad, "tp", 2)
    bias_cols = jnp.transpose(bias_grad.reshape(heads + 1, shard_count, share), (1, 2, 0))
    bias_cols = jnp.pad(bias_cols, ((0, 0), (0, (model_width - head_dim) // shard_count), (0, 0)))
    tiny = jnp.concatenate([gain_grad.T, bias_cols.reshape(model_width, heads + 1)], axis=1)
    tiny = jnp.pad(tiny, ((0, 0), (0, 128 - tiny.shape[1]))).astype(LOW)
    attn_grad = jnp.concatenate([attn_grad, tiny], axis=1)
    if split:
        attn_blocks = attn_grad.reshape(fsdp_count, ctx_count, -1, attn_grad.shape[1])
        kept, sent = scatter_ctx(attn_blocks, ctx_rank)
        attn_held = (kept.astype(WIDE) + from_partner(sent, "ctx", 1).astype(WIDE)).astype(LOW)
        attn_held = attn_held.reshape(-1, attn_grad.shape[1])
        attn_end = lax.psum_scatter(after(attn_held, *unit_sums), "fsdp", scatter_dimension=0, tiled=True)
    else:
        attn_end = scatter_sum(attn_grad, ctx_rank, LOW, *unit_sums)


    def leave(share):
        return lax.ppermute(share, ("fsdp", "tp"), back)

    def arrive(own, *earlier):
        far = from_partner(own, "tp", 2)
        near = from_partner(own, "tp", 1)
        return (own, near, far, from_partner(after(far, *earlier), "tp", 1))

    input_home = leave(input_share)
    if not split:
        block_home = leave(block_share)
    block_out = place_rows(arrive(block_home), home_order)
    if split:
        input_home = after(input_home, attn_held)
        input_rows = arrive(input_home, block_out)
    else:
        input_rows = arrive(input_home)
    input_grad = place_rows(input_rows, home_order)

    small_at = query_cols + head_dim + query_cols
    tiny_grad = attn_end[:, small_at:].astype(WIDE)

    if split:

        def own_half(total):
            rows = total.shape[0] // 2
            return lax.dynamic_slice_in_dim(total, ctx_rank * rows, rows, axis=0)

        (own_a, got_a), *ends = [(own_half(t), got) for t, got in zip(unit_sums, unit_gots)]

        def joined(part, end):
            cols = slice(part * first_units, (part + 1) * first_units)
            own = jnp.concatenate([own_a[:, cols], end[0]], axis=1)
            got = jnp.concatenate([got_a[:, cols], end[1]], axis=1)
            first, second = jnp.where(ctx_rank == 0, own, got), jnp.where(ctx_rank == 0, got, own)
            return jnp.concatenate([first, second], axis=1)[:, :units].astype(WIDE)

        down_end, gate_end, up_end = joined(0, ends[0]), joined(1, ends[2]), joined(2, ends[1])
    else:
        down_end, gate_end, up_end = (t[:, :units].astype(WIDE) for t in unit_sums)
    return (
        block_out,
        input_grad,
        attn_end[:, :query_cols].astype(WIDE),
        attn_end[:, query_cols : query_cols + head_dim].astype(WIDE),
        attn_end[:, query_cols + head_dim : small_at].astype(WIDE).T,
        tiny_grad[:, :2].T,
        tiny_grad[:share, 2 : 2 + heads].T,
        tiny_grad[:share, 2 + heads : 3 + heads].T,
        gate_end,
        up_end,
        down_end.T,
    )


def solution(mesh):
    placed = (
        P("fsdp", "ctx", None),
        P("fsdp", "ctx", None),
        P(),
        P(None, "ctx"),
        P(),
        P(("fsdp", "ctx"), "tp"),
        P(("fsdp", "ctx"), None),
        P("tp", ("fsdp", "ctx")),
        P(None, ("fsdp", "ctx")),
        P("tp", None),
        P(),
        P(("fsdp", "ctx"), "tp"),
        P(("fsdp", "ctx"), "tp"),
        P("tp", ("fsdp", "ctx")),
    )
    return jax.shard_map(
        local,
        mesh=mesh,
        in_specs=placed,
        out_specs=(
            P("fsdp", "ctx", None),
            P("fsdp", "ctx", None),
            P(("fsdp", "ctx"), "tp"),
            P(("fsdp", "ctx"), "tp"),
            P("tp", ("fsdp", "ctx")),
            P(None, ("fsdp", "ctx")),
            P("tp", ("fsdp", "ctx")),
            P("tp", ("fsdp", "ctx")),
            P(("fsdp", "ctx"), "tp"),
            P(("fsdp", "ctx"), "tp"),
            P("tp", ("fsdp", "ctx")),
        ),
        check_vma=False,
    )
```

```python
import functools
import math

import jax
import jax.numpy as jnp
from jax import lax
from jax.experimental import pallas as pl
from jax.experimental.pallas import tpu as pltpu
from jax.sharding import PartitionSpec as P

EPS = 1e-06
ROPE_BASE = 10000.0
NEG_FILL = -1e30
LOW = jnp.bfloat16
WIDE = jnp.float32
DEAL_SHIFT = (0, 2, 1, 3)


def from_partner(value, axis, apart):
    pairs = [(source, source ^ apart) for source in range(lax.axis_size(axis))]
    return lax.ppermute(value, axis, pairs)


def product(left_side, right_side, kind=WIDE):
    return jnp.dot(left_side, right_side, preferred_element_type=WIDE).astype(kind)


def contract_rows(left_side, right_side, kind=WIDE):
    return lax.dot_general(
        left_side, right_side, (((0,), (0,)), ((), ())), preferred_element_type=WIDE
    ).astype(kind)


def contract_cols(left_side, right_side, kind=WIDE):
    return lax.dot_general(
        left_side, right_side, (((1,), (1,)), ((), ())), preferred_element_type=WIDE
    ).astype(kind)


def norm_backward(values, scale_inv, gain_row, upstream):
    scaled = gain_row * upstream
    inner_mean = jnp.mean(values * scaled, axis=-1, keepdims=True)
    grad_in = scale_inv * scaled - values * (scale_inv * scale_inv * scale_inv) * inner_mean
    gain_grad = jnp.sum(upstream * values * scale_inv, axis=0, keepdims=True)
    return (grad_in, gain_grad)


def after(value, *earlier):
    return lax.optimization_barrier((value, *earlier))[0]


def collect_far(far_part, cross_part):
    wide = far_part.astype(WIDE) + from_partner(cross_part, "tp", 1).astype(WIDE)
    return wide.astype(LOW)


def units_split():
    return lax.axis_size("ctx") == 2


def all_rows(shard):
    return lax.all_gather(shard, "fsdp", axis=0, tiled=True)


def scatter_ctx(blocks, ctx_rank):
    kept = lax.dynamic_index_in_dim(blocks, ctx_rank, 1, keepdims=False)
    sent = lax.dynamic_index_in_dim(blocks, 1 - ctx_rank, 1, keepdims=False)
    return kept, sent


def scatter_sum(grad, ctx_rank, kind, *earlier):
    fsdp_count, ctx_count = lax.axis_size("fsdp"), lax.axis_size("ctx")
    rows, cols = grad.shape
    blocks = grad.reshape(fsdp_count, ctx_count, rows // (fsdp_count * ctx_count), cols)
    if ctx_count == 2:
        kept, sent = scatter_ctx(blocks, ctx_rank)
        got = from_partner(sent, "ctx", 1)
        held = (after(kept, *earlier).astype(WIDE) + got.astype(WIDE)).astype(kind)
    else:
        swapped = jnp.swapaxes(blocks, 0, 1).reshape(rows, cols)
        held = lax.psum_scatter(swapped, "ctx", scatter_dimension=0, tiled=True)
    held = held.reshape(rows // ctx_count, cols)
    return lax.psum_scatter(held, "fsdp", scatter_dimension=0, tiled=True)


def estimate(flops, moved, transcendentals=0):
    return pl.CostEstimate(flops=flops, bytes_accessed=moved, transcendentals=transcendentals)


def part_spec(rows, cols, part):
    return pl.BlockSpec((rows, cols), lambda *_: (0, part), pipeline_mode=pl.Buffered(1))


def whole_spec(*shape, once=False):
    mode = {"pipeline_mode": pl.Buffered(1)} if once else {}
    return pl.BlockSpec(shape, lambda *_: (0,) * len(shape), **mode)


def rows_kernel(groups, *refs):
    slot = pl.program_id(0)
    weight, (lin, stacked) = refs[sum(groups)], refs[-2:]

    def run(pieces):
        start = 0
        for piece in pieces:
            stacked[start : start + piece.shape[0]] = piece[...]
            start += piece.shape[0]
        lin[...] = jnp.dot(stacked[...], weight[...], preferred_element_type=WIDE).astype(LOW)

    first = 0
    for r, pieces in enumerate(groups):
        pl.when(slot == r)(functools.partial(run, refs[first : first + pieces]))
        first += pieces


def stack_rows(slots, weight, part, parts, into=None, first=0, total=None):
    groups = [len(s) for s in slots]
    rows = [piece for s in slots for piece in s]
    width, length = rows[0].shape[1], sum(piece.shape[0] for piece in slots[0])
    count, cols = len(slots), weight.shape[1] // parts
    total = total or count
    into = into or ()
    return pl.pallas_call(
        functools.partial(rows_kernel, groups),
        grid=(count,),
        in_specs=[whole_spec(*piece.shape, once=True) for piece in rows]
        + [part_spec(width, cols, part)]
        + [pl.BlockSpec(memory_space=pl.ANY)] * len(into),
        out_specs=[
            pl.BlockSpec((length, cols), lambda s: (first + s, 0)),
            pl.BlockSpec((length, width), lambda s: (first + s, 0)),
        ],
        out_shape=[
            jax.ShapeDtypeStruct((total * length, cols), LOW),
            jax.ShapeDtypeStruct((total * length, width), LOW),
        ],
        input_output_aliases={len(rows) + 1 + i: i for i in range(len(into))},
        compiler_params=pltpu.CompilerParams(vmem_limit_bytes=60 << 20),
        cost_estimate=estimate(
            2 * count * length * width * cols, 2 * (count * length * (2 * width + cols) + width * cols)
        ),
    )(*rows, weight, *into)


def units_kernel(h, up, gate, grad, hid, grad_gate, grad_up):
    up_lin = jnp.dot(h[...], up[...], preferred_element_type=WIDE)
    gate_lin = gate[...].astype(WIDE)
    grad_hidden = grad[...].astype(WIDE)
    sigmoid = 1.0 / (1.0 + jnp.exp(-gate_lin))
    silu = gate_lin * sigmoid
    hid[...] = (silu * up_lin).astype(LOW)
    grad_gate[...] = (grad_hidden * up_lin * (sigmoid + silu * (1.0 - sigmoid))).astype(LOW)
    grad_up[...] = (grad_hidden * silu).astype(LOW)


def hidden_units(h, up, part, parts, gate_lin, grad_hidden):
    tokens, width = h.shape
    cols = up.shape[1] // parts
    step = math.gcd(512, tokens)
    by_row = lambda n: pl.BlockSpec((step, n), lambda i: (i, 0))
    return pl.pallas_call(
        units_kernel,
        grid=(tokens // step,),
        in_specs=[by_row(width), part_spec(width, cols, part), by_row(cols), by_row(cols)],
        out_specs=[by_row(cols)] * 3,
        out_shape=[jax.ShapeDtypeStruct((tokens, cols), LOW)] * 3,
        compiler_params=pltpu.CompilerParams(vmem_limit_bytes=60 << 20),
        cost_estimate=estimate(
            2 * tokens * width * cols, 2 * (tokens * width + width * cols + 5 * tokens * cols)
        ),
    )(h, up, gate_lin, grad_hidden)


def back_kernel(terms, *refs):
    lefts, weights, outs = refs[:terms], refs[terms : 2 * terms], refs[2 * terms :]
    total = None
    for left, weight in zip(lefts, weights):
        term = dot_cols(left[...], weight[...])
        total = term if total is None else total + term
    for i, out in enumerate(outs):

        @pl.when(pl.program_id(0) == i)
        def _():
            out[...] = total.astype(LOW)


def back_rows(lefts, weights, first_slot, slots, length):
    width = weights[0][0].shape[0]
    depth = sum(left.shape[1] for left in lefts)
    return pl.pallas_call(
        functools.partial(back_kernel, len(lefts)),
        grid=(slots,),
        in_specs=[
            pl.BlockSpec((length, left.shape[1]), lambda s: (first_slot + s, 0)) for left in lefts
        ]
        + [part_spec(width, w.shape[1] // parts, part) for w, part, parts in weights],
        out_specs=[whole_spec(length, width)] * slots,
        out_shape=[jax.ShapeDtypeStruct((length, width), LOW)] * slots,
        compiler_params=pltpu.CompilerParams(vmem_limit_bytes=60 << 20),
        cost_estimate=estimate(
            2 * slots * length * width * depth,
            2 * (slots * length * (width + depth) + width * depth),
        ),
    )(*lefts, *[w for w, _, _ in weights])


def chosen_kernel(near, count, info, cotangent, *refs):
    slot = pl.program_id(0)
    others, (weight, lin, stacked) = refs[:count], refs[count:]

    @pl.when(slot < near)
    def _():
        stacked[...] = cotangent[0]

    for k, other in enumerate(others):

        @pl.when((slot >= near) & (info[slot] == k))
        def _():
            stacked[...] = other[...]

    lin[...] = jnp.dot(stacked[...], weight[...], preferred_element_type=WIDE).astype(LOW)


def chosen_rows(info, cotangent, others, weight, part, parts):
    near, length, width = cotangent.shape
    slots, cols = near + len(others), weight.shape[1] // parts
    held = lambda rows, n, at: pl.BlockSpec(
        (rows, n), lambda s, info: (0, at), pipeline_mode=pl.Buffered(1)
    )
    return pl.pallas_call(
        functools.partial(chosen_kernel, near, len(others)),
        grid_spec=pltpu.PrefetchScalarGridSpec(
            num_scalar_prefetch=1,
            grid=(slots,),
            in_specs=[
                pl.BlockSpec((1, length, width), lambda s, info: (info[jnp.minimum(s, near - 1)], 0, 0))
            ]
            + [held(length, width, 0)] * len(others)
            + [held(width, cols, part)],
            out_specs=[
                pl.BlockSpec((length, cols), lambda s, info: (s, 0)),
                pl.BlockSpec((length, width), lambda s, info: (s, 0)),
            ],
        ),
        out_shape=[
            jax.ShapeDtypeStruct((slots * length, cols), LOW),
            jax.ShapeDtypeStruct((slots * length, width), LOW),
        ],
        compiler_params=pltpu.CompilerParams(vmem_limit_bytes=60 << 20),
        cost_estimate=estimate(
            2 * slots * length * width * cols, 2 * (slots * length * (2 * width + cols) + width * cols)
        ),
    )(info, cotangent, *others, weight)


def full_units_kernel(h, g, down, gate, up, hid, grad_gate, grad_up):
    gate_lin = jnp.dot(h[...], gate[...], preferred_element_type=WIDE)
    up_lin = jnp.dot(h[...], up[...], preferred_element_type=WIDE)
    grad_hidden = jnp.dot(g[...], down[...], preferred_element_type=WIDE)
    sigmoid = 1.0 / (1.0 + jnp.exp(-gate_lin))
    silu = gate_lin * sigmoid
    hid[...] = (silu * up_lin).astype(LOW)
    grad_gate[...] = (grad_hidden * up_lin * (sigmoid + silu * (1.0 - sigmoid))).astype(LOW)
    grad_up[...] = (grad_hidden * silu).astype(LOW)


def full_units(h, g, weight):
    tokens, width = h.shape
    cols = weight.shape[1] // 3
    step = math.gcd(512, tokens)
    by_row = lambda n: pl.BlockSpec((step, n), lambda i: (i, 0))
    return pl.pallas_call(
        full_units_kernel,
        grid=(tokens // step,),
        in_specs=[by_row(width)] * 2 + [part_spec(width, cols, i) for i in range(3)],
        out_specs=[by_row(cols)] * 3,
        out_shape=[jax.ShapeDtypeStruct((tokens, cols), LOW)] * 3,
        compiler_params=pltpu.CompilerParams(vmem_limit_bytes=60 << 20),
        cost_estimate=estimate(
            6 * tokens * width * cols, 2 * (2 * tokens * width + 3 * width * cols + 3 * tokens * cols)
        ),
    )(h, g, weight, weight, weight)


def first_grads_kernel(g, h, hid, gate, up, out):
    part = pl.program_id(0)
    for i, (left, right) in enumerate(((g, hid), (h, gate), (h, up))):

        @pl.when(part == i)
        def _():
            out[...] = dot_rows(left[...], right[...]).astype(LOW)


def first_grads(grad_rows, rows, hid, grad_gate, grad_up):
    tokens, width = rows.shape
    cols, tile = hid.shape[1], 256
    tiles = width // tile
    return pl.pallas_call(
        first_grads_kernel,
        grid=(3, tiles),
        in_specs=[
            pl.BlockSpec((tokens, tile), lambda p, i: (0, jnp.where(p == 0, i, tiles - 1))),
            pl.BlockSpec((tokens, tile), lambda p, i: (0, jnp.where(p == 0, 0, i))),
        ]
        + [whole_spec(tokens, cols, once=True)] * 3,
        out_specs=pl.BlockSpec((tile, cols), lambda p, i: (i, p)),
        out_shape=jax.ShapeDtypeStruct((width, 3 * cols), LOW),
        compiler_params=pltpu.CompilerParams(vmem_limit_bytes=60 << 20),
        cost_estimate=estimate(6 * tokens * width * cols, 6 * tokens * cols + 6 * width * cols),
    )(grad_rows, rows, hid, grad_gate, grad_up)


MESH_ID = pl.DeviceIdType.MESH


def meet(partners):
    barrier = pltpu.get_barrier_semaphore()
    for partner in partners:
        pl.semaphore_signal(barrier, inc=1, device_id=partner, device_id_type=MESH_ID)
    pl.semaphore_wait(barrier, len(partners))


def partners_of():
    tensor_rank, ctx_rank = lax.axis_index("tp"), lax.axis_index("ctx")
    return {"tp": tensor_rank ^ 1}, {"tp": tensor_rank ^ 2}, {"ctx": ctx_rank ^ 1}


def collect_kernel(
    slots, tiles, gate_a, up_a, gate_b, up_b, w_gate_a, w_up_a, w_gate_b, w_up_b, left, right, hid, up, total,
    down_out, up_out, parts, sent, core_in, across_in, last_in, held, send, recv, load
):
    step = pl.program_id(0)
    steps = pl.num_programs(0)
    core, far, side = partners_of()
    half = total.shape[0] // 2
    remote = remote_copy(send, recv)
    cores = [remote(sent.at[k % 2], core_in.at[k], k, core) for k in range(4)]
    across = [
        remote(parts.at[3, pl.ds(0, half)], across_in.at[0], 4, far),
        remote(parts.at[3, pl.ds(half, half)], across_in.at[1], 5, side),
    ]
    lasts = [
        remote(parts.at[1], last_in.at[0], 6, far),
        remote(parts.at[2, pl.ds(half, half)], last_in.at[1, pl.ds(half, half)], 7, side),
        remote(parts.at[2, pl.ds(0, half)], last_in.at[1, pl.ds(0, half)], 8, side),
    ]
    loading = [
        pltpu.make_async_copy(source, held.at[i], load.at[i]) for i, source in enumerate((hid, up))
    ]

    @pl.when(step == 0)
    def _():
        for copy in loading:
            copy.start()
        meet((core, far, side))

    for k in (2, 3):
        pl.when(step == 2 * k)(cores[k - 2].wait_send)

    @pl.when(step < slots)
    def _():
        part = (
            dot_cols(gate_a[...], w_gate_a[...])
            + dot_cols(up_a[...], w_up_a[...])
            + dot_cols(gate_b[...], w_gate_b[...])
            + dot_cols(up_b[...], w_up_b[...])
        )

        @pl.when(step == slots - 1)
        def _():
            total[...] = part

        for k in range(4):

            @pl.when(step == 2 * k)
            def _():
                sent[k % 2] = part.astype(LOW)
                cores[k].start()

            if k < 3:

                @pl.when(step == 2 * k + 1)
                def _():
                    cores[k].wait_recv()
                    parts[3 - k] = (part + core_in[k].astype(WIDE)).astype(LOW)

    def add(slot, rows, value):
        parts[slot, rows] = (parts[slot, rows].astype(WIDE) + value.astype(WIDE)).astype(LOW)

    low, high = pl.ds(0, half), pl.ds(half, half)

    @pl.when(step == 1)
    def _():
        for copy in across:
            copy.start()

    pl.when(step == 3)(lasts[1].start)

    @pl.when(step == 5)
    def _():
        across[1].wait_recv()
        add(1, high, across_in[1])
        lasts[0].start()
        across[0].wait_recv()
        add(2, low, across_in[0])
        lasts[2].start()

    @pl.when((step >= slots) & (step < slots + tiles))
    def _():
        pl.when(step == slots)(loading[0].wait)
        down_out[...] = dot_rows(left[...], held[0]).astype(LOW)

    @pl.when(step >= slots + tiles)
    def _():
        pl.when(step == slots + tiles)(loading[1].wait)
        up_out[...] = dot_rows(right[...], held[1]).astype(LOW)

    @pl.when(step == steps - 1)
    def _():
        cores[3].wait_recv()
        for copy in lasts:
            copy.wait_recv()
        total[...] += (
            core_in[3].astype(WIDE) + last_in[0].astype(WIDE) + last_in[1].astype(WIDE)
        )
        for copy in (*cores[2:], *across, *lasts):
            copy.wait_send()


def collect_back(first, second, weight_a, weight_b, grad_rows, rows, hid, length):
    tokens, cols_a = first[0].shape
    cols = second[0].shape[1]
    width = weight_a.shape[0]
    slots, tile = tokens // length, 256
    tiles = width // tile
    row = lambda n: pl.BlockSpec((length, n), lambda i: (jnp.maximum(slots - 1 - i, 0), 0))
    column = lambda i, start: jnp.clip(i - start, 0, tiles - 1)
    down_at, up_at = (lambda i: column(i, slots)), (lambda i: column(i, slots + tiles))
    return pl.pallas_call(
        functools.partial(collect_kernel, slots, tiles),
        grid=(slots + 2 * tiles,),
        in_specs=[row(cols_a), row(cols_a), row(cols), row(cols)]
        + [part_spec(width, cols_a, 1), part_spec(width, cols_a, 2)]
        + [part_spec(width, cols, 1), part_spec(width, cols, 2)]
        + [
            pl.BlockSpec((tokens, tile), lambda i: (0, down_at(i))),
            pl.BlockSpec((tokens, tile), lambda i: (0, up_at(i))),
            ANYWHERE,
            ANYWHERE,
        ],
        out_specs=[
            whole_spec(length, width, once=True),
            pl.BlockSpec((tile, cols), lambda i: (down_at(i), 0)),
            pl.BlockSpec((tile, cols), lambda i: (up_at(i), 0)),
        ],
        out_shape=[
            jax.ShapeDtypeStruct((length, width), WIDE),
            jax.ShapeDtypeStruct((width, cols), LOW),
            jax.ShapeDtypeStruct((width, cols), LOW),
        ],
        scratch_shapes=[
            pltpu.VMEM((4, length, width), LOW),
            pltpu.VMEM((2, length, width), LOW),
            pltpu.VMEM((4, length, width), LOW),
            pltpu.VMEM((2, length // 2, width), LOW),
            pltpu.VMEM((2, length, width), LOW),
            pltpu.VMEM((2, tokens, cols), LOW),
            pltpu.SemaphoreType.DMA((9,)),
            pltpu.SemaphoreType.DMA((9,)),
            pltpu.SemaphoreType.DMA((2,)),
        ],
        compiler_params=pltpu.CompilerParams(
            vmem_limit_bytes=63 << 20, collective_id=1, has_side_effects=True
        ),
        cost_estimate=estimate(6 * tokens * width * cols, 10 * tokens * cols),
    )(*first, *second, weight_a, weight_a, weight_b, weight_b, grad_rows, rows, hid, second[1])


def remote_copy(send, recv):
    def make(source, target, index, partner):
        return pltpu.make_async_remote_copy(
            source, target, send.at[index], recv.at[index], device_id=partner, device_id_type=MESH_ID
        )

    return make


def branch_kernel(
    slots, tiles, total, middle, own_grad, gain, hid_a, hid_b, w_a, w_b, turned, gate, grad_middle, gain_grad,
    gate_out, branch, mlp_own, mlp_far, mlp_side, own, parts, core_in, across_in, held, send, recv, load
):
    step = pl.program_id(0)
    core, far, side = partners_of()
    remote = remote_copy(send, recv)
    to_far = remote(own, branch.at[2], 0, far)
    to_near = remote(own, branch.at[1], 1, core)
    to_cross = remote(branch.at[2], branch.at[3], 2, core)
    keep = pltpu.make_async_copy(own, branch.at[0], load.at[0])
    loading = pltpu.make_async_copy(gate, held, load.at[1])
    cores = [remote(parts.at[7 - 2 * k], core_in.at[k], 3 + k, core) for k in range(4)]
    across = remote(parts.at[6], across_in, 7, side)
    stores = [
        pltpu.make_async_copy(parts.at[4], mlp_side, load.at[2]),
        pltpu.make_async_copy(parts.at[2], mlp_far, load.at[3]),
        pltpu.make_async_copy(parts.at[0], mlp_own, load.at[4]),
    ]

    @pl.when(step == 0)
    def _():
        loading.start()
        meet((core, far, side))
        values, upstream = middle[...], total[...]
        inverse = lax.rsqrt(jnp.mean(values * values, axis=-1, keepdims=True) + EPS)
        grad_in, gain_grad[...] = norm_backward(values, inverse, gain[...], upstream)
        grad_in = own_grad[...].astype(WIDE) + grad_in
        grad_middle[...] = grad_in
        own[...] = grad_in.astype(LOW)
        for copy in (to_far, to_near, keep):
            copy.start()

    @pl.when(step < slots)
    def _():
        part = dot_cols(hid_a[...], w_a[...]) + dot_cols(hid_b[...], w_b[...])
        parts[slots - 1 - step] = part.astype(LOW)

    for k in range(4):
        pl.when(step == 2 * k)(cores[k].start)

        def finish(k=k):
            slot = 6 - 2 * k
            cores[k].wait_recv()
            parts[slot] = (parts[slot].astype(WIDE) + core_in[k].astype(WIDE)).astype(LOW)
            if k == 0:
                across.start()
            if k == 1:
                stores[0].start()
            if k == 3:
                stores[2].start()

        pl.when(step == 2 * k + 1)(finish)

    @pl.when(step >= slots)
    def _():
        pl.when(step == slots)(loading.wait)
        gate_out[...] = dot_rows(turned[...], held[...]).astype(LOW)

    @pl.when(step == slots + tiles - 2)
    def _():
        to_far.wait_recv()
        to_cross.start()

    @pl.when(step == slots + tiles - 1)
    def _():
        to_near.wait_recv()
        to_cross.wait_recv()
        across.wait_recv()
        parts[2] = (parts[2].astype(WIDE) + across_in[...].astype(WIDE)).astype(LOW)
        stores[1].start()
        keep.wait()
        for copy in stores:
            copy.wait()
        for copy in (to_far, to_near, to_cross, *cores, across):
            copy.wait_send()


ANYWHERE = pl.BlockSpec(memory_space=pl.ANY)


def spread_branch(total, middle, own_grad, gain, hid_a, hid_b, weight_a, weight_b, rows, grad_gate):
    length, width = total.shape
    tokens, cols = grad_gate.shape
    slots, tile = tokens // length, 256
    tiles = width // tile
    once = whole_spec(length, width, once=True)
    column = lambda i: jnp.clip(i - slots, 0, tiles - 1)
    part = jax.ShapeDtypeStruct((length, width), LOW)
    return pl.pallas_call(
        functools.partial(branch_kernel, slots, tiles),
        grid=(slots + tiles,),
        in_specs=[
            once,
            once,
            once,
            whole_spec(1, width),
            pl.BlockSpec((length, hid_a.shape[1]), lambda i: (jnp.maximum(slots - 1 - i, 0), 0)),
            pl.BlockSpec((length, cols), lambda i: (jnp.maximum(slots - 1 - i, 0), 0)),
            part_spec(width, hid_a.shape[1], 0),
            part_spec(width, cols, 0),
            pl.BlockSpec((tokens, tile), lambda i: (0, column(i))),
            ANYWHERE,
        ],
        out_specs=[
            whole_spec(length, width, once=True),
            whole_spec(1, width),
            pl.BlockSpec((tile, cols), lambda i: (column(i), 0)),
        ]
        + [ANYWHERE] * 4,
        out_shape=[
            jax.ShapeDtypeStruct((length, width), WIDE),
            jax.ShapeDtypeStruct((1, width), WIDE),
            jax.ShapeDtypeStruct((width, cols), LOW),
            jax.ShapeDtypeStruct((4, length, width), LOW),
            part,
            part,
            part,
        ],
        scratch_shapes=[
            pltpu.VMEM((length, width), LOW),
            pltpu.VMEM((slots, length, width), LOW),
            pltpu.VMEM((4, length, width), LOW),
            pltpu.VMEM((length, width), LOW),
            pltpu.VMEM((tokens, cols), LOW),
            pltpu.SemaphoreType.DMA((8,)),
            pltpu.SemaphoreType.DMA((8,)),
            pltpu.SemaphoreType.DMA((5,)),
        ],
        compiler_params=pltpu.CompilerParams(
            vmem_limit_bytes=63 << 20, collective_id=2, has_side_effects=True
        ),
        cost_estimate=estimate(4 * tokens * width * cols, 10 * tokens * cols),
    )(total, middle, own_grad, gain, hid_a, hid_b, weight_a, weight_b, rows, grad_gate)


def line_kernel(
    slots, tiles, count, line, weight, own_in, grad_middle, gain, gain_two, rows_one, line_all, block, *refs
):
    sums, (share, gain_grad, attn_out, bias_out, home) = refs[:count], refs[count : count + 5]
    gots = refs[count + 5 : 2 * count + 5]
    parts, core_in, far_in, total, gains, gains_in, send, recv, load = refs[2 * count + 5 :]
    step = pl.program_id(0)
    core, far, side = partners_of()
    tensor_rank, group = lax.axis_index("tp"), lax.axis_index("fsdp")
    shift = (tensor_rank % 2) * 2 + tensor_rank // 2
    target = {"fsdp": (group + slots - shift) % slots}
    source = {"fsdp": (group + shift) % slots}
    stays = shift == 0
    remote = remote_copy(send, recv)
    cores = [remote(parts.at[3 - 2 * k], core_in.at[k], k, core) for k in range(2)]
    to_far = remote(parts.at[2], far_in, 2, far)
    leave = remote(block, home, 3, target)
    keep = pltpu.make_async_copy(block, home, load)
    cross = {"tp": tensor_rank ^ 3}
    gain_copies = [
        remote(gains, gains_in.at[i], 4 + i, partner) for i, partner in enumerate((core, far, cross))
    ]
    rows = gots[0].shape[0]
    there = pl.multiple_of((1 - lax.axis_index("ctx")) * rows, rows)
    sides = [
        remote(held.at[pl.ds(there, rows)], got, 7 + i, side) for i, (held, got) in enumerate(zip(sums, gots))
    ]

    @pl.when(step == 0)
    def _():
        barrier = pltpu.get_barrier_semaphore()
        for partner in (core, far, cross, side):
            pl.semaphore_signal(barrier, inc=1, device_id=partner, device_id_type=MESH_ID)

        @pl.when(stays)
        def _():
            pl.semaphore_wait(barrier, 4)
            keep.start()

        @pl.when(jnp.logical_not(stays))
        def _():
            for partner in (target, source):
                pl.semaphore_signal(barrier, inc=1, device_id=partner, device_id_type=MESH_ID)
            pl.semaphore_wait(barrier, 6)
            leave.start()

        for copy in sides:
            copy.start()

    @pl.when(step < slots)
    def _():
        part = dot_cols(line[...], weight[...])
        parts[slots - 1 - step] = part.astype(LOW)

        @pl.when(step == slots - 1)
        def _():
            total[...] = part

    for k in range(2):
        pl.when(step == 2 * k)(cores[k].start)

    @pl.when(step == 1)
    def _():
        cores[0].wait_recv()
        parts[2] = (parts[2].astype(WIDE) + core_in[0].astype(WIDE)).astype(LOW)
        to_far.start()

    @pl.when(step == slots - 1)
    def _():
        bias_out[...] = jnp.sum(line_all[...].astype(WIDE), axis=0, keepdims=True)

    @pl.when(step >= slots)
    def _():
        attn_out[...] = dot_rows(rows_one[...], line_all[...]).astype(LOW)

    @pl.when(step == slots + tiles - 1)
    def _():
        cores[1].wait_recv()
        to_far.wait_recv()
        upstream = total[...] + core_in[1].astype(WIDE) + far_in[...].astype(WIDE)
        values = own_in[...].astype(WIDE)
        inverse = lax.rsqrt(jnp.mean(values * values, axis=-1, keepdims=True) + EPS)
        grad_in, gain_one = norm_backward(values, inverse, gain[...], upstream)
        gains[0:1] = gain_one
        gains[1:2] = gain_two[...]
        for copy in gain_copies:
            copy.start()
        share[...] = (grad_middle[...] + grad_in).astype(LOW)
        for copy in gain_copies:
            copy.wait_recv()
        gain_grad[...] = (gains[...] + gains_in[0]) + (gains_in[1] + gains_in[2])
        for copy in sides:
            copy.wait_recv()
        for copy in (*cores, to_far, *gain_copies, *sides):
            copy.wait_send()
        pl.when(stays)(keep.wait)

        @pl.when(jnp.logical_not(stays))
        def _():
            leave.wait_recv()
            leave.wait_send()


def finish_rows(line, weight, own_in, grad_middle, gain, gain_two, rows_one, block, sums):
    length, width = own_in.shape
    near_tokens, line_cols = line.shape
    slots, tile = near_tokens // length, 256
    tiles = width // tile
    once = whole_spec(length, width, once=True)
    column = lambda i: jnp.clip(i - slots, 0, tiles - 1)
    by_column = lambda n: pl.BlockSpec((n, tile), lambda i: (0, column(i)))
    attn_cols = line_cols
    return pl.pallas_call(
        functools.partial(line_kernel, slots, tiles, len(sums)),
        grid=(slots + tiles,),
        in_specs=[
            pl.BlockSpec((length, line_cols), lambda i: (jnp.maximum(slots - 1 - i, 0), 0)),
            whole_spec(width, line_cols, once=True),
            once,
            once,
            whole_spec(1, width),
            whole_spec(1, width),
            by_column(near_tokens),
            whole_spec(near_tokens, line_cols, once=True),
            ANYWHERE,
        ]
        + [ANYWHERE] * len(sums),
        out_specs=[
            whole_spec(length, width),
            whole_spec(2, width),
            pl.BlockSpec((tile, attn_cols), lambda i: (column(i), 0)),
            whole_spec(1, line_cols),
            ANYWHERE,
        ]
        + [ANYWHERE] * len(sums),
        out_shape=[
            jax.ShapeDtypeStruct((length, width), LOW),
            jax.ShapeDtypeStruct((2, width), WIDE),
            jax.ShapeDtypeStruct((width, attn_cols), LOW),
            jax.ShapeDtypeStruct((1, line_cols), WIDE),
            jax.ShapeDtypeStruct((length, width), LOW),
        ]
        + [jax.ShapeDtypeStruct((t.shape[0] // 2, t.shape[1]), LOW) for t in sums],
        scratch_shapes=[
            pltpu.VMEM((slots, length, width), LOW),
            pltpu.VMEM((2, length, width), LOW),
            pltpu.VMEM((length, width), LOW),
            pltpu.VMEM((length, width), WIDE),
            pltpu.VMEM((2, width), WIDE),
            pltpu.VMEM((3, 2, width), WIDE),
            pltpu.SemaphoreType.DMA((7 + len(sums),)),
            pltpu.SemaphoreType.DMA((7 + len(sums),)),
            pltpu.SemaphoreType.DMA,
        ],
        compiler_params=pltpu.CompilerParams(
            vmem_limit_bytes=63 << 20, collective_id=3, has_side_effects=True
        ),
        cost_estimate=estimate(2 * near_tokens * width * attn_cols, 10 * near_tokens * width),
    )(line, weight, own_in, grad_middle, gain, gain_two, rows_one, line, block, *sums)


def place_kernel(count, info, *refs):
    out = refs[count]
    for r in range(count):

        @pl.when(pl.program_id(0) == r)
        def _():
            out[0] = refs[r][...]


def place_rows(rows, order):
    length, width = rows[0].shape
    count = len(rows)
    held = pl.BlockSpec((length, width), lambda s, info: (0, 0), pipeline_mode=pl.Buffered(1))
    return pl.pallas_call(
        functools.partial(place_kernel, count),
        grid_spec=pltpu.PrefetchScalarGridSpec(
            num_scalar_prefetch=1,
            grid=(count,),
            in_specs=[held] * count,
            out_specs=pl.BlockSpec((1, length, width), lambda s, info: (info[s], 0, 0)),
        ),
        out_shape=jax.ShapeDtypeStruct((count, length, width), LOW),
        compiler_params=pltpu.CompilerParams(vmem_limit_bytes=32 << 20),
        cost_estimate=estimate(0, 4 * count * length * width),
    )(order, *rows)


def turn(values, cosine, sine_signed):
    return values * cosine + pltpu.roll(values, values.shape[-1] // 2, 1) * sine_signed


def turn_back(values, cosine, sine_signed):
    return values * cosine - pltpu.roll(values, values.shape[-1] // 2, 1) * sine_signed


def project_kernel(
    heads, head_dim, x0, x1, x2, x3, gains, weight, bias, cosine, sine, h_out, q_out, k_out, v_out, gain
):
    slot = pl.program_id(0)

    @pl.when(slot == 0)
    def _():
        gain[...] = gains[...].astype(WIDE).T[:8]


    def run(x_ref):
        x = x_ref[...].astype(WIDE)
        scale_inv = lax.rsqrt(jnp.mean(x * x, axis=-1, keepdims=True) + EPS)
        normed = (x * scale_inv * gain[0:1]).astype(LOW)
        h_out[0] = normed
        lin = jnp.dot(normed, weight[...], preferred_element_type=WIDE) + bias[...]
        cos, sin = cosine[0], sine[0]
        for h in range(heads + 1):
            part = turn(lin[:, h * head_dim : (h + 1) * head_dim], cos, sin).astype(LOW)
            if h < heads:
                q_out[0, :, h * head_dim : (h + 1) * head_dim] = part
            else:
                k_out[0] = part
        v_out[0] = lin[:, (heads + 1) * head_dim :].astype(LOW)

    for r, x_ref in enumerate((x0, x1, x2, x3)):
        pl.when(slot == r)(functools.partial(run, x_ref))


def project(rows, held, bias, cosine, sine, heads, head_dim):
    length, width = rows[0].shape
    count = len(rows)
    cols = (heads + 2) * head_dim
    whole = whole_spec
    by_slot = lambda *shape: pl.BlockSpec((1, *shape), lambda s: (s,) + (0,) * len(shape))
    return pl.pallas_call(
        functools.partial(project_kernel, heads, head_dim),
        grid=(count,),
        in_specs=[whole(length, width)] * count
        + [part_spec(width, 128, cols // 128), part_spec(width, cols, 0), whole(1, cols)]
        + [by_slot(length, head_dim)] * 2,
        out_specs=[
            by_slot(length, width),
            by_slot(length, heads * head_dim),
            by_slot(length, head_dim),
            by_slot(length, head_dim),
        ],
        out_shape=[
            jax.ShapeDtypeStruct((count, length, width), LOW),
            jax.ShapeDtypeStruct((count, length, heads * head_dim), LOW),
            jax.ShapeDtypeStruct((count, length, head_dim), LOW),
            jax.ShapeDtypeStruct((count, length, head_dim), LOW),
        ],
        scratch_shapes=[pltpu.VMEM((8, width), WIDE)],
        compiler_params=pltpu.CompilerParams(vmem_limit_bytes=56 << 20),
        cost_estimate=pl.CostEstimate(
            flops=2 * count * length * width * cols,
            bytes_accessed=count * length * (2 * width + cols) * 2 + width * cols * 2,
            transcendentals=0,
        ),
    )(*rows, held, held, bias, cosine, sine)


def row_blocks(length):
    return [(i, min(256, length)) for i in range(0, length, min(256, length))]


def key_biases(length, offset, start, rows, past, keys):
    past_pos = lax.broadcasted_iota(jnp.int32, (1, past), 1)
    past_bias = jnp.where((past_pos < offset) & (past_pos < length), 0.0, NEG_FILL)
    query_pos = offset + start + lax.broadcasted_iota(jnp.int32, (rows, keys), 0)
    own_pos = offset + lax.broadcasted_iota(jnp.int32, (rows, keys), 1)
    own_bias = jnp.where((own_pos <= query_pos) & (own_pos < length), 0.0, NEG_FILL)
    return past_bias, own_bias


def dot_cols(left, right):
    return lax.dot_general(left, right, (((1,), (1,)), ((), ())), preferred_element_type=WIDE)


def dot_rows(left, right):
    return lax.dot_general(left, right, (((0,), (0,)), ((), ())), preferred_element_type=WIDE)


def attend_rows(
    heads, head_dim, scale, length, offset, q, k_past, v_past, k_own, v_own, weight, out, lse, put
):
    past = k_past.shape[1]
    for start, rows in row_blocks(q.shape[1]):
        keys = start + rows
        past_bias, own_bias = key_biases(length, offset, start, rows, past, keys)
        here = slice(start, start + rows)
        for h in range(heads):
            cols = slice(h * head_dim, (h + 1) * head_dim)
            query = q[0, here, cols]
            s_past = dot_cols(query, k_past[0]) * scale + past_bias
            s_own = dot_cols(query, k_own[0, :keys]) * scale + own_bias
            top = jnp.maximum(
                jnp.max(s_past, axis=1, keepdims=True), jnp.max(s_own, axis=1, keepdims=True)
            )
            e_past, e_own = jnp.exp(s_past - top), jnp.exp(s_own - top)
            total = jnp.sum(e_past, axis=1, keepdims=True) + jnp.sum(e_own, axis=1, keepdims=True)
            inverse = 1.0 / total
            mixed = jnp.dot(
                (e_past * inverse).astype(LOW), v_past[0], preferred_element_type=WIDE
            ) + jnp.dot((e_own * inverse).astype(LOW), v_own[0, :keys], preferred_element_type=WIDE)
            out[0, here, cols] = mixed.astype(LOW)
            lse[0, here, h : h + 1] = top + jnp.log(total)
        rows_out = dot_cols(out[0, here], weight[...]).astype(LOW)
        put(here, rows_out)


def attend_kernel(
    heads, head_dim, scale, first, total_slots, info, q, k_past, v_past, k_own, v_own, weight, out, lse, *parts
):
    length, offset = info[first + pl.program_id(0)], info[total_slots]

    def put(here, value):
        for i, part in enumerate(parts):

            @pl.when(pl.program_id(0) == i)
            def _():
                part[here] = value

    attend_rows(heads, head_dim, scale, length, offset, q, k_past, v_past, k_own, v_own, weight, out, lse, put)


def attend_forward(info, q, k_past, v_past, k_own, v_own, weight, heads, head_dim, scale, first, count):
    _, length, width = q.shape
    past = k_past.shape[1]
    by_slot = lambda *shape: pl.BlockSpec((1, *shape), lambda s, info: (first + s,) + (0,) * len(shape))
    out_slot = lambda *shape: pl.BlockSpec((1, *shape), lambda s, info: (s,) + (0,) * len(shape))
    keys = count * length * (past + length) * heads
    return pl.pallas_call(
        functools.partial(attend_kernel, heads, head_dim, scale, first, q.shape[0]),
        grid_spec=pltpu.PrefetchScalarGridSpec(
            num_scalar_prefetch=1,
            grid=(count,),
            in_specs=[
                by_slot(length, width),
                by_slot(past, head_dim),
                by_slot(past, head_dim),
                by_slot(length, head_dim),
                by_slot(length, head_dim),
                whole_spec(*weight.shape, once=True),
            ],
            out_specs=[out_slot(length, width), out_slot(length, 128)]
            + [whole_spec(length, weight.shape[0])] * count,
        ),
        out_shape=[
            jax.ShapeDtypeStruct((count, length, width), LOW),
            jax.ShapeDtypeStruct((count, length, 128), WIDE),
        ]
        + [jax.ShapeDtypeStruct((length, weight.shape[0]), LOW)] * count,
        compiler_params=pltpu.CompilerParams(vmem_limit_bytes=56 << 20),
        cost_estimate=estimate(4 * keys * head_dim, 4 * count * length * width, keys),
    )(info, q, k_past, v_past, k_own, v_own, weight)


def attend_back_rows(
    heads, head_dim, scale, length, offset, q, k_past, v_past, k_own, v_own, grad, lse, cosine, sine, put,
    dk_past, dk_own, dv_past, dv_own
):
    past = k_past.shape[1]
    for start, rows in row_blocks(q.shape[1]):
        keys = start + rows
        past_bias, own_bias = key_biases(length, offset, start, rows, past, keys)
        here = slice(start, start + rows)
        cos, sin = cosine[0, here], sine[0, here]
        for h in range(heads):
            cols = slice(h * head_dim, (h + 1) * head_dim)
            query, upstream = q[0, here, cols], grad[0, here, cols]
            log_total = lse[0, here, h : h + 1]
            p_past = jnp.exp(dot_cols(query, k_past[0]) * scale + past_bias - log_total)
            p_own = jnp.exp(dot_cols(query, k_own[0, :keys]) * scale + own_bias - log_total)
            g_past = dot_cols(upstream, v_past[0])
            g_own = dot_cols(upstream, v_own[0, :keys])
            row_dot = jnp.sum(p_past * g_past, axis=1, keepdims=True) + jnp.sum(
                p_own * g_own, axis=1, keepdims=True
            )
            s_past = (p_past * (g_past - row_dot)).astype(LOW)
            s_own = (p_own * (g_own - row_dot)).astype(LOW)
            dq = (
                jnp.dot(s_past, k_past[0], preferred_element_type=WIDE)
                + jnp.dot(s_own, k_own[0, :keys], preferred_element_type=WIDE)
            ) * scale
            put(here, cols, turn_back(dq, cos, sin).astype(LOW))
            dk_past[...] += dot_rows(s_past, query)
            dk_own[:keys] += dot_rows(s_own, query)
            dv_past[...] += dot_rows(p_past.astype(LOW), upstream)
            dv_own[:keys] += dot_rows(p_own.astype(LOW), upstream)


def attend_back_kernel(
    heads,
    head_dim,
    scale,
    info,
    q,
    k_past,
    v_past,
    k_own,
    v_own,
    grad,
    lse,
    cosine,
    sine,
    dq_out,
    mine_past,
    mine_own,
    other_past,
    other_own,
    dk_past,
    dk_own,
    dv_past,
    dv_own,
):
    slot = pl.program_id(0)
    length, offset = info[slot], info[pl.num_programs(0)]
    parity = info[pl.num_programs(0) + 1]
    for total in (dk_past, dk_own, dv_past, dv_own):
        total[...] = jnp.zeros_like(total)
    attend_back_rows(
        heads, head_dim, scale, length, offset, q, k_past, v_past, k_own, v_own, grad, lse, cosine, sine,
        lambda here, cols, value: dq_out.__setitem__((0, here, cols), value),
        dk_past, dk_own, dv_past, dv_own,
    )

    @pl.when(parity == 0)
    def _():
        mine_past[0] = dk_past[...] * scale
        mine_own[0] = dk_own[...] * scale
        other_past[0] = dv_past[...]
        other_own[0] = dv_own[...]

    @pl.when(parity != 0)
    def _():
        mine_past[0] = dv_past[...]
        mine_own[0] = dv_own[...]
        other_past[0] = dk_past[...] * scale
        other_own[0] = dk_own[...] * scale


def attend_backward(
    info, q, k_past, v_past, k_own, v_own, grad, lse, cosine, sine, heads, head_dim, scale
):
    count, length, width = q.shape
    past = k_past.shape[1]
    by_slot = lambda *shape: pl.BlockSpec((1, *shape), lambda s, info: (s,) + (0,) * len(shape))
    keys = count * length * (past + length) * heads
    return pl.pallas_call(
        functools.partial(attend_back_kernel, heads, head_dim, scale),
        grid_spec=pltpu.PrefetchScalarGridSpec(
            num_scalar_prefetch=1,
            grid=(count,),
            in_specs=[
                by_slot(length, width),
                by_slot(past, head_dim),
                by_slot(past, head_dim),
                by_slot(length, head_dim),
                by_slot(length, head_dim),
                by_slot(length, width),
                by_slot(length, 128),
                by_slot(length, head_dim),
                by_slot(length, head_dim),
            ],
            out_specs=[
                by_slot(length, width),
                by_slot(past, head_dim),
                by_slot(length, head_dim),
                by_slot(past, head_dim),
                by_slot(length, head_dim),
            ],
            scratch_shapes=[
                pltpu.VMEM((past, head_dim), WIDE),
                pltpu.VMEM((length, head_dim), WIDE),
                pltpu.VMEM((past, head_dim), WIDE),
                pltpu.VMEM((length, head_dim), WIDE),
            ],
        ),
        out_shape=[
            jax.ShapeDtypeStruct((count, length, width), LOW),
            jax.ShapeDtypeStruct((count, past, head_dim), WIDE),
            jax.ShapeDtypeStruct((count, length, head_dim), WIDE),
            jax.ShapeDtypeStruct((count, past, head_dim), WIDE),
            jax.ShapeDtypeStruct((count, length, head_dim), WIDE),
        ],
        compiler_params=pltpu.CompilerParams(vmem_limit_bytes=56 << 20),
        cost_estimate=estimate(10 * keys * head_dim, 8 * count * length * width, keys),
    )(info, q, k_past, v_past, k_own, v_own, grad, lse, cosine, sine)


def attend_sum_kernel(
    heads, head_dim, scale, slots, info, q, k_past, v_past, k_own, v_own, weight, own_in, gain, out, lse, middle,
    normed, parts, core_in, far_in, send, recv
):
    step = pl.program_id(0)
    slot = slots - 1 - step
    core, far, _ = partners_of()
    remote = remote_copy(send, recv)
    cores = [remote(parts.at[3 - 2 * k], core_in.at[k], k, core) for k in range(2)]
    to_far = remote(parts.at[2], far_in, 2, far)

    @pl.when(step == 0)
    def _():
        meet((core, far))

    def put(here, value):
        parts[slot, here] = value

    offset = lax.axis_index("ctx") * q.shape[1]
    attend_rows(
        heads, head_dim, scale, info[slot], offset, q, k_past, v_past, k_own, v_own, weight, out, lse, put
    )
    for k in range(2):
        pl.when(step == 2 * k)(cores[k].start)

    @pl.when(step == 1)
    def _():
        cores[0].wait_recv()
        parts[2] = (parts[2].astype(WIDE) + core_in[0].astype(WIDE)).astype(LOW)
        to_far.start()

    @pl.when(step == slots - 1)
    def _():
        cores[1].wait_recv()
        to_far.wait_recv()
        rows = own_in[...].astype(WIDE) + parts[0].astype(WIDE)
        rows = rows + core_in[1].astype(WIDE) + far_in[...].astype(WIDE)
        middle[...] = rows
        inverse = lax.rsqrt(jnp.mean(rows * rows, axis=-1, keepdims=True) + EPS)
        normed[...] = (rows * inverse * gain[...]).astype(LOW)
        for copy in (*cores, to_far):
            copy.wait_send()


def attend_sum(info, q, k_past, v_past, k_own, v_own, weight, own_in, gain, heads, head_dim, scale):
    count, length, width = q.shape
    past, model_width = k_past.shape[1], own_in.shape[1]
    by_slot = lambda *shape: pl.BlockSpec(
        (1, *shape), lambda i, info: (count - 1 - i,) + (0,) * len(shape)
    )
    keys = count * length * (past + length) * heads
    return pl.pallas_call(
        functools.partial(attend_sum_kernel, heads, head_dim, scale, count),
        grid_spec=pltpu.PrefetchScalarGridSpec(
            num_scalar_prefetch=1,
            grid=(count,),
            in_specs=[
                by_slot(length, width),
                by_slot(past, head_dim),
                by_slot(past, head_dim),
                by_slot(length, head_dim),
                by_slot(length, head_dim),
                whole_spec(*weight.shape, once=True),
                whole_spec(length, model_width, once=True),
                whole_spec(1, model_width),
            ],
            out_specs=[
                by_slot(length, width),
                by_slot(length, 128),
                whole_spec(length, model_width, once=True),
                whole_spec(length, model_width, once=True),
            ],
            scratch_shapes=[
                pltpu.VMEM((count, length, model_width), LOW),
                pltpu.VMEM((2, length, model_width), LOW),
                pltpu.VMEM((length, model_width), LOW),
                pltpu.SemaphoreType.DMA((3,)),
                pltpu.SemaphoreType.DMA((3,)),
            ],
        ),
        out_shape=[
            jax.ShapeDtypeStruct((count, length, width), LOW),
            jax.ShapeDtypeStruct((count, length, 128), WIDE),
            jax.ShapeDtypeStruct((length, model_width), WIDE),
            jax.ShapeDtypeStruct((length, model_width), LOW),
        ],
        compiler_params=pltpu.CompilerParams(
            vmem_limit_bytes=56 << 20, collective_id=5, has_side_effects=True
        ),
        cost_estimate=estimate(4 * keys * head_dim, 4 * count * length * width, keys),
    )(info, q, k_past, v_past, k_own, v_own, weight, own_in, gain)


def exchange_kernel(
    heads, head_dim, scale, slots, tiles, info, q, k_past, v_past, k_own, v_own, rows, weight, lse, cosine, sine,
    cosine_all, sine_all, branch, mixed, mlp_far, mlp_side, mlp_own, middle, line, out_grad, block, mine_past,
    mine_own, other_past, other_own, got_past, got_own, side_out, side_in, dk_past, dk_own, dv_past, dv_own,
    own_rows, last_in, grad, send, recv, load
):
    step = pl.program_id(0)
    tensor_rank = lax.axis_index("tp")
    core, far, side = partners_of()
    parity = lax.rem(tensor_rank, 2)
    offset = lax.axis_index("ctx") * q.shape[1]
    remote = remote_copy(send, recv)
    pasts = [remote(other_past.at[r], got_past.at[r ^ 1], r, core) for r in range(slots)]
    owns = [remote(other_own.at[r], got_own.at[r ^ 1], slots + r, core) for r in range(slots)]
    sides = [remote(side_out.at[r], side_in.at[r], 2 * slots + r, side) for r in range(slots)]
    lasts = [
        remote(mlp_far, last_in.at[0], 3 * slots, far),
        remote(mlp_side, last_in.at[1], 3 * slots + 1, side),
    ]
    loading = pltpu.make_async_copy(mlp_own, own_rows, load)

    @pl.when(step == 0)
    def _():
        loading.start()
        meet((core, far, side))
        for copy in lasts:
            copy.start()

    @pl.when(step < slots)
    def _():
        length = info[jnp.minimum(step, slots - 1)]
        for total in (dk_past, dk_own, dv_past, dv_own):
            total[...] = jnp.zeros_like(total)
        grad[0] = jnp.dot(rows[...], weight[...], preferred_element_type=WIDE).astype(LOW)
        attend_back_rows(
            heads, head_dim, scale, length, offset, q, k_past, v_past, k_own, v_own, grad, lse, cosine,
            sine, lambda here, cols, value: line.__setitem__((step, here, cols), value),
            dk_past, dk_own, dv_past, dv_own,
        )

        @pl.when(parity == 0)
        def _():
            mine_past[step] = dk_past[...] * scale
            mine_own[step] = dk_own[...] * scale
            other_past[step] = dv_past[...]
            other_own[step] = dv_own[...]

        @pl.when(parity != 0)
        def _():
            mine_past[step] = dv_past[...]
            mine_own[step] = dv_own[...]
            other_past[step] = dk_past[...] * scale
            other_own[step] = dk_own[...] * scale

    for r in range(slots):

        def start(r=r):
            pasts[r].start()
            owns[r].start()

        pl.when(step == r)(start)

    for pair in range(0, slots, 2):

        def merge(pair=pair):
            for r in (pair, pair + 1):
                pasts[r ^ 1].wait_recv()
                side_out[r] = (mine_past[r] + got_past[r]).astype(LOW)
                sides[r].start()

        pl.when(step == pair + 1)(merge)

    @pl.when(step >= slots)
    def _():
        out_grad[...] = dot_rows(branch[...], mixed[...]).astype(LOW)

    @pl.when(step == slots + tiles - 1)
    def _():
        for r in range(slots):
            owns[r ^ 1].wait_recv()
            sides[r].wait_recv()
            total = mine_own[r] + got_own[r] + side_in[r].astype(WIDE)
            back = turn_back(total, cosine_all[r], sine_all[r])
            line[r, :, heads * head_dim :] = jnp.where(parity == 0, back, total).astype(LOW)
        loading.wait()
        for copy in lasts:
            copy.wait_recv()
        block[...] = (
            middle[...] + own_rows[...].astype(WIDE) + last_in[0].astype(WIDE) + last_in[1].astype(WIDE)
        ).astype(LOW)
        for copy in (*pasts, *owns, *sides, *lasts):
            copy.wait_send()


def attend_exchange(
    info, q, k_past, v_past, k_own, v_own, weight, lse, cosine, sine, heads, head_dim, scale, branch, mixed, mlp,
    middle
):
    count, length, width = q.shape
    past = k_past.shape[1]
    tokens, model_width = branch.shape
    tile = 256
    tiles = model_width // tile
    slot = lambda i: jnp.minimum(i, count - 1)
    by_slot = lambda *shape: pl.BlockSpec((1, *shape), lambda i, info: (slot(i),) + (0,) * len(shape))
    column = lambda i: jnp.clip(i - count, 0, tiles - 1)
    held = lambda *shape: pl.BlockSpec(
        shape, lambda i, info: (0,) * len(shape), pipeline_mode=pl.Buffered(1)
    )
    line_cols = width + head_dim
    return pl.pallas_call(
        functools.partial(exchange_kernel, heads, head_dim, scale, count, tiles),
        grid_spec=pltpu.PrefetchScalarGridSpec(
            num_scalar_prefetch=1,
            grid=(count + tiles,),
            in_specs=[
                by_slot(length, width),
                by_slot(past, head_dim),
                by_slot(past, head_dim),
                by_slot(length, head_dim),
                by_slot(length, head_dim),
                pl.BlockSpec((length, model_width), lambda i, info: (slot(i), 0)),
                held(*weight.shape),
                by_slot(length, 128),
                by_slot(length, head_dim),
                by_slot(length, head_dim),
                held(count, length, head_dim),
                held(count, length, head_dim),
                pl.BlockSpec((tokens, tile), lambda i, info: (0, column(i))),
                held(*mixed.shape),
            ]
            + [ANYWHERE] * 3
            + [held(length, model_width)],
            out_specs=[
                held(count, length, line_cols),
                pl.BlockSpec((tile, width), lambda i, info: (column(i), 0)),
                held(length, model_width),
            ],
            scratch_shapes=[pltpu.VMEM((count, length, head_dim), WIDE)] * 6
            + [pltpu.VMEM((count, length, head_dim), LOW)] * 2
            + [pltpu.VMEM((length, head_dim), WIDE)] * 4
            + [
                pltpu.VMEM((length, model_width), LOW),
                pltpu.VMEM((2, length, model_width), LOW),
                pltpu.VMEM((1, length, width), LOW),
                pltpu.SemaphoreType.DMA((3 * count + 2,)),
                pltpu.SemaphoreType.DMA((3 * count + 2,)),
                pltpu.SemaphoreType.DMA,
            ],
        ),
        out_shape=[
            jax.ShapeDtypeStruct((count, length, line_cols), LOW),
            jax.ShapeDtypeStruct((model_width, width), LOW),
            jax.ShapeDtypeStruct((length, model_width), LOW),
        ],
        compiler_params=pltpu.CompilerParams(
            vmem_limit_bytes=63 << 20, collective_id=4, has_side_effects=True
        ),
        cost_estimate=estimate(2 * tokens * model_width * width, 10 * tokens * width),
    )(info, q, k_past, v_past, k_own, v_own, branch, weight, lse, cosine, sine, cosine, sine, branch, mixed, *mlp, middle)


def local(
    hidden_in,
    cotangent,
    seq_lengths,
    positions,
    permutation,
    query_weight,
    keyval_weight,
    output_weight,
    norm_gains,
    bias_query,
    bias_keyval,
    gate_weight,
    up_weight,
    down_weight,
):
    group_rank = lax.axis_index("fsdp")
    ctx_rank = lax.axis_index("ctx")
    tensor_rank = lax.axis_index("tp")
    fsdp_count = lax.axis_size("fsdp")
    ctx_count = lax.axis_size("ctx")
    tensor_count = lax.axis_size("tp")
    seq_grp, local_len, model_width = hidden_in.shape
    heads, head_dim = bias_query.shape
    keyval_heads = bias_keyval.shape[0] // 2
    assert seq_grp == tensor_count == fsdp_count == len(DEAL_SHIFT)
    token_count = seq_grp * local_len
    scale = 1.0 / math.sqrt(head_dim)
    offset = ctx_rank * local_len
    head_pair = tensor_rank // (tensor_count // keyval_heads)
    parity = tensor_rank % 2
    assert DEAL_SHIFT == tuple((t % 2) * 2 + t // 2 for t in range(tensor_count))

    entry = jnp.arange(permutation.shape[0])
    entry_group, entry_slot = entry // seq_grp, entry % seq_grp
    home_group, home_slot = lax.div(permutation, seq_grp), lax.rem(permutation, seq_grp)
    places = jnp.arange(2 * seq_grp)
    near_places = places < seq_grp
    slot_rank = tensor_rank ^ (places % seq_grp)
    shift_of = lambda rank: lax.rem(rank, 2) * 2 + lax.div(rank, 2)
    target = lax.rem(group_rank + shift_of(tensor_rank), fsdp_count)
    leaving = jnp.sum(jnp.where((entry_group == target) & (home_group == group_rank), home_slot, 0))
    source = lax.rem(group_rank + fsdp_count - shift_of(slot_rank), fsdp_count)
    hit = (entry_group == group_rank)[None] & (home_group[None] == source[:, None])
    slot_now = jnp.sum(jnp.where(hit, entry_slot[None], 0), axis=1)
    seq_now = jnp.sum(jnp.where(hit, permutation[None], 0), axis=1)
    targets = lax.rem(group_rank + shift_of(slot_rank), fsdp_count)
    back_hit = (entry_group[None] == targets[:, None]) & (home_group == group_rank)[None]
    home_order = jnp.sum(jnp.where(back_hit, home_slot[None], 0), axis=1)[:seq_grp]
    there = [
        (f * tensor_count + t, (f + DEAL_SHIFT[t]) % fsdp_count * tensor_count + t)
        for f in range(fsdp_count)
        for t in range(tensor_count)
    ]
    back = [(target, source) for source, target in there]

    split = units_split()
    head_width = 2 * head_dim
    query_cols = heads * head_dim
    near_cols = query_cols + head_width + 128

    outgoing = lax.dynamic_index_in_dim(hidden_in, leaving, 0, keepdims=False)
    own_in = lax.ppermute(outgoing, ("fsdp", "tp"), there)
    small = jnp.concatenate(
        [
            query_weight,
            lax.dynamic_slice_in_dim(keyval_weight, head_pair * head_width, head_width, axis=1),
            jnp.pad(norm_gains.T, ((0, 0), (0, 128 - norm_gains.shape[0]))),
            output_weight.T,
        ],
        axis=1,
    )
    seq_hit = seq_now[:, None] == entry[None]
    lengths_now = jnp.sum(jnp.where(seq_hit, seq_lengths[None], 0), axis=1)
    more = jnp.where(places == seq_grp, offset, jnp.where(places == seq_grp + 1, parity, 0))
    info = jnp.where(near_places, lengths_now, more).astype(jnp.int32)
    positions_now = jnp.sum(
        jnp.where(seq_hit[:seq_grp, :, None], positions[None], 0), axis=1
    )
    lane = jnp.arange(head_dim)
    frequency = 1.0 / ROPE_BASE ** ((lane % (head_dim // 2)).astype(WIDE) * 2.0 / head_dim)
    angles = positions_now.astype(WIDE)[..., None] * frequency
    cosine = jnp.cos(angles)
    sine = jnp.sin(angles) * jnp.where(lane < head_dim // 2, -1.0, 1.0)
    pick_info = jnp.where(near_places, slot_now, slot_now ^ tensor_rank).astype(jnp.int32)
    units = gate_weight.shape[1]
    units_pad = -(-units // 256) * 256
    widen = lambda w: jnp.pad(w, ((0, 0), (0, units_pad - units)))
    shards = [widen(w) for w in (down_weight.T, gate_weight, up_weight)]
    if split:
        half_units = units_pad // 2
        cut = lambda w, c: lax.dynamic_slice_in_dim(w, c * half_units, half_units, axis=1)

        def in_order(own, other):
            return jnp.stack(
                [jnp.where(ctx_rank == 0, own, other), jnp.where(ctx_rank == 0, other, own)]
            )

        def all_rows(both, *earlier):
            full = lax.all_gather(after(both, *earlier), "fsdp", axis=0, tiled=False)
            return full.reshape(-1, both.shape[-1])

        first_units = half_units - half_units // 2 // 256 * 256
        first_cols = 3 * first_units

        def in_parts(c):
            halves = [cut(w, c) for w in shards]
            return jnp.concatenate(
                [w[:, :first_units] for w in halves] + [w[:, first_units:] for w in halves], axis=1
            )

        leaving_units, own_units = in_parts(1 - ctx_rank), in_parts(ctx_rank)
        slot_pick = lax.dynamic_index_in_dim(cotangent, tensor_rank, 0, keepdims=False)
        small = after(small, outgoing, leaving_units, cosine, sine, slot_pick)
        small_both = in_order(small, from_partner(small, "ctx", 1))
        arriving_units = from_partner(after(leaving_units, small_both), "ctx", 1)
        other_own = from_partner(after(slot_pick, arriving_units), "ctx", 1)
        both_a = in_order(own_units[:, :first_cols], arriving_units[:, :first_cols])
        both_b = in_order(own_units[:, first_cols:], arriving_units[:, first_cols:])
    else:
        all_rows = lambda shard, *earlier: lax.all_gather(
            shard, ("fsdp", "ctx"), axis=0, tiled=True
        )
        small_both, unit_both, half_units = small, jnp.concatenate(shards, axis=1), units_pad
    far_in = from_partner(own_in, "tp", 2)
    near_in = from_partner(own_in, "tp", 1)
    ready = (info, pick_info, own_units, home_order) if split else (cosine, sine, info)
    cross_in = from_partner(after(far_in, *ready), "tp", 1)

    near_full = all_rows(small_both, own_in)
    if split:
        units_a = all_rows(both_a, cross_in)
        units_b = all_rows(both_b, cross_in)
    else:
        down_full = all_rows(unit_both[..., :half_units], cross_in)
        gate_up_full = all_rows(unit_both[..., half_units:], cross_in)
    output_full = near_full[:, near_cols:]
    bias_head = lax.dynamic_slice_in_dim(bias_keyval, head_pair * 2, 2, axis=0)
    bias_row = jnp.concatenate([bias_query.reshape(1, -1), bias_head.reshape(1, -1)], axis=1).astype(WIDE)
    normed_one, query_rot, key_own, value_own = project(
        (own_in, near_in, far_in, cross_in),
        near_full,
        bias_row,
        after(cosine, other_own, both_a, both_b, info, pick_info) if split else cosine,
        sine,
        heads,
        head_dim,
    )
    gains_now = near_full[:, query_cols + head_width : near_cols][:, :2].astype(WIDE).T
    if split:
        key_past, value_past = lax.ppermute((key_own, value_own), "ctx", [(0, 1)])
        other_far = from_partner(other_own, "tp", 2)
        other_near = from_partner(after(other_own, key_past), "tp", 1)
        other_cross = from_partner(after(other_far, key_past), "tp", 1)
        other_rows = (other_own, other_near, other_far, other_cross)
        key_past = after(key_past, other_far)
    else:
        key_past = lax.all_gather(key_own, "ctx", axis=1, tiled=True)
        value_past = lax.all_gather(value_own, "ctx", axis=1, tiled=True)
    project_full = after(near_full, query_rot)[:, : query_cols + head_width]
    own_weight = lax.dynamic_slice_in_dim(
        project_full, query_cols + parity * head_dim, head_dim, axis=1
    )
    back_full = jnp.concatenate([project_full[:, :query_cols], own_weight], axis=1)
    in_share = own_in.astype(WIDE)
    if split:
        mixed, lse, middle_share, normed_share = attend_sum(
            info,
            query_rot,
            key_past,
            value_past,
            key_own,
            value_own,
            after(output_full, back_full),
            own_in,
            gains_now[1:2],
            heads,
            head_dim,
            scale,
        )
    else:
        attend = lambda first, *held: attend_forward(
            info, query_rot, *held, key_own, value_own, output_full, heads, head_dim, scale, first, 2
        )

        mixed_far, lse_far, *attn_far = attend(2, key_past, value_past)
        attn_wide = collect_far(attn_far[0], attn_far[1])
        attn_got = from_partner(attn_wide, "tp", 2)
        mixed_near, lse_near, *attn_near = attend(0, after(key_past, attn_wide), value_past)
        attn_core = from_partner(attn_near[1], "tp", 1)
        middle_share = (
            in_share
            + attn_near[0].astype(WIDE)
            + attn_core.astype(WIDE)
            + attn_got.astype(WIDE)
        )
        inv_two = lax.rsqrt(jnp.mean(middle_share * middle_share, axis=-1, keepdims=True) + EPS)
        normed_share = (middle_share * inv_two * gains_now[1]).astype(LOW)
        mixed = jnp.concatenate([mixed_near, mixed_far], axis=0)
        lse = jnp.concatenate([lse_near, lse_far], axis=0)
    half_len = local_len // 2

    if split:
        grad_hidden, grad_rows = chosen_rows(
            pick_info,
            after(cotangent, normed_share),
            other_rows,
            units_a,
            0,
            3,
        )
    else:
        grad_slots = [
            lax.dynamic_index_in_dim(cotangent, slot_now[r], 0, keepdims=False) for r in range(seq_grp)
        ]
        grad_hidden, grad_rows = stack_rows([(g,) for g in grad_slots], down_full, 0, 1)

    def spread_all(own):
        far = from_partner(own, "tp", 2)
        near = from_partner(own, "tp", 1)
        if not split:
            return (own, near, far, from_partner(far, "tp", 1))
        side = from_partner(own, "ctx", 1)
        held = after(far, grad_hidden), after(side, grad_hidden)
        across = from_partner(held[0][:half_len], "ctx", 1), from_partner(held[1][half_len:], "tp", 2)
        cores = [from_partner(v, "tp", 1) for v in held]
        return (own, near, far, cores[0], side, cores[1], *across)

    def in_slots(rows):
        if not split:
            return [(row,) for row in rows]
        return [(row,) for row in rows[:6]] + [rows[6:]]

    mixed_flat = mixed.reshape(token_count, query_cols)
    normed_slots = in_slots(spread_all(normed_share))
    if split:
        ahead = stack_rows(normed_slots[:6], units_a, 1, 3, total=8)
        last = [normed_slots[6], tuple(from_partner(after(v, ahead[0]), "tp", 1) for v in normed_slots[6])]
        gate_lin, normed_two = stack_rows(last, units_a, 1, 3, into=ahead, first=6, total=8)
        hidden_a, gate_a, up_a = hidden_units(normed_two, units_a, 2, 3, gate_lin, grad_hidden)
        grad_a = first_grads(grad_rows, normed_two, hidden_a, gate_a, up_a)
        hidden_b, gate_b, up_b = full_units(after(normed_two, grad_a), grad_rows, units_b)
    else:
        gate_lin, normed_two = stack_rows(normed_slots, gate_up_full, 0, 2)
        hidden_act, grad_gate, grad_up = hidden_units(
            normed_two, gate_up_full, 1, 2, gate_lin, grad_hidden
        )

    def collect_all(lefts, weights, *earlier):
        lefts = list(lefts)
        lefts[0] = after(lefts[0], *earlier)
        last = back_rows(lefts, weights, 2, 2, local_len)
        got = [from_partner(collect_far(last[0], last[1]), "tp", 2)]
        first = back_rows(lefts, weights, 0, 2, local_len)
        got.append(from_partner(first[1], "tp", 1))

        def finish():
            return sum((v.astype(WIDE) for v in got), first[0].astype(WIDE))

        return first[0], finish

    if split:
        grad_two_share, down_b, up_grad_b = collect_back(
            (gate_a, up_a),
            (gate_b, up_b),
            units_a,
            units_b,
            grad_rows,
            normed_two,
            hidden_b,
            local_len,
        )
        grad_middle, gain_two, gate_grad_b, grad_branch, *mlp = spread_branch(
            grad_two_share,
            middle_share,
            grad_rows,
            gains_now[1:2],
            hidden_a,
            hidden_b,
            units_a,
            units_b,
            normed_two,
            gate_b,
        )
        mlp_own, mlp_far, mlp_side = mlp
        grad_branch = grad_branch.reshape(token_count, model_width)
    else:
        first_back, finish_back = collect_all(
            (grad_gate, grad_up), ((gate_up_full, 0, 2), (gate_up_full, 1, 2))
        )
        down_grad = contract_rows(after(grad_rows, first_back), hidden_act, LOW)
        gate_grad = contract_rows(normed_two, after(grad_gate, down_grad), LOW)
        grad_two_share = finish_back()
        grad_norm_two, gain_two = norm_backward(
            middle_share, inv_two, gains_now[1], grad_two_share
        )
        grad_middle = grad_slots[0].astype(WIDE) + grad_norm_two
        branch_own = grad_middle.astype(LOW)
        branch_far = from_partner(branch_own, "tp", 2)
        branch_near = from_partner(branch_own, "tp", 1)
        branch_cross = from_partner(branch_far, "tp", 1)
        grad_branch = jnp.concatenate([branch_own, branch_near, branch_far, branch_cross], axis=0)
        up_grad = contract_rows(normed_two, after(grad_up, branch_own), LOW)

    grad_mixed = None if split else product(grad_branch, output_full, LOW)
    attend_args = (
        info,
        query_rot,
        key_past,
        value_past,
        key_own,
        value_own,
        output_full if split else grad_mixed.reshape(seq_grp, local_len, query_cols),
        lse,
        cosine,
        sine,
        heads,
        head_dim,
        scale,
    )
    if split:
        line_grad, output_grad, block_share = attend_exchange(
            *attend_args,
            grad_branch,
            mixed_flat,
            (mlp_far, mlp_side, mlp_own),
            middle_share,
        )
        line_grad = line_grad.reshape(token_count, -1)
    else:
        grad_query, mine_past, mine_own, other_past, other_own = attend_backward(*attend_args)
        swap = lambda value: jnp.stack([value[r ^ 1] for r in range(seq_grp)])
        got_past, got_own = from_partner((other_past, other_own), "tp", 1)
        past_sum = mine_past + swap(got_past)
        own_sum = mine_own + swap(got_own)
        own_sum = own_sum + lax.psum_scatter(past_sum, "ctx", scatter_dimension=1, tiled=True)
        half_lanes = head_dim // 2
        turned = own_sum * cosine - jnp.roll(own_sum, half_lanes, axis=-1) * sine
        own_grad = jnp.where(parity == 0, turned, own_sum).astype(LOW).reshape(token_count, head_dim)
        line_grad = jnp.concatenate([grad_query.reshape(token_count, query_cols), own_grad], axis=1)
    def scatter_units(grad):
        if not split:
            return scatter_sum(grad, ctx_rank, LOW)
        return lax.psum_scatter(grad, "fsdp", scatter_dimension=0, tiled=True)

    unit_grads = (grad_a, down_b, up_grad_b, gate_grad_b) if split else (down_grad, gate_grad, up_grad)
    unit_sums = [scatter_units(unit_grads[0])]
    if split:
        unit_sums += [scatter_units(after(g, unit_sums[0])) for g in unit_grads[1:3]]
        unit_sums += [scatter_units(after(unit_grads[3], unit_sums[0]))]
    else:
        unit_sums += [scatter_units(g) for g in unit_grads[1:]]

    normed_flat = normed_one.reshape(token_count, model_width)
    if split:
        input_share, gain_grad, attn_grad, bias_grad, block_home, *unit_gots = finish_rows(
            line_grad,
            back_full,
            own_in,
            grad_middle,
            gains_now[0:1],
            gain_two,
            normed_flat,
            block_share,
            unit_sums,
        )
        attn_grad = jnp.concatenate([attn_grad, output_grad], axis=1)
    else:
        half = token_count // 2
        line_far = contract_cols(line_grad[half:], back_full, LOW).reshape(2, local_len, model_width)
        line_near = contract_cols(line_grad[:half], back_full, LOW).reshape(2, local_len, model_width)
        line_wide = collect_far(line_far[0], line_far[1])
        line_got = from_partner(line_wide, "tp", 2)
        line_core = from_partner(line_near[1], "tp", 1)
        first_mlp, finish_mlp = collect_all((hidden_act,), ((down_full, 0, 1),), up_grad, branch_far)
        block_share = (middle_share + finish_mlp()).astype(LOW)
        grad_one_share = line_near[0].astype(WIDE) + line_core.astype(WIDE) + line_got.astype(WIDE)
        inv_one = lax.rsqrt(jnp.mean(in_share * in_share, axis=-1, keepdims=True) + EPS)
        grad_norm_one, gain_one = norm_backward(in_share, inv_one, gains_now[0], grad_one_share)
        input_share = (grad_middle + grad_norm_one).astype(LOW)
        attn_grad = jnp.concatenate(
            [contract_rows(normed_flat, line_grad, LOW), contract_rows(grad_branch, mixed_flat, LOW)],
            axis=1,
        )
        bias_grad = jnp.sum(line_grad.astype(WIDE), axis=0)

    shard_count = fsdp_count * ctx_count
    share = head_dim // shard_count
    if not split:
        gain_grad = jnp.concatenate([gain_one, gain_two], axis=0)
        gain_grad = gain_grad + from_partner(gain_grad, "tp", 1)
        gain_grad = gain_grad + from_partner(gain_grad, "tp", 2)
    bias_cols = jnp.transpose(bias_grad.reshape(heads + 1, shard_count, share), (1, 2, 0))
    bias_cols = jnp.pad(bias_cols, ((0, 0), (0, (model_width - head_dim) // shard_count), (0, 0)))
    tiny = jnp.concatenate([gain_grad.T, bias_cols.reshape(model_width, heads + 1)], axis=1)
    tiny = jnp.pad(tiny, ((0, 0), (0, 128 - tiny.shape[1]))).astype(LOW)
    attn_grad = jnp.concatenate([attn_grad, tiny], axis=1)
    if split:
        attn_blocks = attn_grad.reshape(fsdp_count, ctx_count, -1, attn_grad.shape[1])
        kept, sent = scatter_ctx(attn_blocks, ctx_rank)
        attn_held = (kept.astype(WIDE) + from_partner(sent, "ctx", 1).astype(WIDE)).astype(LOW)
        attn_held = attn_held.reshape(-1, attn_grad.shape[1])
        attn_end = lax.psum_scatter(after(attn_held, *unit_sums), "fsdp", scatter_dimension=0, tiled=True)
    else:
        attn_end = scatter_sum(attn_grad, ctx_rank, LOW, *unit_sums)


    def leave(share):
        return lax.ppermute(share, ("fsdp", "tp"), back)

    def arrive(own, *earlier):
        far = from_partner(own, "tp", 2)
        near = from_partner(own, "tp", 1)
        return (own, near, far, from_partner(after(far, *earlier), "tp", 1))

    input_home = leave(input_share)
    if not split:
        block_home = leave(block_share)
    block_out = place_rows(arrive(block_home), home_order)
    if split:
        input_home = after(input_home, attn_held)
        input_rows = arrive(input_home, block_out)
    else:
        input_rows = arrive(input_home)
    input_grad = place_rows(input_rows, home_order)

    small_at = query_cols + head_dim + query_cols
    tiny_grad = attn_end[:, small_at:].astype(WIDE)

    if split:

        def own_half(total):
            rows = total.shape[0] // 2
            return lax.dynamic_slice_in_dim(total, ctx_rank * rows, rows, axis=0)

        (own_a, got_a), *ends = [(own_half(t), got) for t, got in zip(unit_sums, unit_gots)]

        def joined(part, end):
            cols = slice(part * first_units, (part + 1) * first_units)
            own = jnp.concatenate([own_a[:, cols], end[0]], axis=1)
            got = jnp.concatenate([got_a[:, cols], end[1]], axis=1)
            first, second = jnp.where(ctx_rank == 0, own, got), jnp.where(ctx_rank == 0, got, own)
            return jnp.concatenate([first, second], axis=1)[:, :units].astype(WIDE)

        down_end, gate_end, up_end = joined(0, ends[0]), joined(1, ends[2]), joined(2, ends[1])
    else:
        down_end, gate_end, up_end = (t[:, :units].astype(WIDE) for t in unit_sums)
    return (
        block_out,
        input_grad,
        attn_end[:, :query_cols].astype(WIDE),
        attn_end[:, query_cols : query_cols + head_dim].astype(WIDE),
        attn_end[:, query_cols + head_dim : small_at].astype(WIDE).T,
        tiny_grad[:, :2].T,
        tiny_grad[:share, 2 : 2 + heads].T,
        tiny_grad[:share, 2 + heads : 3 + heads].T,
        gate_end,
        up_end,
        down_end.T,
    )


def solution(mesh):
    placed = (
        P("fsdp", "ctx", None),
        P("fsdp", "ctx", None),
        P(),
        P(None, "ctx"),
        P(),
        P(("fsdp", "ctx"), "tp"),
        P(("fsdp", "ctx"), None),
        P("tp", ("fsdp", "ctx")),
        P(None, ("fsdp", "ctx")),
        P("tp", None),
        P(),
        P(("fsdp", "ctx"), "tp"),
        P(("fsdp", "ctx"), "tp"),
        P("tp", ("fsdp", "ctx")),
    )
    return jax.shard_map(
        local,
        mesh=mesh,
        in_specs=placed,
        out_specs=(
            P("fsdp", "ctx", None),
            P("fsdp", "ctx", None),
            P(("fsdp", "ctx"), "tp"),
            P(("fsdp", "ctx"), "tp"),
            P("tp", ("fsdp", "ctx")),
            P(None, ("fsdp", "ctx")),
            P("tp", ("fsdp", "ctx")),
            P("tp", ("fsdp", "ctx")),
            P(("fsdp", "ctx"), "tp"),
            P(("fsdp", "ctx"), "tp"),
            P("tp", ("fsdp", "ctx")),
        ),
        check_vma=False,
    )
```
